32 devices in a mesh: ctx: 8 (over y, x, core), fsdp: 4 (over z).
Axes of the slice: x: 2, y: 2, z: 4, core: 2. Of those that a mesh axis runs over, the one named last changes fastest.
Arguments:
- layer_input: bfloat16 [4, 1024, 960], P('fsdp', 'ctx'), may hold values from -60 to 60
- output_grad: bfloat16 [4, 1024, 960], P('fsdp', 'ctx'), may hold values from -6 to 6
- query_weight: bfloat16 [960, 960], P('fsdp'), may hold values from -0.1875 to 0.1875
- key_weight: bfloat16 [960, 320], P('fsdp'), may hold values from -0.1875 to 0.1875
- value_weight: bfloat16 [960, 320], P('fsdp'), may hold values from -0.1875 to 0.1875
- output_weight: bfloat16 [960, 960], P('fsdp'), may hold values from -6 to 6
- gate_weight: bfloat16 [960, 2560], P('fsdp'), may hold values from -0.1875 to 0.1875
- up_weight: bfloat16 [960, 2560], P('fsdp'), may hold values from -0.1875 to 0.1875
- down_weight: bfloat16 [2560, 960], P('fsdp'), may hold values from -0.125 to 0.125
- norm_gains: float32 [2, 960], replicated, may hold values from 0.5 to 1.5
- query_momentum: float32 [960, 960], P('fsdp'), may hold values from -160 to 160
- key_momentum: float32 [960, 320], P('fsdp'), may hold values from -384 to 384
- value_momentum: float32 [960, 320], P('fsdp'), may hold values from -384 to 384
- output_momentum: float32 [960, 960], P('fsdp'), may hold values from -40 to 40
- gate_momentum: float32 [960, 2560], P('fsdp'), may hold values from -80 to 80
- up_momentum: float32 [960, 2560], P('fsdp'), may hold values from -80 to 80
- down_momentum: float32 [2560, 960], P('fsdp'), may hold values from -80 to 80
- gain_momentum: float32 [2, 960], P(None, 'fsdp'), may hold values from -1024 to 1024
- block_order: int32 [16], replicated, may hold values from 0 to 15, each once
Outputs:
- layer_output: bfloat16 [4, 1024, 960], P('fsdp', 'ctx')
- input_gradient: float32 [4, 1024, 960], P('fsdp', 'ctx')
- query_gradient: float32 [960, 960], P('fsdp')
- key_gradient: float32 [960, 320], P('fsdp')
- value_gradient: float32 [960, 320], P('fsdp')
- output_gradient: float32 [960, 960], P('fsdp')
- gate_gradient: float32 [960, 2560], P('fsdp')
- up_gradient: float32 [960, 2560], P('fsdp')
- down_gradient: float32 [2560, 960], P('fsdp')
- gain_gradient: float32 [2, 960], P(None, 'fsdp')
- new_query_momentum: float32 [960, 960], P('fsdp')
- new_key_momentum: float32 [960, 320], P('fsdp')
- new_value_momentum: float32 [960, 320], P('fsdp')
- new_output_momentum: float32 [960, 960], P('fsdp')
- new_gate_momentum: float32 [960, 2560], P('fsdp')
- new_up_momentum: float32 [960, 2560], P('fsdp')
- new_down_momentum: float32 [2560, 960], P('fsdp')
- new_gain_momentum: float32 [2, 960], P(None, 'fsdp')
- new_query_weight: float32 [960, 960], P('fsdp')
- new_key_weight: float32 [960, 320], P('fsdp')
- new_value_weight: float32 [960, 320], P('fsdp')
- new_output_weight: float32 [960, 960], P('fsdp')
- new_gate_weight: float32 [960, 2560], P('fsdp')
- new_up_weight: float32 [960, 2560], P('fsdp')
- new_down_weight: float32 [2560, 960], P('fsdp')
- new_norm_gains: float32 [2, 960], P(None, 'fsdp')
The draws below stay inside these ranges and needn't reach their ends.
Inputs may be any that keep to these rules, and one draw needn't show every extreme that they name: `block_order`: every block of a sequence stands in exactly one slot.
All inputs are finite; a program needn't handle non-finite values.
Results may differ from the reference program's by a relative error of at most 0.017.
Values may be sent and summed in bfloat16 or wider, within the bound.
A program may use at most 448 MiB of HBM per device.

```python
import math
import jax
import jax.numpy as jnp
from jax import lax

D = 960
HEADS = 15
KV_HEADS = 5
HEAD = 64
FF = 2560
BLK = 64
NS_ITERS = 5
SEQS = 4
SEQ_LEN = 1024


def draw_layer_input(key, part):
    first, second, third = jax.random.split(key, 3)
    base = jnp.clip(jax.random.normal(first, (SEQS, SEQ_LEN, D), jnp.float32), -3.0, 3.0)
    row_scale = jnp.exp(jax.random.uniform(second, (SEQS, SEQ_LEN, 1), jnp.float32, 0.0, math.log(10.0)))
    column_scale = jnp.exp(jax.random.uniform(third, (1, 1, D), jnp.float32, math.log(0.5), math.log(2.0)))
    return (base * row_scale * column_scale).astype(jnp.bfloat16)


def levels(key, dims, pieces, low, high):
    loudness, own = 1.0, jax.random.fold_in(key, 6)
    for axis_at, parts in pieces:
        draws = jnp.exp(jax.random.uniform(jax.random.fold_in(own, axis_at), (parts,), jnp.float32, low / len(pieces), high / len(pieces)))
        loudness = loudness * jnp.repeat(draws, dims[axis_at] // parts).reshape([-1 if axis == axis_at else 1 for axis in range(len(dims))])
    return loudness


def normal_values(key, shape, width, bound, pieces=(), kind=jnp.bfloat16):
    array = width * jax.random.normal(key, shape, jnp.float32)
    if pieces:
        array = array * levels(key, shape, pieces, -0.22, 0.18)
    return jnp.clip(array, -bound, bound).astype(kind)


def setup_inputs(seed: int = 0) -> dict:
    arg_keys = jax.random.split(jax.random.key(seed), 20)
    layer_input = draw_layer_input(jax.random.fold_in(arg_keys[19], 71), 0)
    output_grad = normal_values(arg_keys[1], (SEQS, SEQ_LEN, D), 1.0, 6.0, ((0, 4), (1, 8)))
    query_weight = normal_values(arg_keys[2], (D, D), D ** -0.5, 0.1875, ((0, 4),))
    key_weight = normal_values(arg_keys[3], (D, KV_HEADS * HEAD), D ** -0.5, 0.1875, ((0, 4),))
    value_weight = normal_values(arg_keys[4], (D, KV_HEADS * HEAD), D ** -0.5, 0.1875, ((0, 4),))
    output_weight = normal_values(arg_keys[5], (D, D), 1.0, 6.0, ((0, 4),))
    gate_weight = normal_values(arg_keys[6], (D, FF), D ** -0.5, 0.1875, ((0, 4),))
    up_weight = normal_values(arg_keys[7], (D, FF), D ** -0.5, 0.1875, ((0, 4),))
    down_weight = normal_values(arg_keys[8], (FF, D), FF ** -0.5, 0.125, ((0, 4),))
    norm_gains = jnp.clip(1.0 + 0.1 * jax.random.normal(arg_keys[9], (2, D), jnp.float32), 0.5, 1.5)
    query_momentum = normal_values(arg_keys[10], (D, D), (0.4 * (SEQS * SEQ_LEN) ** 0.5), 160.0, ((0, 4),), jnp.float32)
    key_momentum = normal_values(arg_keys[11], (D, KV_HEADS * HEAD), (1.0 * (SEQS * SEQ_LEN) ** 0.5), 384.0, ((0, 4),), jnp.float32)
    value_momentum = normal_values(arg_keys[12], (D, KV_HEADS * HEAD), (1.0 * (SEQS * SEQ_LEN) ** 0.5), 384.0, ((0, 4),), jnp.float32)
    output_momentum = normal_values(arg_keys[13], (D, D), (0.1 * (SEQS * SEQ_LEN) ** 0.5), 40.0, ((0, 4),), jnp.float32)
    gate_momentum = normal_values(arg_keys[14], (D, FF), (0.2 * (SEQS * SEQ_LEN) ** 0.5), 80.0, ((0, 4),), jnp.float32)
    up_momentum = normal_values(arg_keys[15], (D, FF), (0.2 * (SEQS * SEQ_LEN) ** 0.5), 80.0, ((0, 4),), jnp.float32)
    down_momentum = normal_values(arg_keys[16], (FF, D), (0.2 * (SEQS * SEQ_LEN) ** 0.5), 80.0, ((0, 4),), jnp.float32)
    gain_momentum = normal_values(arg_keys[17], (2, D), (2.5 * (SEQS * SEQ_LEN) ** 0.5), 1024.0, ((1, 4),), jnp.float32)
    block_order = jax.random.permutation(arg_keys[18], SEQ_LEN // BLK).astype(jnp.int32)
    return {"layer_input": layer_input, "output_grad": output_grad, "query_weight": query_weight, "key_weight": key_weight, "value_weight": value_weight, "output_weight": output_weight, "gate_weight": gate_weight, "up_weight": up_weight, "down_weight": down_weight, "norm_gains": norm_gains, "query_momentum": query_momentum, "key_momentum": key_momentum, "value_momentum": value_momentum, "output_momentum": output_momentum, "gate_momentum": gate_momentum, "up_momentum": up_momentum, "down_momentum": down_momentum, "gain_momentum": gain_momentum, "block_order": block_order}


EPS = 1e-05
THETA = 100000.0
NS_A = 3.4445
NS_B = -4.775
NS_C = 2.0315
MOMENTUM = 0.95
RATE = 0.2
OUT_RATE = 6.0
GAIN_RATE = 0.002
MASKED = -1e+30
HIGH = lax.Precision.HIGHEST

@jax.custom_vjp
def low(v):
    return lax.optimization_barrier(v.astype(jnp.bfloat16)).astype(jnp.float32)

@jax.custom_vjp
def low_back(v):
    return v

def low_keep(v):
    return (low(v), None)

def low_pass(kept, grad):
    return (grad,)

def back_keep(v):
    return (v, None)

def back_low(kept, grad):
    return (low(grad),)
low.defvjp(low_keep, low_pass)
low_back.defvjp(back_keep, back_low)

def product(left, right):
    return jnp.dot(left, right, precision=HIGH, preferred_element_type=jnp.float32)

def rms_scale(value, gain):
    return value * lax.rsqrt(lax.optimization_barrier(jnp.mean(value * value, axis=-1, keepdims=True)) + EPS) * gain

def rotary(value, positions):
    half = value.shape[-1] // 2
    frequency = THETA ** (-(jnp.arange(half, dtype=jnp.float32) * 2.0 / value.shape[-1]))
    angle = positions.astype(jnp.float32)[:, None] * frequency[None, :]
    cosine = jnp.cos(angle)[:, None, :]
    sine = jnp.sin(angle)[:, None, :]
    first = value[..., :half]
    second = value[..., half:]
    return jnp.concatenate([first * cosine - second * sine, second * cosine + first * sine], axis=-1)

def attend(query_block, query_pos, keys, values, key_pos):
    scores = jnp.einsum('qgrd,kgd->grqk', query_block, keys, precision=HIGH) * (1.0 / math.sqrt(HEAD))
    scores = low_back(scores)
    allowed = key_pos[None, :] <= query_pos[:, None]
    scores = jnp.where(allowed[None, None], scores, MASKED)
    weights = low(jax.nn.softmax(scores, axis=-1))
    mixed = jnp.einsum('grqk,kgd->qgrd', weights, values, precision=HIGH)
    return mixed.reshape(query_block.shape[0], HEADS * HEAD)

def layer(residual, positions, w_query, w_key, w_value, w_output, w_gate, w_up, w_down, gains):
    length = residual.shape[0]
    group = HEADS // KV_HEADS
    normed_first = low(rms_scale(residual, gains[0]))
    query_pre = low_back(product(normed_first, w_query)).reshape(length, HEADS, HEAD)
    key_pre = low_back(product(normed_first, w_key)).reshape(length, KV_HEADS, HEAD)
    values = low(low_back(product(normed_first, w_value))).reshape(length, KV_HEADS, HEAD)
    queries = low(rotary(query_pre, positions)).reshape(length, KV_HEADS, group, HEAD)
    keys = low(rotary(key_pre, positions))
    rows_block = min(512, length)
    count = length // rows_block
    checked = jax.checkpoint(attend)

    def one_block(item):
        return checked(item[0], item[1], keys, values, positions)
    mixed = lax.map(one_block, (queries.reshape(count, rows_block, KV_HEADS, group, HEAD), positions.reshape(count, rows_block)))
    attended = low(low_back(mixed.reshape(length, HEADS * HEAD)))
    middle = residual + low_back(product(attended, w_output))
    normed_second = low(rms_scale(middle, gains[1]))
    gate = low_back(product(normed_second, w_gate))
    lifted = low_back(product(normed_second, w_up))
    hidden = low(jax.nn.silu(gate) * lifted)
    return middle + product(hidden, w_down)

def orthogonal(matrix):
    flip = matrix.shape[0] > matrix.shape[1]
    start = lax.optimization_barrier(matrix.astype(jnp.bfloat16))
    if flip:
        start = start.T
    wide = start.astype(jnp.float32)
    scale = jnp.sqrt(jnp.sum(wide * wide))
    current = (wide / (scale + 1e-07)).astype(jnp.bfloat16)
    for count in range(NS_ITERS):
        gram = lax.optimization_barrier(jnp.dot(current, current.T, preferred_element_type=jnp.float32).astype(jnp.bfloat16))
        poly = (NS_B * gram.astype(jnp.float32) + NS_C * jnp.dot(gram, gram, preferred_element_type=jnp.float32)).astype(jnp.bfloat16)
        current = lax.optimization_barrier(current)
        current = (NS_A * current.astype(jnp.float32) + jnp.dot(poly, current, preferred_element_type=jnp.float32)).astype(jnp.bfloat16)
    if flip:
        current = current.T
    return current

def muon_step(weight, moment, rate):
    factor = -rate * max(1.0, moment.shape[1] / moment.shape[0]) ** 0.5
    return weight.astype(jnp.float32) + factor * orthogonal(moment).astype(jnp.float32)

def reference(layer_input, output_grad, query_weight, key_weight, value_weight, output_weight, gate_weight, up_weight, down_weight, norm_gains, query_momentum, key_momentum, value_momentum, output_momentum, gate_momentum, up_momentum, down_momentum, gain_momentum, block_order):
    offsets = jnp.arange(BLK, dtype=jnp.int32)
    positions = (block_order[:, None].astype(jnp.int32) * BLK + offsets[None, :]).reshape(-1).astype(jnp.int32)
    params = (query_weight.astype(jnp.float32), key_weight.astype(jnp.float32), value_weight.astype(jnp.float32), output_weight.astype(jnp.float32), gate_weight.astype(jnp.float32), up_weight.astype(jnp.float32), down_weight.astype(jnp.float32), norm_gains.astype(jnp.float32))

    def one_sequence(totals, item):
        tokens, upstream = item

        def apply(value, *weights):
            return layer(value, positions, *weights)
        result, pull = jax.vjp(apply, tokens.astype(jnp.float32), *params)
        grads = pull(upstream.astype(jnp.float32))
        totals = tuple((acc + new for acc, new in zip(totals, grads[1:])))
        return (totals, (result.astype(jnp.bfloat16), grads[0]))
    zeros = tuple((jnp.zeros_like(param) for param in params))
    totals, outputs = lax.scan(one_sequence, zeros, (layer_input, output_grad))
    layer_output, input_gradient = outputs
    new_query = MOMENTUM * query_momentum + totals[0]
    new_key = MOMENTUM * key_momentum + totals[1]
    new_value = MOMENTUM * value_momentum + totals[2]
    new_output = MOMENTUM * output_momentum + totals[3]
    new_gate = MOMENTUM * gate_momentum + totals[4]
    new_up = MOMENTUM * up_momentum + totals[5]
    new_down = MOMENTUM * down_momentum + totals[6]
    new_gain = MOMENTUM * gain_momentum + totals[7]
    return (layer_output, input_gradient, totals[0], totals[1], totals[2], totals[3], totals[4], totals[5], totals[6], totals[7], new_query, new_key, new_value, new_output, new_gate, new_up, new_down, new_gain, muon_step(query_weight, new_query, RATE), muon_step(key_weight, new_key, RATE), muon_step(value_weight, new_value, RATE), muon_step(output_weight, new_output, OUT_RATE), muon_step(gate_weight, new_gate, RATE), muon_step(up_weight, new_up, RATE), muon_step(down_weight, new_down, RATE), norm_gains - GAIN_RATE * new_gain)
```

```python
import functools
import math

import jax
import jax.numpy as jnp
from jax import lax
from jax.experimental import pallas as pl
from jax.experimental.pallas import tpu as pltpu
from jax.sharding import PartitionSpec as P

HEADS = 15
KV_HEADS = 5
HEAD = 64
NS_ITERS = 5


EPS = 1e-05
THETA = 100000.0
NS_A = 3.4445
NS_B = -4.775
NS_C = 2.0315
MOMENTUM = 0.95
RATE = 0.2
OUT_RATE = 6.0
GAIN_RATE = 0.002
MASKED = -1e30

MESH = pl.DeviceIdType.MESH
BF16 = jnp.bfloat16
F32 = jnp.float32
ANY = pl.BlockSpec(memory_space=pl.ANY)
VMEM = pl.BlockSpec(memory_space=pltpu.VMEM)
CLASSES = 8
WIDE = 6


def contract(left, right, left_dim, right_dim):
    return lax.dot_general(
        left, right, (((left_dim,), (right_dim,)), ((), ())), preferred_element_type=jnp.float32
    )


class Place:
    def __init__(self):
        self.parts = lax.axis_size("fsdp")
        self.extra = lax.axis_size("ctx") // CLASSES
        self.c = lax.axis_index("ctx")
        self.f = lax.axis_index("fsdp")
        self.p = lax.rem(self.c, CLASSES)
        self.core = lax.rem(self.c, 2)
        self.b1 = jnp.where(self.core == 0, 2, 4)
        self.b2 = jnp.where(self.core == 0, 4, 2)

    def peer(self, bits):
        return (self.c ^ bits, self.f)

    def along(self, j):
        return (self.c, self.f ^ j)

    def other(self, j):
        groups = self.extra
        return (lax.rem(self.c + CLASSES * j, CLASSES * groups), self.f)

    def barrier(self, bits=(1, 2, 4), line=True, others=False):
        sem = pltpu.get_barrier_semaphore()
        targets = [self.peer(b) for b in bits]
        if line:
            targets += [self.along(j) for j in range(1, self.parts)]
        if others:
            targets += [self.other(j) for j in range(1, self.extra)]
        for target in targets:
            pl.semaphore_signal(sem, inc=1, device_id=target, device_id_type=MESH)
        pl.semaphore_wait(sem, len(targets))


def remote(src, dst, send, recv, target):
    return pltpu.make_async_remote_copy(
        src_ref=src, dst_ref=dst, send_sem=send, recv_sem=recv, device_id=target, device_id_type=MESH
    )


def by_kind(cls, wide, tall):
    pl.when(cls < WIDE)(wide)
    pl.when(cls >= WIDE)(tall)


def weights_kernel(in_a, in_b, out_a, out_b, local, zs, s1, s2, sc, recv):
    at = Place()
    p, f, parts = at.p, at.f, at.parts
    at.barrier()
    copies = [
        pltpu.make_async_copy(in_a, out_a.at[:, f], local.at[0]),
        pltpu.make_async_copy(in_b, out_b.at[:, f], local.at[1]),
    ]
    for copy in copies:
        copy.start()

    def act(cls, j, g, send, target, what, first=False):
        def wide():
            dst = out_a.at[cls, g]
            src = in_a.at[cls] if first else dst
            getattr(remote(src, dst, send, recv.at[cls, j], target), what)()

        def tall():
            dst = out_b.at[cls - WIDE, g]
            src = in_b.at[cls - WIDE] if first else dst
            getattr(remote(src, dst, send, recv.at[cls, j], target), what)()

        by_kind(cls, wide, tall)

    sends = []

    def send(cls, j, g, sem, target, first=False):
        act(cls, j, g, sem, target, "start", first)
        sends.append((cls, j, g, sem, target, first))

    def arrived(cls, j):
        act(cls, j, f ^ j, zs.at[j], at.along(j), "wait_recv")

    for j in range(1, parts):
        send(p, j, f, zs.at[j], at.along(j), True)
    for j in range(1, parts):
        arrived(p, j)
        send(p, j, f ^ j, s1.at[0, j], at.peer(at.b1))
        send(p, j, f ^ j, s2.at[0, j], at.peer(at.b2))
        send(p, j, f ^ j, sc.at[0, j], at.peer(1))
    for j in range(1, parts):
        arrived(p ^ at.b1, j)
        send(p ^ at.b1, j, f ^ j, s2.at[1, j], at.peer(at.b2))
        send(p ^ at.b1, j, f ^ j, sc.at[1, j], at.peer(1))
    for slot, bits in ((2, at.b2), (3, at.b1 ^ at.b2)):
        for j in range(1, parts):
            arrived(p ^ bits, j)
            send(p ^ bits, j, f ^ j, sc.at[slot, j], at.peer(1))
    for bits in (1, 3, 5, 7):
        for j in range(1, parts):
            arrived(p ^ bits, j)
    for cls, j, g, sem, target, first in sends:
        act(cls, j, g, sem, target, "wait_send", first)
    for copy in copies:
        copy.wait()


def gather_weights(wide, tall):
    parts = lax.axis_size("fsdp")
    dma = pltpu.SemaphoreType.DMA
    return pl.pallas_call(
        weights_kernel,
        out_shape=(
            jax.ShapeDtypeStruct((WIDE, parts) + wide.shape[1:], BF16),
            jax.ShapeDtypeStruct((CLASSES - WIDE, parts) + tall.shape[1:], BF16),
        ),
        in_specs=[ANY, ANY],
        out_specs=(ANY, ANY),
        scratch_shapes=[
            dma((2,)),
            dma((parts,)),
            dma((1, parts)),
            dma((2, parts)),
            dma((4, parts)),
            dma((CLASSES, parts)),
        ],
        compiler_params=pltpu.CompilerParams(collective_id=0, has_side_effects=True),
        name="gather_weights",
    )(wide, tall)


def spread(at, own_a, own_b, out_a, out_b, local, ss, recv):
    p = at.p

    def act(cls, sem, target, what, first=False):
        def wide():
            dst = out_a.at[cls]
            getattr(remote(own_a if first else dst, dst, sem, recv.at[cls], target), what)()

        def tall():
            dst = out_b.at[cls - WIDE]
            getattr(remote(own_b if first else dst, dst, sem, recv.at[cls], target), what)()

        by_kind(cls, wide, tall)

    def keep(what):
        def wide():
            getattr(pltpu.make_async_copy(own_a, out_a.at[p], local), what)()

        def tall():
            getattr(pltpu.make_async_copy(own_b, out_b.at[p - WIDE], local), what)()

        by_kind(p, wide, tall)

    sends = []

    def send(cls, slot, target, first=False):
        act(cls, ss.at[slot], target, "start", first)
        sends.append((cls, slot, target, first))

    def arrived(cls):
        act(cls, ss.at[0], at.peer(1), "wait_recv")

    send(p, 0, at.peer(at.b1), True)
    send(p, 1, at.peer(at.b2), True)
    send(p, 2, at.peer(1), True)
    keep("start")

    def finish():
        arrived(p ^ at.b1)
        send(p ^ at.b1, 3, at.peer(at.b2))
        send(p ^ at.b1, 4, at.peer(1))
        arrived(p ^ at.b2)
        send(p ^ at.b2, 5, at.peer(1))
        arrived(p ^ at.b1 ^ at.b2)
        send(p ^ at.b1 ^ at.b2, 6, at.peer(1))
        for bits in (1, 3, 5, 7):
            arrived(p ^ bits)
        for cls, slot, target, first in sends:
            act(cls, ss.at[slot], target, "wait_send", first)
        keep("wait")

    return finish


def reduce_kernel(
    parts, extra, high,
    xt_in, dy_in, gain_in, m_qk, m_ov, m_gate, m_up, m_down,
    g_a, g_b, s_a, s_b, gain_out,
    xt, dy, p1s, p1r, p2s, p2r, own, own_t, za_s, za_r, zb_s, zb_r, ma, mb, ga, gb, sa, sb, es, er, gain_s, gain_r,
    ls, xs, xr, s1, r1, s2, r2, zs, zr, esem, ersem, msem, gs, gr, ag_l, ag_s, ag_r, ss, sr, sl,
):
    at = Place()
    p, f, core = at.p, at.f, at.core
    tokens = xt_in.shape[2]
    rows = ma.shape[0]
    half = dy.shape[2]

    def moment(what):
        for cls in range(CLASSES):
            @pl.when(p == cls)
            def _(cls=cls):
                side = cls % 2
                if cls < 2:
                    src, dst = (m_qk, m_ov)[cls], ma
                elif cls < WIDE:
                    whole = m_gate if cls < 4 else m_up
                    src, dst = whole.at[:, pl.ds(side * half, half)], ma
                else:
                    src, dst = m_down.at[pl.ds(side * high, high)], mb
                getattr(pltpu.make_async_copy(src, dst, msem), what)()

    moment("start")
    mine = [pltpu.make_async_copy(xt_in, xt.at[:, :, pl.ds(0, tokens)], ls.at[0])]
    for slot in range(4):
        mine.append(
            pltpu.make_async_copy(dy_in.at[core + 2 * slot], dy.at[slot, pl.ds(0, tokens)], ls.at[1 + slot])
        )
    mine.append(pltpu.make_async_copy(dy_in.at[8], dy.at[4, pl.ds(0, tokens)], ls.at[5]))
    for copy in mine:
        copy.start()
    at.barrier(others=True)
    pair = at.peer(1)
    theirs = [remote(xt_in, xt.at[:, :, pl.ds(tokens, tokens)], xs.at[0], xr.at[0], pair)]
    for slot in range(4):
        theirs.append(
            remote(dy_in.at[1 - core + 2 * slot], dy.at[slot, pl.ds(tokens, tokens)], xs.at[1 + slot], xr.at[1 + slot], pair)
        )
    theirs.append(remote(dy_in.at[8], dy.at[4, pl.ds(tokens, tokens)], xs.at[5], xr.at[5], pair))
    for copy in theirs:
        copy.start()

    def swap(slot, target):
        return remote(gain_s.at[slot], gain_r.at[slot], gs.at[slot], gr.at[slot], target)

    gain_s[0] = gain_in[...]
    swaps = [swap(0, pair)]
    swaps[0].start()
    for copy in mine:
        copy.wait()
    for copy in theirs:
        copy.wait()

    def term(cls, r):
        at_rows = pl.ds(pl.multiple_of(r * rows, rows), rows)
        slot = lax.div(cls, 2)
        kind = jnp.where(cls == 0, 0, jnp.where(cls == 1, 1, jnp.where(cls < WIDE, 2, 3)))
        value = jnp.dot(xt[kind, at_rows, :], dy[slot], preferred_element_type=F32)
        return value

    def with_values(cls, r, put):
        at_rows = pl.ds(pl.multiple_of(r * rows, rows), rows)

        @pl.when(cls == 1)
        def _():
            put(term(cls, r) + jnp.dot(xt[0, at_rows, :], dy[4], preferred_element_type=F32))

        @pl.when(cls != 1)
        def _():
            put(term(cls, r))

    def order(i):
        return lax.rem(f + 1 + i, parts)

    def one(slot, i):
        r = order(i)
        return remote(p1s.at[slot, r], p1r.at[slot, r], s1.at[slot, r], r1.at[slot, r], at.peer(at.b1))

    for slot, bits in ((0, at.b1 ^ at.b2), (1, at.b1)):
        def first(i, carry, slot=slot, bits=bits):
            r = order(i)

            def put(value):
                p1s[slot, r] = value.astype(BF16)

            with_values(p ^ bits, r, put)
            one(slot, i).start()
            return carry

        lax.fori_loop(0, parts, first, 0)

    swaps[0].wait()
    gain_s[1] = gain_s[0] + gain_r[0]
    swaps.append(swap(1, at.peer(2)))
    swaps[1].start()

    def two(i):
        r = order(i)
        return remote(p2s.at[r], p2r.at[r], s2.at[r], r2.at[r], at.peer(at.b2))

    def second(i, carry):
        r = order(i)
        one(0, i).wait_recv()

        def put(value):
            p2s[r] = (value + p1r[0, r].astype(F32)).astype(BF16)

        with_values(p ^ at.b2, r, put)
        two(i).start()
        return carry

    lax.fori_loop(0, parts, second, 0)
    swaps[1].wait()
    gain_s[2] = gain_s[1] + gain_r[1]
    swaps.append(swap(2, at.peer(4)))
    swaps[2].start()

    def line_a(r, source):
        return remote(za_s.at[r], za_r.at[source], zs.at[r], zr.at[source], (at.c, r))

    def line_b(r, source):
        return remote(
            zb_s.at[pl.ds(pl.multiple_of(r * high, high), high)],
            zb_r.at[source], zs.at[r], zr.at[source], (at.c, r),
        )

    early = extra == 1

    def third(i, carry):
        r = order(i)
        one(1, i).wait_recv()
        two(i).wait_recv()

        def put(value):
            total = value + p1r[1, r].astype(F32) + p2r[r].astype(F32)
            own[r] = total
            if early:
                za_s[r] = total.astype(BF16)

        with_values(p, r, put)
        if early:
            @pl.when((p < WIDE) & (i < parts - 1))
            def _():
                line_a(r, f).start()
        return carry

    lax.fori_loop(0, parts, third, 0)
    swaps[2].wait()
    gain_s[3] = gain_s[2] + gain_r[2]

    if not early:
        es[...] = own[...].astype(BF16)
        group = [
            remote(es, er.at[j - 1], esem.at[j - 1], ersem.at[j - 1], at.other(j)) for j in range(1, extra)
        ]
        for copy in group:
            copy.start()
        for j in range(1, extra):
            group[j - 1].wait_recv()
            own[...] = own[...] + er[j - 1].astype(F32)
        for copy in group:
            copy.wait_send()
        za_s[...] = own[...].astype(BF16)

        @pl.when(p < WIDE)
        def _():
            for j in range(1, parts):
                line_a(f ^ j, f).start()

    @pl.when(p >= WIDE)
    def _():
        for tile in range(half // 128):
            for r in range(parts):
                block = own[r, :, pl.ds(tile * 128, 128)]
                if rows % 128 == 0:
                    own_t[pl.ds(tile * 128, 128), pl.ds(r * rows, rows)] = block.T
            if rows % 128 != 0:
                column = own[:, :, pl.ds(tile * 128, 128)].reshape(parts * rows, 128)
                own_t[pl.ds(tile * 128, 128), :] = column.T
        zb_s[...] = own_t[...].astype(BF16)
        for j in range(1, parts):
            line_b(f ^ j, f).start()

    line_gain = [
        remote(gain_s.at[3], gain_r.at[3 + j], gs.at[3 + j], gr.at[3 + j], at.along(j)) for j in range(1, parts)
    ]
    other_gain = []
    for copy in line_gain:
        copy.start()

    moment("wait")

    @pl.when(p < WIDE)
    def _():
        total = own[f]
        for j in range(1, parts):
            line_a(f ^ j, f ^ j).wait_recv()
            total = total + za_r[f ^ j].astype(F32)
        ga[...] = total.astype(BF16)
        sa[...] = (MOMENTUM * ma[...] + total).astype(BF16)

    @pl.when(p >= WIDE)
    def _():
        total = own_t[pl.ds(pl.multiple_of(f * high, high), high), :]
        for j in range(1, parts):
            line_b(f ^ j, f ^ j).wait_recv()
            total = total + zb_r[f ^ j].astype(F32)
        gb[...] = total.astype(BF16)
        sb[...] = (MOMENTUM * mb[...] + total).astype(BF16)

    def share_a(j, source):
        return remote(sa, s_a.at[pl.ds(pl.multiple_of(source * rows, rows), rows)], ss.at[j], sr.at[j], at.along(j))

    def share_b(j, source):
        return remote(sb, s_b.at[pl.ds(pl.multiple_of(source * high, high), high)], ss.at[j], sr.at[j], at.along(j))

    @pl.when(p < WIDE)
    def _():
        for j in range(1, parts):
            share_a(j, f).start()
        pltpu.make_async_copy(sa, s_a.at[pl.ds(pl.multiple_of(f * rows, rows), rows)], sl).start()

    @pl.when(p >= WIDE)
    def _():
        for j in range(1, parts):
            share_b(j, f).start()
        pltpu.make_async_copy(sb, s_b.at[pl.ds(pl.multiple_of(f * high, high), high)], sl).start()

    finish = spread(at, ga, gb, g_a, g_b, ag_l, ag_s, ag_r)
    total = gain_s[3]
    for j in range(1, parts):
        line_gain[j - 1].wait()
        total = total + gain_r[3 + j]
    if extra > 1:
        gain_s[4] = total
        other_gain = [
            remote(gain_s.at[4], gain_r.at[3 + parts + j], gs.at[3 + parts + j], gr.at[3 + parts + j], at.other(j))
            for j in range(1, extra)
        ]
        for copy in other_gain:
            copy.start()
        for j in range(1, extra):
            other_gain[j - 1].wait()
            total = total + gain_r[3 + parts + j]
    gain_out[...] = total
    finish()

    for slot in range(2):
        lax.fori_loop(0, parts, lambda i, carry, slot=slot: (one(slot, i).wait_send(), carry)[1], 0)
    lax.fori_loop(0, parts, lambda i, carry: (two(i).wait_send(), carry)[1], 0)

    @pl.when(p < WIDE)
    def _():
        for j in range(1, parts):
            line_a(f ^ j, f).wait_send()
            share_a(j, f).wait_send()
            share_a(j, f ^ j).wait_recv()
        pltpu.make_async_copy(sa, s_a.at[pl.ds(pl.multiple_of(f * rows, rows), rows)], sl).wait()

    @pl.when(p >= WIDE)
    def _():
        for j in range(1, parts):
            line_b(f ^ j, f).wait_send()
            share_b(j, f).wait_send()
            share_b(j, f ^ j).wait_recv()
        pltpu.make_async_copy(sb, s_b.at[pl.ds(pl.multiple_of(f * high, high), high)], sl).wait()


def reduce_gradients(xt, dy, gains, moments, rows, high):
    parts = lax.axis_size("fsdp")
    extra = lax.axis_size("ctx") // CLASSES
    kinds, depth, tokens = xt.shape
    half = dy.shape[2]
    dma = pltpu.SemaphoreType.DMA
    vm = pltpu.VMEM
    n_gain = 4 + parts + extra
    group = max(extra - 1, 1)
    spare = (parts, rows, half) if extra > 1 else (1, 16, 128)
    return pl.pallas_call(
        functools.partial(reduce_kernel, parts, extra, high),
        out_shape=(
            jax.ShapeDtypeStruct((WIDE, rows, half), BF16),
            jax.ShapeDtypeStruct((CLASSES - WIDE, high, depth), BF16),
            jax.ShapeDtypeStruct((depth, half), BF16),
            jax.ShapeDtypeStruct((half, depth), BF16),
            jax.ShapeDtypeStruct(gains.shape, F32),
        ),
        in_specs=[ANY, ANY, VMEM] + [ANY] * 5,
        out_specs=(ANY, ANY, ANY, ANY, VMEM),
        scratch_shapes=[
            vm((kinds, depth, 2 * tokens), BF16),
            vm((5, 2 * tokens, half), BF16),
            vm((2, parts, rows, half), BF16),
            vm((2, parts, rows, half), BF16),
            vm((parts, rows, half), BF16),
            vm((parts, rows, half), BF16),
            vm((parts, rows, half), F32),
            vm((half, depth), F32),
            vm((parts, rows, half), BF16),
            vm((parts, rows, half), BF16),
            vm((half, depth), BF16),
            vm((parts, high, depth), BF16),
            vm((rows, half), F32),
            vm((high, depth), F32),
            vm((rows, half), BF16),
            vm((high, depth), BF16),
            vm((rows, half), BF16),
            vm((high, depth), BF16),
            vm(spare, BF16),
            vm((group,) + spare, BF16),
            vm((5,) + gains.shape, F32),
            vm((n_gain,) + gains.shape, F32),
            dma((6,)), dma((6,)), dma((6,)),
            dma((2, parts)), dma((2, parts)), dma((parts,)), dma((parts,)), dma((parts,)), dma((parts,)),
            dma((group,)), dma((group,)), dma, dma((n_gain,)), dma((n_gain,)),
            dma, dma((7,)), dma((CLASSES,)), dma((parts,)), dma((parts,)), dma,
        ],
        compiler_params=pltpu.CompilerParams(
            collective_id=1, has_side_effects=True, vmem_limit_bytes=62 << 20
        ),
        name="reduce_gradients",
    )(xt, dy, gains, *moments)


def rounded(value):
    return value.astype(BF16)


def poly_rows(g, row_start, count):
    block = g[pl.ds(row_start, count), :]
    return rounded(NS_B * block.astype(F32) + NS_C * jnp.dot(block, g[...], preferred_element_type=F32))


def ortho_kernel(
    parts, rows, high, narrow,
    s_a, s_b, o_a, o_b,
    x, x_t, gs, gr, g, poly, sq, sq_r, pa, pb, kt,
    gsem, rsem, qs, qr, ag_l, ag_s, ag_r,
):
    at = Place()
    p, f = at.p, at.f
    depth, half = x.shape
    step = depth // 4
    at.barrier(line=False)
    pair = at.peer(1)

    @pl.when(p < WIDE)
    def _():
        x[...] = s_a[...]

    @pl.when(p >= WIDE)
    def _():
        for tile in range(half // 128):
            x[:, pl.ds(tile * 128, 128)] = s_b[pl.ds(tile * 128, 128), :].T

    def scale_of(total):
        return 1.0 / (jnp.sqrt(total) + 1e-07)

    def normal(ref, inverse):
        ref[...] = rounded(ref[...].astype(F32) * inverse)

    def exchange(slot, r):
        chunk = pl.ds(r * step, step)
        return remote(gs.at[chunk], gr.at[slot, chunk], gsem.at[r], rsem.at[slot, r], pair)

    def fill_poly():
        for r in range(4):
            poly[pl.ds(r * step, step), :] = poly_rows(g, r * step, step)

    my_rows = pl.ds(pl.multiple_of(f * rows, rows), rows)
    my_high = pl.ds(pl.multiple_of(f * high, high), high)

    @pl.when(p >= 2)
    def _():
        wide = x[...].astype(F32)
        sq[...] = jnp.broadcast_to(jnp.sum(wide * wide), sq.shape)
        copy = remote(sq, sq_r, qs, qr, pair)
        copy.start()
        copy.wait()
        normal(x, scale_of(sq[...] + sq_r[...])[:1, :1])

        def grams(slot):
            for r in range(4):
                gs[pl.ds(r * step, step), :] = rounded(contract(x[pl.ds(r * step, step), :], x[...], 1, 1))
                exchange(slot, r).start()
            for r in range(4):
                chunk = pl.ds(r * step, step)
                exchange(slot, r).wait()
                g[chunk, :] = rounded(gs[chunk, :].astype(F32) + gr[slot, chunk, :].astype(F32))

        def iterate(it, carry):
            grams(lax.rem(it, 2))
            fill_poly()
            for tile in range(half // 256):
                block = pl.ds(tile * 256, 256)
                x[:, block] = rounded(
                    NS_A * x[:, block].astype(F32) + jnp.dot(poly[...], x[:, block], preferred_element_type=F32)
                )
            return carry

        lax.fori_loop(0, NS_ITERS - 1, iterate, 0)
        grams((NS_ITERS - 1) % 2)

        @pl.when(p < WIDE)
        def _():
            mine = poly_rows(g, pl.multiple_of(f * rows, rows), rows)
            pa[...] = rounded(NS_A * x[my_rows, :].astype(F32) + jnp.dot(mine, x[...], preferred_element_type=F32))

        @pl.when(p >= WIDE)
        def _():
            fill_poly()
            for tile in range(half // 128):
                x_t[pl.ds(tile * 128, 128), :] = x[:, pl.ds(tile * 128, 128)].T
            block = x_t[my_high, :]
            pb[...] = rounded(NS_A * block.astype(F32) + jnp.dot(block, poly[...], preferred_element_type=F32))

    @pl.when(p < 2)
    def _():
        kt[...] = x[:, narrow:].T
        inverse_k = scale_of(jnp.sum(jnp.square(kt[...].astype(F32))))
        normal(kt, inverse_k)
        wide = x[:, :narrow].astype(F32)
        x[:, :narrow] = rounded(wide * scale_of(jnp.sum(wide * wide)))

        def narrow_step(it, carry):
            gram = rounded(contract(kt[...], kt[...], 1, 1))
            turn = rounded(NS_B * gram.astype(F32) + NS_C * jnp.dot(gram, gram, preferred_element_type=F32))
            kt[...] = rounded(NS_A * kt[...].astype(F32) + jnp.dot(turn, kt[...], preferred_element_type=F32))
            return carry

        lax.fori_loop(0, NS_ITERS, narrow_step, 0)

        def gram_of():
            for r in range(4):
                chunk = pl.ds(r * step, step)
                g[chunk, :] = rounded(contract(x[chunk, :narrow], x[:, :narrow], 1, 1))

        def square_step(it, carry):
            gram_of()
            fill_poly()
            x[:, :narrow] = rounded(
                NS_A * x[:, :narrow].astype(F32) + jnp.dot(poly[...], x[:, :narrow], preferred_element_type=F32)
            )
            return carry

        lax.fori_loop(0, NS_ITERS - 1, square_step, 0)
        gram_of()
        mine = poly_rows(g, pl.multiple_of(f * rows, rows), rows)
        square = rounded(
            NS_A * x[my_rows, :narrow].astype(F32) + jnp.dot(mine, x[:, :narrow], preferred_element_type=F32)
        )
        x[:, narrow:] = kt[...].T
        pa[:, :narrow] = square
        pa[:, narrow:] = x[my_rows, narrow:]

    spread(at, pa, pb, o_a, o_b, ag_l, ag_s, ag_r)()


def orthogonalize(s_a, s_b, rows, high, narrow):
    parts = lax.axis_size("fsdp")
    depth, half = s_a.shape
    dma = pltpu.SemaphoreType.DMA
    vm = pltpu.VMEM
    return pl.pallas_call(
        functools.partial(ortho_kernel, parts, rows, high, narrow),
        out_shape=(
            jax.ShapeDtypeStruct((WIDE, rows, half), BF16),
            jax.ShapeDtypeStruct((CLASSES - WIDE, high, depth), BF16),
        ),
        in_specs=[VMEM, VMEM],
        out_specs=(ANY, ANY),
        scratch_shapes=[
            vm((depth, half), BF16),
            vm((half, depth), BF16),
            vm((depth, depth), BF16),
            vm((2, depth, depth), BF16),
            vm((depth, depth), BF16),
            vm((depth, depth), BF16),
            vm((8, 128), F32),
            vm((8, 128), F32),
            vm((rows, half), BF16),
            vm((high, depth), BF16),
            vm((half - narrow, depth), BF16),
            dma((4,)), dma((2, 4)), dma, dma, dma, dma((7,)), dma((CLASSES,)),
        ],
        compiler_params=pltpu.CompilerParams(
            collective_id=2, has_side_effects=True, vmem_limit_bytes=62 << 20
        ),
        name="orthogonalize",
    )(s_a, s_b)


def rotary_tables(positions, width):
    half = width // 2
    frequency = THETA ** (-(jnp.arange(half, dtype=jnp.float32) * 2.0 / width))
    angle = positions.astype(jnp.float32)[:, None] * frequency[None, :]
    return (jnp.cos(angle)[:, None, :], jnp.sin(angle)[:, None, :])


def rotate(value, cosine, sine):
    half = value.shape[-1] // 2
    first = value[..., :half]
    second = value[..., half:]
    return jnp.concatenate(
        [first * cosine - second * sine, second * cosine + first * sine], axis=-1
    )


def unrotate(incoming, cosine, sine):
    half = incoming.shape[-1] // 2
    upper = incoming[..., :half]
    lower = incoming[..., half:]
    return jnp.concatenate([upper * cosine + lower * sine, lower * cosine - upper * sine], axis=-1)


def norm_forward(residual, gain):
    inverse = lax.rsqrt(jnp.mean(residual * residual, axis=-1, keepdims=True) + EPS)
    return ((residual * inverse * gain).astype(jnp.bfloat16), inverse)


def norm_backward(residual, inverse, gain, incoming):
    scaled = incoming * gain
    through = inverse * scaled - residual * inverse**3 * jnp.mean(
        scaled * residual, axis=-1, keepdims=True
    )
    return (through, jnp.sum(incoming * residual * inverse, axis=0))


def padded(array, axis, parts, count, full):
    if count == full:
        return array
    shape = array.shape
    split = array.reshape(shape[:axis] + (parts, count) + shape[axis + 1 :])
    pads = [(0, 0)] * split.ndim
    pads[axis + 1] = (0, full - count)
    return jnp.pad(split, pads).reshape(shape[:axis] + (parts * full,) + shape[axis + 1 :])


def trimmed(array, axis, parts, count, full):
    if count == full:
        return array
    shape = array.shape
    split = array.reshape(shape[:axis] + (parts, full) + shape[axis + 1 :])
    kept = lax.slice_in_dim(split, 0, count, axis=axis + 1)
    return kept.reshape(shape[:axis] + (parts * count,) + shape[axis + 1 :])


def on_device(
    layer_input,
    output_grad,
    query_weight,
    key_weight,
    value_weight,
    output_weight,
    gate_weight,
    up_weight,
    down_weight,
    norm_gains,
    query_momentum,
    key_momentum,
    value_momentum,
    output_momentum,
    gate_momentum,
    up_momentum,
    down_momentum,
    gain_momentum,
    block_order,
):
    rows = layer_input.shape[1]
    block = rows // 2
    group = HEADS // KV_HEADS
    scale = 1.0 / math.sqrt(HEAD)
    parts = lax.axis_size("fsdp")
    ctx_place = lax.axis_index("ctx")
    width = layer_input.shape[2]
    hidden_size = gate_weight.shape[1]
    half = hidden_size // 2
    kv = key_weight.shape[1]
    short = width // parts
    full = -(-short // 16) * 16
    high = half // parts
    offsets = jnp.arange(block, dtype=jnp.int32)
    own_blocks = lax.dynamic_slice_in_dim(block_order, 2 * ctx_place, 2)
    query_pos = (own_blocks[:, None] * block + offsets[None, :]).reshape(rows)
    key_pos = (block_order[:, None] * block + offsets[None, :]).reshape(-1)

    wide = jnp.stack(
        [
            jnp.concatenate([query_weight, key_weight], axis=1),
            jnp.concatenate([output_weight, value_weight], axis=1),
            gate_weight[:, :half],
            gate_weight[:, half:],
            up_weight[:, :half],
            up_weight[:, half:],
        ]
    )
    all_wide, all_tall = gather_weights(wide, down_weight.reshape(2, high, width))
    w_qk, w_ov, w_gate_0, w_gate_1, w_up_0, w_up_1 = [all_wide[i].reshape(width, half) for i in range(WIDE)]
    w_down = [all_tall[i].reshape(half, width) for i in range(2)]

    residual = layer_input[0].astype(jnp.float32)
    normed_first, inverse_first = norm_forward(residual, norm_gains[0])
    qk_pre = jnp.dot(normed_first, w_qk, preferred_element_type=jnp.float32)
    query_pre = qk_pre[:, :width].reshape(rows, HEADS, HEAD)
    key_pre = qk_pre[:, width:].reshape(rows, KV_HEADS, HEAD)
    value_low = (
        jnp.dot(normed_first, w_ov, preferred_element_type=jnp.float32)[:, width:]
        .astype(jnp.bfloat16)
        .reshape(rows, KV_HEADS, HEAD)
    )
    cosine, sine = rotary_tables(query_pos, HEAD)
    query_rot = rotate(query_pre, cosine, sine).astype(jnp.bfloat16)
    key_rot = rotate(key_pre, cosine, sine).astype(jnp.bfloat16)
    keys_all, values_all = (
        lax.all_gather(key_rot, "ctx", axis=0, tiled=True),
        lax.all_gather(value_low, "ctx", axis=0, tiled=True),
    )
    keys_head = keys_all.transpose(1, 0, 2)
    values_head = values_all.transpose(1, 0, 2)
    queries_head = (
        query_rot.reshape(rows, KV_HEADS, group, HEAD)
        .transpose(1, 2, 0, 3)
        .reshape(KV_HEADS, group * rows, HEAD)
    )
    row_pos = jnp.tile(query_pos, group)
    allowed = key_pos[None, :] <= row_pos[:, None]

    def head_forward(item):
        query, key, value = item
        scores = jnp.where(allowed, contract(query, key, 1, 1) * scale, MASKED)
        top = jnp.max(scores, axis=-1, keepdims=True)
        expo = jnp.exp(scores - top)
        total = jnp.sum(expo, axis=-1, keepdims=True)
        probs_low = (expo / total).astype(jnp.bfloat16)
        return (
            jnp.dot(probs_low, value, preferred_element_type=jnp.float32),
            (top + jnp.log(total))[:, 0],
        )

    mixed, log_total = lax.map(head_forward, (queries_head, keys_head, values_head))
    attended = (
        mixed.reshape(KV_HEADS, group, rows, HEAD)
        .transpose(2, 0, 1, 3)
        .reshape(rows, HEADS * HEAD)
        .astype(jnp.bfloat16)
    )
    w_out = w_ov[:, :width]
    middle = residual + jnp.dot(attended, w_out, preferred_element_type=jnp.float32)
    normed_second, inverse_second = norm_forward(middle, norm_gains[1])

    def sides(left, right):
        return jnp.concatenate([left, right], axis=1)

    gate = sides(
        jnp.dot(normed_second, w_gate_0, preferred_element_type=jnp.float32),
        jnp.dot(normed_second, w_gate_1, preferred_element_type=jnp.float32),
    )
    lifted = sides(
        jnp.dot(normed_second, w_up_0, preferred_element_type=jnp.float32),
        jnp.dot(normed_second, w_up_1, preferred_element_type=jnp.float32),
    )
    sigma = jax.nn.sigmoid(gate)
    hidden = (gate * sigma * lifted).astype(jnp.bfloat16)
    hidden_split = hidden.reshape(rows, parts, 2, high)
    hidden_sides = [hidden_split[:, :, i].reshape(rows, half) for i in range(2)]
    layer_output = (
        middle
        + jnp.dot(hidden_sides[0], w_down[0], preferred_element_type=jnp.float32)
        + jnp.dot(hidden_sides[1], w_down[1], preferred_element_type=jnp.float32)
    ).astype(jnp.bfloat16)
    upstream = output_grad[0]
    grad_hidden = jnp.stack(
        [contract(upstream, w_down[i], 1, 1).reshape(rows, parts, high) for i in range(2)], axis=2
    ).reshape(rows, hidden_size)
    grad_gate = (grad_hidden * lifted * sigma * (1.0 + gate * (1.0 - sigma))).astype(jnp.bfloat16)
    grad_lifted = (grad_hidden * gate * sigma).astype(jnp.bfloat16)
    grad_normed_second = (
        contract(grad_gate[:, :half], w_gate_0, 1, 1)
        + contract(grad_gate[:, half:], w_gate_1, 1, 1)
        + contract(grad_lifted[:, :half], w_up_0, 1, 1)
        + contract(grad_lifted[:, half:], w_up_1, 1, 1)
    )
    through_second, gain_second = norm_backward(
        middle, inverse_second, norm_gains[1], grad_normed_second
    )
    grad_middle = upstream.astype(jnp.float32) + through_second
    grad_branch = grad_middle.astype(jnp.bfloat16)
    grad_attended = contract(grad_branch, w_out, 1, 1).astype(jnp.bfloat16)
    grad_heads = (
        grad_attended.reshape(rows, KV_HEADS, group, HEAD)
        .transpose(1, 2, 0, 3)
        .reshape(KV_HEADS, group * rows, HEAD)
    )

    def head_backward(item):
        query, key, value, grad_out, log_row = item
        scores = jnp.where(allowed, contract(query, key, 1, 1) * scale, MASKED)
        probs = jnp.exp(scores - log_row[:, None])
        grad_value_part = contract(probs.astype(jnp.bfloat16), grad_out, 0, 0)
        grad_probs = contract(grad_out, value, 1, 1)
        grad_scores = (
            probs * (grad_probs - jnp.sum(grad_probs * probs, axis=-1, keepdims=True))
        ).astype(jnp.bfloat16)
        grad_query_part = jnp.dot(grad_scores, key, preferred_element_type=jnp.float32) * scale
        grad_key_part = contract(grad_scores, query, 0, 0) * scale
        return (grad_query_part, grad_key_part, grad_value_part)

    grad_query_rot, grad_key_all, grad_value_all = lax.map(
        head_backward, (queries_head, keys_head, values_head, grad_heads, log_total)
    )
    grad_key_own, grad_value_own = (
        lax.psum_scatter(
            grad_key_all.astype(jnp.bfloat16), "ctx", scatter_dimension=1, tiled=True
        ).astype(jnp.float32),
        lax.psum_scatter(
            grad_value_all.astype(jnp.bfloat16), "ctx", scatter_dimension=1, tiled=True
        ).astype(jnp.float32),
    )
    grad_query = (
        unrotate(
            grad_query_rot.reshape(KV_HEADS, group, rows, HEAD)
            .transpose(2, 0, 1, 3)
            .reshape(rows, HEADS, HEAD),
            cosine,
            sine,
        )
        .reshape(rows, HEADS * HEAD)
        .astype(jnp.bfloat16)
    )
    grad_key = (
        unrotate(grad_key_own.transpose(1, 0, 2), cosine, sine)
        .reshape(rows, KV_HEADS * HEAD)
        .astype(jnp.bfloat16)
    )
    grad_value = (
        grad_value_own.transpose(1, 0, 2).reshape(rows, KV_HEADS * HEAD).astype(jnp.bfloat16)
    )
    grad_qk = sides(grad_query, grad_key)
    zero_query = jnp.zeros((rows, width), jnp.bfloat16)
    grad_v = sides(zero_query, grad_value)
    grad_normed_first = contract(grad_qk, w_qk, 1, 1) + contract(grad_v, w_ov, 1, 1)
    through_first, gain_first = norm_backward(
        residual, inverse_first, norm_gains[0], grad_normed_first
    )
    input_gradient = (grad_middle + through_first)[None]

    xt = jnp.stack([item.T for item in (normed_first, attended, normed_second, upstream)])
    xt = padded(xt, 1, parts, short, full)
    dy = jnp.stack(
        [
            grad_qk,
            sides(grad_branch, jnp.zeros((rows, kv), jnp.bfloat16)),
            grad_gate[:, :half],
            grad_gate[:, half:],
            grad_lifted[:, :half],
            grad_lifted[:, half:],
            hidden_sides[0],
            hidden_sides[1],
            grad_v,
        ]
    )
    gains = jnp.pad(jnp.stack([gain_first, gain_second]), ((0, 6), (0, 0)))

    def pad_rows(array):
        return padded(array, 0, 1, short, full)

    def pad_columns(array):
        return padded(array, 1, parts, short, full)

    moments = (
        pad_rows(sides(query_momentum, key_momentum)),
        pad_rows(sides(output_momentum, value_momentum)),
        pad_rows(gate_momentum),
        pad_rows(up_momentum),
        pad_columns(down_momentum),
    )
    g_wide, g_tall, s_wide, s_tall, gain_sum = reduce_gradients(xt, dy, gains, moments, full, high)
    o_wide, o_tall = orthogonalize(s_wide, s_tall, full, high, width)

    def unpack(wide_pieces, tall_pieces):
        pieces = wide_pieces[:, :short]
        tall = trimmed(tall_pieces, 2, parts, short, full).reshape(2 * high, width)
        return (
            pieces[0, :, :width],
            pieces[0, :, width:],
            pieces[1, :, width:],
            pieces[1, :, :width],
            sides(pieces[2], pieces[3]),
            sides(pieces[4], pieces[5]),
            tall,
        )

    gradients = [item.astype(jnp.float32) for item in unpack(g_wide, g_tall)]
    orthos = unpack(o_wide, o_tall)
    olds = (
        query_momentum,
        key_momentum,
        value_momentum,
        output_momentum,
        gate_momentum,
        up_momentum,
        down_momentum,
    )
    moments = [MOMENTUM * old + new for old, new in zip(olds, gradients)]
    old_weights = (
        query_weight,
        key_weight,
        value_weight,
        output_weight,
        gate_weight,
        up_weight,
        down_weight,
    )
    new_weights = []
    for index in range(len(olds)):
        cols_full = old_weights[index].shape[1]
        rows_full = old_weights[index].shape[0] * parts
        step_rate = OUT_RATE if index == 3 else RATE
        factor = -step_rate * max(1.0, cols_full / rows_full) ** 0.5
        new_weights.append(
            old_weights[index].astype(jnp.float32) + factor * orthos[index].astype(jnp.float32)
        )
    gain_width = norm_gains.shape[1] // parts
    place = lax.axis_index("fsdp") * gain_width
    gain_gradient = lax.dynamic_slice_in_dim(gain_sum[:2], place, gain_width, 1)
    gain_shard = lax.dynamic_slice_in_dim(norm_gains, place, gain_width, 1)
    gain_moment = MOMENTUM * gain_momentum + gain_gradient
    new_gains = gain_shard - GAIN_RATE * gain_moment
    return (
        layer_output[None],
        input_gradient,
        *gradients,
        gain_gradient,
        *moments,
        gain_moment,
        *new_weights,
        new_gains,
    )


def solution(mesh):
    tokens = P("fsdp", "ctx", None)
    shard = P("fsdp", None)
    gains = P(None, "fsdp")
    return jax.shard_map(
        on_device,
        mesh=mesh,
        in_specs=(tokens, tokens) + (shard,) * 7 + (P(),) + (shard,) * 7 + (gains, P()),
        out_specs=(tokens, tokens) + ((shard,) * 7 + (gains,)) * 3,
        check_vma=False,
    )
```

```python
import functools
import math

import jax
import jax.numpy as jnp
from jax import lax
from jax.experimental import pallas as pl
from jax.experimental.pallas import tpu as pltpu
from jax.sharding import PartitionSpec as P

HEADS = 15
KV_HEADS = 5
HEAD = 64
NS_ITERS = 5


EPS = 1e-05
THETA = 100000.0
NS_A = 3.4445
NS_B = -4.775
NS_C = 2.0315
MOMENTUM = 0.95
RATE = 0.2
OUT_RATE = 6.0
GAIN_RATE = 0.002
MASKED = -1e30

MESH = pl.DeviceIdType.MESH
BF16 = jnp.bfloat16
F32 = jnp.float32
ANY = pl.BlockSpec(memory_space=pl.ANY)
VMEM = pl.BlockSpec(memory_space=pltpu.VMEM)
CLASSES = 8
WIDE = 6


def contract(left, right, left_dim, right_dim):
    return lax.dot_general(
        left, right, (((left_dim,), (right_dim,)), ((), ())), preferred_element_type=jnp.float32
    )


class Place:
    def __init__(self):
        self.parts = lax.axis_size("fsdp")
        self.extra = lax.axis_size("ctx") // CLASSES
        self.c = lax.axis_index("ctx")
        self.f = lax.axis_index("fsdp")
        self.p = lax.rem(self.c, CLASSES)
        self.core = lax.rem(self.c, 2)
        self.b1 = jnp.where(self.core == 0, 2, 4)
        self.b2 = jnp.where(self.core == 0, 4, 2)

    def peer(self, bits):
        return (self.c ^ bits, self.f)

    def along(self, j):
        return (self.c, self.f ^ j)

    def other(self, j):
        groups = self.extra
        return (lax.rem(self.c + CLASSES * j, CLASSES * groups), self.f)

    def barrier(self, bits=(1, 2, 4), line=True, others=False):
        sem = pltpu.get_barrier_semaphore()
        targets = [self.peer(b) for b in bits]
        if line:
            targets += [self.along(j) for j in range(1, self.parts)]
        if others:
            targets += [self.other(j) for j in range(1, self.extra)]
        for target in targets:
            pl.semaphore_signal(sem, inc=1, device_id=target, device_id_type=MESH)
        pl.semaphore_wait(sem, len(targets))


def remote(src, dst, send, recv, target):
    return pltpu.make_async_remote_copy(
        src_ref=src, dst_ref=dst, send_sem=send, recv_sem=recv, device_id=target, device_id_type=MESH
    )


def by_kind(cls, wide, tall):
    pl.when(cls < WIDE)(wide)
    pl.when(cls >= WIDE)(tall)


def weights_kernel(in_a, in_b, out_a, out_b, local, zs, s1, s2, sc, recv):
    at = Place()
    p, f, parts = at.p, at.f, at.parts
    at.barrier()
    copies = [
        pltpu.make_async_copy(in_a, out_a.at[:, f], local.at[0]),
        pltpu.make_async_copy(in_b, out_b.at[:, f], local.at[1]),
    ]
    for copy in copies:
        copy.start()

    def act(cls, j, g, send, target, what, first=False):
        def wide():
            dst = out_a.at[cls, g]
            src = in_a.at[cls] if first else dst
            getattr(remote(src, dst, send, recv.at[cls, j], target), what)()

        def tall():
            dst = out_b.at[cls - WIDE, g]
            src = in_b.at[cls - WIDE] if first else dst
            getattr(remote(src, dst, send, recv.at[cls, j], target), what)()

        by_kind(cls, wide, tall)

    sends = []

    def send(cls, j, g, sem, target, first=False):
        act(cls, j, g, sem, target, "start", first)
        sends.append((cls, j, g, sem, target, first))

    def arrived(cls, j):
        act(cls, j, f ^ j, zs.at[j], at.along(j), "wait_recv")

    for j in range(1, parts):
        send(p, j, f, zs.at[j], at.along(j), True)
    for j in range(1, parts):
        arrived(p, j)
        send(p, j, f ^ j, s1.at[0, j], at.peer(at.b1))
        send(p, j, f ^ j, s2.at[0, j], at.peer(at.b2))
        send(p, j, f ^ j, sc.at[0, j], at.peer(1))
    for j in range(1, parts):
        arrived(p ^ at.b1, j)
        send(p ^ at.b1, j, f ^ j, s2.at[1, j], at.peer(at.b2))
        send(p ^ at.b1, j, f ^ j, sc.at[1, j], at.peer(1))
    for slot, bits in ((2, at.b2), (3, at.b1 ^ at.b2)):
        for j in range(1, parts):
            arrived(p ^ bits, j)
            send(p ^ bits, j, f ^ j, sc.at[slot, j], at.peer(1))
    for bits in (1, 3, 5, 7):
        for j in range(1, parts):
            arrived(p ^ bits, j)
    for cls, j, g, sem, target, first in sends:
        act(cls, j, g, sem, target, "wait_send", first)
    for copy in copies:
        copy.wait()


def gather_weights(wide, tall):
    parts = lax.axis_size("fsdp")
    dma = pltpu.SemaphoreType.DMA
    return pl.pallas_call(
        weights_kernel,
        out_shape=(
            jax.ShapeDtypeStruct((WIDE, parts) + wide.shape[1:], BF16),
            jax.ShapeDtypeStruct((CLASSES - WIDE, parts) + tall.shape[1:], BF16),
        ),
        in_specs=[ANY, ANY],
        out_specs=(ANY, ANY),
        scratch_shapes=[
            dma((2,)),
            dma((parts,)),
            dma((1, parts)),
            dma((2, parts)),
            dma((4, parts)),
            dma((CLASSES, parts)),
        ],
        compiler_params=pltpu.CompilerParams(collective_id=0, has_side_effects=True),
        name="gather_weights",
    )(wide, tall)


def spread(at, own_a, own_b, out_a, out_b, local, ss, recv):
    p = at.p

    def act(cls, sem, target, what, first=False):
        def wide():
            dst = out_a.at[cls]
            getattr(remote(own_a if first else dst, dst, sem, recv.at[cls], target), what)()

        def tall():
            dst = out_b.at[cls - WIDE]
            getattr(remote(own_b if first else dst, dst, sem, recv.at[cls], target), what)()

        by_kind(cls, wide, tall)

    def keep(what):
        def wide():
            getattr(pltpu.make_async_copy(own_a, out_a.at[p], local), what)()

        def tall():
            getattr(pltpu.make_async_copy(own_b, out_b.at[p - WIDE], local), what)()

        by_kind(p, wide, tall)

    sends = []

    def send(cls, slot, target, first=False):
        act(cls, ss.at[slot], target, "start", first)
        sends.append((cls, slot, target, first))

    def arrived(cls):
        act(cls, ss.at[0], at.peer(1), "wait_recv")

    send(p, 0, at.peer(at.b1), True)
    send(p, 1, at.peer(at.b2), True)
    send(p, 2, at.peer(1), True)
    keep("start")

    def finish():
        arrived(p ^ at.b1)
        send(p ^ at.b1, 3, at.peer(at.b2))
        send(p ^ at.b1, 4, at.peer(1))
        arrived(p ^ at.b2)
        send(p ^ at.b2, 5, at.peer(1))
        arrived(p ^ at.b1 ^ at.b2)
        send(p ^ at.b1 ^ at.b2, 6, at.peer(1))
        for bits in (1, 3, 5, 7):
            arrived(p ^ bits)
        for cls, slot, target, first in sends:
            act(cls, ss.at[slot], target, "wait_send", first)
        keep("wait")

    return finish


def reduce_kernel(
    parts, extra, high,
    xt_in, dy_in, gain_in, m_qk, m_ov, m_gate, m_up, m_down,
    g_a, g_b, s_a, s_b, gain_out,
    xt, dy, p1s, p1r, p2s, p2r, own, own_t, za_s, za_r, zb_s, zb_r, ma, mb, ga, gb, sa, sb, es, er, gain_s, gain_r,
    ls, xs, xr, s1, r1, s2, r2, zs, zr, esem, ersem, msem, gs, gr, ag_l, ag_s, ag_r, ss, sr, sl,
):
    at = Place()
    p, f, core = at.p, at.f, at.core
    tokens = xt_in.shape[2]
    rows = ma.shape[0]
    half = dy.shape[2]

    def moment(what):
        for cls in range(CLASSES):
            @pl.when(p == cls)
            def _(cls=cls):
                side = cls % 2
                if cls < 2:
                    src, dst = (m_qk, m_ov)[cls], ma
                elif cls < WIDE:
                    whole = m_gate if cls < 4 else m_up
                    src, dst = whole.at[:, pl.ds(side * half, half)], ma
                else:
                    src, dst = m_down.at[pl.ds(side * high, high)], mb
                getattr(pltpu.make_async_copy(src, dst, msem), what)()

    moment("start")
    mine = [pltpu.make_async_copy(xt_in, xt.at[:, :, pl.ds(0, tokens)], ls.at[0])]
    for slot in range(4):
        mine.append(
            pltpu.make_async_copy(dy_in.at[core + 2 * slot], dy.at[slot, pl.ds(0, tokens)], ls.at[1 + slot])
        )
    mine.append(pltpu.make_async_copy(dy_in.at[8], dy.at[4, pl.ds(0, tokens)], ls.at[5]))
    for copy in mine:
        copy.start()
    at.barrier(others=True)
    pair = at.peer(1)
    theirs = [remote(xt_in, xt.at[:, :, pl.ds(tokens, tokens)], xs.at[0], xr.at[0], pair)]
    for slot in range(4):
        theirs.append(
            remote(dy_in.at[1 - core + 2 * slot], dy.at[slot, pl.ds(tokens, tokens)], xs.at[1 + slot], xr.at[1 + slot], pair)
        )
    theirs.append(remote(dy_in.at[8], dy.at[4, pl.ds(tokens, tokens)], xs.at[5], xr.at[5], pair))
    for copy in theirs:
        copy.start()

    def swap(slot, target):
        return remote(gain_s.at[slot], gain_r.at[slot], gs.at[slot], gr.at[slot], target)

    gain_s[0] = gain_in[...]
    swaps = [swap(0, pair)]
    swaps[0].start()
    for copy in mine:
        copy.wait()
    for copy in theirs:
        copy.wait()

    def term(cls, r):
        at_rows = pl.ds(pl.multiple_of(r * rows, rows), rows)
        slot = lax.div(cls, 2)
        kind = jnp.where(cls == 0, 0, jnp.where(cls == 1, 1, jnp.where(cls < WIDE, 2, 3)))
        value = jnp.dot(xt[kind, at_rows, :], dy[slot], preferred_element_type=F32)
        return value

    def with_values(cls, r, put):
        at_rows = pl.ds(pl.multiple_of(r * rows, rows), rows)

        @pl.when(cls == 1)
        def _():
            put(term(cls, r) + jnp.dot(xt[0, at_rows, :], dy[4], preferred_element_type=F32))

        @pl.when(cls != 1)
        def _():
            put(term(cls, r))

    def order(i):
        return lax.rem(f + 1 + i, parts)

    def one(slot, i):
        r = order(i)
        return remote(p1s.at[slot, r], p1r.at[slot, r], s1.at[slot, r], r1.at[slot, r], at.peer(at.b1))

    for slot, bits in ((0, at.b1 ^ at.b2), (1, at.b1)):
        def first(i, carry, slot=slot, bits=bits):
            r = order(i)

            def put(value):
                p1s[slot, r] = value.astype(BF16)

            with_values(p ^ bits, r, put)
            one(slot, i).start()
            return carry

        lax.fori_loop(0, parts, first, 0)

    swaps[0].wait()
    gain_s[1] = gain_s[0] + gain_r[0]
    swaps.append(swap(1, at.peer(2)))
    swaps[1].start()

    def two(i):
        r = order(i)
        return remote(p2s.at[r], p2r.at[r], s2.at[r], r2.at[r], at.peer(at.b2))

    def second(i, carry):
        r = order(i)
        one(0, i).wait_recv()

        def put(value):
            p2s[r] = (value + p1r[0, r].astype(F32)).astype(BF16)

        with_values(p ^ at.b2, r, put)
        two(i).start()
        return carry

    lax.fori_loop(0, parts, second, 0)
    swaps[1].wait()
    gain_s[2] = gain_s[1] + gain_r[1]
    swaps.append(swap(2, at.peer(4)))
    swaps[2].start()

    def line_a(r, source):
        return remote(za_s.at[r], za_r.at[source], zs.at[r], zr.at[source], (at.c, r))

    def line_b(r, source):
        return remote(
            zb_s.at[pl.ds(pl.multiple_of(r * high, high), high)],
            zb_r.at[source], zs.at[r], zr.at[source], (at.c, r),
        )

    early = extra == 1

    def third(i, carry):
        r = order(i)
        one(1, i).wait_recv()
        two(i).wait_recv()

        def put(value):
            total = value + p1r[1, r].astype(F32) + p2r[r].astype(F32)
            own[r] = total
            if early:
                za_s[r] = total.astype(BF16)

        with_values(p, r, put)
        if early:
            @pl.when((p < WIDE) & (i < parts - 1))
            def _():
                line_a(r, f).start()
        return carry

    lax.fori_loop(0, parts, third, 0)
    swaps[2].wait()
    gain_s[3] = gain_s[2] + gain_r[2]

    if not early:
        es[...] = own[...].astype(BF16)
        group = [
            remote(es, er.at[j - 1], esem.at[j - 1], ersem.at[j - 1], at.other(j)) for j in range(1, extra)
        ]
        for copy in group:
            copy.start()
        for j in range(1, extra):
            group[j - 1].wait_recv()
            own[...] = own[...] + er[j - 1].astype(F32)
        for copy in group:
            copy.wait_send()
        za_s[...] = own[...].astype(BF16)

        @pl.when(p < WIDE)
        def _():
            for j in range(1, parts):
                line_a(f ^ j, f).start()

    @pl.when(p >= WIDE)
    def _():
        for tile in range(half // 128):
            for r in range(parts):
                block = own[r, :, pl.ds(tile * 128, 128)]
                if rows % 128 == 0:
                    own_t[pl.ds(tile * 128, 128), pl.ds(r * rows, rows)] = block.T
            if rows % 128 != 0:
                column = own[:, :, pl.ds(tile * 128, 128)].reshape(parts * rows, 128)
                own_t[pl.ds(tile * 128, 128), :] = column.T
        zb_s[...] = own_t[...].astype(BF16)
        for j in range(1, parts):
            line_b(f ^ j, f).start()

    line_gain = [
        remote(gain_s.at[3], gain_r.at[3 + j], gs.at[3 + j], gr.at[3 + j], at.along(j)) for j in range(1, parts)
    ]
    other_gain = []
    for copy in line_gain:
        copy.start()

    moment("wait")

    @pl.when(p < WIDE)
    def _():
        total = own[f]
        for j in range(1, parts):
            line_a(f ^ j, f ^ j).wait_recv()
            total = total + za_r[f ^ j].astype(F32)
        ga[...] = total.astype(BF16)
        sa[...] = (MOMENTUM * ma[...] + total).astype(BF16)

    @pl.when(p >= WIDE)
    def _():
        total = own_t[pl.ds(pl.multiple_of(f * high, high), high), :]
        for j in range(1, parts):
            line_b(f ^ j, f ^ j).wait_recv()
            total = total + zb_r[f ^ j].astype(F32)
        gb[...] = total.astype(BF16)
        sb[...] = (MOMENTUM * mb[...] + total).astype(BF16)

    def share_a(j, source):
        return remote(sa, s_a.at[pl.ds(pl.multiple_of(source * rows, rows), rows)], ss.at[j], sr.at[j], at.along(j))

    def share_b(j, source):
        return remote(sb, s_b.at[pl.ds(pl.multiple_of(source * high, high), high)], ss.at[j], sr.at[j], at.along(j))

    @pl.when(p < WIDE)
    def _():
        for j in range(1, parts):
            share_a(j, f).start()
        pltpu.make_async_copy(sa, s_a.at[pl.ds(pl.multiple_of(f * rows, rows), rows)], sl).start()

    @pl.when(p >= WIDE)
    def _():
        for j in range(1, parts):
            share_b(j, f).start()
        pltpu.make_async_copy(sb, s_b.at[pl.ds(pl.multiple_of(f * high, high), high)], sl).start()

    finish = spread(at, ga, gb, g_a, g_b, ag_l, ag_s, ag_r)
    total = gain_s[3]
    for j in range(1, parts):
        line_gain[j - 1].wait()
        total = total + gain_r[3 + j]
    if extra > 1:
        gain_s[4] = total
        other_gain = [
            remote(gain_s.at[4], gain_r.at[3 + parts + j], gs.at[3 + parts + j], gr.at[3 + parts + j], at.other(j))
            for j in range(1, extra)
        ]
        for copy in other_gain:
            copy.start()
        for j in range(1, extra):
            other_gain[j - 1].wait()
            total = total + gain_r[3 + parts + j]
    gain_out[...] = total
    finish()

    for slot in range(2):
        lax.fori_loop(0, parts, lambda i, carry, slot=slot: (one(slot, i).wait_send(), carry)[1], 0)
    lax.fori_loop(0, parts, lambda i, carry: (two(i).wait_send(), carry)[1], 0)

    @pl.when(p < WIDE)
    def _():
        for j in range(1, parts):
            line_a(f ^ j, f).wait_send()
            share_a(j, f).wait_send()
            share_a(j, f ^ j).wait_recv()
        pltpu.make_async_copy(sa, s_a.at[pl.ds(pl.multiple_of(f * rows, rows), rows)], sl).wait()

    @pl.when(p >= WIDE)
    def _():
        for j in range(1, parts):
            line_b(f ^ j, f).wait_send()
            share_b(j, f).wait_send()
            share_b(j, f ^ j).wait_recv()
        pltpu.make_async_copy(sb, s_b.at[pl.ds(pl.multiple_of(f * high, high), high)], sl).wait()


def reduce_gradients(xt, dy, gains, moments, rows, high):
    parts = lax.axis_size("fsdp")
    extra = lax.axis_size("ctx") // CLASSES
    kinds, depth, tokens = xt.shape
    half = dy.shape[2]
    dma = pltpu.SemaphoreType.DMA
    vm = pltpu.VMEM
    n_gain = 4 + parts + extra
    group = max(extra - 1, 1)
    spare = (parts, rows, half) if extra > 1 else (1, 16, 128)
    return pl.pallas_call(
        functools.partial(reduce_kernel, parts, extra, high),
        out_shape=(
            jax.ShapeDtypeStruct((WIDE, rows, half), BF16),
            jax.ShapeDtypeStruct((CLASSES - WIDE, high, depth), BF16),
            jax.ShapeDtypeStruct((depth, half), BF16),
            jax.ShapeDtypeStruct((half, depth), BF16),
            jax.ShapeDtypeStruct(gains.shape, F32),
        ),
        in_specs=[ANY, ANY, VMEM] + [ANY] * 5,
        out_specs=(ANY, ANY, ANY, ANY, VMEM),
        scratch_shapes=[
            vm((kinds, depth, 2 * tokens), BF16),
            vm((5, 2 * tokens, half), BF16),
            vm((2, parts, rows, half), BF16),
            vm((2, parts, rows, half), BF16),
            vm((parts, rows, half), BF16),
            vm((parts, rows, half), BF16),
            vm((parts, rows, half), F32),
            vm((half, depth), F32),
            vm((parts, rows, half), BF16),
            vm((parts, rows, half), BF16),
            vm((half, depth), BF16),
            vm((parts, high, depth), BF16),
            vm((rows, half), F32),
            vm((high, depth), F32),
            vm((rows, half), BF16),
            vm((high, depth), BF16),
            vm((rows, half), BF16),
            vm((high, depth), BF16),
            vm(spare, BF16),
            vm((group,) + spare, BF16),
            vm((5,) + gains.shape, F32),
            vm((n_gain,) + gains.shape, F32),
            dma((6,)), dma((6,)), dma((6,)),
            dma((2, parts)), dma((2, parts)), dma((parts,)), dma((parts,)), dma((parts,)), dma((parts,)),
            dma((group,)), dma((group,)), dma, dma((n_gain,)), dma((n_gain,)),
            dma, dma((7,)), dma((CLASSES,)), dma((parts,)), dma((parts,)), dma,
        ],
        compiler_params=pltpu.CompilerParams(
            collective_id=1, has_side_effects=True, vmem_limit_bytes=62 << 20
        ),
        name="reduce_gradients",
    )(xt, dy, gains, *moments)


def rounded(value):
    return value.astype(BF16)


def poly_rows(g, row_start, count):
    block = g[pl.ds(row_start, count), :]
    return rounded(NS_B * block.astype(F32) + NS_C * jnp.dot(block, g[...], preferred_element_type=F32))


def ortho_kernel(
    parts, rows, high, narrow,
    s_a, s_b, o_a, o_b,
    x, x_t, gs, gr, g, poly, sq, sq_r, pa, pb, kt,
    gsem, rsem, qs, qr, ag_l, ag_s, ag_r,
):
    at = Place()
    p, f = at.p, at.f
    depth, half = x.shape
    step = depth // 4
    at.barrier(line=False)
    pair = at.peer(1)

    @pl.when(p < WIDE)
    def _():
        x[...] = s_a[...]

    @pl.when(p >= WIDE)
    def _():
        for tile in range(half // 128):
            x[:, pl.ds(tile * 128, 128)] = s_b[pl.ds(tile * 128, 128), :].T

    def scale_of(total):
        return 1.0 / (jnp.sqrt(total) + 1e-07)

    def normal(ref, inverse):
        ref[...] = rounded(ref[...].astype(F32) * inverse)

    def exchange(slot, r):
        chunk = pl.ds(r * step, step)
        return remote(gs.at[chunk], gr.at[slot, chunk], gsem.at[r], rsem.at[slot, r], pair)

    def fill_poly():
        for r in range(4):
            poly[pl.ds(r * step, step), :] = poly_rows(g, r * step, step)

    my_rows = pl.ds(pl.multiple_of(f * rows, rows), rows)
    my_high = pl.ds(pl.multiple_of(f * high, high), high)

    @pl.when(p >= 2)
    def _():
        wide = x[...].astype(F32)
        sq[...] = jnp.broadcast_to(jnp.sum(wide * wide), sq.shape)
        copy = remote(sq, sq_r, qs, qr, pair)
        copy.start()
        copy.wait()
        normal(x, scale_of(sq[...] + sq_r[...])[:1, :1])

        def grams(slot):
            for r in range(4):
                gs[pl.ds(r * step, step), :] = rounded(contract(x[pl.ds(r * step, step), :], x[...], 1, 1))
                exchange(slot, r).start()
            for r in range(4):
                chunk = pl.ds(r * step, step)
                exchange(slot, r).wait()
                g[chunk, :] = rounded(gs[chunk, :].astype(F32) + gr[slot, chunk, :].astype(F32))

        def iterate(it, carry):
            grams(lax.rem(it, 2))
            fill_poly()
            for tile in range(half // 256):
                block = pl.ds(tile * 256, 256)
                x[:, block] = rounded(
                    NS_A * x[:, block].astype(F32) + jnp.dot(poly[...], x[:, block], preferred_element_type=F32)
                )
            return carry

        lax.fori_loop(0, NS_ITERS - 1, iterate, 0)
        grams((NS_ITERS - 1) % 2)

        @pl.when(p < WIDE)
        def _():
            mine = poly_rows(g, pl.multiple_of(f * rows, rows), rows)
            pa[...] = rounded(NS_A * x[my_rows, :].astype(F32) + jnp.dot(mine, x[...], preferred_element_type=F32))

        @pl.when(p >= WIDE)
        def _():
            fill_poly()
            for tile in range(half // 128):
                x_t[pl.ds(tile * 128, 128), :] = x[:, pl.ds(tile * 128, 128)].T
            block = x_t[my_high, :]
            pb[...] = rounded(NS_A * block.astype(F32) + jnp.dot(block, poly[...], preferred_element_type=F32))

    @pl.when(p < 2)
    def _():
        kt[...] = x[:, narrow:].T
        inverse_k = scale_of(jnp.sum(jnp.square(kt[...].astype(F32))))
        normal(kt, inverse_k)
        wide = x[:, :narrow].astype(F32)
        x[:, :narrow] = rounded(wide * scale_of(jnp.sum(wide * wide)))

        def narrow_step(it, carry):
            gram = rounded(contract(kt[...], kt[...], 1, 1))
            turn = rounded(NS_B * gram.astype(F32) + NS_C * jnp.dot(gram, gram, preferred_element_type=F32))
            kt[...] = rounded(NS_A * kt[...].astype(F32) + jnp.dot(turn, kt[...], preferred_element_type=F32))
            return carry

        lax.fori_loop(0, NS_ITERS, narrow_step, 0)

        def gram_of():
            for r in range(4):
                chunk = pl.ds(r * step, step)
                g[chunk, :] = rounded(contract(x[chunk, :narrow], x[:, :narrow], 1, 1))

        def square_step(it, carry):
            gram_of()
            fill_poly()
            x[:, :narrow] = rounded(
                NS_A * x[:, :narrow].astype(F32) + jnp.dot(poly[...], x[:, :narrow], preferred_element_type=F32)
            )
            return carry

        lax.fori_loop(0, NS_ITERS - 1, square_step, 0)
        gram_of()
        mine = poly_rows(g, pl.multiple_of(f * rows, rows), rows)
        square = rounded(
            NS_A * x[my_rows, :narrow].astype(F32) + jnp.dot(mine, x[:, :narrow], preferred_element_type=F32)
        )
        x[:, narrow:] = kt[...].T
        pa[:, :narrow] = square
        pa[:, narrow:] = x[my_rows, narrow:]

    spread(at, pa, pb, o_a, o_b, ag_l, ag_s, ag_r)()


def orthogonalize(s_a, s_b, rows, high, narrow):
    parts = lax.axis_size("fsdp")
    depth, half = s_a.shape
    dma = pltpu.SemaphoreType.DMA
    vm = pltpu.VMEM
    return pl.pallas_call(
        functools.partial(ortho_kernel, parts, rows, high, narrow),
        out_shape=(
            jax.ShapeDtypeStruct((WIDE, rows, half), BF16),
            jax.ShapeDtypeStruct((CLASSES - WIDE, high, depth), BF16),
        ),
        in_specs=[VMEM, VMEM],
        out_specs=(ANY, ANY),
        scratch_shapes=[
            vm((depth, half), BF16),
            vm((half, depth), BF16),
            vm((depth, depth), BF16),
            vm((2, depth, depth), BF16),
            vm((depth, depth), BF16),
            vm((depth, depth), BF16),
            vm((8, 128), F32),
            vm((8, 128), F32),
            vm((rows, half), BF16),
            vm((high, depth), BF16),
            vm((half - narrow, depth), BF16),
            dma((4,)), dma((2, 4)), dma, dma, dma, dma((7,)), dma((CLASSES,)),
        ],
        compiler_params=pltpu.CompilerParams(
            collective_id=2, has_side_effects=True, vmem_limit_bytes=62 << 20
        ),
        name="orthogonalize",
    )(s_a, s_b)


class Weights:
    def __init__(self, at, in_a, in_b, wa, wb, local, zs, s1, s2, sc, recv):
        self.at, self.in_a, self.in_b, self.wa, self.wb = at, in_a, in_b, wa, wb
        self.local, self.zs, self.s1, self.s2, self.sc, self.recv = local, zs, s1, s2, sc, recv
        self.rows = in_a.shape[1]
        self.high = in_b.shape[1]
        self.unit = -(-self.rows // (16 * CLASSES)) * 16
        self.last = self.rows - (CLASSES - 1) * self.unit
        self.tall = 2 * self.high // CLASSES
        self.sends = []

    def act(self, group, q, j, plane, send, target, what, first=False):
        recv = self.recv.at[group, q, j]
        if group == 3:
            side, start = lax.div(q, CLASSES // 2), lax.rem(q, CLASSES // 2) * self.tall
            dst = self.wb.at[side, pl.ds(pl.multiple_of(plane * self.high + start, 16), self.tall)]
            src = self.in_b.at[side, pl.ds(pl.multiple_of(start, 16), self.tall)] if first else dst
            getattr(remote(src, dst, send, recv, target), what)()
            return

        def piece(count):
            def go():
                pair = pl.ds(2 * group, 2)
                dst = self.wa.at[pair, pl.ds(pl.multiple_of(plane * self.rows + q * self.unit, 16), count)]
                src = self.in_a.at[pair, pl.ds(pl.multiple_of(q * self.unit, 16), count)] if first else dst
                getattr(remote(src, dst, send, recv, target), what)()

            return go

        pl.when(q < CLASSES - 1)(piece(self.unit))
        pl.when(q == CLASSES - 1)(piece(self.last))

    def send(self, group, q, j, plane, sem, target, first=False):
        self.act(group, q, j, plane, sem, target, "start", first)
        self.sends.append((group, q, j, plane, sem, target, "wait_send", first))

    def arrived(self, group, q, j):
        at = self.at
        self.act(group, q, j, at.f ^ j, self.zs.at[group, j], at.peer(1), "wait_recv")

    def keep(self):
        f = self.at.f
        return [
            pltpu.make_async_copy(
                self.in_a, self.wa.at[:, pl.ds(pl.multiple_of(f * self.rows, 16), self.rows)], self.local.at[0]
            ),
            pltpu.make_async_copy(
                self.in_b, self.wb.at[:, pl.ds(pl.multiple_of(f * self.high, 16), self.high)], self.local.at[1]
            ),
        ]

    def along(self, group):
        at = self.at
        for j in range(1, at.parts):
            self.send(group, at.p, j, at.f, self.zs.at[group, j], at.along(j), True)

    def first(self, group):
        at = self.at
        for j in range(1, at.parts):
            self.arrived(group, at.p, j)
            self.send(group, at.p, j, at.f ^ j, self.s1.at[group, j], at.peer(at.b1))
            self.send(group, at.p, j, at.f ^ j, self.s2.at[group, 0, j], at.peer(at.b2))
            self.send(group, at.p, j, at.f ^ j, self.sc.at[group, 0, j], at.peer(1))

    def second(self, group):
        at = self.at
        q = at.p ^ at.b1
        for j in range(1, at.parts):
            self.arrived(group, q, j)
            self.send(group, q, j, at.f ^ j, self.s2.at[group, 1, j], at.peer(at.b2))
            self.send(group, q, j, at.f ^ j, self.sc.at[group, 1, j], at.peer(1))

    def third(self, group):
        at = self.at
        for slot, bits in ((2, at.b2), (3, at.b1 ^ at.b2)):
            for j in range(1, at.parts):
                self.arrived(group, at.p ^ bits, j)
                self.send(group, at.p ^ bits, j, at.f ^ j, self.sc.at[group, slot, j], at.peer(1))

    def ready(self, group):
        at = self.at
        for bits in (1, 3, 5, 7):
            for j in range(1, at.parts):
                self.arrived(group, at.p ^ bits, j)

    def finish(self):
        for item in self.sends:
            self.act(*item)


def layer_kernel(
    x_ref, up_ref, gains_ref, cos_ref, low_ref, high_ref, bias_ref, in_a, in_b,
    out_ref, grad_ref, xt_ref, dy_ref, gain_ref,
    wa, wb, probs, kv, rot, dkv, c4s, c4r, c2s, c2r, c1s, c1r, att, gate, lifted,
    local, zs, s1, s2, sc, recv, kvs, kvr, ds, dr,
):
    at = Place()
    p = at.p
    tokens, width = x_ref.shape
    half = wa.shape[2]
    keys = half - width
    group = HEADS // KV_HEADS
    scale = 1.0 / math.sqrt(HEAD)
    parts = at.parts
    high = half // parts
    wide_heads = group * tokens

    weights = Weights(at, in_a, in_b, wa, wb, local, zs, s1, s2, sc, recv)
    own = weights.keep()
    for copy in own:
        copy.start()
    at.barrier()
    for index in range(4):
        weights.along(index)

    residual = x_ref[...].astype(F32)
    inverse_first = lax.rsqrt(jnp.mean(residual * residual, axis=-1, keepdims=True) + EPS)
    normed_first = (residual * inverse_first * gains_ref[0:1, :]).astype(BF16)
    xt_ref[0] = normed_first.T
    xt_ref[3] = up_ref[...].T

    weights.first(0)
    weights.second(0)
    weights.first(1)
    weights.third(0)
    for copy in own:
        copy.wait()
    weights.ready(0)

    def turn(value, sign):
        tiles = []
        for tile in range(half // 128):
            part = value[:, tile * 128 : (tile + 1) * 128]
            swapped = pltpu.roll(part, HEAD // 2, 1) * low_ref[...] + pltpu.roll(part, 128 - HEAD // 2, 1) * high_ref[...]
            tiles.append(part * cos_ref[...] + swapped if sign > 0 else part * cos_ref[...] - swapped)
        return tiles

    qk = jnp.dot(normed_first, wa[0], preferred_element_type=F32)
    for tile, value in enumerate(turn(qk, 1)):
        rot[:, tile * 128 : (tile + 1) * 128] = value.astype(BF16)
    values = jnp.dot(normed_first, wa[1, :, width:], preferred_element_type=F32).astype(BF16)
    kv[p, :, :keys] = rot[:, width:]
    kv[p, :, keys:] = values

    def block(q, slot, target):
        return remote(kv.at[q], kv.at[q], kvs.at[slot], kvr.at[q], target)

    sent = [block(p, 0, at.peer(at.b1)), block(p, 1, at.peer(at.b2)), block(p, 2, at.peer(1))]
    for copy in sent:
        copy.start()

    def pass_on(q, slots):
        block(q, 0, at.peer(1)).wait_recv()
        for slot, target in slots:
            copy = block(q, slot, target)
            copy.start()
            sent.append(copy)

    pass_on(p ^ at.b1, [(3, at.peer(at.b2)), (4, at.peer(1))])
    pass_on(p ^ at.b2, [(5, at.peer(1))])
    pass_on(p ^ at.b1 ^ at.b2, [(6, at.peer(1))])
    for bits in (1, 3, 5, 7):
        pass_on(p ^ bits, [])

    weights.second(1)
    weights.first(2)
    weights.third(1)

    def keys_of(g):
        return kv[:, :, g * HEAD : (g + 1) * HEAD].reshape(CLASSES * tokens, HEAD)

    def values_of(g):
        return kv[:, :, keys + g * HEAD : keys + (g + 1) * HEAD].reshape(CLASSES * tokens, HEAD)

    def heads_of(ref, g):
        return jnp.concatenate([ref[:, h * HEAD : (h + 1) * HEAD] for h in range(g * group, (g + 1) * group)], axis=0)

    for g in range(KV_HEADS):
        scores = contract(keys_of(g), heads_of(rot, g), 1, 1) * scale
        bias = bias_ref[...]
        scores = scores + jnp.concatenate([bias] * group, axis=1)
        top = jnp.max(scores, axis=0, keepdims=True)
        expo = jnp.exp(scores - top)
        total = jnp.sum(expo, axis=0, keepdims=True)
        chance = expo * (1.0 / total)
        probs[g] = chance
        mixed = contract(values_of(g), chance.astype(BF16), 0, 0)
        turned = mixed.T.astype(BF16)
        for h in range(group):
            at_lane = (g * group + h) * HEAD
            att[:, at_lane : at_lane + HEAD] = turned[h * tokens : (h + 1) * tokens]

    weights.second(2)
    weights.first(3)
    weights.third(2)
    weights.ready(1)

    xt_ref[1] = att[...].T
    middle = residual + jnp.dot(att[...], wa[1, :, :width], preferred_element_type=F32)
    inverse_second = lax.rsqrt(jnp.mean(middle * middle, axis=-1, keepdims=True) + EPS)
    normed_second = (middle * inverse_second * gains_ref[1:2, :]).astype(BF16)
    xt_ref[2] = normed_second.T
    for side in range(2):
        lanes = slice(side * half, (side + 1) * half)
        gate[:, lanes] = jnp.dot(normed_second, wa[2 + side], preferred_element_type=F32)
    weights.second(3)
    weights.ready(2)
    weights.third(3)
    for side in range(2):
        lanes = slice(side * half, (side + 1) * half)
        lifted[:, lanes] = jnp.dot(normed_second, wa[4 + side], preferred_element_type=F32)
    weights.ready(3)

    hidden = (gate[...] * jax.nn.sigmoid(gate[...]) * lifted[...]).astype(BF16)
    for side in range(2):
        dy_ref[6 + side] = jnp.concatenate(
            [hidden[:, (2 * s + side) * high : (2 * s + side + 1) * high] for s in range(parts)], axis=1
        )
    out_ref[...] = (
        middle
        + jnp.dot(dy_ref[6], wb[0], preferred_element_type=F32)
        + jnp.dot(dy_ref[7], wb[1], preferred_element_type=F32)
    ).astype(BF16)

    upstream = up_ref[...]
    turned_sides = [contract(upstream, wb[side], 1, 1) for side in range(2)]
    grad_hidden = jnp.concatenate(
        [turned_sides[i % 2][:, (i // 2) * high : (i // 2 + 1) * high] for i in range(2 * parts)], axis=1
    )
    sigma = jax.nn.sigmoid(gate[...])
    grad_gate = (grad_hidden * lifted[...] * sigma * (1.0 + gate[...] * (1.0 - sigma))).astype(BF16)
    grad_lifted = (grad_hidden * gate[...] * sigma).astype(BF16)
    grad_normed = jnp.zeros((tokens, width), F32)
    for side in range(2):
        lanes = slice(side * half, (side + 1) * half)
        dy_ref[2 + side] = grad_gate[:, lanes]
        dy_ref[4 + side] = grad_lifted[:, lanes]
        grad_normed = grad_normed + contract(grad_gate[:, lanes], wa[2 + side], 1, 1)
        grad_normed = grad_normed + contract(grad_lifted[:, lanes], wa[4 + side], 1, 1)

    def norm_back(value, inverse, gain, incoming):
        scaled = incoming * gain
        mean = jnp.mean(scaled * value, axis=-1, keepdims=True)
        through = inverse * scaled - value * (inverse * inverse * inverse) * mean
        return through, jnp.sum(incoming * value * inverse, axis=0, keepdims=True)

    through, gain_second = norm_back(middle, inverse_second, gains_ref[1:2, :], grad_normed)
    gain_ref[...] = jnp.zeros_like(gain_ref)
    gain_ref[1:2, :] = gain_second
    grad_middle = upstream.astype(F32) + through
    grad_branch = grad_middle.astype(BF16)
    dy_ref[1, :, :width] = grad_branch
    dy_ref[1, :, width:] = jnp.zeros((tokens, keys), BF16)
    att[...] = contract(grad_branch, wa[1, :, :width], 1, 1).astype(BF16)

    queries = []
    for g in range(KV_HEADS):
        chance = probs[g]
        out_grad = heads_of(att, g)
        query = heads_of(rot, g)
        grad_probs = contract(values_of(g), out_grad, 1, 1)
        delta = jnp.sum(grad_probs * chance, axis=0, keepdims=True)
        grad_scores = (chance * (grad_probs - delta)).astype(BF16)
        grad_values = jnp.dot(chance.astype(BF16), out_grad, preferred_element_type=F32)
        grad_keys = jnp.dot(grad_scores, query, preferred_element_type=F32) * scale
        dkv[:, :, g * HEAD : (g + 1) * HEAD] = grad_keys.reshape(CLASSES, tokens, HEAD)
        dkv[:, :, keys + g * HEAD : keys + (g + 1) * HEAD] = grad_values.reshape(CLASSES, tokens, HEAD)
        turned = contract(keys_of(g), grad_scores, 0, 0).T * scale
        for h in range(group):
            at_lane = (g * group + h) * HEAD
            gate[:, at_lane : at_lane + HEAD] = turned[h * tokens : (h + 1) * tokens]

    def halve(bit, rest, sbuf, rbuf, index):
        copies = []
        for i, bits in enumerate(rest):
            sbuf[i] = dkv[p ^ bit ^ bits].astype(BF16)
        copy = remote(sbuf, rbuf, ds.at[index], dr.at[index], at.peer(bit))
        copy.start()
        copy.wait()
        for i, bits in enumerate(rest):
            dkv[p ^ bits] = dkv[p ^ bits] + rbuf[i].astype(F32)

    halve(1, (0, 2, 4, 6), c4s, c4r, 0)
    halve(at.b1, (0, at.b2), c2s, c2r, 1)
    halve(at.b2, (0,), c1s, c1r, 2)

    gate[:, width:half] = dkv[p, :, :keys]
    for tile, value in enumerate(turn(gate[:, :half], -1)):
        dy_ref[0, :, tile * 128 : (tile + 1) * 128] = value.astype(BF16)
    dy_ref[8, :, :width] = jnp.zeros((tokens, width), BF16)
    dy_ref[8, :, width:] = dkv[p, :, keys:].astype(BF16)
    grad_normed = contract(dy_ref[0], wa[0], 1, 1) + contract(dy_ref[8], wa[1], 1, 1)
    through, gain_first = norm_back(residual, inverse_first, gains_ref[0:1, :], grad_normed)
    gain_ref[0:1, :] = gain_first
    grad_ref[...] = grad_middle + through

    weights.finish()
    for copy in sent:
        copy.wait_send()


def layer_pass(x, up, gains, tables, bias, wide, tall):
    parts = lax.axis_size("fsdp")
    tokens, width = x.shape
    _, rows, half = wide.shape
    high = tall.shape[1]
    dma = pltpu.SemaphoreType.DMA
    vm = pltpu.VMEM
    group = HEADS // KV_HEADS
    two = 2 * (half - width)
    return pl.pallas_call(
        layer_kernel,
        out_shape=(
            jax.ShapeDtypeStruct((tokens, width), BF16),
            jax.ShapeDtypeStruct((tokens, width), F32),
            jax.ShapeDtypeStruct((4, width, tokens), BF16),
            jax.ShapeDtypeStruct((9, tokens, half), BF16),
            jax.ShapeDtypeStruct((8, width), F32),
        ),
        in_specs=[VMEM] * 7 + [ANY, ANY],
        out_specs=(VMEM,) * 5,
        scratch_shapes=[
            vm((WIDE, parts * rows, half), BF16),
            vm((2, parts * high, width), BF16),
            vm((KV_HEADS, CLASSES * tokens, group * tokens), F32),
            vm((CLASSES, tokens, two), BF16),
            vm((tokens, half), BF16),
            vm((CLASSES, tokens, two), F32),
            vm((4, tokens, two), BF16),
            vm((4, tokens, two), BF16),
            vm((2, tokens, two), BF16),
            vm((2, tokens, two), BF16),
            vm((1, tokens, two), BF16),
            vm((1, tokens, two), BF16),
            vm((tokens, width), BF16),
            vm((tokens, 2 * half), F32),
            vm((tokens, 2 * half), F32),
            dma((2,)), dma((4, parts)), dma((4, parts)), dma((4, 2, parts)), dma((4, 4, parts)),
            dma((4, CLASSES, parts)), dma((7,)), dma((CLASSES,)), dma((3,)), dma((3,)),
        ],
        compiler_params=pltpu.CompilerParams(
            collective_id=3, has_side_effects=True, vmem_limit_bytes=62 << 20
        ),
        name="layer_pass",
    )(x, up, gains, *tables, bias, wide, tall)


def rotary_tables(positions, width):
    half = width // 2
    frequency = THETA ** (-(jnp.arange(half, dtype=jnp.float32) * 2.0 / width))
    angle = positions.astype(jnp.float32)[:, None] * frequency[None, :]
    return (jnp.cos(angle)[:, None, :], jnp.sin(angle)[:, None, :])


def rotate(value, cosine, sine):
    half = value.shape[-1] // 2
    first = value[..., :half]
    second = value[..., half:]
    return jnp.concatenate(
        [first * cosine - second * sine, second * cosine + first * sine], axis=-1
    )


def unrotate(incoming, cosine, sine):
    half = incoming.shape[-1] // 2
    upper = incoming[..., :half]
    lower = incoming[..., half:]
    return jnp.concatenate([upper * cosine + lower * sine, lower * cosine - upper * sine], axis=-1)


def norm_forward(residual, gain):
    inverse = lax.rsqrt(jnp.mean(residual * residual, axis=-1, keepdims=True) + EPS)
    return ((residual * inverse * gain).astype(jnp.bfloat16), inverse)


def norm_backward(residual, inverse, gain, incoming):
    scaled = incoming * gain
    through = inverse * scaled - residual * inverse**3 * jnp.mean(
        scaled * residual, axis=-1, keepdims=True
    )
    return (through, jnp.sum(incoming * residual * inverse, axis=0))


def padded(array, axis, parts, count, full):
    if count == full:
        return array
    shape = array.shape
    split = array.reshape(shape[:axis] + (parts, count) + shape[axis + 1 :])
    pads = [(0, 0)] * split.ndim
    pads[axis + 1] = (0, full - count)
    return jnp.pad(split, pads).reshape(shape[:axis] + (parts * full,) + shape[axis + 1 :])


def trimmed(array, axis, parts, count, full):
    if count == full:
        return array
    shape = array.shape
    split = array.reshape(shape[:axis] + (parts, full) + shape[axis + 1 :])
    kept = lax.slice_in_dim(split, 0, count, axis=axis + 1)
    return kept.reshape(shape[:axis] + (parts * count,) + shape[axis + 1 :])


def plain_layer(
    layer_input, output_grad, wide, tall, norm_gains, block_order, sizes
):
    parts, width, half, kv, short, full, high = sizes
    hidden_size = 2 * half
    rows = layer_input.shape[1]
    block = rows // 2
    group = HEADS // KV_HEADS
    scale = 1.0 / math.sqrt(HEAD)
    ctx_place = lax.axis_index("ctx")
    offsets = jnp.arange(block, dtype=jnp.int32)
    own_blocks = lax.dynamic_slice_in_dim(block_order, 2 * ctx_place, 2)
    query_pos = (own_blocks[:, None] * block + offsets[None, :]).reshape(rows)
    key_pos = (block_order[:, None] * block + offsets[None, :]).reshape(-1)

    all_wide, all_tall = gather_weights(wide, tall)
    w_qk, w_ov, w_gate_0, w_gate_1, w_up_0, w_up_1 = [all_wide[i].reshape(width, half) for i in range(WIDE)]
    w_down = [all_tall[i].reshape(half, width) for i in range(2)]

    residual = layer_input[0].astype(jnp.float32)
    normed_first, inverse_first = norm_forward(residual, norm_gains[0])
    qk_pre = jnp.dot(normed_first, w_qk, preferred_element_type=jnp.float32)
    query_pre = qk_pre[:, :width].reshape(rows, HEADS, HEAD)
    key_pre = qk_pre[:, width:].reshape(rows, KV_HEADS, HEAD)
    value_low = (
        jnp.dot(normed_first, w_ov, preferred_element_type=jnp.float32)[:, width:]
        .astype(jnp.bfloat16)
        .reshape(rows, KV_HEADS, HEAD)
    )
    cosine, sine = rotary_tables(query_pos, HEAD)
    query_rot = rotate(query_pre, cosine, sine).astype(jnp.bfloat16)
    key_rot = rotate(key_pre, cosine, sine).astype(jnp.bfloat16)
    keys_all, values_all = (
        lax.all_gather(key_rot, "ctx", axis=0, tiled=True),
        lax.all_gather(value_low, "ctx", axis=0, tiled=True),
    )
    keys_head = keys_all.transpose(1, 0, 2)
    values_head = values_all.transpose(1, 0, 2)
    queries_head = (
        query_rot.reshape(rows, KV_HEADS, group, HEAD)
        .transpose(1, 2, 0, 3)
        .reshape(KV_HEADS, group * rows, HEAD)
    )
    row_pos = jnp.tile(query_pos, group)
    allowed = key_pos[None, :] <= row_pos[:, None]

    def head_forward(item):
        query, key, value = item
        scores = jnp.where(allowed, contract(query, key, 1, 1) * scale, MASKED)
        top = jnp.max(scores, axis=-1, keepdims=True)
        expo = jnp.exp(scores - top)
        total = jnp.sum(expo, axis=-1, keepdims=True)
        probs_low = (expo / total).astype(jnp.bfloat16)
        return (
            jnp.dot(probs_low, value, preferred_element_type=jnp.float32),
            (top + jnp.log(total))[:, 0],
        )

    mixed, log_total = lax.map(head_forward, (queries_head, keys_head, values_head))
    attended = (
        mixed.reshape(KV_HEADS, group, rows, HEAD)
        .transpose(2, 0, 1, 3)
        .reshape(rows, HEADS * HEAD)
        .astype(jnp.bfloat16)
    )
    w_out = w_ov[:, :width]
    middle = residual + jnp.dot(attended, w_out, preferred_element_type=jnp.float32)
    normed_second, inverse_second = norm_forward(middle, norm_gains[1])

    def sides(left, right):
        return jnp.concatenate([left, right], axis=1)

    gate = sides(
        jnp.dot(normed_second, w_gate_0, preferred_element_type=jnp.float32),
        jnp.dot(normed_second, w_gate_1, preferred_element_type=jnp.float32),
    )
    lifted = sides(
        jnp.dot(normed_second, w_up_0, preferred_element_type=jnp.float32),
        jnp.dot(normed_second, w_up_1, preferred_element_type=jnp.float32),
    )
    sigma = jax.nn.sigmoid(gate)
    hidden = (gate * sigma * lifted).astype(jnp.bfloat16)
    hidden_split = hidden.reshape(rows, parts, 2, high)
    hidden_sides = [hidden_split[:, :, i].reshape(rows, half) for i in range(2)]
    layer_output = (
        middle
        + jnp.dot(hidden_sides[0], w_down[0], preferred_element_type=jnp.float32)
        + jnp.dot(hidden_sides[1], w_down[1], preferred_element_type=jnp.float32)
    ).astype(jnp.bfloat16)
    upstream = output_grad[0]
    grad_hidden = jnp.stack(
        [contract(upstream, w_down[i], 1, 1).reshape(rows, parts, high) for i in range(2)], axis=2
    ).reshape(rows, hidden_size)
    grad_gate = (grad_hidden * lifted * sigma * (1.0 + gate * (1.0 - sigma))).astype(jnp.bfloat16)
    grad_lifted = (grad_hidden * gate * sigma).astype(jnp.bfloat16)
    grad_normed_second = (
        contract(grad_gate[:, :half], w_gate_0, 1, 1)
        + contract(grad_gate[:, half:], w_gate_1, 1, 1)
        + contract(grad_lifted[:, :half], w_up_0, 1, 1)
        + contract(grad_lifted[:, half:], w_up_1, 1, 1)
    )
    through_second, gain_second = norm_backward(
        middle, inverse_second, norm_gains[1], grad_normed_second
    )
    grad_middle = upstream.astype(jnp.float32) + through_second
    grad_branch = grad_middle.astype(jnp.bfloat16)
    grad_attended = contract(grad_branch, w_out, 1, 1).astype(jnp.bfloat16)
    grad_heads = (
        grad_attended.reshape(rows, KV_HEADS, group, HEAD)
        .transpose(1, 2, 0, 3)
        .reshape(KV_HEADS, group * rows, HEAD)
    )

    def head_backward(item):
        query, key, value, grad_out, log_row = item
        scores = jnp.where(allowed, contract(query, key, 1, 1) * scale, MASKED)
        probs = jnp.exp(scores - log_row[:, None])
        grad_value_part = contract(probs.astype(jnp.bfloat16), grad_out, 0, 0)
        grad_probs = contract(grad_out, value, 1, 1)
        grad_scores = (
            probs * (grad_probs - jnp.sum(grad_probs * probs, axis=-1, keepdims=True))
        ).astype(jnp.bfloat16)
        grad_query_part = jnp.dot(grad_scores, key, preferred_element_type=jnp.float32) * scale
        grad_key_part = contract(grad_scores, query, 0, 0) * scale
        return (grad_query_part, grad_key_part, grad_value_part)

    grad_query_rot, grad_key_all, grad_value_all = lax.map(
        head_backward, (queries_head, keys_head, values_head, grad_heads, log_total)
    )
    grad_key_own, grad_value_own = (
        lax.psum_scatter(
            grad_key_all.astype(jnp.bfloat16), "ctx", scatter_dimension=1, tiled=True
        ).astype(jnp.float32),
        lax.psum_scatter(
            grad_value_all.astype(jnp.bfloat16), "ctx", scatter_dimension=1, tiled=True
        ).astype(jnp.float32),
    )
    grad_query = (
        unrotate(
            grad_query_rot.reshape(KV_HEADS, group, rows, HEAD)
            .transpose(2, 0, 1, 3)
            .reshape(rows, HEADS, HEAD),
            cosine,
            sine,
        )
        .reshape(rows, HEADS * HEAD)
        .astype(jnp.bfloat16)
    )
    grad_key = (
        unrotate(grad_key_own.transpose(1, 0, 2), cosine, sine)
        .reshape(rows, KV_HEADS * HEAD)
        .astype(jnp.bfloat16)
    )
    grad_value = (
        grad_value_own.transpose(1, 0, 2).reshape(rows, KV_HEADS * HEAD).astype(jnp.bfloat16)
    )
    grad_qk = sides(grad_query, grad_key)
    zero_query = jnp.zeros((rows, width), jnp.bfloat16)
    grad_v = sides(zero_query, grad_value)
    grad_normed_first = contract(grad_qk, w_qk, 1, 1) + contract(grad_v, w_ov, 1, 1)
    through_first, gain_first = norm_backward(
        residual, inverse_first, norm_gains[0], grad_normed_first
    )
    input_gradient = grad_middle + through_first

    xt = jnp.stack([item.T for item in (normed_first, attended, normed_second, upstream)])
    xt = padded(xt, 1, parts, short, full)
    dy = jnp.stack(
        [
            grad_qk,
            sides(grad_branch, jnp.zeros((rows, kv), jnp.bfloat16)),
            grad_gate[:, :half],
            grad_gate[:, half:],
            grad_lifted[:, :half],
            grad_lifted[:, half:],
            hidden_sides[0],
            hidden_sides[1],
            grad_v,
        ]
    )
    gains = jnp.pad(jnp.stack([gain_first, gain_second]), ((0, 6), (0, 0)))
    return layer_output, input_gradient, xt, dy, gains


def fused_layer(
    layer_input, output_grad, wide, tall, norm_gains, block_order, sizes
):
    rows = layer_input.shape[1]
    block = rows // 2
    ctx_place = lax.axis_index("ctx")
    offsets = jnp.arange(block, dtype=jnp.int32)
    own_blocks = lax.dynamic_slice_in_dim(block_order, 2 * ctx_place, 2)
    query_pos = (own_blocks[:, None] * block + offsets[None, :]).reshape(rows)
    key_pos = (block_order[:, None] * block + offsets[None, :]).reshape(-1)
    bias = jnp.where(key_pos[:, None] <= query_pos[None, :], 0.0, MASKED).astype(jnp.float32)
    lane = jnp.arange(128, dtype=jnp.int32)
    index = (lane % (HEAD // 2)).astype(jnp.float32)
    frequency = THETA ** (-(index * 2.0 / HEAD))
    angle = query_pos.astype(jnp.float32)[:, None] * frequency[None, :]
    cosine, sine = jnp.cos(angle), jnp.sin(angle)
    early = (lane % HEAD < HEAD // 2)[None, :]
    tables = (cosine, jnp.where(early, 0.0, sine), jnp.where(early, -sine, 0.0))
    return layer_pass(layer_input[0], output_grad[0], norm_gains, tables, bias, wide, tall)


def on_device(
    layer_input,
    output_grad,
    query_weight,
    key_weight,
    value_weight,
    output_weight,
    gate_weight,
    up_weight,
    down_weight,
    norm_gains,
    query_momentum,
    key_momentum,
    value_momentum,
    output_momentum,
    gate_momentum,
    up_momentum,
    down_momentum,
    gain_momentum,
    block_order,
):
    parts = lax.axis_size("fsdp")
    width = layer_input.shape[2]
    half = gate_weight.shape[1] // 2
    kv = key_weight.shape[1]
    short = width // parts
    full = -(-short // 16) * 16
    high = half // parts
    sizes = (parts, width, half, kv, short, full, high)

    def sides(left, right):
        return jnp.concatenate([left, right], axis=1)

    wide = jnp.stack(
        [
            jnp.concatenate([query_weight, key_weight], axis=1),
            jnp.concatenate([output_weight, value_weight], axis=1),
            gate_weight[:, :half],
            gate_weight[:, half:],
            up_weight[:, :half],
            up_weight[:, half:],
        ]
    )
    tall = down_weight.reshape(2, high, width)
    fused = lax.axis_size("ctx") == CLASSES and short == full and layer_input.shape[1] == 128
    layer = fused_layer if fused else plain_layer
    layer_output, input_gradient, xt, dy, gains = layer(
        layer_input, output_grad, wide, tall, norm_gains, block_order, sizes
    )

    def pad_rows(array):
        return padded(array, 0, 1, short, full)

    def pad_columns(array):
        return padded(array, 1, parts, short, full)

    moments = (
        pad_rows(sides(query_momentum, key_momentum)),
        pad_rows(sides(output_momentum, value_momentum)),
        pad_rows(gate_momentum),
        pad_rows(up_momentum),
        pad_columns(down_momentum),
    )
    g_wide, g_tall, s_wide, s_tall, gain_sum = reduce_gradients(xt, dy, gains, moments, full, high)
    o_wide, o_tall = orthogonalize(s_wide, s_tall, full, high, width)

    def unpack(wide_pieces, tall_pieces):
        pieces = wide_pieces[:, :short]
        tall = trimmed(tall_pieces, 2, parts, short, full).reshape(2 * high, width)
        return (
            pieces[0, :, :width],
            pieces[0, :, width:],
            pieces[1, :, width:],
            pieces[1, :, :width],
            sides(pieces[2], pieces[3]),
            sides(pieces[4], pieces[5]),
            tall,
        )

    gradients = [item.astype(jnp.float32) for item in unpack(g_wide, g_tall)]
    orthos = unpack(o_wide, o_tall)
    olds = (
        query_momentum,
        key_momentum,
        value_momentum,
        output_momentum,
        gate_momentum,
        up_momentum,
        down_momentum,
    )
    moments = [MOMENTUM * old + new for old, new in zip(olds, gradients)]
    old_weights = (
        query_weight,
        key_weight,
        value_weight,
        output_weight,
        gate_weight,
        up_weight,
        down_weight,
    )
    new_weights = []
    for index in range(len(olds)):
        cols_full = old_weights[index].shape[1]
        rows_full = old_weights[index].shape[0] * parts
        step_rate = OUT_RATE if index == 3 else RATE
        factor = -step_rate * max(1.0, cols_full / rows_full) ** 0.5
        new_weights.append(
            old_weights[index].astype(jnp.float32) + factor * orthos[index].astype(jnp.float32)
        )
    gain_width = norm_gains.shape[1] // parts
    place = lax.axis_index("fsdp") * gain_width
    gain_gradient = lax.dynamic_slice_in_dim(gain_sum[:2], place, gain_width, 1)
    gain_shard = lax.dynamic_slice_in_dim(norm_gains, place, gain_width, 1)
    gain_moment = MOMENTUM * gain_momentum + gain_gradient
    new_gains = gain_shard - GAIN_RATE * gain_moment
    return (
        layer_output[None],
        input_gradient[None],
        *gradients,
        gain_gradient,
        *moments,
        gain_moment,
        *new_weights,
        new_gains,
    )


def solution(mesh):
    tokens = P("fsdp", "ctx", None)
    shard = P("fsdp", None)
    gains = P(None, "fsdp")
    return jax.shard_map(
        on_device,
        mesh=mesh,
        in_specs=(tokens, tokens) + (shard,) * 7 + (P(),) + (shard,) * 7 + (gains, P()),
        out_specs=(tokens, tokens) + ((shard,) * 7 + (gains,)) * 3,
        check_vma=False,
    )
```

```python
import functools
import math

import jax
import jax.numpy as jnp
from jax import lax
from jax.experimental import pallas as pl
from jax.experimental.pallas import tpu as pltpu
from jax.sharding import PartitionSpec as P

HEADS = 15
KV_HEADS = 5
HEAD = 64
NS_ITERS = 5


EPS = 1e-05
THETA = 100000.0
NS_A = 3.4445
NS_B = -4.775
NS_C = 2.0315
MOMENTUM = 0.95
RATE = 0.2
OUT_RATE = 6.0
GAIN_RATE = 0.002
MASKED = -1e30

MESH = pl.DeviceIdType.MESH
BF16 = jnp.bfloat16
F32 = jnp.float32
ANY = pl.BlockSpec(memory_space=pl.ANY)
VMEM = pl.BlockSpec(memory_space=pltpu.VMEM)
CLASSES = 8
WIDE = 6


def contract(left, right, left_dim, right_dim):
    return lax.dot_general(
        left, right, (((left_dim,), (right_dim,)), ((), ())), preferred_element_type=jnp.float32
    )


class Place:
    def __init__(self):
        self.parts = lax.axis_size("fsdp")
        self.extra = lax.axis_size("ctx") // CLASSES
        self.c = lax.axis_index("ctx")
        self.f = lax.axis_index("fsdp")
        self.p = lax.rem(self.c, CLASSES)
        self.core = lax.rem(self.c, 2)
        self.b1 = jnp.where(self.core == 0, 2, 4)
        self.b2 = jnp.where(self.core == 0, 4, 2)

    def peer(self, bits):
        return (self.c ^ bits, self.f)

    def along(self, j):
        return (self.c, self.f ^ j)

    def other(self, j):
        groups = self.extra
        return (lax.rem(self.c + CLASSES * j, CLASSES * groups), self.f)

    def barrier(self, bits=(1, 2, 4), line=True, others=False):
        sem = pltpu.get_barrier_semaphore()
        targets = [self.peer(b) for b in bits]
        if line:
            targets += [self.along(j) for j in range(1, self.parts)]
        if others:
            targets += [self.other(j) for j in range(1, self.extra)]
        for target in targets:
            pl.semaphore_signal(sem, inc=1, device_id=target, device_id_type=MESH)
        pl.semaphore_wait(sem, len(targets))


def remote(src, dst, send, recv, target):
    return pltpu.make_async_remote_copy(
        src_ref=src, dst_ref=dst, send_sem=send, recv_sem=recv, device_id=target, device_id_type=MESH
    )


def by_kind(cls, wide, tall):
    pl.when(cls < WIDE)(wide)
    pl.when(cls >= WIDE)(tall)


def weights_kernel(in_a, in_b, out_a, out_b, local, zs, s1, s2, sc, recv):
    at = Place()
    p, f, parts = at.p, at.f, at.parts
    at.barrier()
    copies = [
        pltpu.make_async_copy(in_a, out_a.at[:, f], local.at[0]),
        pltpu.make_async_copy(in_b, out_b.at[:, f], local.at[1]),
    ]
    for copy in copies:
        copy.start()

    def act(cls, j, g, send, target, what, first=False):
        def wide():
            dst = out_a.at[cls, g]
            src = in_a.at[cls] if first else dst
            getattr(remote(src, dst, send, recv.at[cls, j], target), what)()

        def tall():
            dst = out_b.at[cls - WIDE, g]
            src = in_b.at[cls - WIDE] if first else dst
            getattr(remote(src, dst, send, recv.at[cls, j], target), what)()

        by_kind(cls, wide, tall)

    sends = []

    def send(cls, j, g, sem, target, first=False):
        act(cls, j, g, sem, target, "start", first)
        sends.append((cls, j, g, sem, target, first))

    def arrived(cls, j):
        act(cls, j, f ^ j, zs.at[j], at.along(j), "wait_recv")

    for j in range(1, parts):
        send(p, j, f, zs.at[j], at.along(j), True)
    for j in range(1, parts):
        arrived(p, j)
        send(p, j, f ^ j, s1.at[0, j], at.peer(at.b1))
        send(p, j, f ^ j, s2.at[0, j], at.peer(at.b2))
        send(p, j, f ^ j, sc.at[0, j], at.peer(1))
    for j in range(1, parts):
        arrived(p ^ at.b1, j)
        send(p ^ at.b1, j, f ^ j, s2.at[1, j], at.peer(at.b2))
        send(p ^ at.b1, j, f ^ j, sc.at[1, j], at.peer(1))
    for slot, bits in ((2, at.b2), (3, at.b1 ^ at.b2)):
        for j in range(1, parts):
            arrived(p ^ bits, j)
            send(p ^ bits, j, f ^ j, sc.at[slot, j], at.peer(1))
    for bits in (1, 3, 5, 7):
        for j in range(1, parts):
            arrived(p ^ bits, j)
    for cls, j, g, sem, target, first in sends:
        act(cls, j, g, sem, target, "wait_send", first)
    for copy in copies:
        copy.wait()


def gather_weights(wide, tall):
    parts = lax.axis_size("fsdp")
    dma = pltpu.SemaphoreType.DMA
    return pl.pallas_call(
        weights_kernel,
        out_shape=(
            jax.ShapeDtypeStruct((WIDE, parts) + wide.shape[1:], BF16),
            jax.ShapeDtypeStruct((CLASSES - WIDE, parts) + tall.shape[1:], BF16),
        ),
        in_specs=[ANY, ANY],
        out_specs=(ANY, ANY),
        scratch_shapes=[
            dma((2,)),
            dma((parts,)),
            dma((1, parts)),
            dma((2, parts)),
            dma((4, parts)),
            dma((CLASSES, parts)),
        ],
        compiler_params=pltpu.CompilerParams(collective_id=0, has_side_effects=True),
        name="gather_weights",
    )(wide, tall)


def spread(at, own_a, own_b, out_a, out_b, local, ss, recv):
    p = at.p

    def act(cls, sem, target, what, first=False):
        def wide():
            dst = out_a.at[cls]
            getattr(remote(own_a if first else dst, dst, sem, recv.at[cls], target), what)()

        def tall():
            dst = out_b.at[cls - WIDE]
            getattr(remote(own_b if first else dst, dst, sem, recv.at[cls], target), what)()

        by_kind(cls, wide, tall)

    def keep(what):
        def wide():
            getattr(pltpu.make_async_copy(own_a, out_a.at[p], local), what)()

        def tall():
            getattr(pltpu.make_async_copy(own_b, out_b.at[p - WIDE], local), what)()

        by_kind(p, wide, tall)

    sends = []

    def send(cls, slot, target, first=False):
        act(cls, ss.at[slot], target, "start", first)
        sends.append((cls, slot, target, first))

    def arrived(cls):
        act(cls, ss.at[0], at.peer(1), "wait_recv")

    send(p, 0, at.peer(at.b1), True)
    send(p, 1, at.peer(at.b2), True)
    send(p, 2, at.peer(1), True)
    keep("start")

    def finish():
        arrived(p ^ at.b1)
        send(p ^ at.b1, 3, at.peer(at.b2))
        send(p ^ at.b1, 4, at.peer(1))
        arrived(p ^ at.b2)
        send(p ^ at.b2, 5, at.peer(1))
        arrived(p ^ at.b1 ^ at.b2)
        send(p ^ at.b1 ^ at.b2, 6, at.peer(1))
        for bits in (1, 3, 5, 7):
            arrived(p ^ bits)
        for cls, slot, target, first in sends:
            act(cls, ss.at[slot], target, "wait_send", first)
        keep("wait")

    return finish


def reduce_kernel(
    parts, extra, high,
    xt_in, dy_in, gain_in, m_qk, m_ov, m_gate, m_up, m_down,
    g_a, g_b, s_a, s_b, gain_out,
    xt, dy, p1s, p1r, p2s, p2r, own, own_t, za_s, za_r, zb_s, zb_r, ma, mb, ga, gb, sa, sb, es, er, gain_s, gain_r,
    ls, xs, xr, s1, r1, s2, r2, zs, zr, esem, ersem, msem, gs, gr, ag_l, ag_s, ag_r, ss, sr, sl,
):
    at = Place()
    p, f, core = at.p, at.f, at.core
    tokens = xt_in.shape[2]
    rows = ma.shape[0]
    half = dy.shape[2]

    def moment(what):
        for cls in range(CLASSES):
            @pl.when(p == cls)
            def _(cls=cls):
                side = cls % 2
                if cls < 2:
                    src, dst = (m_qk, m_ov)[cls], ma
                elif cls < WIDE:
                    whole = m_gate if cls < 4 else m_up
                    src, dst = whole.at[:, pl.ds(side * half, half)], ma
                else:
                    src, dst = m_down.at[pl.ds(side * high, high)], mb
                getattr(pltpu.make_async_copy(src, dst, msem), what)()

    moment("start")
    mine = [pltpu.make_async_copy(xt_in, xt.at[:, :, pl.ds(0, tokens)], ls.at[0])]
    for slot in range(4):
        mine.append(
            pltpu.make_async_copy(dy_in.at[core + 2 * slot], dy.at[slot, pl.ds(0, tokens)], ls.at[1 + slot])
        )
    mine.append(pltpu.make_async_copy(dy_in.at[8], dy.at[4, pl.ds(0, tokens)], ls.at[5]))
    for copy in mine:
        copy.start()
    at.barrier(others=True)
    pair = at.peer(1)
    theirs = [remote(xt_in, xt.at[:, :, pl.ds(tokens, tokens)], xs.at[0], xr.at[0], pair)]
    for slot in range(4):
        theirs.append(
            remote(dy_in.at[1 - core + 2 * slot], dy.at[slot, pl.ds(tokens, tokens)], xs.at[1 + slot], xr.at[1 + slot], pair)
        )
    theirs.append(remote(dy_in.at[8], dy.at[4, pl.ds(tokens, tokens)], xs.at[5], xr.at[5], pair))
    for copy in theirs:
        copy.start()

    def swap(slot, target):
        return remote(gain_s.at[slot], gain_r.at[slot], gs.at[slot], gr.at[slot], target)

    gain_s[0] = gain_in[...]
    swaps = [swap(0, pair)]
    swaps[0].start()
    for copy in mine:
        copy.wait()
    for copy in theirs:
        copy.wait()

    def term(cls, r):
        at_rows = pl.ds(pl.multiple_of(r * rows, rows), rows)
        slot = lax.div(cls, 2)
        kind = jnp.where(cls == 0, 0, jnp.where(cls == 1, 1, jnp.where(cls < WIDE, 2, 3)))
        value = jnp.dot(xt[kind, at_rows, :], dy[slot], preferred_element_type=F32)
        return value

    def with_values(cls, r, put):
        at_rows = pl.ds(pl.multiple_of(r * rows, rows), rows)

        @pl.when(cls == 1)
        def _():
            put(term(cls, r) + jnp.dot(xt[0, at_rows, :], dy[4], preferred_element_type=F32))

        @pl.when(cls != 1)
        def _():
            put(term(cls, r))

    def order(i):
        return lax.rem(f + 1 + i, parts)

    def one(slot, i):
        r = order(i)
        return remote(p1s.at[slot, r], p1r.at[slot, r], s1.at[slot, r], r1.at[slot, r], at.peer(at.b1))

    for slot, bits in ((0, at.b1 ^ at.b2), (1, at.b1)):
        def first(i, carry, slot=slot, bits=bits):
            r = order(i)

            def put(value):
                p1s[slot, r] = value.astype(BF16)

            with_values(p ^ bits, r, put)
            one(slot, i).start()
            return carry

        lax.fori_loop(0, parts, first, 0)

    swaps[0].wait()
    gain_s[1] = gain_s[0] + gain_r[0]
    swaps.append(swap(1, at.peer(2)))
    swaps[1].start()

    def two(i):
        r = order(i)
        return remote(p2s.at[r], p2r.at[r], s2.at[r], r2.at[r], at.peer(at.b2))

    def second(i, carry):
        r = order(i)
        one(0, i).wait_recv()

        def put(value):
            p2s[r] = (value + p1r[0, r].astype(F32)).astype(BF16)

        with_values(p ^ at.b2, r, put)
        two(i).start()
        return carry

    lax.fori_loop(0, parts, second, 0)
    swaps[1].wait()
    gain_s[2] = gain_s[1] + gain_r[1]
    swaps.append(swap(2, at.peer(4)))
    swaps[2].start()

    def line_a(r, source):
        return remote(za_s.at[r], za_r.at[source], zs.at[r], zr.at[source], (at.c, r))

    def line_b(r, source):
        return remote(
            zb_s.at[pl.ds(pl.multiple_of(r * high, high), high)],
            zb_r.at[source], zs.at[r], zr.at[source], (at.c, r),
        )

    early = extra == 1

    def third(i, carry):
        r = order(i)
        one(1, i).wait_recv()
        two(i).wait_recv()

        def put(value):
            total = value + p1r[1, r].astype(F32) + p2r[r].astype(F32)
            own[r] = total
            if early:
                za_s[r] = total.astype(BF16)

        with_values(p, r, put)
        if early:
            @pl.when((p < WIDE) & (i < parts - 1))
            def _():
                line_a(r, f).start()
        return carry

    lax.fori_loop(0, parts, third, 0)
    swaps[2].wait()
    gain_s[3] = gain_s[2] + gain_r[2]

    if not early:
        es[...] = own[...].astype(BF16)
        group = [
            remote(es, er.at[j - 1], esem.at[j - 1], ersem.at[j - 1], at.other(j)) for j in range(1, extra)
        ]
        for copy in group:
            copy.start()
        for j in range(1, extra):
            group[j - 1].wait_recv()
            own[...] = own[...] + er[j - 1].astype(F32)
        for copy in group:
            copy.wait_send()
        za_s[...] = own[...].astype(BF16)

        @pl.when(p < WIDE)
        def _():
            for j in range(1, parts):
                line_a(f ^ j, f).start()

    @pl.when(p >= WIDE)
    def _():
        for tile in range(half // 128):
            for r in range(parts):
                block = own[r, :, pl.ds(tile * 128, 128)]
                if rows % 128 == 0:
                    own_t[pl.ds(tile * 128, 128), pl.ds(r * rows, rows)] = block.T
            if rows % 128 != 0:
                column = own[:, :, pl.ds(tile * 128, 128)].reshape(parts * rows, 128)
                own_t[pl.ds(tile * 128, 128), :] = column.T
        zb_s[...] = own_t[...].astype(BF16)
        for j in range(1, parts):
            line_b(f ^ j, f).start()

    line_gain = [
        remote(gain_s.at[3], gain_r.at[3 + j], gs.at[3 + j], gr.at[3 + j], at.along(j)) for j in range(1, parts)
    ]
    other_gain = []
    for copy in line_gain:
        copy.start()

    moment("wait")

    @pl.when(p < WIDE)
    def _():
        total = own[f]
        for j in range(1, parts):
            line_a(f ^ j, f ^ j).wait_recv()
            total = total + za_r[f ^ j].astype(F32)
        ga[...] = total.astype(BF16)
        sa[...] = (MOMENTUM * ma[...] + total).astype(BF16)

    @pl.when(p >= WIDE)
    def _():
        total = own_t[pl.ds(pl.multiple_of(f * high, high), high), :]
        for j in range(1, parts):
            line_b(f ^ j, f ^ j).wait_recv()
            total = total + zb_r[f ^ j].astype(F32)
        gb[...] = total.astype(BF16)
        sb[...] = (MOMENTUM * mb[...] + total).astype(BF16)

    def share_a(j, source):
        return remote(sa, s_a.at[pl.ds(pl.multiple_of(source * rows, rows), rows)], ss.at[j], sr.at[j], at.along(j))

    def share_b(j, source):
        return remote(sb, s_b.at[pl.ds(pl.multiple_of(source * high, high), high)], ss.at[j], sr.at[j], at.along(j))

    @pl.when(p < WIDE)
    def _():
        for j in range(1, parts):
            share_a(j, f).start()
        pltpu.make_async_copy(sa, s_a.at[pl.ds(pl.multiple_of(f * rows, rows), rows)], sl).start()

    @pl.when(p >= WIDE)
    def _():
        for j in range(1, parts):
            share_b(j, f).start()
        pltpu.make_async_copy(sb, s_b.at[pl.ds(pl.multiple_of(f * high, high), high)], sl).start()

    finish = spread(at, ga, gb, g_a, g_b, ag_l, ag_s, ag_r)
    total = gain_s[3]
    for j in range(1, parts):
        line_gain[j - 1].wait()
        total = total + gain_r[3 + j]
    if extra > 1:
        gain_s[4] = total
        other_gain = [
            remote(gain_s.at[4], gain_r.at[3 + parts + j], gs.at[3 + parts + j], gr.at[3 + parts + j], at.other(j))
            for j in range(1, extra)
        ]
        for copy in other_gain:
            copy.start()
        for j in range(1, extra):
            other_gain[j - 1].wait()
            total = total + gain_r[3 + parts + j]
    gain_out[...] = total
    finish()

    for slot in range(2):
        lax.fori_loop(0, parts, lambda i, carry, slot=slot: (one(slot, i).wait_send(), carry)[1], 0)
    lax.fori_loop(0, parts, lambda i, carry: (two(i).wait_send(), carry)[1], 0)

    @pl.when(p < WIDE)
    def _():
        for j in range(1, parts):
            line_a(f ^ j, f).wait_send()
            share_a(j, f).wait_send()
            share_a(j, f ^ j).wait_recv()
        pltpu.make_async_copy(sa, s_a.at[pl.ds(pl.multiple_of(f * rows, rows), rows)], sl).wait()

    @pl.when(p >= WIDE)
    def _():
        for j in range(1, parts):
            line_b(f ^ j, f).wait_send()
            share_b(j, f).wait_send()
            share_b(j, f ^ j).wait_recv()
        pltpu.make_async_copy(sb, s_b.at[pl.ds(pl.multiple_of(f * high, high), high)], sl).wait()


def reduce_gradients(xt, dy, gains, moments, rows, high):
    parts = lax.axis_size("fsdp")
    extra = lax.axis_size("ctx") // CLASSES
    kinds, depth, tokens = xt.shape
    half = dy.shape[2]
    dma = pltpu.SemaphoreType.DMA
    vm = pltpu.VMEM
    n_gain = 4 + parts + extra
    group = max(extra - 1, 1)
    spare = (parts, rows, half) if extra > 1 else (1, 16, 128)
    return pl.pallas_call(
        functools.partial(reduce_kernel, parts, extra, high),
        out_shape=(
            jax.ShapeDtypeStruct((WIDE, rows, half), BF16),
            jax.ShapeDtypeStruct((CLASSES - WIDE, high, depth), BF16),
            jax.ShapeDtypeStruct((depth, half), BF16),
            jax.ShapeDtypeStruct((half, depth), BF16),
            jax.ShapeDtypeStruct(gains.shape, F32),
        ),
        in_specs=[ANY, ANY, VMEM] + [ANY] * 5,
        out_specs=(ANY, ANY, ANY, ANY, VMEM),
        scratch_shapes=[
            vm((kinds, depth, 2 * tokens), BF16),
            vm((5, 2 * tokens, half), BF16),
            vm((2, parts, rows, half), BF16),
            vm((2, parts, rows, half), BF16),
            vm((parts, rows, half), BF16),
            vm((parts, rows, half), BF16),
            vm((parts, rows, half), F32),
            vm((half, depth), F32),
            vm((parts, rows, half), BF16),
            vm((parts, rows, half), BF16),
            vm((half, depth), BF16),
            vm((parts, high, depth), BF16),
            vm((rows, half), F32),
            vm((high, depth), F32),
            vm((rows, half), BF16),
            vm((high, depth), BF16),
            vm((rows, half), BF16),
            vm((high, depth), BF16),
            vm(spare, BF16),
            vm((group,) + spare, BF16),
            vm((5,) + gains.shape, F32),
            vm((n_gain,) + gains.shape, F32),
            dma((6,)), dma((6,)), dma((6,)),
            dma((2, parts)), dma((2, parts)), dma((parts,)), dma((parts,)), dma((parts,)), dma((parts,)),
            dma((group,)), dma((group,)), dma, dma((n_gain,)), dma((n_gain,)),
            dma, dma((7,)), dma((CLASSES,)), dma((parts,)), dma((parts,)), dma,
        ],
        compiler_params=pltpu.CompilerParams(
            collective_id=1, has_side_effects=True, vmem_limit_bytes=62 << 20
        ),
        name="reduce_gradients",
    )(xt, dy, gains, *moments)


def rounded(value):
    return value.astype(BF16)


def poly_rows(g, row_start, count):
    block = g[pl.ds(row_start, count), :]
    return rounded(NS_B * block.astype(F32) + NS_C * jnp.dot(block, g[...], preferred_element_type=F32))


def ortho_kernel(
    parts, rows, high, narrow,
    s_a, s_b, o_a, o_b,
    x, x_t, gs, gr, g, poly, sq, sq_r, pa, pb, kt,
    gsem, rsem, qs, qr, ag_l, ag_s, ag_r,
):
    at = Place()
    p, f = at.p, at.f
    depth, half = x.shape
    step = depth // 4
    at.barrier(line=False)
    pair = at.peer(1)

    @pl.when(p < WIDE)
    def _():
        x[...] = s_a[...]

    @pl.when(p >= WIDE)
    def _():
        for tile in range(half // 128):
            x[:, pl.ds(tile * 128, 128)] = s_b[pl.ds(tile * 128, 128), :].T

    def scale_of(total):
        return 1.0 / (jnp.sqrt(total) + 1e-07)

    def normal(ref, inverse):
        ref[...] = rounded(ref[...].astype(F32) * inverse)

    def exchange(slot, r):
        chunk = pl.ds(r * step, step)
        return remote(gs.at[chunk], gr.at[slot, chunk], gsem.at[r], rsem.at[slot, r], pair)

    def fill_poly():
        for r in range(4):
            poly[pl.ds(r * step, step), :] = poly_rows(g, r * step, step)

    my_rows = pl.ds(pl.multiple_of(f * rows, rows), rows)
    my_high = pl.ds(pl.multiple_of(f * high, high), high)

    @pl.when(p >= 2)
    def _():
        wide = x[...].astype(F32)
        sq[...] = jnp.broadcast_to(jnp.sum(wide * wide), sq.shape)
        copy = remote(sq, sq_r, qs, qr, pair)
        copy.start()
        copy.wait()
        normal(x, scale_of(sq[...] + sq_r[...])[:1, :1])

        def grams(slot):
            for r in range(4):
                gs[pl.ds(r * step, step), :] = rounded(contract(x[pl.ds(r * step, step), :], x[...], 1, 1))
                exchange(slot, r).start()
            for r in range(4):
                chunk = pl.ds(r * step, step)
                exchange(slot, r).wait()
                g[chunk, :] = rounded(gs[chunk, :].astype(F32) + gr[slot, chunk, :].astype(F32))

        def iterate(it, carry):
            grams(lax.rem(it, 2))
            fill_poly()
            for tile in range(half // 256):
                block = pl.ds(tile * 256, 256)
                x[:, block] = rounded(
                    NS_A * x[:, block].astype(F32) + jnp.dot(poly[...], x[:, block], preferred_element_type=F32)
                )
            return carry

        lax.fori_loop(0, NS_ITERS - 1, iterate, 0)
        grams((NS_ITERS - 1) % 2)

        @pl.when(p < WIDE)
        def _():
            mine = poly_rows(g, pl.multiple_of(f * rows, rows), rows)
            pa[...] = rounded(NS_A * x[my_rows, :].astype(F32) + jnp.dot(mine, x[...], preferred_element_type=F32))

        @pl.when(p >= WIDE)
        def _():
            fill_poly()
            for tile in range(half // 128):
                x_t[pl.ds(tile * 128, 128), :] = x[:, pl.ds(tile * 128, 128)].T
            block = x_t[my_high, :]
            pb[...] = rounded(NS_A * block.astype(F32) + jnp.dot(block, poly[...], preferred_element_type=F32))

    @pl.when(p < 2)
    def _():
        kt[...] = x[:, narrow:].T
        inverse_k = scale_of(jnp.sum(jnp.square(kt[...].astype(F32))))
        normal(kt, inverse_k)
        wide = x[:, :narrow].astype(F32)
        x[:, :narrow] = rounded(wide * scale_of(jnp.sum(wide * wide)))

        def narrow_step(it, carry):
            gram = rounded(contract(kt[...], kt[...], 1, 1))
            turn = rounded(NS_B * gram.astype(F32) + NS_C * jnp.dot(gram, gram, preferred_element_type=F32))
            kt[...] = rounded(NS_A * kt[...].astype(F32) + jnp.dot(turn, kt[...], preferred_element_type=F32))
            return carry

        lax.fori_loop(0, NS_ITERS, narrow_step, 0)

        def gram_of():
            for r in range(4):
                chunk = pl.ds(r * step, step)
                g[chunk, :] = rounded(contract(x[chunk, :narrow], x[:, :narrow], 1, 1))

        def square_step(it, carry):
            gram_of()
            fill_poly()
            x[:, :narrow] = rounded(
                NS_A * x[:, :narrow].astype(F32) + jnp.dot(poly[...], x[:, :narrow], preferred_element_type=F32)
            )
            return carry

        lax.fori_loop(0, NS_ITERS - 1, square_step, 0)
        gram_of()
        mine = poly_rows(g, pl.multiple_of(f * rows, rows), rows)
        square = rounded(
            NS_A * x[my_rows, :narrow].astype(F32) + jnp.dot(mine, x[:, :narrow], preferred_element_type=F32)
        )
        x[:, narrow:] = kt[...].T
        pa[:, :narrow] = square
        pa[:, narrow:] = x[my_rows, narrow:]

    spread(at, pa, pb, o_a, o_b, ag_l, ag_s, ag_r)()


def orthogonalize(s_a, s_b, rows, high, narrow):
    parts = lax.axis_size("fsdp")
    depth, half = s_a.shape
    dma = pltpu.SemaphoreType.DMA
    vm = pltpu.VMEM
    return pl.pallas_call(
        functools.partial(ortho_kernel, parts, rows, high, narrow),
        out_shape=(
            jax.ShapeDtypeStruct((WIDE, rows, half), BF16),
            jax.ShapeDtypeStruct((CLASSES - WIDE, high, depth), BF16),
        ),
        in_specs=[VMEM, VMEM],
        out_specs=(ANY, ANY),
        scratch_shapes=[
            vm((depth, half), BF16),
            vm((half, depth), BF16),
            vm((depth, depth), BF16),
            vm((2, depth, depth), BF16),
            vm((depth, depth), BF16),
            vm((depth, depth), BF16),
            vm((8, 128), F32),
            vm((8, 128), F32),
            vm((rows, half), BF16),
            vm((high, depth), BF16),
            vm((half - narrow, depth), BF16),
            dma((4,)), dma((2, 4)), dma, dma, dma, dma((7,)), dma((CLASSES,)),
        ],
        compiler_params=pltpu.CompilerParams(
            collective_id=2, has_side_effects=True, vmem_limit_bytes=62 << 20
        ),
        name="orthogonalize",
    )(s_a, s_b)


class Weights:
    def __init__(self, at, sources, homes, zs, s1, s2, sc, recv):
        self.at, self.sources, self.homes = at, sources, homes
        self.zs, self.s1, self.s2, self.sc, self.recv = zs, s1, s2, sc, recv
        self.sends = []

    def act(self, group, q, j, plane, send, target, what, first=False):
        recv = self.recv.at[group, q, j]
        home, source = self.homes[group], self.sources[group]
        rows = home.shape[-2] // (1 if group == 3 else self.at.parts)
        unit = -(-rows // (16 * CLASSES)) * 16
        last = rows - (CLASSES - 1) * unit

        def piece(count):
            def go():
                start = pl.multiple_of(q * unit, 16)
                if group == 3:
                    columns = home.shape[1] // self.at.parts
                    dst = home.at[pl.ds(start, count), pl.ds(pl.multiple_of(plane * columns, 128), columns)]
                    src = source.at[pl.ds(start, count)]
                elif group == 0:
                    dst = home.at[:, pl.ds(pl.multiple_of(plane * rows + start, 16), count)]
                    src = dst
                else:
                    dst = home.at[pl.ds(pl.multiple_of(plane * rows + start, 16), count)]
                    src = source.at[pl.ds(start, count)]
                getattr(remote(src if first else dst, dst, send, recv, target), what)()

            return go

        pl.when(q < CLASSES - 1)(piece(unit))
        pl.when(q == CLASSES - 1)(piece(last))

    def send(self, group, q, j, plane, sem, target, first=False):
        self.act(group, q, j, plane, sem, target, "start", first)
        self.sends.append((group, q, j, plane, sem, target, "wait_send", first))

    def arrived(self, group, q, j):
        at = self.at
        self.act(group, q, j, at.f ^ j, self.zs.at[group, j], at.peer(1), "wait_recv")

    def along(self, group):
        at = self.at
        for j in range(1, at.parts):
            self.send(group, at.p, j, at.f, self.zs.at[group, j], at.along(j), True)

    def first(self, group):
        at = self.at
        for j in range(1, at.parts):
            self.arrived(group, at.p, j)
            self.send(group, at.p, j, at.f ^ j, self.s1.at[group, j], at.peer(at.b1))
            self.send(group, at.p, j, at.f ^ j, self.s2.at[group, 0, j], at.peer(at.b2))
            self.send(group, at.p, j, at.f ^ j, self.sc.at[group, 0, j], at.peer(1))

    def second(self, group):
        at = self.at
        q = at.p ^ at.b1
        for j in range(1, at.parts):
            self.arrived(group, q, j)
            self.send(group, q, j, at.f ^ j, self.s2.at[group, 1, j], at.peer(at.b2))
            self.send(group, q, j, at.f ^ j, self.sc.at[group, 1, j], at.peer(1))

    def third(self, group):
        at = self.at
        for slot, bits in ((2, at.b2), (3, at.b1 ^ at.b2)):
            for j in range(1, at.parts):
                self.arrived(group, at.p ^ bits, j)
                self.send(group, at.p ^ bits, j, at.f ^ j, self.sc.at[group, slot, j], at.peer(1))

    def ready(self, group):
        at = self.at
        for bits in (1, 3, 5, 7):
            for j in range(1, at.parts):
                self.arrived(group, at.p ^ bits, j)

    def finish(self):
        for item in self.sends:
            self.act(*item)


def layer_kernel(
    x_ref, up_ref, gains_ref, cos_ref, low_ref, high_ref, bias_ref, wq, wk, wo, wv, wg_in, wu_in, wd_in,
    out_ref, grad_ref, xt_ref, dy_ref, gain_ref,
    w01, wg, wu, wd, probs, kv, rot, dkv, c4s, c4r, c2s, c2r, c1s, c1r, att, gate, lifted,
    local, zs, s1, s2, sc, recv, kvs, kvr, ds, dr,
):
    at = Place()
    p, f = at.p, at.f
    width, tokens = x_ref.shape
    half = w01.shape[2]
    keys = half - width
    group = HEADS // KV_HEADS
    scale = 1.0 / math.sqrt(HEAD)
    parts = at.parts
    rows = width // parts
    columns = 2 * half // parts

    weights = Weights(at, (None, wg_in, wu_in, wd_in), (w01, wg, wu, wd), zs, s1, s2, sc, recv)
    my_rows = pl.ds(pl.multiple_of(f * rows, 16), rows)
    own = [
        pltpu.make_async_copy(wg_in, wg.at[my_rows], local.at[0]),
        pltpu.make_async_copy(wu_in, wu.at[my_rows], local.at[1]),
        pltpu.make_async_copy(
            wd_in, wd.at[:, pl.ds(pl.multiple_of(f * columns, 128), columns)], local.at[2]
        ),
    ]
    for copy in own:
        copy.start()
    w01[0, my_rows, :width] = wq[...]
    w01[0, my_rows, width:] = wk[...].T
    w01[1, my_rows, :width] = wo[...]
    w01[1, my_rows, width:] = wv[...].T
    at.barrier()
    for index in range(4):
        weights.along(index)

    residual = x_ref[...].astype(F32).T
    upstream = up_ref[...].astype(F32).T
    inverse_first = lax.rsqrt(jnp.mean(residual * residual, axis=-1, keepdims=True) + EPS)
    normed_first = (residual * inverse_first * gains_ref[0:1, :]).astype(BF16)
    xt_ref[0] = normed_first.T
    xt_ref[3] = up_ref[...]

    weights.first(0)
    weights.second(0)
    weights.first(1)
    weights.third(0)
    weights.ready(0)

    def turn(value, sign):
        tiles = []
        for tile in range(half // 128):
            part = value[:, tile * 128 : (tile + 1) * 128]
            swapped = pltpu.roll(part, HEAD // 2, 1) * low_ref[...] + pltpu.roll(part, 128 - HEAD // 2, 1) * high_ref[...]
            tiles.append(part * cos_ref[...] + swapped if sign > 0 else part * cos_ref[...] - swapped)
        return tiles

    qk = jnp.dot(normed_first, w01[0], preferred_element_type=F32)
    for tile, value in enumerate(turn(qk, 1)):
        rot[:, tile * 128 : (tile + 1) * 128] = value.astype(BF16)
    values = jnp.dot(normed_first, w01[1, :, width:], preferred_element_type=F32).astype(BF16)
    kv[p, :, :keys] = rot[:, width:]
    kv[p, :, keys:] = values

    def block(q, slot, target):
        return remote(kv.at[q], kv.at[q], kvs.at[slot], kvr.at[q], target)

    sent = [block(p, 0, at.peer(at.b1)), block(p, 1, at.peer(at.b2)), block(p, 2, at.peer(1))]
    for copy in sent:
        copy.start()

    def pass_on(q, slots):
        block(q, 0, at.peer(1)).wait_recv()
        for slot, target in slots:
            copy = block(q, slot, target)
            copy.start()
            sent.append(copy)

    pass_on(p ^ at.b1, [(3, at.peer(at.b2)), (4, at.peer(1))])
    pass_on(p ^ at.b2, [(5, at.peer(1))])
    pass_on(p ^ at.b1 ^ at.b2, [(6, at.peer(1))])
    for bits in (1, 3, 5, 7):
        pass_on(p ^ bits, [])

    weights.second(1)
    weights.first(2)
    weights.third(1)

    def keys_of(g):
        return kv[:, :, g * HEAD : (g + 1) * HEAD].reshape(CLASSES * tokens, HEAD)

    def values_of(g):
        return kv[:, :, keys + g * HEAD : keys + (g + 1) * HEAD].reshape(CLASSES * tokens, HEAD)

    def heads_of(ref, g):
        return jnp.concatenate([ref[:, h * HEAD : (h + 1) * HEAD] for h in range(g * group, (g + 1) * group)], axis=0)

    for g in range(KV_HEADS):
        scores = contract(keys_of(g), heads_of(rot, g), 1, 1) * scale
        bias = bias_ref[...]
        scores = scores + jnp.concatenate([bias] * group, axis=1)
        top = jnp.max(scores, axis=0, keepdims=True)
        expo = jnp.exp(scores - top)
        total = jnp.sum(expo, axis=0, keepdims=True)
        chance = expo * (1.0 / total)
        probs[g] = chance
        mixed = contract(values_of(g), chance.astype(BF16), 0, 0)
        turned = mixed.T.astype(BF16)
        for h in range(group):
            at_lane = (g * group + h) * HEAD
            att[:, at_lane : at_lane + HEAD] = turned[h * tokens : (h + 1) * tokens]

    weights.second(2)
    weights.first(3)
    weights.third(2)
    for copy in own:
        copy.wait()
    weights.ready(1)

    xt_ref[1] = att[...].T
    middle = residual + jnp.dot(att[...], w01[1, :, :width], preferred_element_type=F32)
    inverse_second = lax.rsqrt(jnp.mean(middle * middle, axis=-1, keepdims=True) + EPS)
    normed_second = (middle * inverse_second * gains_ref[1:2, :]).astype(BF16)
    xt_ref[2] = normed_second.T
    gate[...] = jnp.dot(normed_second, wg[...], preferred_element_type=F32)
    weights.second(3)
    weights.ready(2)
    weights.third(3)
    lifted[...] = jnp.dot(normed_second, wu[...], preferred_element_type=F32)
    weights.ready(3)

    hidden = (gate[...] * jax.nn.sigmoid(gate[...]) * lifted[...]).astype(BF16)
    dy_ref[6] = hidden[:, :half]
    dy_ref[7] = hidden[:, half:]
    out_ref[...] = (middle + contract(hidden, wd[...], 1, 1)).T.astype(BF16)

    grad_hidden = jnp.dot(upstream.astype(BF16), wd[...], preferred_element_type=F32)
    sigma = jax.nn.sigmoid(gate[...])
    grad_gate = (grad_hidden * lifted[...] * sigma * (1.0 + gate[...] * (1.0 - sigma))).astype(BF16)
    grad_lifted = (grad_hidden * gate[...] * sigma).astype(BF16)
    for side in range(2):
        lanes = slice(side * half, (side + 1) * half)
        dy_ref[2 + side] = grad_gate[:, lanes]
        dy_ref[4 + side] = grad_lifted[:, lanes]
    grad_normed = contract(grad_gate, wg[...], 1, 1) + contract(grad_lifted, wu[...], 1, 1)

    def norm_back(value, inverse, gain, incoming):
        scaled = incoming * gain
        mean = jnp.mean(scaled * value, axis=-1, keepdims=True)
        through = inverse * scaled - value * (inverse * inverse * inverse) * mean
        return through, jnp.sum(incoming * value * inverse, axis=0, keepdims=True)

    through, gain_second = norm_back(middle, inverse_second, gains_ref[1:2, :], grad_normed)
    gain_ref[...] = jnp.zeros_like(gain_ref)
    gain_ref[1:2, :] = gain_second
    grad_middle = upstream + through
    grad_branch = grad_middle.astype(BF16)
    dy_ref[1, :, :width] = grad_branch
    dy_ref[1, :, width:] = jnp.zeros((tokens, keys), BF16)
    att[...] = contract(grad_branch, w01[1, :, :width], 1, 1).astype(BF16)

    for g in range(KV_HEADS):
        chance = probs[g]
        out_grad = heads_of(att, g)
        query = heads_of(rot, g)
        grad_probs = contract(values_of(g), out_grad, 1, 1)
        delta = jnp.sum(grad_probs * chance, axis=0, keepdims=True)
        grad_scores = (chance * (grad_probs - delta)).astype(BF16)
        grad_values = jnp.dot(chance.astype(BF16), out_grad, preferred_element_type=F32)
        grad_keys = jnp.dot(grad_scores, query, preferred_element_type=F32) * scale
        dkv[:, :, g * HEAD : (g + 1) * HEAD] = grad_keys.reshape(CLASSES, tokens, HEAD)
        dkv[:, :, keys + g * HEAD : keys + (g + 1) * HEAD] = grad_values.reshape(CLASSES, tokens, HEAD)
        turned = contract(keys_of(g), grad_scores, 0, 0).T * scale
        for h in range(group):
            at_lane = (g * group + h) * HEAD
            gate[:, at_lane : at_lane + HEAD] = turned[h * tokens : (h + 1) * tokens]

    def halve(bit, rest, sbuf, rbuf, index):
        for i, bits in enumerate(rest):
            sbuf[i] = dkv[p ^ bit ^ bits].astype(BF16)
        copy = remote(sbuf, rbuf, ds.at[index], dr.at[index], at.peer(bit))
        copy.start()
        copy.wait()
        for i, bits in enumerate(rest):
            dkv[p ^ bits] = dkv[p ^ bits] + rbuf[i].astype(F32)

    halve(1, (0, 2, 4, 6), c4s, c4r, 0)
    halve(at.b1, (0, at.b2), c2s, c2r, 1)
    halve(at.b2, (0,), c1s, c1r, 2)

    gate[:, width:half] = dkv[p, :, :keys]
    for tile, value in enumerate(turn(gate[:, :half], -1)):
        dy_ref[0, :, tile * 128 : (tile + 1) * 128] = value.astype(BF16)
    dy_ref[8, :, :width] = jnp.zeros((tokens, width), BF16)
    dy_ref[8, :, width:] = dkv[p, :, keys:].astype(BF16)
    grad_normed = contract(dy_ref[0], w01[0], 1, 1) + contract(dy_ref[8], w01[1], 1, 1)
    through, gain_first = norm_back(residual, inverse_first, gains_ref[0:1, :], grad_normed)
    gain_ref[0:1, :] = gain_first
    grad_ref[...] = (grad_middle + through).T

    weights.finish()
    for copy in sent:
        copy.wait_send()


def layer_pass(x, up, gains, tables, bias, shards):
    parts = lax.axis_size("fsdp")
    width, tokens = x.shape
    half = shards[4].shape[1] // 2
    dma = pltpu.SemaphoreType.DMA
    vm = pltpu.VMEM
    group = HEADS // KV_HEADS
    two = 2 * (half - width)
    return pl.pallas_call(
        layer_kernel,
        out_shape=(
            jax.ShapeDtypeStruct((width, tokens), BF16),
            jax.ShapeDtypeStruct((width, tokens), F32),
            jax.ShapeDtypeStruct((4, width, tokens), BF16),
            jax.ShapeDtypeStruct((9, tokens, half), BF16),
            jax.ShapeDtypeStruct((8, width), F32),
        ),
        in_specs=[VMEM] * 11 + [ANY] * 3,
        out_specs=(VMEM,) * 5,
        scratch_shapes=[
            vm((2, width, half), BF16),
            vm((width, 2 * half), BF16),
            vm((width, 2 * half), BF16),
            vm((width, 2 * half), BF16),
            vm((KV_HEADS, CLASSES * tokens, group * tokens), F32),
            vm((CLASSES, tokens, two), BF16),
            vm((tokens, half), BF16),
            vm((CLASSES, tokens, two), F32),
            vm((4, tokens, two), BF16),
            vm((4, tokens, two), BF16),
            vm((2, tokens, two), BF16),
            vm((2, tokens, two), BF16),
            vm((1, tokens, two), BF16),
            vm((1, tokens, two), BF16),
            vm((tokens, width), BF16),
            vm((tokens, 2 * half), F32),
            vm((tokens, 2 * half), F32),
            dma((3,)), dma((4, parts)), dma((4, parts)), dma((4, 2, parts)), dma((4, 4, parts)),
            dma((4, CLASSES, parts)), dma((7,)), dma((CLASSES,)), dma((3,)), dma((3,)),
        ],
        compiler_params=pltpu.CompilerParams(
            collective_id=3, has_side_effects=True, vmem_limit_bytes=62 << 20
        ),
        name="layer_pass",
    )(x, up, gains, *tables, bias, *shards)


def spread_even(at, own, out, local, ss, recv):
    p = at.p

    def copy_of(cls, slot, target, first=False):
        return remote(own if first else out.at[cls], out.at[cls], ss.at[slot], recv.at[cls], target)

    keep = pltpu.make_async_copy(own, out.at[p], local)
    sends = []

    def send(cls, slot, target, first=False):
        copy = copy_of(cls, slot, target, first)
        copy.start()
        sends.append(copy)

    def arrived(cls):
        copy_of(cls, 0, at.peer(1)).wait_recv()

    send(p, 0, at.peer(at.b1), True)
    send(p, 1, at.peer(at.b2), True)
    send(p, 2, at.peer(1), True)
    keep.start()

    def pass_on():
        arrived(p ^ at.b1)
        send(p ^ at.b1, 3, at.peer(at.b2))
        send(p ^ at.b1, 4, at.peer(1))
        arrived(p ^ at.b2)
        send(p ^ at.b2, 5, at.peer(1))
        arrived(p ^ at.b1 ^ at.b2)
        send(p ^ at.b1 ^ at.b2, 6, at.peer(1))

    def finish():
        for bits in (1, 3, 5, 7):
            arrived(p ^ bits)
        for copy in sends:
            copy.wait_send()
        keep.wait()

    return pass_on, finish


def update_kernel(
    xt_in, dy_in, gain_in, m_q, m_k, m_o, m_v, m_gate, m_up, m_down,
    g_out, o_out, gain_out,
    xt, dy, p1s, p1r, p2s, p2r, own, za_s, za_r, ma, mq, mk, ga, sall, gain_s, gain_r,
    x, gram_s, gram_r, g, poly, sq, sq_r, pa, kt, xo, xf,
    ls, xs, xr, s1, r1, s2, r2, zs, zr, msem, gs, gr, ag_l, ag_s, ag_r, ls_l, ls_r, lr_l, lr_r,
    gsem, rsem, qs, qr, ex_s, ex_r, fx_s, fx_r, og_l, og_s, og_r,
):
    at = Place()
    p, f, core, parts = at.p, at.f, at.core, at.parts
    tokens = xt_in.shape[2]
    rows, half = ma.shape
    width = xt.shape[1]
    keys = half - width
    columns = 2 * half // parts
    tall = width // 2

    def moment(what):
        for cls in range(CLASSES):
            @pl.when(p == cls)
            def _(cls=cls):
                side = cls % 2
                if cls < 2:
                    pairs = [((m_q, m_o)[cls], mq, 0), ((m_k, m_v)[cls], mk, 1)]
                elif cls < WIDE:
                    whole = m_gate if cls < 4 else m_up
                    pairs = [(whole.at[:, pl.ds(side * half, half)], ma, 0)]
                else:
                    pairs = [
                        (
                            m_down.at[pl.ds(side * tall + t * rows, rows)],
                            ma.at[:, pl.ds(t * columns, columns)],
                            t,
                        )
                        for t in range(2)
                    ]
                for src, dst, index in pairs:
                    getattr(pltpu.make_async_copy(src, dst, msem.at[index]), what)()

    moment("start")
    slabs = [core, 2 + core, 4 + core, 6, 7, 8]
    theirs_slabs = [1 - core, 3 - core, 5 - core, 6, 7, 8]
    mine = [pltpu.make_async_copy(xt_in, xt.at[:, :, pl.ds(0, tokens)], ls.at[0])]
    for slot, slab in enumerate(slabs):
        mine.append(pltpu.make_async_copy(dy_in.at[slab], dy.at[slot, pl.ds(0, tokens)], ls.at[1 + slot]))
    for copy in mine:
        copy.start()
    at.barrier()
    pair = at.peer(1)
    theirs = [remote(xt_in, xt.at[:, :, pl.ds(tokens, tokens)], xs.at[0], xr.at[0], pair)]
    for slot, slab in enumerate(theirs_slabs):
        theirs.append(
            remote(dy_in.at[slab], dy.at[slot, pl.ds(tokens, tokens)], xs.at[1 + slot], xr.at[1 + slot], pair)
        )
    for copy in theirs:
        copy.start()

    def swap(slot, target):
        return remote(gain_s.at[slot], gain_r.at[slot], gs.at[slot], gr.at[slot], target)

    gain_s[0] = gain_in[...]
    swaps = [swap(0, pair)]
    swaps[0].start()
    for copy in mine:
        copy.wait()
    for copy in theirs:
        copy.wait()

    def produce(cls, r, put):
        at_rows = pl.ds(pl.multiple_of(r * rows, 16), rows)
        slot = lax.div(cls, 2)
        every = slice(0, half)

        @pl.when(cls == 1)
        def _():
            put(
                every,
                jnp.dot(xt[1, at_rows, :], dy[0], preferred_element_type=F32)
                + jnp.dot(xt[0, at_rows, :], dy[5], preferred_element_type=F32),
            )

        @pl.when((cls != 1) & (cls < WIDE))
        def _():
            kind = jnp.where(cls == 0, 0, 2)
            put(every, jnp.dot(xt[kind, at_rows, :], dy[slot], preferred_element_type=F32))

        @pl.when(cls >= WIDE)
        def _():
            side, start = lax.div(r * columns, half), lax.rem(r * columns, half)
            block = dy[3 + side, :, pl.ds(pl.multiple_of(start, 128), columns)]
            for t in range(2):
                top = pl.multiple_of((cls - WIDE) * tall + t * rows, 16)
                put(
                    slice(t * columns, (t + 1) * columns),
                    jnp.dot(xt[3, pl.ds(top, rows), :], block, preferred_element_type=F32),
                )

    def order(i):
        return lax.rem(f + 1 + i, parts)

    def one(slot, i):
        r = order(i)
        return remote(p1s.at[slot, r], p1r.at[slot, r], s1.at[slot, r], r1.at[slot, r], at.peer(at.b1))

    def first(i, carry):
        r = order(i)
        for slot, bits in ((0, at.b1 ^ at.b2), (1, at.b1)):

            def put(lanes, value, slot=slot):
                p1s[slot, r, :, lanes] = value.astype(BF16)

            produce(p ^ bits, r, put)
            one(slot, i).start()
        return carry

    lax.fori_loop(0, parts, first, 0)
    swaps[0].wait()
    gain_s[1] = gain_s[0] + gain_r[0]
    swaps.append(swap(1, at.peer(2)))
    swaps[1].start()

    def two(i):
        r = order(i)
        return remote(p2s.at[r], p2r.at[r], s2.at[r], r2.at[r], at.peer(at.b2))

    def second(i):
        r = order(i)
        one(0, i).wait_recv()

        def put(lanes, value):
            p2s[r, :, lanes] = (value + p1r[0, r, :, lanes].astype(F32)).astype(BF16)

        produce(p ^ at.b2, r, put)
        two(i).start()

    def line(r, source):
        return remote(za_s.at[r], za_r.at[source], zs.at[r], zr.at[source], (at.c, r))

    def third(i):
        r = order(i)
        one(1, i).wait_recv()
        two(i).wait_recv()

        def put(lanes, value):
            total = value + p1r[1, r, :, lanes].astype(F32) + p2r[r, :, lanes].astype(F32)
            own[:, lanes] = total
            za_s[r, :, lanes] = total.astype(BF16)

        produce(p, r, put)

        @pl.when(i < parts - 1)
        def _():
            line(r, f).start()

    def both(i, carry):
        second(i)

        @pl.when(i > 0)
        def _():
            third(i - 1)

        return carry

    lax.fori_loop(0, parts, both, 0)
    third(parts - 1)
    swaps[1].wait()
    gain_s[2] = gain_s[1] + gain_r[1]
    swaps.append(swap(2, at.peer(4)))
    swaps[2].start()

    moment("wait")

    @pl.when(p < 2)
    def _():
        ma[:, :width] = mq[...]
        ma[:, width:] = mk[...].T

    total = own[...]
    for j in range(1, parts):
        line(f ^ j, f ^ j).wait_recv()
        total = total + za_r[f ^ j].astype(F32)
    ga[...] = total.astype(BF16)
    my_rows = pl.ds(pl.multiple_of(f * rows, 16), rows)
    sall[my_rows, :] = (MOMENTUM * ma[...] + total).astype(BF16)

    def shard(index):
        return sall.at[pl.ds(pl.multiple_of(index * rows, 16), rows)]

    def rightward(index):
        return remote(shard(index), shard(index), ls_r.at[index], lr_r.at[index], (at.c, lax.rem(f + 1, parts)))

    def leftward(index):
        return remote(shard(index), shard(index), ls_l.at[index], lr_l.at[index], (at.c, lax.rem(f + parts - 1, parts)))

    def can_right():
        return f < parts - 1

    def can_left():
        return f > 0

    pl.when(can_right())(lambda: rightward(f).start())
    pl.when(can_left())(lambda: leftward(f).start())

    pass_on, finish = spread_even(at, ga, g_out, ag_l, ag_s, ag_r)
    swaps[2].wait()
    gain_s[3] = gain_s[2] + gain_r[2]
    line_gain = [
        remote(gain_s.at[3], gain_r.at[3 + j], gs.at[3 + j], gr.at[3 + j], at.along(j)) for j in range(1, parts)
    ]
    for copy in line_gain:
        copy.start()
    pass_on()

    for hop in range(1, parts):
        @pl.when(f - hop >= 0)
        def _(hop=hop):
            rightward(f - hop).wait_recv()
            pl.when(can_right())(lambda: rightward(f - hop).start())

        @pl.when(f + hop < parts)
        def _(hop=hop):
            leftward(f + hop).wait_recv()
            pl.when(can_left())(lambda: leftward(f + hop).start())

    step = width // 4

    def scale_of(total):
        return 1.0 / (jnp.sqrt(total) + 1e-07)

    def normal(ref, inverse):
        ref[...] = rounded(ref[...].astype(F32) * inverse)

    def exchange(slot, r):
        chunk = pl.ds(r * step, step)
        return remote(gram_s.at[chunk], gram_r.at[slot, chunk], gsem.at[r], rsem.at[slot, r], pair)

    def fill_poly():
        for r in range(4):
            poly[pl.ds(r * step, step), :] = poly_rows(g, r * step, step)

    near = parts // 2
    mine_at = core * near
    last_core = lax.div(f, near)
    f_lanes = pl.ds(pl.multiple_of(lax.rem(f, near) * columns, 128), columns)

    def give():
        return [
            remote(
                sall.at[pl.ds(pl.multiple_of(((1 - core) * near + i) * rows, 16), rows)],
                xo.at[i], ex_s.at[i], ex_r.at[i], pair,
            )
            for i in range(near)
        ]

    def give_last():
        return remote(x.at[:, f_lanes], xf, fx_s, fx_r, pair)

    @pl.when(p >= 2)
    def _():
        @pl.when(p < WIDE)
        def _():
            x[...] = sall[...]

        @pl.when(p >= WIDE)
        def _():
            copies = give()
            for copy in copies:
                copy.start()
            for i in range(near):
                block = sall[pl.ds(pl.multiple_of((mine_at + i) * rows, 16), rows), :]
                for t in range(2):
                    x[pl.ds(pl.multiple_of(core * tall + t * rows, 16), rows), pl.ds(i * columns, columns)] = block[
                        :, t * columns : (t + 1) * columns
                    ]
            for i, copy in enumerate(copies):
                copy.wait()
                for t in range(2):
                    x[pl.ds(pl.multiple_of((1 - core) * tall + t * rows, 16), rows), pl.ds(i * columns, columns)] = xo[
                        i, :, pl.ds(t * columns, columns)
                    ]

        wide = x[...].astype(F32)
        sq[...] = jnp.broadcast_to(jnp.sum(wide * wide), sq.shape)
        copy = remote(sq, sq_r, qs, qr, pair)
        copy.start()
        copy.wait()
        normal(x, scale_of(sq[...] + sq_r[...])[:1, :1])

        def grams(slot):
            for r in range(4):
                gram_s[pl.ds(r * step, step), :] = rounded(contract(x[pl.ds(r * step, step), :], x[...], 1, 1))
                exchange(slot, r).start()
            for r in range(4):
                chunk = pl.ds(r * step, step)
                exchange(slot, r).wait()
                g[chunk, :] = rounded(gram_s[chunk, :].astype(F32) + gram_r[slot, chunk, :].astype(F32))

        def iterate(it, carry):
            grams(lax.rem(it, 2))
            fill_poly()
            for tile in range(half // 256):
                block = pl.ds(tile * 256, 256)
                x[:, block] = rounded(
                    NS_A * x[:, block].astype(F32) + jnp.dot(poly[...], x[:, block], preferred_element_type=F32)
                )
            return carry

        lax.fori_loop(0, NS_ITERS - 1, iterate, 0)

        @pl.when((p >= WIDE) & (core == last_core))
        def _():
            give_last().start()
            xf[...] = x[:, f_lanes]

        grams((NS_ITERS - 1) % 2)

        @pl.when(p < WIDE)
        def _():
            part = poly_rows(g, pl.multiple_of(f * rows, 16), rows)
            pa[...] = rounded(NS_A * x[my_rows, :].astype(F32) + jnp.dot(part, x[...], preferred_element_type=F32))

        @pl.when(p >= WIDE)
        def _():
            pl.when(core == last_core)(lambda: give_last().wait_send())
            pl.when(core != last_core)(lambda: give_last().wait_recv())
            for t in range(2):
                top = pl.multiple_of(core * tall + t * rows, 16)
                part = poly_rows(g, top, rows)
                pa[:, t * columns : (t + 1) * columns] = rounded(
                    NS_A * xf[pl.ds(top, rows), :].astype(F32) + jnp.dot(part, xf[...], preferred_element_type=F32)
                )

    @pl.when(p < 2)
    def _():
        x[...] = sall[...]
        kt[...] = x[:, width:].T
        normal(kt, scale_of(jnp.sum(jnp.square(kt[...].astype(F32)))))
        wide = x[:, :width].astype(F32)
        x[:, :width] = rounded(wide * scale_of(jnp.sum(wide * wide)))

        def narrow_step(it, carry):
            gram = rounded(contract(kt[...], kt[...], 1, 1))
            turn = rounded(NS_B * gram.astype(F32) + NS_C * jnp.dot(gram, gram, preferred_element_type=F32))
            kt[...] = rounded(NS_A * kt[...].astype(F32) + jnp.dot(turn, kt[...], preferred_element_type=F32))
            return carry

        lax.fori_loop(0, NS_ITERS, narrow_step, 0)

        def gram_of():
            for r in range(4):
                chunk = pl.ds(r * step, step)
                g[chunk, :] = rounded(contract(x[chunk, :width], x[:, :width], 1, 1))

        def square_step(it, carry):
            gram_of()
            fill_poly()
            x[:, :width] = rounded(
                NS_A * x[:, :width].astype(F32) + jnp.dot(poly[...], x[:, :width], preferred_element_type=F32)
            )
            return carry

        lax.fori_loop(0, NS_ITERS - 1, square_step, 0)
        gram_of()
        part = poly_rows(g, pl.multiple_of(f * rows, 16), rows)
        square = rounded(
            NS_A * x[my_rows, :width].astype(F32) + jnp.dot(part, x[:, :width], preferred_element_type=F32)
        )
        x[:, width:] = kt[...].T
        pa[:, :width] = square
        pa[:, width:] = x[my_rows, width:]

    out_on, out_finish = spread_even(at, pa, o_out, og_l, og_s, og_r)
    total = gain_s[3]
    for j in range(1, parts):
        line_gain[j - 1].wait()
        total = total + gain_r[3 + j]
    gain_out[...] = total
    finish()
    out_on()

    def left(i, carry):
        one(0, i).wait_send()
        one(1, i).wait_send()
        two(i).wait_send()
        return carry

    lax.fori_loop(0, parts, left, 0)
    for j in range(1, parts):
        line(f ^ j, f).wait_send()
    pl.when(can_right())(lambda: rightward(f).wait_send())
    pl.when(can_left())(lambda: leftward(f).wait_send())
    for hop in range(1, parts):
        pl.when((f - hop >= 0) & can_right())(lambda hop=hop: rightward(f - hop).wait_send())
        pl.when((f + hop < parts) & can_left())(lambda hop=hop: leftward(f + hop).wait_send())
    out_finish()


def update_pass(xt, dy, gains, moments):
    parts = lax.axis_size("fsdp")
    kinds, width, tokens = xt.shape
    half = dy.shape[2]
    rows = width // parts
    keys = half - width
    columns = 2 * half // parts
    near = parts // 2
    dma = pltpu.SemaphoreType.DMA
    vm = pltpu.VMEM
    n_gain = 3 + parts
    return pl.pallas_call(
        update_kernel,
        out_shape=(
            jax.ShapeDtypeStruct((CLASSES, rows, half), BF16),
            jax.ShapeDtypeStruct((CLASSES, rows, half), BF16),
            jax.ShapeDtypeStruct(gains.shape, F32),
        ),
        in_specs=[ANY, ANY, VMEM] + [ANY] * 7,
        out_specs=(ANY, ANY, VMEM),
        scratch_shapes=[
            vm((kinds, width, 2 * tokens), BF16),
            vm((6, 2 * tokens, half), BF16),
            vm((2, parts, rows, half), BF16),
            vm((2, parts, rows, half), BF16),
            vm((parts, rows, half), BF16),
            vm((parts, rows, half), BF16),
            vm((rows, half), F32),
            vm((parts, rows, half), BF16),
            vm((parts, rows, half), BF16),
            vm((rows, half), F32),
            vm((rows, width), F32),
            vm((keys, rows), F32),
            vm((rows, half), BF16),
            vm((width, half), BF16),
            vm((4,) + gains.shape, F32),
            vm((n_gain,) + gains.shape, F32),
            vm((width, half), BF16),
            vm((width, width), BF16),
            vm((2, width, width), BF16),
            vm((width, width), BF16),
            vm((width, width), BF16),
            vm((8, 128), F32),
            vm((8, 128), F32),
            vm((rows, half), BF16),
            vm((keys, width), BF16),
            vm((near, rows, half), BF16),
            vm((width, columns), BF16),
            dma((7,)), dma((7,)), dma((7,)),
            dma((2, parts)), dma((2, parts)), dma((parts,)), dma((parts,)), dma((parts,)), dma((parts,)),
            dma((2,)), dma((n_gain,)), dma((n_gain,)),
            dma, dma((7,)), dma((CLASSES,)),
            dma((parts,)), dma((parts,)), dma((parts,)), dma((parts,)),
            dma((4,)), dma((2, 4)), dma, dma,
            dma((near,)), dma((near,)), dma, dma,
            dma, dma((7,)), dma((CLASSES,)),
        ],
        compiler_params=pltpu.CompilerParams(
            collective_id=4, has_side_effects=True, vmem_limit_bytes=62 << 20
        ),
        name="update_pass",
    )(xt, dy, gains, *moments)


def settle_wide(factors, *refs):
    gs, os = refs[0], refs[1]
    ms, ws, outs = refs[2:6], refs[6:10], refs[10:]
    width = ms[0].shape[1]
    half = gs.shape[2]

    def one(index, g, o, lanes):
        grad, moment, weight = (outs[3 * index + i] for i in range(3))
        value = g.astype(F32)
        grad[:, lanes] = value
        moment[:, lanes] = MOMENTUM * ms[index][:, lanes] + value
        weight[:, lanes] = ws[index][:, lanes].astype(F32) + factors[index] * o.astype(F32)

    for index in range(2):
        one(index, gs[index, :, :width], os[index, :, :width], slice(0, width))
    for index in range(2):
        for side in range(2):
            cls = 2 + 2 * index + side
            one(2 + index, gs[cls], os[cls], slice(side * half, (side + 1) * half))


def settle_turned(factors, g_tall, o_tall, g_pair, o_pair, *refs):
    ms, ws, outs = refs[0:3], refs[3:6], refs[6:]
    keys = ms[1].shape[0]

    def one(index, g, o):
        grad, moment, weight = (outs[3 * index + i] for i in range(3))
        grad[...] = g
        moment[...] = MOMENTUM * ms[index][...] + g
        weight[...] = ws[index][...].astype(F32) + factors[index] * o

    one(0, g_tall[0].astype(F32), o_tall[0].astype(F32))

    @pl.when(pl.program_id(0) == 0)
    def _():
        for index in range(2):
            start = g_pair.shape[2] - keys
            one(1 + index, g_pair[index, :, start:].astype(F32).T, o_pair[index, :, start:].astype(F32).T)


def settle(g, o, moments, shards, factors):
    m_q, m_k, m_o, m_v, m_gate, m_up, m_down = moments
    w_q, w_k, w_o, w_v, w_gate, w_up, w_down = shards
    f_q, f_k, f_v, f_o, f_gate, f_up, f_down = factors
    _, rows, half = g.shape
    width, columns = m_down.shape
    block = 48 if rows % 48 == 0 else rows
    piece = pl.BlockSpec((WIDE, block, half), lambda i: (0, i, 0))

    def row_block(array):
        return pl.BlockSpec((block, array.shape[1]), lambda i: (i, 0))

    def result(arrays):
        return tuple(jax.ShapeDtypeStruct(array.shape, F32) for array in arrays for _ in range(3))

    wide = (m_q, m_o, m_gate, m_up)
    first = pl.pallas_call(
        functools.partial(settle_wide, (f_q, f_o, f_gate, f_up)),
        grid=(rows // block,),
        out_shape=result(wide),
        in_specs=[piece, piece] + [row_block(array) for array in wide] * 2,
        out_specs=tuple(row_block(array) for array in wide for _ in range(3)),
        compiler_params=pltpu.CompilerParams(vmem_limit_bytes=48 << 20),
        name="settle_wide",
    )(g, o, *wide, w_q, w_o, w_gate, w_up)

    turned = (m_down, m_k, m_v)
    halves = half // columns
    tile = pl.BlockSpec((1, rows, columns), lambda i: (WIDE + i // halves, 0, i % halves))
    both = pl.BlockSpec((2, rows, half), lambda i: (0, 0, 0))
    specs = [pl.BlockSpec((rows, columns), lambda i: (i, 0))] + [
        pl.BlockSpec(array.shape, lambda i: (0, 0)) for array in turned[1:]
    ]
    second = pl.pallas_call(
        functools.partial(settle_turned, (f_down, f_k, f_v)),
        grid=(width // rows,),
        out_shape=result(turned),
        in_specs=[tile, tile, both, both] + specs * 2,
        out_specs=tuple(spec for spec in specs for _ in range(3)),
        compiler_params=pltpu.CompilerParams(vmem_limit_bytes=48 << 20),
        name="settle_turned",
    )(g, o, g, o, *turned, w_down, w_k, w_v)
    q, out, gate, up = (first[3 * i : 3 * i + 3] for i in range(4))
    down, k, v = (tuple(item.T for item in second[3 * i : 3 * i + 3]) for i in range(3))
    return list(zip(q, k, v, out, gate, up, down))


def rotary_tables(positions, width):
    half = width // 2
    frequency = THETA ** (-(jnp.arange(half, dtype=jnp.float32) * 2.0 / width))
    angle = positions.astype(jnp.float32)[:, None] * frequency[None, :]
    return (jnp.cos(angle)[:, None, :], jnp.sin(angle)[:, None, :])


def rotate(value, cosine, sine):
    half = value.shape[-1] // 2
    first = value[..., :half]
    second = value[..., half:]
    return jnp.concatenate(
        [first * cosine - second * sine, second * cosine + first * sine], axis=-1
    )


def unrotate(incoming, cosine, sine):
    half = incoming.shape[-1] // 2
    upper = incoming[..., :half]
    lower = incoming[..., half:]
    return jnp.concatenate([upper * cosine + lower * sine, lower * cosine - upper * sine], axis=-1)


def norm_forward(residual, gain):
    inverse = lax.rsqrt(jnp.mean(residual * residual, axis=-1, keepdims=True) + EPS)
    return ((residual * inverse * gain).astype(jnp.bfloat16), inverse)


def norm_backward(residual, inverse, gain, incoming):
    scaled = incoming * gain
    through = inverse * scaled - residual * inverse**3 * jnp.mean(
        scaled * residual, axis=-1, keepdims=True
    )
    return (through, jnp.sum(incoming * residual * inverse, axis=0))


def padded(array, axis, parts, count, full):
    if count == full:
        return array
    shape = array.shape
    split = array.reshape(shape[:axis] + (parts, count) + shape[axis + 1 :])
    pads = [(0, 0)] * split.ndim
    pads[axis + 1] = (0, full - count)
    return jnp.pad(split, pads).reshape(shape[:axis] + (parts * full,) + shape[axis + 1 :])


def trimmed(array, axis, parts, count, full):
    if count == full:
        return array
    shape = array.shape
    split = array.reshape(shape[:axis] + (parts, full) + shape[axis + 1 :])
    kept = lax.slice_in_dim(split, 0, count, axis=axis + 1)
    return kept.reshape(shape[:axis] + (parts * count,) + shape[axis + 1 :])


def plain_layer(
    layer_input, output_grad, wide, tall, norm_gains, block_order, sizes
):
    parts, width, half, kv, short, full, high = sizes
    hidden_size = 2 * half
    rows = layer_input.shape[1]
    block = rows // 2
    group = HEADS // KV_HEADS
    scale = 1.0 / math.sqrt(HEAD)
    ctx_place = lax.axis_index("ctx")
    offsets = jnp.arange(block, dtype=jnp.int32)
    own_blocks = lax.dynamic_slice_in_dim(block_order, 2 * ctx_place, 2)
    query_pos = (own_blocks[:, None] * block + offsets[None, :]).reshape(rows)
    key_pos = (block_order[:, None] * block + offsets[None, :]).reshape(-1)

    all_wide, all_tall = gather_weights(wide, tall)
    w_qk, w_ov, w_gate_0, w_gate_1, w_up_0, w_up_1 = [all_wide[i].reshape(width, half) for i in range(WIDE)]
    w_down = [all_tall[i].reshape(half, width) for i in range(2)]

    residual = layer_input[0].astype(jnp.float32)
    normed_first, inverse_first = norm_forward(residual, norm_gains[0])
    qk_pre = jnp.dot(normed_first, w_qk, preferred_element_type=jnp.float32)
    query_pre = qk_pre[:, :width].reshape(rows, HEADS, HEAD)
    key_pre = qk_pre[:, width:].reshape(rows, KV_HEADS, HEAD)
    value_low = (
        jnp.dot(normed_first, w_ov, preferred_element_type=jnp.float32)[:, width:]
        .astype(jnp.bfloat16)
        .reshape(rows, KV_HEADS, HEAD)
    )
    cosine, sine = rotary_tables(query_pos, HEAD)
    query_rot = rotate(query_pre, cosine, sine).astype(jnp.bfloat16)
    key_rot = rotate(key_pre, cosine, sine).astype(jnp.bfloat16)
    keys_all, values_all = (
        lax.all_gather(key_rot, "ctx", axis=0, tiled=True),
        lax.all_gather(value_low, "ctx", axis=0, tiled=True),
    )
    keys_head = keys_all.transpose(1, 0, 2)
    values_head = values_all.transpose(1, 0, 2)
    queries_head = (
        query_rot.reshape(rows, KV_HEADS, group, HEAD)
        .transpose(1, 2, 0, 3)
        .reshape(KV_HEADS, group * rows, HEAD)
    )
    row_pos = jnp.tile(query_pos, group)
    allowed = key_pos[None, :] <= row_pos[:, None]

    def head_forward(item):
        query, key, value = item
        scores = jnp.where(allowed, contract(query, key, 1, 1) * scale, MASKED)
        top = jnp.max(scores, axis=-1, keepdims=True)
        expo = jnp.exp(scores - top)
        total = jnp.sum(expo, axis=-1, keepdims=True)
        probs_low = (expo / total).astype(jnp.bfloat16)
        return (
            jnp.dot(probs_low, value, preferred_element_type=jnp.float32),
            (top + jnp.log(total))[:, 0],
        )

    mixed, log_total = lax.map(head_forward, (queries_head, keys_head, values_head))
    attended = (
        mixed.reshape(KV_HEADS, group, rows, HEAD)
        .transpose(2, 0, 1, 3)
        .reshape(rows, HEADS * HEAD)
        .astype(jnp.bfloat16)
    )
    w_out = w_ov[:, :width]
    middle = residual + jnp.dot(attended, w_out, preferred_element_type=jnp.float32)
    normed_second, inverse_second = norm_forward(middle, norm_gains[1])

    def sides(left, right):
        return jnp.concatenate([left, right], axis=1)

    gate = sides(
        jnp.dot(normed_second, w_gate_0, preferred_element_type=jnp.float32),
        jnp.dot(normed_second, w_gate_1, preferred_element_type=jnp.float32),
    )
    lifted = sides(
        jnp.dot(normed_second, w_up_0, preferred_element_type=jnp.float32),
        jnp.dot(normed_second, w_up_1, preferred_element_type=jnp.float32),
    )
    sigma = jax.nn.sigmoid(gate)
    hidden = (gate * sigma * lifted).astype(jnp.bfloat16)
    hidden_split = hidden.reshape(rows, parts, 2, high)
    hidden_sides = [hidden_split[:, :, i].reshape(rows, half) for i in range(2)]
    layer_output = (
        middle
        + jnp.dot(hidden_sides[0], w_down[0], preferred_element_type=jnp.float32)
        + jnp.dot(hidden_sides[1], w_down[1], preferred_element_type=jnp.float32)
    ).astype(jnp.bfloat16)
    upstream = output_grad[0]
    grad_hidden = jnp.stack(
        [contract(upstream, w_down[i], 1, 1).reshape(rows, parts, high) for i in range(2)], axis=2
    ).reshape(rows, hidden_size)
    grad_gate = (grad_hidden * lifted * sigma * (1.0 + gate * (1.0 - sigma))).astype(jnp.bfloat16)
    grad_lifted = (grad_hidden * gate * sigma).astype(jnp.bfloat16)
    grad_normed_second = (
        contract(grad_gate[:, :half], w_gate_0, 1, 1)
        + contract(grad_gate[:, half:], w_gate_1, 1, 1)
        + contract(grad_lifted[:, :half], w_up_0, 1, 1)
        + contract(grad_lifted[:, half:], w_up_1, 1, 1)
    )
    through_second, gain_second = norm_backward(
        middle, inverse_second, norm_gains[1], grad_normed_second
    )
    grad_middle = upstream.astype(jnp.float32) + through_second
    grad_branch = grad_middle.astype(jnp.bfloat16)
    grad_attended = contract(grad_branch, w_out, 1, 1).astype(jnp.bfloat16)
    grad_heads = (
        grad_attended.reshape(rows, KV_HEADS, group, HEAD)
        .transpose(1, 2, 0, 3)
        .reshape(KV_HEADS, group * rows, HEAD)
    )

    def head_backward(item):
        query, key, value, grad_out, log_row = item
        scores = jnp.where(allowed, contract(query, key, 1, 1) * scale, MASKED)
        probs = jnp.exp(scores - log_row[:, None])
        grad_value_part = contract(probs.astype(jnp.bfloat16), grad_out, 0, 0)
        grad_probs = contract(grad_out, value, 1, 1)
        grad_scores = (
            probs * (grad_probs - jnp.sum(grad_probs * probs, axis=-1, keepdims=True))
        ).astype(jnp.bfloat16)
        grad_query_part = jnp.dot(grad_scores, key, preferred_element_type=jnp.float32) * scale
        grad_key_part = contract(grad_scores, query, 0, 0) * scale
        return (grad_query_part, grad_key_part, grad_value_part)

    grad_query_rot, grad_key_all, grad_value_all = lax.map(
        head_backward, (queries_head, keys_head, values_head, grad_heads, log_total)
    )
    grad_key_own, grad_value_own = (
        lax.psum_scatter(
            grad_key_all.astype(jnp.bfloat16), "ctx", scatter_dimension=1, tiled=True
        ).astype(jnp.float32),
        lax.psum_scatter(
            grad_value_all.astype(jnp.bfloat16), "ctx", scatter_dimension=1, tiled=True
        ).astype(jnp.float32),
    )
    grad_query = (
        unrotate(
            grad_query_rot.reshape(KV_HEADS, group, rows, HEAD)
            .transpose(2, 0, 1, 3)
            .reshape(rows, HEADS, HEAD),
            cosine,
            sine,
        )
        .reshape(rows, HEADS * HEAD)
        .astype(jnp.bfloat16)
    )
    grad_key = (
        unrotate(grad_key_own.transpose(1, 0, 2), cosine, sine)
        .reshape(rows, KV_HEADS * HEAD)
        .astype(jnp.bfloat16)
    )
    grad_value = (
        grad_value_own.transpose(1, 0, 2).reshape(rows, KV_HEADS * HEAD).astype(jnp.bfloat16)
    )
    grad_qk = sides(grad_query, grad_key)
    zero_query = jnp.zeros((rows, width), jnp.bfloat16)
    grad_v = sides(zero_query, grad_value)
    grad_normed_first = contract(grad_qk, w_qk, 1, 1) + contract(grad_v, w_ov, 1, 1)
    through_first, gain_first = norm_backward(
        residual, inverse_first, norm_gains[0], grad_normed_first
    )
    input_gradient = grad_middle + through_first

    xt = jnp.stack([item.T for item in (normed_first, attended, normed_second, upstream)])
    xt = padded(xt, 1, parts, short, full)
    dy = jnp.stack(
        [
            grad_qk,
            sides(grad_branch, jnp.zeros((rows, kv), jnp.bfloat16)),
            grad_gate[:, :half],
            grad_gate[:, half:],
            grad_lifted[:, :half],
            grad_lifted[:, half:],
            hidden_sides[0],
            hidden_sides[1],
            grad_v,
        ]
    )
    gains = jnp.pad(jnp.stack([gain_first, gain_second]), ((0, 6), (0, 0)))
    return layer_output, input_gradient, xt, dy, gains


def rotation(block_order, rows):
    block = rows // 2
    ctx_place = lax.axis_index("ctx")
    offsets = jnp.arange(block, dtype=jnp.int32)
    own_blocks = lax.dynamic_slice_in_dim(block_order, 2 * ctx_place, 2)
    query_pos = (own_blocks[:, None] * block + offsets[None, :]).reshape(rows)
    key_pos = (block_order[:, None] * block + offsets[None, :]).reshape(-1)
    bias = jnp.where(key_pos[:, None] <= query_pos[None, :], 0.0, MASKED).astype(jnp.float32)
    lane = jnp.arange(128, dtype=jnp.int32)
    index = (lane % (HEAD // 2)).astype(jnp.float32)
    frequency = THETA ** (-(index * 2.0 / HEAD))
    angle = query_pos.astype(jnp.float32)[:, None] * frequency[None, :]
    cosine, sine = jnp.cos(angle), jnp.sin(angle)
    early = (lane % HEAD < HEAD // 2)[None, :]
    return (cosine, jnp.where(early, 0.0, sine), jnp.where(early, -sine, 0.0)), bias


def plain_step(layer_input, output_grad, norm_gains, block_order, weights, olds, factors, sizes):
    parts, width, half, kv, short, full, high = sizes
    query_weight, key_weight, value_weight, output_weight, gate_weight, up_weight, down_weight = weights
    (
        query_momentum,
        key_momentum,
        value_momentum,
        output_momentum,
        gate_momentum,
        up_momentum,
        down_momentum,
    ) = olds

    def sides(left, right):
        return jnp.concatenate([left, right], axis=1)

    wide = jnp.stack(
        [
            jnp.concatenate([query_weight, key_weight], axis=1),
            jnp.concatenate([output_weight, value_weight], axis=1),
            gate_weight[:, :half],
            gate_weight[:, half:],
            up_weight[:, :half],
            up_weight[:, half:],
        ]
    )
    tall = down_weight.reshape(2, high, width)
    layer_output, input_gradient, xt, dy, gains = plain_layer(
        layer_input, output_grad, wide, tall, norm_gains, block_order, sizes
    )

    def pad_rows(array):
        return padded(array, 0, 1, short, full)

    def pad_columns(array):
        return padded(array, 1, parts, short, full)

    moments = (
        pad_rows(sides(query_momentum, key_momentum)),
        pad_rows(sides(output_momentum, value_momentum)),
        pad_rows(gate_momentum),
        pad_rows(up_momentum),
        pad_columns(down_momentum),
    )
    g_wide, g_tall, s_wide, s_tall, gain_sum = reduce_gradients(xt, dy, gains, moments, full, high)
    o_wide, o_tall = orthogonalize(s_wide, s_tall, full, high, width)

    def unpack(wide_pieces, tall_pieces):
        pieces = wide_pieces[:, :short]
        tall = trimmed(tall_pieces, 2, parts, short, full).reshape(2 * high, width)
        return (
            pieces[0, :, :width],
            pieces[0, :, width:],
            pieces[1, :, width:],
            pieces[1, :, :width],
            sides(pieces[2], pieces[3]),
            sides(pieces[4], pieces[5]),
            tall,
        )

    gradients = [item.astype(jnp.float32) for item in unpack(g_wide, g_tall)]
    orthos = unpack(o_wide, o_tall)
    moments = [MOMENTUM * old + new for old, new in zip(olds, gradients)]
    new_weights = [
        weight.astype(jnp.float32) + factor * ortho.astype(jnp.float32)
        for weight, factor, ortho in zip(weights, factors, orthos)
    ]
    return layer_output, input_gradient, gradients, moments, new_weights, gain_sum


def on_device(
    layer_input,
    output_grad,
    query_weight,
    key_weight,
    value_weight,
    output_weight,
    gate_weight,
    up_weight,
    down_weight,
    norm_gains,
    query_momentum,
    key_momentum,
    value_momentum,
    output_momentum,
    gate_momentum,
    up_momentum,
    down_momentum,
    gain_momentum,
    block_order,
):
    parts = lax.axis_size("fsdp")
    width = layer_input.shape[2]
    half = gate_weight.shape[1] // 2
    kv = key_weight.shape[1]
    short = width // parts
    full = -(-short // 16) * 16
    high = half // parts
    sizes = (parts, width, half, kv, short, full, high)

    weights = (query_weight, key_weight, value_weight, output_weight, gate_weight, up_weight, down_weight)
    olds = (
        query_momentum,
        key_momentum,
        value_momentum,
        output_momentum,
        gate_momentum,
        up_momentum,
        down_momentum,
    )
    factors = []
    for index, weight in enumerate(weights):
        step_rate = OUT_RATE if index == 3 else RATE
        factors.append(-step_rate * max(1.0, weight.shape[1] / (weight.shape[0] * parts)) ** 0.5)

    fused = (
        lax.axis_size("ctx") == CLASSES
        and short == full
        and parts % 2 == 0
        and half % (2 * half // parts) == 0
        and (2 * half // parts) % 128 == 0
        and layer_input.shape[1] == 128
    )
    if fused:
        tables, bias = rotation(block_order, layer_input.shape[1])

        def turned(items):
            q, k, v, o, gate, up, down = items
            return (q, k.T, o, v.T, gate, up, down.T)

        shards, moments = turned(weights), turned(olds)
        out_turned, grad_turned, xt, dy, gains = layer_pass(
            layer_input[0].T, output_grad[0].T, norm_gains, tables, bias, shards
        )
        g, o, gain_sum = update_pass(xt, dy, gains, moments)
        gradients, moments, new_weights = settle(g, o, moments, shards, factors)
        layer_output, input_gradient = out_turned.T, grad_turned.T
    else:
        layer_output, input_gradient, gradients, moments, new_weights, gain_sum = plain_step(
            layer_input, output_grad, norm_gains, block_order, weights, olds, factors, sizes
        )
    gain_width = norm_gains.shape[1] // parts
    place = lax.axis_index("fsdp") * gain_width
    gain_gradient = lax.dynamic_slice_in_dim(gain_sum[:2], place, gain_width, 1)
    gain_shard = lax.dynamic_slice_in_dim(norm_gains, place, gain_width, 1)
    gain_moment = MOMENTUM * gain_momentum + gain_gradient
    new_gains = gain_shard - GAIN_RATE * gain_moment
    return (
        layer_output[None],
        input_gradient[None],
        *gradients,
        gain_gradient,
        *moments,
        gain_moment,
        *new_weights,
        new_gains,
    )


def solution(mesh):
    tokens = P("fsdp", "ctx", None)
    shard = P("fsdp", None)
    gains = P(None, "fsdp")
    return jax.shard_map(
        on_device,
        mesh=mesh,
        in_specs=(tokens, tokens) + (shard,) * 7 + (P(),) + (shard,) * 7 + (gains, P()),
        out_specs=(tokens, tokens) + ((shard,) * 7 + (gains,)) * 3,
        check_vma=False,
    )
```

```python
import functools
import math

import jax
import jax.numpy as jnp
from jax import lax
from jax.experimental import pallas as pl
from jax.experimental.pallas import tpu as pltpu
from jax.sharding import PartitionSpec as P

HEADS = 15
KV_HEADS = 5
HEAD = 64
NS_ITERS = 5


EPS = 1e-05
THETA = 100000.0
NS_A = 3.4445
NS_B = -4.775
NS_C = 2.0315
MOMENTUM = 0.95
RATE = 0.2
OUT_RATE = 6.0
GAIN_RATE = 0.002
MASKED = -1e30

MESH = pl.DeviceIdType.MESH
BF16 = jnp.bfloat16
F32 = jnp.float32
ANY = pl.BlockSpec(memory_space=pl.ANY)
VMEM = pl.BlockSpec(memory_space=pltpu.VMEM)
CLASSES = 8
WIDE = 6


def contract(left, right, left_dim, right_dim):
    return lax.dot_general(
        left, right, (((left_dim,), (right_dim,)), ((), ())), preferred_element_type=jnp.float32
    )


class Place:
    def __init__(self):
        self.parts = lax.axis_size("fsdp")
        self.extra = lax.axis_size("ctx") // CLASSES
        self.c = lax.axis_index("ctx")
        self.f = lax.axis_index("fsdp")
        self.p = lax.rem(self.c, CLASSES)
        self.core = lax.rem(self.c, 2)
        self.b1 = jnp.where(self.core == 0, 2, 4)
        self.b2 = jnp.where(self.core == 0, 4, 2)

    def peer(self, bits):
        return (self.c ^ bits, self.f)

    def along(self, j):
        return (self.c, self.f ^ j)

    def other(self, j):
        groups = self.extra
        return (lax.rem(self.c + CLASSES * j, CLASSES * groups), self.f)

    def barrier(self, bits=(1, 2, 4), line=True, others=False):
        sem = pltpu.get_barrier_semaphore()
        targets = [self.peer(b) for b in bits]
        if line:
            targets += [self.along(j) for j in range(1, self.parts)]
        if others:
            targets += [self.other(j) for j in range(1, self.extra)]
        for target in targets:
            pl.semaphore_signal(sem, inc=1, device_id=target, device_id_type=MESH)
        pl.semaphore_wait(sem, len(targets))


def remote(src, dst, send, recv, target):
    return pltpu.make_async_remote_copy(
        src_ref=src, dst_ref=dst, send_sem=send, recv_sem=recv, device_id=target, device_id_type=MESH
    )


def by_kind(cls, wide, tall):
    pl.when(cls < WIDE)(wide)
    pl.when(cls >= WIDE)(tall)


def weights_kernel(in_a, in_b, out_a, out_b, local, zs, s1, s2, sc, recv):
    at = Place()
    p, f, parts = at.p, at.f, at.parts
    at.barrier()
    copies = [
        pltpu.make_async_copy(in_a, out_a.at[:, f], local.at[0]),
        pltpu.make_async_copy(in_b, out_b.at[:, f], local.at[1]),
    ]
    for copy in copies:
        copy.start()

    def act(cls, j, g, send, target, what, first=False):
        def wide():
            dst = out_a.at[cls, g]
            src = in_a.at[cls] if first else dst
            getattr(remote(src, dst, send, recv.at[cls, j], target), what)()

        def tall():
            dst = out_b.at[cls - WIDE, g]
            src = in_b.at[cls - WIDE] if first else dst
            getattr(remote(src, dst, send, recv.at[cls, j], target), what)()

        by_kind(cls, wide, tall)

    sends = []

    def send(cls, j, g, sem, target, first=False):
        act(cls, j, g, sem, target, "start", first)
        sends.append((cls, j, g, sem, target, first))

    def arrived(cls, j):
        act(cls, j, f ^ j, zs.at[j], at.along(j), "wait_recv")

    for j in range(1, parts):
        send(p, j, f, zs.at[j], at.along(j), True)
    for j in range(1, parts):
        arrived(p, j)
        send(p, j, f ^ j, s1.at[0, j], at.peer(at.b1))
        send(p, j, f ^ j, s2.at[0, j], at.peer(at.b2))
        send(p, j, f ^ j, sc.at[0, j], at.peer(1))
    for j in range(1, parts):
        arrived(p ^ at.b1, j)
        send(p ^ at.b1, j, f ^ j, s2.at[1, j], at.peer(at.b2))
        send(p ^ at.b1, j, f ^ j, sc.at[1, j], at.peer(1))
    for slot, bits in ((2, at.b2), (3, at.b1 ^ at.b2)):
        for j in range(1, parts):
            arrived(p ^ bits, j)
            send(p ^ bits, j, f ^ j, sc.at[slot, j], at.peer(1))
    for bits in (1, 3, 5, 7):
        for j in range(1, parts):
            arrived(p ^ bits, j)
    for cls, j, g, sem, target, first in sends:
        act(cls, j, g, sem, target, "wait_send", first)
    for copy in copies:
        copy.wait()


def gather_weights(wide, tall):
    parts = lax.axis_size("fsdp")
    dma = pltpu.SemaphoreType.DMA
    return pl.pallas_call(
        weights_kernel,
        out_shape=(
            jax.ShapeDtypeStruct((WIDE, parts) + wide.shape[1:], BF16),
            jax.ShapeDtypeStruct((CLASSES - WIDE, parts) + tall.shape[1:], BF16),
        ),
        in_specs=[ANY, ANY],
        out_specs=(ANY, ANY),
        scratch_shapes=[
            dma((2,)),
            dma((parts,)),
            dma((1, parts)),
            dma((2, parts)),
            dma((4, parts)),
            dma((CLASSES, parts)),
        ],
        compiler_params=pltpu.CompilerParams(collective_id=0, has_side_effects=True),
        name="gather_weights",
    )(wide, tall)


def spread(at, own_a, own_b, out_a, out_b, local, ss, recv):
    p = at.p

    def act(cls, sem, target, what, first=False):
        def wide():
            dst = out_a.at[cls]
            getattr(remote(own_a if first else dst, dst, sem, recv.at[cls], target), what)()

        def tall():
            dst = out_b.at[cls - WIDE]
            getattr(remote(own_b if first else dst, dst, sem, recv.at[cls], target), what)()

        by_kind(cls, wide, tall)

    def keep(what):
        def wide():
            getattr(pltpu.make_async_copy(own_a, out_a.at[p], local), what)()

        def tall():
            getattr(pltpu.make_async_copy(own_b, out_b.at[p - WIDE], local), what)()

        by_kind(p, wide, tall)

    sends = []

    def send(cls, slot, target, first=False):
        act(cls, ss.at[slot], target, "start", first)
        sends.append((cls, slot, target, first))

    def arrived(cls):
        act(cls, ss.at[0], at.peer(1), "wait_recv")

    send(p, 0, at.peer(at.b1), True)
    send(p, 1, at.peer(at.b2), True)
    send(p, 2, at.peer(1), True)
    keep("start")

    def finish():
        arrived(p ^ at.b1)
        send(p ^ at.b1, 3, at.peer(at.b2))
        send(p ^ at.b1, 4, at.peer(1))
        arrived(p ^ at.b2)
        send(p ^ at.b2, 5, at.peer(1))
        arrived(p ^ at.b1 ^ at.b2)
        send(p ^ at.b1 ^ at.b2, 6, at.peer(1))
        for bits in (1, 3, 5, 7):
            arrived(p ^ bits)
        for cls, slot, target, first in sends:
            act(cls, ss.at[slot], target, "wait_send", first)
        keep("wait")

    return finish


def reduce_kernel(
    parts, extra, high,
    xt_in, dy_in, gain_in, m_qk, m_ov, m_gate, m_up, m_down,
    g_a, g_b, s_a, s_b, gain_out,
    xt, dy, p1s, p1r, p2s, p2r, own, own_t, za_s, za_r, zb_s, zb_r, ma, mb, ga, gb, sa, sb, es, er, gain_s, gain_r,
    ls, xs, xr, s1, r1, s2, r2, zs, zr, esem, ersem, msem, gs, gr, ag_l, ag_s, ag_r, ss, sr, sl,
):
    at = Place()
    p, f, core = at.p, at.f, at.core
    tokens = xt_in.shape[2]
    rows = ma.shape[0]
    half = dy.shape[2]

    def moment(what):
        for cls in range(CLASSES):
            @pl.when(p == cls)
            def _(cls=cls):
                side = cls % 2
                if cls < 2:
                    src, dst = (m_qk, m_ov)[cls], ma
                elif cls < WIDE:
                    whole = m_gate if cls < 4 else m_up
                    src, dst = whole.at[:, pl.ds(side * half, half)], ma
                else:
                    src, dst = m_down.at[pl.ds(side * high, high)], mb
                getattr(pltpu.make_async_copy(src, dst, msem), what)()

    moment("start")
    mine = [pltpu.make_async_copy(xt_in, xt.at[:, :, pl.ds(0, tokens)], ls.at[0])]
    for slot in range(4):
        mine.append(
            pltpu.make_async_copy(dy_in.at[core + 2 * slot], dy.at[slot, pl.ds(0, tokens)], ls.at[1 + slot])
        )
    mine.append(pltpu.make_async_copy(dy_in.at[8], dy.at[4, pl.ds(0, tokens)], ls.at[5]))
    for copy in mine:
        copy.start()
    at.barrier(others=True)
    pair = at.peer(1)
    theirs = [remote(xt_in, xt.at[:, :, pl.ds(tokens, tokens)], xs.at[0], xr.at[0], pair)]
    for slot in range(4):
        theirs.append(
            remote(dy_in.at[1 - core + 2 * slot], dy.at[slot, pl.ds(tokens, tokens)], xs.at[1 + slot], xr.at[1 + slot], pair)
        )
    theirs.append(remote(dy_in.at[8], dy.at[4, pl.ds(tokens, tokens)], xs.at[5], xr.at[5], pair))
    for copy in theirs:
        copy.start()

    def swap(slot, target):
        return remote(gain_s.at[slot], gain_r.at[slot], gs.at[slot], gr.at[slot], target)

    gain_s[0] = gain_in[...]
    swaps = [swap(0, pair)]
    swaps[0].start()
    for copy in mine:
        copy.wait()
    for copy in theirs:
        copy.wait()

    def term(cls, r):
        at_rows = pl.ds(pl.multiple_of(r * rows, rows), rows)
        slot = lax.div(cls, 2)
        kind = jnp.where(cls == 0, 0, jnp.where(cls == 1, 1, jnp.where(cls < WIDE, 2, 3)))
        value = jnp.dot(xt[kind, at_rows, :], dy[slot], preferred_element_type=F32)
        return value

    def with_values(cls, r, put):
        at_rows = pl.ds(pl.multiple_of(r * rows, rows), rows)

        @pl.when(cls == 1)
        def _():
            put(term(cls, r) + jnp.dot(xt[0, at_rows, :], dy[4], preferred_element_type=F32))

        @pl.when(cls != 1)
        def _():
            put(term(cls, r))

    def order(i):
        return lax.rem(f + 1 + i, parts)

    def one(slot, i):
        r = order(i)
        return remote(p1s.at[slot, r], p1r.at[slot, r], s1.at[slot, r], r1.at[slot, r], at.peer(at.b1))

    for slot, bits in ((0, at.b1 ^ at.b2), (1, at.b1)):
        def first(i, carry, slot=slot, bits=bits):
            r = order(i)

            def put(value):
                p1s[slot, r] = value.astype(BF16)

            with_values(p ^ bits, r, put)
            one(slot, i).start()
            return carry

        lax.fori_loop(0, parts, first, 0)

    swaps[0].wait()
    gain_s[1] = gain_s[0] + gain_r[0]
    swaps.append(swap(1, at.peer(2)))
    swaps[1].start()

    def two(i):
        r = order(i)
        return remote(p2s.at[r], p2r.at[r], s2.at[r], r2.at[r], at.peer(at.b2))

    def second(i, carry):
        r = order(i)
        one(0, i).wait_recv()

        def put(value):
            p2s[r] = (value + p1r[0, r].astype(F32)).astype(BF16)

        with_values(p ^ at.b2, r, put)
        two(i).start()
        return carry

    lax.fori_loop(0, parts, second, 0)
    swaps[1].wait()
    gain_s[2] = gain_s[1] + gain_r[1]
    swaps.append(swap(2, at.peer(4)))
    swaps[2].start()

    def line_a(r, source):
        return remote(za_s.at[r], za_r.at[source], zs.at[r], zr.at[source], (at.c, r))

    def line_b(r, source):
        return remote(
            zb_s.at[pl.ds(pl.multiple_of(r * high, high), high)],
            zb_r.at[source], zs.at[r], zr.at[source], (at.c, r),
        )

    early = extra == 1

    def third(i, carry):
        r = order(i)
        one(1, i).wait_recv()
        two(i).wait_recv()

        def put(value):
            total = value + p1r[1, r].astype(F32) + p2r[r].astype(F32)
            own[r] = total
            if early:
                za_s[r] = total.astype(BF16)

        with_values(p, r, put)
        if early:
            @pl.when((p < WIDE) & (i < parts - 1))
            def _():
                line_a(r, f).start()
        return carry

    lax.fori_loop(0, parts, third, 0)
    swaps[2].wait()
    gain_s[3] = gain_s[2] + gain_r[2]

    if not early:
        es[...] = own[...].astype(BF16)
        group = [
            remote(es, er.at[j - 1], esem.at[j - 1], ersem.at[j - 1], at.other(j)) for j in range(1, extra)
        ]
        for copy in group:
            copy.start()
        for j in range(1, extra):
            group[j - 1].wait_recv()
            own[...] = own[...] + er[j - 1].astype(F32)
        for copy in group:
            copy.wait_send()
        za_s[...] = own[...].astype(BF16)

        @pl.when(p < WIDE)
        def _():
            for j in range(1, parts):
                line_a(f ^ j, f).start()

    @pl.when(p >= WIDE)
    def _():
        for tile in range(half // 128):
            for r in range(parts):
                block = own[r, :, pl.ds(tile * 128, 128)]
                if rows % 128 == 0:
                    own_t[pl.ds(tile * 128, 128), pl.ds(r * rows, rows)] = block.T
            if rows % 128 != 0:
                column = own[:, :, pl.ds(tile * 128, 128)].reshape(parts * rows, 128)
                own_t[pl.ds(tile * 128, 128), :] = column.T
        zb_s[...] = own_t[...].astype(BF16)
        for j in range(1, parts):
            line_b(f ^ j, f).start()

    line_gain = [
        remote(gain_s.at[3], gain_r.at[3 + j], gs.at[3 + j], gr.at[3 + j], at.along(j)) for j in range(1, parts)
    ]
    other_gain = []
    for copy in line_gain:
        copy.start()

    moment("wait")

    @pl.when(p < WIDE)
    def _():
        total = own[f]
        for j in range(1, parts):
            line_a(f ^ j, f ^ j).wait_recv()
            total = total + za_r[f ^ j].astype(F32)
        ga[...] = total.astype(BF16)
        sa[...] = (MOMENTUM * ma[...] + total).astype(BF16)

    @pl.when(p >= WIDE)
    def _():
        total = own_t[pl.ds(pl.multiple_of(f * high, high), high), :]
        for j in range(1, parts):
            line_b(f ^ j, f ^ j).wait_recv()
            total = total + zb_r[f ^ j].astype(F32)
        gb[...] = total.astype(BF16)
        sb[...] = (MOMENTUM * mb[...] + total).astype(BF16)

    def share_a(j, source):
        return remote(sa, s_a.at[pl.ds(pl.multiple_of(source * rows, rows), rows)], ss.at[j], sr.at[j], at.along(j))

    def share_b(j, source):
        return remote(sb, s_b.at[pl.ds(pl.multiple_of(source * high, high), high)], ss.at[j], sr.at[j], at.along(j))

    @pl.when(p < WIDE)
    def _():
        for j in range(1, parts):
            share_a(j, f).start()
        pltpu.make_async_copy(sa, s_a.at[pl.ds(pl.multiple_of(f * rows, rows), rows)], sl).start()

    @pl.when(p >= WIDE)
    def _():
        for j in range(1, parts):
            share_b(j, f).start()
        pltpu.make_async_copy(sb, s_b.at[pl.ds(pl.multiple_of(f * high, high), high)], sl).start()

    finish = spread(at, ga, gb, g_a, g_b, ag_l, ag_s, ag_r)
    total = gain_s[3]
    for j in range(1, parts):
        line_gain[j - 1].wait()
        total = total + gain_r[3 + j]
    if extra > 1:
        gain_s[4] = total
        other_gain = [
            remote(gain_s.at[4], gain_r.at[3 + parts + j], gs.at[3 + parts + j], gr.at[3 + parts + j], at.other(j))
            for j in range(1, extra)
        ]
        for copy in other_gain:
            copy.start()
        for j in range(1, extra):
            other_gain[j - 1].wait()
            total = total + gain_r[3 + parts + j]
    gain_out[...] = total
    finish()

    for slot in range(2):
        lax.fori_loop(0, parts, lambda i, carry, slot=slot: (one(slot, i).wait_send(), carry)[1], 0)
    lax.fori_loop(0, parts, lambda i, carry: (two(i).wait_send(), carry)[1], 0)

    @pl.when(p < WIDE)
    def _():
        for j in range(1, parts):
            line_a(f ^ j, f).wait_send()
            share_a(j, f).wait_send()
            share_a(j, f ^ j).wait_recv()
        pltpu.make_async_copy(sa, s_a.at[pl.ds(pl.multiple_of(f * rows, rows), rows)], sl).wait()

    @pl.when(p >= WIDE)
    def _():
        for j in range(1, parts):
            line_b(f ^ j, f).wait_send()
            share_b(j, f).wait_send()
            share_b(j, f ^ j).wait_recv()
        pltpu.make_async_copy(sb, s_b.at[pl.ds(pl.multiple_of(f * high, high), high)], sl).wait()


def reduce_gradients(xt, dy, gains, moments, rows, high):
    parts = lax.axis_size("fsdp")
    extra = lax.axis_size("ctx") // CLASSES
    kinds, depth, tokens = xt.shape
    half = dy.shape[2]
    dma = pltpu.SemaphoreType.DMA
    vm = pltpu.VMEM
    n_gain = 4 + parts + extra
    group = max(extra - 1, 1)
    spare = (parts, rows, half) if extra > 1 else (1, 16, 128)
    return pl.pallas_call(
        functools.partial(reduce_kernel, parts, extra, high),
        out_shape=(
            jax.ShapeDtypeStruct((WIDE, rows, half), BF16),
            jax.ShapeDtypeStruct((CLASSES - WIDE, high, depth), BF16),
            jax.ShapeDtypeStruct((depth, half), BF16),
            jax.ShapeDtypeStruct((half, depth), BF16),
            jax.ShapeDtypeStruct(gains.shape, F32),
        ),
        in_specs=[ANY, ANY, VMEM] + [ANY] * 5,
        out_specs=(ANY, ANY, ANY, ANY, VMEM),
        scratch_shapes=[
            vm((kinds, depth, 2 * tokens), BF16),
            vm((5, 2 * tokens, half), BF16),
            vm((2, parts, rows, half), BF16),
            vm((2, parts, rows, half), BF16),
            vm((parts, rows, half), BF16),
            vm((parts, rows, half), BF16),
            vm((parts, rows, half), F32),
            vm((half, depth), F32),
            vm((parts, rows, half), BF16),
            vm((parts, rows, half), BF16),
            vm((half, depth), BF16),
            vm((parts, high, depth), BF16),
            vm((rows, half), F32),
            vm((high, depth), F32),
            vm((rows, half), BF16),
            vm((high, depth), BF16),
            vm((rows, half), BF16),
            vm((high, depth), BF16),
            vm(spare, BF16),
            vm((group,) + spare, BF16),
            vm((5,) + gains.shape, F32),
            vm((n_gain,) + gains.shape, F32),
            dma((6,)), dma((6,)), dma((6,)),
            dma((2, parts)), dma((2, parts)), dma((parts,)), dma((parts,)), dma((parts,)), dma((parts,)),
            dma((group,)), dma((group,)), dma, dma((n_gain,)), dma((n_gain,)),
            dma, dma((7,)), dma((CLASSES,)), dma((parts,)), dma((parts,)), dma,
        ],
        compiler_params=pltpu.CompilerParams(
            collective_id=1, has_side_effects=True, vmem_limit_bytes=62 << 20
        ),
        name="reduce_gradients",
    )(xt, dy, gains, *moments)


def rounded(value):
    return value.astype(BF16)


def poly_rows(g, row_start, count):
    block = g[pl.ds(row_start, count), :]
    return rounded(NS_B * block.astype(F32) + NS_C * jnp.dot(block, g[...], preferred_element_type=F32))


def ortho_kernel(
    parts, rows, high, narrow,
    s_a, s_b, o_a, o_b,
    x, x_t, gs, gr, g, poly, sq, sq_r, pa, pb, kt,
    gsem, rsem, qs, qr, ag_l, ag_s, ag_r,
):
    at = Place()
    p, f = at.p, at.f
    depth, half = x.shape
    step = depth // 4
    at.barrier(line=False)
    pair = at.peer(1)

    @pl.when(p < WIDE)
    def _():
        x[...] = s_a[...]

    @pl.when(p >= WIDE)
    def _():
        for tile in range(half // 128):
            x[:, pl.ds(tile * 128, 128)] = s_b[pl.ds(tile * 128, 128), :].T

    def scale_of(total):
        return 1.0 / (jnp.sqrt(total) + 1e-07)

    def normal(ref, inverse):
        ref[...] = rounded(ref[...].astype(F32) * inverse)

    def exchange(slot, r):
        chunk = pl.ds(r * step, step)
        return remote(gs.at[chunk], gr.at[slot, chunk], gsem.at[r], rsem.at[slot, r], pair)

    def fill_poly():
        for r in range(4):
            poly[pl.ds(r * step, step), :] = poly_rows(g, r * step, step)

    my_rows = pl.ds(pl.multiple_of(f * rows, rows), rows)
    my_high = pl.ds(pl.multiple_of(f * high, high), high)

    @pl.when(p >= 2)
    def _():
        wide = x[...].astype(F32)
        sq[...] = jnp.broadcast_to(jnp.sum(wide * wide), sq.shape)
        copy = remote(sq, sq_r, qs, qr, pair)
        copy.start()
        copy.wait()
        normal(x, scale_of(sq[...] + sq_r[...])[:1, :1])

        def grams(slot):
            for r in range(4):
                gs[pl.ds(r * step, step), :] = rounded(contract(x[pl.ds(r * step, step), :], x[...], 1, 1))
                exchange(slot, r).start()
            for r in range(4):
                chunk = pl.ds(r * step, step)
                exchange(slot, r).wait()
                g[chunk, :] = rounded(gs[chunk, :].astype(F32) + gr[slot, chunk, :].astype(F32))

        def iterate(it, carry):
            grams(lax.rem(it, 2))
            fill_poly()
            for tile in range(half // 256):
                block = pl.ds(tile * 256, 256)
                x[:, block] = rounded(
                    NS_A * x[:, block].astype(F32) + jnp.dot(poly[...], x[:, block], preferred_element_type=F32)
                )
            return carry

        lax.fori_loop(0, NS_ITERS - 1, iterate, 0)
        grams((NS_ITERS - 1) % 2)

        @pl.when(p < WIDE)
        def _():
            mine = poly_rows(g, pl.multiple_of(f * rows, rows), rows)
            pa[...] = rounded(NS_A * x[my_rows, :].astype(F32) + jnp.dot(mine, x[...], preferred_element_type=F32))

        @pl.when(p >= WIDE)
        def _():
            fill_poly()
            for tile in range(half // 128):
                x_t[pl.ds(tile * 128, 128), :] = x[:, pl.ds(tile * 128, 128)].T
            block = x_t[my_high, :]
            pb[...] = rounded(NS_A * block.astype(F32) + jnp.dot(block, poly[...], preferred_element_type=F32))

    @pl.when(p < 2)
    def _():
        kt[...] = x[:, narrow:].T
        inverse_k = scale_of(jnp.sum(jnp.square(kt[...].astype(F32))))
        normal(kt, inverse_k)
        wide = x[:, :narrow].astype(F32)
        x[:, :narrow] = rounded(wide * scale_of(jnp.sum(wide * wide)))

        def narrow_step(it, carry):
            gram = rounded(contract(kt[...], kt[...], 1, 1))
            turn = rounded(NS_B * gram.astype(F32) + NS_C * jnp.dot(gram, gram, preferred_element_type=F32))
            kt[...] = rounded(NS_A * kt[...].astype(F32) + jnp.dot(turn, kt[...], preferred_element_type=F32))
            return carry

        lax.fori_loop(0, NS_ITERS, narrow_step, 0)

        def gram_of():
            for r in range(4):
                chunk = pl.ds(r * step, step)
                g[chunk, :] = rounded(contract(x[chunk, :narrow], x[:, :narrow], 1, 1))

        def square_step(it, carry):
            gram_of()
            fill_poly()
            x[:, :narrow] = rounded(
                NS_A * x[:, :narrow].astype(F32) + jnp.dot(poly[...], x[:, :narrow], preferred_element_type=F32)
            )
            return carry

        lax.fori_loop(0, NS_ITERS - 1, square_step, 0)
        gram_of()
        mine = poly_rows(g, pl.multiple_of(f * rows, rows), rows)
        square = rounded(
            NS_A * x[my_rows, :narrow].astype(F32) + jnp.dot(mine, x[:, :narrow], preferred_element_type=F32)
        )
        x[:, narrow:] = kt[...].T
        pa[:, :narrow] = square
        pa[:, narrow:] = x[my_rows, narrow:]

    spread(at, pa, pb, o_a, o_b, ag_l, ag_s, ag_r)()


def orthogonalize(s_a, s_b, rows, high, narrow):
    parts = lax.axis_size("fsdp")
    depth, half = s_a.shape
    dma = pltpu.SemaphoreType.DMA
    vm = pltpu.VMEM
    return pl.pallas_call(
        functools.partial(ortho_kernel, parts, rows, high, narrow),
        out_shape=(
            jax.ShapeDtypeStruct((WIDE, rows, half), BF16),
            jax.ShapeDtypeStruct((CLASSES - WIDE, high, depth), BF16),
        ),
        in_specs=[VMEM, VMEM],
        out_specs=(ANY, ANY),
        scratch_shapes=[
            vm((depth, half), BF16),
            vm((half, depth), BF16),
            vm((depth, depth), BF16),
            vm((2, depth, depth), BF16),
            vm((depth, depth), BF16),
            vm((depth, depth), BF16),
            vm((8, 128), F32),
            vm((8, 128), F32),
            vm((rows, half), BF16),
            vm((high, depth), BF16),
            vm((half - narrow, depth), BF16),
            dma((4,)), dma((2, 4)), dma, dma, dma, dma((7,)), dma((CLASSES,)),
        ],
        compiler_params=pltpu.CompilerParams(
            collective_id=2, has_side_effects=True, vmem_limit_bytes=62 << 20
        ),
        name="orthogonalize",
    )(s_a, s_b)


class Weights:
    def __init__(self, at, sources, homes, zs, s1, s2, sc, recv):
        self.at, self.sources, self.homes = at, sources, homes
        self.zs, self.s1, self.s2, self.sc, self.recv = zs, s1, s2, sc, recv
        self.sends = []

    def act(self, group, q, j, plane, send, target, what, first=False):
        recv = self.recv.at[group, q, j]
        home, source = self.homes[group], self.sources[group]
        rows = home.shape[-2] // (1 if group == 3 else self.at.parts)
        unit = -(-rows // (16 * CLASSES)) * 16
        last = rows - (CLASSES - 1) * unit

        def piece(count):
            def go():
                start = pl.multiple_of(q * unit, 16)
                if group == 3:
                    columns = home.shape[1] // self.at.parts
                    dst = home.at[pl.ds(start, count), pl.ds(pl.multiple_of(plane * columns, 128), columns)]
                    src = source.at[pl.ds(start, count)]
                elif group == 0:
                    dst = home.at[:, pl.ds(pl.multiple_of(plane * rows + start, 16), count)]
                    src = dst
                else:
                    dst = home.at[pl.ds(pl.multiple_of(plane * rows + start, 16), count)]
                    src = source.at[pl.ds(start, count)]
                getattr(remote(src if first else dst, dst, send, recv, target), what)()

            return go

        pl.when(q < CLASSES - 1)(piece(unit))
        pl.when(q == CLASSES - 1)(piece(last))

    def send(self, group, q, j, plane, sem, target, first=False):
        self.act(group, q, j, plane, sem, target, "start", first)
        self.sends.append((group, q, j, plane, sem, target, "wait_send", first))

    def arrived(self, group, q, j):
        at = self.at
        self.act(group, q, j, at.f ^ j, self.zs.at[group, j], at.peer(1), "wait_recv")

    def along(self, group):
        at = self.at
        for j in range(1, at.parts):
            self.send(group, at.p, j, at.f, self.zs.at[group, j], at.along(j), True)

    def first(self, group):
        at = self.at
        for j in range(1, at.parts):
            self.arrived(group, at.p, j)
            self.send(group, at.p, j, at.f ^ j, self.s1.at[group, j], at.peer(at.b1))
            self.send(group, at.p, j, at.f ^ j, self.s2.at[group, 0, j], at.peer(at.b2))
            self.send(group, at.p, j, at.f ^ j, self.sc.at[group, 0, j], at.peer(1))

    def second(self, group):
        at = self.at
        q = at.p ^ at.b1
        for j in range(1, at.parts):
            self.arrived(group, q, j)
            self.send(group, q, j, at.f ^ j, self.s2.at[group, 1, j], at.peer(at.b2))
            self.send(group, q, j, at.f ^ j, self.sc.at[group, 1, j], at.peer(1))

    def third(self, group):
        at = self.at
        for slot, bits in ((2, at.b2), (3, at.b1 ^ at.b2)):
            for j in range(1, at.parts):
                self.arrived(group, at.p ^ bits, j)
                self.send(group, at.p ^ bits, j, at.f ^ j, self.sc.at[group, slot, j], at.peer(1))

    def ready(self, group):
        at = self.at
        for bits in (1, 3, 5, 7):
            for j in range(1, at.parts):
                self.arrived(group, at.p ^ bits, j)

    def finish(self):
        for item in self.sends:
            self.act(*item)


def spread_even(at, own, out, local, ss, recv):
    p = at.p

    def copy_of(cls, slot, target, first=False):
        return remote(own if first else out.at[cls], out.at[cls], ss.at[slot], recv.at[cls], target)

    keep = pltpu.make_async_copy(own, out.at[p], local)
    sends = []

    def send(cls, slot, target, first=False):
        copy = copy_of(cls, slot, target, first)
        copy.start()
        sends.append(copy)

    def arrived(cls):
        copy_of(cls, 0, at.peer(1)).wait_recv()

    send(p, 0, at.peer(at.b1), True)
    send(p, 1, at.peer(at.b2), True)
    send(p, 2, at.peer(1), True)
    keep.start()

    def pass_on():
        arrived(p ^ at.b1)
        send(p ^ at.b1, 3, at.peer(at.b2))
        send(p ^ at.b1, 4, at.peer(1))
        arrived(p ^ at.b2)
        send(p ^ at.b2, 5, at.peer(1))
        arrived(p ^ at.b1 ^ at.b2)
        send(p ^ at.b1 ^ at.b2, 6, at.peer(1))

    def finish():
        for bits in (1, 3, 5, 7):
            arrived(p ^ bits)
        for copy in sends:
            copy.wait_send()
        keep.wait()

    return pass_on, finish


def step_kernel(
    x_ref, up_ref, gains_ref, cos_ref, low_ref, high_ref, bias_ref, wq, wk, wo, wv, wg_in, wu_in, wd_in,
    m_q, m_k, m_o, m_v, m_gate, m_up, m_down,
    out_ref, grad_ref, g_out, o_out, gain_out,
    w01, wg, wu, wd, probs, kv, rot, dkv, c4r, c2r, c1r, att, gate, lifted,
    xt, dy_in, dy, own, za_r, ma, mq, mk, sall, gain_s, gain_r, sq, sq_r,
    local, zs, s1, s2, sc, recv, kvs, kvr, ds, dr,
    ls, xs, xr, os1, or1, os2, or2, ozs, ozr, msem, gs, gr, ag_l, ag_s, ag_r, ls_l, ls_r, lr_l, lr_r,
    gsem, rsem, qs, qr, ex_s, ex_r, fx_s, fx_r, og_l, og_s, og_r, free,
):
    at = Place()
    p, f, core, parts = at.p, at.f, at.core, at.parts
    width, tokens = x_ref.shape
    half = w01.shape[2]
    keys = half - width
    group = HEADS // KV_HEADS
    scale = 1.0 / math.sqrt(HEAD)
    rows = width // parts
    columns = 2 * half // parts
    tall = width // 2
    pair = at.peer(1)
    my_rows = pl.ds(pl.multiple_of(f * rows, 16), rows)

    weights = Weights(at, (None, wg_in, wu_in, wd_in), (w01, wg, wu, wd), zs, s1, s2, sc, recv)
    keep = [
        pltpu.make_async_copy(wg_in, wg.at[my_rows], local.at[0]),
        pltpu.make_async_copy(wu_in, wu.at[my_rows], local.at[1]),
        pltpu.make_async_copy(
            wd_in, wd.at[:, pl.ds(pl.multiple_of(f * columns, 128), columns)], local.at[2]
        ),
    ]

    def moment(what):
        for cls in range(CLASSES):
            @pl.when(p == cls)
            def _(cls=cls):
                side = cls % 2
                if cls < 2:
                    pairs = [((m_q, m_o)[cls], mq, 0), ((m_k, m_v)[cls], mk, 1)]
                elif cls < WIDE:
                    whole = m_gate if cls < 4 else m_up
                    pairs = [(whole.at[:, pl.ds(side * half, half)], ma, 0)]
                else:
                    pairs = [
                        (
                            m_down.at[pl.ds(side * tall + t * rows, rows)],
                            ma.at[:, pl.ds(t * columns, columns)],
                            t,
                        )
                        for t in range(2)
                    ]
                for src, dst, index in pairs:
                    getattr(pltpu.make_async_copy(src, dst, msem.at[index]), what)()

    w01[0, my_rows, :width] = wq[...]
    w01[0, my_rows, width:] = wk[...].T
    w01[1, my_rows, :width] = wo[...]
    w01[1, my_rows, width:] = wv[...].T
    at.barrier()
    for index in range(4):
        weights.along(index)
    for copy in keep:
        copy.start()
    moment("start")

    residual = x_ref[...].astype(F32).T
    upstream = up_ref[...].astype(F32).T
    inverse_first = lax.rsqrt(jnp.mean(residual * residual, axis=-1, keepdims=True) + EPS)
    normed_first = (residual * inverse_first * gains_ref[0:1, :]).astype(BF16)
    xt[0, :, pl.ds(0, tokens)] = normed_first.T
    xt[3, :, pl.ds(0, tokens)] = up_ref[...]

    weights.first(0)
    weights.second(0)
    weights.first(1)
    weights.third(0)
    weights.ready(0)

    def turn(value, sign):
        tiles = []
        for tile in range(half // 128):
            part = value[:, tile * 128 : (tile + 1) * 128]
            swapped = pltpu.roll(part, HEAD // 2, 1) * low_ref[...] + pltpu.roll(part, 128 - HEAD // 2, 1) * high_ref[...]
            tiles.append(part * cos_ref[...] + swapped if sign > 0 else part * cos_ref[...] - swapped)
        return tiles

    qk = jnp.dot(normed_first, w01[0], preferred_element_type=F32)
    for tile, value in enumerate(turn(qk, 1)):
        rot[:, tile * 128 : (tile + 1) * 128] = value.astype(BF16)
    values = jnp.dot(normed_first, w01[1, :, width:], preferred_element_type=F32).astype(BF16)
    kv[p, :, :keys] = rot[:, width:]
    kv[p, :, keys:] = values

    def block(q, slot, target):
        return remote(kv.at[q], kv.at[q], kvs.at[slot], kvr.at[q], target)

    sent = [block(p, 0, at.peer(at.b1)), block(p, 1, at.peer(at.b2)), block(p, 2, at.peer(1))]
    for copy in sent:
        copy.start()

    def pass_keys(q, slots):
        block(q, 0, at.peer(1)).wait_recv()
        for slot, target in slots:
            copy = block(q, slot, target)
            copy.start()
            sent.append(copy)

    weights.second(1)
    pass_keys(p ^ at.b1, [(3, at.peer(at.b2)), (4, at.peer(1))])
    pass_keys(p ^ at.b2, [(5, at.peer(1))])
    weights.first(2)
    pass_keys(p ^ at.b1 ^ at.b2, [(6, at.peer(1))])
    for bits in (1, 3, 5, 7):
        pass_keys(p ^ bits, [])
    weights.third(1)

    def keys_of(g):
        return kv[:, :, g * HEAD : (g + 1) * HEAD].reshape(CLASSES * tokens, HEAD)

    def values_of(g):
        return kv[:, :, keys + g * HEAD : keys + (g + 1) * HEAD].reshape(CLASSES * tokens, HEAD)

    def heads_of(ref, g):
        return jnp.concatenate([ref[:, h * HEAD : (h + 1) * HEAD] for h in range(g * group, (g + 1) * group)], axis=0)

    def attend(g):
        scores = contract(keys_of(g), heads_of(rot, g), 1, 1) * scale
        bias = bias_ref[...]
        scores = scores + jnp.concatenate([bias] * group, axis=1)
        top = jnp.max(scores, axis=0, keepdims=True)
        expo = jnp.exp(scores - top)
        total = jnp.sum(expo, axis=0, keepdims=True)
        chance = expo * (1.0 / total)
        probs[g] = chance
        mixed = contract(values_of(g), chance.astype(BF16), 0, 0)
        turned = mixed.T.astype(BF16)
        for h in range(group):
            at_lane = (g * group + h) * HEAD
            att[:, at_lane : at_lane + HEAD] = turned[h * tokens : (h + 1) * tokens]

    attend(0)
    attend(1)
    weights.second(2)
    attend(2)
    weights.first(3)
    attend(3)
    weights.third(2)
    attend(4)
    for copy in keep:
        copy.wait()
    weights.ready(1)

    xt[1, :, pl.ds(0, tokens)] = att[...].T
    middle = residual + jnp.dot(att[...], w01[1, :, :width], preferred_element_type=F32)
    inverse_second = lax.rsqrt(jnp.mean(middle * middle, axis=-1, keepdims=True) + EPS)
    normed_second = (middle * inverse_second * gains_ref[1:2, :]).astype(BF16)
    xt[2, :, pl.ds(0, tokens)] = normed_second.T
    weights.second(3)
    gate[...] = jnp.dot(normed_second, wg[...], preferred_element_type=F32)
    weights.third(3)
    weights.ready(2)
    lifted[...] = jnp.dot(normed_second, wu[...], preferred_element_type=F32)
    hidden = (gate[...] * jax.nn.sigmoid(gate[...]) * lifted[...]).astype(BF16)
    dy_in[6] = hidden[:, :half]
    dy_in[7] = hidden[:, half:]
    weights.ready(3)

    grad_hidden = jnp.dot(upstream.astype(BF16), wd[...], preferred_element_type=F32)
    sigma = jax.nn.sigmoid(gate[...])
    grad_gate = (grad_hidden * lifted[...] * sigma * (1.0 + gate[...] * (1.0 - sigma))).astype(BF16)
    grad_lifted = (grad_hidden * gate[...] * sigma).astype(BF16)
    for side in range(2):
        lanes = slice(side * half, (side + 1) * half)
        dy_in[2 + side] = grad_gate[:, lanes]
        dy_in[4 + side] = grad_lifted[:, lanes]

    slabs = [core, 2 + core, 4 + core, 6, 7, 8]
    theirs_slabs = [1 - core, 3 - core, 5 - core, 6, 7, 8]

    def kinds_moves():
        return [
            remote(
                xt.at[:, :, pl.ds(0, tokens)], xt.at[:, :, pl.ds(tokens, tokens)], xs.at[6], xr.at[6], pair
            )
        ]

    def slab_moves(slot):
        return [
            pltpu.make_async_copy(dy_in.at[slabs[slot]], dy.at[slot, pl.ds(0, tokens)], ls.at[slot]),
            remote(dy_in.at[theirs_slabs[slot]], dy.at[slot, pl.ds(tokens, tokens)], xs.at[slot], xr.at[slot], pair),
        ]

    early_moves = kinds_moves()
    for slot in (1, 2, 3, 4):
        early_moves += slab_moves(slot)
    for copy in early_moves:
        copy.start()

    out_ref[...] = (middle + contract(hidden, wd[...], 1, 1)).T.astype(BF16)
    weights.finish()
    pl.semaphore_signal(free.at[1], inc=1, device_id=at.peer(at.b2), device_id_type=MESH)
    grad_normed = contract(grad_gate, wg[...], 1, 1) + contract(grad_lifted, wu[...], 1, 1)
    pl.semaphore_signal(free.at[0], inc=1, device_id=at.peer(at.b1), device_id_type=MESH)

    def norm_back(value, inverse, gain, incoming):
        scaled = incoming * gain
        mean = jnp.mean(scaled * value, axis=-1, keepdims=True)
        through = inverse * scaled - value * (inverse * inverse * inverse) * mean
        return through, jnp.sum(incoming * value * inverse, axis=0, keepdims=True)

    through, gain_second = norm_back(middle, inverse_second, gains_ref[1:2, :], grad_normed)
    gain_s[0] = jnp.zeros(gain_s.shape[1:], F32)
    gain_s[0, 1:2, :] = gain_second
    grad_middle = upstream + through
    grad_branch = grad_middle.astype(BF16)
    dy_in[1, :, :width] = grad_branch
    dy_in[1, :, width:] = jnp.zeros((tokens, keys), BF16)
    att[...] = contract(grad_branch, w01[1, :, :width], 1, 1).astype(BF16)

    for copy in early_moves:
        copy.wait()

    def produce(cls, r, put):
        at_rows = pl.ds(pl.multiple_of(r * rows, 16), rows)
        slot = lax.div(cls, 2)
        every = slice(0, half)

        @pl.when(cls == 1)
        def _():
            put(
                every,
                jnp.dot(xt[1, at_rows, :], dy[0], preferred_element_type=F32)
                + jnp.dot(xt[0, at_rows, :], dy[5], preferred_element_type=F32),
            )

        @pl.when((cls != 1) & (cls < WIDE))
        def _():
            kind = jnp.where(cls == 0, 0, 2)
            put(every, jnp.dot(xt[kind, at_rows, :], dy[slot], preferred_element_type=F32))

        @pl.when(cls >= WIDE)
        def _():
            side, start = lax.div(r * columns, half), lax.rem(r * columns, half)
            part = dy[3 + side, :, pl.ds(pl.multiple_of(start, 128), columns)]
            for t in range(2):
                top = pl.multiple_of((cls - WIDE) * tall + t * rows, 16)
                put(
                    slice(t * columns, (t + 1) * columns),
                    jnp.dot(xt[3, pl.ds(top, rows), :], part, preferred_element_type=F32),
                )

    def order(i):
        return lax.rem(f + 1 + i, parts)

    def chunk(ref, r, side):
        return ref.at[pl.ds(pl.multiple_of(r * rows, 16), rows), pl.ds(side * half, half)]

    def early(cls):
        return cls >= 2

    def late(cls):
        return cls < 2

    bits_of = (at.b1 ^ at.b2, at.b1)

    def one(slot, i):
        r = order(i)
        return remote(chunk(wg, r, slot), chunk(wu, r, slot), os1.at[slot, r], or1.at[slot, r], at.peer(at.b1))

    def first(slot, i, when):
        r = order(i)
        cls = p ^ bits_of[slot]

        @pl.when(when(cls))
        def _():
            room = chunk(wg, r, slot)

            def put(lanes, value):
                room[:, lanes] = value.astype(BF16)

            produce(cls, r, put)
            one(slot, i).start()

    def two(i):
        r = order(i)
        return remote(chunk(wu, r, 0), chunk(wd, r, 1), os2.at[r], or2.at[r], at.peer(at.b2))

    def second(i, when):
        r = order(i)
        cls = p ^ at.b2

        @pl.when(when(cls))
        def _():
            one(0, i).wait_recv()
            room = chunk(wu, r, 0)

            def put(lanes, value):
                room[:, lanes] = (value + room[:, lanes].astype(F32)).astype(BF16)

            produce(cls, r, put)
            two(i).start()

    def line(r, source):
        return remote(chunk(wd, r, 0), za_r.at[(r ^ source) - 1], ozs.at[r], ozr.at[source], (at.c, r))

    def arrival(j):
        return remote(chunk(wd, f, 0), za_r.at[j - 1], ozs.at[f], ozr.at[f ^ j], at.along(j))

    def third(i, when):
        r = order(i)

        @pl.when(when(p))
        def _():
            one(1, i).wait_recv()
            two(i).wait_recv()
            from_one, from_two, room = chunk(wu, r, 1), chunk(wd, r, 1), chunk(wd, r, 0)

            def put(lanes, value):
                total = value + from_one[:, lanes].astype(F32) + from_two[:, lanes].astype(F32)
                if i == parts - 1:
                    own[:, lanes] = total
                else:
                    room[:, lanes] = total.astype(BF16)

            produce(p, r, put)
            if i < parts - 1:
                line(r, f).start()

    def swap(slot, target):
        return remote(gain_s.at[slot], gain_r.at[slot], gs.at[slot], gr.at[slot], target)

    pl.semaphore_wait(free.at[0], 1)
    first(0, 0, early)
    first(1, 0, early)

    def attend_back(g):
        chance = probs[g]
        out_grad = heads_of(att, g)
        query = heads_of(rot, g)
        grad_probs = contract(values_of(g), out_grad, 1, 1)
        delta = jnp.sum(grad_probs * chance, axis=0, keepdims=True)
        grad_scores = (chance * (grad_probs - delta)).astype(BF16)
        grad_values = jnp.dot(chance.astype(BF16), out_grad, preferred_element_type=F32)
        grad_keys = jnp.dot(grad_scores, query, preferred_element_type=F32) * scale
        dkv[:, :, g * HEAD : (g + 1) * HEAD] = grad_keys.reshape(CLASSES, tokens, HEAD)
        dkv[:, :, keys + g * HEAD : keys + (g + 1) * HEAD] = grad_values.reshape(CLASSES, tokens, HEAD)
        turned = contract(keys_of(g), grad_scores, 0, 0).T * scale
        for h in range(group):
            at_lane = (g * group + h) * HEAD
            gate[:, at_lane : at_lane + HEAD] = turned[h * tokens : (h + 1) * tokens]

    attend_back(0)
    attend_back(1)
    attend_back(2)
    first(0, 1, early)
    attend_back(3)
    attend_back(4)

    def halve(bit, rest, sbuf, rbuf, index, between=None):
        for i, bits in enumerate(rest):
            sbuf[i // 2, :, pl.ds(i % 2 * 2 * keys, 2 * keys)] = dkv[p ^ bit ^ bits].astype(BF16)
        copy = remote(sbuf, rbuf, ds.at[index], dr.at[index], at.peer(bit))
        copy.start()
        if between is not None:
            between()
        copy.wait()
        for i, bits in enumerate(rest):
            dkv[p ^ bits] = dkv[p ^ bits] + rbuf[i // 2, :, pl.ds(i % 2 * 2 * keys, 2 * keys)].astype(F32)

    def more():
        first(1, 1, early)
        first(0, 2, early)

    halve(1, (0, 2, 4, 6), dy_in.at[pl.ds(2, 2)], c4r, 0)
    halve(at.b1, (0, at.b2), dy_in.at[pl.ds(4, 1)], c2r, 1, more)
    halve(at.b2, (0,), dy_in.at[pl.ds(5, 1), :, pl.ds(0, 2 * keys)], c1r, 2)

    gate[:, width:half] = dkv[p, :, :keys]
    for tile, value in enumerate(turn(gate[:, :half], -1)):
        dy_in[0, :, tile * 128 : (tile + 1) * 128] = value.astype(BF16)
    dy_in[8, :, :width] = jnp.zeros((tokens, width), BF16)
    dy_in[8, :, width:] = dkv[p, :, keys:].astype(BF16)
    late_moves = slab_moves(0) + slab_moves(5)
    for copy in late_moves:
        copy.start()
    pl.semaphore_wait(free.at[1], 1)
    second(0, early)
    grad_normed = contract(dy_in[0], w01[0], 1, 1) + contract(dy_in[8], w01[1], 1, 1)
    for copy in late_moves:
        copy.wait()
    for i in range(parts):
        first(0, i, late)
        first(1, i, late)
    first(1, 2, early)
    first(0, 3, early)
    first(1, 3, early)
    second(1, early)
    through, gain_first = norm_back(residual, inverse_first, gains_ref[0:1, :], grad_normed)
    gain_s[0, 0:1, :] = gain_first
    swaps = [swap(0, pair)]
    swaps[0].start()
    grad_ref[...] = (grad_middle + through).T
    third(0, early)

    second(0, late)
    second(2, early)
    third(1, early)
    swaps[0].wait()
    gain_s[1] = gain_s[0] + gain_r[0]
    swaps.append(swap(1, at.peer(2)))
    swaps[1].start()
    second(1, late)
    third(0, late)
    second(3, early)
    third(2, early)
    second(2, late)
    third(1, late)
    swaps[1].wait()
    gain_s[2] = gain_s[1] + gain_r[1]
    swaps.append(swap(2, at.peer(4)))
    swaps[2].start()
    second(3, late)
    third(3, early)
    third(2, late)
    third(3, late)

    moment("wait")

    @pl.when(p < 2)
    def _():
        ma[:, :width] = mq[...]
        ma[:, width:] = mk[...].T

    ga, pa = (w01.at[1, pl.ds((parts - 1 - i) * rows, rows)] for i in range(2))
    total = own[...]
    for j in range(1, parts):
        arrival(j).wait_recv()
        total = total + za_r[j - 1].astype(F32)
    ga[...] = total.astype(BF16)
    sall[my_rows, :] = (MOMENTUM * ma[...] + total).astype(BF16)

    def shard(index):
        return sall.at[pl.ds(pl.multiple_of(index * rows, 16), rows)]

    def rightward(index):
        return remote(shard(index), shard(index), ls_r.at[index], lr_r.at[index], (at.c, lax.rem(f + 1, parts)))

    def leftward(index):
        return remote(shard(index), shard(index), ls_l.at[index], lr_l.at[index], (at.c, lax.rem(f + parts - 1, parts)))

    def can_right():
        return f < parts - 1

    def can_left():
        return f > 0

    pl.when(can_right())(lambda: rightward(f).start())
    pl.when(can_left())(lambda: leftward(f).start())

    pass_on, finish = spread_even(at, ga, g_out, ag_l, ag_s, ag_r)
    swaps[2].wait()
    gain_s[3] = gain_s[2] + gain_r[2]
    line_gain = [
        remote(gain_s.at[3], gain_r.at[3 + j], gs.at[3 + j], gr.at[3 + j], at.along(j)) for j in range(1, parts)
    ]
    for copy in line_gain:
        copy.start()

    for hop in range(1, parts):
        @pl.when(f - hop >= 0)
        def _(hop=hop):
            rightward(f - hop).wait_recv()
            pl.when(can_right())(lambda: rightward(f - hop).start())

        @pl.when(f + hop < parts)
        def _(hop=hop):
            leftward(f + hop).wait_recv()
            pl.when(can_left())(lambda: leftward(f + hop).start())

    pass_on()

    for i in range(parts):
        one(0, i).wait_send()
        one(1, i).wait_send()
        two(i).wait_send()
    for j in range(1, parts):
        line(f ^ j, f).wait_send()
    pl.semaphore_signal(free.at[2], inc=1, device_id=pair, device_id_type=MESH)
    pl.semaphore_wait(free.at[2], 1)

    x = w01.at[0]
    wide_gram = 1024
    gram_s, g = wg.at[:, pl.ds(0, wide_gram)], wg.at[:, pl.ds(wide_gram, wide_gram)]
    poly, xf = wd.at[:, pl.ds(0, wide_gram)], wd.at[:, pl.ds(half, columns)]
    step = width // 4

    def gram_r(slot):
        return wu.at[:, pl.ds(slot * wide_gram, wide_gram)]

    def scale_of(total):
        return 1.0 / (jnp.sqrt(total) + 1e-07)

    def normal(ref, inverse):
        ref[...] = rounded(ref[...].astype(F32) * inverse)

    def exchange(slot, r):
        part = pl.ds(r * step, step)
        return remote(gram_s.at[part], gram_r(slot).at[part], gsem.at[r], rsem.at[slot, r], pair)

    def poly_of(start, count):
        part = g[pl.ds(start, count), pl.ds(0, width)]
        square = jnp.dot(part, g[:, pl.ds(0, width)], preferred_element_type=F32)
        return rounded(NS_B * part.astype(F32) + NS_C * square)

    def fill_poly():
        for r in range(4):
            poly[pl.ds(r * step, step), pl.ds(0, width)] = poly_of(r * step, step)

    near = parts // 2
    mine_at = core * near
    last_core = lax.div(f, near)
    f_lanes = pl.ds(pl.multiple_of(lax.rem(f, near) * columns, 128), columns)

    kt = wd.at[pl.ds(0, keys), pl.ds(half + 256, wide_gram)]

    def xo(i):
        return w01.at[1, pl.ds(i * rows, rows)]

    def give():
        return [
            remote(
                sall.at[pl.ds(pl.multiple_of(((1 - core) * near + i) * rows, 16), rows)],
                xo(i), ex_s.at[i], ex_r.at[i], pair,
            )
            for i in range(near)
        ]

    def give_last():
        return remote(x.at[:, f_lanes], xf, fx_s, fx_r, pair)

    @pl.when(p >= 2)
    def _():
        @pl.when(p < WIDE)
        def _():
            x[...] = sall[...]

        @pl.when(p >= WIDE)
        def _():
            copies = give()
            for copy in copies:
                copy.start()
            for i in range(near):
                part = sall[pl.ds(pl.multiple_of((mine_at + i) * rows, 16), rows), :]
                for t in range(2):
                    x[pl.ds(pl.multiple_of(core * tall + t * rows, 16), rows), pl.ds(i * columns, columns)] = part[
                        :, t * columns : (t + 1) * columns
                    ]
            for i, copy in enumerate(copies):
                copy.wait()
                part = xo(i)
                for t in range(2):
                    x[pl.ds(pl.multiple_of((1 - core) * tall + t * rows, 16), rows), pl.ds(i * columns, columns)] = part[
                        :, pl.ds(t * columns, columns)
                    ]

        wide = x[...].astype(F32)
        sq[...] = jnp.broadcast_to(jnp.sum(wide * wide), sq.shape)
        copy = remote(sq, sq_r, qs, qr, pair)
        copy.start()
        copy.wait()
        normal(x, scale_of(sq[...] + sq_r[...])[:1, :1])

        def grams(slot):
            for r in range(4):
                gram_s[pl.ds(r * step, step), pl.ds(0, width)] = rounded(
                    contract(x[pl.ds(r * step, step), :], x[...], 1, 1)
                )
                exchange(slot, r).start()
            for r in range(4):
                part = pl.ds(r * step, step)
                exchange(slot, r).wait()
                g[part, pl.ds(0, width)] = rounded(
                    gram_s[part, pl.ds(0, width)].astype(F32) + gram_r(slot)[part, pl.ds(0, width)].astype(F32)
                )

        def iterate(slot):
            grams(slot)
            fill_poly()
            for tile in range(half // 256):
                part = pl.ds(tile * 256, 256)
                x[:, part] = rounded(
                    NS_A * x[:, part].astype(F32) + jnp.dot(poly[:, pl.ds(0, width)], x[:, part], preferred_element_type=F32)
                )

        def iterate_twice(it, carry):
            iterate(0)
            iterate(1)
            return carry

        lax.fori_loop(0, (NS_ITERS - 1) // 2, iterate_twice, 0)

        @pl.when((p >= WIDE) & (core == last_core))
        def _():
            give_last().start()
            xf[...] = x[:, f_lanes]

        grams(0)

        @pl.when(p < WIDE)
        def _():
            part = poly_of(pl.multiple_of(f * rows, 16), rows)
            pa[...] = rounded(NS_A * x[my_rows, :].astype(F32) + jnp.dot(part, x[...], preferred_element_type=F32))

        @pl.when(p >= WIDE)
        def _():
            pl.when(core == last_core)(lambda: give_last().wait_send())
            pl.when(core != last_core)(lambda: give_last().wait_recv())
            for t in range(2):
                top = pl.multiple_of(core * tall + t * rows, 16)
                part = poly_of(top, rows)
                pa[:, t * columns : (t + 1) * columns] = rounded(
                    NS_A * xf[pl.ds(top, rows), :].astype(F32) + jnp.dot(part, xf[...], preferred_element_type=F32)
                )

    @pl.when(p < 2)
    def _():
        x[...] = sall[...]
        kt[:, pl.ds(0, width)] = x[:, pl.ds(width, keys)].T
        turned = kt[:, pl.ds(0, width)].astype(F32)
        kt[:, pl.ds(0, width)] = rounded(turned * scale_of(jnp.sum(turned * turned)))
        wide = x[:, pl.ds(0, width)].astype(F32)
        x[:, pl.ds(0, width)] = rounded(wide * scale_of(jnp.sum(wide * wide)))

        def narrow_step(it, carry):
            now = kt[:, pl.ds(0, width)]
            gram = rounded(contract(now, now, 1, 1))
            turned = rounded(NS_B * gram.astype(F32) + NS_C * jnp.dot(gram, gram, preferred_element_type=F32))
            kt[:, pl.ds(0, width)] = rounded(
                NS_A * now.astype(F32) + jnp.dot(turned, now, preferred_element_type=F32)
            )
            return carry

        lax.fori_loop(0, NS_ITERS, narrow_step, 0)

        def gram_of():
            for r in range(4):
                part = pl.ds(r * step, step)
                g[part, pl.ds(0, width)] = rounded(contract(x[part, pl.ds(0, width)], x[:, pl.ds(0, width)], 1, 1))

        def square_step(it, carry):
            gram_of()
            fill_poly()
            x[:, pl.ds(0, width)] = rounded(
                NS_A * x[:, pl.ds(0, width)].astype(F32) + jnp.dot(poly[:, pl.ds(0, width)], x[:, pl.ds(0, width)], preferred_element_type=F32)
            )
            return carry

        lax.fori_loop(0, NS_ITERS - 1, square_step, 0)
        gram_of()
        part = poly_of(pl.multiple_of(f * rows, 16), rows)
        square = rounded(
            NS_A * x[my_rows, pl.ds(0, width)].astype(F32) + jnp.dot(part, x[:, pl.ds(0, width)], preferred_element_type=F32)
        )
        x[:, pl.ds(width, keys)] = kt[:, pl.ds(0, width)].T
        pa[:, :width] = square
        pa[:, width:] = x[my_rows, pl.ds(width, keys)]

    out_on, out_finish = spread_even(at, pa, o_out, og_l, og_s, og_r)
    total = gain_s[3]
    for j in range(1, parts):
        line_gain[j - 1].wait()
        total = total + gain_r[3 + j]
    gain_out[...] = total
    finish()
    out_on()
    pl.when(can_right())(lambda: rightward(f).wait_send())
    pl.when(can_left())(lambda: leftward(f).wait_send())
    for hop in range(1, parts):
        pl.when((f - hop >= 0) & can_right())(lambda hop=hop: rightward(f - hop).wait_send())
        pl.when((f + hop < parts) & can_left())(lambda hop=hop: leftward(f + hop).wait_send())
    for copy in sent:
        copy.wait_send()
    out_finish()


def step_pass(x, up, gains, tables, bias, shards, moments):
    parts = lax.axis_size("fsdp")
    width, tokens = x.shape
    half = shards[4].shape[1] // 2
    rows = width // parts
    keys = half - width
    near = parts // 2
    dma = pltpu.SemaphoreType.DMA
    vm = pltpu.VMEM
    group = HEADS // KV_HEADS
    two = 2 * keys
    n_gain = 3 + parts
    return pl.pallas_call(
        step_kernel,
        out_shape=(
            jax.ShapeDtypeStruct((width, tokens), BF16),
            jax.ShapeDtypeStruct((width, tokens), F32),
            jax.ShapeDtypeStruct((CLASSES, rows, half), BF16),
            jax.ShapeDtypeStruct((CLASSES, rows, half), BF16),
            jax.ShapeDtypeStruct((8, width), F32),
        ),
        in_specs=[VMEM] * 11 + [ANY] * 10,
        out_specs=(VMEM, VMEM, ANY, ANY, VMEM),
        scratch_shapes=[
            vm((2, width, half), BF16),
            vm((width, 2 * half), BF16),
            vm((width, 2 * half), BF16),
            vm((width, 2 * half), BF16),
            vm((KV_HEADS, CLASSES * tokens, group * tokens), F32),
            vm((CLASSES, tokens, two), BF16),
            vm((tokens, half), BF16),
            vm((CLASSES, tokens, two), F32),
            vm((2, tokens, 2 * two), BF16),
            vm((1, tokens, 2 * two), BF16),
            vm((1, tokens, two), BF16),
            vm((tokens, width), BF16),
            vm((tokens, 2 * half), F32),
            vm((tokens, 2 * half), F32),
            vm((4, width, 2 * tokens), BF16),
            vm((9, tokens, half), BF16),
            vm((6, 2 * tokens, half), BF16),
            vm((rows, half), F32),
            vm((parts - 1, rows, half), BF16),
            vm((rows, half), F32),
            vm((rows, width), F32),
            vm((keys, rows), F32),
            vm((width, half), BF16),
            vm((4, 8, width), F32),
            vm((n_gain, 8, width), F32),
            vm((8, 128), F32),
            vm((8, 128), F32),
            dma((3,)), dma((4, parts)), dma((4, parts)), dma((4, 2, parts)), dma((4, 4, parts)),
            dma((4, CLASSES, parts)), dma((7,)), dma((CLASSES,)), dma((3,)), dma((3,)),
            dma((7,)), dma((7,)), dma((7,)),
            dma((2, parts)), dma((2, parts)), dma((parts,)), dma((parts,)), dma((parts,)), dma((parts,)),
            dma((2,)), dma((n_gain,)), dma((n_gain,)),
            dma, dma((7,)), dma((CLASSES,)),
            dma((parts,)), dma((parts,)), dma((parts,)), dma((parts,)),
            dma((4,)), dma((2, 4)), dma, dma,
            dma((near,)), dma((near,)), dma, dma,
            dma, dma((7,)), dma((CLASSES,)), pltpu.SemaphoreType.REGULAR((3,)),
        ],
        compiler_params=pltpu.CompilerParams(
            collective_id=3, has_side_effects=True, vmem_limit_bytes=63 << 20
        ),
        name="step_pass",
    )(x, up, gains, *tables, bias, *shards, *moments)


def settle_wide(factors, *refs):
    gs, os = refs[0], refs[1]
    ms, ws, outs = refs[2:6], refs[6:10], refs[10:]
    width = ms[0].shape[1]
    half = gs.shape[2]

    def one(index, g, o, lanes):
        grad, moment, weight = (outs[3 * index + i] for i in range(3))
        value = g.astype(F32)
        grad[:, lanes] = value
        moment[:, lanes] = MOMENTUM * ms[index][:, lanes] + value
        weight[:, lanes] = ws[index][:, lanes].astype(F32) + factors[index] * o.astype(F32)

    for index in range(2):
        one(index, gs[index, :, :width], os[index, :, :width], slice(0, width))
    for index in range(2):
        for side in range(2):
            cls = 2 + 2 * index + side
            one(2 + index, gs[cls], os[cls], slice(side * half, (side + 1) * half))


def settle_turned(factors, g_tall, o_tall, g_pair, o_pair, *refs):
    ms, ws, outs = refs[0:3], refs[3:6], refs[6:]
    keys = ms[1].shape[0]

    def one(index, g, o):
        grad, moment, weight = (outs[3 * index + i] for i in range(3))
        grad[...] = g
        moment[...] = MOMENTUM * ms[index][...] + g
        weight[...] = ws[index][...].astype(F32) + factors[index] * o

    one(0, g_tall[0].astype(F32), o_tall[0].astype(F32))

    @pl.when(pl.program_id(0) == 0)
    def _():
        for index in range(2):
            start = g_pair.shape[2] - keys
            one(1 + index, g_pair[index, :, start:].astype(F32).T, o_pair[index, :, start:].astype(F32).T)


def settle(g, o, moments, shards, factors):
    m_q, m_k, m_o, m_v, m_gate, m_up, m_down = moments
    w_q, w_k, w_o, w_v, w_gate, w_up, w_down = shards
    f_q, f_k, f_v, f_o, f_gate, f_up, f_down = factors
    _, rows, half = g.shape
    width, columns = m_down.shape
    block = 48 if rows % 48 == 0 else rows
    piece = pl.BlockSpec((WIDE, block, half), lambda i: (0, i, 0))

    def row_block(array):
        return pl.BlockSpec((block, array.shape[1]), lambda i: (i, 0))

    def result(arrays):
        return tuple(jax.ShapeDtypeStruct(array.shape, F32) for array in arrays for _ in range(3))

    wide = (m_q, m_o, m_gate, m_up)
    first = pl.pallas_call(
        functools.partial(settle_wide, (f_q, f_o, f_gate, f_up)),
        grid=(rows // block,),
        out_shape=result(wide),
        in_specs=[piece, piece] + [row_block(array) for array in wide] * 2,
        out_specs=tuple(row_block(array) for array in wide for _ in range(3)),
        compiler_params=pltpu.CompilerParams(vmem_limit_bytes=48 << 20),
        name="settle_wide",
    )(g, o, *wide, w_q, w_o, w_gate, w_up)

    turned = (m_down, m_k, m_v)
    halves = half // columns
    tile = pl.BlockSpec((1, rows, columns), lambda i: (WIDE + i // halves, 0, i % halves))
    both = pl.BlockSpec((2, rows, half), lambda i: (0, 0, 0))
    specs = [pl.BlockSpec((rows, columns), lambda i: (i, 0))] + [
        pl.BlockSpec(array.shape, lambda i: (0, 0)) for array in turned[1:]
    ]
    second = pl.pallas_call(
        functools.partial(settle_turned, (f_down, f_k, f_v)),
        grid=(width // rows,),
        out_shape=result(turned),
        in_specs=[tile, tile, both, both] + specs * 2,
        out_specs=tuple(spec for spec in specs for _ in range(3)),
        compiler_params=pltpu.CompilerParams(vmem_limit_bytes=48 << 20),
        name="settle_turned",
    )(g, o, g, o, *turned, w_down, w_k, w_v)
    q, out, gate, up = (first[3 * i : 3 * i + 3] for i in range(4))
    down, k, v = (tuple(item.T for item in second[3 * i : 3 * i + 3]) for i in range(3))
    return list(zip(q, k, v, out, gate, up, down))


def rotary_tables(positions, width):
    half = width // 2
    frequency = THETA ** (-(jnp.arange(half, dtype=jnp.float32) * 2.0 / width))
    angle = positions.astype(jnp.float32)[:, None] * frequency[None, :]
    return (jnp.cos(angle)[:, None, :], jnp.sin(angle)[:, None, :])


def rotate(value, cosine, sine):
    half = value.shape[-1] // 2
    first = value[..., :half]
    second = value[..., half:]
    return jnp.concatenate(
        [first * cosine - second * sine, second * cosine + first * sine], axis=-1
    )


def unrotate(incoming, cosine, sine):
    half = incoming.shape[-1] // 2
    upper = incoming[..., :half]
    lower = incoming[..., half:]
    return jnp.concatenate([upper * cosine + lower * sine, lower * cosine - upper * sine], axis=-1)


def norm_forward(residual, gain):
    inverse = lax.rsqrt(jnp.mean(residual * residual, axis=-1, keepdims=True) + EPS)
    return ((residual * inverse * gain).astype(jnp.bfloat16), inverse)


def norm_backward(residual, inverse, gain, incoming):
    scaled = incoming * gain
    through = inverse * scaled - residual * inverse**3 * jnp.mean(
        scaled * residual, axis=-1, keepdims=True
    )
    return (through, jnp.sum(incoming * residual * inverse, axis=0))


def padded(array, axis, parts, count, full):
    if count == full:
        return array
    shape = array.shape
    split = array.reshape(shape[:axis] + (parts, count) + shape[axis + 1 :])
    pads = [(0, 0)] * split.ndim
    pads[axis + 1] = (0, full - count)
    return jnp.pad(split, pads).reshape(shape[:axis] + (parts * full,) + shape[axis + 1 :])


def trimmed(array, axis, parts, count, full):
    if count == full:
        return array
    shape = array.shape
    split = array.reshape(shape[:axis] + (parts, full) + shape[axis + 1 :])
    kept = lax.slice_in_dim(split, 0, count, axis=axis + 1)
    return kept.reshape(shape[:axis] + (parts * count,) + shape[axis + 1 :])


def plain_layer(
    layer_input, output_grad, wide, tall, norm_gains, block_order, sizes
):
    parts, width, half, kv, short, full, high = sizes
    hidden_size = 2 * half
    rows = layer_input.shape[1]
    block = rows // 2
    group = HEADS // KV_HEADS
    scale = 1.0 / math.sqrt(HEAD)
    ctx_place = lax.axis_index("ctx")
    offsets = jnp.arange(block, dtype=jnp.int32)
    own_blocks = lax.dynamic_slice_in_dim(block_order, 2 * ctx_place, 2)
    query_pos = (own_blocks[:, None] * block + offsets[None, :]).reshape(rows)
    key_pos = (block_order[:, None] * block + offsets[None, :]).reshape(-1)

    all_wide, all_tall = gather_weights(wide, tall)
    w_qk, w_ov, w_gate_0, w_gate_1, w_up_0, w_up_1 = [all_wide[i].reshape(width, half) for i in range(WIDE)]
    w_down = [all_tall[i].reshape(half, width) for i in range(2)]

    residual = layer_input[0].astype(jnp.float32)
    normed_first, inverse_first = norm_forward(residual, norm_gains[0])
    qk_pre = jnp.dot(normed_first, w_qk, preferred_element_type=jnp.float32)
    query_pre = qk_pre[:, :width].reshape(rows, HEADS, HEAD)
    key_pre = qk_pre[:, width:].reshape(rows, KV_HEADS, HEAD)
    value_low = (
        jnp.dot(normed_first, w_ov, preferred_element_type=jnp.float32)[:, width:]
        .astype(jnp.bfloat16)
        .reshape(rows, KV_HEADS, HEAD)
    )
    cosine, sine = rotary_tables(query_pos, HEAD)
    query_rot = rotate(query_pre, cosine, sine).astype(jnp.bfloat16)
    key_rot = rotate(key_pre, cosine, sine).astype(jnp.bfloat16)
    keys_all, values_all = (
        lax.all_gather(key_rot, "ctx", axis=0, tiled=True),
        lax.all_gather(value_low, "ctx", axis=0, tiled=True),
    )
    keys_head = keys_all.transpose(1, 0, 2)
    values_head = values_all.transpose(1, 0, 2)
    queries_head = (
        query_rot.reshape(rows, KV_HEADS, group, HEAD)
        .transpose(1, 2, 0, 3)
        .reshape(KV_HEADS, group * rows, HEAD)
    )
    row_pos = jnp.tile(query_pos, group)
    allowed = key_pos[None, :] <= row_pos[:, None]

    def head_forward(item):
        query, key, value = item
        scores = jnp.where(allowed, contract(query, key, 1, 1) * scale, MASKED)
        top = jnp.max(scores, axis=-1, keepdims=True)
        expo = jnp.exp(scores - top)
        total = jnp.sum(expo, axis=-1, keepdims=True)
        probs_low = (expo / total).astype(jnp.bfloat16)
        return (
            jnp.dot(probs_low, value, preferred_element_type=jnp.float32),
            (top + jnp.log(total))[:, 0],
        )

    mixed, log_total = lax.map(head_forward, (queries_head, keys_head, values_head))
    attended = (
        mixed.reshape(KV_HEADS, group, rows, HEAD)
        .transpose(2, 0, 1, 3)
        .reshape(rows, HEADS * HEAD)
        .astype(jnp.bfloat16)
    )
    w_out = w_ov[:, :width]
    middle = residual + jnp.dot(attended, w_out, preferred_element_type=jnp.float32)
    normed_second, inverse_second = norm_forward(middle, norm_gains[1])

    def sides(left, right):
        return jnp.concatenate([left, right], axis=1)

    gate = sides(
        jnp.dot(normed_second, w_gate_0, preferred_element_type=jnp.float32),
        jnp.dot(normed_second, w_gate_1, preferred_element_type=jnp.float32),
    )
    lifted = sides(
        jnp.dot(normed_second, w_up_0, preferred_element_type=jnp.float32),
        jnp.dot(normed_second, w_up_1, preferred_element_type=jnp.float32),
    )
    sigma = jax.nn.sigmoid(gate)
    hidden = (gate * sigma * lifted).astype(jnp.bfloat16)
    hidden_split = hidden.reshape(rows, parts, 2, high)
    hidden_sides = [hidden_split[:, :, i].reshape(rows, half) for i in range(2)]
    layer_output = (
        middle
        + jnp.dot(hidden_sides[0], w_down[0], preferred_element_type=jnp.float32)
        + jnp.dot(hidden_sides[1], w_down[1], preferred_element_type=jnp.float32)
    ).astype(jnp.bfloat16)
    upstream = output_grad[0]
    grad_hidden = jnp.stack(
        [contract(upstream, w_down[i], 1, 1).reshape(rows, parts, high) for i in range(2)], axis=2
    ).reshape(rows, hidden_size)
    grad_gate = (grad_hidden * lifted * sigma * (1.0 + gate * (1.0 - sigma))).astype(jnp.bfloat16)
    grad_lifted = (grad_hidden * gate * sigma).astype(jnp.bfloat16)
    grad_normed_second = (
        contract(grad_gate[:, :half], w_gate_0, 1, 1)
        + contract(grad_gate[:, half:], w_gate_1, 1, 1)
        + contract(grad_lifted[:, :half], w_up_0, 1, 1)
        + contract(grad_lifted[:, half:], w_up_1, 1, 1)
    )
    through_second, gain_second = norm_backward(
        middle, inverse_second, norm_gains[1], grad_normed_second
    )
    grad_middle = upstream.astype(jnp.float32) + through_second
    grad_branch = grad_middle.astype(jnp.bfloat16)
    grad_attended = contract(grad_branch, w_out, 1, 1).astype(jnp.bfloat16)
    grad_heads = (
        grad_attended.reshape(rows, KV_HEADS, group, HEAD)
        .transpose(1, 2, 0, 3)
        .reshape(KV_HEADS, group * rows, HEAD)
    )

    def head_backward(item):
        query, key, value, grad_out, log_row = item
        scores = jnp.where(allowed, contract(query, key, 1, 1) * scale, MASKED)
        probs = jnp.exp(scores - log_row[:, None])
        grad_value_part = contract(probs.astype(jnp.bfloat16), grad_out, 0, 0)
        grad_probs = contract(grad_out, value, 1, 1)
        grad_scores = (
            probs * (grad_probs - jnp.sum(grad_probs * probs, axis=-1, keepdims=True))
        ).astype(jnp.bfloat16)
        grad_query_part = jnp.dot(grad_scores, key, preferred_element_type=jnp.float32) * scale
        grad_key_part = contract(grad_scores, query, 0, 0) * scale
        return (grad_query_part, grad_key_part, grad_value_part)

    grad_query_rot, grad_key_all, grad_value_all = lax.map(
        head_backward, (queries_head, keys_head, values_head, grad_heads, log_total)
    )
    grad_key_own, grad_value_own = (
        lax.psum_scatter(
            grad_key_all.astype(jnp.bfloat16), "ctx", scatter_dimension=1, tiled=True
        ).astype(jnp.float32),
        lax.psum_scatter(
            grad_value_all.astype(jnp.bfloat16), "ctx", scatter_dimension=1, tiled=True
        ).astype(jnp.float32),
    )
    grad_query = (
        unrotate(
            grad_query_rot.reshape(KV_HEADS, group, rows, HEAD)
            .transpose(2, 0, 1, 3)
            .reshape(rows, HEADS, HEAD),
            cosine,
            sine,
        )
        .reshape(rows, HEADS * HEAD)
        .astype(jnp.bfloat16)
    )
    grad_key = (
        unrotate(grad_key_own.transpose(1, 0, 2), cosine, sine)
        .reshape(rows, KV_HEADS * HEAD)
        .astype(jnp.bfloat16)
    )
    grad_value = (
        grad_value_own.transpose(1, 0, 2).reshape(rows, KV_HEADS * HEAD).astype(jnp.bfloat16)
    )
    grad_qk = sides(grad_query, grad_key)
    zero_query = jnp.zeros((rows, width), jnp.bfloat16)
    grad_v = sides(zero_query, grad_value)
    grad_normed_first = contract(grad_qk, w_qk, 1, 1) + contract(grad_v, w_ov, 1, 1)
    through_first, gain_first = norm_backward(
        residual, inverse_first, norm_gains[0], grad_normed_first
    )
    input_gradient = grad_middle + through_first

    xt = jnp.stack([item.T for item in (normed_first, attended, normed_second, upstream)])
    xt = padded(xt, 1, parts, short, full)
    dy = jnp.stack(
        [
            grad_qk,
            sides(grad_branch, jnp.zeros((rows, kv), jnp.bfloat16)),
            grad_gate[:, :half],
            grad_gate[:, half:],
            grad_lifted[:, :half],
            grad_lifted[:, half:],
            hidden_sides[0],
            hidden_sides[1],
            grad_v,
        ]
    )
    gains = jnp.pad(jnp.stack([gain_first, gain_second]), ((0, 6), (0, 0)))
    return layer_output, input_gradient, xt, dy, gains


def rotation(block_order, rows):
    block = rows // 2
    ctx_place = lax.axis_index("ctx")
    offsets = jnp.arange(block, dtype=jnp.int32)
    own_blocks = lax.dynamic_slice_in_dim(block_order, 2 * ctx_place, 2)
    query_pos = (own_blocks[:, None] * block + offsets[None, :]).reshape(rows)
    key_pos = (block_order[:, None] * block + offsets[None, :]).reshape(-1)
    bias = jnp.where(key_pos[:, None] <= query_pos[None, :], 0.0, MASKED).astype(jnp.float32)
    lane = jnp.arange(128, dtype=jnp.int32)
    index = (lane % (HEAD // 2)).astype(jnp.float32)
    frequency = THETA ** (-(index * 2.0 / HEAD))
    angle = query_pos.astype(jnp.float32)[:, None] * frequency[None, :]
    cosine, sine = jnp.cos(angle), jnp.sin(angle)
    early = (lane % HEAD < HEAD // 2)[None, :]
    return (cosine, jnp.where(early, 0.0, sine), jnp.where(early, -sine, 0.0)), bias


def plain_step(layer_input, output_grad, norm_gains, block_order, weights, olds, factors, sizes):
    parts, width, half, kv, short, full, high = sizes
    query_weight, key_weight, value_weight, output_weight, gate_weight, up_weight, down_weight = weights
    (
        query_momentum,
        key_momentum,
        value_momentum,
        output_momentum,
        gate_momentum,
        up_momentum,
        down_momentum,
    ) = olds

    def sides(left, right):
        return jnp.concatenate([left, right], axis=1)

    wide = jnp.stack(
        [
            jnp.concatenate([query_weight, key_weight], axis=1),
            jnp.concatenate([output_weight, value_weight], axis=1),
            gate_weight[:, :half],
            gate_weight[:, half:],
            up_weight[:, :half],
            up_weight[:, half:],
        ]
    )
    tall = down_weight.reshape(2, high, width)
    layer_output, input_gradient, xt, dy, gains = plain_layer(
        layer_input, output_grad, wide, tall, norm_gains, block_order, sizes
    )

    def pad_rows(array):
        return padded(array, 0, 1, short, full)

    def pad_columns(array):
        return padded(array, 1, parts, short, full)

    moments = (
        pad_rows(sides(query_momentum, key_momentum)),
        pad_rows(sides(output_momentum, value_momentum)),
        pad_rows(gate_momentum),
        pad_rows(up_momentum),
        pad_columns(down_momentum),
    )
    g_wide, g_tall, s_wide, s_tall, gain_sum = reduce_gradients(xt, dy, gains, moments, full, high)
    o_wide, o_tall = orthogonalize(s_wide, s_tall, full, high, width)

    def unpack(wide_pieces, tall_pieces):
        pieces = wide_pieces[:, :short]
        tall = trimmed(tall_pieces, 2, parts, short, full).reshape(2 * high, width)
        return (
            pieces[0, :, :width],
            pieces[0, :, width:],
            pieces[1, :, width:],
            pieces[1, :, :width],
            sides(pieces[2], pieces[3]),
            sides(pieces[4], pieces[5]),
            tall,
        )

    gradients = [item.astype(jnp.float32) for item in unpack(g_wide, g_tall)]
    orthos = unpack(o_wide, o_tall)
    moments = [MOMENTUM * old + new for old, new in zip(olds, gradients)]
    new_weights = [
        weight.astype(jnp.float32) + factor * ortho.astype(jnp.float32)
        for weight, factor, ortho in zip(weights, factors, orthos)
    ]
    return layer_output, input_gradient, gradients, moments, new_weights, gain_sum


def on_device(
    layer_input,
    output_grad,
    query_weight,
    key_weight,
    value_weight,
    output_weight,
    gate_weight,
    up_weight,
    down_weight,
    norm_gains,
    query_momentum,
    key_momentum,
    value_momentum,
    output_momentum,
    gate_momentum,
    up_momentum,
    down_momentum,
    gain_momentum,
    block_order,
):
    parts = lax.axis_size("fsdp")
    width = layer_input.shape[2]
    half = gate_weight.shape[1] // 2
    kv = key_weight.shape[1]
    short = width // parts
    full = -(-short // 16) * 16
    high = half // parts
    sizes = (parts, width, half, kv, short, full, high)

    weights = (query_weight, key_weight, value_weight, output_weight, gate_weight, up_weight, down_weight)
    olds = (
        query_momentum,
        key_momentum,
        value_momentum,
        output_momentum,
        gate_momentum,
        up_momentum,
        down_momentum,
    )
    factors = []
    for index, weight in enumerate(weights):
        step_rate = OUT_RATE if index == 3 else RATE
        factors.append(-step_rate * max(1.0, weight.shape[1] / (weight.shape[0] * parts)) ** 0.5)

    fused = (
        lax.axis_size("ctx") == CLASSES
        and short == full
        and parts % 2 == 0
        and half % (2 * half // parts) == 0
        and (2 * half // parts) % 128 == 0
        and layer_input.shape[1] == 128
    )
    if fused:
        tables, bias = rotation(block_order, layer_input.shape[1])

        def turned(items):
            q, k, v, o, gate, up, down = items
            return (q, k.T, o, v.T, gate, up, down.T)

        shards, moments = turned(weights), turned(olds)
        out_turned, grad_turned, g, o, gain_sum = step_pass(
            layer_input[0].T, output_grad[0].T, norm_gains, tables, bias, shards, moments
        )
        gradients, moments, new_weights = settle(g, o, moments, shards, factors)
        layer_output, input_gradient = out_turned.T, grad_turned.T
    else:
        layer_output, input_gradient, gradients, moments, new_weights, gain_sum = plain_step(
            layer_input, output_grad, norm_gains, block_order, weights, olds, factors, sizes
        )
    gain_width = norm_gains.shape[1] // parts
    place = lax.axis_index("fsdp") * gain_width
    gain_gradient = lax.dynamic_slice_in_dim(gain_sum[:2], place, gain_width, 1)
    gain_shard = lax.dynamic_slice_in_dim(norm_gains, place, gain_width, 1)
    gain_moment = MOMENTUM * gain_momentum + gain_gradient
    new_gains = gain_shard - GAIN_RATE * gain_moment
    return (
        layer_output[None],
        input_gradient[None],
        *gradients,
        gain_gradient,
        *moments,
        gain_moment,
        *new_weights,
        new_gains,
    )


def solution(mesh):
    tokens = P("fsdp", "ctx", None)
    shard = P("fsdp", None)
    gains = P(None, "fsdp")
    return jax.shard_map(
        on_device,
        mesh=mesh,
        in_specs=(tokens, tokens) + (shard,) * 7 + (P(),) + (shard,) * 7 + (gains, P()),
        out_specs=(tokens, tokens) + ((shard,) * 7 + (gains,)) * 3,
        check_vma=False,
    )
```

```python
import functools
import math

import jax
import jax.numpy as jnp
from jax import lax
from jax.experimental import pallas as pl
from jax.experimental.pallas import tpu as pltpu
from jax.sharding import PartitionSpec as P

HEADS = 15
KV_HEADS = 5
HEAD = 64
NS_ITERS = 5


EPS = 1e-05
THETA = 100000.0
NS_A = 3.4445
NS_B = -4.775
NS_C = 2.0315
MOMENTUM = 0.95
RATE = 0.2
OUT_RATE = 6.0
GAIN_RATE = 0.002
MASKED = -1e30

MESH = pl.DeviceIdType.MESH
BF16 = jnp.bfloat16
F32 = jnp.float32
ANY = pl.BlockSpec(memory_space=pl.ANY)
VMEM = pl.BlockSpec(memory_space=pltpu.VMEM)
CLASSES = 8
WIDE = 6


def contract(left, right, left_dim, right_dim):
    return lax.dot_general(
        left, right, (((left_dim,), (right_dim,)), ((), ())), preferred_element_type=jnp.float32
    )


class Place:
    def __init__(self):
        self.parts = lax.axis_size("fsdp")
        self.extra = lax.axis_size("ctx") // CLASSES
        self.c = lax.axis_index("ctx")
        self.f = lax.axis_index("fsdp")
        self.p = lax.rem(self.c, CLASSES)
        self.core = lax.rem(self.c, 2)
        self.b1 = jnp.where(self.core == 0, 2, 4)
        self.b2 = jnp.where(self.core == 0, 4, 2)

    def peer(self, bits):
        return (self.c ^ bits, self.f)

    def along(self, j):
        return (self.c, self.f ^ j)

    def other(self, j):
        groups = self.extra
        return (lax.rem(self.c + CLASSES * j, CLASSES * groups), self.f)

    def barrier(self, bits=(1, 2, 4), line=True, others=False):
        sem = pltpu.get_barrier_semaphore()
        targets = [self.peer(b) for b in bits]
        if line:
            targets += [self.along(j) for j in range(1, self.parts)]
        if others:
            targets += [self.other(j) for j in range(1, self.extra)]
        for target in targets:
            pl.semaphore_signal(sem, inc=1, device_id=target, device_id_type=MESH)
        pl.semaphore_wait(sem, len(targets))


def remote(src, dst, send, recv, target):
    return pltpu.make_async_remote_copy(
        src_ref=src, dst_ref=dst, send_sem=send, recv_sem=recv, device_id=target, device_id_type=MESH
    )


def by_kind(cls, wide, tall):
    pl.when(cls < WIDE)(wide)
    pl.when(cls >= WIDE)(tall)


def weights_kernel(in_a, in_b, out_a, out_b, local, zs, s1, s2, sc, recv):
    at = Place()
    p, f, parts = at.p, at.f, at.parts
    at.barrier()
    copies = [
        pltpu.make_async_copy(in_a, out_a.at[:, f], local.at[0]),
        pltpu.make_async_copy(in_b, out_b.at[:, f], local.at[1]),
    ]
    for copy in copies:
        copy.start()

    def act(cls, j, g, send, target, what, first=False):
        def wide():
            dst = out_a.at[cls, g]
            src = in_a.at[cls] if first else dst
            getattr(remote(src, dst, send, recv.at[cls, j], target), what)()

        def tall():
            dst = out_b.at[cls - WIDE, g]
            src = in_b.at[cls - WIDE] if first else dst
            getattr(remote(src, dst, send, recv.at[cls, j], target), what)()

        by_kind(cls, wide, tall)

    sends = []

    def send(cls, j, g, sem, target, first=False):
        act(cls, j, g, sem, target, "start", first)
        sends.append((cls, j, g, sem, target, first))

    def arrived(cls, j):
        act(cls, j, f ^ j, zs.at[j], at.along(j), "wait_recv")

    for j in range(1, parts):
        send(p, j, f, zs.at[j], at.along(j), True)
    for j in range(1, parts):
        arrived(p, j)
        send(p, j, f ^ j, s1.at[0, j], at.peer(at.b1))
        send(p, j, f ^ j, s2.at[0, j], at.peer(at.b2))
        send(p, j, f ^ j, sc.at[0, j], at.peer(1))
    for j in range(1, parts):
        arrived(p ^ at.b1, j)
        send(p ^ at.b1, j, f ^ j, s2.at[1, j], at.peer(at.b2))
        send(p ^ at.b1, j, f ^ j, sc.at[1, j], at.peer(1))
    for slot, bits in ((2, at.b2), (3, at.b1 ^ at.b2)):
        for j in range(1, parts):
            arrived(p ^ bits, j)
            send(p ^ bits, j, f ^ j, sc.at[slot, j], at.peer(1))
    for bits in (1, 3, 5, 7):
        for j in range(1, parts):
            arrived(p ^ bits, j)
    for cls, j, g, sem, target, first in sends:
        act(cls, j, g, sem, target, "wait_send", first)
    for copy in copies:
        copy.wait()


def gather_weights(wide, tall):
    parts = lax.axis_size("fsdp")
    dma = pltpu.SemaphoreType.DMA
    return pl.pallas_call(
        weights_kernel,
        out_shape=(
            jax.ShapeDtypeStruct((WIDE, parts) + wide.shape[1:], BF16),
            jax.ShapeDtypeStruct((CLASSES - WIDE, parts) + tall.shape[1:], BF16),
        ),
        in_specs=[ANY, ANY],
        out_specs=(ANY, ANY),
        scratch_shapes=[
            dma((2,)),
            dma((parts,)),
            dma((1, parts)),
            dma((2, parts)),
            dma((4, parts)),
            dma((CLASSES, parts)),
        ],
        compiler_params=pltpu.CompilerParams(collective_id=0, has_side_effects=True),
        name="gather_weights",
    )(wide, tall)


def spread(at, own_a, own_b, out_a, out_b, local, ss, recv):
    p = at.p

    def act(cls, sem, target, what, first=False):
        def wide():
            dst = out_a.at[cls]
            getattr(remote(own_a if first else dst, dst, sem, recv.at[cls], target), what)()

        def tall():
            dst = out_b.at[cls - WIDE]
            getattr(remote(own_b if first else dst, dst, sem, recv.at[cls], target), what)()

        by_kind(cls, wide, tall)

    def keep(what):
        def wide():
            getattr(pltpu.make_async_copy(own_a, out_a.at[p], local), what)()

        def tall():
            getattr(pltpu.make_async_copy(own_b, out_b.at[p - WIDE], local), what)()

        by_kind(p, wide, tall)

    sends = []

    def send(cls, slot, target, first=False):
        act(cls, ss.at[slot], target, "start", first)
        sends.append((cls, slot, target, first))

    def arrived(cls):
        act(cls, ss.at[0], at.peer(1), "wait_recv")

    send(p, 0, at.peer(at.b1), True)
    send(p, 1, at.peer(at.b2), True)
    send(p, 2, at.peer(1), True)
    keep("start")

    def finish():
        arrived(p ^ at.b1)
        send(p ^ at.b1, 3, at.peer(at.b2))
        send(p ^ at.b1, 4, at.peer(1))
        arrived(p ^ at.b2)
        send(p ^ at.b2, 5, at.peer(1))
        arrived(p ^ at.b1 ^ at.b2)
        send(p ^ at.b1 ^ at.b2, 6, at.peer(1))
        for bits in (1, 3, 5, 7):
            arrived(p ^ bits)
        for cls, slot, target, first in sends:
            act(cls, ss.at[slot], target, "wait_send", first)
        keep("wait")

    return finish


def reduce_kernel(
    parts, extra, high,
    xt_in, dy_in, gain_in, m_qk, m_ov, m_gate, m_up, m_down,
    g_a, g_b, s_a, s_b, gain_out,
    xt, dy, p1s, p1r, p2s, p2r, own, own_t, za_s, za_r, zb_s, zb_r, ma, mb, ga, gb, sa, sb, es, er, gain_s, gain_r,
    ls, xs, xr, s1, r1, s2, r2, zs, zr, esem, ersem, msem, gs, gr, ag_l, ag_s, ag_r, ss, sr, sl,
):
    at = Place()
    p, f, core = at.p, at.f, at.core
    tokens = xt_in.shape[2]
    rows = ma.shape[0]
    half = dy.shape[2]

    def moment(what):
        for cls in range(CLASSES):
            @pl.when(p == cls)
            def _(cls=cls):
                side = cls % 2
                if cls < 2:
                    src, dst = (m_qk, m_ov)[cls], ma
                elif cls < WIDE:
                    whole = m_gate if cls < 4 else m_up
                    src, dst = whole.at[:, pl.ds(side * half, half)], ma
                else:
                    src, dst = m_down.at[pl.ds(side * high, high)], mb
                getattr(pltpu.make_async_copy(src, dst, msem), what)()

    moment("start")
    mine = [pltpu.make_async_copy(xt_in, xt.at[:, :, pl.ds(0, tokens)], ls.at[0])]
    for slot in range(4):
        mine.append(
            pltpu.make_async_copy(dy_in.at[core + 2 * slot], dy.at[slot, pl.ds(0, tokens)], ls.at[1 + slot])
        )
    mine.append(pltpu.make_async_copy(dy_in.at[8], dy.at[4, pl.ds(0, tokens)], ls.at[5]))
    for copy in mine:
        copy.start()
    at.barrier(others=True)
    pair = at.peer(1)
    theirs = [remote(xt_in, xt.at[:, :, pl.ds(tokens, tokens)], xs.at[0], xr.at[0], pair)]
    for slot in range(4):
        theirs.append(
            remote(dy_in.at[1 - core + 2 * slot], dy.at[slot, pl.ds(tokens, tokens)], xs.at[1 + slot], xr.at[1 + slot], pair)
        )
    theirs.append(remote(dy_in.at[8], dy.at[4, pl.ds(tokens, tokens)], xs.at[5], xr.at[5], pair))
    for copy in theirs:
        copy.start()

    def swap(slot, target):
        return remote(gain_s.at[slot], gain_r.at[slot], gs.at[slot], gr.at[slot], target)

    gain_s[0] = gain_in[...]
    swaps = [swap(0, pair)]
    swaps[0].start()
    for copy in mine:
        copy.wait()
    for copy in theirs:
        copy.wait()

    def term(cls, r):
        at_rows = pl.ds(pl.multiple_of(r * rows, rows), rows)
        slot = lax.div(cls, 2)
        kind = jnp.where(cls == 0, 0, jnp.where(cls == 1, 1, jnp.where(cls < WIDE, 2, 3)))
        value = jnp.dot(xt[kind, at_rows, :], dy[slot], preferred_element_type=F32)
        return value

    def with_values(cls, r, put):
        at_rows = pl.ds(pl.multiple_of(r * rows, rows), rows)

        @pl.when(cls == 1)
        def _():
            put(term(cls, r) + jnp.dot(xt[0, at_rows, :], dy[4], preferred_element_type=F32))

        @pl.when(cls != 1)
        def _():
            put(term(cls, r))

    def order(i):
        return lax.rem(f + 1 + i, parts)

    def one(slot, i):
        r = order(i)
        return remote(p1s.at[slot, r], p1r.at[slot, r], s1.at[slot, r], r1.at[slot, r], at.peer(at.b1))

    for slot, bits in ((0, at.b1 ^ at.b2), (1, at.b1)):
        def first(i, carry, slot=slot, bits=bits):
            r = order(i)

            def put(value):
                p1s[slot, r] = value.astype(BF16)

            with_values(p ^ bits, r, put)
            one(slot, i).start()
            return carry

        lax.fori_loop(0, parts, first, 0)

    swaps[0].wait()
    gain_s[1] = gain_s[0] + gain_r[0]
    swaps.append(swap(1, at.peer(2)))
    swaps[1].start()

    def two(i):
        r = order(i)
        return remote(p2s.at[r], p2r.at[r], s2.at[r], r2.at[r], at.peer(at.b2))

    def second(i, carry):
        r = order(i)
        one(0, i).wait_recv()

        def put(value):
            p2s[r] = (value + p1r[0, r].astype(F32)).astype(BF16)

        with_values(p ^ at.b2, r, put)
        two(i).start()
        return carry

    lax.fori_loop(0, parts, second, 0)
    swaps[1].wait()
    gain_s[2] = gain_s[1] + gain_r[1]
    swaps.append(swap(2, at.peer(4)))
    swaps[2].start()

    def line_a(r, source):
        return remote(za_s.at[r], za_r.at[source], zs.at[r], zr.at[source], (at.c, r))

    def line_b(r, source):
        return remote(
            zb_s.at[pl.ds(pl.multiple_of(r * high, high), high)],
            zb_r.at[source], zs.at[r], zr.at[source], (at.c, r),
        )

    early = extra == 1

    def third(i, carry):
        r = order(i)
        one(1, i).wait_recv()
        two(i).wait_recv()

        def put(value):
            total = value + p1r[1, r].astype(F32) + p2r[r].astype(F32)
            own[r] = total
            if early:
                za_s[r] = total.astype(BF16)

        with_values(p, r, put)
        if early:
            @pl.when((p < WIDE) & (i < parts - 1))
            def _():
                line_a(r, f).start()
        return carry

    lax.fori_loop(0, parts, third, 0)
    swaps[2].wait()
    gain_s[3] = gain_s[2] + gain_r[2]

    if not early:
        es[...] = own[...].astype(BF16)
        group = [
            remote(es, er.at[j - 1], esem.at[j - 1], ersem.at[j - 1], at.other(j)) for j in range(1, extra)
        ]
        for copy in group:
            copy.start()
        for j in range(1, extra):
            group[j - 1].wait_recv()
            own[...] = own[...] + er[j - 1].astype(F32)
        for copy in group:
            copy.wait_send()
        za_s[...] = own[...].astype(BF16)

        @pl.when(p < WIDE)
        def _():
            for j in range(1, parts):
                line_a(f ^ j, f).start()

    @pl.when(p >= WIDE)
    def _():
        for tile in range(half // 128):
            for r in range(parts):
                block = own[r, :, pl.ds(tile * 128, 128)]
                if rows % 128 == 0:
                    own_t[pl.ds(tile * 128, 128), pl.ds(r * rows, rows)] = block.T
            if rows % 128 != 0:
                column = own[:, :, pl.ds(tile * 128, 128)].reshape(parts * rows, 128)
                own_t[pl.ds(tile * 128, 128), :] = column.T
        zb_s[...] = own_t[...].astype(BF16)
        for j in range(1, parts):
            line_b(f ^ j, f).start()

    line_gain = [
        remote(gain_s.at[3], gain_r.at[3 + j], gs.at[3 + j], gr.at[3 + j], at.along(j)) for j in range(1, parts)
    ]
    other_gain = []
    for copy in line_gain:
        copy.start()

    moment("wait")

    @pl.when(p < WIDE)
    def _():
        total = own[f]
        for j in range(1, parts):
            line_a(f ^ j, f ^ j).wait_recv()
            total = total + za_r[f ^ j].astype(F32)
        ga[...] = total.astype(BF16)
        sa[...] = (MOMENTUM * ma[...] + total).astype(BF16)

    @pl.when(p >= WIDE)
    def _():
        total = own_t[pl.ds(pl.multiple_of(f * high, high), high), :]
        for j in range(1, parts):
            line_b(f ^ j, f ^ j).wait_recv()
            total = total + zb_r[f ^ j].astype(F32)
        gb[...] = total.astype(BF16)
        sb[...] = (MOMENTUM * mb[...] + total).astype(BF16)

    def share_a(j, source):
        return remote(sa, s_a.at[pl.ds(pl.multiple_of(source * rows, rows), rows)], ss.at[j], sr.at[j], at.along(j))

    def share_b(j, source):
        return remote(sb, s_b.at[pl.ds(pl.multiple_of(source * high, high), high)], ss.at[j], sr.at[j], at.along(j))

    @pl.when(p < WIDE)
    def _():
        for j in range(1, parts):
            share_a(j, f).start()
        pltpu.make_async_copy(sa, s_a.at[pl.ds(pl.multiple_of(f * rows, rows), rows)], sl).start()

    @pl.when(p >= WIDE)
    def _():
        for j in range(1, parts):
            share_b(j, f).start()
        pltpu.make_async_copy(sb, s_b.at[pl.ds(pl.multiple_of(f * high, high), high)], sl).start()

    finish = spread(at, ga, gb, g_a, g_b, ag_l, ag_s, ag_r)
    total = gain_s[3]
    for j in range(1, parts):
        line_gain[j - 1].wait()
        total = total + gain_r[3 + j]
    if extra > 1:
        gain_s[4] = total
        other_gain = [
            remote(gain_s.at[4], gain_r.at[3 + parts + j], gs.at[3 + parts + j], gr.at[3 + parts + j], at.other(j))
            for j in range(1, extra)
        ]
        for copy in other_gain:
            copy.start()
        for j in range(1, extra):
            other_gain[j - 1].wait()
            total = total + gain_r[3 + parts + j]
    gain_out[...] = total
    finish()

    for slot in range(2):
        lax.fori_loop(0, parts, lambda i, carry, slot=slot: (one(slot, i).wait_send(), carry)[1], 0)
    lax.fori_loop(0, parts, lambda i, carry: (two(i).wait_send(), carry)[1], 0)

    @pl.when(p < WIDE)
    def _():
        for j in range(1, parts):
            line_a(f ^ j, f).wait_send()
            share_a(j, f).wait_send()
            share_a(j, f ^ j).wait_recv()
        pltpu.make_async_copy(sa, s_a.at[pl.ds(pl.multiple_of(f * rows, rows), rows)], sl).wait()

    @pl.when(p >= WIDE)
    def _():
        for j in range(1, parts):
            line_b(f ^ j, f).wait_send()
            share_b(j, f).wait_send()
            share_b(j, f ^ j).wait_recv()
        pltpu.make_async_copy(sb, s_b.at[pl.ds(pl.multiple_of(f * high, high), high)], sl).wait()


def reduce_gradients(xt, dy, gains, moments, rows, high):
    parts = lax.axis_size("fsdp")
    extra = lax.axis_size("ctx") // CLASSES
    kinds, depth, tokens = xt.shape
    half = dy.shape[2]
    dma = pltpu.SemaphoreType.DMA
    vm = pltpu.VMEM
    n_gain = 4 + parts + extra
    group = max(extra - 1, 1)
    spare = (parts, rows, half) if extra > 1 else (1, 16, 128)
    return pl.pallas_call(
        functools.partial(reduce_kernel, parts, extra, high),
        out_shape=(
            jax.ShapeDtypeStruct((WIDE, rows, half), BF16),
            jax.ShapeDtypeStruct((CLASSES - WIDE, high, depth), BF16),
            jax.ShapeDtypeStruct((depth, half), BF16),
            jax.ShapeDtypeStruct((half, depth), BF16),
            jax.ShapeDtypeStruct(gains.shape, F32),
        ),
        in_specs=[ANY, ANY, VMEM] + [ANY] * 5,
        out_specs=(ANY, ANY, ANY, ANY, VMEM),
        scratch_shapes=[
            vm((kinds, depth, 2 * tokens), BF16),
            vm((5, 2 * tokens, half), BF16),
            vm((2, parts, rows, half), BF16),
            vm((2, parts, rows, half), BF16),
            vm((parts, rows, half), BF16),
            vm((parts, rows, half), BF16),
            vm((parts, rows, half), F32),
            vm((half, depth), F32),
            vm((parts, rows, half), BF16),
            vm((parts, rows, half), BF16),
            vm((half, depth), BF16),
            vm((parts, high, depth), BF16),
            vm((rows, half), F32),
            vm((high, depth), F32),
            vm((rows, half), BF16),
            vm((high, depth), BF16),
            vm((rows, half), BF16),
            vm((high, depth), BF16),
            vm(spare, BF16),
            vm((group,) + spare, BF16),
            vm((5,) + gains.shape, F32),
            vm((n_gain,) + gains.shape, F32),
            dma((6,)), dma((6,)), dma((6,)),
            dma((2, parts)), dma((2, parts)), dma((parts,)), dma((parts,)), dma((parts,)), dma((parts,)),
            dma((group,)), dma((group,)), dma, dma((n_gain,)), dma((n_gain,)),
            dma, dma((7,)), dma((CLASSES,)), dma((parts,)), dma((parts,)), dma,
        ],
        compiler_params=pltpu.CompilerParams(
            collective_id=1, has_side_effects=True, vmem_limit_bytes=62 << 20
        ),
        name="reduce_gradients",
    )(xt, dy, gains, *moments)


def rounded(value):
    return value.astype(BF16)


def poly_rows(g, row_start, count):
    block = g[pl.ds(row_start, count), :]
    return rounded(NS_B * block.astype(F32) + NS_C * jnp.dot(block, g[...], preferred_element_type=F32))


def ortho_kernel(
    parts, rows, high, narrow,
    s_a, s_b, o_a, o_b,
    x, x_t, gs, gr, g, poly, sq, sq_r, pa, pb, kt,
    gsem, rsem, qs, qr, ag_l, ag_s, ag_r,
):
    at = Place()
    p, f = at.p, at.f
    depth, half = x.shape
    step = depth // 4
    at.barrier(line=False)
    pair = at.peer(1)

    @pl.when(p < WIDE)
    def _():
        x[...] = s_a[...]

    @pl.when(p >= WIDE)
    def _():
        for tile in range(half // 128):
            x[:, pl.ds(tile * 128, 128)] = s_b[pl.ds(tile * 128, 128), :].T

    def scale_of(total):
        return 1.0 / (jnp.sqrt(total) + 1e-07)

    def normal(ref, inverse):
        ref[...] = rounded(ref[...].astype(F32) * inverse)

    def exchange(slot, r):
        chunk = pl.ds(r * step, step)
        return remote(gs.at[chunk], gr.at[slot, chunk], gsem.at[r], rsem.at[slot, r], pair)

    def fill_poly():
        for r in range(4):
            poly[pl.ds(r * step, step), :] = poly_rows(g, r * step, step)

    my_rows = pl.ds(pl.multiple_of(f * rows, rows), rows)
    my_high = pl.ds(pl.multiple_of(f * high, high), high)

    @pl.when(p >= 2)
    def _():
        wide = x[...].astype(F32)
        sq[...] = jnp.broadcast_to(jnp.sum(wide * wide), sq.shape)
        copy = remote(sq, sq_r, qs, qr, pair)
        copy.start()
        copy.wait()
        normal(x, scale_of(sq[...] + sq_r[...])[:1, :1])

        def grams(slot):
            for r in range(4):
                gs[pl.ds(r * step, step), :] = rounded(contract(x[pl.ds(r * step, step), :], x[...], 1, 1))
                exchange(slot, r).start()
            for r in range(4):
                chunk = pl.ds(r * step, step)
                exchange(slot, r).wait()
                g[chunk, :] = rounded(gs[chunk, :].astype(F32) + gr[slot, chunk, :].astype(F32))

        def iterate(it, carry):
            grams(lax.rem(it, 2))
            fill_poly()
            for tile in range(half // 256):
                block = pl.ds(tile * 256, 256)
                x[:, block] = rounded(
                    NS_A * x[:, block].astype(F32) + jnp.dot(poly[...], x[:, block], preferred_element_type=F32)
                )
            return carry

        lax.fori_loop(0, NS_ITERS - 1, iterate, 0)
        grams((NS_ITERS - 1) % 2)

        @pl.when(p < WIDE)
        def _():
            mine = poly_rows(g, pl.multiple_of(f * rows, rows), rows)
            pa[...] = rounded(NS_A * x[my_rows, :].astype(F32) + jnp.dot(mine, x[...], preferred_element_type=F32))

        @pl.when(p >= WIDE)
        def _():
            fill_poly()
            for tile in range(half // 128):
                x_t[pl.ds(tile * 128, 128), :] = x[:, pl.ds(tile * 128, 128)].T
            block = x_t[my_high, :]
            pb[...] = rounded(NS_A * block.astype(F32) + jnp.dot(block, poly[...], preferred_element_type=F32))

    @pl.when(p < 2)
    def _():
        kt[...] = x[:, narrow:].T
        inverse_k = scale_of(jnp.sum(jnp.square(kt[...].astype(F32))))
        normal(kt, inverse_k)
        wide = x[:, :narrow].astype(F32)
        x[:, :narrow] = rounded(wide * scale_of(jnp.sum(wide * wide)))

        def narrow_step(it, carry):
            gram = rounded(contract(kt[...], kt[...], 1, 1))
            turn = rounded(NS_B * gram.astype(F32) + NS_C * jnp.dot(gram, gram, preferred_element_type=F32))
            kt[...] = rounded(NS_A * kt[...].astype(F32) + jnp.dot(turn, kt[...], preferred_element_type=F32))
            return carry

        lax.fori_loop(0, NS_ITERS, narrow_step, 0)

        def gram_of():
            for r in range(4):
                chunk = pl.ds(r * step, step)
                g[chunk, :] = rounded(contract(x[chunk, :narrow], x[:, :narrow], 1, 1))

        def square_step(it, carry):
            gram_of()
            fill_poly()
            x[:, :narrow] = rounded(
                NS_A * x[:, :narrow].astype(F32) + jnp.dot(poly[...], x[:, :narrow], preferred_element_type=F32)
            )
            return carry

        lax.fori_loop(0, NS_ITERS - 1, square_step, 0)
        gram_of()
        mine = poly_rows(g, pl.multiple_of(f * rows, rows), rows)
        square = rounded(
            NS_A * x[my_rows, :narrow].astype(F32) + jnp.dot(mine, x[:, :narrow], preferred_element_type=F32)
        )
        x[:, narrow:] = kt[...].T
        pa[:, :narrow] = square
        pa[:, narrow:] = x[my_rows, narrow:]

    spread(at, pa, pb, o_a, o_b, ag_l, ag_s, ag_r)()


def orthogonalize(s_a, s_b, rows, high, narrow):
    parts = lax.axis_size("fsdp")
    depth, half = s_a.shape
    dma = pltpu.SemaphoreType.DMA
    vm = pltpu.VMEM
    return pl.pallas_call(
        functools.partial(ortho_kernel, parts, rows, high, narrow),
        out_shape=(
            jax.ShapeDtypeStruct((WIDE, rows, half), BF16),
            jax.ShapeDtypeStruct((CLASSES - WIDE, high, depth), BF16),
        ),
        in_specs=[VMEM, VMEM],
        out_specs=(ANY, ANY),
        scratch_shapes=[
            vm((depth, half), BF16),
            vm((half, depth), BF16),
            vm((depth, depth), BF16),
            vm((2, depth, depth), BF16),
            vm((depth, depth), BF16),
            vm((depth, depth), BF16),
            vm((8, 128), F32),
            vm((8, 128), F32),
            vm((rows, half), BF16),
            vm((high, depth), BF16),
            vm((half - narrow, depth), BF16),
            dma((4,)), dma((2, 4)), dma, dma, dma, dma((7,)), dma((CLASSES,)),
        ],
        compiler_params=pltpu.CompilerParams(
            collective_id=2, has_side_effects=True, vmem_limit_bytes=62 << 20
        ),
        name="orthogonalize",
    )(s_a, s_b)


class Weights:
    def __init__(self, at, sources, homes, zs, s1, s2, sc, recv):
        self.at, self.sources, self.homes = at, sources, homes
        self.zs, self.s1, self.s2, self.sc, self.recv = zs, s1, s2, sc, recv
        self.sends = []

    def act(self, group, q, j, plane, send, target, what, first=False):
        recv = self.recv.at[group, q, j]
        home, source = self.homes[group], self.sources[group]
        rows = home.shape[-2] // (1 if group == 3 else self.at.parts)
        unit = -(-rows // (16 * CLASSES)) * 16
        last = rows - (CLASSES - 1) * unit

        def piece(count):
            def go():
                start = pl.multiple_of(q * unit, 16)
                if group == 3:
                    columns = home.shape[1] // self.at.parts
                    dst = home.at[pl.ds(start, count), pl.ds(pl.multiple_of(plane * columns, 128), columns)]
                    src = source.at[pl.ds(start, count)]
                elif group == 0:
                    dst = home.at[:, pl.ds(pl.multiple_of(plane * rows + start, 16), count)]
                    src = dst
                else:
                    dst = home.at[pl.ds(pl.multiple_of(plane * rows + start, 16), count)]
                    src = source.at[pl.ds(start, count)]
                getattr(remote(src if first else dst, dst, send, recv, target), what)()

            return go

        pl.when(q < CLASSES - 1)(piece(unit))
        pl.when(q == CLASSES - 1)(piece(last))

    def send(self, group, q, j, plane, sem, target, first=False):
        self.act(group, q, j, plane, sem, target, "start", first)
        self.sends.append((group, q, j, plane, sem, target, "wait_send", first))

    def arrived(self, group, q, j):
        at = self.at
        self.act(group, q, j, at.f ^ j, self.zs.at[group, j], at.peer(1), "wait_recv")

    def along(self, group):
        at = self.at
        for j in range(1, at.parts):
            self.send(group, at.p, j, at.f, self.zs.at[group, j], at.along(j), True)

    def first(self, group):
        at = self.at
        for j in range(1, at.parts):
            self.arrived(group, at.p, j)
            self.send(group, at.p, j, at.f ^ j, self.s1.at[group, j], at.peer(at.b1))
            self.send(group, at.p, j, at.f ^ j, self.s2.at[group, 0, j], at.peer(at.b2))
            self.send(group, at.p, j, at.f ^ j, self.sc.at[group, 0, j], at.peer(1))

    def second(self, group):
        at = self.at
        q = at.p ^ at.b1
        for j in range(1, at.parts):
            self.arrived(group, q, j)
            self.send(group, q, j, at.f ^ j, self.s2.at[group, 1, j], at.peer(at.b2))
            self.send(group, q, j, at.f ^ j, self.sc.at[group, 1, j], at.peer(1))

    def third(self, group):
        at = self.at
        for slot, bits in ((2, at.b2), (3, at.b1 ^ at.b2)):
            for j in range(1, at.parts):
                self.arrived(group, at.p ^ bits, j)
                self.send(group, at.p ^ bits, j, at.f ^ j, self.sc.at[group, slot, j], at.peer(1))

    def ready(self, group):
        at = self.at
        for bits in (1, 3, 5, 7):
            for j in range(1, at.parts):
                self.arrived(group, at.p ^ bits, j)

    def finish(self):
        for item in self.sends:
            self.act(*item)


def spread_even(at, own, out, local, ss, recv):
    p = at.p

    def copy_of(cls, slot, target, first=False):
        return remote(own if first else out.at[cls], out.at[cls], ss.at[slot], recv.at[cls], target)

    keep = pltpu.make_async_copy(own, out.at[p], local)
    sends = []

    def send(cls, slot, target, first=False):
        copy = copy_of(cls, slot, target, first)
        copy.start()
        sends.append(copy)

    def arrived(cls):
        copy_of(cls, 0, at.peer(1)).wait_recv()

    send(p, 0, at.peer(at.b1), True)
    send(p, 1, at.peer(at.b2), True)
    send(p, 2, at.peer(1), True)
    keep.start()

    def pass_on():
        arrived(p ^ at.b1)
        send(p ^ at.b1, 3, at.peer(at.b2))
        send(p ^ at.b1, 4, at.peer(1))
        arrived(p ^ at.b2)
        send(p ^ at.b2, 5, at.peer(1))
        arrived(p ^ at.b1 ^ at.b2)
        send(p ^ at.b1 ^ at.b2, 6, at.peer(1))

    def finish():
        for bits in (1, 3, 5, 7):
            arrived(p ^ bits)
        for copy in sends:
            copy.wait_send()
        keep.wait()

    return pass_on, finish


def step_kernel(
    x_ref, up_ref, gains_ref, cos_ref, low_ref, high_ref, bias_ref, wq, wk, wo, wv, wg_in, wu_in, wd_in,
    m_q, m_k, m_o, m_v, m_gate, m_up, m_down,
    out_ref, grad_ref, g_out, o_out, gain_out,
    w01, wg, wu, wd, probs, kv, rot, dkv, c_send, c4r, c2r, c1r, att, gate, lifted,
    xt_in, dy_in, dv_in, xf_all, xa_all, yf_all, yv_all, za_r, ma, mq, mk, gain_s, gain_r, sq, sq_r,
    local, zs, s1, s2, sc, recv, kvs, kvr, ds, dr,
    ls, xs, xr, ps, pr, ys, yr, as_, ar, vs, vr, hs, hr, ozs, ozr, msem, gs, gr, ag_l, ag_s, ag_r, ls_l, ls_r, lr_l, lr_r,
    gsem, rsem, qs, qr, ex_s, ex_r, fx_s, fx_r, og_l, og_s, og_r, free,
):
    at = Place()
    p, f, core, parts = at.p, at.f, at.core, at.parts
    width, tokens = x_ref.shape
    half = w01.shape[2]
    keys = half - width
    group = HEADS // KV_HEADS
    scale = 1.0 / math.sqrt(HEAD)
    rows = width // parts
    columns = 2 * half // parts
    tall = width // 2
    pair = at.peer(1)
    my_rows = pl.ds(pl.multiple_of(f * rows, 16), rows)

    weights = Weights(at, (None, wg_in, wu_in, wd_in), (w01, wg, wu, wd), zs, s1, s2, sc, recv)
    keep = [
        pltpu.make_async_copy(wg_in, wg.at[my_rows], local.at[0]),
        pltpu.make_async_copy(wu_in, wu.at[my_rows], local.at[1]),
        pltpu.make_async_copy(
            wd_in, wd.at[:, pl.ds(pl.multiple_of(f * columns, 128), columns)], local.at[2]
        ),
    ]

    def moment(what):
        for cls in range(CLASSES):
            @pl.when(p == cls)
            def _(cls=cls):
                side = cls % 2
                if cls < 2:
                    pairs = [((m_q, m_o)[cls], mq, 0), ((m_k, m_v)[cls], mk, 1)]
                elif cls < WIDE:
                    whole = m_gate if cls < 4 else m_up
                    pairs = [(whole.at[:, pl.ds(side * half, half)], ma, 0)]
                else:
                    pairs = [
                        (
                            m_down.at[pl.ds(side * tall + t * rows, rows)],
                            ma.at[:, pl.ds(t * columns, columns)],
                            t,
                        )
                        for t in range(2)
                    ]
                for src, dst, index in pairs:
                    getattr(pltpu.make_async_copy(src, dst, msem.at[index]), what)()

    w01[0, my_rows, :width] = wq[...]
    w01[0, my_rows, width:] = wk[...].T
    w01[1, my_rows, :width] = wo[...]
    w01[1, my_rows, width:] = wv[...].T
    at.barrier(bits=range(1, CLASSES))
    for index in range(4):
        weights.along(index)
    for copy in keep:
        copy.start()
    moment("start")

    residual = x_ref[...].astype(F32).T
    upstream = up_ref[...].astype(F32).T
    inverse_first = lax.rsqrt(jnp.mean(residual * residual, axis=-1, keepdims=True) + EPS)
    normed_first = (residual * inverse_first * gains_ref[0:1, :]).astype(BF16)
    xt_in[0] = normed_first.T
    xt_in[3] = up_ref[...]

    weights.first(0)
    weights.second(0)
    weights.first(1)
    weights.third(0)
    weights.ready(0)

    def turn(value, sign):
        tiles = []
        for tile in range(half // 128):
            part = value[:, tile * 128 : (tile + 1) * 128]
            swapped = pltpu.roll(part, HEAD // 2, 1) * low_ref[...] + pltpu.roll(part, 128 - HEAD // 2, 1) * high_ref[...]
            tiles.append(part * cos_ref[...] + swapped if sign > 0 else part * cos_ref[...] - swapped)
        return tiles

    qk = jnp.dot(normed_first, w01[0], preferred_element_type=F32)
    for tile, value in enumerate(turn(qk, 1)):
        rot[:, tile * 128 : (tile + 1) * 128] = value.astype(BF16)
    values = jnp.dot(normed_first, w01[1, :, width:], preferred_element_type=F32).astype(BF16)
    kv[p, :, :keys] = rot[:, width:]
    kv[p, :, keys:] = values

    def block(q, slot, target):
        return remote(kv.at[q], kv.at[q], kvs.at[slot], kvr.at[q], target)

    sent = [block(p, 0, at.peer(at.b1)), block(p, 1, at.peer(at.b2)), block(p, 2, at.peer(1))]
    for copy in sent:
        copy.start()

    def pass_keys(q, slots):
        block(q, 0, at.peer(1)).wait_recv()
        for slot, target in slots:
            copy = block(q, slot, target)
            copy.start()
            sent.append(copy)

    weights.second(1)
    pass_keys(p ^ at.b1, [(3, at.peer(at.b2)), (4, at.peer(1))])
    pass_keys(p ^ at.b2, [(5, at.peer(1))])
    weights.first(2)
    pass_keys(p ^ at.b1 ^ at.b2, [(6, at.peer(1))])
    for bits in (1, 3, 5, 7):
        pass_keys(p ^ bits, [])
    weights.third(1)

    def keys_of(g):
        return kv[:, :, g * HEAD : (g + 1) * HEAD].reshape(CLASSES * tokens, HEAD)

    def values_of(g):
        return kv[:, :, keys + g * HEAD : keys + (g + 1) * HEAD].reshape(CLASSES * tokens, HEAD)

    def heads_of(ref, g):
        return jnp.concatenate([ref[:, h * HEAD : (h + 1) * HEAD] for h in range(g * group, (g + 1) * group)], axis=0)

    def attend(g):
        scores = contract(keys_of(g), heads_of(rot, g), 1, 1) * scale
        bias = bias_ref[...].astype(F32)
        scores = scores + jnp.concatenate([bias] * group, axis=1)
        top = jnp.max(scores, axis=0, keepdims=True)
        expo = jnp.exp(scores - top)
        total = jnp.sum(expo, axis=0, keepdims=True)
        chance = expo * (1.0 / total)
        probs[g] = chance
        mixed = contract(values_of(g), chance.astype(BF16), 0, 0)
        turned = mixed.T.astype(BF16)
        for h in range(group):
            at_lane = (g * group + h) * HEAD
            att[:, at_lane : at_lane + HEAD] = turned[h * tokens : (h + 1) * tokens]

    attend(0)
    attend(1)
    weights.second(2)
    attend(2)
    weights.first(3)
    attend(3)
    weights.third(2)
    attend(4)
    for copy in keep:
        copy.wait()
    weights.ready(1)

    xt_in[1] = att[...].T
    middle = residual + jnp.dot(att[...], w01[1, :, :width], preferred_element_type=F32)
    inverse_second = lax.rsqrt(jnp.mean(middle * middle, axis=-1, keepdims=True) + EPS)
    normed_second = (middle * inverse_second * gains_ref[1:2, :]).astype(BF16)
    xt_in[2] = normed_second.T
    weights.second(3)
    gate[...] = jnp.dot(normed_second, wg[...], preferred_element_type=F32)
    weights.third(3)

    def tokens_of(q):
        return pl.ds(pl.multiple_of(q * tokens, tokens), tokens)

    def kind_of(q):
        return jnp.where(q < 2, 0, jnp.where(q < WIDE, 2, 3))

    own_x = pltpu.make_async_copy(xt_in.at[kind_of(p)], xf_all.at[:, tokens_of(p)], ls.at[0])

    def x_move(bits):
        q = p ^ bits
        return remote(xt_in.at[kind_of(q)], xf_all.at[:, tokens_of(p)], xs.at[bits], xr.at[p], at.peer(bits))

    def a_move():
        return remote(xt_in.at[1], xa_all.at[:, tokens_of(p)], as_, ar.at[p], at.peer(p ^ 1))

    def own_a():
        return pltpu.make_async_copy(xt_in.at[1], xa_all.at[:, tokens_of(p)], ls.at[1])

    def y_move(bits):
        q = p ^ bits
        return remote(dy_in.at[q], yf_all.at[tokens_of(p)], ys.at[bits], yr.at[p], at.peer(bits))

    def own_y():
        return pltpu.make_async_copy(dy_in.at[p], yf_all.at[tokens_of(p)], ls.at[2])

    def v_move():
        return remote(dv_in, yv_all.at[tokens_of(p)], vs, vr.at[p], at.peer(p ^ 1))

    def own_v():
        return pltpu.make_async_copy(dv_in, yv_all.at[tokens_of(p)], ls.at[3])

    own_x.start()
    for bits in (2, 4, 6):
        x_move(bits).start()
    pl.when(p != 1)(lambda: a_move().start())
    pl.when(p == 1)(lambda: own_a().start())

    def give_y(bits, low, high):
        q = p ^ bits

        @pl.when((q >= low) & (q < high))
        def _():
            y_move(bits).start()

    weights.ready(2)
    for side in range(2):
        lifted[side * tokens : (side + 1) * tokens] = jnp.dot(
            normed_second, wu[:, side * half : (side + 1) * half], preferred_element_type=F32
        )

    def lift():
        return jnp.concatenate([lifted[:tokens], lifted[tokens:]], axis=1)

    hidden = (gate[...] * jax.nn.sigmoid(gate[...]) * lift()).astype(BF16)
    dy_in[6] = hidden[:, :half]
    dy_in[7] = hidden[:, half:]
    for bits in range(1, CLASSES):
        give_y(bits, WIDE, CLASSES)
    weights.ready(3)

    grad_hidden = jnp.dot(upstream.astype(BF16), wd[...], preferred_element_type=F32)
    sigma = jax.nn.sigmoid(gate[...])
    grad_gate = (grad_hidden * lift() * sigma * (1.0 + gate[...] * (1.0 - sigma))).astype(BF16)
    grad_lifted = (grad_hidden * gate[...] * sigma).astype(BF16)
    for side in range(2):
        lanes = slice(side * half, (side + 1) * half)
        dy_in[2 + side] = grad_gate[:, lanes]
        dy_in[4 + side] = grad_lifted[:, lanes]
    for bits in (1, at.b1, at.b1 ^ 1, at.b2, at.b2 ^ 1):
        give_y(bits, 2, WIDE)

    out_ref[...] = (middle + contract(hidden, wd[...], 1, 1)).T.astype(BF16)
    weights.finish()
    grad_normed = contract(grad_gate, wg[...], 1, 1) + contract(grad_lifted, wu[...], 1, 1)
    pl.semaphore_signal(free.at[0], inc=1, device_id=pair, device_id_type=MESH)

    def norm_back(value, inverse, gain, incoming):
        scaled = incoming * gain
        mean = jnp.mean(scaled * value, axis=-1, keepdims=True)
        through = inverse * scaled - value * (inverse * inverse * inverse) * mean
        return through, jnp.sum(incoming * value * inverse, axis=0, keepdims=True)

    through, gain_second = norm_back(middle, inverse_second, gains_ref[1:2, :], grad_normed)
    gain_s[0] = jnp.zeros(gain_s.shape[1:], F32)
    gain_s[0, 1:2, :] = gain_second
    grad_middle = upstream + through
    grad_branch = grad_middle.astype(BF16)
    dy_in[1, :, :width] = grad_branch
    dy_in[1, :, width:] = jnp.zeros((tokens, keys), BF16)
    att[...] = contract(grad_branch, w01[1, :, :width], 1, 1).astype(BF16)

    for bits in (1, at.b1, at.b1 ^ 1, at.b2, at.b2 ^ 1):
        give_y(bits, 1, 2)

    own = lifted.at[pl.ds(0, rows)]

    def swap(slot, target):
        return remote(gain_s.at[slot], gain_r.at[slot], gs.at[slot], gr.at[slot], target)

    def order(i):
        return lax.rem(f + 1 + i, parts)

    def room(r):
        return wd.at[pl.ds(pl.multiple_of(r * rows, 16), rows), pl.ds(half, half)]

    def line(r, source):
        return remote(room(r), za_r.at[(r ^ source) - 1], ozs.at[r], ozr.at[source], (at.c, r))

    def arrival(j):
        return remote(room(f), za_r.at[j - 1], ozs.at[f], ozr.at[f ^ j], at.along(j))

    middle_token = CLASSES // 2 * tokens

    def sides_of():
        return [
            remote(
                yf_all.at[pl.ds(side * middle_token, middle_token)],
                wu.at[pl.ds(0, middle_token), pl.ds(side * half, half)],
                hs.at[side], hr.at[side], pair,
            )
            for side in range(2)
        ]

    def produce(r, put):
        at_rows = pl.ds(pl.multiple_of(r * rows, 16), rows)
        every = slice(0, half)

        @pl.when(p == 1)
        def _():
            value = jnp.dot(xf_all[at_rows, :], yv_all[...], preferred_element_type=F32)
            put(slice(0, width), jnp.dot(xa_all[at_rows, :], yf_all[:, pl.ds(0, width)], preferred_element_type=F32))
            put(slice(width, half), value[:, :keys])

        @pl.when((p != 1) & (p < WIDE))
        def _():
            put(every, jnp.dot(xf_all[at_rows, :], yf_all[...], preferred_element_type=F32))

        @pl.when(p >= WIDE)
        def _():
            side, start = lax.div(r * columns, half), pl.multiple_of(lax.rem(r * columns, half), 128)
            for t in range(2):
                part_rows = pl.ds(pl.multiple_of((p - WIDE) * tall + t * rows, 16), rows)
                lanes = slice(t * columns, (t + 1) * columns)

                @pl.when(side == core)
                def _():
                    put(
                        lanes,
                        jnp.dot(xf_all[part_rows, :], yf_all[:, pl.ds(start, columns)], preferred_element_type=F32),
                    )

                @pl.when(side != core)
                def _():
                    put(
                        lanes,
                        jnp.dot(
                            xf_all[part_rows, pl.ds(0, middle_token)],
                            wu[pl.ds(0, middle_token), pl.ds(start, columns)],
                            preferred_element_type=F32,
                        )
                        + jnp.dot(
                            xf_all[part_rows, pl.ds(middle_token, middle_token)],
                            wu[pl.ds(0, middle_token), pl.ds(pl.multiple_of(half + start, 128), columns)],
                            preferred_element_type=F32,
                        ),
                    )

    def gradients():
        for bits in range(1, CLASSES):
            arrived_y(p ^ bits)

        @pl.when(p >= WIDE)
        def _():
            pl.semaphore_wait(free.at[0], 1)
            for copy in sides_of():
                copy.start()
            for copy in sides_of():
                copy.wait()

        @pl.when(p < WIDE)
        def _():
            pl.semaphore_wait(free.at[0], 1)

        def step_of(i, carry):
            r = order(i)

            def put(lanes, value):
                own[:, lanes] = value
                room(r)[:, lanes] = value.astype(BF16)

            produce(r, put)

            @pl.when(i < parts - 1)
            def _():
                line(r, f).start()

            return carry

        lax.fori_loop(0, parts, step_of, 0)

    def arrived_y(q):
        remote(dy_in.at[0], yf_all.at[tokens_of(q)], ys.at[1], yr.at[q], pair).wait_recv()

    def arrived_x(q):
        remote(xt_in.at[0], xf_all.at[:, tokens_of(q)], xs.at[2], xr.at[q], pair).wait_recv()

    def x_pair(bits):
        q = p ^ bits
        return remote(xf_all.at[:, tokens_of(q)], xf_all.at[:, tokens_of(q)], ps.at[bits], pr.at[q], pair)

    def attend_back(g):
        chance = probs[g]
        out_grad = heads_of(att, g)
        query = heads_of(rot, g)
        grad_probs = contract(values_of(g), out_grad, 1, 1)
        delta = jnp.sum(grad_probs * chance, axis=0, keepdims=True)
        grad_scores = (chance * (grad_probs - delta)).astype(BF16)
        grad_values = jnp.dot(chance.astype(BF16), out_grad, preferred_element_type=F32)
        grad_keys = jnp.dot(grad_scores, query, preferred_element_type=F32) * scale
        dkv[:, :, g * HEAD : (g + 1) * HEAD] = grad_keys.reshape(CLASSES, tokens, HEAD)
        dkv[:, :, keys + g * HEAD : keys + (g + 1) * HEAD] = grad_values.reshape(CLASSES, tokens, HEAD)
        turned = contract(keys_of(g), grad_scores, 0, 0).T * scale
        for h in range(group):
            at_lane = (g * group + h) * HEAD
            gate[:, at_lane : at_lane + HEAD] = turned[h * tokens : (h + 1) * tokens]

    for g in range(KV_HEADS):
        attend_back(g)

    def halve(bit, rest, sbuf, rbuf, index, between=None):
        for i, bits in enumerate(rest):
            sbuf[i // 2, :, pl.ds(i % 2 * 2 * keys, 2 * keys)] = dkv[p ^ bit ^ bits].astype(BF16)
        copy = remote(sbuf, rbuf, ds.at[index], dr.at[index], at.peer(bit))
        copy.start()
        if between is not None:
            between()
        copy.wait()
        for i, bits in enumerate(rest):
            dkv[p ^ bits] = dkv[p ^ bits] + rbuf[i // 2, :, pl.ds(i % 2 * 2 * keys, 2 * keys)].astype(F32)

    def diagonal():
        for bits in (at.b1 ^ at.b2, at.b1 ^ at.b2 ^ 1):
            give_y(bits, 1, WIDE)

    halve(1, (0, 2, 4, 6), c_send, c4r, 0)
    halve(at.b1, (0, at.b2), c4r.at[pl.ds(0, 1)], c2r, 1)
    halve(at.b2, (0,), c4r.at[pl.ds(1, 1), :, pl.ds(0, 2 * keys)], c1r, 2, diagonal)

    gate[:, width:half] = dkv[p, :, :keys]
    for tile, value in enumerate(turn(gate[:, :half], -1)):
        dy_in[0, :, tile * 128 : (tile + 1) * 128] = value.astype(BF16)
    dv_in[...] = jnp.zeros(dv_in.shape, BF16)
    dv_in[:, :keys] = dkv[p, :, keys:].astype(BF16)
    for bits in range(1, CLASSES):
        give_y(bits, 0, 1)
    pl.when(p != 1)(lambda: v_move().start())
    pl.when(p == 1)(lambda: own_v().start())
    own_y().start()

    own_x.wait()
    for bits in (2, 4, 6):
        arrived_x(p ^ bits)
    for bits in (0, 2, 4, 6):
        x_pair(bits).start()

    grad_normed = contract(dy_in[0], w01[0], 1, 1)
    grad_normed = grad_normed + contract(dv_in[:, :keys], w01[1, :, width:], 1, 1)
    through, gain_first = norm_back(residual, inverse_first, gains_ref[0:1, :], grad_normed)
    gain_s[0, 0:1, :] = gain_first
    swaps = [swap(0, pair)]
    swaps[0].start()
    grad_ref[...] = (grad_middle + through).T
    own_y().wait()
    for bits in (0, 2, 4, 6):
        x_pair(bits).wait_send()
        remote(
            xf_all.at[:, tokens_of(p ^ bits ^ 1)], xf_all.at[:, tokens_of(p ^ bits ^ 1)],
            ps.at[bits], pr.at[p ^ bits ^ 1], pair,
        ).wait_recv()

    @pl.when(p == 1)
    def _():
        own_a().wait()
        own_v().wait()
        for q in range(CLASSES):
            if q != 1:
                remote(xt_in.at[1], xa_all.at[:, tokens_of(q)], as_, ar.at[q], pair).wait_recv()
                remote(dv_in, yv_all.at[tokens_of(q)], vs, vr.at[q], pair).wait_recv()

    gradients()
    swaps[0].wait()
    gain_s[1] = gain_s[0] + gain_r[0]
    swaps.append(swap(1, at.peer(2)))
    swaps[1].start()
    for bits in range(1, CLASSES):
        y_move(bits).wait_send()
    for bits in (2, 4, 6):
        x_move(bits).wait_send()

    @pl.when(p != 1)
    def _():
        a_move().wait_send()
        v_move().wait_send()

    swaps[1].wait()
    gain_s[2] = gain_s[1] + gain_r[1]
    swaps.append(swap(2, at.peer(4)))
    swaps[2].start()

    moment("wait")

    @pl.when(p < 2)
    def _():
        ma[:, :width] = mq[...]
        ma[:, width:] = mk[...].T

    sall = wd.at[:, pl.ds(0, half)]
    ga, pa = (w01.at[1, pl.ds((parts - 1 - i) * rows, rows)] for i in range(2))
    total = own[...]
    for j in range(1, parts):
        arrival(j).wait_recv()
        total = total + za_r[j - 1].astype(F32)
    ga[...] = total.astype(BF16)
    sall[my_rows, :] = (MOMENTUM * ma[...] + total).astype(BF16)

    def shard(index):
        return sall.at[pl.ds(pl.multiple_of(index * rows, 16), rows)]

    def rightward(index):
        return remote(shard(index), shard(index), ls_r.at[index], lr_r.at[index], (at.c, lax.rem(f + 1, parts)))

    def leftward(index):
        return remote(shard(index), shard(index), ls_l.at[index], lr_l.at[index], (at.c, lax.rem(f + parts - 1, parts)))

    def can_right():
        return f < parts - 1

    def can_left():
        return f > 0

    pl.when(can_right())(lambda: rightward(f).start())
    pl.when(can_left())(lambda: leftward(f).start())

    pass_on, finish = spread_even(at, ga, g_out, ag_l, ag_s, ag_r)
    swaps[2].wait()
    gain_s[3] = gain_s[2] + gain_r[2]
    line_gain = [
        remote(gain_s.at[3], gain_r.at[3 + j], gs.at[3 + j], gr.at[3 + j], at.along(j)) for j in range(1, parts)
    ]
    for copy in line_gain:
        copy.start()

    for hop in range(1, parts):
        @pl.when(f - hop >= 0)
        def _(hop=hop):
            rightward(f - hop).wait_recv()
            pl.when(can_right())(lambda: rightward(f - hop).start())

        @pl.when(f + hop < parts)
        def _(hop=hop):
            leftward(f + hop).wait_recv()
            pl.when(can_left())(lambda: leftward(f + hop).start())

    pass_on()

    for j in range(1, parts):
        line(f ^ j, f).wait_send()
    pl.when(can_right())(lambda: rightward(f).wait_send())
    pl.when(can_left())(lambda: leftward(f).wait_send())
    for hop in range(1, parts):
        pl.when((f - hop >= 0) & can_right())(lambda hop=hop: rightward(f - hop).wait_send())
        pl.when((f + hop < parts) & can_left())(lambda hop=hop: leftward(f + hop).wait_send())
    pl.semaphore_signal(free.at[1], inc=1, device_id=pair, device_id_type=MESH)
    pl.semaphore_wait(free.at[1], 1)

    x = w01.at[0]
    wide_gram = 1024
    gram_s, g = wg.at[:, pl.ds(0, wide_gram)], wg.at[:, pl.ds(wide_gram, wide_gram)]
    poly, xf = wd.at[:, pl.ds(0, wide_gram)], wd.at[:, pl.ds(half, columns)]
    step = width // 4

    def gram_r(slot):
        return wu.at[:, pl.ds(slot * wide_gram, wide_gram)]

    def scale_of(total):
        return 1.0 / (jnp.sqrt(total) + 1e-07)

    def normal(ref, inverse):
        ref[...] = rounded(ref[...].astype(F32) * inverse)

    def exchange(slot, r):
        part = pl.ds(r * step, step)
        return remote(gram_s.at[part], gram_r(slot).at[part], gsem.at[r], rsem.at[slot, r], pair)

    def poly_of(start, count):
        part = g[pl.ds(start, count), pl.ds(0, width)]
        square = jnp.dot(part, g[:, pl.ds(0, width)], preferred_element_type=F32)
        return rounded(NS_B * part.astype(F32) + NS_C * square)

    def fill_poly():
        for r in range(4):
            poly[pl.ds(r * step, step), pl.ds(0, width)] = poly_of(r * step, step)

    near = parts // 2
    mine_at = core * near
    last_core = lax.div(f, near)
    f_lanes = pl.ds(pl.multiple_of(lax.rem(f, near) * columns, 128), columns)

    kt = wd.at[pl.ds(0, keys), pl.ds(half + 256, wide_gram)]

    def xo(i):
        return w01.at[1, pl.ds(i * rows, rows)]

    def give():
        return [
            remote(
                sall.at[pl.ds(pl.multiple_of(((1 - core) * near + i) * rows, 16), rows)],
                xo(i), ex_s.at[i], ex_r.at[i], pair,
            )
            for i in range(near)
        ]

    def give_last():
        return remote(x.at[:, f_lanes], xf, fx_s, fx_r, pair)

    @pl.when(p >= 2)
    def _():
        @pl.when(p < WIDE)
        def _():
            x[...] = sall[...]

        @pl.when(p >= WIDE)
        def _():
            copies = give()
            for copy in copies:
                copy.start()
            for i in range(near):
                part = sall[pl.ds(pl.multiple_of((mine_at + i) * rows, 16), rows), :]
                for t in range(2):
                    x[pl.ds(pl.multiple_of(core * tall + t * rows, 16), rows), pl.ds(i * columns, columns)] = part[
                        :, t * columns : (t + 1) * columns
                    ]
            for i, copy in enumerate(copies):
                copy.wait()
                part = xo(i)
                for t in range(2):
                    x[pl.ds(pl.multiple_of((1 - core) * tall + t * rows, 16), rows), pl.ds(i * columns, columns)] = part[
                        :, pl.ds(t * columns, columns)
                    ]

        wide = x[...].astype(F32)
        sq[...] = jnp.broadcast_to(jnp.sum(wide * wide), sq.shape)
        copy = remote(sq, sq_r, qs, qr, pair)
        copy.start()
        copy.wait()
        normal(x, scale_of(sq[...] + sq_r[...])[:1, :1])

        def grams(slot):
            for r in range(4):
                gram_s[pl.ds(r * step, step), pl.ds(0, width)] = rounded(
                    contract(x[pl.ds(r * step, step), :], x[...], 1, 1)
                )
                exchange(slot, r).start()
            for r in range(4):
                part = pl.ds(r * step, step)
                exchange(slot, r).wait()
                g[part, pl.ds(0, width)] = rounded(
                    gram_s[part, pl.ds(0, width)].astype(F32) + gram_r(slot)[part, pl.ds(0, width)].astype(F32)
                )

        def iterate(slot):
            grams(slot)
            fill_poly()
            for tile in range(half // 256):
                part = pl.ds(tile * 256, 256)
                x[:, part] = rounded(
                    NS_A * x[:, part].astype(F32) + jnp.dot(poly[:, pl.ds(0, width)], x[:, part], preferred_element_type=F32)
                )

        def iterate_twice(it, carry):
            iterate(0)
            iterate(1)
            return carry

        lax.fori_loop(0, (NS_ITERS - 1) // 2, iterate_twice, 0)

        @pl.when((p >= WIDE) & (core == last_core))
        def _():
            give_last().start()
            xf[...] = x[:, f_lanes]

        grams(0)

        @pl.when(p < WIDE)
        def _():
            part = poly_of(pl.multiple_of(f * rows, 16), rows)
            pa[...] = rounded(NS_A * x[my_rows, :].astype(F32) + jnp.dot(part, x[...], preferred_element_type=F32))

        @pl.when(p >= WIDE)
        def _():
            pl.when(core == last_core)(lambda: give_last().wait_send())
            pl.when(core != last_core)(lambda: give_last().wait_recv())
            for t in range(2):
                top = pl.multiple_of(core * tall + t * rows, 16)
                part = poly_of(top, rows)
                pa[:, t * columns : (t + 1) * columns] = rounded(
                    NS_A * xf[pl.ds(top, rows), :].astype(F32) + jnp.dot(part, xf[...], preferred_element_type=F32)
                )

    @pl.when(p < 2)
    def _():
        x[...] = sall[...]
        kt[:, pl.ds(0, width)] = x[:, pl.ds(width, keys)].T
        turned = kt[:, pl.ds(0, width)].astype(F32)
        kt[:, pl.ds(0, width)] = rounded(turned * scale_of(jnp.sum(turned * turned)))
        wide = x[:, pl.ds(0, width)].astype(F32)
        x[:, pl.ds(0, width)] = rounded(wide * scale_of(jnp.sum(wide * wide)))

        def narrow_step(it, carry):
            now = kt[:, pl.ds(0, width)]
            gram = rounded(contract(now, now, 1, 1))
            turned = rounded(NS_B * gram.astype(F32) + NS_C * jnp.dot(gram, gram, preferred_element_type=F32))
            kt[:, pl.ds(0, width)] = rounded(
                NS_A * now.astype(F32) + jnp.dot(turned, now, preferred_element_type=F32)
            )
            return carry

        lax.fori_loop(0, NS_ITERS, narrow_step, 0)

        def gram_of():
            for r in range(4):
                part = pl.ds(r * step, step)
                g[part, pl.ds(0, width)] = rounded(contract(x[part, pl.ds(0, width)], x[:, pl.ds(0, width)], 1, 1))

        def square_step(it, carry):
            gram_of()
            fill_poly()
            x[:, pl.ds(0, width)] = rounded(
                NS_A * x[:, pl.ds(0, width)].astype(F32) + jnp.dot(poly[:, pl.ds(0, width)], x[:, pl.ds(0, width)], preferred_element_type=F32)
            )
            return carry

        lax.fori_loop(0, NS_ITERS - 1, square_step, 0)
        gram_of()
        part = poly_of(pl.multiple_of(f * rows, 16), rows)
        square = rounded(
            NS_A * x[my_rows, pl.ds(0, width)].astype(F32) + jnp.dot(part, x[:, pl.ds(0, width)], preferred_element_type=F32)
        )
        x[:, pl.ds(width, keys)] = kt[:, pl.ds(0, width)].T
        pa[:, :width] = square
        pa[:, width:] = x[my_rows, pl.ds(width, keys)]

    out_on, out_finish = spread_even(at, pa, o_out, og_l, og_s, og_r)
    total = gain_s[3]
    for j in range(1, parts):
        line_gain[j - 1].wait()
        total = total + gain_r[3 + j]
    gain_out[...] = total
    finish()
    out_on()
    for copy in sent:
        copy.wait_send()
    out_finish()


def step_pass(x, up, gains, tables, bias, shards, moments):
    parts = lax.axis_size("fsdp")
    width, tokens = x.shape
    half = shards[4].shape[1] // 2
    rows = width // parts
    keys = half - width
    near = parts // 2
    dma = pltpu.SemaphoreType.DMA
    vm = pltpu.VMEM
    group = HEADS // KV_HEADS
    two = 2 * keys
    n_gain = 3 + parts
    return pl.pallas_call(
        step_kernel,
        out_shape=(
            jax.ShapeDtypeStruct((width, tokens), BF16),
            jax.ShapeDtypeStruct((width, tokens), F32),
            jax.ShapeDtypeStruct((CLASSES, rows, half), BF16),
            jax.ShapeDtypeStruct((CLASSES, rows, half), BF16),
            jax.ShapeDtypeStruct((8, width), F32),
        ),
        in_specs=[VMEM] * 11 + [ANY] * 10,
        out_specs=(VMEM, VMEM, ANY, ANY, VMEM),
        scratch_shapes=[
            vm((2, width, half), BF16),
            vm((width, 2 * half), BF16),
            vm((width, 2 * half), BF16),
            vm((width, 2 * half), BF16),
            vm((KV_HEADS, CLASSES * tokens, group * tokens), F32),
            vm((CLASSES, tokens, two), BF16),
            vm((tokens, half), BF16),
            vm((CLASSES, tokens, two), F32),
            vm((2, tokens, 2 * two), BF16),
            vm((2, tokens, 2 * two), BF16),
            vm((1, tokens, 2 * two), BF16),
            vm((1, tokens, two), BF16),
            vm((tokens, width), BF16),
            vm((tokens, 2 * half), F32),
            vm((2 * tokens, half), F32),
            vm((4, width, tokens), BF16),
            vm((CLASSES, tokens, half), BF16),
            vm((tokens, -(-keys // 128) * 128), BF16),
            vm((width, CLASSES * tokens), BF16),
            vm((width, CLASSES * tokens), BF16),
            vm((CLASSES * tokens, half), BF16),
            vm((CLASSES * tokens, -(-keys // 128) * 128), BF16),
            vm((parts - 1, rows, half), BF16),
            vm((rows, half), F32),
            vm((rows, width), F32),
            vm((keys, rows), F32),
            vm((4, 8, width), F32),
            vm((n_gain, 8, width), F32),
            vm((8, 128), F32),
            vm((8, 128), F32),
            dma((3,)), dma((4, parts)), dma((4, parts)), dma((4, 2, parts)), dma((4, 4, parts)),
            dma((4, CLASSES, parts)), dma((7,)), dma((CLASSES,)), dma((3,)), dma((3,)),
            dma((4,)), dma((CLASSES,)), dma((CLASSES,)), dma((CLASSES,)), dma((CLASSES,)),
            dma((CLASSES,)), dma((CLASSES,)), dma, dma((CLASSES,)), dma, dma((CLASSES,)),
            dma((2,)), dma((2,)), dma((parts,)), dma((parts,)),
            dma((2,)), dma((n_gain,)), dma((n_gain,)),
            dma, dma((7,)), dma((CLASSES,)),
            dma((parts,)), dma((parts,)), dma((parts,)), dma((parts,)),
            dma((4,)), dma((2, 4)), dma, dma,
            dma((near,)), dma((near,)), dma, dma,
            dma, dma((7,)), dma((CLASSES,)), pltpu.SemaphoreType.REGULAR((2,)),
        ],
        compiler_params=pltpu.CompilerParams(
            collective_id=3, has_side_effects=True, vmem_limit_bytes=63 << 20
        ),
        name="step_pass",
    )(x, up, gains, *tables, bias, *shards, *moments)


def settle_wide(factors, *refs):
    gs, os = refs[0], refs[1]
    ms, ws, outs = refs[2:6], refs[6:10], refs[10:]
    width = ms[0].shape[1]
    half = gs.shape[2]

    def one(index, g, o, lanes):
        grad, moment, weight = (outs[3 * index + i] for i in range(3))
        value = g.astype(F32)
        grad[:, lanes] = value
        moment[:, lanes] = MOMENTUM * ms[index][:, lanes] + value
        weight[:, lanes] = ws[index][:, lanes].astype(F32) + factors[index] * o.astype(F32)

    for index in range(2):
        one(index, gs[index, :, :width], os[index, :, :width], slice(0, width))
    for index in range(2):
        for side in range(2):
            cls = 2 + 2 * index + side
            one(2 + index, gs[cls], os[cls], slice(side * half, (side + 1) * half))


def settle_turned(factors, g_tall, o_tall, g_pair, o_pair, *refs):
    ms, ws, outs = refs[0:3], refs[3:6], refs[6:]
    keys = ms[1].shape[0]

    def one(index, g, o):
        grad, moment, weight = (outs[3 * index + i] for i in range(3))
        grad[...] = g
        moment[...] = MOMENTUM * ms[index][...] + g
        weight[...] = ws[index][...].astype(F32) + factors[index] * o

    one(0, g_tall[0].astype(F32), o_tall[0].astype(F32))

    @pl.when(pl.program_id(0) == 0)
    def _():
        for index in range(2):
            start = g_pair.shape[2] - keys
            one(1 + index, g_pair[index, :, start:].astype(F32).T, o_pair[index, :, start:].astype(F32).T)


def settle(g, o, moments, shards, factors):
    m_q, m_k, m_o, m_v, m_gate, m_up, m_down = moments
    w_q, w_k, w_o, w_v, w_gate, w_up, w_down = shards
    f_q, f_k, f_v, f_o, f_gate, f_up, f_down = factors
    _, rows, half = g.shape
    width, columns = m_down.shape
    block = 48 if rows % 48 == 0 else rows
    piece = pl.BlockSpec((WIDE, block, half), lambda i: (0, i, 0))

    def row_block(array):
        return pl.BlockSpec((block, array.shape[1]), lambda i: (i, 0))

    def result(arrays):
        return tuple(jax.ShapeDtypeStruct(array.shape, F32) for array in arrays for _ in range(3))

    wide = (m_q, m_o, m_gate, m_up)
    first = pl.pallas_call(
        functools.partial(settle_wide, (f_q, f_o, f_gate, f_up)),
        grid=(rows // block,),
        out_shape=result(wide),
        in_specs=[piece, piece] + [row_block(array) for array in wide] * 2,
        out_specs=tuple(row_block(array) for array in wide for _ in range(3)),
        compiler_params=pltpu.CompilerParams(vmem_limit_bytes=48 << 20),
        name="settle_wide",
    )(g, o, *wide, w_q, w_o, w_gate, w_up)

    turned = (m_down, m_k, m_v)
    halves = half // columns
    tile = pl.BlockSpec((1, rows, columns), lambda i: (WIDE + i // halves, 0, i % halves))
    both = pl.BlockSpec((2, rows, half), lambda i: (0, 0, 0))
    specs = [pl.BlockSpec((rows, columns), lambda i: (i, 0))] + [
        pl.BlockSpec(array.shape, lambda i: (0, 0)) for array in turned[1:]
    ]
    second = pl.pallas_call(
        functools.partial(settle_turned, (f_down, f_k, f_v)),
        grid=(width // rows,),
        out_shape=result(turned),
        in_specs=[tile, tile, both, both] + specs * 2,
        out_specs=tuple(spec for spec in specs for _ in range(3)),
        compiler_params=pltpu.CompilerParams(vmem_limit_bytes=48 << 20),
        name="settle_turned",
    )(g, o, g, o, *turned, w_down, w_k, w_v)
    q, out, gate, up = (first[3 * i : 3 * i + 3] for i in range(4))
    down, k, v = (tuple(item.T for item in second[3 * i : 3 * i + 3]) for i in range(3))
    return list(zip(q, k, v, out, gate, up, down))


def rotary_tables(positions, width):
    half = width // 2
    frequency = THETA ** (-(jnp.arange(half, dtype=jnp.float32) * 2.0 / width))
    angle = positions.astype(jnp.float32)[:, None] * frequency[None, :]
    return (jnp.cos(angle)[:, None, :], jnp.sin(angle)[:, None, :])


def rotate(value, cosine, sine):
    half = value.shape[-1] // 2
    first = value[..., :half]
    second = value[..., half:]
    return jnp.concatenate(
        [first * cosine - second * sine, second * cosine + first * sine], axis=-1
    )


def unrotate(incoming, cosine, sine):
    half = incoming.shape[-1] // 2
    upper = incoming[..., :half]
    lower = incoming[..., half:]
    return jnp.concatenate([upper * cosine + lower * sine, lower * cosine - upper * sine], axis=-1)


def norm_forward(residual, gain):
    inverse = lax.rsqrt(jnp.mean(residual * residual, axis=-1, keepdims=True) + EPS)
    return ((residual * inverse * gain).astype(jnp.bfloat16), inverse)


def norm_backward(residual, inverse, gain, incoming):
    scaled = incoming * gain
    through = inverse * scaled - residual * inverse**3 * jnp.mean(
        scaled * residual, axis=-1, keepdims=True
    )
    return (through, jnp.sum(incoming * residual * inverse, axis=0))


def padded(array, axis, parts, count, full):
    if count == full:
        return array
    shape = array.shape
    split = array.reshape(shape[:axis] + (parts, count) + shape[axis + 1 :])
    pads = [(0, 0)] * split.ndim
    pads[axis + 1] = (0, full - count)
    return jnp.pad(split, pads).reshape(shape[:axis] + (parts * full,) + shape[axis + 1 :])


def trimmed(array, axis, parts, count, full):
    if count == full:
        return array
    shape = array.shape
    split = array.reshape(shape[:axis] + (parts, full) + shape[axis + 1 :])
    kept = lax.slice_in_dim(split, 0, count, axis=axis + 1)
    return kept.reshape(shape[:axis] + (parts * count,) + shape[axis + 1 :])


def plain_layer(
    layer_input, output_grad, wide, tall, norm_gains, block_order, sizes
):
    parts, width, half, kv, short, full, high = sizes
    hidden_size = 2 * half
    rows = layer_input.shape[1]
    block = rows // 2
    group = HEADS // KV_HEADS
    scale = 1.0 / math.sqrt(HEAD)
    ctx_place = lax.axis_index("ctx")
    offsets = jnp.arange(block, dtype=jnp.int32)
    own_blocks = lax.dynamic_slice_in_dim(block_order, 2 * ctx_place, 2)
    query_pos = (own_blocks[:, None] * block + offsets[None, :]).reshape(rows)
    key_pos = (block_order[:, None] * block + offsets[None, :]).reshape(-1)

    all_wide, all_tall = gather_weights(wide, tall)
    w_qk, w_ov, w_gate_0, w_gate_1, w_up_0, w_up_1 = [all_wide[i].reshape(width, half) for i in range(WIDE)]
    w_down = [all_tall[i].reshape(half, width) for i in range(2)]

    residual = layer_input[0].astype(jnp.float32)
    normed_first, inverse_first = norm_forward(residual, norm_gains[0])
    qk_pre = jnp.dot(normed_first, w_qk, preferred_element_type=jnp.float32)
    query_pre = qk_pre[:, :width].reshape(rows, HEADS, HEAD)
    key_pre = qk_pre[:, width:].reshape(rows, KV_HEADS, HEAD)
    value_low = (
        jnp.dot(normed_first, w_ov, preferred_element_type=jnp.float32)[:, width:]
        .astype(jnp.bfloat16)
        .reshape(rows, KV_HEADS, HEAD)
    )
    cosine, sine = rotary_tables(query_pos, HEAD)
    query_rot = rotate(query_pre, cosine, sine).astype(jnp.bfloat16)
    key_rot = rotate(key_pre, cosine, sine).astype(jnp.bfloat16)
    keys_all, values_all = (
        lax.all_gather(key_rot, "ctx", axis=0, tiled=True),
        lax.all_gather(value_low, "ctx", axis=0, tiled=True),
    )
    keys_head = keys_all.transpose(1, 0, 2)
    values_head = values_all.transpose(1, 0, 2)
    queries_head = (
        query_rot.reshape(rows, KV_HEADS, group, HEAD)
        .transpose(1, 2, 0, 3)
        .reshape(KV_HEADS, group * rows, HEAD)
    )
    row_pos = jnp.tile(query_pos, group)
    allowed = key_pos[None, :] <= row_pos[:, None]

    def head_forward(item):
        query, key, value = item
        scores = jnp.where(allowed, contract(query, key, 1, 1) * scale, MASKED)
        top = jnp.max(scores, axis=-1, keepdims=True)
        expo = jnp.exp(scores - top)
        total = jnp.sum(expo, axis=-1, keepdims=True)
        probs_low = (expo / total).astype(jnp.bfloat16)
        return (
            jnp.dot(probs_low, value, preferred_element_type=jnp.float32),
            (top + jnp.log(total))[:, 0],
        )

    mixed, log_total = lax.map(head_forward, (queries_head, keys_head, values_head))
    attended = (
        mixed.reshape(KV_HEADS, group, rows, HEAD)
        .transpose(2, 0, 1, 3)
        .reshape(rows, HEADS * HEAD)
        .astype(jnp.bfloat16)
    )
    w_out = w_ov[:, :width]
    middle = residual + jnp.dot(attended, w_out, preferred_element_type=jnp.float32)
    normed_second, inverse_second = norm_forward(middle, norm_gains[1])

    def sides(left, right):
        return jnp.concatenate([left, right], axis=1)

    gate = sides(
        jnp.dot(normed_second, w_gate_0, preferred_element_type=jnp.float32),
        jnp.dot(normed_second, w_gate_1, preferred_element_type=jnp.float32),
    )
    lifted = sides(
        jnp.dot(normed_second, w_up_0, preferred_element_type=jnp.float32),
        jnp.dot(normed_second, w_up_1, preferred_element_type=jnp.float32),
    )
    sigma = jax.nn.sigmoid(gate)
    hidden = (gate * sigma * lifted).astype(jnp.bfloat16)
    hidden_split = hidden.reshape(rows, parts, 2, high)
    hidden_sides = [hidden_split[:, :, i].reshape(rows, half) for i in range(2)]
    layer_output = (
        middle
        + jnp.dot(hidden_sides[0], w_down[0], preferred_element_type=jnp.float32)
        + jnp.dot(hidden_sides[1], w_down[1], preferred_element_type=jnp.float32)
    ).astype(jnp.bfloat16)
    upstream = output_grad[0]
    grad_hidden = jnp.stack(
        [contract(upstream, w_down[i], 1, 1).reshape(rows, parts, high) for i in range(2)], axis=2
    ).reshape(rows, hidden_size)
    grad_gate = (grad_hidden * lifted * sigma * (1.0 + gate * (1.0 - sigma))).astype(jnp.bfloat16)
    grad_lifted = (grad_hidden * gate * sigma).astype(jnp.bfloat16)
    grad_normed_second = (
        contract(grad_gate[:, :half], w_gate_0, 1, 1)
        + contract(grad_gate[:, half:], w_gate_1, 1, 1)
        + contract(grad_lifted[:, :half], w_up_0, 1, 1)
        + contract(grad_lifted[:, half:], w_up_1, 1, 1)
    )
    through_second, gain_second = norm_backward(
        middle, inverse_second, norm_gains[1], grad_normed_second
    )
    grad_middle = upstream.astype(jnp.float32) + through_second
    grad_branch = grad_middle.astype(jnp.bfloat16)
    grad_attended = contract(grad_branch, w_out, 1, 1).astype(jnp.bfloat16)
    grad_heads = (
        grad_attended.reshape(rows, KV_HEADS, group, HEAD)
        .transpose(1, 2, 0, 3)
        .reshape(KV_HEADS, group * rows, HEAD)
    )

    def head_backward(item):
        query, key, value, grad_out, log_row = item
        scores = jnp.where(allowed, contract(query, key, 1, 1) * scale, MASKED)
        probs = jnp.exp(scores - log_row[:, None])
        grad_value_part = contract(probs.astype(jnp.bfloat16), grad_out, 0, 0)
        grad_probs = contract(grad_out, value, 1, 1)
        grad_scores = (
            probs * (grad_probs - jnp.sum(grad_probs * probs, axis=-1, keepdims=True))
        ).astype(jnp.bfloat16)
        grad_query_part = jnp.dot(grad_scores, key, preferred_element_type=jnp.float32) * scale
        grad_key_part = contract(grad_scores, query, 0, 0) * scale
        return (grad_query_part, grad_key_part, grad_value_part)

    grad_query_rot, grad_key_all, grad_value_all = lax.map(
        head_backward, (queries_head, keys_head, values_head, grad_heads, log_total)
    )
    grad_key_own, grad_value_own = (
        lax.psum_scatter(
            grad_key_all.astype(jnp.bfloat16), "ctx", scatter_dimension=1, tiled=True
        ).astype(jnp.float32),
        lax.psum_scatter(
            grad_value_all.astype(jnp.bfloat16), "ctx", scatter_dimension=1, tiled=True
        ).astype(jnp.float32),
    )
    grad_query = (
        unrotate(
            grad_query_rot.reshape(KV_HEADS, group, rows, HEAD)
            .transpose(2, 0, 1, 3)
            .reshape(rows, HEADS, HEAD),
            cosine,
            sine,
        )
        .reshape(rows, HEADS * HEAD)
        .astype(jnp.bfloat16)
    )
    grad_key = (
        unrotate(grad_key_own.transpose(1, 0, 2), cosine, sine)
        .reshape(rows, KV_HEADS * HEAD)
        .astype(jnp.bfloat16)
    )
    grad_value = (
        grad_value_own.transpose(1, 0, 2).reshape(rows, KV_HEADS * HEAD).astype(jnp.bfloat16)
    )
    grad_qk = sides(grad_query, grad_key)
    zero_query = jnp.zeros((rows, width), jnp.bfloat16)
    grad_v = sides(zero_query, grad_value)
    grad_normed_first = contract(grad_qk, w_qk, 1, 1) + contract(grad_v, w_ov, 1, 1)
    through_first, gain_first = norm_backward(
        residual, inverse_first, norm_gains[0], grad_normed_first
    )
    input_gradient = grad_middle + through_first

    xt = jnp.stack([item.T for item in (normed_first, attended, normed_second, upstream)])
    xt = padded(xt, 1, parts, short, full)
    dy = jnp.stack(
        [
            grad_qk,
            sides(grad_branch, jnp.zeros((rows, kv), jnp.bfloat16)),
            grad_gate[:, :half],
            grad_gate[:, half:],
            grad_lifted[:, :half],
            grad_lifted[:, half:],
            hidden_sides[0],
            hidden_sides[1],
            grad_v,
        ]
    )
    gains = jnp.pad(jnp.stack([gain_first, gain_second]), ((0, 6), (0, 0)))
    return layer_output, input_gradient, xt, dy, gains


def rotation(block_order, rows):
    block = rows // 2
    ctx_place = lax.axis_index("ctx")
    offsets = jnp.arange(block, dtype=jnp.int32)
    own_blocks = lax.dynamic_slice_in_dim(block_order, 2 * ctx_place, 2)
    query_pos = (own_blocks[:, None] * block + offsets[None, :]).reshape(rows)
    key_pos = (block_order[:, None] * block + offsets[None, :]).reshape(-1)
    bias = jnp.where(key_pos[:, None] <= query_pos[None, :], 0.0, MASKED).astype(jnp.bfloat16)
    lane = jnp.arange(128, dtype=jnp.int32)
    index = (lane % (HEAD // 2)).astype(jnp.float32)
    frequency = THETA ** (-(index * 2.0 / HEAD))
    angle = query_pos.astype(jnp.float32)[:, None] * frequency[None, :]
    cosine, sine = jnp.cos(angle), jnp.sin(angle)
    early = (lane % HEAD < HEAD // 2)[None, :]
    return (cosine, jnp.where(early, 0.0, sine), jnp.where(early, -sine, 0.0)), bias


def plain_step(layer_input, output_grad, norm_gains, block_order, weights, olds, factors, sizes):
    parts, width, half, kv, short, full, high = sizes
    query_weight, key_weight, value_weight, output_weight, gate_weight, up_weight, down_weight = weights
    (
        query_momentum,
        key_momentum,
        value_momentum,
        output_momentum,
        gate_momentum,
        up_momentum,
        down_momentum,
    ) = olds

    def sides(left, right):
        return jnp.concatenate([left, right], axis=1)

    wide = jnp.stack(
        [
            jnp.concatenate([query_weight, key_weight], axis=1),
            jnp.concatenate([output_weight, value_weight], axis=1),
            gate_weight[:, :half],
            gate_weight[:, half:],
            up_weight[:, :half],
            up_weight[:, half:],
        ]
    )
    tall = down_weight.reshape(2, high, width)
    layer_output, input_gradient, xt, dy, gains = plain_layer(
        layer_input, output_grad, wide, tall, norm_gains, block_order, sizes
    )

    def pad_rows(array):
        return padded(array, 0, 1, short, full)

    def pad_columns(array):
        return padded(array, 1, parts, short, full)

    moments = (
        pad_rows(sides(query_momentum, key_momentum)),
        pad_rows(sides(output_momentum, value_momentum)),
        pad_rows(gate_momentum),
        pad_rows(up_momentum),
        pad_columns(down_momentum),
    )
    g_wide, g_tall, s_wide, s_tall, gain_sum = reduce_gradients(xt, dy, gains, moments, full, high)
    o_wide, o_tall = orthogonalize(s_wide, s_tall, full, high, width)

    def unpack(wide_pieces, tall_pieces):
        pieces = wide_pieces[:, :short]
        tall = trimmed(tall_pieces, 2, parts, short, full).reshape(2 * high, width)
        return (
            pieces[0, :, :width],
            pieces[0, :, width:],
            pieces[1, :, width:],
            pieces[1, :, :width],
            sides(pieces[2], pieces[3]),
            sides(pieces[4], pieces[5]),
            tall,
        )

    gradients = [item.astype(jnp.float32) for item in unpack(g_wide, g_tall)]
    orthos = unpack(o_wide, o_tall)
    moments = [MOMENTUM * old + new for old, new in zip(olds, gradients)]
    new_weights = [
        weight.astype(jnp.float32) + factor * ortho.astype(jnp.float32)
        for weight, factor, ortho in zip(weights, factors, orthos)
    ]
    return layer_output, input_gradient, gradients, moments, new_weights, gain_sum


def on_device(
    layer_input,
    output_grad,
    query_weight,
    key_weight,
    value_weight,
    output_weight,
    gate_weight,
    up_weight,
    down_weight,
    norm_gains,
    query_momentum,
    key_momentum,
    value_momentum,
    output_momentum,
    gate_momentum,
    up_momentum,
    down_momentum,
    gain_momentum,
    block_order,
):
    parts = lax.axis_size("fsdp")
    width = layer_input.shape[2]
    half = gate_weight.shape[1] // 2
    kv = key_weight.shape[1]
    short = width // parts
    full = -(-short // 16) * 16
    high = half // parts
    sizes = (parts, width, half, kv, short, full, high)

    weights = (query_weight, key_weight, value_weight, output_weight, gate_weight, up_weight, down_weight)
    olds = (
        query_momentum,
        key_momentum,
        value_momentum,
        output_momentum,
        gate_momentum,
        up_momentum,
        down_momentum,
    )
    factors = []
    for index, weight in enumerate(weights):
        step_rate = OUT_RATE if index == 3 else RATE
        factors.append(-step_rate * max(1.0, weight.shape[1] / (weight.shape[0] * parts)) ** 0.5)

    fused = (
        lax.axis_size("ctx") == CLASSES
        and short == full
        and parts % 2 == 0
        and half % (2 * half // parts) == 0
        and (2 * half // parts) % 128 == 0
        and layer_input.shape[1] == 128
        and short <= 256
    )
    if fused:
        tables, bias = rotation(block_order, layer_input.shape[1])

        def turned(items):
            q, k, v, o, gate, up, down = items
            return (q, k.T, o, v.T, gate, up, down.T)

        shards, moments = turned(weights), turned(olds)
        out_turned, grad_turned, g, o, gain_sum = step_pass(
            layer_input[0].T, output_grad[0].T, norm_gains, tables, bias, shards, moments
        )
        gradients, moments, new_weights = settle(g, o, moments, shards, factors)
        layer_output, input_gradient = out_turned.T, grad_turned.T
    else:
        layer_output, input_gradient, gradients, moments, new_weights, gain_sum = plain_step(
            layer_input, output_grad, norm_gains, block_order, weights, olds, factors, sizes
        )
    gain_width = norm_gains.shape[1] // parts
    place = lax.axis_index("fsdp") * gain_width
    gain_gradient = lax.dynamic_slice_in_dim(gain_sum[:2], place, gain_width, 1)
    gain_shard = lax.dynamic_slice_in_dim(norm_gains, place, gain_width, 1)
    gain_moment = MOMENTUM * gain_momentum + gain_gradient
    new_gains = gain_shard - GAIN_RATE * gain_moment
    return (
        layer_output[None],
        input_gradient[None],
        *gradients,
        gain_gradient,
        *moments,
        gain_moment,
        *new_weights,
        new_gains,
    )


def solution(mesh):
    tokens = P("fsdp", "ctx", None)
    shard = P("fsdp", None)
    gains = P(None, "fsdp")
    return jax.shard_map(
        on_device,
        mesh=mesh,
        in_specs=(tokens, tokens) + (shard,) * 7 + (P(),) + (shard,) * 7 + (gains, P()),
        out_specs=(tokens, tokens) + ((shard,) * 7 + (gains,)) * 3,
        check_vma=False,
    )
```

```python
import functools
import math

import jax
import jax.numpy as jnp
from jax import lax
from jax.experimental import pallas as pl
from jax.experimental.pallas import tpu as pltpu
from jax.sharding import PartitionSpec as P

HEADS = 15
KV_HEADS = 5
HEAD = 64
NS_ITERS = 5


EPS = 1e-05
THETA = 100000.0
NS_A = 3.4445
NS_B = -4.775
NS_C = 2.0315
MOMENTUM = 0.95
RATE = 0.2
OUT_RATE = 6.0
GAIN_RATE = 0.002
MASKED = -1e30

MESH = pl.DeviceIdType.MESH
BF16 = jnp.bfloat16
F32 = jnp.float32
ANY = pl.BlockSpec(memory_space=pl.ANY)
VMEM = pl.BlockSpec(memory_space=pltpu.VMEM)
CLASSES = 8
WIDE = 6


def contract(left, right, left_dim, right_dim):
    return lax.dot_general(
        left, right, (((left_dim,), (right_dim,)), ((), ())), preferred_element_type=jnp.float32
    )


class Place:
    def __init__(self):
        self.parts = lax.axis_size("fsdp")
        self.extra = lax.axis_size("ctx") // CLASSES
        self.c = lax.axis_index("ctx")
        self.f = lax.axis_index("fsdp")
        self.p = lax.rem(self.c, CLASSES)
        self.core = lax.rem(self.c, 2)
        self.b1 = jnp.where(self.core == 0, 2, 4)
        self.b2 = jnp.where(self.core == 0, 4, 2)

    def peer(self, bits):
        return (self.c ^ bits, self.f)

    def along(self, j):
        return (self.c, self.f ^ j)

    def other(self, j):
        groups = self.extra
        return (lax.rem(self.c + CLASSES * j, CLASSES * groups), self.f)

    def barrier(self, bits=(1, 2, 4), line=True, others=False):
        sem = pltpu.get_barrier_semaphore()
        targets = [self.peer(b) for b in bits]
        if line:
            targets += [self.along(j) for j in range(1, self.parts)]
        if others:
            targets += [self.other(j) for j in range(1, self.extra)]
        for target in targets:
            pl.semaphore_signal(sem, inc=1, device_id=target, device_id_type=MESH)
        pl.semaphore_wait(sem, len(targets))


def remote(src, dst, send, recv, target):
    return pltpu.make_async_remote_copy(
        src_ref=src, dst_ref=dst, send_sem=send, recv_sem=recv, device_id=target, device_id_type=MESH
    )


def by_kind(cls, wide, tall):
    pl.when(cls < WIDE)(wide)
    pl.when(cls >= WIDE)(tall)


def weights_kernel(in_a, in_b, out_a, out_b, local, zs, s1, s2, sc, recv):
    at = Place()
    p, f, parts = at.p, at.f, at.parts
    at.barrier()
    copies = [
        pltpu.make_async_copy(in_a, out_a.at[:, f], local.at[0]),
        pltpu.make_async_copy(in_b, out_b.at[:, f], local.at[1]),
    ]
    for copy in copies:
        copy.start()

    def act(cls, j, g, send, target, what, first=False):
        def wide():
            dst = out_a.at[cls, g]
            src = in_a.at[cls] if first else dst
            getattr(remote(src, dst, send, recv.at[cls, j], target), what)()

        def tall():
            dst = out_b.at[cls - WIDE, g]
            src = in_b.at[cls - WIDE] if first else dst
            getattr(remote(src, dst, send, recv.at[cls, j], target), what)()

        by_kind(cls, wide, tall)

    sends = []

    def send(cls, j, g, sem, target, first=False):
        act(cls, j, g, sem, target, "start", first)
        sends.append((cls, j, g, sem, target, first))

    def arrived(cls, j):
        act(cls, j, f ^ j, zs.at[j], at.along(j), "wait_recv")

    for j in range(1, parts):
        send(p, j, f, zs.at[j], at.along(j), True)
    for j in range(1, parts):
        arrived(p, j)
        send(p, j, f ^ j, s1.at[0, j], at.peer(at.b1))
        send(p, j, f ^ j, s2.at[0, j], at.peer(at.b2))
        send(p, j, f ^ j, sc.at[0, j], at.peer(1))
    for j in range(1, parts):
        arrived(p ^ at.b1, j)
        send(p ^ at.b1, j, f ^ j, s2.at[1, j], at.peer(at.b2))
        send(p ^ at.b1, j, f ^ j, sc.at[1, j], at.peer(1))
    for slot, bits in ((2, at.b2), (3, at.b1 ^ at.b2)):
        for j in range(1, parts):
            arrived(p ^ bits, j)
            send(p ^ bits, j, f ^ j, sc.at[slot, j], at.peer(1))
    for bits in (1, 3, 5, 7):
        for j in range(1, parts):
            arrived(p ^ bits, j)
    for cls, j, g, sem, target, first in sends:
        act(cls, j, g, sem, target, "wait_send", first)
    for copy in copies:
        copy.wait()


def gather_weights(wide, tall):
    parts = lax.axis_size("fsdp")
    dma = pltpu.SemaphoreType.DMA
    return pl.pallas_call(
        weights_kernel,
        out_shape=(
            jax.ShapeDtypeStruct((WIDE, parts) + wide.shape[1:], BF16),
            jax.ShapeDtypeStruct((CLASSES - WIDE, parts) + tall.shape[1:], BF16),
        ),
        in_specs=[ANY, ANY],
        out_specs=(ANY, ANY),
        scratch_shapes=[
            dma((2,)),
            dma((parts,)),
            dma((1, parts)),
            dma((2, parts)),
            dma((4, parts)),
            dma((CLASSES, parts)),
        ],
        compiler_params=pltpu.CompilerParams(collective_id=0, has_side_effects=True),
        name="gather_weights",
    )(wide, tall)


def spread(at, own_a, own_b, out_a, out_b, local, ss, recv):
    p = at.p

    def act(cls, sem, target, what, first=False):
        def wide():
            dst = out_a.at[cls]
            getattr(remote(own_a if first else dst, dst, sem, recv.at[cls], target), what)()

        def tall():
            dst = out_b.at[cls - WIDE]
            getattr(remote(own_b if first else dst, dst, sem, recv.at[cls], target), what)()

        by_kind(cls, wide, tall)

    def keep(what):
        def wide():
            getattr(pltpu.make_async_copy(own_a, out_a.at[p], local), what)()

        def tall():
            getattr(pltpu.make_async_copy(own_b, out_b.at[p - WIDE], local), what)()

        by_kind(p, wide, tall)

    sends = []

    def send(cls, slot, target, first=False):
        act(cls, ss.at[slot], target, "start", first)
        sends.append((cls, slot, target, first))

    def arrived(cls):
        act(cls, ss.at[0], at.peer(1), "wait_recv")

    send(p, 0, at.peer(at.b1), True)
    send(p, 1, at.peer(at.b2), True)
    send(p, 2, at.peer(1), True)
    keep("start")

    def finish():
        arrived(p ^ at.b1)
        send(p ^ at.b1, 3, at.peer(at.b2))
        send(p ^ at.b1, 4, at.peer(1))
        arrived(p ^ at.b2)
        send(p ^ at.b2, 5, at.peer(1))
        arrived(p ^ at.b1 ^ at.b2)
        send(p ^ at.b1 ^ at.b2, 6, at.peer(1))
        for bits in (1, 3, 5, 7):
            arrived(p ^ bits)
        for cls, slot, target, first in sends:
            act(cls, ss.at[slot], target, "wait_send", first)
        keep("wait")

    return finish


def reduce_kernel(
    parts, extra, high,
    xt_in, dy_in, gain_in, m_qk, m_ov, m_gate, m_up, m_down,
    g_a, g_b, s_a, s_b, gain_out,
    xt, dy, p1s, p1r, p2s, p2r, own, own_t, za_s, za_r, zb_s, zb_r, ma, mb, ga, gb, sa, sb, es, er, gain_s, gain_r,
    ls, xs, xr, s1, r1, s2, r2, zs, zr, esem, ersem, msem, gs, gr, ag_l, ag_s, ag_r, ss, sr, sl,
):
    at = Place()
    p, f, core = at.p, at.f, at.core
    tokens = xt_in.shape[2]
    rows = ma.shape[0]
    half = dy.shape[2]

    def moment(what):
        for cls in range(CLASSES):
            @pl.when(p == cls)
            def _(cls=cls):
                side = cls % 2
                if cls < 2:
                    src, dst = (m_qk, m_ov)[cls], ma
                elif cls < WIDE:
                    whole = m_gate if cls < 4 else m_up
                    src, dst = whole.at[:, pl.ds(side * half, half)], ma
                else:
                    src, dst = m_down.at[pl.ds(side * high, high)], mb
                getattr(pltpu.make_async_copy(src, dst, msem), what)()

    moment("start")
    mine = [pltpu.make_async_copy(xt_in, xt.at[:, :, pl.ds(0, tokens)], ls.at[0])]
    for slot in range(4):
        mine.append(
            pltpu.make_async_copy(dy_in.at[core + 2 * slot], dy.at[slot, pl.ds(0, tokens)], ls.at[1 + slot])
        )
    mine.append(pltpu.make_async_copy(dy_in.at[8], dy.at[4, pl.ds(0, tokens)], ls.at[5]))
    for copy in mine:
        copy.start()
    at.barrier(others=True)
    pair = at.peer(1)
    theirs = [remote(xt_in, xt.at[:, :, pl.ds(tokens, tokens)], xs.at[0], xr.at[0], pair)]
    for slot in range(4):
        theirs.append(
            remote(dy_in.at[1 - core + 2 * slot], dy.at[slot, pl.ds(tokens, tokens)], xs.at[1 + slot], xr.at[1 + slot], pair)
        )
    theirs.append(remote(dy_in.at[8], dy.at[4, pl.ds(tokens, tokens)], xs.at[5], xr.at[5], pair))
    for copy in theirs:
        copy.start()

    def swap(slot, target):
        return remote(gain_s.at[slot], gain_r.at[slot], gs.at[slot], gr.at[slot], target)

    gain_s[0] = gain_in[...]
    swaps = [swap(0, pair)]
    swaps[0].start()
    for copy in mine:
        copy.wait()
    for copy in theirs:
        copy.wait()

    def term(cls, r):
        at_rows = pl.ds(pl.multiple_of(r * rows, rows), rows)
        slot = lax.div(cls, 2)
        kind = jnp.where(cls == 0, 0, jnp.where(cls == 1, 1, jnp.where(cls < WIDE, 2, 3)))
        value = jnp.dot(xt[kind, at_rows, :], dy[slot], preferred_element_type=F32)
        return value

    def with_values(cls, r, put):
        at_rows = pl.ds(pl.multiple_of(r * rows, rows), rows)

        @pl.when(cls == 1)
        def _():
            put(term(cls, r) + jnp.dot(xt[0, at_rows, :], dy[4], preferred_element_type=F32))

        @pl.when(cls != 1)
        def _():
            put(term(cls, r))

    def order(i):
        return lax.rem(f + 1 + i, parts)

    def one(slot, i):
        r = order(i)
        return remote(p1s.at[slot, r], p1r.at[slot, r], s1.at[slot, r], r1.at[slot, r], at.peer(at.b1))

    for slot, bits in ((0, at.b1 ^ at.b2), (1, at.b1)):
        def first(i, carry, slot=slot, bits=bits):
            r = order(i)

            def put(value):
                p1s[slot, r] = value.astype(BF16)

            with_values(p ^ bits, r, put)
            one(slot, i).start()
            return carry

        lax.fori_loop(0, parts, first, 0)

    swaps[0].wait()
    gain_s[1] = gain_s[0] + gain_r[0]
    swaps.append(swap(1, at.peer(2)))
    swaps[1].start()

    def two(i):
        r = order(i)
        return remote(p2s.at[r], p2r.at[r], s2.at[r], r2.at[r], at.peer(at.b2))

    def second(i, carry):
        r = order(i)
        one(0, i).wait_recv()

        def put(value):
            p2s[r] = (value + p1r[0, r].astype(F32)).astype(BF16)

        with_values(p ^ at.b2, r, put)
        two(i).start()
        return carry

    lax.fori_loop(0, parts, second, 0)
    swaps[1].wait()
    gain_s[2] = gain_s[1] + gain_r[1]
    swaps.append(swap(2, at.peer(4)))
    swaps[2].start()

    def line_a(r, source):
        return remote(za_s.at[r], za_r.at[source], zs.at[r], zr.at[source], (at.c, r))

    def line_b(r, source):
        return remote(
            zb_s.at[pl.ds(pl.multiple_of(r * high, high), high)],
            zb_r.at[source], zs.at[r], zr.at[source], (at.c, r),
        )

    early = extra == 1

    def third(i, carry):
        r = order(i)
        one(1, i).wait_recv()
        two(i).wait_recv()

        def put(value):
            total = value + p1r[1, r].astype(F32) + p2r[r].astype(F32)
            own[r] = total
            if early:
                za_s[r] = total.astype(BF16)

        with_values(p, r, put)
        if early:
            @pl.when((p < WIDE) & (i < parts - 1))
            def _():
                line_a(r, f).start()
        return carry

    lax.fori_loop(0, parts, third, 0)
    swaps[2].wait()
    gain_s[3] = gain_s[2] + gain_r[2]

    if not early:
        es[...] = own[...].astype(BF16)
        group = [
            remote(es, er.at[j - 1], esem.at[j - 1], ersem.at[j - 1], at.other(j)) for j in range(1, extra)
        ]
        for copy in group:
            copy.start()
        for j in range(1, extra):
            group[j - 1].wait_recv()
            own[...] = own[...] + er[j - 1].astype(F32)
        for copy in group:
            copy.wait_send()
        za_s[...] = own[...].astype(BF16)

        @pl.when(p < WIDE)
        def _():
            for j in range(1, parts):
                line_a(f ^ j, f).start()

    @pl.when(p >= WIDE)
    def _():
        for tile in range(half // 128):
            for r in range(parts):
                block = own[r, :, pl.ds(tile * 128, 128)]
                if rows % 128 == 0:
                    own_t[pl.ds(tile * 128, 128), pl.ds(r * rows, rows)] = block.T
            if rows % 128 != 0:
                column = own[:, :, pl.ds(tile * 128, 128)].reshape(parts * rows, 128)
                own_t[pl.ds(tile * 128, 128), :] = column.T
        zb_s[...] = own_t[...].astype(BF16)
        for j in range(1, parts):
            line_b(f ^ j, f).start()

    line_gain = [
        remote(gain_s.at[3], gain_r.at[3 + j], gs.at[3 + j], gr.at[3 + j], at.along(j)) for j in range(1, parts)
    ]
    other_gain = []
    for copy in line_gain:
        copy.start()

    moment("wait")

    @pl.when(p < WIDE)
    def _():
        total = own[f]
        for j in range(1, parts):
            line_a(f ^ j, f ^ j).wait_recv()
            total = total + za_r[f ^ j].astype(F32)
        ga[...] = total.astype(BF16)
        sa[...] = (MOMENTUM * ma[...] + total).astype(BF16)

    @pl.when(p >= WIDE)
    def _():
        total = own_t[pl.ds(pl.multiple_of(f * high, high), high), :]
        for j in range(1, parts):
            line_b(f ^ j, f ^ j).wait_recv()
            total = total + zb_r[f ^ j].astype(F32)
        gb[...] = total.astype(BF16)
        sb[...] = (MOMENTUM * mb[...] + total).astype(BF16)

    def share_a(j, source):
        return remote(sa, s_a.at[pl.ds(pl.multiple_of(source * rows, rows), rows)], ss.at[j], sr.at[j], at.along(j))

    def share_b(j, source):
        return remote(sb, s_b.at[pl.ds(pl.multiple_of(source * high, high), high)], ss.at[j], sr.at[j], at.along(j))

    @pl.when(p < WIDE)
    def _():
        for j in range(1, parts):
            share_a(j, f).start()
        pltpu.make_async_copy(sa, s_a.at[pl.ds(pl.multiple_of(f * rows, rows), rows)], sl).start()

    @pl.when(p >= WIDE)
    def _():
        for j in range(1, parts):
            share_b(j, f).start()
        pltpu.make_async_copy(sb, s_b.at[pl.ds(pl.multiple_of(f * high, high), high)], sl).start()

    finish = spread(at, ga, gb, g_a, g_b, ag_l, ag_s, ag_r)
    total = gain_s[3]
    for j in range(1, parts):
        line_gain[j - 1].wait()
        total = total + gain_r[3 + j]
    if extra > 1:
        gain_s[4] = total
        other_gain = [
            remote(gain_s.at[4], gain_r.at[3 + parts + j], gs.at[3 + parts + j], gr.at[3 + parts + j], at.other(j))
            for j in range(1, extra)
        ]
        for copy in other_gain:
            copy.start()
        for j in range(1, extra):
            other_gain[j - 1].wait()
            total = total + gain_r[3 + parts + j]
    gain_out[...] = total
    finish()

    for slot in range(2):
        lax.fori_loop(0, parts, lambda i, carry, slot=slot: (one(slot, i).wait_send(), carry)[1], 0)
    lax.fori_loop(0, parts, lambda i, carry: (two(i).wait_send(), carry)[1], 0)

    @pl.when(p < WIDE)
    def _():
        for j in range(1, parts):
            line_a(f ^ j, f).wait_send()
            share_a(j, f).wait_send()
            share_a(j, f ^ j).wait_recv()
        pltpu.make_async_copy(sa, s_a.at[pl.ds(pl.multiple_of(f * rows, rows), rows)], sl).wait()

    @pl.when(p >= WIDE)
    def _():
        for j in range(1, parts):
            line_b(f ^ j, f).wait_send()
            share_b(j, f).wait_send()
            share_b(j, f ^ j).wait_recv()
        pltpu.make_async_copy(sb, s_b.at[pl.ds(pl.multiple_of(f * high, high), high)], sl).wait()


def reduce_gradients(xt, dy, gains, moments, rows, high):
    parts = lax.axis_size("fsdp")
    extra = lax.axis_size("ctx") // CLASSES
    kinds, depth, tokens = xt.shape
    half = dy.shape[2]
    dma = pltpu.SemaphoreType.DMA
    vm = pltpu.VMEM
    n_gain = 4 + parts + extra
    group = max(extra - 1, 1)
    spare = (parts, rows, half) if extra > 1 else (1, 16, 128)
    return pl.pallas_call(
        functools.partial(reduce_kernel, parts, extra, high),
        out_shape=(
            jax.ShapeDtypeStruct((WIDE, rows, half), BF16),
            jax.ShapeDtypeStruct((CLASSES - WIDE, high, depth), BF16),
            jax.ShapeDtypeStruct((depth, half), BF16),
            jax.ShapeDtypeStruct((half, depth), BF16),
            jax.ShapeDtypeStruct(gains.shape, F32),
        ),
        in_specs=[ANY, ANY, VMEM] + [ANY] * 5,
        out_specs=(ANY, ANY, ANY, ANY, VMEM),
        scratch_shapes=[
            vm((kinds, depth, 2 * tokens), BF16),
            vm((5, 2 * tokens, half), BF16),
            vm((2, parts, rows, half), BF16),
            vm((2, parts, rows, half), BF16),
            vm((parts, rows, half), BF16),
            vm((parts, rows, half), BF16),
            vm((parts, rows, half), F32),
            vm((half, depth), F32),
            vm((parts, rows, half), BF16),
            vm((parts, rows, half), BF16),
            vm((half, depth), BF16),
            vm((parts, high, depth), BF16),
            vm((rows, half), F32),
            vm((high, depth), F32),
            vm((rows, half), BF16),
            vm((high, depth), BF16),
            vm((rows, half), BF16),
            vm((high, depth), BF16),
            vm(spare, BF16),
            vm((group,) + spare, BF16),
            vm((5,) + gains.shape, F32),
            vm((n_gain,) + gains.shape, F32),
            dma((6,)), dma((6,)), dma((6,)),
            dma((2, parts)), dma((2, parts)), dma((parts,)), dma((parts,)), dma((parts,)), dma((parts,)),
            dma((group,)), dma((group,)), dma, dma((n_gain,)), dma((n_gain,)),
            dma, dma((7,)), dma((CLASSES,)), dma((parts,)), dma((parts,)), dma,
        ],
        compiler_params=pltpu.CompilerParams(
            collective_id=1, has_side_effects=True, vmem_limit_bytes=62 << 20
        ),
        name="reduce_gradients",
    )(xt, dy, gains, *moments)


def rounded(value):
    return value.astype(BF16)


def poly_rows(g, row_start, count):
    block = g[pl.ds(row_start, count), :]
    return rounded(NS_B * block.astype(F32) + NS_C * jnp.dot(block, g[...], preferred_element_type=F32))


def ortho_kernel(
    parts, rows, high, narrow,
    s_a, s_b, o_a, o_b,
    x, x_t, gs, gr, g, poly, sq, sq_r, pa, pb, kt,
    gsem, rsem, qs, qr, ag_l, ag_s, ag_r,
):
    at = Place()
    p, f = at.p, at.f
    depth, half = x.shape
    step = depth // 4
    at.barrier(line=False)
    pair = at.peer(1)

    @pl.when(p < WIDE)
    def _():
        x[...] = s_a[...]

    @pl.when(p >= WIDE)
    def _():
        for tile in range(half // 128):
            x[:, pl.ds(tile * 128, 128)] = s_b[pl.ds(tile * 128, 128), :].T

    def scale_of(total):
        return 1.0 / (jnp.sqrt(total) + 1e-07)

    def normal(ref, inverse):
        ref[...] = rounded(ref[...].astype(F32) * inverse)

    def exchange(slot, r):
        chunk = pl.ds(r * step, step)
        return remote(gs.at[chunk], gr.at[slot, chunk], gsem.at[r], rsem.at[slot, r], pair)

    def fill_poly():
        for r in range(4):
            poly[pl.ds(r * step, step), :] = poly_rows(g, r * step, step)

    my_rows = pl.ds(pl.multiple_of(f * rows, rows), rows)
    my_high = pl.ds(pl.multiple_of(f * high, high), high)

    @pl.when(p >= 2)
    def _():
        wide = x[...].astype(F32)
        sq[...] = jnp.broadcast_to(jnp.sum(wide * wide), sq.shape)
        copy = remote(sq, sq_r, qs, qr, pair)
        copy.start()
        copy.wait()
        normal(x, scale_of(sq[...] + sq_r[...])[:1, :1])

        def grams(slot):
            for r in range(4):
                gs[pl.ds(r * step, step), :] = rounded(contract(x[pl.ds(r * step, step), :], x[...], 1, 1))
                exchange(slot, r).start()
            for r in range(4):
                chunk = pl.ds(r * step, step)
                exchange(slot, r).wait()
                g[chunk, :] = rounded(gs[chunk, :].astype(F32) + gr[slot, chunk, :].astype(F32))

        def iterate(it, carry):
            grams(lax.rem(it, 2))
            fill_poly()
            for tile in range(half // 256):
                block = pl.ds(tile * 256, 256)
                x[:, block] = rounded(
                    NS_A * x[:, block].astype(F32) + jnp.dot(poly[...], x[:, block], preferred_element_type=F32)
                )
            return carry

        lax.fori_loop(0, NS_ITERS - 1, iterate, 0)
        grams((NS_ITERS - 1) % 2)

        @pl.when(p < WIDE)
        def _():
            mine = poly_rows(g, pl.multiple_of(f * rows, rows), rows)
            pa[...] = rounded(NS_A * x[my_rows, :].astype(F32) + jnp.dot(mine, x[...], preferred_element_type=F32))

        @pl.when(p >= WIDE)
        def _():
            fill_poly()
            for tile in range(half // 128):
                x_t[pl.ds(tile * 128, 128), :] = x[:, pl.ds(tile * 128, 128)].T
            block = x_t[my_high, :]
            pb[...] = rounded(NS_A * block.astype(F32) + jnp.dot(block, poly[...], preferred_element_type=F32))

    @pl.when(p < 2)
    def _():
        kt[...] = x[:, narrow:].T
        inverse_k = scale_of(jnp.sum(jnp.square(kt[...].astype(F32))))
        normal(kt, inverse_k)
        wide = x[:, :narrow].astype(F32)
        x[:, :narrow] = rounded(wide * scale_of(jnp.sum(wide * wide)))

        def narrow_step(it, carry):
            gram = rounded(contract(kt[...], kt[...], 1, 1))
            turn = rounded(NS_B * gram.astype(F32) + NS_C * jnp.dot(gram, gram, preferred_element_type=F32))
            kt[...] = rounded(NS_A * kt[...].astype(F32) + jnp.dot(turn, kt[...], preferred_element_type=F32))
            return carry

        lax.fori_loop(0, NS_ITERS, narrow_step, 0)

        def gram_of():
            for r in range(4):
                chunk = pl.ds(r * step, step)
                g[chunk, :] = rounded(contract(x[chunk, :narrow], x[:, :narrow], 1, 1))

        def square_step(it, carry):
            gram_of()
            fill_poly()
            x[:, :narrow] = rounded(
                NS_A * x[:, :narrow].astype(F32) + jnp.dot(poly[...], x[:, :narrow], preferred_element_type=F32)
            )
            return carry

        lax.fori_loop(0, NS_ITERS - 1, square_step, 0)
        gram_of()
        mine = poly_rows(g, pl.multiple_of(f * rows, rows), rows)
        square = rounded(
            NS_A * x[my_rows, :narrow].astype(F32) + jnp.dot(mine, x[:, :narrow], preferred_element_type=F32)
        )
        x[:, narrow:] = kt[...].T
        pa[:, :narrow] = square
        pa[:, narrow:] = x[my_rows, narrow:]

    spread(at, pa, pb, o_a, o_b, ag_l, ag_s, ag_r)()


def orthogonalize(s_a, s_b, rows, high, narrow):
    parts = lax.axis_size("fsdp")
    depth, half = s_a.shape
    dma = pltpu.SemaphoreType.DMA
    vm = pltpu.VMEM
    return pl.pallas_call(
        functools.partial(ortho_kernel, parts, rows, high, narrow),
        out_shape=(
            jax.ShapeDtypeStruct((WIDE, rows, half), BF16),
            jax.ShapeDtypeStruct((CLASSES - WIDE, high, depth), BF16),
        ),
        in_specs=[VMEM, VMEM],
        out_specs=(ANY, ANY),
        scratch_shapes=[
            vm((depth, half), BF16),
            vm((half, depth), BF16),
            vm((depth, depth), BF16),
            vm((2, depth, depth), BF16),
            vm((depth, depth), BF16),
            vm((depth, depth), BF16),
            vm((8, 128), F32),
            vm((8, 128), F32),
            vm((rows, half), BF16),
            vm((high, depth), BF16),
            vm((half - narrow, depth), BF16),
            dma((4,)), dma((2, 4)), dma, dma, dma, dma((7,)), dma((CLASSES,)),
        ],
        compiler_params=pltpu.CompilerParams(
            collective_id=2, has_side_effects=True, vmem_limit_bytes=62 << 20
        ),
        name="orthogonalize",
    )(s_a, s_b)


class Weights:
    def __init__(self, at, sources, homes, zs, s1, s2, sc, recv):
        self.at, self.sources, self.homes = at, sources, homes
        self.zs, self.s1, self.s2, self.sc, self.recv = zs, s1, s2, sc, recv
        self.sends = []

    def act(self, group, q, j, plane, send, target, what, first=False):
        recv = self.recv.at[group, q, j]
        home, source = self.homes[group], self.sources[group]
        rows = home.shape[-2] // (1 if group == 3 else self.at.parts)
        unit = -(-rows // (16 * CLASSES)) * 16
        last = rows - (CLASSES - 1) * unit

        def piece(count):
            def go():
                start = pl.multiple_of(q * unit, 16)
                if group == 3:
                    columns = home.shape[1] // self.at.parts
                    dst = home.at[pl.ds(start, count), pl.ds(pl.multiple_of(plane * columns, 128), columns)]
                    src = source.at[pl.ds(start, count)]
                elif group == 0:
                    dst = home.at[:, pl.ds(pl.multiple_of(plane * rows + start, 16), count)]
                    src = dst
                else:
                    dst = home.at[pl.ds(pl.multiple_of(plane * rows + start, 16), count)]
                    src = source.at[pl.ds(start, count)]
                getattr(remote(src if first else dst, dst, send, recv, target), what)()

            return go

        pl.when(q < CLASSES - 1)(piece(unit))
        pl.when(q == CLASSES - 1)(piece(last))

    def send(self, group, q, j, plane, sem, target, first=False):
        self.act(group, q, j, plane, sem, target, "start", first)
        self.sends.append((group, q, j, plane, sem, target, "wait_send", first))

    def arrived(self, group, q, j):
        at = self.at
        self.act(group, q, j, at.f ^ j, self.zs.at[group, j], at.peer(1), "wait_recv")

    def along(self, group):
        at = self.at
        for j in range(1, at.parts):
            self.send(group, at.p, j, at.f, self.zs.at[group, j], at.along(j), True)

    def first(self, group):
        at = self.at
        for j in range(1, at.parts):
            self.arrived(group, at.p, j)
            self.send(group, at.p, j, at.f ^ j, self.s1.at[group, j], at.peer(at.b1))
            self.send(group, at.p, j, at.f ^ j, self.s2.at[group, 0, j], at.peer(at.b2))
            self.send(group, at.p, j, at.f ^ j, self.sc.at[group, 0, j], at.peer(1))

    def second(self, group):
        at = self.at
        q = at.p ^ at.b1
        for j in range(1, at.parts):
            self.arrived(group, q, j)
            self.send(group, q, j, at.f ^ j, self.s2.at[group, 1, j], at.peer(at.b2))
            self.send(group, q, j, at.f ^ j, self.sc.at[group, 1, j], at.peer(1))

    def third(self, group):
        at = self.at
        for slot, bits in ((2, at.b2), (3, at.b1 ^ at.b2)):
            for j in range(1, at.parts):
                self.arrived(group, at.p ^ bits, j)
                self.send(group, at.p ^ bits, j, at.f ^ j, self.sc.at[group, slot, j], at.peer(1))

    def ready(self, group):
        at = self.at
        for bits in (1, 3, 5, 7):
            for j in range(1, at.parts):
                self.arrived(group, at.p ^ bits, j)

    def finish(self):
        for item in self.sends:
            self.act(*item)


def spread_even(at, own, out, local, ss, recv):
    p = at.p

    def copy_of(cls, slot, target, first=False):
        return remote(own if first else out.at[cls], out.at[cls], ss.at[slot], recv.at[cls], target)

    keep = pltpu.make_async_copy(own, out.at[p], local)
    sends = []

    def send(cls, slot, target, first=False):
        copy = copy_of(cls, slot, target, first)
        copy.start()
        sends.append(copy)

    def arrived(cls):
        copy_of(cls, 0, at.peer(1)).wait_recv()

    send(p, 0, at.peer(at.b1), True)
    send(p, 1, at.peer(at.b2), True)
    send(p, 2, at.peer(1), True)
    keep.start()

    def pass_on():
        arrived(p ^ at.b1)
        send(p ^ at.b1, 3, at.peer(at.b2))
        send(p ^ at.b1, 4, at.peer(1))
        arrived(p ^ at.b2)
        send(p ^ at.b2, 5, at.peer(1))
        arrived(p ^ at.b1 ^ at.b2)
        send(p ^ at.b1 ^ at.b2, 6, at.peer(1))

    def finish():
        for bits in (1, 3, 5, 7):
            arrived(p ^ bits)
        for copy in sends:
            copy.wait_send()
        keep.wait()

    return pass_on, finish


def step_kernel(
    x_ref, up_ref, gains_ref, cos_ref, low_ref, high_ref, bias_ref, wq, wk, wo, wv, wg_in, wu_in, wd_in,
    m_q, m_k, m_o, m_v, m_gate, m_up, m_down,
    out_ref, grad_ref, g_out, o_out, gain_out,
    w01, wg, wu, wd, probs, kv, rot, dkv, c_send, c4r, c2r, c1r, att, gate, lifted,
    xt_in, dy_in, dv_in, xf_all, xa_all, yf_all, yv_all, za_r, ma, mq, mk, gain_s, gain_r, sq, sq_r,
    local, zs, s1, s2, sc, recv, kvs, kvr, ds, dr,
    ls, xs, xr, ps, pr, ys, yr, as_, ar, vs, vr, hs, hr, ozs, ozr, msem, gs, gr, ag_l, ag_s, ag_r, ls_l, ls_r, lr_l, lr_r,
    gsem, rsem, qs, qr, ex_s, ex_r, fx_s, fx_r, og_l, og_s, og_r, free,
):
    at = Place()
    p, f, core, parts = at.p, at.f, at.core, at.parts
    width, tokens = x_ref.shape
    half = w01.shape[2]
    keys = half - width
    group = HEADS // KV_HEADS
    scale = 1.0 / math.sqrt(HEAD)
    rows = width // parts
    columns = 2 * half // parts
    tall = width // 2
    pair = at.peer(1)
    my_rows = pl.ds(pl.multiple_of(f * rows, 16), rows)

    weights = Weights(at, (None, wg_in, wu_in, wd_in), (w01, wg, wu, wd), zs, s1, s2, sc, recv)
    keep = [
        pltpu.make_async_copy(wg_in, wg.at[my_rows], local.at[0]),
        pltpu.make_async_copy(wu_in, wu.at[my_rows], local.at[1]),
        pltpu.make_async_copy(
            wd_in, wd.at[:, pl.ds(pl.multiple_of(f * columns, 128), columns)], local.at[2]
        ),
    ]

    def moment(what):
        for cls in range(CLASSES):
            @pl.when(p == cls)
            def _(cls=cls):
                side = cls % 2
                if cls < 2:
                    pairs = [((m_q, m_o)[cls], mq, 0), ((m_k, m_v)[cls], mk, 1)]
                elif cls < WIDE:
                    whole = m_gate if cls < 4 else m_up
                    pairs = [(whole.at[:, pl.ds(side * half, half)], ma, 0)]
                else:
                    pairs = [
                        (
                            m_down.at[pl.ds(side * tall + t * rows, rows)],
                            ma.at[:, pl.ds(t * columns, columns)],
                            t,
                        )
                        for t in range(2)
                    ]
                for src, dst, index in pairs:
                    getattr(pltpu.make_async_copy(src, dst, msem.at[index]), what)()

    w01[0, my_rows, :width] = wq[...]
    w01[0, my_rows, width:] = wk[...].T
    w01[1, my_rows, :width] = wo[...]
    w01[1, my_rows, width:] = wv[...].T
    at.barrier(bits=range(1, CLASSES))
    for index in range(4):
        weights.along(index)
    for copy in keep:
        copy.start()
    moment("start")

    residual = x_ref[...].astype(F32).T
    upstream = up_ref[...].astype(F32).T
    inverse_first = lax.rsqrt(jnp.mean(residual * residual, axis=-1, keepdims=True) + EPS)
    normed_first = (residual * inverse_first * gains_ref[0:1, :]).astype(BF16)
    xt_in[0] = normed_first.T
    xt_in[3] = up_ref[...]

    weights.first(0)
    weights.second(0)
    weights.first(1)
    weights.third(0)
    weights.ready(0)

    def turn(value, sign):
        tiles = []
        for tile in range(half // 128):
            part = value[:, tile * 128 : (tile + 1) * 128]
            swapped = pltpu.roll(part, HEAD // 2, 1) * low_ref[...] + pltpu.roll(part, 128 - HEAD // 2, 1) * high_ref[...]
            tiles.append(part * cos_ref[...] + swapped if sign > 0 else part * cos_ref[...] - swapped)
        return tiles

    qk = jnp.dot(normed_first, w01[0], preferred_element_type=F32)
    for tile, value in enumerate(turn(qk, 1)):
        rot[:, tile * 128 : (tile + 1) * 128] = value.astype(BF16)
    values = jnp.dot(normed_first, w01[1, :, width:], preferred_element_type=F32).astype(BF16)
    kv[p, :, :keys] = rot[:, width:]
    kv[p, :, keys:] = values

    def block(q, slot, target):
        return remote(kv.at[q], kv.at[q], kvs.at[slot], kvr.at[q], target)

    sent = [block(p, 0, at.peer(at.b1)), block(p, 1, at.peer(at.b2)), block(p, 2, at.peer(1))]
    for copy in sent:
        copy.start()

    def pass_keys(q, slots):
        block(q, 0, at.peer(1)).wait_recv()
        for slot, target in slots:
            copy = block(q, slot, target)
            copy.start()
            sent.append(copy)

    weights.second(1)
    pass_keys(p ^ at.b1, [(3, at.peer(at.b2)), (4, at.peer(1))])
    pass_keys(p ^ at.b2, [(5, at.peer(1))])
    weights.first(2)
    pass_keys(p ^ at.b1 ^ at.b2, [(6, at.peer(1))])
    for bits in (1, 3, 5, 7):
        pass_keys(p ^ bits, [])
    weights.third(1)

    def keys_of(g):
        return kv[:, :, g * HEAD : (g + 1) * HEAD].reshape(CLASSES * tokens, HEAD)

    def values_of(g):
        return kv[:, :, keys + g * HEAD : keys + (g + 1) * HEAD].reshape(CLASSES * tokens, HEAD)

    def heads_of(ref, g):
        return jnp.concatenate([ref[:, h * HEAD : (h + 1) * HEAD] for h in range(g * group, (g + 1) * group)], axis=0)

    def attend(g):
        scores = contract(keys_of(g), heads_of(rot, g), 1, 1) * scale
        bias = bias_ref[...].astype(F32)
        scores = scores + jnp.concatenate([bias] * group, axis=1)
        top = jnp.max(scores, axis=0, keepdims=True)
        expo = jnp.exp(scores - top)
        total = jnp.sum(expo, axis=0, keepdims=True)
        chance = expo * (1.0 / total)
        probs[g] = chance
        mixed = contract(values_of(g), chance.astype(BF16), 0, 0)
        turned = mixed.T.astype(BF16)
        for h in range(group):
            at_lane = (g * group + h) * HEAD
            att[:, at_lane : at_lane + HEAD] = turned[h * tokens : (h + 1) * tokens]

    attend(0)
    attend(1)
    weights.second(2)
    attend(2)
    weights.first(3)
    attend(3)
    weights.third(2)
    attend(4)
    for copy in keep:
        copy.wait()
    weights.ready(1)

    xt_in[1] = att[...].T
    middle = residual + jnp.dot(att[...], w01[1, :, :width], preferred_element_type=F32)
    inverse_second = lax.rsqrt(jnp.mean(middle * middle, axis=-1, keepdims=True) + EPS)
    normed_second = (middle * inverse_second * gains_ref[1:2, :]).astype(BF16)
    xt_in[2] = normed_second.T
    weights.second(3)
    gate[...] = jnp.dot(normed_second, wg[...], preferred_element_type=F32)
    weights.third(3)

    def tokens_of(q):
        return pl.ds(pl.multiple_of(q * tokens, tokens), tokens)

    def kind_of(q):
        return jnp.where(q < 2, 0, jnp.where(q < WIDE, 2, 3))

    own_x = pltpu.make_async_copy(xt_in.at[kind_of(p)], xf_all.at[:, tokens_of(p)], ls.at[0])

    def x_move(bits):
        q = p ^ bits
        return remote(xt_in.at[kind_of(q)], xf_all.at[:, tokens_of(p)], xs.at[bits], xr.at[p], at.peer(bits))

    def a_move():
        return remote(xt_in.at[1], xa_all.at[:, tokens_of(p)], as_, ar.at[p], at.peer(p ^ 1))

    def own_a():
        return pltpu.make_async_copy(xt_in.at[1], xa_all.at[:, tokens_of(p)], ls.at[1])

    def y_move(bits):
        q = p ^ bits
        return remote(dy_in.at[q], yf_all.at[tokens_of(p)], ys.at[bits], yr.at[p], at.peer(bits))

    def own_y():
        return pltpu.make_async_copy(dy_in.at[p], yf_all.at[tokens_of(p)], ls.at[2])

    def v_move():
        return remote(dv_in, yv_all.at[tokens_of(p)], vs, vr.at[p], at.peer(p ^ 1))

    def own_v():
        return pltpu.make_async_copy(dv_in, yv_all.at[tokens_of(p)], ls.at[3])

    own_x.start()
    for bits in (2, 4, 6):
        x_move(bits).start()
    pl.when(p != 1)(lambda: a_move().start())
    pl.when(p == 1)(lambda: own_a().start())

    def give_y(bits, low, high):
        q = p ^ bits

        @pl.when((q >= low) & (q < high))
        def _():
            y_move(bits).start()

    weights.ready(2)
    for side in range(2):
        lifted[side * tokens : (side + 1) * tokens] = jnp.dot(
            normed_second, wu[:, side * half : (side + 1) * half], preferred_element_type=F32
        )

    def lift():
        return jnp.concatenate([lifted[:tokens], lifted[tokens:]], axis=1)

    hidden = (gate[...] * jax.nn.sigmoid(gate[...]) * lift()).astype(BF16)
    dy_in[6] = hidden[:, :half]
    dy_in[7] = hidden[:, half:]
    for bits in range(1, CLASSES):
        give_y(bits, WIDE, CLASSES)
    weights.ready(3)

    grad_hidden = jnp.dot(upstream.astype(BF16), wd[...], preferred_element_type=F32)
    sigma = jax.nn.sigmoid(gate[...])
    grad_gate = (grad_hidden * lift() * sigma * (1.0 + gate[...] * (1.0 - sigma))).astype(BF16)
    grad_lifted = (grad_hidden * gate[...] * sigma).astype(BF16)
    for side in range(2):
        lanes = slice(side * half, (side + 1) * half)
        dy_in[2 + side] = grad_gate[:, lanes]
        dy_in[4 + side] = grad_lifted[:, lanes]
    for bits in range(1, CLASSES):
        give_y(bits, 2, WIDE)

    out_ref[...] = (middle + contract(hidden, wd[...], 1, 1)).T.astype(BF16)
    weights.finish()
    grad_normed = contract(grad_gate, wg[...], 1, 1) + contract(grad_lifted, wu[...], 1, 1)
    pl.semaphore_signal(free.at[0], inc=1, device_id=pair, device_id_type=MESH)

    def norm_back(value, inverse, gain, incoming):
        scaled = incoming * gain
        mean = jnp.mean(scaled * value, axis=-1, keepdims=True)
        through = inverse * scaled - value * (inverse * inverse * inverse) * mean
        return through, jnp.sum(incoming * value * inverse, axis=0, keepdims=True)

    through, gain_second = norm_back(middle, inverse_second, gains_ref[1:2, :], grad_normed)
    gain_s[0] = jnp.zeros(gain_s.shape[1:], F32)
    gain_s[0, 1:2, :] = gain_second
    grad_middle = upstream + through
    grad_branch = grad_middle.astype(BF16)
    dy_in[1, :, :width] = grad_branch
    dy_in[1, :, width:] = jnp.zeros((tokens, keys), BF16)
    att[...] = contract(grad_branch, w01[1, :, :width], 1, 1).astype(BF16)

    for bits in range(1, CLASSES):
        give_y(bits, 1, 2)

    own = lifted.at[pl.ds(0, rows)]

    def swap(slot, target):
        return remote(gain_s.at[slot], gain_r.at[slot], gs.at[slot], gr.at[slot], target)

    def order(i):
        return lax.rem(f + 1 + i, parts)

    cut = width // 128 * 128
    part_lanes = (pl.ds(0, cut), pl.ds(cut, half - cut))
    parts_early = (lambda: p >= 1, lambda: p >= 2)
    parts_late = (lambda: p < 1, lambda: p < 2)

    def room(r):
        return wd.at[pl.ds(pl.multiple_of(r * rows, 16), rows), pl.ds(half, half)]

    def line(r, source, part):
        lanes = part_lanes[part]
        return remote(
            room(r).at[:, lanes], za_r.at[(r ^ source) - 1, :, lanes], ozs.at[part, r], ozr.at[part, source], (at.c, r)
        )

    def arrival(j, part):
        lanes = part_lanes[part]
        return remote(
            room(f).at[:, lanes], za_r.at[j - 1, :, lanes], ozs.at[part, f], ozr.at[part, f ^ j], at.along(j)
        )

    middle_token = CLASSES // 2 * tokens

    def sides_of():
        return [
            remote(
                yf_all.at[pl.ds(side * middle_token, middle_token)],
                wu.at[pl.ds(0, middle_token), pl.ds(side * half, half)],
                hs.at[side], hr.at[side], pair,
            )
            for side in range(2)
        ]

    def produce(r, put):
        at_rows = pl.ds(pl.multiple_of(r * rows, 16), rows)
        every = slice(0, half)

        @pl.when(p == 1)
        def _():
            put(slice(0, width), jnp.dot(xa_all[at_rows, :], yf_all[:, pl.ds(0, width)], preferred_element_type=F32))

        @pl.when((p != 1) & (p < WIDE))
        def _():
            put(every, jnp.dot(xf_all[at_rows, :], yf_all[...], preferred_element_type=F32))

        @pl.when(p >= WIDE)
        def _():
            side, start = lax.div(r * columns, half), pl.multiple_of(lax.rem(r * columns, half), 128)
            for t in range(2):
                part_rows = pl.ds(pl.multiple_of((p - WIDE) * tall + t * rows, 16), rows)
                lanes = slice(t * columns, (t + 1) * columns)

                @pl.when(side == core)
                def _():
                    put(
                        lanes,
                        jnp.dot(xf_all[part_rows, :], yf_all[:, pl.ds(start, columns)], preferred_element_type=F32),
                    )

                @pl.when(side != core)
                def _():
                    put(
                        lanes,
                        jnp.dot(
                            xf_all[part_rows, pl.ds(0, middle_token)],
                            wu[pl.ds(0, middle_token), pl.ds(start, columns)],
                            preferred_element_type=F32,
                        )
                        + jnp.dot(
                            xf_all[part_rows, pl.ds(middle_token, middle_token)],
                            wu[pl.ds(0, middle_token), pl.ds(pl.multiple_of(half + start, 128), columns)],
                            preferred_element_type=F32,
                        ),
                    )

    def keep_chunk(r):
        def put(lanes, value):
            own[:, lanes] = value
            room(r)[:, lanes] = value.astype(BF16)

        return put

    def gradients(conditions):
        for bits in range(1, CLASSES):
            arrived_y(p ^ bits)

        @pl.when(p >= WIDE)
        def _():
            for copy in sides_of():
                copy.start()
            for copy in sides_of():
                copy.wait()

        def step_of(i, carry):
            r = order(i)
            produce(r, keep_chunk(r))
            for part in range(2):
                pl.when((i < parts - 1) & conditions[part]())(lambda part=part: line(r, f, part).start())
            return carry

        lax.fori_loop(0, parts, step_of, 0)

    def value_gradient():
        for q in range(CLASSES):
            if q != 1:
                remote(dv_in, yv_all.at[tokens_of(q)], vs, vr.at[q], pair).wait_recv()

        def step_of(i, carry):
            r = order(i)
            at_rows = pl.ds(pl.multiple_of(r * rows, 16), rows)
            value = jnp.dot(xf_all[at_rows, :], yv_all[...], preferred_element_type=F32)

            @pl.when(i < parts - 1)
            def _():
                room(r)[:, pl.ds(width, keys)] = value[:, :keys].astype(BF16)
                line(r, f, 1).start()

            @pl.when(i == parts - 1)
            def _():
                own[:, pl.ds(width, keys)] = value[:, :keys]

            return carry

        lax.fori_loop(0, parts, step_of, 0)

    def arrived_y(q):
        remote(dy_in.at[0], yf_all.at[tokens_of(q)], ys.at[1], yr.at[q], pair).wait_recv()

    def arrived_x(q):
        remote(xt_in.at[0], xf_all.at[:, tokens_of(q)], xs.at[2], xr.at[q], pair).wait_recv()

    def x_pair(bits):
        q = p ^ bits
        return remote(xf_all.at[:, tokens_of(q)], xf_all.at[:, tokens_of(q)], ps.at[bits], pr.at[q], pair)

    def attend_back(g):
        chance = probs[g]
        out_grad = heads_of(att, g)
        query = heads_of(rot, g)
        grad_probs = contract(values_of(g), out_grad, 1, 1)
        delta = jnp.sum(grad_probs * chance, axis=0, keepdims=True)
        grad_scores = (chance * (grad_probs - delta)).astype(BF16)
        grad_values = jnp.dot(chance.astype(BF16), out_grad, preferred_element_type=F32)
        grad_keys = jnp.dot(grad_scores, query, preferred_element_type=F32) * scale
        dkv[:, :, g * HEAD : (g + 1) * HEAD] = grad_keys.reshape(CLASSES, tokens, HEAD)
        dkv[:, :, keys + g * HEAD : keys + (g + 1) * HEAD] = grad_values.reshape(CLASSES, tokens, HEAD)
        turned = contract(keys_of(g), grad_scores, 0, 0).T * scale
        for h in range(group):
            at_lane = (g * group + h) * HEAD
            gate[:, at_lane : at_lane + HEAD] = turned[h * tokens : (h + 1) * tokens]

    for g in range(KV_HEADS):
        attend_back(g)

    def halve(bit, rest, sbuf, rbuf, index, between=None):
        for i, bits in enumerate(rest):
            sbuf[i // 2, :, pl.ds(i % 2 * 2 * keys, 2 * keys)] = dkv[p ^ bit ^ bits].astype(BF16)
        copy = remote(sbuf, rbuf, ds.at[index], dr.at[index], at.peer(bit))
        copy.start()
        if between is not None:
            between()
        copy.wait()
        for i, bits in enumerate(rest):
            dkv[p ^ bits] = dkv[p ^ bits] + rbuf[i // 2, :, pl.ds(i % 2 * 2 * keys, 2 * keys)].astype(F32)

    own_x.wait()
    for bits in (2, 4, 6):
        arrived_x(p ^ bits)
    for bits in (0, 2, 4, 6):
        x_pair(bits).start()

    def early():
        for bits in (0, 2, 4, 6):
            remote(
                xf_all.at[:, tokens_of(p ^ bits ^ 1)], xf_all.at[:, tokens_of(p ^ bits ^ 1)],
                ps.at[bits], pr.at[p ^ bits ^ 1], pair,
            ).wait_recv()
        pl.semaphore_wait(free.at[0], 1)

        @pl.when(p == 1)
        def _():
            own_a().wait()
            for q in range(CLASSES):
                if q != 1:
                    remote(xt_in.at[1], xa_all.at[:, tokens_of(q)], as_, ar.at[q], pair).wait_recv()

        @pl.when(p >= 1)
        def _():
            own_y().start()
            own_y().wait()
            gradients(parts_early)

    halve(1, (0, 2, 4, 6), c_send, c4r, 0)
    halve(at.b1, (0, at.b2), c4r.at[pl.ds(0, 1)], c2r, 1, early)
    halve(at.b2, (0,), c4r.at[pl.ds(1, 1), :, pl.ds(0, 2 * keys)], c1r, 2)

    gate[:, width:half] = dkv[p, :, :keys]
    for tile, value in enumerate(turn(gate[:, :half], -1)):
        dy_in[0, :, tile * 128 : (tile + 1) * 128] = value.astype(BF16)
    dv_in[...] = jnp.zeros(dv_in.shape, BF16)
    dv_in[:, :keys] = dkv[p, :, keys:].astype(BF16)
    for bits in range(1, CLASSES):
        give_y(bits, 0, 1)
    pl.when(p != 1)(lambda: v_move().start())
    pl.when(p == 1)(lambda: own_v().start())
    grad_normed = contract(dy_in[0], w01[0], 1, 1)
    grad_normed = grad_normed + contract(dv_in[:, :keys], w01[1, :, width:], 1, 1)
    through, gain_first = norm_back(residual, inverse_first, gains_ref[0:1, :], grad_normed)
    gain_s[0, 0:1, :] = gain_first
    swaps = [swap(0, pair)]
    swaps[0].start()
    grad_ref[...] = (grad_middle + through).T
    @pl.when(p == 0)
    def _():
        own_y().start()
        own_y().wait()
        gradients(parts_late)

    @pl.when(p == 1)
    def _():
        own_v().wait()
        value_gradient()

    swaps[0].wait()
    gain_s[1] = gain_s[0] + gain_r[0]
    swaps.append(swap(1, at.peer(2)))
    swaps[1].start()
    for bits in (0, 2, 4, 6):
        x_pair(bits).wait_send()
    for bits in range(1, CLASSES):
        y_move(bits).wait_send()
    for bits in (2, 4, 6):
        x_move(bits).wait_send()

    @pl.when(p != 1)
    def _():
        a_move().wait_send()
        v_move().wait_send()

    swaps[1].wait()
    gain_s[2] = gain_s[1] + gain_r[1]
    swaps.append(swap(2, at.peer(4)))
    swaps[2].start()

    moment("wait")

    @pl.when(p < 2)
    def _():
        ma[:, :width] = mq[...]
        ma[:, width:] = mk[...].T

    sall = wd.at[:, pl.ds(0, half)]
    ga, pa = (w01.at[1, pl.ds((parts - 1 - i) * rows, rows)] for i in range(2))

    def shard(index, part):
        return sall.at[pl.ds(pl.multiple_of(index * rows, 16), rows), part_lanes[part]]

    def rightward(index, part):
        here = shard(index, part)
        return remote(here, here, ls_r.at[part, index], lr_r.at[part, index], (at.c, lax.rem(f + 1, parts)))

    def leftward(index, part):
        here = shard(index, part)
        return remote(here, here, ls_l.at[part, index], lr_l.at[part, index], (at.c, lax.rem(f + parts - 1, parts)))

    can_right = f < parts - 1
    can_left = f > 0

    def settle_part(part):
        lanes = part_lanes[part]
        total = own[:, lanes]
        for j in range(1, parts):
            arrival(j, part).wait_recv()
            total = total + za_r[j - 1, :, lanes].astype(F32)
        ga[:, lanes] = total.astype(BF16)
        sall[my_rows, lanes] = (MOMENTUM * ma[:, lanes] + total).astype(BF16)
        pl.when(can_right)(lambda: rightward(f, part).start())
        pl.when(can_left)(lambda: leftward(f, part).start())

    def hop_part(hop, part):
        @pl.when(f - hop >= 0)
        def _():
            rightward(f - hop, part).wait_recv()
            pl.when(can_right)(lambda: rightward(f - hop, part).start())

        @pl.when(f + hop < parts)
        def _():
            leftward(f + hop, part).wait_recv()
            pl.when(can_left)(lambda: leftward(f + hop, part).start())

    for conditions in (parts_early, parts_late):
        for part in range(2):
            pl.when(conditions[part]())(lambda part=part: settle_part(part))
        for hop in range(1, parts):
            for part in range(2):
                pl.when(conditions[part]())(lambda hop=hop, part=part: hop_part(hop, part))

    pass_on, finish = spread_even(at, ga, g_out, ag_l, ag_s, ag_r)
    swaps[2].wait()
    gain_s[3] = gain_s[2] + gain_r[2]
    line_gain = [
        remote(gain_s.at[3], gain_r.at[3 + j], gs.at[3 + j], gr.at[3 + j], at.along(j)) for j in range(1, parts)
    ]
    for copy in line_gain:
        copy.start()

    pass_on()

    for part in range(2):
        for j in range(1, parts):
            line(f ^ j, f, part).wait_send()
        pl.when(can_right)(lambda: rightward(f, part).wait_send())
        pl.when(can_left)(lambda: leftward(f, part).wait_send())
        for hop in range(1, parts):
            pl.when((f - hop >= 0) & can_right)(lambda hop=hop: rightward(f - hop, part).wait_send())
            pl.when((f + hop < parts) & can_left)(lambda hop=hop: leftward(f + hop, part).wait_send())
    pl.semaphore_signal(free.at[1], inc=1, device_id=pair, device_id_type=MESH)
    pl.semaphore_wait(free.at[1], 1)

    x = w01.at[0]
    wide_gram = 1024
    gram_s, g = wg.at[:, pl.ds(0, wide_gram)], wg.at[:, pl.ds(wide_gram, wide_gram)]
    poly, xf = wd.at[:, pl.ds(0, wide_gram)], wd.at[:, pl.ds(half, columns)]
    step = width // 4

    def gram_r(slot):
        return wu.at[:, pl.ds(slot * wide_gram, wide_gram)]

    def scale_of(total):
        return 1.0 / (jnp.sqrt(total) + 1e-07)

    def normal(ref, inverse):
        ref[...] = rounded(ref[...].astype(F32) * inverse)

    def exchange(slot, r):
        part = pl.ds(r * step, step)
        return remote(gram_s.at[part], gram_r(slot).at[part], gsem.at[r], rsem.at[slot, r], pair)

    def poly_of(start, count):
        part = g[pl.ds(start, count), pl.ds(0, width)]
        square = jnp.dot(part, g[:, pl.ds(0, width)], preferred_element_type=F32)
        return rounded(NS_B * part.astype(F32) + NS_C * square)

    def fill_poly():
        for r in range(4):
            poly[pl.ds(r * step, step), pl.ds(0, width)] = poly_of(r * step, step)

    near = parts // 2
    mine_at = core * near
    last_core = lax.div(f, near)
    f_lanes = pl.ds(pl.multiple_of(lax.rem(f, near) * columns, 128), columns)

    kt = wd.at[pl.ds(0, keys), pl.ds(half + 256, wide_gram)]

    def xo(i):
        return w01.at[1, pl.ds(i * rows, rows)]

    def give():
        return [
            remote(
                sall.at[pl.ds(pl.multiple_of(((1 - core) * near + i) * rows, 16), rows)],
                xo(i), ex_s.at[i], ex_r.at[i], pair,
            )
            for i in range(near)
        ]

    def give_last():
        return remote(x.at[:, f_lanes], xf, fx_s, fx_r, pair)

    @pl.when(p >= 2)
    def _():
        @pl.when(p < WIDE)
        def _():
            x[...] = sall[...]

        @pl.when(p >= WIDE)
        def _():
            copies = give()
            for copy in copies:
                copy.start()
            for i in range(near):
                part = sall[pl.ds(pl.multiple_of((mine_at + i) * rows, 16), rows), :]
                for t in range(2):
                    x[pl.ds(pl.multiple_of(core * tall + t * rows, 16), rows), pl.ds(i * columns, columns)] = part[
                        :, t * columns : (t + 1) * columns
                    ]
            for i, copy in enumerate(copies):
                copy.wait()
                part = xo(i)
                for t in range(2):
                    x[pl.ds(pl.multiple_of((1 - core) * tall + t * rows, 16), rows), pl.ds(i * columns, columns)] = part[
                        :, pl.ds(t * columns, columns)
                    ]

        wide = x[...].astype(F32)
        sq[...] = jnp.broadcast_to(jnp.sum(wide * wide), sq.shape)
        copy = remote(sq, sq_r, qs, qr, pair)
        copy.start()
        copy.wait()
        normal(x, scale_of(sq[...] + sq_r[...])[:1, :1])

        def grams(slot):
            for r in range(4):
                gram_s[pl.ds(r * step, step), pl.ds(0, width)] = rounded(
                    contract(x[pl.ds(r * step, step), :], x[...], 1, 1)
                )
                exchange(slot, r).start()
            for r in range(4):
                part = pl.ds(r * step, step)
                exchange(slot, r).wait()
                g[part, pl.ds(0, width)] = rounded(
                    gram_s[part, pl.ds(0, width)].astype(F32) + gram_r(slot)[part, pl.ds(0, width)].astype(F32)
                )

        def iterate(slot):
            grams(slot)
            fill_poly()
            for tile in range(half // 256):
                part = pl.ds(tile * 256, 256)
                x[:, part] = rounded(
                    NS_A * x[:, part].astype(F32) + jnp.dot(poly[:, pl.ds(0, width)], x[:, part], preferred_element_type=F32)
                )

        def iterate_twice(it, carry):
            iterate(0)
            iterate(1)
            return carry

        lax.fori_loop(0, (NS_ITERS - 1) // 2, iterate_twice, 0)

        @pl.when((p >= WIDE) & (core == last_core))
        def _():
            give_last().start()
            xf[...] = x[:, f_lanes]

        grams(0)

        @pl.when(p < WIDE)
        def _():
            part = poly_of(pl.multiple_of(f * rows, 16), rows)
            pa[...] = rounded(NS_A * x[my_rows, :].astype(F32) + jnp.dot(part, x[...], preferred_element_type=F32))

        @pl.when(p >= WIDE)
        def _():
            pl.when(core == last_core)(lambda: give_last().wait_send())
            pl.when(core != last_core)(lambda: give_last().wait_recv())
            for t in range(2):
                top = pl.multiple_of(core * tall + t * rows, 16)
                part = poly_of(top, rows)
                pa[:, t * columns : (t + 1) * columns] = rounded(
                    NS_A * xf[pl.ds(top, rows), :].astype(F32) + jnp.dot(part, xf[...], preferred_element_type=F32)
                )

    @pl.when(p < 2)
    def _():
        x[...] = sall[...]
        kt[:, pl.ds(0, width)] = x[:, pl.ds(width, keys)].T
        turned = kt[:, pl.ds(0, width)].astype(F32)
        kt[:, pl.ds(0, width)] = rounded(turned * scale_of(jnp.sum(turned * turned)))
        wide = x[:, pl.ds(0, width)].astype(F32)
        x[:, pl.ds(0, width)] = rounded(wide * scale_of(jnp.sum(wide * wide)))

        def narrow_step(it, carry):
            now = kt[:, pl.ds(0, width)]
            gram = rounded(contract(now, now, 1, 1))
            turned = rounded(NS_B * gram.astype(F32) + NS_C * jnp.dot(gram, gram, preferred_element_type=F32))
            kt[:, pl.ds(0, width)] = rounded(
                NS_A * now.astype(F32) + jnp.dot(turned, now, preferred_element_type=F32)
            )
            return carry

        lax.fori_loop(0, NS_ITERS, narrow_step, 0)

        def gram_of():
            for r in range(4):
                part = pl.ds(r * step, step)
                g[part, pl.ds(0, width)] = rounded(contract(x[part, pl.ds(0, width)], x[:, pl.ds(0, width)], 1, 1))

        def square_step(it, carry):
            gram_of()
            fill_poly()
            x[:, pl.ds(0, width)] = rounded(
                NS_A * x[:, pl.ds(0, width)].astype(F32) + jnp.dot(poly[:, pl.ds(0, width)], x[:, pl.ds(0, width)], preferred_element_type=F32)
            )
            return carry

        lax.fori_loop(0, NS_ITERS - 1, square_step, 0)
        gram_of()
        part = poly_of(pl.multiple_of(f * rows, 16), rows)
        square = rounded(
            NS_A * x[my_rows, pl.ds(0, width)].astype(F32) + jnp.dot(part, x[:, pl.ds(0, width)], preferred_element_type=F32)
        )
        x[:, pl.ds(width, keys)] = kt[:, pl.ds(0, width)].T
        pa[:, :width] = square
        pa[:, width:] = x[my_rows, pl.ds(width, keys)]

    out_on, out_finish = spread_even(at, pa, o_out, og_l, og_s, og_r)
    total = gain_s[3]
    for j in range(1, parts):
        line_gain[j - 1].wait()
        total = total + gain_r[3 + j]
    gain_out[...] = total
    finish()
    out_on()
    for copy in sent:
        copy.wait_send()
    out_finish()


def step_pass(x, up, gains, tables, bias, shards, moments):
    parts = lax.axis_size("fsdp")
    width, tokens = x.shape
    half = shards[4].shape[1] // 2
    rows = width // parts
    keys = half - width
    near = parts // 2
    dma = pltpu.SemaphoreType.DMA
    vm = pltpu.VMEM
    group = HEADS // KV_HEADS
    two = 2 * keys
    n_gain = 3 + parts
    return pl.pallas_call(
        step_kernel,
        out_shape=(
            jax.ShapeDtypeStruct((width, tokens), BF16),
            jax.ShapeDtypeStruct((width, tokens), F32),
            jax.ShapeDtypeStruct((CLASSES, rows, half), BF16),
            jax.ShapeDtypeStruct((CLASSES, rows, half), BF16),
            jax.ShapeDtypeStruct((8, width), F32),
        ),
        in_specs=[VMEM] * 11 + [ANY] * 10,
        out_specs=(VMEM, VMEM, ANY, ANY, VMEM),
        scratch_shapes=[
            vm((2, width, half), BF16),
            vm((width, 2 * half), BF16),
            vm((width, 2 * half), BF16),
            vm((width, 2 * half), BF16),
            vm((KV_HEADS, CLASSES * tokens, group * tokens), F32),
            vm((CLASSES, tokens, two), BF16),
            vm((tokens, half), BF16),
            vm((CLASSES, tokens, two), F32),
            vm((2, tokens, 2 * two), BF16),
            vm((2, tokens, 2 * two), BF16),
            vm((1, tokens, 2 * two), BF16),
            vm((1, tokens, two), BF16),
            vm((tokens, width), BF16),
            vm((tokens, 2 * half), F32),
            vm((2 * tokens, half), F32),
            vm((4, width, tokens), BF16),
            vm((CLASSES, tokens, half), BF16),
            vm((tokens, -(-keys // 128) * 128), BF16),
            vm((width, CLASSES * tokens), BF16),
            vm((width, CLASSES * tokens), BF16),
            vm((CLASSES * tokens, half), BF16),
            vm((CLASSES * tokens, -(-keys // 128) * 128), BF16),
            vm((parts - 1, rows, half), BF16),
            vm((rows, half), F32),
            vm((rows, width), F32),
            vm((keys, rows), F32),
            vm((4, 8, width), F32),
            vm((n_gain, 8, width), F32),
            vm((8, 128), F32),
            vm((8, 128), F32),
            dma((3,)), dma((4, parts)), dma((4, parts)), dma((4, 2, parts)), dma((4, 4, parts)),
            dma((4, CLASSES, parts)), dma((7,)), dma((CLASSES,)), dma((3,)), dma((3,)),
            dma((4,)), dma((CLASSES,)), dma((CLASSES,)), dma((CLASSES,)), dma((CLASSES,)),
            dma((CLASSES,)), dma((CLASSES,)), dma, dma((CLASSES,)), dma, dma((CLASSES,)),
            dma((2,)), dma((2,)), dma((2, parts)), dma((2, parts)),
            dma((2,)), dma((n_gain,)), dma((n_gain,)),
            dma, dma((7,)), dma((CLASSES,)),
            dma((2, parts)), dma((2, parts)), dma((2, parts)), dma((2, parts)),
            dma((4,)), dma((2, 4)), dma, dma,
            dma((near,)), dma((near,)), dma, dma,
            dma, dma((7,)), dma((CLASSES,)), pltpu.SemaphoreType.REGULAR((2,)),
        ],
        compiler_params=pltpu.CompilerParams(
            collective_id=3, has_side_effects=True, vmem_limit_bytes=63 << 20
        ),
        name="step_pass",
    )(x, up, gains, *tables, bias, *shards, *moments)


def settle_wide(factors, *refs):
    gs, os = refs[0], refs[1]
    ms, ws, outs = refs[2:6], refs[6:10], refs[10:]
    width = ms[0].shape[1]
    half = gs.shape[2]

    def one(index, g, o, lanes):
        grad, moment, weight = (outs[3 * index + i] for i in range(3))
        value = g.astype(F32)
        grad[:, lanes] = value
        moment[:, lanes] = MOMENTUM * ms[index][:, lanes] + value
        weight[:, lanes] = ws[index][:, lanes].astype(F32) + factors[index] * o.astype(F32)

    for index in range(2):
        one(index, gs[index, :, :width], os[index, :, :width], slice(0, width))
    for index in range(2):
        for side in range(2):
            cls = 2 + 2 * index + side
            one(2 + index, gs[cls], os[cls], slice(side * half, (side + 1) * half))


def settle_turned(factors, g_tall, o_tall, g_pair, o_pair, *refs):
    ms, ws, outs = refs[0:3], refs[3:6], refs[6:]
    keys = ms[1].shape[0]

    def one(index, g, o):
        grad, moment, weight = (outs[3 * index + i] for i in range(3))
        grad[...] = g
        moment[...] = MOMENTUM * ms[index][...] + g
        weight[...] = ws[index][...].astype(F32) + factors[index] * o

    one(0, g_tall[0].astype(F32), o_tall[0].astype(F32))

    @pl.when(pl.program_id(0) == 0)
    def _():
        for index in range(2):
            start = g_pair.shape[2] - keys
            one(1 + index, g_pair[index, :, start:].astype(F32).T, o_pair[index, :, start:].astype(F32).T)


def settle(g, o, moments, shards, factors):
    m_q, m_k, m_o, m_v, m_gate, m_up, m_down = moments
    w_q, w_k, w_o, w_v, w_gate, w_up, w_down = shards
    f_q, f_k, f_v, f_o, f_gate, f_up, f_down = factors
    _, rows, half = g.shape
    width, columns = m_down.shape
    block = 48 if rows % 48 == 0 else rows
    piece = pl.BlockSpec((WIDE, block, half), lambda i: (0, i, 0))

    def row_block(array):
        return pl.BlockSpec((block, array.shape[1]), lambda i: (i, 0))

    def result(arrays):
        return tuple(jax.ShapeDtypeStruct(array.shape, F32) for array in arrays for _ in range(3))

    wide = (m_q, m_o, m_gate, m_up)
    first = pl.pallas_call(
        functools.partial(settle_wide, (f_q, f_o, f_gate, f_up)),
        grid=(rows // block,),
        out_shape=result(wide),
        in_specs=[piece, piece] + [row_block(array) for array in wide] * 2,
        out_specs=tuple(row_block(array) for array in wide for _ in range(3)),
        compiler_params=pltpu.CompilerParams(vmem_limit_bytes=48 << 20),
        name="settle_wide",
    )(g, o, *wide, w_q, w_o, w_gate, w_up)

    turned = (m_down, m_k, m_v)
    halves = half // columns
    tile = pl.BlockSpec((1, rows, columns), lambda i: (WIDE + i // halves, 0, i % halves))
    both = pl.BlockSpec((2, rows, half), lambda i: (0, 0, 0))
    specs = [pl.BlockSpec((rows, columns), lambda i: (i, 0))] + [
        pl.BlockSpec(array.shape, lambda i: (0, 0)) for array in turned[1:]
    ]
    second = pl.pallas_call(
        functools.partial(settle_turned, (f_down, f_k, f_v)),
        grid=(width // rows,),
        out_shape=result(turned),
        in_specs=[tile, tile, both, both] + specs * 2,
        out_specs=tuple(spec for spec in specs for _ in range(3)),
        compiler_params=pltpu.CompilerParams(vmem_limit_bytes=48 << 20),
        name="settle_turned",
    )(g, o, g, o, *turned, w_down, w_k, w_v)
    q, out, gate, up = (first[3 * i : 3 * i + 3] for i in range(4))
    down, k, v = (tuple(item.T for item in second[3 * i : 3 * i + 3]) for i in range(3))
    return list(zip(q, k, v, out, gate, up, down))


def rotary_tables(positions, width):
    half = width // 2
    frequency = THETA ** (-(jnp.arange(half, dtype=jnp.float32) * 2.0 / width))
    angle = positions.astype(jnp.float32)[:, None] * frequency[None, :]
    return (jnp.cos(angle)[:, None, :], jnp.sin(angle)[:, None, :])


def rotate(value, cosine, sine):
    half = value.shape[-1] // 2
    first = value[..., :half]
    second = value[..., half:]
    return jnp.concatenate(
        [first * cosine - second * sine, second * cosine + first * sine], axis=-1
    )


def unrotate(incoming, cosine, sine):
    half = incoming.shape[-1] // 2
    upper = incoming[..., :half]
    lower = incoming[..., half:]
    return jnp.concatenate([upper * cosine + lower * sine, lower * cosine - upper * sine], axis=-1)


def norm_forward(residual, gain):
    inverse = lax.rsqrt(jnp.mean(residual * residual, axis=-1, keepdims=True) + EPS)
    return ((residual * inverse * gain).astype(jnp.bfloat16), inverse)


def norm_backward(residual, inverse, gain, incoming):
    scaled = incoming * gain
    through = inverse * scaled - residual * inverse**3 * jnp.mean(
        scaled * residual, axis=-1, keepdims=True
    )
    return (through, jnp.sum(incoming * residual * inverse, axis=0))


def padded(array, axis, parts, count, full):
    if count == full:
        return array
    shape = array.shape
    split = array.reshape(shape[:axis] + (parts, count) + shape[axis + 1 :])
    pads = [(0, 0)] * split.ndim
    pads[axis + 1] = (0, full - count)
    return jnp.pad(split, pads).reshape(shape[:axis] + (parts * full,) + shape[axis + 1 :])


def trimmed(array, axis, parts, count, full):
    if count == full:
        return array
    shape = array.shape
    split = array.reshape(shape[:axis] + (parts, full) + shape[axis + 1 :])
    kept = lax.slice_in_dim(split, 0, count, axis=axis + 1)
    return kept.reshape(shape[:axis] + (parts * count,) + shape[axis + 1 :])


def plain_layer(
    layer_input, output_grad, wide, tall, norm_gains, block_order, sizes
):
    parts, width, half, kv, short, full, high = sizes
    hidden_size = 2 * half
    rows = layer_input.shape[1]
    block = rows // 2
    group = HEADS // KV_HEADS
    scale = 1.0 / math.sqrt(HEAD)
    ctx_place = lax.axis_index("ctx")
    offsets = jnp.arange(block, dtype=jnp.int32)
    own_blocks = lax.dynamic_slice_in_dim(block_order, 2 * ctx_place, 2)
    query_pos = (own_blocks[:, None] * block + offsets[None, :]).reshape(rows)
    key_pos = (block_order[:, None] * block + offsets[None, :]).reshape(-1)

    all_wide, all_tall = gather_weights(wide, tall)
    w_qk, w_ov, w_gate_0, w_gate_1, w_up_0, w_up_1 = [all_wide[i].reshape(width, half) for i in range(WIDE)]
    w_down = [all_tall[i].reshape(half, width) for i in range(2)]

    residual = layer_input[0].astype(jnp.float32)
    normed_first, inverse_first = norm_forward(residual, norm_gains[0])
    qk_pre = jnp.dot(normed_first, w_qk, preferred_element_type=jnp.float32)
    query_pre = qk_pre[:, :width].reshape(rows, HEADS, HEAD)
    key_pre = qk_pre[:, width:].reshape(rows, KV_HEADS, HEAD)
    value_low = (
        jnp.dot(normed_first, w_ov, preferred_element_type=jnp.float32)[:, width:]
        .astype(jnp.bfloat16)
        .reshape(rows, KV_HEADS, HEAD)
    )
    cosine, sine = rotary_tables(query_pos, HEAD)
    query_rot = rotate(query_pre, cosine, sine).astype(jnp.bfloat16)
    key_rot = rotate(key_pre, cosine, sine).astype(jnp.bfloat16)
    keys_all, values_all = (
        lax.all_gather(key_rot, "ctx", axis=0, tiled=True),
        lax.all_gather(value_low, "ctx", axis=0, tiled=True),
    )
    keys_head = keys_all.transpose(1, 0, 2)
    values_head = values_all.transpose(1, 0, 2)
    queries_head = (
        query_rot.reshape(rows, KV_HEADS, group, HEAD)
        .transpose(1, 2, 0, 3)
        .reshape(KV_HEADS, group * rows, HEAD)
    )
    row_pos = jnp.tile(query_pos, group)
    allowed = key_pos[None, :] <= row_pos[:, None]

    def head_forward(item):
        query, key, value = item
        scores = jnp.where(allowed, contract(query, key, 1, 1) * scale, MASKED)
        top = jnp.max(scores, axis=-1, keepdims=True)
        expo = jnp.exp(scores - top)
        total = jnp.sum(expo, axis=-1, keepdims=True)
        probs_low = (expo / total).astype(jnp.bfloat16)
        return (
            jnp.dot(probs_low, value, preferred_element_type=jnp.float32),
            (top + jnp.log(total))[:, 0],
        )

    mixed, log_total = lax.map(head_forward, (queries_head, keys_head, values_head))
    attended = (
        mixed.reshape(KV_HEADS, group, rows, HEAD)
        .transpose(2, 0, 1, 3)
        .reshape(rows, HEADS * HEAD)
        .astype(jnp.bfloat16)
    )
    w_out = w_ov[:, :width]
    middle = residual + jnp.dot(attended, w_out, preferred_element_type=jnp.float32)
    normed_second, inverse_second = norm_forward(middle, norm_gains[1])

    def sides(left, right):
        return jnp.concatenate([left, right], axis=1)

    gate = sides(
        jnp.dot(normed_second, w_gate_0, preferred_element_type=jnp.float32),
        jnp.dot(normed_second, w_gate_1, preferred_element_type=jnp.float32),
    )
    lifted = sides(
        jnp.dot(normed_second, w_up_0, preferred_element_type=jnp.float32),
        jnp.dot(normed_second, w_up_1, preferred_element_type=jnp.float32),
    )
    sigma = jax.nn.sigmoid(gate)
    hidden = (gate * sigma * lifted).astype(jnp.bfloat16)
    hidden_split = hidden.reshape(rows, parts, 2, high)
    hidden_sides = [hidden_split[:, :, i].reshape(rows, half) for i in range(2)]
    layer_output = (
        middle
        + jnp.dot(hidden_sides[0], w_down[0], preferred_element_type=jnp.float32)
        + jnp.dot(hidden_sides[1], w_down[1], preferred_element_type=jnp.float32)
    ).astype(jnp.bfloat16)
    upstream = output_grad[0]
    grad_hidden = jnp.stack(
        [contract(upstream, w_down[i], 1, 1).reshape(rows, parts, high) for i in range(2)], axis=2
    ).reshape(rows, hidden_size)
    grad_gate = (grad_hidden * lifted * sigma * (1.0 + gate * (1.0 - sigma))).astype(jnp.bfloat16)
    grad_lifted = (grad_hidden * gate * sigma).astype(jnp.bfloat16)
    grad_normed_second = (
        contract(grad_gate[:, :half], w_gate_0, 1, 1)
        + contract(grad_gate[:, half:], w_gate_1, 1, 1)
        + contract(grad_lifted[:, :half], w_up_0, 1, 1)
        + contract(grad_lifted[:, half:], w_up_1, 1, 1)
    )
    through_second, gain_second = norm_backward(
        middle, inverse_second, norm_gains[1], grad_normed_second
    )
    grad_middle = upstream.astype(jnp.float32) + through_second
    grad_branch = grad_middle.astype(jnp.bfloat16)
    grad_attended = contract(grad_branch, w_out, 1, 1).astype(jnp.bfloat16)
    grad_heads = (
        grad_attended.reshape(rows, KV_HEADS, group, HEAD)
        .transpose(1, 2, 0, 3)
        .reshape(KV_HEADS, group * rows, HEAD)
    )

    def head_backward(item):
        query, key, value, grad_out, log_row = item
        scores = jnp.where(allowed, contract(query, key, 1, 1) * scale, MASKED)
        probs = jnp.exp(scores - log_row[:, None])
        grad_value_part = contract(probs.astype(jnp.bfloat16), grad_out, 0, 0)
        grad_probs = contract(grad_out, value, 1, 1)
        grad_scores = (
            probs * (grad_probs - jnp.sum(grad_probs * probs, axis=-1, keepdims=True))
        ).astype(jnp.bfloat16)
        grad_query_part = jnp.dot(grad_scores, key, preferred_element_type=jnp.float32) * scale
        grad_key_part = contract(grad_scores, query, 0, 0) * scale
        return (grad_query_part, grad_key_part, grad_value_part)

    grad_query_rot, grad_key_all, grad_value_all = lax.map(
        head_backward, (queries_head, keys_head, values_head, grad_heads, log_total)
    )
    grad_key_own, grad_value_own = (
        lax.psum_scatter(
            grad_key_all.astype(jnp.bfloat16), "ctx", scatter_dimension=1, tiled=True
        ).astype(jnp.float32),
        lax.psum_scatter(
            grad_value_all.astype(jnp.bfloat16), "ctx", scatter_dimension=1, tiled=True
        ).astype(jnp.float32),
    )
    grad_query = (
        unrotate(
            grad_query_rot.reshape(KV_HEADS, group, rows, HEAD)
            .transpose(2, 0, 1, 3)
            .reshape(rows, HEADS, HEAD),
            cosine,
            sine,
        )
        .reshape(rows, HEADS * HEAD)
        .astype(jnp.bfloat16)
    )
    grad_key = (
        unrotate(grad_key_own.transpose(1, 0, 2), cosine, sine)
        .reshape(rows, KV_HEADS * HEAD)
        .astype(jnp.bfloat16)
    )
    grad_value = (
        grad_value_own.transpose(1, 0, 2).reshape(rows, KV_HEADS * HEAD).astype(jnp.bfloat16)
    )
    grad_qk = sides(grad_query, grad_key)
    zero_query = jnp.zeros((rows, width), jnp.bfloat16)
    grad_v = sides(zero_query, grad_value)
    grad_normed_first = contract(grad_qk, w_qk, 1, 1) + contract(grad_v, w_ov, 1, 1)
    through_first, gain_first = norm_backward(
        residual, inverse_first, norm_gains[0], grad_normed_first
    )
    input_gradient = grad_middle + through_first

    xt = jnp.stack([item.T for item in (normed_first, attended, normed_second, upstream)])
    xt = padded(xt, 1, parts, short, full)
    dy = jnp.stack(
        [
            grad_qk,
            sides(grad_branch, jnp.zeros((rows, kv), jnp.bfloat16)),
            grad_gate[:, :half],
            grad_gate[:, half:],
            grad_lifted[:, :half],
            grad_lifted[:, half:],
            hidden_sides[0],
            hidden_sides[1],
            grad_v,
        ]
    )
    gains = jnp.pad(jnp.stack([gain_first, gain_second]), ((0, 6), (0, 0)))
    return layer_output, input_gradient, xt, dy, gains


def rotation(block_order, rows):
    block = rows // 2
    ctx_place = lax.axis_index("ctx")
    offsets = jnp.arange(block, dtype=jnp.int32)
    own_blocks = lax.dynamic_slice_in_dim(block_order, 2 * ctx_place, 2)
    query_pos = (own_blocks[:, None] * block + offsets[None, :]).reshape(rows)
    key_pos = (block_order[:, None] * block + offsets[None, :]).reshape(-1)
    bias = jnp.where(key_pos[:, None] <= query_pos[None, :], 0.0, MASKED).astype(jnp.bfloat16)
    lane = jnp.arange(128, dtype=jnp.int32)
    index = (lane % (HEAD // 2)).astype(jnp.float32)
    frequency = THETA ** (-(index * 2.0 / HEAD))
    angle = query_pos.astype(jnp.float32)[:, None] * frequency[None, :]
    cosine, sine = jnp.cos(angle), jnp.sin(angle)
    early = (lane % HEAD < HEAD // 2)[None, :]
    return (cosine, jnp.where(early, 0.0, sine), jnp.where(early, -sine, 0.0)), bias


def plain_step(layer_input, output_grad, norm_gains, block_order, weights, olds, factors, sizes):
    parts, width, half, kv, short, full, high = sizes
    query_weight, key_weight, value_weight, output_weight, gate_weight, up_weight, down_weight = weights
    (
        query_momentum,
        key_momentum,
        value_momentum,
        output_momentum,
        gate_momentum,
        up_momentum,
        down_momentum,
    ) = olds

    def sides(left, right):
        return jnp.concatenate([left, right], axis=1)

    wide = jnp.stack(
        [
            jnp.concatenate([query_weight, key_weight], axis=1),
            jnp.concatenate([output_weight, value_weight], axis=1),
            gate_weight[:, :half],
            gate_weight[:, half:],
            up_weight[:, :half],
            up_weight[:, half:],
        ]
    )
    tall = down_weight.reshape(2, high, width)
    layer_output, input_gradient, xt, dy, gains = plain_layer(
        layer_input, output_grad, wide, tall, norm_gains, block_order, sizes
    )

    def pad_rows(array):
        return padded(array, 0, 1, short, full)

    def pad_columns(array):
        return padded(array, 1, parts, short, full)

    moments = (
        pad_rows(sides(query_momentum, key_momentum)),
        pad_rows(sides(output_momentum, value_momentum)),
        pad_rows(gate_momentum),
        pad_rows(up_momentum),
        pad_columns(down_momentum),
    )
    g_wide, g_tall, s_wide, s_tall, gain_sum = reduce_gradients(xt, dy, gains, moments, full, high)
    o_wide, o_tall = orthogonalize(s_wide, s_tall, full, high, width)

    def unpack(wide_pieces, tall_pieces):
        pieces = wide_pieces[:, :short]
        tall = trimmed(tall_pieces, 2, parts, short, full).reshape(2 * high, width)
        return (
            pieces[0, :, :width],
            pieces[0, :, width:],
            pieces[1, :, width:],
            pieces[1, :, :width],
            sides(pieces[2], pieces[3]),
            sides(pieces[4], pieces[5]),
            tall,
        )

    gradients = [item.astype(jnp.float32) for item in unpack(g_wide, g_tall)]
    orthos = unpack(o_wide, o_tall)
    moments = [MOMENTUM * old + new for old, new in zip(olds, gradients)]
    new_weights = [
        weight.astype(jnp.float32) + factor * ortho.astype(jnp.float32)
        for weight, factor, ortho in zip(weights, factors, orthos)
    ]
    return layer_output, input_gradient, gradients, moments, new_weights, gain_sum


def on_device(
    layer_input,
    output_grad,
    query_weight,
    key_weight,
    value_weight,
    output_weight,
    gate_weight,
    up_weight,
    down_weight,
    norm_gains,
    query_momentum,
    key_momentum,
    value_momentum,
    output_momentum,
    gate_momentum,
    up_momentum,
    down_momentum,
    gain_momentum,
    block_order,
):
    parts = lax.axis_size("fsdp")
    width = layer_input.shape[2]
    half = gate_weight.shape[1] // 2
    kv = key_weight.shape[1]
    short = width // parts
    full = -(-short // 16) * 16
    high = half // parts
    sizes = (parts, width, half, kv, short, full, high)

    weights = (query_weight, key_weight, value_weight, output_weight, gate_weight, up_weight, down_weight)
    olds = (
        query_momentum,
        key_momentum,
        value_momentum,
        output_momentum,
        gate_momentum,
        up_momentum,
        down_momentum,
    )
    factors = []
    for index, weight in enumerate(weights):
        step_rate = OUT_RATE if index == 3 else RATE
        factors.append(-step_rate * max(1.0, weight.shape[1] / (weight.shape[0] * parts)) ** 0.5)

    fused = (
        lax.axis_size("ctx") == CLASSES
        and short == full
        and parts % 2 == 0
        and half % (2 * half // parts) == 0
        and (2 * half // parts) % 128 == 0
        and layer_input.shape[1] == 128
        and short <= 256
    )
    if fused:
        tables, bias = rotation(block_order, layer_input.shape[1])

        def turned(items):
            q, k, v, o, gate, up, down = items
            return (q, k.T, o, v.T, gate, up, down.T)

        shards, moments = turned(weights), turned(olds)
        out_turned, grad_turned, g, o, gain_sum = step_pass(
            layer_input[0].T, output_grad[0].T, norm_gains, tables, bias, shards, moments
        )
        gradients, moments, new_weights = settle(g, o, moments, shards, factors)
        layer_output, input_gradient = out_turned.T, grad_turned.T
    else:
        layer_output, input_gradient, gradients, moments, new_weights, gain_sum = plain_step(
            layer_input, output_grad, norm_gains, block_order, weights, olds, factors, sizes
        )
    gain_width = norm_gains.shape[1] // parts
    place = lax.axis_index("fsdp") * gain_width
    gain_gradient = lax.dynamic_slice_in_dim(gain_sum[:2], place, gain_width, 1)
    gain_shard = lax.dynamic_slice_in_dim(norm_gains, place, gain_width, 1)
    gain_moment = MOMENTUM * gain_momentum + gain_gradient
    new_gains = gain_shard - GAIN_RATE * gain_moment
    return (
        layer_output[None],
        input_gradient[None],
        *gradients,
        gain_gradient,
        *moments,
        gain_moment,
        *new_weights,
        new_gains,
    )


def solution(mesh):
    tokens = P("fsdp", "ctx", None)
    shard = P("fsdp", None)
    gains = P(None, "fsdp")
    return jax.shard_map(
        on_device,
        mesh=mesh,
        in_specs=(tokens, tokens) + (shard,) * 7 + (P(),) + (shard,) * 7 + (gains, P()),
        out_specs=(tokens, tokens) + ((shard,) * 7 + (gains,)) * 3,
        check_vma=False,
    )
```

```python
import functools
import math

import jax
import jax.numpy as jnp
from jax import lax
from jax.experimental import pallas as pl
from jax.experimental.pallas import tpu as pltpu
from jax.sharding import PartitionSpec as P

HEADS = 15
KV_HEADS = 5
HEAD = 64
NS_ITERS = 5


EPS = 1e-05
THETA = 100000.0
NS_A = 3.4445
NS_B = -4.775
NS_C = 2.0315
MOMENTUM = 0.95
RATE = 0.2
OUT_RATE = 6.0
GAIN_RATE = 0.002
MASKED = -1e30

MESH = pl.DeviceIdType.MESH
BF16 = jnp.bfloat16
F32 = jnp.float32
ANY = pl.BlockSpec(memory_space=pl.ANY)
VMEM = pl.BlockSpec(memory_space=pltpu.VMEM)
CLASSES = 8
WIDE = 6


def contract(left, right, left_dim, right_dim):
    return lax.dot_general(
        left, right, (((left_dim,), (right_dim,)), ((), ())), preferred_element_type=jnp.float32
    )


class Place:
    def __init__(self):
        self.parts = lax.axis_size("fsdp")
        self.extra = lax.axis_size("ctx") // CLASSES
        self.c = lax.axis_index("ctx")
        self.f = lax.axis_index("fsdp")
        self.p = lax.rem(self.c, CLASSES)
        self.core = lax.rem(self.c, 2)
        self.b1 = jnp.where(self.core == 0, 2, 4)
        self.b2 = jnp.where(self.core == 0, 4, 2)

    def peer(self, bits):
        return (self.c ^ bits, self.f)

    def along(self, j):
        return (self.c, self.f ^ j)

    def other(self, j):
        groups = self.extra
        return (lax.rem(self.c + CLASSES * j, CLASSES * groups), self.f)

    def barrier(self, bits=(1, 2, 4), line=True, others=False):
        sem = pltpu.get_barrier_semaphore()
        targets = [self.peer(b) for b in bits]
        if line:
            targets += [self.along(j) for j in range(1, self.parts)]
        if others:
            targets += [self.other(j) for j in range(1, self.extra)]
        for target in targets:
            pl.semaphore_signal(sem, inc=1, device_id=target, device_id_type=MESH)
        pl.semaphore_wait(sem, len(targets))


def remote(src, dst, send, recv, target):
    return pltpu.make_async_remote_copy(
        src_ref=src, dst_ref=dst, send_sem=send, recv_sem=recv, device_id=target, device_id_type=MESH
    )


def by_kind(cls, wide, tall):
    pl.when(cls < WIDE)(wide)
    pl.when(cls >= WIDE)(tall)


def weights_kernel(in_a, in_b, out_a, out_b, local, zs, s1, s2, sc, recv):
    at = Place()
    p, f, parts = at.p, at.f, at.parts
    at.barrier()
    copies = [
        pltpu.make_async_copy(in_a, out_a.at[:, f], local.at[0]),
        pltpu.make_async_copy(in_b, out_b.at[:, f], local.at[1]),
    ]
    for copy in copies:
        copy.start()

    def act(cls, j, g, send, target, what, first=False):
        def wide():
            dst = out_a.at[cls, g]
            src = in_a.at[cls] if first else dst
            getattr(remote(src, dst, send, recv.at[cls, j], target), what)()

        def tall():
            dst = out_b.at[cls - WIDE, g]
            src = in_b.at[cls - WIDE] if first else dst
            getattr(remote(src, dst, send, recv.at[cls, j], target), what)()

        by_kind(cls, wide, tall)

    sends = []

    def send(cls, j, g, sem, target, first=False):
        act(cls, j, g, sem, target, "start", first)
        sends.append((cls, j, g, sem, target, first))

    def arrived(cls, j):
        act(cls, j, f ^ j, zs.at[j], at.along(j), "wait_recv")

    for j in range(1, parts):
        send(p, j, f, zs.at[j], at.along(j), True)
    for j in range(1, parts):
        arrived(p, j)
        send(p, j, f ^ j, s1.at[0, j], at.peer(at.b1))
        send(p, j, f ^ j, s2.at[0, j], at.peer(at.b2))
        send(p, j, f ^ j, sc.at[0, j], at.peer(1))
    for j in range(1, parts):
        arrived(p ^ at.b1, j)
        send(p ^ at.b1, j, f ^ j, s2.at[1, j], at.peer(at.b2))
        send(p ^ at.b1, j, f ^ j, sc.at[1, j], at.peer(1))
    for slot, bits in ((2, at.b2), (3, at.b1 ^ at.b2)):
        for j in range(1, parts):
            arrived(p ^ bits, j)
            send(p ^ bits, j, f ^ j, sc.at[slot, j], at.peer(1))
    for bits in (1, 3, 5, 7):
        for j in range(1, parts):
            arrived(p ^ bits, j)
    for cls, j, g, sem, target, first in sends:
        act(cls, j, g, sem, target, "wait_send", first)
    for copy in copies:
        copy.wait()


def gather_weights(wide, tall):
    parts = lax.axis_size("fsdp")
    dma = pltpu.SemaphoreType.DMA
    return pl.pallas_call(
        weights_kernel,
        out_shape=(
            jax.ShapeDtypeStruct((WIDE, parts) + wide.shape[1:], BF16),
            jax.ShapeDtypeStruct((CLASSES - WIDE, parts) + tall.shape[1:], BF16),
        ),
        in_specs=[ANY, ANY],
        out_specs=(ANY, ANY),
        scratch_shapes=[
            dma((2,)),
            dma((parts,)),
            dma((1, parts)),
            dma((2, parts)),
            dma((4, parts)),
            dma((CLASSES, parts)),
        ],
        compiler_params=pltpu.CompilerParams(collective_id=0, has_side_effects=True),
        name="gather_weights",
    )(wide, tall)


def spread(at, own_a, own_b, out_a, out_b, local, ss, recv):
    p = at.p

    def act(cls, sem, target, what, first=False):
        def wide():
            dst = out_a.at[cls]
            getattr(remote(own_a if first else dst, dst, sem, recv.at[cls], target), what)()

        def tall():
            dst = out_b.at[cls - WIDE]
            getattr(remote(own_b if first else dst, dst, sem, recv.at[cls], target), what)()

        by_kind(cls, wide, tall)

    def keep(what):
        def wide():
            getattr(pltpu.make_async_copy(own_a, out_a.at[p], local), what)()

        def tall():
            getattr(pltpu.make_async_copy(own_b, out_b.at[p - WIDE], local), what)()

        by_kind(p, wide, tall)

    sends = []

    def send(cls, slot, target, first=False):
        act(cls, ss.at[slot], target, "start", first)
        sends.append((cls, slot, target, first))

    def arrived(cls):
        act(cls, ss.at[0], at.peer(1), "wait_recv")

    send(p, 0, at.peer(at.b1), True)
    send(p, 1, at.peer(at.b2), True)
    send(p, 2, at.peer(1), True)
    keep("start")

    def finish():
        arrived(p ^ at.b1)
        send(p ^ at.b1, 3, at.peer(at.b2))
        send(p ^ at.b1, 4, at.peer(1))
        arrived(p ^ at.b2)
        send(p ^ at.b2, 5, at.peer(1))
        arrived(p ^ at.b1 ^ at.b2)
        send(p ^ at.b1 ^ at.b2, 6, at.peer(1))
        for bits in (1, 3, 5, 7):
            arrived(p ^ bits)
        for cls, slot, target, first in sends:
            act(cls, ss.at[slot], target, "wait_send", first)
        keep("wait")

    return finish


def reduce_kernel(
    parts, extra, high,
    xt_in, dy_in, gain_in, m_qk, m_ov, m_gate, m_up, m_down,
    g_a, g_b, s_a, s_b, gain_out,
    xt, dy, p1s, p1r, p2s, p2r, own, own_t, za_s, za_r, zb_s, zb_r, ma, mb, ga, gb, sa, sb, es, er, gain_s, gain_r,
    ls, xs, xr, s1, r1, s2, r2, zs, zr, esem, ersem, msem, gs, gr, ag_l, ag_s, ag_r, ss, sr, sl,
):
    at = Place()
    p, f, core = at.p, at.f, at.core
    tokens = xt_in.shape[2]
    rows = ma.shape[0]
    half = dy.shape[2]

    def moment(what):
        for cls in range(CLASSES):
            @pl.when(p == cls)
            def _(cls=cls):
                side = cls % 2
                if cls < 2:
                    src, dst = (m_qk, m_ov)[cls], ma
                elif cls < WIDE:
                    whole = m_gate if cls < 4 else m_up
                    src, dst = whole.at[:, pl.ds(side * half, half)], ma
                else:
                    src, dst = m_down.at[pl.ds(side * high, high)], mb
                getattr(pltpu.make_async_copy(src, dst, msem), what)()

    moment("start")
    mine = [pltpu.make_async_copy(xt_in, xt.at[:, :, pl.ds(0, tokens)], ls.at[0])]
    for slot in range(4):
        mine.append(
            pltpu.make_async_copy(dy_in.at[core + 2 * slot], dy.at[slot, pl.ds(0, tokens)], ls.at[1 + slot])
        )
    mine.append(pltpu.make_async_copy(dy_in.at[8], dy.at[4, pl.ds(0, tokens)], ls.at[5]))
    for copy in mine:
        copy.start()
    at.barrier(others=True)
    pair = at.peer(1)
    theirs = [remote(xt_in, xt.at[:, :, pl.ds(tokens, tokens)], xs.at[0], xr.at[0], pair)]
    for slot in range(4):
        theirs.append(
            remote(dy_in.at[1 - core + 2 * slot], dy.at[slot, pl.ds(tokens, tokens)], xs.at[1 + slot], xr.at[1 + slot], pair)
        )
    theirs.append(remote(dy_in.at[8], dy.at[4, pl.ds(tokens, tokens)], xs.at[5], xr.at[5], pair))
    for copy in theirs:
        copy.start()

    def swap(slot, target):
        return remote(gain_s.at[slot], gain_r.at[slot], gs.at[slot], gr.at[slot], target)

    gain_s[0] = gain_in[...]
    swaps = [swap(0, pair)]
    swaps[0].start()
    for copy in mine:
        copy.wait()
    for copy in theirs:
        copy.wait()

    def term(cls, r):
        at_rows = pl.ds(pl.multiple_of(r * rows, rows), rows)
        slot = lax.div(cls, 2)
        kind = jnp.where(cls == 0, 0, jnp.where(cls == 1, 1, jnp.where(cls < WIDE, 2, 3)))
        value = jnp.dot(xt[kind, at_rows, :], dy[slot], preferred_element_type=F32)
        return value

    def with_values(cls, r, put):
        at_rows = pl.ds(pl.multiple_of(r * rows, rows), rows)

        @pl.when(cls == 1)
        def _():
            put(term(cls, r) + jnp.dot(xt[0, at_rows, :], dy[4], preferred_element_type=F32))

        @pl.when(cls != 1)
        def _():
            put(term(cls, r))

    def order(i):
        return lax.rem(f + 1 + i, parts)

    def one(slot, i):
        r = order(i)
        return remote(p1s.at[slot, r], p1r.at[slot, r], s1.at[slot, r], r1.at[slot, r], at.peer(at.b1))

    for slot, bits in ((0, at.b1 ^ at.b2), (1, at.b1)):
        def first(i, carry, slot=slot, bits=bits):
            r = order(i)

            def put(value):
                p1s[slot, r] = value.astype(BF16)

            with_values(p ^ bits, r, put)
            one(slot, i).start()
            return carry

        lax.fori_loop(0, parts, first, 0)

    swaps[0].wait()
    gain_s[1] = gain_s[0] + gain_r[0]
    swaps.append(swap(1, at.peer(2)))
    swaps[1].start()

    def two(i):
        r = order(i)
        return remote(p2s.at[r], p2r.at[r], s2.at[r], r2.at[r], at.peer(at.b2))

    def second(i, carry):
        r = order(i)
        one(0, i).wait_recv()

        def put(value):
            p2s[r] = (value + p1r[0, r].astype(F32)).astype(BF16)

        with_values(p ^ at.b2, r, put)
        two(i).start()
        return carry

    lax.fori_loop(0, parts, second, 0)
    swaps[1].wait()
    gain_s[2] = gain_s[1] + gain_r[1]
    swaps.append(swap(2, at.peer(4)))
    swaps[2].start()

    def line_a(r, source):
        return remote(za_s.at[r], za_r.at[source], zs.at[r], zr.at[source], (at.c, r))

    def line_b(r, source):
        return remote(
            zb_s.at[pl.ds(pl.multiple_of(r * high, high), high)],
            zb_r.at[source], zs.at[r], zr.at[source], (at.c, r),
        )

    early = extra == 1

    def third(i, carry):
        r = order(i)
        one(1, i).wait_recv()
        two(i).wait_recv()

        def put(value):
            total = value + p1r[1, r].astype(F32) + p2r[r].astype(F32)
            own[r] = total
            if early:
                za_s[r] = total.astype(BF16)

        with_values(p, r, put)
        if early:
            @pl.when((p < WIDE) & (i < parts - 1))
            def _():
                line_a(r, f).start()
        return carry

    lax.fori_loop(0, parts, third, 0)
    swaps[2].wait()
    gain_s[3] = gain_s[2] + gain_r[2]

    if not early:
        es[...] = own[...].astype(BF16)
        group = [
            remote(es, er.at[j - 1], esem.at[j - 1], ersem.at[j - 1], at.other(j)) for j in range(1, extra)
        ]
        for copy in group:
            copy.start()
        for j in range(1, extra):
            group[j - 1].wait_recv()
            own[...] = own[...] + er[j - 1].astype(F32)
        for copy in group:
            copy.wait_send()
        za_s[...] = own[...].astype(BF16)

        @pl.when(p < WIDE)
        def _():
            for j in range(1, parts):
                line_a(f ^ j, f).start()

    @pl.when(p >= WIDE)
    def _():
        for tile in range(half // 128):
            for r in range(parts):
                block = own[r, :, pl.ds(tile * 128, 128)]
                if rows % 128 == 0:
                    own_t[pl.ds(tile * 128, 128), pl.ds(r * rows, rows)] = block.T
            if rows % 128 != 0:
                column = own[:, :, pl.ds(tile * 128, 128)].reshape(parts * rows, 128)
                own_t[pl.ds(tile * 128, 128), :] = column.T
        zb_s[...] = own_t[...].astype(BF16)
        for j in range(1, parts):
            line_b(f ^ j, f).start()

    line_gain = [
        remote(gain_s.at[3], gain_r.at[3 + j], gs.at[3 + j], gr.at[3 + j], at.along(j)) for j in range(1, parts)
    ]
    other_gain = []
    for copy in line_gain:
        copy.start()

    moment("wait")

    @pl.when(p < WIDE)
    def _():
        total = own[f]
        for j in range(1, parts):
            line_a(f ^ j, f ^ j).wait_recv()
            total = total + za_r[f ^ j].astype(F32)
        ga[...] = total.astype(BF16)
        sa[...] = (MOMENTUM * ma[...] + total).astype(BF16)

    @pl.when(p >= WIDE)
    def _():
        total = own_t[pl.ds(pl.multiple_of(f * high, high), high), :]
        for j in range(1, parts):
            line_b(f ^ j, f ^ j).wait_recv()
            total = total + zb_r[f ^ j].astype(F32)
        gb[...] = total.astype(BF16)
        sb[...] = (MOMENTUM * mb[...] + total).astype(BF16)

    def share_a(j, source):
        return remote(sa, s_a.at[pl.ds(pl.multiple_of(source * rows, rows), rows)], ss.at[j], sr.at[j], at.along(j))

    def share_b(j, source):
        return remote(sb, s_b.at[pl.ds(pl.multiple_of(source * high, high), high)], ss.at[j], sr.at[j], at.along(j))

    @pl.when(p < WIDE)
    def _():
        for j in range(1, parts):
            share_a(j, f).start()
        pltpu.make_async_copy(sa, s_a.at[pl.ds(pl.multiple_of(f * rows, rows), rows)], sl).start()

    @pl.when(p >= WIDE)
    def _():
        for j in range(1, parts):
            share_b(j, f).start()
        pltpu.make_async_copy(sb, s_b.at[pl.ds(pl.multiple_of(f * high, high), high)], sl).start()

    finish = spread(at, ga, gb, g_a, g_b, ag_l, ag_s, ag_r)
    total = gain_s[3]
    for j in range(1, parts):
        line_gain[j - 1].wait()
        total = total + gain_r[3 + j]
    if extra > 1:
        gain_s[4] = total
        other_gain = [
            remote(gain_s.at[4], gain_r.at[3 + parts + j], gs.at[3 + parts + j], gr.at[3 + parts + j], at.other(j))
            for j in range(1, extra)
        ]
        for copy in other_gain:
            copy.start()
        for j in range(1, extra):
            other_gain[j - 1].wait()
            total = total + gain_r[3 + parts + j]
    gain_out[...] = total
    finish()

    for slot in range(2):
        lax.fori_loop(0, parts, lambda i, carry, slot=slot: (one(slot, i).wait_send(), carry)[1], 0)
    lax.fori_loop(0, parts, lambda i, carry: (two(i).wait_send(), carry)[1], 0)

    @pl.when(p < WIDE)
    def _():
        for j in range(1, parts):
            line_a(f ^ j, f).wait_send()
            share_a(j, f).wait_send()
            share_a(j, f ^ j).wait_recv()
        pltpu.make_async_copy(sa, s_a.at[pl.ds(pl.multiple_of(f * rows, rows), rows)], sl).wait()

    @pl.when(p >= WIDE)
    def _():
        for j in range(1, parts):
            line_b(f ^ j, f).wait_send()
            share_b(j, f).wait_send()
            share_b(j, f ^ j).wait_recv()
        pltpu.make_async_copy(sb, s_b.at[pl.ds(pl.multiple_of(f * high, high), high)], sl).wait()


def reduce_gradients(xt, dy, gains, moments, rows, high):
    parts = lax.axis_size("fsdp")
    extra = lax.axis_size("ctx") // CLASSES
    kinds, depth, tokens = xt.shape
    half = dy.shape[2]
    dma = pltpu.SemaphoreType.DMA
    vm = pltpu.VMEM
    n_gain = 4 + parts + extra
    group = max(extra - 1, 1)
    spare = (parts, rows, half) if extra > 1 else (1, 16, 128)
    return pl.pallas_call(
        functools.partial(reduce_kernel, parts, extra, high),
        out_shape=(
            jax.ShapeDtypeStruct((WIDE, rows, half), BF16),
            jax.ShapeDtypeStruct((CLASSES - WIDE, high, depth), BF16),
            jax.ShapeDtypeStruct((depth, half), BF16),
            jax.ShapeDtypeStruct((half, depth), BF16),
            jax.ShapeDtypeStruct(gains.shape, F32),
        ),
        in_specs=[ANY, ANY, VMEM] + [ANY] * 5,
        out_specs=(ANY, ANY, ANY, ANY, VMEM),
        scratch_shapes=[
            vm((kinds, depth, 2 * tokens), BF16),
            vm((5, 2 * tokens, half), BF16),
            vm((2, parts, rows, half), BF16),
            vm((2, parts, rows, half), BF16),
            vm((parts, rows, half), BF16),
            vm((parts, rows, half), BF16),
            vm((parts, rows, half), F32),
            vm((half, depth), F32),
            vm((parts, rows, half), BF16),
            vm((parts, rows, half), BF16),
            vm((half, depth), BF16),
            vm((parts, high, depth), BF16),
            vm((rows, half), F32),
            vm((high, depth), F32),
            vm((rows, half), BF16),
            vm((high, depth), BF16),
            vm((rows, half), BF16),
            vm((high, depth), BF16),
            vm(spare, BF16),
            vm((group,) + spare, BF16),
            vm((5,) + gains.shape, F32),
            vm((n_gain,) + gains.shape, F32),
            dma((6,)), dma((6,)), dma((6,)),
            dma((2, parts)), dma((2, parts)), dma((parts,)), dma((parts,)), dma((parts,)), dma((parts,)),
            dma((group,)), dma((group,)), dma, dma((n_gain,)), dma((n_gain,)),
            dma, dma((7,)), dma((CLASSES,)), dma((parts,)), dma((parts,)), dma,
        ],
        compiler_params=pltpu.CompilerParams(
            collective_id=1, has_side_effects=True, vmem_limit_bytes=62 << 20
        ),
        name="reduce_gradients",
    )(xt, dy, gains, *moments)


def rounded(value):
    return value.astype(BF16)


def poly_rows(g, row_start, count):
    block = g[pl.ds(row_start, count), :]
    return rounded(NS_B * block.astype(F32) + NS_C * jnp.dot(block, g[...], preferred_element_type=F32))


def ortho_kernel(
    parts, rows, high, narrow,
    s_a, s_b, o_a, o_b,
    x, x_t, gs, gr, g, poly, sq, sq_r, pa, pb, kt,
    gsem, rsem, qs, qr, ag_l, ag_s, ag_r,
):
    at = Place()
    p, f = at.p, at.f
    depth, half = x.shape
    step = depth // 4
    at.barrier(line=False)
    pair = at.peer(1)

    @pl.when(p < WIDE)
    def _():
        x[...] = s_a[...]

    @pl.when(p >= WIDE)
    def _():
        for tile in range(half // 128):
            x[:, pl.ds(tile * 128, 128)] = s_b[pl.ds(tile * 128, 128), :].T

    def scale_of(total):
        return 1.0 / (jnp.sqrt(total) + 1e-07)

    def normal(ref, inverse):
        ref[...] = rounded(ref[...].astype(F32) * inverse)

    def exchange(slot, r):
        chunk = pl.ds(r * step, step)
        return remote(gs.at[chunk], gr.at[slot, chunk], gsem.at[r], rsem.at[slot, r], pair)

    def fill_poly():
        for r in range(4):
            poly[pl.ds(r * step, step), :] = poly_rows(g, r * step, step)

    my_rows = pl.ds(pl.multiple_of(f * rows, rows), rows)
    my_high = pl.ds(pl.multiple_of(f * high, high), high)

    @pl.when(p >= 2)
    def _():
        wide = x[...].astype(F32)
        sq[...] = jnp.broadcast_to(jnp.sum(wide * wide), sq.shape)
        copy = remote(sq, sq_r, qs, qr, pair)
        copy.start()
        copy.wait()
        normal(x, scale_of(sq[...] + sq_r[...])[:1, :1])

        def grams(slot):
            for r in range(4):
                gs[pl.ds(r * step, step), :] = rounded(contract(x[pl.ds(r * step, step), :], x[...], 1, 1))
                exchange(slot, r).start()
            for r in range(4):
                chunk = pl.ds(r * step, step)
                exchange(slot, r).wait()
                g[chunk, :] = rounded(gs[chunk, :].astype(F32) + gr[slot, chunk, :].astype(F32))

        def iterate(it, carry):
            grams(lax.rem(it, 2))
            fill_poly()
            for tile in range(half // 256):
                block = pl.ds(tile * 256, 256)
                x[:, block] = rounded(
                    NS_A * x[:, block].astype(F32) + jnp.dot(poly[...], x[:, block], preferred_element_type=F32)
                )
            return carry

        lax.fori_loop(0, NS_ITERS - 1, iterate, 0)
        grams((NS_ITERS - 1) % 2)

        @pl.when(p < WIDE)
        def _():
            mine = poly_rows(g, pl.multiple_of(f * rows, rows), rows)
            pa[...] = rounded(NS_A * x[my_rows, :].astype(F32) + jnp.dot(mine, x[...], preferred_element_type=F32))

        @pl.when(p >= WIDE)
        def _():
            fill_poly()
            for tile in range(half // 128):
                x_t[pl.ds(tile * 128, 128), :] = x[:, pl.ds(tile * 128, 128)].T
            block = x_t[my_high, :]
            pb[...] = rounded(NS_A * block.astype(F32) + jnp.dot(block, poly[...], preferred_element_type=F32))

    @pl.when(p < 2)
    def _():
        kt[...] = x[:, narrow:].T
        inverse_k = scale_of(jnp.sum(jnp.square(kt[...].astype(F32))))
        normal(kt, inverse_k)
        wide = x[:, :narrow].astype(F32)
        x[:, :narrow] = rounded(wide * scale_of(jnp.sum(wide * wide)))

        def narrow_step(it, carry):
            gram = rounded(contract(kt[...], kt[...], 1, 1))
            turn = rounded(NS_B * gram.astype(F32) + NS_C * jnp.dot(gram, gram, preferred_element_type=F32))
            kt[...] = rounded(NS_A * kt[...].astype(F32) + jnp.dot(turn, kt[...], preferred_element_type=F32))
            return carry

        lax.fori_loop(0, NS_ITERS, narrow_step, 0)

        def gram_of():
            for r in range(4):
                chunk = pl.ds(r * step, step)
                g[chunk, :] = rounded(contract(x[chunk, :narrow], x[:, :narrow], 1, 1))

        def square_step(it, carry):
            gram_of()
            fill_poly()
            x[:, :narrow] = rounded(
                NS_A * x[:, :narrow].astype(F32) + jnp.dot(poly[...], x[:, :narrow], preferred_element_type=F32)
            )
            return carry

        lax.fori_loop(0, NS_ITERS - 1, square_step, 0)
        gram_of()
        mine = poly_rows(g, pl.multiple_of(f * rows, rows), rows)
        square = rounded(
            NS_A * x[my_rows, :narrow].astype(F32) + jnp.dot(mine, x[:, :narrow], preferred_element_type=F32)
        )
        x[:, narrow:] = kt[...].T
        pa[:, :narrow] = square
        pa[:, narrow:] = x[my_rows, narrow:]

    spread(at, pa, pb, o_a, o_b, ag_l, ag_s, ag_r)()


def orthogonalize(s_a, s_b, rows, high, narrow):
    parts = lax.axis_size("fsdp")
    depth, half = s_a.shape
    dma = pltpu.SemaphoreType.DMA
    vm = pltpu.VMEM
    return pl.pallas_call(
        functools.partial(ortho_kernel, parts, rows, high, narrow),
        out_shape=(
            jax.ShapeDtypeStruct((WIDE, rows, half), BF16),
            jax.ShapeDtypeStruct((CLASSES - WIDE, high, depth), BF16),
        ),
        in_specs=[VMEM, VMEM],
        out_specs=(ANY, ANY),
        scratch_shapes=[
            vm((depth, half), BF16),
            vm((half, depth), BF16),
            vm((depth, depth), BF16),
            vm((2, depth, depth), BF16),
            vm((depth, depth), BF16),
            vm((depth, depth), BF16),
            vm((8, 128), F32),
            vm((8, 128), F32),
            vm((rows, half), BF16),
            vm((high, depth), BF16),
            vm((half - narrow, depth), BF16),
            dma((4,)), dma((2, 4)), dma, dma, dma, dma((7,)), dma((CLASSES,)),
        ],
        compiler_params=pltpu.CompilerParams(
            collective_id=2, has_side_effects=True, vmem_limit_bytes=62 << 20
        ),
        name="orthogonalize",
    )(s_a, s_b)


class Weights:
    def __init__(self, at, sources, homes, zs, s1, s2, sc, recv):
        self.at, self.sources, self.homes = at, sources, homes
        self.zs, self.s1, self.s2, self.sc, self.recv = zs, s1, s2, sc, recv
        self.sends = []

    def act(self, group, q, j, plane, send, target, what, first=False):
        recv = self.recv.at[group, q, j]
        home, source = self.homes[group], self.sources[group]
        rows = home.shape[-2] // (1 if group == 3 else self.at.parts)
        unit = -(-rows // (16 * CLASSES)) * 16
        last = rows - (CLASSES - 1) * unit

        def piece(count):
            def go():
                start = pl.multiple_of(q * unit, 16)
                if group == 3:
                    columns = home.shape[1] // self.at.parts
                    dst = home.at[pl.ds(start, count), pl.ds(pl.multiple_of(plane * columns, 128), columns)]
                    src = source.at[pl.ds(start, count)]
                elif group == 0:
                    dst = home.at[:, pl.ds(pl.multiple_of(plane * rows + start, 16), count)]
                    src = dst
                else:
                    dst = home.at[pl.ds(pl.multiple_of(plane * rows + start, 16), count)]
                    src = source.at[pl.ds(start, count)]
                getattr(remote(src if first else dst, dst, send, recv, target), what)()

            return go

        pl.when(q < CLASSES - 1)(piece(unit))
        pl.when(q == CLASSES - 1)(piece(last))

    def send(self, group, q, j, plane, sem, target, first=False):
        self.act(group, q, j, plane, sem, target, "start", first)
        self.sends.append((group, q, j, plane, sem, target, "wait_send", first))

    def arrived(self, group, q, j):
        at = self.at
        self.act(group, q, j, at.f ^ j, self.zs.at[group, j], at.peer(1), "wait_recv")

    def along(self, group):
        at = self.at
        for j in range(1, at.parts):
            self.send(group, at.p, j, at.f, self.zs.at[group, j], at.along(j), True)

    def first(self, group):
        at = self.at
        for j in range(1, at.parts):
            self.arrived(group, at.p, j)
            self.send(group, at.p, j, at.f ^ j, self.s1.at[group, j], at.peer(at.b1))
            self.send(group, at.p, j, at.f ^ j, self.s2.at[group, 0, j], at.peer(at.b2))
            self.send(group, at.p, j, at.f ^ j, self.sc.at[group, 0, j], at.peer(1))

    def second(self, group):
        at = self.at
        q = at.p ^ at.b1
        for j in range(1, at.parts):
            self.arrived(group, q, j)
            self.send(group, q, j, at.f ^ j, self.s2.at[group, 1, j], at.peer(at.b2))
            self.send(group, q, j, at.f ^ j, self.sc.at[group, 1, j], at.peer(1))

    def third(self, group):
        at = self.at
        for slot, bits in ((2, at.b2), (3, at.b1 ^ at.b2)):
            for j in range(1, at.parts):
                self.arrived(group, at.p ^ bits, j)
                self.send(group, at.p ^ bits, j, at.f ^ j, self.sc.at[group, slot, j], at.peer(1))

    def ready(self, group):
        at = self.at
        for bits in (1, 3, 5, 7):
            for j in range(1, at.parts):
                self.arrived(group, at.p ^ bits, j)

    def finish(self):
        for item in self.sends:
            self.act(*item)


def spread_even(at, own, out, local, ss, recv):
    p = at.p

    def copy_of(cls, slot, target, first=False):
        return remote(own if first else out.at[cls], out.at[cls], ss.at[slot], recv.at[cls], target)

    keep = pltpu.make_async_copy(own, out.at[p], local)
    b1, b2 = at.b1, at.b2
    own_sends = [(p, 0, b1, True), (p, 1, b2, True), (p, 2, 1, True)]
    steps = (
        (p ^ b1, [(p ^ b1, 3, b2, False), (p ^ b1, 4, 1, False)]),
        (p ^ b2, [(p ^ b2, 5, 1, False)]),
        (p ^ b1 ^ b2, [(p ^ b1 ^ b2, 6, 1, False)]),
    )

    def move(cls, slot, bits, first):
        return copy_of(cls, slot, at.peer(bits), first)

    def arrived(cls):
        copy_of(cls, 0, at.peer(1)).wait_recv()

    def begin():
        for item in own_sends:
            move(*item).start()
        keep.start()

    def step(k):
        cls, sends = steps[k]
        arrived(cls)
        for item in sends:
            move(*item).start()

    def finish():
        for bits in (1, 3, 5, 7):
            arrived(p ^ bits)
        for item in own_sends + [item for _, sends in steps for item in sends]:
            move(*item).wait_send()
        keep.wait()

    return begin, step, finish


def step_kernel(
    x_ref, up_ref, gains_ref, cos_ref, low_ref, high_ref, bias_ref, wq, wk, wo, wv, wg_in, wu_in, wd_in,
    m_q, m_k, m_o, m_v, m_gate, m_up, m_down,
    out_ref, grad_ref, g_out, o_out, gain_out,
    w01, wg, wu, wd, probs, kv, rot, dkv, c_send, c4r, c2r, c1r, att, gate, lifted,
    xt_in, dy_in, dv_in, xf_all, xa_all, yf_all, yv_all, za_r, ma, mq, mk, gain_s, gain_r, sq, sq_r,
    local, zs, s1, s2, sc, recv, kvs, kvr, ds, dr,
    ls, xs, xr, ps, pr, ys, yr, as_, ar, vs, vr, hs, hr, ozs, ozr, msem, gs, gr, ag_l, ag_s, ag_r, ls_l, ls_r, lr_l, lr_r,
    gsem, rsem, qs, qr, ex_s, ex_r, fx_s, fx_r, og_l, og_s, og_r, free,
):
    at = Place()
    p, f, core, parts = at.p, at.f, at.core, at.parts
    width, tokens = x_ref.shape
    half = w01.shape[2]
    keys = half - width
    group = HEADS // KV_HEADS
    scale = 1.0 / math.sqrt(HEAD)
    rows = width // parts
    columns = 2 * half // parts
    tall = width // 2
    pair = at.peer(1)
    my_rows = pl.ds(pl.multiple_of(f * rows, 16), rows)

    weights = Weights(at, (None, wg_in, wu_in, wd_in), (w01, wg, wu, wd), zs, s1, s2, sc, recv)
    keep = [
        pltpu.make_async_copy(wg_in, wg.at[my_rows], local.at[0]),
        pltpu.make_async_copy(wu_in, wu.at[my_rows], local.at[1]),
        pltpu.make_async_copy(
            wd_in, wd.at[:, pl.ds(pl.multiple_of(f * columns, 128), columns)], local.at[2]
        ),
    ]

    def moment(what):
        for cls in range(CLASSES):
            @pl.when(p == cls)
            def _(cls=cls):
                side = cls % 2
                if cls < 2:
                    pairs = [((m_q, m_o)[cls], mq, 0), ((m_k, m_v)[cls], mk, 1)]
                elif cls < WIDE:
                    whole = m_gate if cls < 4 else m_up
                    pairs = [(whole.at[:, pl.ds(side * half, half)], ma, 0)]
                else:
                    pairs = [
                        (
                            m_down.at[pl.ds(side * tall + t * rows, rows)],
                            ma.at[:, pl.ds(t * columns, columns)],
                            t,
                        )
                        for t in range(2)
                    ]
                for src, dst, index in pairs:
                    getattr(pltpu.make_async_copy(src, dst, msem.at[index]), what)()

    w01[0, my_rows, :width] = wq[...]
    w01[0, my_rows, width:] = wk[...].T
    w01[1, my_rows, :width] = wo[...]
    w01[1, my_rows, width:] = wv[...].T
    at.barrier(bits=range(1, CLASSES))
    for index in range(4):
        weights.along(index)
    for copy in keep:
        copy.start()
    moment("start")

    residual = x_ref[...].astype(F32).T
    upstream = up_ref[...].astype(F32).T
    inverse_first = lax.rsqrt(jnp.mean(residual * residual, axis=-1, keepdims=True) + EPS)
    normed_first = (residual * inverse_first * gains_ref[0:1, :]).astype(BF16)
    xt_in[0] = normed_first.T
    xt_in[3] = up_ref[...]

    weights.first(0)
    weights.second(0)
    weights.third(0)
    weights.ready(0)

    def turn(value, sign):
        tiles = []
        for tile in range(half // 128):
            part = value[:, tile * 128 : (tile + 1) * 128]
            swapped = pltpu.roll(part, HEAD // 2, 1) * low_ref[...] + pltpu.roll(part, 128 - HEAD // 2, 1) * high_ref[...]
            tiles.append(part * cos_ref[...] + swapped if sign > 0 else part * cos_ref[...] - swapped)
        return tiles

    qk = jnp.dot(normed_first, w01[0], preferred_element_type=F32)
    for tile, value in enumerate(turn(qk, 1)):
        rot[:, tile * 128 : (tile + 1) * 128] = value.astype(BF16)
    values = jnp.dot(normed_first, w01[1, :, width:], preferred_element_type=F32).astype(BF16)
    kv[p, :, :keys] = rot[:, width:]
    kv[p, :, keys:] = values

    def block(q, slot, target):
        return remote(kv.at[q], kv.at[q], kvs.at[slot], kvr.at[q], target)

    sent = [block(p, 0, at.peer(at.b1)), block(p, 1, at.peer(at.b2)), block(p, 2, at.peer(1))]
    for copy in sent:
        copy.start()

    def pass_keys(q, slots):
        block(q, 0, at.peer(1)).wait_recv()
        for slot, target in slots:
            copy = block(q, slot, target)
            copy.start()
            sent.append(copy)

    weights.first(1)
    pass_keys(p ^ at.b1, [(3, at.peer(at.b2)), (4, at.peer(1))])
    pass_keys(p ^ at.b2, [(5, at.peer(1))])
    weights.second(1)
    pass_keys(p ^ at.b1 ^ at.b2, [(6, at.peer(1))])
    for bits in (1, 3, 5, 7):
        pass_keys(p ^ bits, [])
    weights.third(1)

    def keys_of(g):
        return kv[:, :, g * HEAD : (g + 1) * HEAD].reshape(CLASSES * tokens, HEAD)

    def values_of(g):
        return kv[:, :, keys + g * HEAD : keys + (g + 1) * HEAD].reshape(CLASSES * tokens, HEAD)

    def heads_of(ref, g):
        return jnp.concatenate([ref[:, h * HEAD : (h + 1) * HEAD] for h in range(g * group, (g + 1) * group)], axis=0)

    def attend(g):
        scores = contract(keys_of(g), heads_of(rot, g), 1, 1) * scale
        bias = bias_ref[...].astype(F32)
        scores = scores + jnp.concatenate([bias] * group, axis=1)
        top = jnp.max(scores, axis=0, keepdims=True)
        expo = jnp.exp(scores - top)
        total = jnp.sum(expo, axis=0, keepdims=True)
        chance = expo * (1.0 / total)
        probs[g] = chance
        mixed = contract(values_of(g), chance.astype(BF16), 0, 0)
        turned = mixed.T.astype(BF16)
        for h in range(group):
            at_lane = (g * group + h) * HEAD
            att[:, at_lane : at_lane + HEAD] = turned[h * tokens : (h + 1) * tokens]

    attend(0)
    weights.first(2)
    attend(1)
    weights.second(2)
    attend(2)
    weights.third(2)
    attend(3)
    weights.first(3)
    attend(4)
    weights.second(3)
    for copy in keep:
        copy.wait()
    weights.ready(1)

    xt_in[1] = att[...].T
    middle = residual + jnp.dot(att[...], w01[1, :, :width], preferred_element_type=F32)
    inverse_second = lax.rsqrt(jnp.mean(middle * middle, axis=-1, keepdims=True) + EPS)
    normed_second = (middle * inverse_second * gains_ref[1:2, :]).astype(BF16)
    xt_in[2] = normed_second.T
    gate[...] = jnp.dot(normed_second, wg[...], preferred_element_type=F32)
    weights.third(3)

    def tokens_of(q):
        return pl.ds(pl.multiple_of(q * tokens, tokens), tokens)

    def kind_of(q):
        return jnp.where(q < 2, 0, jnp.where(q < WIDE, 2, 3))

    own_x = pltpu.make_async_copy(xt_in.at[kind_of(p)], xf_all.at[:, tokens_of(p)], ls.at[0])

    def x_move(bits):
        q = p ^ bits
        return remote(xt_in.at[kind_of(q)], xf_all.at[:, tokens_of(p)], xs.at[bits], xr.at[p], at.peer(bits))

    def a_move():
        return remote(xt_in.at[1], xa_all.at[:, tokens_of(p)], as_, ar.at[p], at.peer(p ^ 1))

    def own_a():
        return pltpu.make_async_copy(xt_in.at[1], xa_all.at[:, tokens_of(p)], ls.at[1])

    def y_move(bits):
        q = p ^ bits
        return remote(dy_in.at[q], yf_all.at[tokens_of(p)], ys.at[bits], yr.at[p], at.peer(bits))

    def own_y():
        return pltpu.make_async_copy(dy_in.at[p], yf_all.at[tokens_of(p)], ls.at[2])

    def v_move():
        return remote(dv_in, yv_all.at[tokens_of(p)], vs, vr.at[p], at.peer(p ^ 1))

    def own_v():
        return pltpu.make_async_copy(dv_in, yv_all.at[tokens_of(p)], ls.at[3])

    own_x.start()
    for bits in (2, 4, 6):
        x_move(bits).start()
    pl.when(p != 1)(lambda: a_move().start())
    pl.when(p == 1)(lambda: own_a().start())

    def give_y(bits, low, high):
        q = p ^ bits

        @pl.when((q >= low) & (q < high))
        def _():
            y_move(bits).start()

    weights.ready(2)
    for side in range(2):
        lifted[side * tokens : (side + 1) * tokens] = jnp.dot(
            normed_second, wu[:, side * half : (side + 1) * half], preferred_element_type=F32
        )

    def lift():
        return jnp.concatenate([lifted[:tokens], lifted[tokens:]], axis=1)

    hidden = (gate[...] * jax.nn.sigmoid(gate[...]) * lift()).astype(BF16)
    dy_in[6] = hidden[:, :half]
    dy_in[7] = hidden[:, half:]
    for bits in range(1, CLASSES):
        give_y(bits, WIDE, CLASSES)
    weights.ready(3)

    grad_hidden = jnp.dot(upstream.astype(BF16), wd[...], preferred_element_type=F32)
    sigma = jax.nn.sigmoid(gate[...])
    grad_gate = (grad_hidden * lift() * sigma * (1.0 + gate[...] * (1.0 - sigma))).astype(BF16)
    grad_lifted = (grad_hidden * gate[...] * sigma).astype(BF16)
    for side in range(2):
        lanes = slice(side * half, (side + 1) * half)
        dy_in[2 + side] = grad_gate[:, lanes]
        dy_in[4 + side] = grad_lifted[:, lanes]
    for bits in range(1, CLASSES):
        give_y(bits, 2, WIDE)

    out_ref[...] = (middle + contract(hidden, wd[...], 1, 1)).T.astype(BF16)
    weights.finish()
    grad_normed = contract(grad_gate, wg[...], 1, 1) + contract(grad_lifted, wu[...], 1, 1)
    pl.semaphore_signal(free.at[0], inc=1, device_id=pair, device_id_type=MESH)

    def norm_back(value, inverse, gain, incoming):
        scaled = incoming * gain
        mean = jnp.mean(scaled * value, axis=-1, keepdims=True)
        through = inverse * scaled - value * (inverse * inverse * inverse) * mean
        return through, jnp.sum(incoming * value * inverse, axis=0, keepdims=True)

    through, gain_second = norm_back(middle, inverse_second, gains_ref[1:2, :], grad_normed)
    gain_s[0] = jnp.zeros(gain_s.shape[1:], F32)
    gain_s[0, 1:2, :] = gain_second
    grad_middle = upstream + through
    grad_branch = grad_middle.astype(BF16)
    dy_in[1, :, :width] = grad_branch
    dy_in[1, :, width:] = jnp.zeros((tokens, keys), BF16)
    att[...] = contract(grad_branch, w01[1, :, :width], 1, 1).astype(BF16)

    for bits in range(1, CLASSES):
        give_y(bits, 1, 2)

    own = lifted.at[pl.ds(0, rows)]

    def swap(slot, target):
        return remote(gain_s.at[slot], gain_r.at[slot], gs.at[slot], gr.at[slot], target)

    def order(i):
        return lax.rem(f + 1 + i, parts)

    cut = width // 128 * 128
    part_lanes = (pl.ds(0, cut), pl.ds(cut, half - cut))
    parts_early = (lambda: p >= 1, lambda: p >= 2)
    parts_late = (lambda: p < 1, lambda: p < 2)

    def room(r):
        return wd.at[pl.ds(pl.multiple_of(r * rows, 16), rows), pl.ds(half, half)]

    def line(r, source, part):
        lanes = part_lanes[part]
        return remote(
            room(r).at[:, lanes], za_r.at[(r ^ source) - 1, :, lanes], ozs.at[part, r], ozr.at[part, source], (at.c, r)
        )

    def arrival(j, part):
        lanes = part_lanes[part]
        return remote(
            room(f).at[:, lanes], za_r.at[j - 1, :, lanes], ozs.at[part, f], ozr.at[part, f ^ j], at.along(j)
        )

    middle_token = CLASSES // 2 * tokens

    def sides_of():
        return [
            remote(
                yf_all.at[pl.ds(side * middle_token, middle_token)],
                wu.at[pl.ds(0, middle_token), pl.ds(side * half, half)],
                hs.at[side], hr.at[side], pair,
            )
            for side in range(2)
        ]

    def produce(r, put):
        at_rows = pl.ds(pl.multiple_of(r * rows, 16), rows)
        every = slice(0, half)

        @pl.when(p == 1)
        def _():
            put(slice(0, width), jnp.dot(xa_all[at_rows, :], yf_all[:, pl.ds(0, width)], preferred_element_type=F32))

        @pl.when((p != 1) & (p < WIDE))
        def _():
            put(every, jnp.dot(xf_all[at_rows, :], yf_all[...], preferred_element_type=F32))

        @pl.when(p >= WIDE)
        def _():
            side, start = lax.div(r * columns, half), pl.multiple_of(lax.rem(r * columns, half), 128)
            for t in range(2):
                part_rows = pl.ds(pl.multiple_of((p - WIDE) * tall + t * rows, 16), rows)
                lanes = slice(t * columns, (t + 1) * columns)

                @pl.when(side == core)
                def _():
                    put(
                        lanes,
                        jnp.dot(xf_all[part_rows, :], yf_all[:, pl.ds(start, columns)], preferred_element_type=F32),
                    )

                @pl.when(side != core)
                def _():
                    put(
                        lanes,
                        jnp.dot(
                            xf_all[part_rows, pl.ds(0, middle_token)],
                            wu[pl.ds(0, middle_token), pl.ds(start, columns)],
                            preferred_element_type=F32,
                        )
                        + jnp.dot(
                            xf_all[part_rows, pl.ds(middle_token, middle_token)],
                            wu[pl.ds(0, middle_token), pl.ds(pl.multiple_of(half + start, 128), columns)],
                            preferred_element_type=F32,
                        ),
                    )

    def keep_chunk(r):
        def put(lanes, value):
            own[:, lanes] = value
            room(r)[:, lanes] = value.astype(BF16)

        return put

    def gradients(conditions):
        for bits in range(1, CLASSES):
            arrived_y(p ^ bits)

        @pl.when(p >= WIDE)
        def _():
            for copy in sides_of():
                copy.start()
            for copy in sides_of():
                copy.wait()

        def step_of(i, carry):
            r = order(i)
            produce(r, keep_chunk(r))
            for part in range(2):
                pl.when((i < parts - 1) & conditions[part]())(lambda part=part: line(r, f, part).start())
            return carry

        lax.fori_loop(0, parts, step_of, 0)

    def value_gradient():
        for q in range(CLASSES):
            if q != 1:
                remote(dv_in, yv_all.at[tokens_of(q)], vs, vr.at[q], pair).wait_recv()

        def step_of(i, carry):
            r = order(i)
            at_rows = pl.ds(pl.multiple_of(r * rows, 16), rows)
            value = jnp.dot(xf_all[at_rows, :], yv_all[...], preferred_element_type=F32)

            @pl.when(i < parts - 1)
            def _():
                room(r)[:, pl.ds(width, keys)] = value[:, :keys].astype(BF16)
                line(r, f, 1).start()

            @pl.when(i == parts - 1)
            def _():
                own[:, pl.ds(width, keys)] = value[:, :keys]

            return carry

        lax.fori_loop(0, parts, step_of, 0)

    def arrived_y(q):
        remote(dy_in.at[0], yf_all.at[tokens_of(q)], ys.at[1], yr.at[q], pair).wait_recv()

    def arrived_x(q):
        remote(xt_in.at[0], xf_all.at[:, tokens_of(q)], xs.at[2], xr.at[q], pair).wait_recv()

    def x_pair(bits):
        q = p ^ bits
        return remote(xf_all.at[:, tokens_of(q)], xf_all.at[:, tokens_of(q)], ps.at[bits], pr.at[q], pair)

    def attend_back(g):
        chance = probs[g]
        out_grad = heads_of(att, g)
        query = heads_of(rot, g)
        grad_probs = contract(values_of(g), out_grad, 1, 1)
        delta = jnp.sum(grad_probs * chance, axis=0, keepdims=True)
        grad_scores = (chance * (grad_probs - delta)).astype(BF16)
        grad_values = jnp.dot(chance.astype(BF16), out_grad, preferred_element_type=F32)
        grad_keys = jnp.dot(grad_scores, query, preferred_element_type=F32) * scale
        dkv[:, :, g * HEAD : (g + 1) * HEAD] = grad_keys.reshape(CLASSES, tokens, HEAD)
        dkv[:, :, keys + g * HEAD : keys + (g + 1) * HEAD] = grad_values.reshape(CLASSES, tokens, HEAD)
        turned = contract(keys_of(g), grad_scores, 0, 0).T * scale
        for h in range(group):
            at_lane = (g * group + h) * HEAD
            gate[:, at_lane : at_lane + HEAD] = turned[h * tokens : (h + 1) * tokens]

    for g in range(KV_HEADS):
        attend_back(g)

    def halve(bit, rest, sbuf, rbuf, index, between=None):
        for i, bits in enumerate(rest):
            sbuf[i // 2, :, pl.ds(i % 2 * 2 * keys, 2 * keys)] = dkv[p ^ bit ^ bits].astype(BF16)
        copy = remote(sbuf, rbuf, ds.at[index], dr.at[index], at.peer(bit))
        copy.start()
        if between is not None:
            between()
        copy.wait()
        for i, bits in enumerate(rest):
            dkv[p ^ bits] = dkv[p ^ bits] + rbuf[i // 2, :, pl.ds(i % 2 * 2 * keys, 2 * keys)].astype(F32)

    own_x.wait()
    for bits in (2, 4, 6):
        arrived_x(p ^ bits)
    for bits in (0, 2, 4, 6):
        x_pair(bits).start()

    def early():
        for bits in (0, 2, 4, 6):
            remote(
                xf_all.at[:, tokens_of(p ^ bits ^ 1)], xf_all.at[:, tokens_of(p ^ bits ^ 1)],
                ps.at[bits], pr.at[p ^ bits ^ 1], pair,
            ).wait_recv()
        pl.semaphore_wait(free.at[0], 1)

        @pl.when(p == 1)
        def _():
            own_a().wait()
            for q in range(CLASSES):
                if q != 1:
                    remote(xt_in.at[1], xa_all.at[:, tokens_of(q)], as_, ar.at[q], pair).wait_recv()

        @pl.when(p >= 1)
        def _():
            own_y().start()
            own_y().wait()
            gradients(parts_early)

    halve(1, (0, 2, 4, 6), c_send, c4r, 0)
    halve(at.b1, (0, at.b2), c4r.at[pl.ds(0, 1)], c2r, 1, early)
    halve(at.b2, (0,), c4r.at[pl.ds(1, 1), :, pl.ds(0, 2 * keys)], c1r, 2)

    gate[:, width:half] = dkv[p, :, :keys]
    for tile, value in enumerate(turn(gate[:, :half], -1)):
        dy_in[0, :, tile * 128 : (tile + 1) * 128] = value.astype(BF16)
    dv_in[...] = jnp.zeros(dv_in.shape, BF16)
    dv_in[:, :keys] = dkv[p, :, keys:].astype(BF16)
    for bits in range(1, CLASSES):
        give_y(bits, 0, 1)
    pl.when(p != 1)(lambda: v_move().start())
    pl.when(p == 1)(lambda: own_v().start())
    grad_normed = contract(dy_in[0], w01[0], 1, 1)
    grad_normed = grad_normed + contract(dv_in[:, :keys], w01[1, :, width:], 1, 1)
    through, gain_first = norm_back(residual, inverse_first, gains_ref[0:1, :], grad_normed)
    gain_s[0, 0:1, :] = gain_first
    swaps = [swap(0, pair)]
    swaps[0].start()
    grad_ref[...] = (grad_middle + through).T
    @pl.when(p == 0)
    def _():
        own_y().start()
        own_y().wait()
        gradients(parts_late)

    @pl.when(p == 1)
    def _():
        own_v().wait()
        value_gradient()

    swaps[0].wait()
    gain_s[1] = gain_s[0] + gain_r[0]
    swaps.append(swap(1, at.peer(2)))
    swaps[1].start()
    for bits in (0, 2, 4, 6):
        x_pair(bits).wait_send()
    for bits in range(1, CLASSES):
        y_move(bits).wait_send()
    for bits in (2, 4, 6):
        x_move(bits).wait_send()

    @pl.when(p != 1)
    def _():
        a_move().wait_send()
        v_move().wait_send()

    swaps[1].wait()
    gain_s[2] = gain_s[1] + gain_r[1]
    swaps.append(swap(2, at.peer(4)))
    swaps[2].start()

    moment("wait")

    @pl.when(p < 2)
    def _():
        ma[:, :width] = mq[...]
        ma[:, width:] = mk[...].T

    sall = wd.at[:, pl.ds(0, half)]
    ga, pa = (w01.at[1, pl.ds((parts - 1 - i) * rows, rows)] for i in range(2))

    def shard(index, part):
        return sall.at[pl.ds(pl.multiple_of(index * rows, 16), rows), part_lanes[part]]

    def rightward(index, part):
        here = shard(index, part)
        return remote(here, here, ls_r.at[part, index], lr_r.at[part, index], (at.c, lax.rem(f + 1, parts)))

    def leftward(index, part):
        here = shard(index, part)
        return remote(here, here, ls_l.at[part, index], lr_l.at[part, index], (at.c, lax.rem(f + parts - 1, parts)))

    can_right = f < parts - 1
    can_left = f > 0

    def settle_part(part):
        lanes = part_lanes[part]
        total = own[:, lanes]
        for j in range(1, parts):
            arrival(j, part).wait_recv()
            total = total + za_r[j - 1, :, lanes].astype(F32)
        ga[:, lanes] = total.astype(BF16)
        sall[my_rows, lanes] = (MOMENTUM * ma[:, lanes] + total).astype(BF16)
        pl.when(can_right)(lambda: rightward(f, part).start())
        pl.when(can_left)(lambda: leftward(f, part).start())

    def hop_part(hop, part):
        @pl.when(f - hop >= 0)
        def _():
            rightward(f - hop, part).wait_recv()
            pl.when(can_right)(lambda: rightward(f - hop, part).start())

        @pl.when(f + hop < parts)
        def _():
            leftward(f + hop, part).wait_recv()
            pl.when(can_left)(lambda: leftward(f + hop, part).start())

    spread_begin, spread_step, spread_finish = spread_even(at, ga, g_out, ag_l, ag_s, ag_r)
    for conditions, whole in ((parts_early, p >= 2), (parts_late, p < 2)):
        for part in range(2):
            pl.when(conditions[part]())(lambda part=part: settle_part(part))
        pl.when(whole)(spread_begin)
        for hop in range(1, parts):
            for part in range(2):
                pl.when(conditions[part]())(lambda hop=hop, part=part: hop_part(hop, part))

    swaps[2].wait()
    gain_s[3] = gain_s[2] + gain_r[2]
    line_gain = [
        remote(gain_s.at[3], gain_r.at[3 + j], gs.at[3 + j], gr.at[3 + j], at.along(j)) for j in range(1, parts)
    ]
    for copy in line_gain:
        copy.start()

    for part in range(2):
        for j in range(1, parts):
            line(f ^ j, f, part).wait_send()
        pl.when(can_right)(lambda: rightward(f, part).wait_send())
        pl.when(can_left)(lambda: leftward(f, part).wait_send())
        for hop in range(1, parts):
            pl.when((f - hop >= 0) & can_right)(lambda hop=hop: rightward(f - hop, part).wait_send())
            pl.when((f + hop < parts) & can_left)(lambda hop=hop: leftward(f + hop, part).wait_send())
    pl.semaphore_signal(free.at[1], inc=1, device_id=pair, device_id_type=MESH)
    pl.semaphore_wait(free.at[1], 1)

    x = w01.at[0]
    wide_gram = 1024
    gram_s, g = wg.at[:, pl.ds(0, wide_gram)], wg.at[:, pl.ds(wide_gram, wide_gram)]
    poly, xf = wd.at[:, pl.ds(0, wide_gram)], wd.at[:, pl.ds(half, columns)]
    step = width // 4

    def gram_r(slot):
        return wu.at[:, pl.ds(slot * wide_gram, wide_gram)]

    def scale_of(total):
        return 1.0 / (jnp.sqrt(total) + 1e-07)

    def normal(ref, inverse):
        ref[...] = rounded(ref[...].astype(F32) * inverse)

    def exchange(slot, r):
        part = pl.ds(r * step, step)
        return remote(gram_s.at[part], gram_r(slot).at[part], gsem.at[r], rsem.at[slot, r], pair)

    def poly_of(start, count):
        part = g[pl.ds(start, count), pl.ds(0, width)]
        square = jnp.dot(part, g[:, pl.ds(0, width)], preferred_element_type=F32)
        return rounded(NS_B * part.astype(F32) + NS_C * square)

    def fill_poly():
        for r in range(4):
            poly[pl.ds(r * step, step), pl.ds(0, width)] = poly_of(r * step, step)

    near = parts // 2
    mine_at = core * near
    last_core = lax.div(f, near)
    f_lanes = pl.ds(pl.multiple_of(lax.rem(f, near) * columns, 128), columns)

    kt = wd.at[pl.ds(0, keys), pl.ds(half + 256, wide_gram)]

    def xo(i):
        return w01.at[1, pl.ds(i * rows, rows)]

    def give():
        return [
            remote(
                sall.at[pl.ds(pl.multiple_of(((1 - core) * near + i) * rows, 16), rows)],
                xo(i), ex_s.at[i], ex_r.at[i], pair,
            )
            for i in range(near)
        ]

    def give_last():
        return remote(x.at[:, f_lanes], xf, fx_s, fx_r, pair)

    @pl.when(p >= 2)
    def _():
        @pl.when(p >= WIDE)
        def _():
            copies = give()
            for copy in copies:
                copy.start()
            for i in range(near):
                part = sall[pl.ds(pl.multiple_of((mine_at + i) * rows, 16), rows), :]
                for t in range(2):
                    x[pl.ds(pl.multiple_of(core * tall + t * rows, 16), rows), pl.ds(i * columns, columns)] = part[
                        :, t * columns : (t + 1) * columns
                    ]
            for i, copy in enumerate(copies):
                copy.wait()
                part = xo(i)
                for t in range(2):
                    x[pl.ds(pl.multiple_of((1 - core) * tall + t * rows, 16), rows), pl.ds(i * columns, columns)] = part[
                        :, pl.ds(t * columns, columns)
                    ]

        def squares(ref):
            wide = ref[...].astype(F32)
            sq[...] = jnp.broadcast_to(jnp.sum(wide * wide), sq.shape)

        pl.when(p < WIDE)(lambda: squares(sall))
        pl.when(p >= WIDE)(lambda: squares(x))
        copy = remote(sq, sq_r, qs, qr, pair)
        copy.start()
        copy.wait()
        inverse = scale_of(sq[...] + sq_r[...])[:1, :1]

        @pl.when(p < WIDE)
        def _():
            x[...] = rounded(sall[...].astype(F32) * inverse)

        pl.when(p >= WIDE)(lambda: normal(x, inverse))

        def grams(slot):
            for r in range(4):
                gram_s[pl.ds(r * step, step), pl.ds(0, width)] = rounded(
                    contract(x[pl.ds(r * step, step), :], x[...], 1, 1)
                )
                exchange(slot, r).start()
            for r in range(4):
                part = pl.ds(r * step, step)
                exchange(slot, r).wait()
                g[part, pl.ds(0, width)] = rounded(
                    gram_s[part, pl.ds(0, width)].astype(F32) + gram_r(slot)[part, pl.ds(0, width)].astype(F32)
                )

        def iterate(slot):
            grams(slot)
            fill_poly()
            for tile in range(half // 256):
                part = pl.ds(tile * 256, 256)
                x[:, part] = rounded(
                    NS_A * x[:, part].astype(F32) + jnp.dot(poly[:, pl.ds(0, width)], x[:, part], preferred_element_type=F32)
                )

        def iterate_twice(it, carry):
            iterate(0)
            pl.when(it == 1)(lambda: spread_step(1))
            iterate(1)
            pl.when(it == 0)(lambda: spread_step(0))
            pl.when(it == 1)(lambda: spread_step(2))
            return carry

        lax.fori_loop(0, (NS_ITERS - 1) // 2, iterate_twice, 0)

        @pl.when((p >= WIDE) & (core == last_core))
        def _():
            give_last().start()
            xf[...] = x[:, f_lanes]

        grams(0)

        @pl.when(p < WIDE)
        def _():
            part = poly_of(pl.multiple_of(f * rows, 16), rows)
            pa[...] = rounded(NS_A * x[my_rows, :].astype(F32) + jnp.dot(part, x[...], preferred_element_type=F32))

        @pl.when(p >= WIDE)
        def _():
            pl.when(core == last_core)(lambda: give_last().wait_send())
            pl.when(core != last_core)(lambda: give_last().wait_recv())
            for t in range(2):
                top = pl.multiple_of(core * tall + t * rows, 16)
                part = poly_of(top, rows)
                pa[:, t * columns : (t + 1) * columns] = rounded(
                    NS_A * xf[pl.ds(top, rows), :].astype(F32) + jnp.dot(part, xf[...], preferred_element_type=F32)
                )

    @pl.when(p < 2)
    def _():
        x[...] = sall[...]
        kt[:, pl.ds(0, width)] = x[:, pl.ds(width, keys)].T
        turned = kt[:, pl.ds(0, width)].astype(F32)
        kt[:, pl.ds(0, width)] = rounded(turned * scale_of(jnp.sum(turned * turned)))
        wide = x[:, pl.ds(0, width)].astype(F32)
        x[:, pl.ds(0, width)] = rounded(wide * scale_of(jnp.sum(wide * wide)))

        def narrow_step(it, carry):
            now = kt[:, pl.ds(0, width)]
            gram = rounded(contract(now, now, 1, 1))
            turned = rounded(NS_B * gram.astype(F32) + NS_C * jnp.dot(gram, gram, preferred_element_type=F32))
            kt[:, pl.ds(0, width)] = rounded(
                NS_A * now.astype(F32) + jnp.dot(turned, now, preferred_element_type=F32)
            )
            return carry

        lax.fori_loop(0, NS_ITERS, narrow_step, 0)

        def gram_of():
            for r in range(4):
                part = pl.ds(r * step, step)
                g[part, pl.ds(0, width)] = rounded(contract(x[part, pl.ds(0, width)], x[:, pl.ds(0, width)], 1, 1))

        def square_step(it, carry):
            gram_of()
            fill_poly()
            x[:, pl.ds(0, width)] = rounded(
                NS_A * x[:, pl.ds(0, width)].astype(F32) + jnp.dot(poly[:, pl.ds(0, width)], x[:, pl.ds(0, width)], preferred_element_type=F32)
            )
            for k in range(3):
                pl.when(it == k + 1)(lambda k=k: spread_step(k))
            return carry

        lax.fori_loop(0, NS_ITERS - 1, square_step, 0)
        gram_of()
        part = poly_of(pl.multiple_of(f * rows, 16), rows)
        square = rounded(
            NS_A * x[my_rows, pl.ds(0, width)].astype(F32) + jnp.dot(part, x[:, pl.ds(0, width)], preferred_element_type=F32)
        )
        x[:, pl.ds(width, keys)] = kt[:, pl.ds(0, width)].T
        pa[:, :width] = square
        pa[:, width:] = x[my_rows, pl.ds(width, keys)]

    out_begin, out_step, out_finish = spread_even(at, pa, o_out, og_l, og_s, og_r)
    out_begin()
    total = gain_s[3]
    for j in range(1, parts):
        line_gain[j - 1].wait()
        total = total + gain_r[3 + j]
    gain_out[...] = total
    spread_finish()
    for k in range(3):
        out_step(k)
    for copy in sent:
        copy.wait_send()
    out_finish()


def step_pass(x, up, gains, tables, bias, shards, moments):
    parts = lax.axis_size("fsdp")
    width, tokens = x.shape
    half = shards[4].shape[1] // 2
    rows = width // parts
    keys = half - width
    near = parts // 2
    dma = pltpu.SemaphoreType.DMA
    vm = pltpu.VMEM
    group = HEADS // KV_HEADS
    two = 2 * keys
    n_gain = 3 + parts
    return pl.pallas_call(
        step_kernel,
        out_shape=(
            jax.ShapeDtypeStruct((width, tokens), BF16),
            jax.ShapeDtypeStruct((width, tokens), F32),
            jax.ShapeDtypeStruct((CLASSES, rows, half), BF16),
            jax.ShapeDtypeStruct((CLASSES, rows, half), BF16),
            jax.ShapeDtypeStruct((8, width), F32),
        ),
        in_specs=[VMEM] * 11 + [ANY] * 10,
        out_specs=(VMEM, VMEM, ANY, ANY, VMEM),
        scratch_shapes=[
            vm((2, width, half), BF16),
            vm((width, 2 * half), BF16),
            vm((width, 2 * half), BF16),
            vm((width, 2 * half), BF16),
            vm((KV_HEADS, CLASSES * tokens, group * tokens), F32),
            vm((CLASSES, tokens, two), BF16),
            vm((tokens, half), BF16),
            vm((CLASSES, tokens, two), F32),
            vm((2, tokens, 2 * two), BF16),
            vm((2, tokens, 2 * two), BF16),
            vm((1, tokens, 2 * two), BF16),
            vm((1, tokens, two), BF16),
            vm((tokens, width), BF16),
            vm((tokens, 2 * half), F32),
            vm((2 * tokens, half), F32),
            vm((4, width, tokens), BF16),
            vm((CLASSES, tokens, half), BF16),
            vm((tokens, -(-keys // 128) * 128), BF16),
            vm((width, CLASSES * tokens), BF16),
            vm((width, CLASSES * tokens), BF16),
            vm((CLASSES * tokens, half), BF16),
            vm((CLASSES * tokens, -(-keys // 128) * 128), BF16),
            vm((parts - 1, rows, half), BF16),
            vm((rows, half), F32),
            vm((rows, width), F32),
            vm((keys, rows), F32),
            vm((4, 8, width), F32),
            vm((n_gain, 8, width), F32),
            vm((8, 128), F32),
            vm((8, 128), F32),
            dma((3,)), dma((4, parts)), dma((4, parts)), dma((4, 2, parts)), dma((4, 4, parts)),
            dma((4, CLASSES, parts)), dma((7,)), dma((CLASSES,)), dma((3,)), dma((3,)),
            dma((4,)), dma((CLASSES,)), dma((CLASSES,)), dma((CLASSES,)), dma((CLASSES,)),
            dma((CLASSES,)), dma((CLASSES,)), dma, dma((CLASSES,)), dma, dma((CLASSES,)),
            dma((2,)), dma((2,)), dma((2, parts)), dma((2, parts)),
            dma((2,)), dma((n_gain,)), dma((n_gain,)),
            dma, dma((7,)), dma((CLASSES,)),
            dma((2, parts)), dma((2, parts)), dma((2, parts)), dma((2, parts)),
            dma((4,)), dma((2, 4)), dma, dma,
            dma((near,)), dma((near,)), dma, dma,
            dma, dma((7,)), dma((CLASSES,)), pltpu.SemaphoreType.REGULAR((2,)),
        ],
        compiler_params=pltpu.CompilerParams(
            collective_id=3, has_side_effects=True, vmem_limit_bytes=63 << 20
        ),
        name="step_pass",
    )(x, up, gains, *tables, bias, *shards, *moments)


def settle_wide(factors, *refs):
    gs, os = refs[0], refs[1]
    ms, ws, outs = refs[2:6], refs[6:10], refs[10:]
    width = ms[0].shape[1]
    half = gs.shape[2]

    def one(index, g, o, lanes):
        grad, moment, weight = (outs[3 * index + i] for i in range(3))
        value = g.astype(F32)
        grad[:, lanes] = value
        moment[:, lanes] = MOMENTUM * ms[index][:, lanes] + value
        weight[:, lanes] = ws[index][:, lanes].astype(F32) + factors[index] * o.astype(F32)

    for index in range(2):
        one(index, gs[index, :, :width], os[index, :, :width], slice(0, width))
    for index in range(2):
        for side in range(2):
            cls = 2 + 2 * index + side
            one(2 + index, gs[cls], os[cls], slice(side * half, (side + 1) * half))


def settle_turned(factors, g_tall, o_tall, g_pair, o_pair, *refs):
    ms, ws, outs = refs[0:3], refs[3:6], refs[6:]
    keys = ms[1].shape[0]

    def one(index, g, o):
        grad, moment, weight = (outs[3 * index + i] for i in range(3))
        grad[...] = g
        moment[...] = MOMENTUM * ms[index][...] + g
        weight[...] = ws[index][...].astype(F32) + factors[index] * o

    one(0, g_tall[0].astype(F32), o_tall[0].astype(F32))

    @pl.when(pl.program_id(0) == 0)
    def _():
        for index in range(2):
            start = g_pair.shape[2] - keys
            one(1 + index, g_pair[index, :, start:].astype(F32).T, o_pair[index, :, start:].astype(F32).T)


def settle(g, o, moments, shards, factors):
    m_q, m_k, m_o, m_v, m_gate, m_up, m_down = moments
    w_q, w_k, w_o, w_v, w_gate, w_up, w_down = shards
    f_q, f_k, f_v, f_o, f_gate, f_up, f_down = factors
    _, rows, half = g.shape
    width, columns = m_down.shape
    block = 48 if rows % 48 == 0 else rows
    piece = pl.BlockSpec((WIDE, block, half), lambda i: (0, i, 0))

    def row_block(array):
        return pl.BlockSpec((block, array.shape[1]), lambda i: (i, 0))

    def result(arrays):
        return tuple(jax.ShapeDtypeStruct(array.shape, F32) for array in arrays for _ in range(3))

    wide = (m_q, m_o, m_gate, m_up)
    first = pl.pallas_call(
        functools.partial(settle_wide, (f_q, f_o, f_gate, f_up)),
        grid=(rows // block,),
        out_shape=result(wide),
        in_specs=[piece, piece] + [row_block(array) for array in wide] * 2,
        out_specs=tuple(row_block(array) for array in wide for _ in range(3)),
        compiler_params=pltpu.CompilerParams(vmem_limit_bytes=48 << 20),
        name="settle_wide",
    )(g, o, *wide, w_q, w_o, w_gate, w_up)

    turned = (m_down, m_k, m_v)
    halves = half // columns
    tile = pl.BlockSpec((1, rows, columns), lambda i: (WIDE + i // halves, 0, i % halves))
    both = pl.BlockSpec((2, rows, half), lambda i: (0, 0, 0))
    specs = [pl.BlockSpec((rows, columns), lambda i: (i, 0))] + [
        pl.BlockSpec(array.shape, lambda i: (0, 0)) for array in turned[1:]
    ]
    second = pl.pallas_call(
        functools.partial(settle_turned, (f_down, f_k, f_v)),
        grid=(width // rows,),
        out_shape=result(turned),
        in_specs=[tile, tile, both, both] + specs * 2,
        out_specs=tuple(spec for spec in specs for _ in range(3)),
        compiler_params=pltpu.CompilerParams(vmem_limit_bytes=48 << 20),
        name="settle_turned",
    )(g, o, g, o, *turned, w_down, w_k, w_v)
    q, out, gate, up = (first[3 * i : 3 * i + 3] for i in range(4))
    down, k, v = (tuple(item.T for item in second[3 * i : 3 * i + 3]) for i in range(3))
    return list(zip(q, k, v, out, gate, up, down))


def rotary_tables(positions, width):
    half = width // 2
    frequency = THETA ** (-(jnp.arange(half, dtype=jnp.float32) * 2.0 / width))
    angle = positions.astype(jnp.float32)[:, None] * frequency[None, :]
    return (jnp.cos(angle)[:, None, :], jnp.sin(angle)[:, None, :])


def rotate(value, cosine, sine):
    half = value.shape[-1] // 2
    first = value[..., :half]
    second = value[..., half:]
    return jnp.concatenate(
        [first * cosine - second * sine, second * cosine + first * sine], axis=-1
    )


def unrotate(incoming, cosine, sine):
    half = incoming.shape[-1] // 2
    upper = incoming[..., :half]
    lower = incoming[..., half:]
    return jnp.concatenate([upper * cosine + lower * sine, lower * cosine - upper * sine], axis=-1)


def norm_forward(residual, gain):
    inverse = lax.rsqrt(jnp.mean(residual * residual, axis=-1, keepdims=True) + EPS)
    return ((residual * inverse * gain).astype(jnp.bfloat16), inverse)


def norm_backward(residual, inverse, gain, incoming):
    scaled = incoming * gain
    through = inverse * scaled - residual * inverse**3 * jnp.mean(
        scaled * residual, axis=-1, keepdims=True
    )
    return (through, jnp.sum(incoming * residual * inverse, axis=0))


def padded(array, axis, parts, count, full):
    if count == full:
        return array
    shape = array.shape
    split = array.reshape(shape[:axis] + (parts, count) + shape[axis + 1 :])
    pads = [(0, 0)] * split.ndim
    pads[axis + 1] = (0, full - count)
    return jnp.pad(split, pads).reshape(shape[:axis] + (parts * full,) + shape[axis + 1 :])


def trimmed(array, axis, parts, count, full):
    if count == full:
        return array
    shape = array.shape
    split = array.reshape(shape[:axis] + (parts, full) + shape[axis + 1 :])
    kept = lax.slice_in_dim(split, 0, count, axis=axis + 1)
    return kept.reshape(shape[:axis] + (parts * count,) + shape[axis + 1 :])


def plain_layer(
    layer_input, output_grad, wide, tall, norm_gains, block_order, sizes
):
    parts, width, half, kv, short, full, high = sizes
    hidden_size = 2 * half
    rows = layer_input.shape[1]
    block = rows // 2
    group = HEADS // KV_HEADS
    scale = 1.0 / math.sqrt(HEAD)
    ctx_place = lax.axis_index("ctx")
    offsets = jnp.arange(block, dtype=jnp.int32)
    own_blocks = lax.dynamic_slice_in_dim(block_order, 2 * ctx_place, 2)
    query_pos = (own_blocks[:, None] * block + offsets[None, :]).reshape(rows)
    key_pos = (block_order[:, None] * block + offsets[None, :]).reshape(-1)

    all_wide, all_tall = gather_weights(wide, tall)
    w_qk, w_ov, w_gate_0, w_gate_1, w_up_0, w_up_1 = [all_wide[i].reshape(width, half) for i in range(WIDE)]
    w_down = [all_tall[i].reshape(half, width) for i in range(2)]

    residual = layer_input[0].astype(jnp.float32)
    normed_first, inverse_first = norm_forward(residual, norm_gains[0])
    qk_pre = jnp.dot(normed_first, w_qk, preferred_element_type=jnp.float32)
    query_pre = qk_pre[:, :width].reshape(rows, HEADS, HEAD)
    key_pre = qk_pre[:, width:].reshape(rows, KV_HEADS, HEAD)
    value_low = (
        jnp.dot(normed_first, w_ov, preferred_element_type=jnp.float32)[:, width:]
        .astype(jnp.bfloat16)
        .reshape(rows, KV_HEADS, HEAD)
    )
    cosine, sine = rotary_tables(query_pos, HEAD)
    query_rot = rotate(query_pre, cosine, sine).astype(jnp.bfloat16)
    key_rot = rotate(key_pre, cosine, sine).astype(jnp.bfloat16)
    keys_all, values_all = (
        lax.all_gather(key_rot, "ctx", axis=0, tiled=True),
        lax.all_gather(value_low, "ctx", axis=0, tiled=True),
    )
    keys_head = keys_all.transpose(1, 0, 2)
    values_head = values_all.transpose(1, 0, 2)
    queries_head = (
        query_rot.reshape(rows, KV_HEADS, group, HEAD)
        .transpose(1, 2, 0, 3)
        .reshape(KV_HEADS, group * rows, HEAD)
    )
    row_pos = jnp.tile(query_pos, group)
    allowed = key_pos[None, :] <= row_pos[:, None]

    def head_forward(item):
        query, key, value = item
        scores = jnp.where(allowed, contract(query, key, 1, 1) * scale, MASKED)
        top = jnp.max(scores, axis=-1, keepdims=True)
        expo = jnp.exp(scores - top)
        total = jnp.sum(expo, axis=-1, keepdims=True)
        probs_low = (expo / total).astype(jnp.bfloat16)
        return (
            jnp.dot(probs_low, value, preferred_element_type=jnp.float32),
            (top + jnp.log(total))[:, 0],
        )

    mixed, log_total = lax.map(head_forward, (queries_head, keys_head, values_head))
    attended = (
        mixed.reshape(KV_HEADS, group, rows, HEAD)
        .transpose(2, 0, 1, 3)
        .reshape(rows, HEADS * HEAD)
        .astype(jnp.bfloat16)
    )
    w_out = w_ov[:, :width]
    middle = residual + jnp.dot(attended, w_out, preferred_element_type=jnp.float32)
    normed_second, inverse_second = norm_forward(middle, norm_gains[1])

    def sides(left, right):
        return jnp.concatenate([left, right], axis=1)

    gate = sides(
        jnp.dot(normed_second, w_gate_0, preferred_element_type=jnp.float32),
        jnp.dot(normed_second, w_gate_1, preferred_element_type=jnp.float32),
    )
    lifted = sides(
        jnp.dot(normed_second, w_up_0, preferred_element_type=jnp.float32),
        jnp.dot(normed_second, w_up_1, preferred_element_type=jnp.float32),
    )
    sigma = jax.nn.sigmoid(gate)
    hidden = (gate * sigma * lifted).astype(jnp.bfloat16)
    hidden_split = hidden.reshape(rows, parts, 2, high)
    hidden_sides = [hidden_split[:, :, i].reshape(rows, half) for i in range(2)]
    layer_output = (
        middle
        + jnp.dot(hidden_sides[0], w_down[0], preferred_element_type=jnp.float32)
        + jnp.dot(hidden_sides[1], w_down[1], preferred_element_type=jnp.float32)
    ).astype(jnp.bfloat16)
    upstream = output_grad[0]
    grad_hidden = jnp.stack(
        [contract(upstream, w_down[i], 1, 1).reshape(rows, parts, high) for i in range(2)], axis=2
    ).reshape(rows, hidden_size)
    grad_gate = (grad_hidden * lifted * sigma * (1.0 + gate * (1.0 - sigma))).astype(jnp.bfloat16)
    grad_lifted = (grad_hidden * gate * sigma).astype(jnp.bfloat16)
    grad_normed_second = (
        contract(grad_gate[:, :half], w_gate_0, 1, 1)
        + contract(grad_gate[:, half:], w_gate_1, 1, 1)
        + contract(grad_lifted[:, :half], w_up_0, 1, 1)
        + contract(grad_lifted[:, half:], w_up_1, 1, 1)
    )
    through_second, gain_second = norm_backward(
        middle, inverse_second, norm_gains[1], grad_normed_second
    )
    grad_middle = upstream.astype(jnp.float32) + through_second
    grad_branch = grad_middle.astype(jnp.bfloat16)
    grad_attended = contract(grad_branch, w_out, 1, 1).astype(jnp.bfloat16)
    grad_heads = (
        grad_attended.reshape(rows, KV_HEADS, group, HEAD)
        .transpose(1, 2, 0, 3)
        .reshape(KV_HEADS, group * rows, HEAD)
    )

    def head_backward(item):
        query, key, value, grad_out, log_row = item
        scores = jnp.where(allowed, contract(query, key, 1, 1) * scale, MASKED)
        probs = jnp.exp(scores - log_row[:, None])
        grad_value_part = contract(probs.astype(jnp.bfloat16), grad_out, 0, 0)
        grad_probs = contract(grad_out, value, 1, 1)
        grad_scores = (
            probs * (grad_probs - jnp.sum(grad_probs * probs, axis=-1, keepdims=True))
        ).astype(jnp.bfloat16)
        grad_query_part = jnp.dot(grad_scores, key, preferred_element_type=jnp.float32) * scale
        grad_key_part = contract(grad_scores, query, 0, 0) * scale
        return (grad_query_part, grad_key_part, grad_value_part)

    grad_query_rot, grad_key_all, grad_value_all = lax.map(
        head_backward, (queries_head, keys_head, values_head, grad_heads, log_total)
    )
    grad_key_own, grad_value_own = (
        lax.psum_scatter(
            grad_key_all.astype(jnp.bfloat16), "ctx", scatter_dimension=1, tiled=True
        ).astype(jnp.float32),
        lax.psum_scatter(
            grad_value_all.astype(jnp.bfloat16), "ctx", scatter_dimension=1, tiled=True
        ).astype(jnp.float32),
    )
    grad_query = (
        unrotate(
            grad_query_rot.reshape(KV_HEADS, group, rows, HEAD)
            .transpose(2, 0, 1, 3)
            .reshape(rows, HEADS, HEAD),
            cosine,
            sine,
        )
        .reshape(rows, HEADS * HEAD)
        .astype(jnp.bfloat16)
    )
    grad_key = (
        unrotate(grad_key_own.transpose(1, 0, 2), cosine, sine)
        .reshape(rows, KV_HEADS * HEAD)
        .astype(jnp.bfloat16)
    )
    grad_value = (
        grad_value_own.transpose(1, 0, 2).reshape(rows, KV_HEADS * HEAD).astype(jnp.bfloat16)
    )
    grad_qk = sides(grad_query, grad_key)
    zero_query = jnp.zeros((rows, width), jnp.bfloat16)
    grad_v = sides(zero_query, grad_value)
    grad_normed_first = contract(grad_qk, w_qk, 1, 1) + contract(grad_v, w_ov, 1, 1)
    through_first, gain_first = norm_backward(
        residual, inverse_first, norm_gains[0], grad_normed_first
    )
    input_gradient = grad_middle + through_first

    xt = jnp.stack([item.T for item in (normed_first, attended, normed_second, upstream)])
    xt = padded(xt, 1, parts, short, full)
    dy = jnp.stack(
        [
            grad_qk,
            sides(grad_branch, jnp.zeros((rows, kv), jnp.bfloat16)),
            grad_gate[:, :half],
            grad_gate[:, half:],
            grad_lifted[:, :half],
            grad_lifted[:, half:],
            hidden_sides[0],
            hidden_sides[1],
            grad_v,
        ]
    )
    gains = jnp.pad(jnp.stack([gain_first, gain_second]), ((0, 6), (0, 0)))
    return layer_output, input_gradient, xt, dy, gains


def rotation(block_order, rows):
    block = rows // 2
    ctx_place = lax.axis_index("ctx")
    offsets = jnp.arange(block, dtype=jnp.int32)
    own_blocks = lax.dynamic_slice_in_dim(block_order, 2 * ctx_place, 2)
    query_pos = (own_blocks[:, None] * block + offsets[None, :]).reshape(rows)
    key_pos = (block_order[:, None] * block + offsets[None, :]).reshape(-1)
    bias = jnp.where(key_pos[:, None] <= query_pos[None, :], 0.0, MASKED).astype(jnp.bfloat16)
    lane = jnp.arange(128, dtype=jnp.int32)
    index = (lane % (HEAD // 2)).astype(jnp.float32)
    frequency = THETA ** (-(index * 2.0 / HEAD))
    angle = query_pos.astype(jnp.float32)[:, None] * frequency[None, :]
    cosine, sine = jnp.cos(angle), jnp.sin(angle)
    early = (lane % HEAD < HEAD // 2)[None, :]
    return (cosine, jnp.where(early, 0.0, sine), jnp.where(early, -sine, 0.0)), bias


def plain_step(layer_input, output_grad, norm_gains, block_order, weights, olds, factors, sizes):
    parts, width, half, kv, short, full, high = sizes
    query_weight, key_weight, value_weight, output_weight, gate_weight, up_weight, down_weight = weights
    (
        query_momentum,
        key_momentum,
        value_momentum,
        output_momentum,
        gate_momentum,
        up_momentum,
        down_momentum,
    ) = olds

    def sides(left, right):
        return jnp.concatenate([left, right], axis=1)

    wide = jnp.stack(
        [
            jnp.concatenate([query_weight, key_weight], axis=1),
            jnp.concatenate([output_weight, value_weight], axis=1),
            gate_weight[:, :half],
            gate_weight[:, half:],
            up_weight[:, :half],
            up_weight[:, half:],
        ]
    )
    tall = down_weight.reshape(2, high, width)
    layer_output, input_gradient, xt, dy, gains = plain_layer(
        layer_input, output_grad, wide, tall, norm_gains, block_order, sizes
    )

    def pad_rows(array):
        return padded(array, 0, 1, short, full)

    def pad_columns(array):
        return padded(array, 1, parts, short, full)

    moments = (
        pad_rows(sides(query_momentum, key_momentum)),
        pad_rows(sides(output_momentum, value_momentum)),
        pad_rows(gate_momentum),
        pad_rows(up_momentum),
        pad_columns(down_momentum),
    )
    g_wide, g_tall, s_wide, s_tall, gain_sum = reduce_gradients(xt, dy, gains, moments, full, high)
    o_wide, o_tall = orthogonalize(s_wide, s_tall, full, high, width)

    def unpack(wide_pieces, tall_pieces):
        pieces = wide_pieces[:, :short]
        tall = trimmed(tall_pieces, 2, parts, short, full).reshape(2 * high, width)
        return (
            pieces[0, :, :width],
            pieces[0, :, width:],
            pieces[1, :, width:],
            pieces[1, :, :width],
            sides(pieces[2], pieces[3]),
            sides(pieces[4], pieces[5]),
            tall,
        )

    gradients = [item.astype(jnp.float32) for item in unpack(g_wide, g_tall)]
    orthos = unpack(o_wide, o_tall)
    moments = [MOMENTUM * old + new for old, new in zip(olds, gradients)]
    new_weights = [
        weight.astype(jnp.float32) + factor * ortho.astype(jnp.float32)
        for weight, factor, ortho in zip(weights, factors, orthos)
    ]
    return layer_output, input_gradient, gradients, moments, new_weights, gain_sum


def on_device(
    layer_input,
    output_grad,
    query_weight,
    key_weight,
    value_weight,
    output_weight,
    gate_weight,
    up_weight,
    down_weight,
    norm_gains,
    query_momentum,
    key_momentum,
    value_momentum,
    output_momentum,
    gate_momentum,
    up_momentum,
    down_momentum,
    gain_momentum,
    block_order,
):
    parts = lax.axis_size("fsdp")
    width = layer_input.shape[2]
    half = gate_weight.shape[1] // 2
    kv = key_weight.shape[1]
    short = width // parts
    full = -(-short // 16) * 16
    high = half // parts
    sizes = (parts, width, half, kv, short, full, high)

    weights = (query_weight, key_weight, value_weight, output_weight, gate_weight, up_weight, down_weight)
    olds = (
        query_momentum,
        key_momentum,
        value_momentum,
        output_momentum,
        gate_momentum,
        up_momentum,
        down_momentum,
    )
    factors = []
    for index, weight in enumerate(weights):
        step_rate = OUT_RATE if index == 3 else RATE
        factors.append(-step_rate * max(1.0, weight.shape[1] / (weight.shape[0] * parts)) ** 0.5)

    fused = (
        lax.axis_size("ctx") == CLASSES
        and short == full
        and parts % 2 == 0
        and half % (2 * half // parts) == 0
        and (2 * half // parts) % 128 == 0
        and layer_input.shape[1] == 128
        and short <= 256
    )
    if fused:
        tables, bias = rotation(block_order, layer_input.shape[1])

        def turned(items):
            q, k, v, o, gate, up, down = items
            return (q, k.T, o, v.T, gate, up, down.T)

        shards, moments = turned(weights), turned(olds)
        out_turned, grad_turned, g, o, gain_sum = step_pass(
            layer_input[0].T, output_grad[0].T, norm_gains, tables, bias, shards, moments
        )
        gradients, moments, new_weights = settle(g, o, moments, shards, factors)
        layer_output, input_gradient = out_turned.T, grad_turned.T
    else:
        layer_output, input_gradient, gradients, moments, new_weights, gain_sum = plain_step(
            layer_input, output_grad, norm_gains, block_order, weights, olds, factors, sizes
        )
    gain_width = norm_gains.shape[1] // parts
    place = lax.axis_index("fsdp") * gain_width
    gain_gradient = lax.dynamic_slice_in_dim(gain_sum[:2], place, gain_width, 1)
    gain_shard = lax.dynamic_slice_in_dim(norm_gains, place, gain_width, 1)
    gain_moment = MOMENTUM * gain_momentum + gain_gradient
    new_gains = gain_shard - GAIN_RATE * gain_moment
    return (
        layer_output[None],
        input_gradient[None],
        *gradients,
        gain_gradient,
        *moments,
        gain_moment,
        *new_weights,
        new_gains,
    )


def solution(mesh):
    tokens = P("fsdp", "ctx", None)
    shard = P("fsdp", None)
    gains = P(None, "fsdp")
    return jax.shard_map(
        on_device,
        mesh=mesh,
        in_specs=(tokens, tokens) + (shard,) * 7 + (P(),) + (shard,) * 7 + (gains, P()),
        out_specs=(tokens, tokens) + ((shard,) * 7 + (gains,)) * 3,
        check_vma=False,
    )
```

```python
import functools
import math

import jax
import jax.numpy as jnp
from jax import lax
from jax.experimental import pallas as pl
from jax.experimental.pallas import tpu as pltpu
from jax.sharding import PartitionSpec as P

HEADS = 15
KV_HEADS = 5
HEAD = 64
NS_ITERS = 5


EPS = 1e-05
THETA = 100000.0
NS_A = 3.4445
NS_B = -4.775
NS_C = 2.0315
MOMENTUM = 0.95
RATE = 0.2
OUT_RATE = 6.0
GAIN_RATE = 0.002
MASKED = -1e30

MESH = pl.DeviceIdType.MESH
BF16 = jnp.bfloat16
F32 = jnp.float32
ANY = pl.BlockSpec(memory_space=pl.ANY)
VMEM = pl.BlockSpec(memory_space=pltpu.VMEM)
CLASSES = 8
WIDE = 6


def contract(left, right, left_dim, right_dim):
    return lax.dot_general(
        left, right, (((left_dim,), (right_dim,)), ((), ())), preferred_element_type=jnp.float32
    )


class Place:
    def __init__(self):
        self.parts = lax.axis_size("fsdp")
        self.extra = lax.axis_size("ctx") // CLASSES
        self.c = lax.axis_index("ctx")
        self.f = lax.axis_index("fsdp")
        self.p = lax.rem(self.c, CLASSES)
        self.core = lax.rem(self.c, 2)
        self.b1 = jnp.where(self.core == 0, 2, 4)
        self.b2 = jnp.where(self.core == 0, 4, 2)

    def peer(self, bits):
        return (self.c ^ bits, self.f)

    def along(self, j):
        return (self.c, self.f ^ j)

    def other(self, j):
        groups = self.extra
        return (lax.rem(self.c + CLASSES * j, CLASSES * groups), self.f)

    def barrier(self, bits=(1, 2, 4), line=True, others=False):
        sem = pltpu.get_barrier_semaphore()
        targets = [self.peer(b) for b in bits]
        if line:
            targets += [self.along(j) for j in range(1, self.parts)]
        if others:
            targets += [self.other(j) for j in range(1, self.extra)]
        for target in targets:
            pl.semaphore_signal(sem, inc=1, device_id=target, device_id_type=MESH)
        pl.semaphore_wait(sem, len(targets))


def remote(src, dst, send, recv, target):
    return pltpu.make_async_remote_copy(
        src_ref=src, dst_ref=dst, send_sem=send, recv_sem=recv, device_id=target, device_id_type=MESH
    )


def by_kind(cls, wide, tall):
    pl.when(cls < WIDE)(wide)
    pl.when(cls >= WIDE)(tall)


def weights_kernel(in_a, in_b, out_a, out_b, local, zs, s1, s2, sc, recv):
    at = Place()
    p, f, parts = at.p, at.f, at.parts
    at.barrier()
    copies = [
        pltpu.make_async_copy(in_a, out_a.at[:, f], local.at[0]),
        pltpu.make_async_copy(in_b, out_b.at[:, f], local.at[1]),
    ]
    for copy in copies:
        copy.start()

    def act(cls, j, g, send, target, what, first=False):
        def wide():
            dst = out_a.at[cls, g]
            src = in_a.at[cls] if first else dst
            getattr(remote(src, dst, send, recv.at[cls, j], target), what)()

        def tall():
            dst = out_b.at[cls - WIDE, g]
            src = in_b.at[cls - WIDE] if first else dst
            getattr(remote(src, dst, send, recv.at[cls, j], target), what)()

        by_kind(cls, wide, tall)

    sends = []

    def send(cls, j, g, sem, target, first=False):
        act(cls, j, g, sem, target, "start", first)
        sends.append((cls, j, g, sem, target, first))

    def arrived(cls, j):
        act(cls, j, f ^ j, zs.at[j], at.along(j), "wait_recv")

    for j in range(1, parts):
        send(p, j, f, zs.at[j], at.along(j), True)
    for j in range(1, parts):
        arrived(p, j)
        send(p, j, f ^ j, s1.at[0, j], at.peer(at.b1))
        send(p, j, f ^ j, s2.at[0, j], at.peer(at.b2))
        send(p, j, f ^ j, sc.at[0, j], at.peer(1))
    for j in range(1, parts):
        arrived(p ^ at.b1, j)
        send(p ^ at.b1, j, f ^ j, s2.at[1, j], at.peer(at.b2))
        send(p ^ at.b1, j, f ^ j, sc.at[1, j], at.peer(1))
    for slot, bits in ((2, at.b2), (3, at.b1 ^ at.b2)):
        for j in range(1, parts):
            arrived(p ^ bits, j)
            send(p ^ bits, j, f ^ j, sc.at[slot, j], at.peer(1))
    for bits in (1, 3, 5, 7):
        for j in range(1, parts):
            arrived(p ^ bits, j)
    for cls, j, g, sem, target, first in sends:
        act(cls, j, g, sem, target, "wait_send", first)
    for copy in copies:
        copy.wait()


def gather_weights(wide, tall):
    parts = lax.axis_size("fsdp")
    dma = pltpu.SemaphoreType.DMA
    return pl.pallas_call(
        weights_kernel,
        out_shape=(
            jax.ShapeDtypeStruct((WIDE, parts) + wide.shape[1:], BF16),
            jax.ShapeDtypeStruct((CLASSES - WIDE, parts) + tall.shape[1:], BF16),
        ),
        in_specs=[ANY, ANY],
        out_specs=(ANY, ANY),
        scratch_shapes=[
            dma((2,)),
            dma((parts,)),
            dma((1, parts)),
            dma((2, parts)),
            dma((4, parts)),
            dma((CLASSES, parts)),
        ],
        compiler_params=pltpu.CompilerParams(collective_id=0, has_side_effects=True),
        name="gather_weights",
    )(wide, tall)


def spread(at, own_a, own_b, out_a, out_b, local, ss, recv):
    p = at.p

    def act(cls, sem, target, what, first=False):
        def wide():
            dst = out_a.at[cls]
            getattr(remote(own_a if first else dst, dst, sem, recv.at[cls], target), what)()

        def tall():
            dst = out_b.at[cls - WIDE]
            getattr(remote(own_b if first else dst, dst, sem, recv.at[cls], target), what)()

        by_kind(cls, wide, tall)

    def keep(what):
        def wide():
            getattr(pltpu.make_async_copy(own_a, out_a.at[p], local), what)()

        def tall():
            getattr(pltpu.make_async_copy(own_b, out_b.at[p - WIDE], local), what)()

        by_kind(p, wide, tall)

    sends = []

    def send(cls, slot, target, first=False):
        act(cls, ss.at[slot], target, "start", first)
        sends.append((cls, slot, target, first))

    def arrived(cls):
        act(cls, ss.at[0], at.peer(1), "wait_recv")

    send(p, 0, at.peer(at.b1), True)
    send(p, 1, at.peer(at.b2), True)
    send(p, 2, at.peer(1), True)
    keep("start")

    def finish():
        arrived(p ^ at.b1)
        send(p ^ at.b1, 3, at.peer(at.b2))
        send(p ^ at.b1, 4, at.peer(1))
        arrived(p ^ at.b2)
        send(p ^ at.b2, 5, at.peer(1))
        arrived(p ^ at.b1 ^ at.b2)
        send(p ^ at.b1 ^ at.b2, 6, at.peer(1))
        for bits in (1, 3, 5, 7):
            arrived(p ^ bits)
        for cls, slot, target, first in sends:
            act(cls, ss.at[slot], target, "wait_send", first)
        keep("wait")

    return finish


def reduce_kernel(
    parts, extra, high,
    xt_in, dy_in, gain_in, m_qk, m_ov, m_gate, m_up, m_down,
    g_a, g_b, s_a, s_b, gain_out,
    xt, dy, p1s, p1r, p2s, p2r, own, own_t, za_s, za_r, zb_s, zb_r, ma, mb, ga, gb, sa, sb, es, er, gain_s, gain_r,
    ls, xs, xr, s1, r1, s2, r2, zs, zr, esem, ersem, msem, gs, gr, ag_l, ag_s, ag_r, ss, sr, sl,
):
    at = Place()
    p, f, core = at.p, at.f, at.core
    tokens = xt_in.shape[2]
    rows = ma.shape[0]
    half = dy.shape[2]

    def moment(what):
        for cls in range(CLASSES):
            @pl.when(p == cls)
            def _(cls=cls):
                side = cls % 2
                if cls < 2:
                    src, dst = (m_qk, m_ov)[cls], ma
                elif cls < WIDE:
                    whole = m_gate if cls < 4 else m_up
                    src, dst = whole.at[:, pl.ds(side * half, half)], ma
                else:
                    src, dst = m_down.at[pl.ds(side * high, high)], mb
                getattr(pltpu.make_async_copy(src, dst, msem), what)()

    moment("start")
    mine = [pltpu.make_async_copy(xt_in, xt.at[:, :, pl.ds(0, tokens)], ls.at[0])]
    for slot in range(4):
        mine.append(
            pltpu.make_async_copy(dy_in.at[core + 2 * slot], dy.at[slot, pl.ds(0, tokens)], ls.at[1 + slot])
        )
    mine.append(pltpu.make_async_copy(dy_in.at[8], dy.at[4, pl.ds(0, tokens)], ls.at[5]))
    for copy in mine:
        copy.start()
    at.barrier(others=True)
    pair = at.peer(1)
    theirs = [remote(xt_in, xt.at[:, :, pl.ds(tokens, tokens)], xs.at[0], xr.at[0], pair)]
    for slot in range(4):
        theirs.append(
            remote(dy_in.at[1 - core + 2 * slot], dy.at[slot, pl.ds(tokens, tokens)], xs.at[1 + slot], xr.at[1 + slot], pair)
        )
    theirs.append(remote(dy_in.at[8], dy.at[4, pl.ds(tokens, tokens)], xs.at[5], xr.at[5], pair))
    for copy in theirs:
        copy.start()

    def swap(slot, target):
        return remote(gain_s.at[slot], gain_r.at[slot], gs.at[slot], gr.at[slot], target)

    gain_s[0] = gain_in[...]
    swaps = [swap(0, pair)]
    swaps[0].start()
    for copy in mine:
        copy.wait()
    for copy in theirs:
        copy.wait()

    def term(cls, r):
        at_rows = pl.ds(pl.multiple_of(r * rows, rows), rows)
        slot = lax.div(cls, 2)
        kind = jnp.where(cls == 0, 0, jnp.where(cls == 1, 1, jnp.where(cls < WIDE, 2, 3)))
        value = jnp.dot(xt[kind, at_rows, :], dy[slot], preferred_element_type=F32)
        return value

    def with_values(cls, r, put):
        at_rows = pl.ds(pl.multiple_of(r * rows, rows), rows)

        @pl.when(cls == 1)
        def _():
            put(term(cls, r) + jnp.dot(xt[0, at_rows, :], dy[4], preferred_element_type=F32))

        @pl.when(cls != 1)
        def _():
            put(term(cls, r))

    def order(i):
        return lax.rem(f + 1 + i, parts)

    def one(slot, i):
        r = order(i)
        return remote(p1s.at[slot, r], p1r.at[slot, r], s1.at[slot, r], r1.at[slot, r], at.peer(at.b1))

    for slot, bits in ((0, at.b1 ^ at.b2), (1, at.b1)):
        def first(i, carry, slot=slot, bits=bits):
            r = order(i)

            def put(value):
                p1s[slot, r] = value.astype(BF16)

            with_values(p ^ bits, r, put)
            one(slot, i).start()
            return carry

        lax.fori_loop(0, parts, first, 0)

    swaps[0].wait()
    gain_s[1] = gain_s[0] + gain_r[0]
    swaps.append(swap(1, at.peer(2)))
    swaps[1].start()

    def two(i):
        r = order(i)
        return remote(p2s.at[r], p2r.at[r], s2.at[r], r2.at[r], at.peer(at.b2))

    def second(i, carry):
        r = order(i)
        one(0, i).wait_recv()

        def put(value):
            p2s[r] = (value + p1r[0, r].astype(F32)).astype(BF16)

        with_values(p ^ at.b2, r, put)
        two(i).start()
        return carry

    lax.fori_loop(0, parts, second, 0)
    swaps[1].wait()
    gain_s[2] = gain_s[1] + gain_r[1]
    swaps.append(swap(2, at.peer(4)))
    swaps[2].start()

    def line_a(r, source):
        return remote(za_s.at[r], za_r.at[source], zs.at[r], zr.at[source], (at.c, r))

    def line_b(r, source):
        return remote(
            zb_s.at[pl.ds(pl.multiple_of(r * high, high), high)],
            zb_r.at[source], zs.at[r], zr.at[source], (at.c, r),
        )

    early = extra == 1

    def third(i, carry):
        r = order(i)
        one(1, i).wait_recv()
        two(i).wait_recv()

        def put(value):
            total = value + p1r[1, r].astype(F32) + p2r[r].astype(F32)
            own[r] = total
            if early:
                za_s[r] = total.astype(BF16)

        with_values(p, r, put)
        if early:
            @pl.when((p < WIDE) & (i < parts - 1))
            def _():
                line_a(r, f).start()
        return carry

    lax.fori_loop(0, parts, third, 0)
    swaps[2].wait()
    gain_s[3] = gain_s[2] + gain_r[2]

    if not early:
        es[...] = own[...].astype(BF16)
        group = [
            remote(es, er.at[j - 1], esem.at[j - 1], ersem.at[j - 1], at.other(j)) for j in range(1, extra)
        ]
        for copy in group:
            copy.start()
        for j in range(1, extra):
            group[j - 1].wait_recv()
            own[...] = own[...] + er[j - 1].astype(F32)
        for copy in group:
            copy.wait_send()
        za_s[...] = own[...].astype(BF16)

        @pl.when(p < WIDE)
        def _():
            for j in range(1, parts):
                line_a(f ^ j, f).start()

    @pl.when(p >= WIDE)
    def _():
        for tile in range(half // 128):
            for r in range(parts):
                block = own[r, :, pl.ds(tile * 128, 128)]
                if rows % 128 == 0:
                    own_t[pl.ds(tile * 128, 128), pl.ds(r * rows, rows)] = block.T
            if rows % 128 != 0:
                column = own[:, :, pl.ds(tile * 128, 128)].reshape(parts * rows, 128)
                own_t[pl.ds(tile * 128, 128), :] = column.T
        zb_s[...] = own_t[...].astype(BF16)
        for j in range(1, parts):
            line_b(f ^ j, f).start()

    line_gain = [
        remote(gain_s.at[3], gain_r.at[3 + j], gs.at[3 + j], gr.at[3 + j], at.along(j)) for j in range(1, parts)
    ]
    other_gain = []
    for copy in line_gain:
        copy.start()

    moment("wait")

    @pl.when(p < WIDE)
    def _():
        total = own[f]
        for j in range(1, parts):
            line_a(f ^ j, f ^ j).wait_recv()
            total = total + za_r[f ^ j].astype(F32)
        ga[...] = total.astype(BF16)
        sa[...] = (MOMENTUM * ma[...] + total).astype(BF16)

    @pl.when(p >= WIDE)
    def _():
        total = own_t[pl.ds(pl.multiple_of(f * high, high), high), :]
        for j in range(1, parts):
            line_b(f ^ j, f ^ j).wait_recv()
            total = total + zb_r[f ^ j].astype(F32)
        gb[...] = total.astype(BF16)
        sb[...] = (MOMENTUM * mb[...] + total).astype(BF16)

    def share_a(j, source):
        return remote(sa, s_a.at[pl.ds(pl.multiple_of(source * rows, rows), rows)], ss.at[j], sr.at[j], at.along(j))

    def share_b(j, source):
        return remote(sb, s_b.at[pl.ds(pl.multiple_of(source * high, high), high)], ss.at[j], sr.at[j], at.along(j))

    @pl.when(p < WIDE)
    def _():
        for j in range(1, parts):
            share_a(j, f).start()
        pltpu.make_async_copy(sa, s_a.at[pl.ds(pl.multiple_of(f * rows, rows), rows)], sl).start()

    @pl.when(p >= WIDE)
    def _():
        for j in range(1, parts):
            share_b(j, f).start()
        pltpu.make_async_copy(sb, s_b.at[pl.ds(pl.multiple_of(f * high, high), high)], sl).start()

    finish = spread(at, ga, gb, g_a, g_b, ag_l, ag_s, ag_r)
    total = gain_s[3]
    for j in range(1, parts):
        line_gain[j - 1].wait()
        total = total + gain_r[3 + j]
    if extra > 1:
        gain_s[4] = total
        other_gain = [
            remote(gain_s.at[4], gain_r.at[3 + parts + j], gs.at[3 + parts + j], gr.at[3 + parts + j], at.other(j))
            for j in range(1, extra)
        ]
        for copy in other_gain:
            copy.start()
        for j in range(1, extra):
            other_gain[j - 1].wait()
            total = total + gain_r[3 + parts + j]
    gain_out[...] = total
    finish()

    for slot in range(2):
        lax.fori_loop(0, parts, lambda i, carry, slot=slot: (one(slot, i).wait_send(), carry)[1], 0)
    lax.fori_loop(0, parts, lambda i, carry: (two(i).wait_send(), carry)[1], 0)

    @pl.when(p < WIDE)
    def _():
        for j in range(1, parts):
            line_a(f ^ j, f).wait_send()
            share_a(j, f).wait_send()
            share_a(j, f ^ j).wait_recv()
        pltpu.make_async_copy(sa, s_a.at[pl.ds(pl.multiple_of(f * rows, rows), rows)], sl).wait()

    @pl.when(p >= WIDE)
    def _():
        for j in range(1, parts):
            line_b(f ^ j, f).wait_send()
            share_b(j, f).wait_send()
            share_b(j, f ^ j).wait_recv()
        pltpu.make_async_copy(sb, s_b.at[pl.ds(pl.multiple_of(f * high, high), high)], sl).wait()


def reduce_gradients(xt, dy, gains, moments, rows, high):
    parts = lax.axis_size("fsdp")
    extra = lax.axis_size("ctx") // CLASSES
    kinds, depth, tokens = xt.shape
    half = dy.shape[2]
    dma = pltpu.SemaphoreType.DMA
    vm = pltpu.VMEM
    n_gain = 4 + parts + extra
    group = max(extra - 1, 1)
    spare = (parts, rows, half) if extra > 1 else (1, 16, 128)
    return pl.pallas_call(
        functools.partial(reduce_kernel, parts, extra, high),
        out_shape=(
            jax.ShapeDtypeStruct((WIDE, rows, half), BF16),
            jax.ShapeDtypeStruct((CLASSES - WIDE, high, depth), BF16),
            jax.ShapeDtypeStruct((depth, half), BF16),
            jax.ShapeDtypeStruct((half, depth), BF16),
            jax.ShapeDtypeStruct(gains.shape, F32),
        ),
        in_specs=[ANY, ANY, VMEM] + [ANY] * 5,
        out_specs=(ANY, ANY, ANY, ANY, VMEM),
        scratch_shapes=[
            vm((kinds, depth, 2 * tokens), BF16),
            vm((5, 2 * tokens, half), BF16),
            vm((2, parts, rows, half), BF16),
            vm((2, parts, rows, half), BF16),
            vm((parts, rows, half), BF16),
            vm((parts, rows, half), BF16),
            vm((parts, rows, half), F32),
            vm((half, depth), F32),
            vm((parts, rows, half), BF16),
            vm((parts, rows, half), BF16),
            vm((half, depth), BF16),
            vm((parts, high, depth), BF16),
            vm((rows, half), F32),
            vm((high, depth), F32),
            vm((rows, half), BF16),
            vm((high, depth), BF16),
            vm((rows, half), BF16),
            vm((high, depth), BF16),
            vm(spare, BF16),
            vm((group,) + spare, BF16),
            vm((5,) + gains.shape, F32),
            vm((n_gain,) + gains.shape, F32),
            dma((6,)), dma((6,)), dma((6,)),
            dma((2, parts)), dma((2, parts)), dma((parts,)), dma((parts,)), dma((parts,)), dma((parts,)),
            dma((group,)), dma((group,)), dma, dma((n_gain,)), dma((n_gain,)),
            dma, dma((7,)), dma((CLASSES,)), dma((parts,)), dma((parts,)), dma,
        ],
        compiler_params=pltpu.CompilerParams(
            collective_id=1, has_side_effects=True, vmem_limit_bytes=62 << 20
        ),
        name="reduce_gradients",
    )(xt, dy, gains, *moments)


def rounded(value):
    return value.astype(BF16)


def poly_rows(g, row_start, count):
    block = g[pl.ds(row_start, count), :]
    return rounded(NS_B * block.astype(F32) + NS_C * jnp.dot(block, g[...], preferred_element_type=F32))


def ortho_kernel(
    parts, rows, high, narrow,
    s_a, s_b, o_a, o_b,
    x, x_t, gs, gr, g, poly, sq, sq_r, pa, pb, kt,
    gsem, rsem, qs, qr, ag_l, ag_s, ag_r,
):
    at = Place()
    p, f = at.p, at.f
    depth, half = x.shape
    step = depth // 4
    at.barrier(line=False)
    pair = at.peer(1)

    @pl.when(p < WIDE)
    def _():
        x[...] = s_a[...]

    @pl.when(p >= WIDE)
    def _():
        for tile in range(half // 128):
            x[:, pl.ds(tile * 128, 128)] = s_b[pl.ds(tile * 128, 128), :].T

    def scale_of(total):
        return 1.0 / (jnp.sqrt(total) + 1e-07)

    def normal(ref, inverse):
        ref[...] = rounded(ref[...].astype(F32) * inverse)

    def exchange(slot, r):
        chunk = pl.ds(r * step, step)
        return remote(gs.at[chunk], gr.at[slot, chunk], gsem.at[r], rsem.at[slot, r], pair)

    def fill_poly():
        for r in range(4):
            poly[pl.ds(r * step, step), :] = poly_rows(g, r * step, step)

    my_rows = pl.ds(pl.multiple_of(f * rows, rows), rows)
    my_high = pl.ds(pl.multiple_of(f * high, high), high)

    @pl.when(p >= 2)
    def _():
        wide = x[...].astype(F32)
        sq[...] = jnp.broadcast_to(jnp.sum(wide * wide), sq.shape)
        copy = remote(sq, sq_r, qs, qr, pair)
        copy.start()
        copy.wait()
        normal(x, scale_of(sq[...] + sq_r[...])[:1, :1])

        def grams(slot):
            for r in range(4):
                gs[pl.ds(r * step, step), :] = rounded(contract(x[pl.ds(r * step, step), :], x[...], 1, 1))
                exchange(slot, r).start()
            for r in range(4):
                chunk = pl.ds(r * step, step)
                exchange(slot, r).wait()
                g[chunk, :] = rounded(gs[chunk, :].astype(F32) + gr[slot, chunk, :].astype(F32))

        def iterate(it, carry):
            grams(lax.rem(it, 2))
            fill_poly()
            for tile in range(half // 256):
                block = pl.ds(tile * 256, 256)
                x[:, block] = rounded(
                    NS_A * x[:, block].astype(F32) + jnp.dot(poly[...], x[:, block], preferred_element_type=F32)
                )
            return carry

        lax.fori_loop(0, NS_ITERS - 1, iterate, 0)
        grams((NS_ITERS - 1) % 2)

        @pl.when(p < WIDE)
        def _():
            mine = poly_rows(g, pl.multiple_of(f * rows, rows), rows)
            pa[...] = rounded(NS_A * x[my_rows, :].astype(F32) + jnp.dot(mine, x[...], preferred_element_type=F32))

        @pl.when(p >= WIDE)
        def _():
            fill_poly()
            for tile in range(half // 128):
                x_t[pl.ds(tile * 128, 128), :] = x[:, pl.ds(tile * 128, 128)].T
            block = x_t[my_high, :]
            pb[...] = rounded(NS_A * block.astype(F32) + jnp.dot(block, poly[...], preferred_element_type=F32))

    @pl.when(p < 2)
    def _():
        kt[...] = x[:, narrow:].T
        inverse_k = scale_of(jnp.sum(jnp.square(kt[...].astype(F32))))
        normal(kt, inverse_k)
        wide = x[:, :narrow].astype(F32)
        x[:, :narrow] = rounded(wide * scale_of(jnp.sum(wide * wide)))

        def narrow_step(it, carry):
            gram = rounded(contract(kt[...], kt[...], 1, 1))
            turn = rounded(NS_B * gram.astype(F32) + NS_C * jnp.dot(gram, gram, preferred_element_type=F32))
            kt[...] = rounded(NS_A * kt[...].astype(F32) + jnp.dot(turn, kt[...], preferred_element_type=F32))
            return carry

        lax.fori_loop(0, NS_ITERS, narrow_step, 0)

        def gram_of():
            for r in range(4):
                chunk = pl.ds(r * step, step)
                g[chunk, :] = rounded(contract(x[chunk, :narrow], x[:, :narrow], 1, 1))

        def square_step(it, carry):
            gram_of()
            fill_poly()
            x[:, :narrow] = rounded(
                NS_A * x[:, :narrow].astype(F32) + jnp.dot(poly[...], x[:, :narrow], preferred_element_type=F32)
            )
            return carry

        lax.fori_loop(0, NS_ITERS - 1, square_step, 0)
        gram_of()
        mine = poly_rows(g, pl.multiple_of(f * rows, rows), rows)
        square = rounded(
            NS_A * x[my_rows, :narrow].astype(F32) + jnp.dot(mine, x[:, :narrow], preferred_element_type=F32)
        )
        x[:, narrow:] = kt[...].T
        pa[:, :narrow] = square
        pa[:, narrow:] = x[my_rows, narrow:]

    spread(at, pa, pb, o_a, o_b, ag_l, ag_s, ag_r)()


def orthogonalize(s_a, s_b, rows, high, narrow):
    parts = lax.axis_size("fsdp")
    depth, half = s_a.shape
    dma = pltpu.SemaphoreType.DMA
    vm = pltpu.VMEM
    return pl.pallas_call(
        functools.partial(ortho_kernel, parts, rows, high, narrow),
        out_shape=(
            jax.ShapeDtypeStruct((WIDE, rows, half), BF16),
            jax.ShapeDtypeStruct((CLASSES - WIDE, high, depth), BF16),
        ),
        in_specs=[VMEM, VMEM],
        out_specs=(ANY, ANY),
        scratch_shapes=[
            vm((depth, half), BF16),
            vm((half, depth), BF16),
            vm((depth, depth), BF16),
            vm((2, depth, depth), BF16),
            vm((depth, depth), BF16),
            vm((depth, depth), BF16),
            vm((8, 128), F32),
            vm((8, 128), F32),
            vm((rows, half), BF16),
            vm((high, depth), BF16),
            vm((half - narrow, depth), BF16),
            dma((4,)), dma((2, 4)), dma, dma, dma, dma((7,)), dma((CLASSES,)),
        ],
        compiler_params=pltpu.CompilerParams(
            collective_id=2, has_side_effects=True, vmem_limit_bytes=62 << 20
        ),
        name="orthogonalize",
    )(s_a, s_b)


class Weights:
    def __init__(self, at, sources, homes, zs, s1, s2, sc, recv):
        self.at, self.sources, self.homes = at, sources, homes
        self.zs, self.s1, self.s2, self.sc, self.recv = zs, s1, s2, sc, recv
        self.sends = []
        self.done = 0

    def act(self, group, q, j, plane, send, target, what, first=False):
        recv = self.recv.at[group, q, j]
        home, source = self.homes[group], self.sources[group]
        rows = home.shape[-2] // (1 if group == 3 else self.at.parts)
        unit = -(-rows // (16 * CLASSES)) * 16
        last = rows - (CLASSES - 1) * unit

        def piece(count):
            def go():
                start = pl.multiple_of(q * unit, 16)
                if group == 3:
                    columns = home.shape[1] // self.at.parts
                    dst = home.at[pl.ds(start, count), pl.ds(pl.multiple_of(plane * columns, 128), columns)]
                    src = source.at[pl.ds(start, count)]
                elif group == 0:
                    dst = home.at[:, pl.ds(pl.multiple_of(plane * rows + start, 16), count)]
                    src = dst
                else:
                    dst = home.at[pl.ds(pl.multiple_of(plane * rows + start, 16), count)]
                    src = source.at[pl.ds(start, count)]
                getattr(remote(src if first else dst, dst, send, recv, target), what)()

            return go

        pl.when(q < CLASSES - 1)(piece(unit))
        pl.when(q == CLASSES - 1)(piece(last))

    def send(self, group, q, j, plane, sem, target, first=False):
        self.act(group, q, j, plane, sem, target, "start", first)
        self.sends.append((group, q, j, plane, sem, target, "wait_send", first))

    def arrived(self, group, q, j):
        at = self.at
        self.act(group, q, j, at.f ^ j, self.zs.at[group, j], at.peer(1), "wait_recv")

    def along(self, group):
        at = self.at
        for j in range(1, at.parts):
            self.send(group, at.p, j, at.f, self.zs.at[group, j], at.along(j), True)

    def first(self, group, j):
        at = self.at
        self.arrived(group, at.p, j)
        self.send(group, at.p, j, at.f ^ j, self.s1.at[group, j], at.peer(at.b1))
        self.send(group, at.p, j, at.f ^ j, self.s2.at[group, 0, j], at.peer(at.b2))
        self.send(group, at.p, j, at.f ^ j, self.sc.at[group, 0, j], at.peer(1))

    def second(self, group, j):
        at = self.at
        q = at.p ^ at.b1
        self.arrived(group, q, j)
        self.send(group, q, j, at.f ^ j, self.s2.at[group, 1, j], at.peer(at.b2))
        self.send(group, q, j, at.f ^ j, self.sc.at[group, 1, j], at.peer(1))

    def third(self, group, j):
        at = self.at
        for slot, bits in ((2, at.b2), (3, at.b1 ^ at.b2)):
            self.arrived(group, at.p ^ bits, j)
            self.send(group, at.p ^ bits, j, at.f ^ j, self.sc.at[group, slot, j], at.peer(1))

    def advance(self, count):
        each = self.at.parts - 1
        total = 4 * each
        count = max(count, 0)
        for n in range(self.done, min(self.done + count, total + 2)):
            for lag, act in ((0, self.first), (1, self.second), (2, self.third)):
                if 0 <= n - lag < total:
                    act((n - lag) // each, (n - lag) % each + 1)
        self.done += count

    def ready(self, group):
        at = self.at
        for bits in (1, 3, 5, 7):
            for j in range(1, at.parts):
                self.arrived(group, at.p ^ bits, j)

    def finish(self):
        for item in self.sends:
            self.act(*item)


def spread_even(at, own, out, local, ss, recv):
    p = at.p

    def copy_of(cls, slot, target, first=False):
        return remote(own if first else out.at[cls], out.at[cls], ss.at[slot], recv.at[cls], target)

    keep = pltpu.make_async_copy(own, out.at[p], local)
    b1, b2 = at.b1, at.b2
    own_sends = [(p, 0, b1, True), (p, 1, b2, True), (p, 2, 1, True)]
    steps = (
        (p ^ b1, [(p ^ b1, 3, b2, False), (p ^ b1, 4, 1, False)]),
        (p ^ b2, [(p ^ b2, 5, 1, False)]),
        (p ^ b1 ^ b2, [(p ^ b1 ^ b2, 6, 1, False)]),
    )

    def move(cls, slot, bits, first):
        return copy_of(cls, slot, at.peer(bits), first)

    def arrived(cls):
        copy_of(cls, 0, at.peer(1)).wait_recv()

    def begin():
        for item in own_sends:
            move(*item).start()
        keep.start()

    def step(k):
        cls, sends = steps[k]
        arrived(cls)
        for item in sends:
            move(*item).start()

    def finish():
        for bits in (1, 3, 5, 7):
            arrived(p ^ bits)
        for item in own_sends + [item for _, sends in steps for item in sends]:
            move(*item).wait_send()
        keep.wait()

    return begin, step, finish


def step_kernel(
    x_ref, up_ref, gains_ref, cos_ref, low_ref, high_ref, bias_ref, wq, wk, wo, wv, wg_in, wu_in, wd_in,
    m_q, m_k, m_o, m_v, m_gate, m_up, m_down,
    out_ref, grad_ref, g_out, o_out, gain_out,
    w01, wg, wu, wd, probs, kv, rot, dkv, c4r, c2r, c1r, att, gate, lifted,
    xt_in, dy_in, dv_in, xf_all, xa_all, yf_all, yv_all, za_r, ma, mq, mk, gain_s, gain_r, sq, sq_r,
    local, zs, s1, s2, sc, recv, kvs, kvr, ds, dr,
    ls, xs, xr, ps, pr, ys, yr, as_, ar, vs, vr, hs, hr, ozs, ozr, msem, gs, gr, ag_l, ag_s, ag_r, ls_l, ls_r, lr_l, lr_r,
    gsem, rsem, qs, qr, ex_s, ex_r, fx_s, fx_r, og_l, og_s, og_r, free,
):
    at = Place()
    p, f, core, parts = at.p, at.f, at.core, at.parts
    width, tokens = x_ref.shape
    half = w01.shape[2]
    keys = half - width
    group = HEADS // KV_HEADS
    scale = 1.0 / math.sqrt(HEAD)
    rows = width // parts
    columns = 2 * half // parts
    tall = width // 2
    pair = at.peer(1)
    my_rows = pl.ds(pl.multiple_of(f * rows, 16), rows)

    weights = Weights(at, (None, wg_in, wu_in, wd_in), (w01, wg, wu, wd), zs, s1, s2, sc, recv)
    keep = [
        pltpu.make_async_copy(wg_in, wg.at[my_rows], local.at[0]),
        pltpu.make_async_copy(wu_in, wu.at[my_rows], local.at[1]),
        pltpu.make_async_copy(
            wd_in, wd.at[:, pl.ds(pl.multiple_of(f * columns, 128), columns)], local.at[2]
        ),
    ]

    def moment(what):
        for cls in range(CLASSES):
            @pl.when(p == cls)
            def _(cls=cls):
                side = cls % 2
                if cls < 2:
                    pairs = [((m_q, m_o)[cls], mq, 0), ((m_k, m_v)[cls], mk, 1)]
                elif cls < WIDE:
                    whole = m_gate if cls < 4 else m_up
                    pairs = [(whole.at[:, pl.ds(side * half, half)], ma, 0)]
                else:
                    pairs = [
                        (
                            m_down.at[pl.ds(side * tall + t * rows, rows)],
                            ma.at[:, pl.ds(t * columns, columns)],
                            t,
                        )
                        for t in range(2)
                    ]
                for src, dst, index in pairs:
                    getattr(pltpu.make_async_copy(src, dst, msem.at[index]), what)()

    w01[0, my_rows, :width] = wq[...]
    w01[0, my_rows, width:] = wk[...].T
    w01[1, my_rows, :width] = wo[...]
    w01[1, my_rows, width:] = wv[...].T
    at.barrier(bits=range(1, CLASSES))
    for index in range(4):
        weights.along(index)
    for copy in keep:
        copy.start()
    moment("start")

    residual = x_ref[...].astype(F32).T
    upstream = up_ref[...].astype(F32).T
    inverse_first = lax.rsqrt(jnp.mean(residual * residual, axis=-1, keepdims=True) + EPS)
    normed_first = (residual * inverse_first * gains_ref[0:1, :]).astype(BF16)
    xt_in[0] = normed_first.T
    xt_in[3] = up_ref[...]

    each = parts - 1
    weights.advance(each + 2)
    weights.ready(0)

    def turn(value, sign):
        tiles = []
        for tile in range(half // 128):
            part = value[:, tile * 128 : (tile + 1) * 128]
            swapped = pltpu.roll(part, HEAD // 2, 1) * low_ref[...] + pltpu.roll(part, 128 - HEAD // 2, 1) * high_ref[...]
            tiles.append(part * cos_ref[...] + swapped if sign > 0 else part * cos_ref[...] - swapped)
        return tiles

    qk = jnp.dot(normed_first, w01[0], preferred_element_type=F32)
    for tile, value in enumerate(turn(qk, 1)):
        rot[:, tile * 128 : (tile + 1) * 128] = value.astype(BF16)
    values = jnp.dot(normed_first, w01[1, :, width:], preferred_element_type=F32).astype(BF16)
    kv[p, :, :keys] = rot[:, width:]
    kv[p, :, keys:] = values

    def block(q, slot, target):
        return remote(kv.at[q], kv.at[q], kvs.at[slot], kvr.at[q], target)

    sent = [block(p, 0, at.peer(at.b1)), block(p, 1, at.peer(at.b2)), block(p, 2, at.peer(1))]
    for copy in sent:
        copy.start()

    def pass_keys(q, slots):
        block(q, 0, at.peer(1)).wait_recv()
        for slot, target in slots:
            copy = block(q, slot, target)
            copy.start()
            sent.append(copy)

    weights.advance(1)
    pass_keys(p ^ at.b1, [(3, at.peer(at.b2)), (4, at.peer(1))])
    pass_keys(p ^ at.b2, [(5, at.peer(1))])
    weights.advance(1)
    pass_keys(p ^ at.b1 ^ at.b2, [(6, at.peer(1))])
    for bits in (1, 3, 5, 7):
        pass_keys(p ^ bits, [])
    weights.advance(1)

    def keys_of(g):
        return kv[:, :, g * HEAD : (g + 1) * HEAD].reshape(CLASSES * tokens, HEAD)

    def values_of(g):
        return kv[:, :, keys + g * HEAD : keys + (g + 1) * HEAD].reshape(CLASSES * tokens, HEAD)

    def heads_of(ref, g):
        return jnp.concatenate([ref[:, h * HEAD : (h + 1) * HEAD] for h in range(g * group, (g + 1) * group)], axis=0)

    def attend(g):
        scores = contract(keys_of(g), heads_of(rot, g), 1, 1) * scale
        bias = bias_ref[...].astype(F32)
        scores = scores + jnp.concatenate([bias] * group, axis=1)
        top = jnp.max(scores, axis=0, keepdims=True)
        expo = jnp.exp(scores - top)
        total = jnp.sum(expo, axis=0, keepdims=True)
        chance = expo * (1.0 / total)
        probs[g] = chance
        mixed = contract(values_of(g), chance.astype(BF16), 0, 0)
        turned = mixed.T.astype(BF16)
        for h in range(group):
            at_lane = (g * group + h) * HEAD
            att[:, at_lane : at_lane + HEAD] = turned[h * tokens : (h + 1) * tokens]

    for g in range(KV_HEADS):
        attend(g)
        weights.advance(1 if g < KV_HEADS - 1 else 4 * each - weights.done)
    for copy in keep:
        copy.wait()
    weights.ready(1)

    xt_in[1] = att[...].T
    middle = residual + jnp.dot(att[...], w01[1, :, :width], preferred_element_type=F32)
    inverse_second = lax.rsqrt(jnp.mean(middle * middle, axis=-1, keepdims=True) + EPS)
    normed_second = (middle * inverse_second * gains_ref[1:2, :]).astype(BF16)
    xt_in[2] = normed_second.T
    weights.advance(1)
    gate[...] = jnp.dot(normed_second, wg[...], preferred_element_type=F32)
    weights.advance(1)

    def tokens_of(q):
        return pl.ds(pl.multiple_of(q * tokens, tokens), tokens)

    def kind_of(q):
        return jnp.where(q < 2, 0, jnp.where(q < WIDE, 2, 3))

    own_x = pltpu.make_async_copy(xt_in.at[kind_of(p)], xf_all.at[:, tokens_of(p)], ls.at[0])

    def x_move(bits):
        q = p ^ bits
        return remote(xt_in.at[kind_of(q)], xf_all.at[:, tokens_of(p)], xs.at[bits], xr.at[p], at.peer(bits))

    def a_move():
        return remote(xt_in.at[1], xa_all.at[:, tokens_of(p)], as_, ar.at[p], at.peer(p ^ 1))

    def own_a():
        return pltpu.make_async_copy(xt_in.at[1], xa_all.at[:, tokens_of(p)], ls.at[1])

    def y_move(bits):
        q = p ^ bits
        return remote(dy_in.at[q], yf_all.at[tokens_of(p)], ys.at[bits], yr.at[p], at.peer(bits))

    def own_y():
        return pltpu.make_async_copy(dy_in.at[p], yf_all.at[tokens_of(p)], ls.at[2])

    def v_move():
        return remote(dv_in, yv_all.at[tokens_of(p)], vs, vr.at[p], at.peer(p ^ 1))

    def own_v():
        return pltpu.make_async_copy(dv_in, yv_all.at[tokens_of(p)], ls.at[3])

    own_x.start()
    for bits in (2, 4, 6):
        x_move(bits).start()
    pl.when(p != 1)(lambda: a_move().start())
    pl.when(p == 1)(lambda: own_a().start())

    def give_y(bits, low, high):
        q = p ^ bits

        @pl.when((q >= low) & (q < high))
        def _():
            y_move(bits).start()

    weights.ready(2)
    for side in range(2):
        lifted[side * tokens : (side + 1) * tokens] = jnp.dot(
            normed_second, wu[:, side * half : (side + 1) * half], preferred_element_type=F32
        )

    def lift():
        return jnp.concatenate([lifted[:tokens], lifted[tokens:]], axis=1)

    hidden = (gate[...] * jax.nn.sigmoid(gate[...]) * lift()).astype(BF16)
    dy_in[6] = hidden[:, :half]
    dy_in[7] = hidden[:, half:]
    for bits in range(1, CLASSES):
        give_y(bits, WIDE, CLASSES)
    weights.ready(3)

    grad_hidden = jnp.dot(upstream.astype(BF16), wd[...], preferred_element_type=F32)
    sigma = jax.nn.sigmoid(gate[...])
    grad_gate = (grad_hidden * lift() * sigma * (1.0 + gate[...] * (1.0 - sigma))).astype(BF16)
    grad_lifted = (grad_hidden * gate[...] * sigma).astype(BF16)
    for side in range(2):
        lanes = slice(side * half, (side + 1) * half)
        dy_in[2 + side] = grad_gate[:, lanes]
        dy_in[4 + side] = grad_lifted[:, lanes]
    for bits in range(1, CLASSES):
        give_y(bits, 2, WIDE)

    out_ref[...] = (middle + contract(hidden, wd[...], 1, 1)).T.astype(BF16)
    weights.finish()
    grad_normed = contract(grad_gate, wg[...], 1, 1) + contract(grad_lifted, wu[...], 1, 1)
    pl.semaphore_signal(free.at[0], inc=1, device_id=pair, device_id_type=MESH)

    def norm_back(value, inverse, gain, incoming):
        scaled = incoming * gain
        mean = jnp.mean(scaled * value, axis=-1, keepdims=True)
        through = inverse * scaled - value * (inverse * inverse * inverse) * mean
        return through, jnp.sum(incoming * value * inverse, axis=0, keepdims=True)

    through, gain_second = norm_back(middle, inverse_second, gains_ref[1:2, :], grad_normed)
    gain_s[0] = jnp.zeros(gain_s.shape[1:], F32)
    gain_s[0, 1:2, :] = gain_second
    grad_middle = upstream + through
    grad_branch = grad_middle.astype(BF16)
    dy_in[1, :, :width] = grad_branch
    dy_in[1, :, width:] = jnp.zeros((tokens, keys), BF16)
    att[...] = contract(grad_branch, w01[1, :, :width], 1, 1).astype(BF16)

    for bits in range(1, CLASSES):
        give_y(bits, 1, 2)

    own = lifted.at[pl.ds(0, rows)]

    def swap(slot, target):
        return remote(gain_s.at[slot], gain_r.at[slot], gs.at[slot], gr.at[slot], target)

    outer = (f == 0) | (f == parts - 1)
    lower = f < parts // 2
    beside = jnp.where(lower, 1 - f, 2 * parts - 3 - f)
    far_outer = jnp.where(lower, parts - 1, 0)
    far_inner = jnp.where(lower, parts // 2, parts // 2 - 1)

    def order(i):
        falling = jnp.where(outer, parts - 1 - i, jnp.where(i == 0, 0, parts - i))
        return jnp.where(lower, falling, parts - 1 - falling)

    cut = width // 128 * 128
    part_lanes = (pl.ds(0, cut), pl.ds(cut, half - cut))
    parts_early = (lambda: p >= 1, lambda: p >= 2)
    parts_late = (lambda: p < 1, lambda: p < 2)

    def room(r):
        return wd.at[pl.ds(pl.multiple_of(r * rows, 16), rows), pl.ds(half, half)]

    def line(r, part):
        lanes = part_lanes[part]
        near_slot = jnp.where(lower, r - 1, parts - 2 - r)
        slot = jnp.where(outer, 2 - near_slot, jnp.where(r == beside, 0, jnp.where(r == far_outer, 1, 3)))
        target = jnp.where(outer, beside, r)
        return remote(
            room(r).at[:, lanes], za_r.at[slot, :, lanes], ozs.at[part, r], ozr.at[part, slot], (at.c, target)
        )

    def arrival(slot, part):
        lanes = part_lanes[part]
        return remote(
            room(f).at[:, lanes], za_r.at[slot, :, lanes], ozs.at[part, f], ozr.at[part, slot], at.along(1)
        )

    def relay(k, part):
        r = (far_outer, far_inner)[k]
        lanes = part_lanes[part]

        @pl.when(jnp.logical_not(outer))
        def _():
            arrival(k, part).wait_recv()
            total = room(r)[:, lanes].astype(F32) + za_r[k, :, lanes].astype(F32)
            room(r)[:, lanes] = total.astype(BF16)
            line(r, part).start()

    middle_token = CLASSES // 2 * tokens

    def sides_of():
        return [
            remote(
                yf_all.at[pl.ds(side * middle_token, middle_token)],
                wu.at[pl.ds(0, middle_token), pl.ds(side * half, half)],
                hs.at[side], hr.at[side], pair,
            )
            for side in range(2)
        ]

    def produce(r, put):
        at_rows = pl.ds(pl.multiple_of(r * rows, 16), rows)
        every = slice(0, half)

        @pl.when(p == 1)
        def _():
            put(slice(0, width), jnp.dot(xa_all[at_rows, :], yf_all[:, pl.ds(0, width)], preferred_element_type=F32))

        @pl.when((p != 1) & (p < WIDE))
        def _():
            put(every, jnp.dot(xf_all[at_rows, :], yf_all[...], preferred_element_type=F32))

        @pl.when(p >= WIDE)
        def _():
            side, start = lax.div(r * columns, half), pl.multiple_of(lax.rem(r * columns, half), 128)
            for t in range(2):
                part_rows = pl.ds(pl.multiple_of((p - WIDE) * tall + t * rows, 16), rows)
                lanes = slice(t * columns, (t + 1) * columns)

                @pl.when(side == core)
                def _():
                    put(
                        lanes,
                        jnp.dot(xf_all[part_rows, :], yf_all[:, pl.ds(start, columns)], preferred_element_type=F32),
                    )

                @pl.when(side != core)
                def _():
                    put(
                        lanes,
                        jnp.dot(
                            xf_all[part_rows, pl.ds(0, middle_token)],
                            wu[pl.ds(0, middle_token), pl.ds(start, columns)],
                            preferred_element_type=F32,
                        )
                        + jnp.dot(
                            xf_all[part_rows, pl.ds(middle_token, middle_token)],
                            wu[pl.ds(0, middle_token), pl.ds(pl.multiple_of(half + start, 128), columns)],
                            preferred_element_type=F32,
                        ),
                    )

    def keep_chunk(r):
        def put(lanes, value):
            own[:, lanes] = value
            room(r)[:, lanes] = value.astype(BF16)

        return put

    def gradients(conditions):
        for bits in range(1, CLASSES):
            arrived_y(p ^ bits)

        @pl.when(p >= WIDE)
        def _():
            for copy in sides_of():
                copy.start()
            for copy in sides_of():
                copy.wait()

        def step_of(i, carry):
            r = order(i)
            produce(r, keep_chunk(r))
            goes = (i == 0) | (outer & (i < parts - 1))
            for part in range(2):
                pl.when(goes & conditions[part]())(lambda part=part: line(r, part).start())
            return carry

        lax.fori_loop(0, parts, step_of, 0)

    def value_gradient():
        for q in range(CLASSES):
            if q != 1:
                remote(dv_in, yv_all.at[tokens_of(q)], vs, vr.at[q], pair).wait_recv()

        def step_of(i, carry):
            r = order(i)
            at_rows = pl.ds(pl.multiple_of(r * rows, 16), rows)
            value = jnp.dot(xf_all[at_rows, :], yv_all[...], preferred_element_type=F32)

            @pl.when(i < parts - 1)
            def _():
                room(r)[:, pl.ds(width, keys)] = value[:, :keys].astype(BF16)
                pl.when((i == 0) | outer)(lambda: line(r, 1).start())

            @pl.when(i == parts - 1)
            def _():
                own[:, pl.ds(width, keys)] = value[:, :keys]

            return carry

        lax.fori_loop(0, parts, step_of, 0)

    def arrived_y(q):
        remote(dy_in.at[0], yf_all.at[tokens_of(q)], ys.at[1], yr.at[q], pair).wait_recv()

    def arrived_x(q):
        remote(xt_in.at[0], xf_all.at[:, tokens_of(q)], xs.at[2], xr.at[q], pair).wait_recv()

    def x_pair(bits):
        q = p ^ bits
        return remote(xf_all.at[:, tokens_of(q)], xf_all.at[:, tokens_of(q)], ps.at[bits], pr.at[q], pair)

    def attend_back(g):
        chance = probs[g]
        out_grad = heads_of(att, g)
        query = heads_of(rot, g)
        grad_probs = contract(values_of(g), out_grad, 1, 1)
        delta = jnp.sum(grad_probs * chance, axis=0, keepdims=True)
        grad_scores = (chance * (grad_probs - delta)).astype(BF16)
        grad_values = jnp.dot(chance.astype(BF16), out_grad, preferred_element_type=F32)
        grad_keys = jnp.dot(grad_scores, query, preferred_element_type=F32) * scale
        dkv[:, :, g * HEAD : (g + 1) * HEAD] = grad_keys.reshape(CLASSES, tokens, HEAD)
        dkv[:, :, keys + g * HEAD : keys + (g + 1) * HEAD] = grad_values.reshape(CLASSES, tokens, HEAD)
        turned = contract(keys_of(g), grad_scores, 0, 0).T * scale
        for h in range(group):
            at_lane = (g * group + h) * HEAD
            gate[:, at_lane : at_lane + HEAD] = turned[h * tokens : (h + 1) * tokens]

    for g in range(KV_HEADS):
        attend_back(g)

    def halve(bit, rest, sbuf, rbuf, index, between=None):
        for i, bits in enumerate(rest):
            sbuf[pl.ds(i // 2 * tokens, tokens), pl.ds(i % 2 * 2 * keys, 2 * keys)] = dkv[p ^ bit ^ bits].astype(BF16)
        copy = remote(sbuf, rbuf, ds.at[index], dr.at[index], at.peer(bit))
        copy.start()
        if between is not None:
            between()
        copy.wait()
        for i, bits in enumerate(rest):
            dkv[p ^ bits] = dkv[p ^ bits] + rbuf[pl.ds(i // 2 * tokens, tokens), pl.ds(i % 2 * 2 * keys, 2 * keys)].astype(F32)

    own_x.wait()
    for bits in (2, 4, 6):
        arrived_x(p ^ bits)
    for bits in (0, 2, 4, 6):
        x_pair(bits).start()

    def early():
        for bits in (0, 2, 4, 6):
            remote(
                xf_all.at[:, tokens_of(p ^ bits ^ 1)], xf_all.at[:, tokens_of(p ^ bits ^ 1)],
                ps.at[bits], pr.at[p ^ bits ^ 1], pair,
            ).wait_recv()
        pl.semaphore_wait(free.at[0], 1)

        @pl.when(p == 1)
        def _():
            own_a().wait()
            for q in range(CLASSES):
                if q != 1:
                    remote(xt_in.at[1], xa_all.at[:, tokens_of(q)], as_, ar.at[q], pair).wait_recv()

        @pl.when(p >= 1)
        def _():
            own_y().start()
            own_y().wait()
            gradients(parts_early)

    halve(1, (0, 2, 4, 6), wg.at[pl.ds(0, 2 * tokens), pl.ds(0, half)], c4r, 0)
    halve(at.b1, (0, at.b2), wg.at[pl.ds(2 * tokens, tokens), pl.ds(0, half)], c2r, 1, early)
    halve(at.b2, (0,), wg.at[pl.ds(3 * tokens, tokens), pl.ds(0, 2 * keys)], c1r, 2)

    gate[:, width:half] = dkv[p, :, :keys]
    for tile, value in enumerate(turn(gate[:, :half], -1)):
        dy_in[0, :, tile * 128 : (tile + 1) * 128] = value.astype(BF16)
    dv_in[...] = jnp.zeros(dv_in.shape, BF16)
    dv_in[:, :keys] = dkv[p, :, keys:].astype(BF16)
    for bits in range(1, CLASSES):
        give_y(bits, 0, 1)
    pl.when(p != 1)(lambda: v_move().start())
    pl.when(p == 1)(lambda: own_v().start())
    grad_normed = contract(dy_in[0], w01[0], 1, 1)
    grad_normed = grad_normed + contract(dv_in[:, :keys], w01[1, :, width:], 1, 1)
    through, gain_first = norm_back(residual, inverse_first, gains_ref[0:1, :], grad_normed)
    gain_s[0, 0:1, :] = gain_first
    swaps = [swap(0, pair)]
    swaps[0].start()
    grad_ref[...] = (grad_middle + through).T
    def relays(k, conditions):
        for part in range(2):
            pl.when(conditions[part]())(lambda part=part: relay(k, part))

    relays(0, parts_early)

    @pl.when(p == 0)
    def _():
        own_y().start()
        own_y().wait()
        gradients(parts_late)

    @pl.when(p == 1)
    def _():
        own_v().wait()
        value_gradient()

    relays(1, parts_early)
    relays(0, parts_late)
    relays(1, parts_late)
    swaps[0].wait()
    gain_s[1] = gain_s[0] + gain_r[0]
    swaps.append(swap(1, at.peer(2)))
    swaps[1].start()
    for bits in (0, 2, 4, 6):
        x_pair(bits).wait_send()
    for bits in range(1, CLASSES):
        y_move(bits).wait_send()
    for bits in (2, 4, 6):
        x_move(bits).wait_send()

    @pl.when(p != 1)
    def _():
        a_move().wait_send()
        v_move().wait_send()

    swaps[1].wait()
    gain_s[2] = gain_s[1] + gain_r[1]
    swaps.append(swap(2, at.peer(4)))
    swaps[2].start()

    moment("wait")

    @pl.when(p < 2)
    def _():
        ma[:, :width] = mq[...]
        ma[:, width:] = mk[...].T

    sall = wd.at[:, pl.ds(0, half)]
    ga, pa = (w01.at[1, pl.ds((parts - 1 - i) * rows, rows)] for i in range(2))

    def shard(index, part):
        return sall.at[pl.ds(pl.multiple_of(index * rows, 16), rows), part_lanes[part]]

    def rightward(index, part):
        here = shard(index, part)
        return remote(here, here, ls_r.at[part, index], lr_r.at[part, index], (at.c, lax.rem(f + 1, parts)))

    def leftward(index, part):
        here = shard(index, part)
        return remote(here, here, ls_l.at[part, index], lr_l.at[part, index], (at.c, lax.rem(f + parts - 1, parts)))

    can_right = f < parts - 1
    can_left = f > 0

    def settle_part(part):
        lanes = part_lanes[part]
        total = own[:, lanes]
        for k in range(2):
            slot = jnp.where(outer, k, 2 + k)
            arrival(slot, part).wait_recv()
            total = total + za_r[slot, :, lanes].astype(F32)
        ga[:, lanes] = total.astype(BF16)
        sall[my_rows, lanes] = (MOMENTUM * ma[:, lanes] + total).astype(BF16)
        pl.when(can_right)(lambda: rightward(f, part).start())
        pl.when(can_left)(lambda: leftward(f, part).start())

    def hop_part(hop, part):
        @pl.when(f - hop >= 0)
        def _():
            rightward(f - hop, part).wait_recv()
            pl.when(can_right)(lambda: rightward(f - hop, part).start())

        @pl.when(f + hop < parts)
        def _():
            leftward(f + hop, part).wait_recv()
            pl.when(can_left)(lambda: leftward(f + hop, part).start())

    spread_begin, spread_step, spread_finish = spread_even(at, ga, g_out, ag_l, ag_s, ag_r)
    for conditions, whole in ((parts_early, p >= 2), (parts_late, p < 2)):
        for part in range(2):
            pl.when(conditions[part]())(lambda part=part: settle_part(part))
        pl.when(whole)(spread_begin)
        for hop in range(1, parts):
            for part in range(2):
                pl.when(conditions[part]())(lambda hop=hop, part=part: hop_part(hop, part))

    swaps[2].wait()
    gain_s[3] = gain_s[2] + gain_r[2]
    line_gain = [
        remote(gain_s.at[3], gain_r.at[3 + j], gs.at[3 + j], gr.at[3 + j], at.along(j)) for j in range(1, parts)
    ]
    for copy in line_gain:
        copy.start()

    for part in range(2):
        for j in range(1, parts):
            line(f ^ j, part).wait_send()
        pl.when(can_right)(lambda: rightward(f, part).wait_send())
        pl.when(can_left)(lambda: leftward(f, part).wait_send())
        for hop in range(1, parts):
            pl.when((f - hop >= 0) & can_right)(lambda hop=hop: rightward(f - hop, part).wait_send())
            pl.when((f + hop < parts) & can_left)(lambda hop=hop: leftward(f + hop, part).wait_send())
    pl.semaphore_signal(free.at[1], inc=1, device_id=pair, device_id_type=MESH)
    pl.semaphore_wait(free.at[1], 1)

    x = w01.at[0]
    wide_gram = 1024
    gram_s, g = wg.at[:, pl.ds(0, wide_gram)], wg.at[:, pl.ds(wide_gram, wide_gram)]
    poly, xf = wd.at[:, pl.ds(0, wide_gram)], wd.at[:, pl.ds(half, columns)]
    step = width // 4

    def gram_r(slot):
        return wu.at[:, pl.ds(slot * wide_gram, wide_gram)]

    def scale_of(total):
        return 1.0 / (jnp.sqrt(total) + 1e-07)

    def normal(ref, inverse):
        ref[...] = rounded(ref[...].astype(F32) * inverse)

    def exchange(slot, r):
        part = pl.ds(r * step, step)
        return remote(gram_s.at[part], gram_r(slot).at[part], gsem.at[r], rsem.at[slot, r], pair)

    def poly_of(start, count):
        part = g[pl.ds(start, count), pl.ds(0, width)]
        square = jnp.dot(part, g[:, pl.ds(0, width)], preferred_element_type=F32)
        return rounded(NS_B * part.astype(F32) + NS_C * square)

    def fill_poly():
        for r in range(4):
            poly[pl.ds(r * step, step), pl.ds(0, width)] = poly_of(r * step, step)

    near = parts // 2
    mine_at = core * near
    last_core = lax.div(f, near)
    f_lanes = pl.ds(pl.multiple_of(lax.rem(f, near) * columns, 128), columns)

    kt = wd.at[pl.ds(0, keys), pl.ds(half + 256, wide_gram)]

    def xo(i):
        return w01.at[1, pl.ds(i * rows, rows)]

    def give():
        return [
            remote(
                sall.at[pl.ds(pl.multiple_of(((1 - core) * near + i) * rows, 16), rows)],
                xo(i), ex_s.at[i], ex_r.at[i], pair,
            )
            for i in range(near)
        ]

    def give_last():
        return remote(x.at[:, f_lanes], xf, fx_s, fx_r, pair)

    @pl.when(p >= 2)
    def _():
        @pl.when(p >= WIDE)
        def _():
            copies = give()
            for copy in copies:
                copy.start()
            for i in range(near):
                part = sall[pl.ds(pl.multiple_of((mine_at + i) * rows, 16), rows), :]
                for t in range(2):
                    x[pl.ds(pl.multiple_of(core * tall + t * rows, 16), rows), pl.ds(i * columns, columns)] = part[
                        :, t * columns : (t + 1) * columns
                    ]
            for i, copy in enumerate(copies):
                copy.wait()
                part = xo(i)
                for t in range(2):
                    x[pl.ds(pl.multiple_of((1 - core) * tall + t * rows, 16), rows), pl.ds(i * columns, columns)] = part[
                        :, pl.ds(t * columns, columns)
                    ]

        def squares(ref):
            wide = ref[...].astype(F32)
            sq[...] = jnp.broadcast_to(jnp.sum(wide * wide), sq.shape)

        pl.when(p < WIDE)(lambda: squares(sall))
        pl.when(p >= WIDE)(lambda: squares(x))
        copy = remote(sq, sq_r, qs, qr, pair)
        copy.start()
        copy.wait()
        inverse = scale_of(sq[...] + sq_r[...])[:1, :1]

        @pl.when(p < WIDE)
        def _():
            x[...] = rounded(sall[...].astype(F32) * inverse)

        pl.when(p >= WIDE)(lambda: normal(x, inverse))

        def grams(slot):
            for r in range(4):
                gram_s[pl.ds(r * step, step), pl.ds(0, width)] = rounded(
                    contract(x[pl.ds(r * step, step), :], x[...], 1, 1)
                )
                exchange(slot, r).start()
            for r in range(4):
                part = pl.ds(r * step, step)
                exchange(slot, r).wait()
                g[part, pl.ds(0, width)] = rounded(
                    gram_s[part, pl.ds(0, width)].astype(F32) + gram_r(slot)[part, pl.ds(0, width)].astype(F32)
                )

        def iterate(slot):
            grams(slot)
            fill_poly()
            for tile in range(half // 256):
                part = pl.ds(tile * 256, 256)
                x[:, part] = rounded(
                    NS_A * x[:, part].astype(F32) + jnp.dot(poly[:, pl.ds(0, width)], x[:, part], preferred_element_type=F32)
                )

        def iterate_twice(it, carry):
            iterate(0)
            pl.when(it == 1)(lambda: spread_step(1))
            iterate(1)
            pl.when(it == 0)(lambda: spread_step(0))
            pl.when(it == 1)(lambda: spread_step(2))
            return carry

        lax.fori_loop(0, (NS_ITERS - 1) // 2, iterate_twice, 0)

        @pl.when((p >= WIDE) & (core == last_core))
        def _():
            give_last().start()
            xf[...] = x[:, f_lanes]

        grams(0)

        @pl.when(p < WIDE)
        def _():
            part = poly_of(pl.multiple_of(f * rows, 16), rows)
            pa[...] = rounded(NS_A * x[my_rows, :].astype(F32) + jnp.dot(part, x[...], preferred_element_type=F32))

        @pl.when(p >= WIDE)
        def _():
            pl.when(core == last_core)(lambda: give_last().wait_send())
            pl.when(core != last_core)(lambda: give_last().wait_recv())
            for t in range(2):
                top = pl.multiple_of(core * tall + t * rows, 16)
                part = poly_of(top, rows)
                pa[:, t * columns : (t + 1) * columns] = rounded(
                    NS_A * xf[pl.ds(top, rows), :].astype(F32) + jnp.dot(part, xf[...], preferred_element_type=F32)
                )

    @pl.when(p < 2)
    def _():
        x[...] = sall[...]
        kt[:, pl.ds(0, width)] = x[:, pl.ds(width, keys)].T
        turned = kt[:, pl.ds(0, width)].astype(F32)
        kt[:, pl.ds(0, width)] = rounded(turned * scale_of(jnp.sum(turned * turned)))
        wide = x[:, pl.ds(0, width)].astype(F32)
        x[:, pl.ds(0, width)] = rounded(wide * scale_of(jnp.sum(wide * wide)))

        def narrow_step(it, carry):
            now = kt[:, pl.ds(0, width)]
            gram = rounded(contract(now, now, 1, 1))
            turned = rounded(NS_B * gram.astype(F32) + NS_C * jnp.dot(gram, gram, preferred_element_type=F32))
            kt[:, pl.ds(0, width)] = rounded(
                NS_A * now.astype(F32) + jnp.dot(turned, now, preferred_element_type=F32)
            )
            return carry

        lax.fori_loop(0, NS_ITERS, narrow_step, 0)

        def gram_of():
            for r in range(4):
                part = pl.ds(r * step, step)
                g[part, pl.ds(0, width)] = rounded(contract(x[part, pl.ds(0, width)], x[:, pl.ds(0, width)], 1, 1))

        def square_step(it, carry):
            gram_of()
            fill_poly()
            x[:, pl.ds(0, width)] = rounded(
                NS_A * x[:, pl.ds(0, width)].astype(F32) + jnp.dot(poly[:, pl.ds(0, width)], x[:, pl.ds(0, width)], preferred_element_type=F32)
            )
            for k in range(3):
                pl.when(it == k + 1)(lambda k=k: spread_step(k))
            return carry

        lax.fori_loop(0, NS_ITERS - 1, square_step, 0)
        gram_of()
        part = poly_of(pl.multiple_of(f * rows, 16), rows)
        square = rounded(
            NS_A * x[my_rows, pl.ds(0, width)].astype(F32) + jnp.dot(part, x[:, pl.ds(0, width)], preferred_element_type=F32)
        )
        x[:, pl.ds(width, keys)] = kt[:, pl.ds(0, width)].T
        pa[:, :width] = square
        pa[:, width:] = x[my_rows, pl.ds(width, keys)]

    out_begin, out_step, out_finish = spread_even(at, pa, o_out, og_l, og_s, og_r)
    out_begin()
    total = gain_s[3]
    for j in range(1, parts):
        line_gain[j - 1].wait()
        total = total + gain_r[3 + j]
    gain_out[...] = total
    spread_finish()
    for k in range(3):
        out_step(k)
    for copy in sent:
        copy.wait_send()
    out_finish()


def step_pass(x, up, gains, tables, bias, shards, moments):
    parts = lax.axis_size("fsdp")
    width, tokens = x.shape
    half = shards[4].shape[1] // 2
    rows = width // parts
    keys = half - width
    near = parts // 2
    dma = pltpu.SemaphoreType.DMA
    vm = pltpu.VMEM
    group = HEADS // KV_HEADS
    two = 2 * keys
    n_gain = 3 + parts
    return pl.pallas_call(
        step_kernel,
        out_shape=(
            jax.ShapeDtypeStruct((width, tokens), BF16),
            jax.ShapeDtypeStruct((width, tokens), F32),
            jax.ShapeDtypeStruct((CLASSES, rows, half), BF16),
            jax.ShapeDtypeStruct((CLASSES, rows, half), BF16),
            jax.ShapeDtypeStruct((8, width), F32),
        ),
        in_specs=[VMEM] * 11 + [ANY] * 10,
        out_specs=(VMEM, VMEM, ANY, ANY, VMEM),
        scratch_shapes=[
            vm((2, width, half), BF16),
            vm((width, 2 * half), BF16),
            vm((width, 2 * half), BF16),
            vm((width, 2 * half), BF16),
            vm((KV_HEADS, CLASSES * tokens, group * tokens), F32),
            vm((CLASSES, tokens, two), BF16),
            vm((tokens, half), BF16),
            vm((CLASSES, tokens, two), F32),
            vm((2 * tokens, 2 * two), BF16),
            vm((tokens, 2 * two), BF16),
            vm((tokens, two), BF16),
            vm((tokens, width), BF16),
            vm((tokens, 2 * half), F32),
            vm((2 * tokens, half), F32),
            vm((4, width, tokens), BF16),
            vm((CLASSES, tokens, half), BF16),
            vm((tokens, -(-keys // 128) * 128), BF16),
            vm((width, CLASSES * tokens), BF16),
            vm((width, CLASSES * tokens), BF16),
            vm((CLASSES * tokens, half), BF16),
            vm((CLASSES * tokens, -(-keys // 128) * 128), BF16),
            vm((4, rows, half), BF16),
            vm((rows, half), F32),
            vm((rows, width), F32),
            vm((keys, rows), F32),
            vm((4, 8, width), F32),
            vm((n_gain, 8, width), F32),
            vm((8, 128), F32),
            vm((8, 128), F32),
            dma((3,)), dma((4, parts)), dma((4, parts)), dma((4, 2, parts)), dma((4, 4, parts)),
            dma((4, CLASSES, parts)), dma((7,)), dma((CLASSES,)), dma((3,)), dma((3,)),
            dma((4,)), dma((CLASSES,)), dma((CLASSES,)), dma((CLASSES,)), dma((CLASSES,)),
            dma((CLASSES,)), dma((CLASSES,)), dma, dma((CLASSES,)), dma, dma((CLASSES,)),
            dma((2,)), dma((2,)), dma((2, parts)), dma((2, parts)),
            dma((2,)), dma((n_gain,)), dma((n_gain,)),
            dma, dma((7,)), dma((CLASSES,)),
            dma((2, parts)), dma((2, parts)), dma((2, parts)), dma((2, parts)),
            dma((4,)), dma((2, 4)), dma, dma,
            dma((near,)), dma((near,)), dma, dma,
            dma, dma((7,)), dma((CLASSES,)), pltpu.SemaphoreType.REGULAR((2,)),
        ],
        compiler_params=pltpu.CompilerParams(
            collective_id=3, has_side_effects=True, vmem_limit_bytes=63 << 20
        ),
        name="step_pass",
    )(x, up, gains, *tables, bias, *shards, *moments)


def settle_wide(factors, *refs):
    gs, os = refs[0], refs[1]
    ms, ws, outs = refs[2:6], refs[6:10], refs[10:]
    width = ms[0].shape[1]
    half = gs.shape[2]

    def one(index, g, o, lanes):
        grad, moment, weight = (outs[3 * index + i] for i in range(3))
        value = g.astype(F32)
        grad[:, lanes] = value
        moment[:, lanes] = MOMENTUM * ms[index][:, lanes] + value
        weight[:, lanes] = ws[index][:, lanes].astype(F32) + factors[index] * o.astype(F32)

    for index in range(2):
        one(index, gs[index, :, :width], os[index, :, :width], slice(0, width))
    for index in range(2):
        for side in range(2):
            cls = 2 + 2 * index + side
            one(2 + index, gs[cls], os[cls], slice(side * half, (side + 1) * half))


def settle_turned(factors, g_tall, o_tall, g_pair, o_pair, *refs):
    ms, ws, outs = refs[0:3], refs[3:6], refs[6:]
    keys = ms[1].shape[0]

    def one(index, g, o):
        grad, moment, weight = (outs[3 * index + i] for i in range(3))
        grad[...] = g
        moment[...] = MOMENTUM * ms[index][...] + g
        weight[...] = ws[index][...].astype(F32) + factors[index] * o

    one(0, g_tall[0].astype(F32), o_tall[0].astype(F32))

    @pl.when(pl.program_id(0) == 0)
    def _():
        for index in range(2):
            start = g_pair.shape[2] - keys
            one(1 + index, g_pair[index, :, start:].astype(F32).T, o_pair[index, :, start:].astype(F32).T)


def settle(g, o, moments, shards, factors):
    m_q, m_k, m_o, m_v, m_gate, m_up, m_down = moments
    w_q, w_k, w_o, w_v, w_gate, w_up, w_down = shards
    f_q, f_k, f_v, f_o, f_gate, f_up, f_down = factors
    _, rows, half = g.shape
    width, columns = m_down.shape
    block = 48 if rows % 48 == 0 else rows
    piece = pl.BlockSpec((WIDE, block, half), lambda i: (0, i, 0))

    def row_block(array):
        return pl.BlockSpec((block, array.shape[1]), lambda i: (i, 0))

    def result(arrays):
        return tuple(jax.ShapeDtypeStruct(array.shape, F32) for array in arrays for _ in range(3))

    wide = (m_q, m_o, m_gate, m_up)
    first = pl.pallas_call(
        functools.partial(settle_wide, (f_q, f_o, f_gate, f_up)),
        grid=(rows // block,),
        out_shape=result(wide),
        in_specs=[piece, piece] + [row_block(array) for array in wide] * 2,
        out_specs=tuple(row_block(array) for array in wide for _ in range(3)),
        compiler_params=pltpu.CompilerParams(vmem_limit_bytes=60 << 20),
        name="settle_wide",
    )(g, o, *wide, w_q, w_o, w_gate, w_up)

    turned = (m_down, m_k, m_v)
    halves = half // columns
    tile = pl.BlockSpec((1, rows, columns), lambda i: (WIDE + i // halves, 0, i % halves))
    both = pl.BlockSpec((2, rows, half), lambda i: (0, 0, 0))
    specs = [pl.BlockSpec((rows, columns), lambda i: (i, 0))] + [
        pl.BlockSpec(array.shape, lambda i: (0, 0)) for array in turned[1:]
    ]
    second = pl.pallas_call(
        functools.partial(settle_turned, (f_down, f_k, f_v)),
        grid=(width // rows,),
        out_shape=result(turned),
        in_specs=[tile, tile, both, both] + specs * 2,
        out_specs=tuple(spec for spec in specs for _ in range(3)),
        compiler_params=pltpu.CompilerParams(vmem_limit_bytes=60 << 20),
        name="settle_turned",
    )(g, o, g, o, *turned, w_down, w_k, w_v)
    q, out, gate, up = (first[3 * i : 3 * i + 3] for i in range(4))
    down, k, v = (tuple(item.T for item in second[3 * i : 3 * i + 3]) for i in range(3))
    return list(zip(q, k, v, out, gate, up, down))


def rotary_tables(positions, width):
    half = width // 2
    frequency = THETA ** (-(jnp.arange(half, dtype=jnp.float32) * 2.0 / width))
    angle = positions.astype(jnp.float32)[:, None] * frequency[None, :]
    return (jnp.cos(angle)[:, None, :], jnp.sin(angle)[:, None, :])


def rotate(value, cosine, sine):
    half = value.shape[-1] // 2
    first = value[..., :half]
    second = value[..., half:]
    return jnp.concatenate(
        [first * cosine - second * sine, second * cosine + first * sine], axis=-1
    )


def unrotate(incoming, cosine, sine):
    half = incoming.shape[-1] // 2
    upper = incoming[..., :half]
    lower = incoming[..., half:]
    return jnp.concatenate([upper * cosine + lower * sine, lower * cosine - upper * sine], axis=-1)


def norm_forward(residual, gain):
    inverse = lax.rsqrt(jnp.mean(residual * residual, axis=-1, keepdims=True) + EPS)
    return ((residual * inverse * gain).astype(jnp.bfloat16), inverse)


def norm_backward(residual, inverse, gain, incoming):
    scaled = incoming * gain
    through = inverse * scaled - residual * inverse**3 * jnp.mean(
        scaled * residual, axis=-1, keepdims=True
    )
    return (through, jnp.sum(incoming * residual * inverse, axis=0))


def padded(array, axis, parts, count, full):
    if count == full:
        return array
    shape = array.shape
    split = array.reshape(shape[:axis] + (parts, count) + shape[axis + 1 :])
    pads = [(0, 0)] * split.ndim
    pads[axis + 1] = (0, full - count)
    return jnp.pad(split, pads).reshape(shape[:axis] + (parts * full,) + shape[axis + 1 :])


def trimmed(array, axis, parts, count, full):
    if count == full:
        return array
    shape = array.shape
    split = array.reshape(shape[:axis] + (parts, full) + shape[axis + 1 :])
    kept = lax.slice_in_dim(split, 0, count, axis=axis + 1)
    return kept.reshape(shape[:axis] + (parts * count,) + shape[axis + 1 :])


def plain_layer(
    layer_input, output_grad, wide, tall, norm_gains, block_order, sizes
):
    parts, width, half, kv, short, full, high = sizes
    hidden_size = 2 * half
    rows = layer_input.shape[1]
    block = rows // 2
    group = HEADS // KV_HEADS
    scale = 1.0 / math.sqrt(HEAD)
    ctx_place = lax.axis_index("ctx")
    offsets = jnp.arange(block, dtype=jnp.int32)
    own_blocks = lax.dynamic_slice_in_dim(block_order, 2 * ctx_place, 2)
    query_pos = (own_blocks[:, None] * block + offsets[None, :]).reshape(rows)
    key_pos = (block_order[:, None] * block + offsets[None, :]).reshape(-1)

    all_wide, all_tall = gather_weights(wide, tall)
    w_qk, w_ov, w_gate_0, w_gate_1, w_up_0, w_up_1 = [all_wide[i].reshape(width, half) for i in range(WIDE)]
    w_down = [all_tall[i].reshape(half, width) for i in range(2)]

    residual = layer_input[0].astype(jnp.float32)
    normed_first, inverse_first = norm_forward(residual, norm_gains[0])
    qk_pre = jnp.dot(normed_first, w_qk, preferred_element_type=jnp.float32)
    query_pre = qk_pre[:, :width].reshape(rows, HEADS, HEAD)
    key_pre = qk_pre[:, width:].reshape(rows, KV_HEADS, HEAD)
    value_low = (
        jnp.dot(normed_first, w_ov, preferred_element_type=jnp.float32)[:, width:]
        .astype(jnp.bfloat16)
        .reshape(rows, KV_HEADS, HEAD)
    )
    cosine, sine = rotary_tables(query_pos, HEAD)
    query_rot = rotate(query_pre, cosine, sine).astype(jnp.bfloat16)
    key_rot = rotate(key_pre, cosine, sine).astype(jnp.bfloat16)
    keys_all, values_all = (
        lax.all_gather(key_rot, "ctx", axis=0, tiled=True),
        lax.all_gather(value_low, "ctx", axis=0, tiled=True),
    )
    keys_head = keys_all.transpose(1, 0, 2)
    values_head = values_all.transpose(1, 0, 2)
    queries_head = (
        query_rot.reshape(rows, KV_HEADS, group, HEAD)
        .transpose(1, 2, 0, 3)
        .reshape(KV_HEADS, group * rows, HEAD)
    )
    row_pos = jnp.tile(query_pos, group)
    allowed = key_pos[None, :] <= row_pos[:, None]

    def head_forward(item):
        query, key, value = item
        scores = jnp.where(allowed, contract(query, key, 1, 1) * scale, MASKED)
        top = jnp.max(scores, axis=-1, keepdims=True)
        expo = jnp.exp(scores - top)
        total = jnp.sum(expo, axis=-1, keepdims=True)
        probs_low = (expo / total).astype(jnp.bfloat16)
        return (
            jnp.dot(probs_low, value, preferred_element_type=jnp.float32),
            (top + jnp.log(total))[:, 0],
        )

    mixed, log_total = lax.map(head_forward, (queries_head, keys_head, values_head))
    attended = (
        mixed.reshape(KV_HEADS, group, rows, HEAD)
        .transpose(2, 0, 1, 3)
        .reshape(rows, HEADS * HEAD)
        .astype(jnp.bfloat16)
    )
    w_out = w_ov[:, :width]
    middle = residual + jnp.dot(attended, w_out, preferred_element_type=jnp.float32)
    normed_second, inverse_second = norm_forward(middle, norm_gains[1])

    def sides(left, right):
        return jnp.concatenate([left, right], axis=1)

    gate = sides(
        jnp.dot(normed_second, w_gate_0, preferred_element_type=jnp.float32),
        jnp.dot(normed_second, w_gate_1, preferred_element_type=jnp.float32),
    )
    lifted = sides(
        jnp.dot(normed_second, w_up_0, preferred_element_type=jnp.float32),
        jnp.dot(normed_second, w_up_1, preferred_element_type=jnp.float32),
    )
    sigma = jax.nn.sigmoid(gate)
    hidden = (gate * sigma * lifted).astype(jnp.bfloat16)
    hidden_split = hidden.reshape(rows, parts, 2, high)
    hidden_sides = [hidden_split[:, :, i].reshape(rows, half) for i in range(2)]
    layer_output = (
        middle
        + jnp.dot(hidden_sides[0], w_down[0], preferred_element_type=jnp.float32)
        + jnp.dot(hidden_sides[1], w_down[1], preferred_element_type=jnp.float32)
    ).astype(jnp.bfloat16)
    upstream = output_grad[0]
    grad_hidden = jnp.stack(
        [contract(upstream, w_down[i], 1, 1).reshape(rows, parts, high) for i in range(2)], axis=2
    ).reshape(rows, hidden_size)
    grad_gate = (grad_hidden * lifted * sigma * (1.0 + gate * (1.0 - sigma))).astype(jnp.bfloat16)
    grad_lifted = (grad_hidden * gate * sigma).astype(jnp.bfloat16)
    grad_normed_second = (
        contract(grad_gate[:, :half], w_gate_0, 1, 1)
        + contract(grad_gate[:, half:], w_gate_1, 1, 1)
        + contract(grad_lifted[:, :half], w_up_0, 1, 1)
        + contract(grad_lifted[:, half:], w_up_1, 1, 1)
    )
    through_second, gain_second = norm_backward(
        middle, inverse_second, norm_gains[1], grad_normed_second
    )
    grad_middle = upstream.astype(jnp.float32) + through_second
    grad_branch = grad_middle.astype(jnp.bfloat16)
    grad_attended = contract(grad_branch, w_out, 1, 1).astype(jnp.bfloat16)
    grad_heads = (
        grad_attended.reshape(rows, KV_HEADS, group, HEAD)
        .transpose(1, 2, 0, 3)
        .reshape(KV_HEADS, group * rows, HEAD)
    )

    def head_backward(item):
        query, key, value, grad_out, log_row = item
        scores = jnp.where(allowed, contract(query, key, 1, 1) * scale, MASKED)
        probs = jnp.exp(scores - log_row[:, None])
        grad_value_part = contract(probs.astype(jnp.bfloat16), grad_out, 0, 0)
        grad_probs = contract(grad_out, value, 1, 1)
        grad_scores = (
            probs * (grad_probs - jnp.sum(grad_probs * probs, axis=-1, keepdims=True))
        ).astype(jnp.bfloat16)
        grad_query_part = jnp.dot(grad_scores, key, preferred_element_type=jnp.float32) * scale
        grad_key_part = contract(grad_scores, query, 0, 0) * scale
        return (grad_query_part, grad_key_part, grad_value_part)

    grad_query_rot, grad_key_all, grad_value_all = lax.map(
        head_backward, (queries_head, keys_head, values_head, grad_heads, log_total)
    )
    grad_key_own, grad_value_own = (
        lax.psum_scatter(
            grad_key_all.astype(jnp.bfloat16), "ctx", scatter_dimension=1, tiled=True
        ).astype(jnp.float32),
        lax.psum_scatter(
            grad_value_all.astype(jnp.bfloat16), "ctx", scatter_dimension=1, tiled=True
        ).astype(jnp.float32),
    )
    grad_query = (
        unrotate(
            grad_query_rot.reshape(KV_HEADS, group, rows, HEAD)
            .transpose(2, 0, 1, 3)
            .reshape(rows, HEADS, HEAD),
            cosine,
            sine,
        )
        .reshape(rows, HEADS * HEAD)
        .astype(jnp.bfloat16)
    )
    grad_key = (
        unrotate(grad_key_own.transpose(1, 0, 2), cosine, sine)
        .reshape(rows, KV_HEADS * HEAD)
        .astype(jnp.bfloat16)
    )
    grad_value = (
        grad_value_own.transpose(1, 0, 2).reshape(rows, KV_HEADS * HEAD).astype(jnp.bfloat16)
    )
    grad_qk = sides(grad_query, grad_key)
    zero_query = jnp.zeros((rows, width), jnp.bfloat16)
    grad_v = sides(zero_query, grad_value)
    grad_normed_first = contract(grad_qk, w_qk, 1, 1) + contract(grad_v, w_ov, 1, 1)
    through_first, gain_first = norm_backward(
        residual, inverse_first, norm_gains[0], grad_normed_first
    )
    input_gradient = grad_middle + through_first

    xt = jnp.stack([item.T for item in (normed_first, attended, normed_second, upstream)])
    xt = padded(xt, 1, parts, short, full)
    dy = jnp.stack(
        [
            grad_qk,
            sides(grad_branch, jnp.zeros((rows, kv), jnp.bfloat16)),
            grad_gate[:, :half],
            grad_gate[:, half:],
            grad_lifted[:, :half],
            grad_lifted[:, half:],
            hidden_sides[0],
            hidden_sides[1],
            grad_v,
        ]
    )
    gains = jnp.pad(jnp.stack([gain_first, gain_second]), ((0, 6), (0, 0)))
    return layer_output, input_gradient, xt, dy, gains


def rotation(block_order, rows):
    block = rows // 2
    ctx_place = lax.axis_index("ctx")
    offsets = jnp.arange(block, dtype=jnp.int32)
    own_blocks = lax.dynamic_slice_in_dim(block_order, 2 * ctx_place, 2)
    query_pos = (own_blocks[:, None] * block + offsets[None, :]).reshape(rows)
    key_pos = (block_order[:, None] * block + offsets[None, :]).reshape(-1)
    bias = jnp.where(key_pos[:, None] <= query_pos[None, :], 0.0, MASKED).astype(jnp.bfloat16)
    lane = jnp.arange(128, dtype=jnp.int32)
    index = (lane % (HEAD // 2)).astype(jnp.float32)
    frequency = THETA ** (-(index * 2.0 / HEAD))
    angle = query_pos.astype(jnp.float32)[:, None] * frequency[None, :]
    cosine, sine = jnp.cos(angle), jnp.sin(angle)
    early = (lane % HEAD < HEAD // 2)[None, :]
    return (cosine, jnp.where(early, 0.0, sine), jnp.where(early, -sine, 0.0)), bias


def plain_step(layer_input, output_grad, norm_gains, block_order, weights, olds, factors, sizes):
    parts, width, half, kv, short, full, high = sizes
    query_weight, key_weight, value_weight, output_weight, gate_weight, up_weight, down_weight = weights
    (
        query_momentum,
        key_momentum,
        value_momentum,
        output_momentum,
        gate_momentum,
        up_momentum,
        down_momentum,
    ) = olds

    def sides(left, right):
        return jnp.concatenate([left, right], axis=1)

    wide = jnp.stack(
        [
            jnp.concatenate([query_weight, key_weight], axis=1),
            jnp.concatenate([output_weight, value_weight], axis=1),
            gate_weight[:, :half],
            gate_weight[:, half:],
            up_weight[:, :half],
            up_weight[:, half:],
        ]
    )
    tall = down_weight.reshape(2, high, width)
    layer_output, input_gradient, xt, dy, gains = plain_layer(
        layer_input, output_grad, wide, tall, norm_gains, block_order, sizes
    )

    def pad_rows(array):
        return padded(array, 0, 1, short, full)

    def pad_columns(array):
        return padded(array, 1, parts, short, full)

    moments = (
        pad_rows(sides(query_momentum, key_momentum)),
        pad_rows(sides(output_momentum, value_momentum)),
        pad_rows(gate_momentum),
        pad_rows(up_momentum),
        pad_columns(down_momentum),
    )
    g_wide, g_tall, s_wide, s_tall, gain_sum = reduce_gradients(xt, dy, gains, moments, full, high)
    o_wide, o_tall = orthogonalize(s_wide, s_tall, full, high, width)

    def unpack(wide_pieces, tall_pieces):
        pieces = wide_pieces[:, :short]
        tall = trimmed(tall_pieces, 2, parts, short, full).reshape(2 * high, width)
        return (
            pieces[0, :, :width],
            pieces[0, :, width:],
            pieces[1, :, width:],
            pieces[1, :, :width],
            sides(pieces[2], pieces[3]),
            sides(pieces[4], pieces[5]),
            tall,
        )

    gradients = [item.astype(jnp.float32) for item in unpack(g_wide, g_tall)]
    orthos = unpack(o_wide, o_tall)
    moments = [MOMENTUM * old + new for old, new in zip(olds, gradients)]
    new_weights = [
        weight.astype(jnp.float32) + factor * ortho.astype(jnp.float32)
        for weight, factor, ortho in zip(weights, factors, orthos)
    ]
    return layer_output, input_gradient, gradients, moments, new_weights, gain_sum


def on_device(
    layer_input,
    output_grad,
    query_weight,
    key_weight,
    value_weight,
    output_weight,
    gate_weight,
    up_weight,
    down_weight,
    norm_gains,
    query_momentum,
    key_momentum,
    value_momentum,
    output_momentum,
    gate_momentum,
    up_momentum,
    down_momentum,
    gain_momentum,
    block_order,
):
    parts = lax.axis_size("fsdp")
    width = layer_input.shape[2]
    half = gate_weight.shape[1] // 2
    kv = key_weight.shape[1]
    short = width // parts
    full = -(-short // 16) * 16
    high = half // parts
    sizes = (parts, width, half, kv, short, full, high)

    weights = (query_weight, key_weight, value_weight, output_weight, gate_weight, up_weight, down_weight)
    olds = (
        query_momentum,
        key_momentum,
        value_momentum,
        output_momentum,
        gate_momentum,
        up_momentum,
        down_momentum,
    )
    factors = []
    for index, weight in enumerate(weights):
        step_rate = OUT_RATE if index == 3 else RATE
        factors.append(-step_rate * max(1.0, weight.shape[1] / (weight.shape[0] * parts)) ** 0.5)

    fused = (
        lax.axis_size("ctx") == CLASSES
        and short == full
        and parts == 4
        and half % (2 * half // parts) == 0
        and (2 * half // parts) % 128 == 0
        and layer_input.shape[1] == 128
        and short <= 256
    )
    if fused:
        tables, bias = rotation(block_order, layer_input.shape[1])

        def turned(items):
            q, k, v, o, gate, up, down = items
            return (q, k.T, o, v.T, gate, up, down.T)

        shards, moments = turned(weights), turned(olds)
        out_turned, grad_turned, g, o, gain_sum = step_pass(
            layer_input[0].T, output_grad[0].T, norm_gains, tables, bias, shards, moments
        )
        gradients, moments, new_weights = settle(g, o, moments, shards, factors)
        layer_output, input_gradient = out_turned.T, grad_turned.T
    else:
        layer_output, input_gradient, gradients, moments, new_weights, gain_sum = plain_step(
            layer_input, output_grad, norm_gains, block_order, weights, olds, factors, sizes
        )
    gain_width = norm_gains.shape[1] // parts
    place = lax.axis_index("fsdp") * gain_width
    gain_gradient = lax.dynamic_slice_in_dim(gain_sum[:2], place, gain_width, 1)
    gain_shard = lax.dynamic_slice_in_dim(norm_gains, place, gain_width, 1)
    gain_moment = MOMENTUM * gain_momentum + gain_gradient
    new_gains = gain_shard - GAIN_RATE * gain_moment
    return (
        layer_output[None],
        input_gradient[None],
        *gradients,
        gain_gradient,
        *moments,
        gain_moment,
        *new_weights,
        new_gains,
    )


def solution(mesh):
    tokens = P("fsdp", "ctx", None)
    shard = P("fsdp", None)
    gains = P(None, "fsdp")
    return jax.shard_map(
        on_device,
        mesh=mesh,
        in_specs=(tokens, tokens) + (shard,) * 7 + (P(),) + (shard,) * 7 + (gains, P()),
        out_specs=(tokens, tokens) + ((shard,) * 7 + (gains,)) * 3,
        check_vma=False,
    )
```

```python
import functools
import math

import jax
import jax.numpy as jnp
from jax import lax
from jax.experimental import pallas as pl
from jax.experimental.pallas import tpu as pltpu
from jax.sharding import PartitionSpec as P

HEADS = 15
KV_HEADS = 5
HEAD = 64
NS_ITERS = 5


EPS = 1e-05
THETA = 100000.0
NS_A = 3.4445
NS_B = -4.775
NS_C = 2.0315
MOMENTUM = 0.95
RATE = 0.2
OUT_RATE = 6.0
GAIN_RATE = 0.002
MASKED = -1e30

MESH = pl.DeviceIdType.MESH
BF16 = jnp.bfloat16
F32 = jnp.float32
ANY = pl.BlockSpec(memory_space=pl.ANY)
VMEM = pl.BlockSpec(memory_space=pltpu.VMEM)
CLASSES = 8
WIDE = 6


def contract(left, right, left_dim, right_dim):
    return lax.dot_general(
        left, right, (((left_dim,), (right_dim,)), ((), ())), preferred_element_type=jnp.float32
    )


class Place:
    def __init__(self):
        self.parts = lax.axis_size("fsdp")
        self.extra = lax.axis_size("ctx") // CLASSES
        self.c = lax.axis_index("ctx")
        self.f = lax.axis_index("fsdp")
        self.p = lax.rem(self.c, CLASSES)
        self.core = lax.rem(self.c, 2)
        self.b1 = jnp.where(self.core == 0, 2, 4)
        self.b2 = jnp.where(self.core == 0, 4, 2)

    def peer(self, bits):
        return (self.c ^ bits, self.f)

    def along(self, j):
        return (self.c, self.f ^ j)

    def other(self, j):
        groups = self.extra
        return (lax.rem(self.c + CLASSES * j, CLASSES * groups), self.f)

    def barrier(self, bits=(1, 2, 4), line=True, others=False):
        sem = pltpu.get_barrier_semaphore()
        targets = [self.peer(b) for b in bits]
        if line:
            targets += [self.along(j) for j in range(1, self.parts)]
        if others:
            targets += [self.other(j) for j in range(1, self.extra)]
        for target in targets:
            pl.semaphore_signal(sem, inc=1, device_id=target, device_id_type=MESH)
        pl.semaphore_wait(sem, len(targets))


def remote(src, dst, send, recv, target):
    return pltpu.make_async_remote_copy(
        src_ref=src, dst_ref=dst, send_sem=send, recv_sem=recv, device_id=target, device_id_type=MESH
    )


def by_kind(cls, wide, tall):
    pl.when(cls < WIDE)(wide)
    pl.when(cls >= WIDE)(tall)


def weights_kernel(in_a, in_b, out_a, out_b, local, zs, s1, s2, sc, recv):
    at = Place()
    p, f, parts = at.p, at.f, at.parts
    at.barrier()
    copies = [
        pltpu.make_async_copy(in_a, out_a.at[:, f], local.at[0]),
        pltpu.make_async_copy(in_b, out_b.at[:, f], local.at[1]),
    ]
    for copy in copies:
        copy.start()

    def act(cls, j, g, send, target, what, first=False):
        def wide():
            dst = out_a.at[cls, g]
            src = in_a.at[cls] if first else dst
            getattr(remote(src, dst, send, recv.at[cls, j], target), what)()

        def tall():
            dst = out_b.at[cls - WIDE, g]
            src = in_b.at[cls - WIDE] if first else dst
            getattr(remote(src, dst, send, recv.at[cls, j], target), what)()

        by_kind(cls, wide, tall)

    sends = []

    def send(cls, j, g, sem, target, first=False):
        act(cls, j, g, sem, target, "start", first)
        sends.append((cls, j, g, sem, target, first))

    def arrived(cls, j):
        act(cls, j, f ^ j, zs.at[j], at.along(j), "wait_recv")

    for j in range(1, parts):
        send(p, j, f, zs.at[j], at.along(j), True)
    for j in range(1, parts):
        arrived(p, j)
        send(p, j, f ^ j, s1.at[0, j], at.peer(at.b1))
        send(p, j, f ^ j, s2.at[0, j], at.peer(at.b2))
        send(p, j, f ^ j, sc.at[0, j], at.peer(1))
    for j in range(1, parts):
        arrived(p ^ at.b1, j)
        send(p ^ at.b1, j, f ^ j, s2.at[1, j], at.peer(at.b2))
        send(p ^ at.b1, j, f ^ j, sc.at[1, j], at.peer(1))
    for slot, bits in ((2, at.b2), (3, at.b1 ^ at.b2)):
        for j in range(1, parts):
            arrived(p ^ bits, j)
            send(p ^ bits, j, f ^ j, sc.at[slot, j], at.peer(1))
    for bits in (1, 3, 5, 7):
        for j in range(1, parts):
            arrived(p ^ bits, j)
    for cls, j, g, sem, target, first in sends:
        act(cls, j, g, sem, target, "wait_send", first)
    for copy in copies:
        copy.wait()


def gather_weights(wide, tall):
    parts = lax.axis_size("fsdp")
    dma = pltpu.SemaphoreType.DMA
    return pl.pallas_call(
        weights_kernel,
        out_shape=(
            jax.ShapeDtypeStruct((WIDE, parts) + wide.shape[1:], BF16),
            jax.ShapeDtypeStruct((CLASSES - WIDE, parts) + tall.shape[1:], BF16),
        ),
        in_specs=[ANY, ANY],
        out_specs=(ANY, ANY),
        scratch_shapes=[
            dma((2,)),
            dma((parts,)),
            dma((1, parts)),
            dma((2, parts)),
            dma((4, parts)),
            dma((CLASSES, parts)),
        ],
        compiler_params=pltpu.CompilerParams(collective_id=0, has_side_effects=True),
        name="gather_weights",
    )(wide, tall)


def spread(at, own_a, own_b, out_a, out_b, local, ss, recv):
    p = at.p

    def act(cls, sem, target, what, first=False):
        def wide():
            dst = out_a.at[cls]
            getattr(remote(own_a if first else dst, dst, sem, recv.at[cls], target), what)()

        def tall():
            dst = out_b.at[cls - WIDE]
            getattr(remote(own_b if first else dst, dst, sem, recv.at[cls], target), what)()

        by_kind(cls, wide, tall)

    def keep(what):
        def wide():
            getattr(pltpu.make_async_copy(own_a, out_a.at[p], local), what)()

        def tall():
            getattr(pltpu.make_async_copy(own_b, out_b.at[p - WIDE], local), what)()

        by_kind(p, wide, tall)

    sends = []

    def send(cls, slot, target, first=False):
        act(cls, ss.at[slot], target, "start", first)
        sends.append((cls, slot, target, first))

    def arrived(cls):
        act(cls, ss.at[0], at.peer(1), "wait_recv")

    send(p, 0, at.peer(at.b1), True)
    send(p, 1, at.peer(at.b2), True)
    send(p, 2, at.peer(1), True)
    keep("start")

    def finish():
        arrived(p ^ at.b1)
        send(p ^ at.b1, 3, at.peer(at.b2))
        send(p ^ at.b1, 4, at.peer(1))
        arrived(p ^ at.b2)
        send(p ^ at.b2, 5, at.peer(1))
        arrived(p ^ at.b1 ^ at.b2)
        send(p ^ at.b1 ^ at.b2, 6, at.peer(1))
        for bits in (1, 3, 5, 7):
            arrived(p ^ bits)
        for cls, slot, target, first in sends:
            act(cls, ss.at[slot], target, "wait_send", first)
        keep("wait")

    return finish


def reduce_kernel(
    parts, extra, high,
    xt_in, dy_in, gain_in, m_qk, m_ov, m_gate, m_up, m_down,
    g_a, g_b, s_a, s_b, gain_out,
    xt, dy, p1s, p1r, p2s, p2r, own, own_t, za_s, za_r, zb_s, zb_r, ma, mb, ga, gb, sa, sb, es, er, gain_s, gain_r,
    ls, xs, xr, s1, r1, s2, r2, zs, zr, esem, ersem, msem, gs, gr, ag_l, ag_s, ag_r, ss, sr, sl,
):
    at = Place()
    p, f, core = at.p, at.f, at.core
    tokens = xt_in.shape[2]
    rows = ma.shape[0]
    half = dy.shape[2]

    def moment(what):
        for cls in range(CLASSES):
            @pl.when(p == cls)
            def _(cls=cls):
                side = cls % 2
                if cls < 2:
                    src, dst = (m_qk, m_ov)[cls], ma
                elif cls < WIDE:
                    whole = m_gate if cls < 4 else m_up
                    src, dst = whole.at[:, pl.ds(side * half, half)], ma
                else:
                    src, dst = m_down.at[pl.ds(side * high, high)], mb
                getattr(pltpu.make_async_copy(src, dst, msem), what)()

    moment("start")
    mine = [pltpu.make_async_copy(xt_in, xt.at[:, :, pl.ds(0, tokens)], ls.at[0])]
    for slot in range(4):
        mine.append(
            pltpu.make_async_copy(dy_in.at[core + 2 * slot], dy.at[slot, pl.ds(0, tokens)], ls.at[1 + slot])
        )
    mine.append(pltpu.make_async_copy(dy_in.at[8], dy.at[4, pl.ds(0, tokens)], ls.at[5]))
    for copy in mine:
        copy.start()
    at.barrier(others=True)
    pair = at.peer(1)
    theirs = [remote(xt_in, xt.at[:, :, pl.ds(tokens, tokens)], xs.at[0], xr.at[0], pair)]
    for slot in range(4):
        theirs.append(
            remote(dy_in.at[1 - core + 2 * slot], dy.at[slot, pl.ds(tokens, tokens)], xs.at[1 + slot], xr.at[1 + slot], pair)
        )
    theirs.append(remote(dy_in.at[8], dy.at[4, pl.ds(tokens, tokens)], xs.at[5], xr.at[5], pair))
    for copy in theirs:
        copy.start()

    def swap(slot, target):
        return remote(gain_s.at[slot], gain_r.at[slot], gs.at[slot], gr.at[slot], target)

    gain_s[0] = gain_in[...]
    swaps = [swap(0, pair)]
    swaps[0].start()
    for copy in mine:
        copy.wait()
    for copy in theirs:
        copy.wait()

    def term(cls, r):
        at_rows = pl.ds(pl.multiple_of(r * rows, rows), rows)
        slot = lax.div(cls, 2)
        kind = jnp.where(cls == 0, 0, jnp.where(cls == 1, 1, jnp.where(cls < WIDE, 2, 3)))
        value = jnp.dot(xt[kind, at_rows, :], dy[slot], preferred_element_type=F32)
        return value

    def with_values(cls, r, put):
        at_rows = pl.ds(pl.multiple_of(r * rows, rows), rows)

        @pl.when(cls == 1)
        def _():
            put(term(cls, r) + jnp.dot(xt[0, at_rows, :], dy[4], preferred_element_type=F32))

        @pl.when(cls != 1)
        def _():
            put(term(cls, r))

    def order(i):
        return lax.rem(f + 1 + i, parts)

    def one(slot, i):
        r = order(i)
        return remote(p1s.at[slot, r], p1r.at[slot, r], s1.at[slot, r], r1.at[slot, r], at.peer(at.b1))

    for slot, bits in ((0, at.b1 ^ at.b2), (1, at.b1)):
        def first(i, carry, slot=slot, bits=bits):
            r = order(i)

            def put(value):
                p1s[slot, r] = value.astype(BF16)

            with_values(p ^ bits, r, put)
            one(slot, i).start()
            return carry

        lax.fori_loop(0, parts, first, 0)

    swaps[0].wait()
    gain_s[1] = gain_s[0] + gain_r[0]
    swaps.append(swap(1, at.peer(2)))
    swaps[1].start()

    def two(i):
        r = order(i)
        return remote(p2s.at[r], p2r.at[r], s2.at[r], r2.at[r], at.peer(at.b2))

    def second(i, carry):
        r = order(i)
        one(0, i).wait_recv()

        def put(value):
            p2s[r] = (value + p1r[0, r].astype(F32)).astype(BF16)

        with_values(p ^ at.b2, r, put)
        two(i).start()
        return carry

    lax.fori_loop(0, parts, second, 0)
    swaps[1].wait()
    gain_s[2] = gain_s[1] + gain_r[1]
    swaps.append(swap(2, at.peer(4)))
    swaps[2].start()

    def line_a(r, source):
        return remote(za_s.at[r], za_r.at[source], zs.at[r], zr.at[source], (at.c, r))

    def line_b(r, source):
        return remote(
            zb_s.at[pl.ds(pl.multiple_of(r * high, high), high)],
            zb_r.at[source], zs.at[r], zr.at[source], (at.c, r),
        )

    early = extra == 1

    def third(i, carry):
        r = order(i)
        one(1, i).wait_recv()
        two(i).wait_recv()

        def put(value):
            total = value + p1r[1, r].astype(F32) + p2r[r].astype(F32)
            own[r] = total
            if early:
                za_s[r] = total.astype(BF16)

        with_values(p, r, put)
        if early:
            @pl.when((p < WIDE) & (i < parts - 1))
            def _():
                line_a(r, f).start()
        return carry

    lax.fori_loop(0, parts, third, 0)
    swaps[2].wait()
    gain_s[3] = gain_s[2] + gain_r[2]

    if not early:
        es[...] = own[...].astype(BF16)
        group = [
            remote(es, er.at[j - 1], esem.at[j - 1], ersem.at[j - 1], at.other(j)) for j in range(1, extra)
        ]
        for copy in group:
            copy.start()
        for j in range(1, extra):
            group[j - 1].wait_recv()
            own[...] = own[...] + er[j - 1].astype(F32)
        for copy in group:
            copy.wait_send()
        za_s[...] = own[...].astype(BF16)

        @pl.when(p < WIDE)
        def _():
            for j in range(1, parts):
                line_a(f ^ j, f).start()

    @pl.when(p >= WIDE)
    def _():
        for tile in range(half // 128):
            for r in range(parts):
                block = own[r, :, pl.ds(tile * 128, 128)]
                if rows % 128 == 0:
                    own_t[pl.ds(tile * 128, 128), pl.ds(r * rows, rows)] = block.T
            if rows % 128 != 0:
                column = own[:, :, pl.ds(tile * 128, 128)].reshape(parts * rows, 128)
                own_t[pl.ds(tile * 128, 128), :] = column.T
        zb_s[...] = own_t[...].astype(BF16)
        for j in range(1, parts):
            line_b(f ^ j, f).start()

    line_gain = [
        remote(gain_s.at[3], gain_r.at[3 + j], gs.at[3 + j], gr.at[3 + j], at.along(j)) for j in range(1, parts)
    ]
    other_gain = []
    for copy in line_gain:
        copy.start()

    moment("wait")

    @pl.when(p < WIDE)
    def _():
        total = own[f]
        for j in range(1, parts):
            line_a(f ^ j, f ^ j).wait_recv()
            total = total + za_r[f ^ j].astype(F32)
        ga[...] = total.astype(BF16)
        sa[...] = (MOMENTUM * ma[...] + total).astype(BF16)

    @pl.when(p >= WIDE)
    def _():
        total = own_t[pl.ds(pl.multiple_of(f * high, high), high), :]
        for j in range(1, parts):
            line_b(f ^ j, f ^ j).wait_recv()
            total = total + zb_r[f ^ j].astype(F32)
        gb[...] = total.astype(BF16)
        sb[...] = (MOMENTUM * mb[...] + total).astype(BF16)

    def share_a(j, source):
        return remote(sa, s_a.at[pl.ds(pl.multiple_of(source * rows, rows), rows)], ss.at[j], sr.at[j], at.along(j))

    def share_b(j, source):
        return remote(sb, s_b.at[pl.ds(pl.multiple_of(source * high, high), high)], ss.at[j], sr.at[j], at.along(j))

    @pl.when(p < WIDE)
    def _():
        for j in range(1, parts):
            share_a(j, f).start()
        pltpu.make_async_copy(sa, s_a.at[pl.ds(pl.multiple_of(f * rows, rows), rows)], sl).start()

    @pl.when(p >= WIDE)
    def _():
        for j in range(1, parts):
            share_b(j, f).start()
        pltpu.make_async_copy(sb, s_b.at[pl.ds(pl.multiple_of(f * high, high), high)], sl).start()

    finish = spread(at, ga, gb, g_a, g_b, ag_l, ag_s, ag_r)
    total = gain_s[3]
    for j in range(1, parts):
        line_gain[j - 1].wait()
        total = total + gain_r[3 + j]
    if extra > 1:
        gain_s[4] = total
        other_gain = [
            remote(gain_s.at[4], gain_r.at[3 + parts + j], gs.at[3 + parts + j], gr.at[3 + parts + j], at.other(j))
            for j in range(1, extra)
        ]
        for copy in other_gain:
            copy.start()
        for j in range(1, extra):
            other_gain[j - 1].wait()
            total = total + gain_r[3 + parts + j]
    gain_out[...] = total
    finish()

    for slot in range(2):
        lax.fori_loop(0, parts, lambda i, carry, slot=slot: (one(slot, i).wait_send(), carry)[1], 0)
    lax.fori_loop(0, parts, lambda i, carry: (two(i).wait_send(), carry)[1], 0)

    @pl.when(p < WIDE)
    def _():
        for j in range(1, parts):
            line_a(f ^ j, f).wait_send()
            share_a(j, f).wait_send()
            share_a(j, f ^ j).wait_recv()
        pltpu.make_async_copy(sa, s_a.at[pl.ds(pl.multiple_of(f * rows, rows), rows)], sl).wait()

    @pl.when(p >= WIDE)
    def _():
        for j in range(1, parts):
            line_b(f ^ j, f).wait_send()
            share_b(j, f).wait_send()
            share_b(j, f ^ j).wait_recv()
        pltpu.make_async_copy(sb, s_b.at[pl.ds(pl.multiple_of(f * high, high), high)], sl).wait()


def reduce_gradients(xt, dy, gains, moments, rows, high):
    parts = lax.axis_size("fsdp")
    extra = lax.axis_size("ctx") // CLASSES
    kinds, depth, tokens = xt.shape
    half = dy.shape[2]
    dma = pltpu.SemaphoreType.DMA
    vm = pltpu.VMEM
    n_gain = 4 + parts + extra
    group = max(extra - 1, 1)
    spare = (parts, rows, half) if extra > 1 else (1, 16, 128)
    return pl.pallas_call(
        functools.partial(reduce_kernel, parts, extra, high),
        out_shape=(
            jax.ShapeDtypeStruct((WIDE, rows, half), BF16),
            jax.ShapeDtypeStruct((CLASSES - WIDE, high, depth), BF16),
            jax.ShapeDtypeStruct((depth, half), BF16),
            jax.ShapeDtypeStruct((half, depth), BF16),
            jax.ShapeDtypeStruct(gains.shape, F32),
        ),
        in_specs=[ANY, ANY, VMEM] + [ANY] * 5,
        out_specs=(ANY, ANY, ANY, ANY, VMEM),
        scratch_shapes=[
            vm((kinds, depth, 2 * tokens), BF16),
            vm((5, 2 * tokens, half), BF16),
            vm((2, parts, rows, half), BF16),
            vm((2, parts, rows, half), BF16),
            vm((parts, rows, half), BF16),
            vm((parts, rows, half), BF16),
            vm((parts, rows, half), F32),
            vm((half, depth), F32),
            vm((parts, rows, half), BF16),
            vm((parts, rows, half), BF16),
            vm((half, depth), BF16),
            vm((parts, high, depth), BF16),
            vm((rows, half), F32),
            vm((high, depth), F32),
            vm((rows, half), BF16),
            vm((high, depth), BF16),
            vm((rows, half), BF16),
            vm((high, depth), BF16),
            vm(spare, BF16),
            vm((group,) + spare, BF16),
            vm((5,) + gains.shape, F32),
            vm((n_gain,) + gains.shape, F32),
            dma((6,)), dma((6,)), dma((6,)),
            dma((2, parts)), dma((2, parts)), dma((parts,)), dma((parts,)), dma((parts,)), dma((parts,)),
            dma((group,)), dma((group,)), dma, dma((n_gain,)), dma((n_gain,)),
            dma, dma((7,)), dma((CLASSES,)), dma((parts,)), dma((parts,)), dma,
        ],
        compiler_params=pltpu.CompilerParams(
            collective_id=1, has_side_effects=True, vmem_limit_bytes=62 << 20
        ),
        name="reduce_gradients",
    )(xt, dy, gains, *moments)


def rounded(value):
    return value.astype(BF16)


def poly_rows(g, row_start, count):
    block = g[pl.ds(row_start, count), :]
    return rounded(NS_B * block.astype(F32) + NS_C * jnp.dot(block, g[...], preferred_element_type=F32))


def ortho_kernel(
    parts, rows, high, narrow,
    s_a, s_b, o_a, o_b,
    x, x_t, gs, gr, g, poly, sq, sq_r, pa, pb, kt,
    gsem, rsem, qs, qr, ag_l, ag_s, ag_r,
):
    at = Place()
    p, f = at.p, at.f
    depth, half = x.shape
    step = depth // 4
    at.barrier(line=False)
    pair = at.peer(1)

    @pl.when(p < WIDE)
    def _():
        x[...] = s_a[...]

    @pl.when(p >= WIDE)
    def _():
        for tile in range(half // 128):
            x[:, pl.ds(tile * 128, 128)] = s_b[pl.ds(tile * 128, 128), :].T

    def scale_of(total):
        return 1.0 / (jnp.sqrt(total) + 1e-07)

    def normal(ref, inverse):
        ref[...] = rounded(ref[...].astype(F32) * inverse)

    def exchange(slot, r):
        chunk = pl.ds(r * step, step)
        return remote(gs.at[chunk], gr.at[slot, chunk], gsem.at[r], rsem.at[slot, r], pair)

    def fill_poly():
        for r in range(4):
            poly[pl.ds(r * step, step), :] = poly_rows(g, r * step, step)

    my_rows = pl.ds(pl.multiple_of(f * rows, rows), rows)
    my_high = pl.ds(pl.multiple_of(f * high, high), high)

    @pl.when(p >= 2)
    def _():
        wide = x[...].astype(F32)
        sq[...] = jnp.broadcast_to(jnp.sum(wide * wide), sq.shape)
        copy = remote(sq, sq_r, qs, qr, pair)
        copy.start()
        copy.wait()
        normal(x, scale_of(sq[...] + sq_r[...])[:1, :1])

        def grams(slot):
            for r in range(4):
                gs[pl.ds(r * step, step), :] = rounded(contract(x[pl.ds(r * step, step), :], x[...], 1, 1))
                exchange(slot, r).start()
            for r in range(4):
                chunk = pl.ds(r * step, step)
                exchange(slot, r).wait()
                g[chunk, :] = rounded(gs[chunk, :].astype(F32) + gr[slot, chunk, :].astype(F32))

        def iterate(it, carry):
            grams(lax.rem(it, 2))
            fill_poly()
            for tile in range(half // 256):
                block = pl.ds(tile * 256, 256)
                x[:, block] = rounded(
                    NS_A * x[:, block].astype(F32) + jnp.dot(poly[...], x[:, block], preferred_element_type=F32)
                )
            return carry

        lax.fori_loop(0, NS_ITERS - 1, iterate, 0)
        grams((NS_ITERS - 1) % 2)

        @pl.when(p < WIDE)
        def _():
            mine = poly_rows(g, pl.multiple_of(f * rows, rows), rows)
            pa[...] = rounded(NS_A * x[my_rows, :].astype(F32) + jnp.dot(mine, x[...], preferred_element_type=F32))

        @pl.when(p >= WIDE)
        def _():
            fill_poly()
            for tile in range(half // 128):
                x_t[pl.ds(tile * 128, 128), :] = x[:, pl.ds(tile * 128, 128)].T
            block = x_t[my_high, :]
            pb[...] = rounded(NS_A * block.astype(F32) + jnp.dot(block, poly[...], preferred_element_type=F32))

    @pl.when(p < 2)
    def _():
        kt[...] = x[:, narrow:].T
        inverse_k = scale_of(jnp.sum(jnp.square(kt[...].astype(F32))))
        normal(kt, inverse_k)
        wide = x[:, :narrow].astype(F32)
        x[:, :narrow] = rounded(wide * scale_of(jnp.sum(wide * wide)))

        def narrow_step(it, carry):
            gram = rounded(contract(kt[...], kt[...], 1, 1))
            turn = rounded(NS_B * gram.astype(F32) + NS_C * jnp.dot(gram, gram, preferred_element_type=F32))
            kt[...] = rounded(NS_A * kt[...].astype(F32) + jnp.dot(turn, kt[...], preferred_element_type=F32))
            return carry

        lax.fori_loop(0, NS_ITERS, narrow_step, 0)

        def gram_of():
            for r in range(4):
                chunk = pl.ds(r * step, step)
                g[chunk, :] = rounded(contract(x[chunk, :narrow], x[:, :narrow], 1, 1))

        def square_step(it, carry):
            gram_of()
            fill_poly()
            x[:, :narrow] = rounded(
                NS_A * x[:, :narrow].astype(F32) + jnp.dot(poly[...], x[:, :narrow], preferred_element_type=F32)
            )
            return carry

        lax.fori_loop(0, NS_ITERS - 1, square_step, 0)
        gram_of()
        mine = poly_rows(g, pl.multiple_of(f * rows, rows), rows)
        square = rounded(
            NS_A * x[my_rows, :narrow].astype(F32) + jnp.dot(mine, x[:, :narrow], preferred_element_type=F32)
        )
        x[:, narrow:] = kt[...].T
        pa[:, :narrow] = square
        pa[:, narrow:] = x[my_rows, narrow:]

    spread(at, pa, pb, o_a, o_b, ag_l, ag_s, ag_r)()


def orthogonalize(s_a, s_b, rows, high, narrow):
    parts = lax.axis_size("fsdp")
    depth, half = s_a.shape
    dma = pltpu.SemaphoreType.DMA
    vm = pltpu.VMEM
    return pl.pallas_call(
        functools.partial(ortho_kernel, parts, rows, high, narrow),
        out_shape=(
            jax.ShapeDtypeStruct((WIDE, rows, half), BF16),
            jax.ShapeDtypeStruct((CLASSES - WIDE, high, depth), BF16),
        ),
        in_specs=[VMEM, VMEM],
        out_specs=(ANY, ANY),
        scratch_shapes=[
            vm((depth, half), BF16),
            vm((half, depth), BF16),
            vm((depth, depth), BF16),
            vm((2, depth, depth), BF16),
            vm((depth, depth), BF16),
            vm((depth, depth), BF16),
            vm((8, 128), F32),
            vm((8, 128), F32),
            vm((rows, half), BF16),
            vm((high, depth), BF16),
            vm((half - narrow, depth), BF16),
            dma((4,)), dma((2, 4)), dma, dma, dma, dma((7,)), dma((CLASSES,)),
        ],
        compiler_params=pltpu.CompilerParams(
            collective_id=2, has_side_effects=True, vmem_limit_bytes=62 << 20
        ),
        name="orthogonalize",
    )(s_a, s_b)


class Weights:
    def __init__(self, at, sources, homes, zs, s1, s2, sc, recv):
        self.at, self.sources, self.homes = at, sources, homes
        self.zs, self.s1, self.s2, self.sc, self.recv = zs, s1, s2, sc, recv
        self.sends = []
        self.done = 0

    def act(self, group, q, j, plane, send, target, what, first=False):
        recv = self.recv.at[group, q, j]
        home, source = self.homes[group], self.sources[group]
        rows = home.shape[-2] // (1 if group == 3 else self.at.parts)
        unit = -(-rows // (16 * CLASSES)) * 16
        last = rows - (CLASSES - 1) * unit

        def piece(count):
            def go():
                start = pl.multiple_of(q * unit, 16)
                if group == 3:
                    columns = home.shape[1] // self.at.parts
                    dst = home.at[pl.ds(start, count), pl.ds(pl.multiple_of(plane * columns, 128), columns)]
                    src = source.at[pl.ds(start, count)]
                elif group == 0:
                    dst = home.at[:, pl.ds(pl.multiple_of(plane * rows + start, 16), count)]
                    src = dst
                else:
                    dst = home.at[pl.ds(pl.multiple_of(plane * rows + start, 16), count)]
                    src = source.at[pl.ds(start, count)]
                getattr(remote(src if first else dst, dst, send, recv, target), what)()

            return go

        pl.when(q < CLASSES - 1)(piece(unit))
        pl.when(q == CLASSES - 1)(piece(last))

    def send(self, group, q, j, plane, sem, target, first=False):
        self.act(group, q, j, plane, sem, target, "start", first)
        self.sends.append((group, q, j, plane, sem, target, "wait_send", first))

    def arrived(self, group, q, j):
        at = self.at
        self.act(group, q, j, at.f ^ j, self.zs.at[group, j], at.peer(1), "wait_recv")

    def outer(self):
        return (self.at.f == 0) | (self.at.f == self.at.parts - 1)

    def beside(self):
        f, parts = self.at.f, self.at.parts
        lower = f < parts // 2
        return jnp.where(lower, 1 - f, 2 * parts - 3 - f), jnp.where(lower, parts // 2, parts // 2 - 1)

    def hop(self, group, plane, target, sem, first=False, condition=None):
        at = self.at
        item = (group, at.p, target ^ plane, plane, sem, (at.c, target))
        if condition is None:
            self.send(*item, first)
            return
        pl.when(condition)(lambda: self.act(*item, "start", first))
        self.sends.append((condition,) + item + ("wait_send", first))

    def along(self, group):
        near, inner = self.beside()
        self.hop(group, self.at.f, near, self.zs.at[group, 0], True)
        self.hop(group, self.at.f, inner, self.zs.at[group, 1], True, jnp.logical_not(self.outer()))

    def first(self, group, k):
        at = self.at
        j = (1, jnp.where(self.outer(), 2, 3), jnp.where(self.outer(), 3, 2))[k - 1]
        source = at.f ^ j
        near, inner = self.beside()
        self.arrived(group, at.p, j)
        target = jnp.where(source == near, inner, near)
        self.hop(group, source, target, self.zs.at[group, 1 + k], condition=jnp.logical_not(self.outer()))
        self.send(group, at.p, j, source, self.s1.at[group, k], at.peer(at.b1))
        self.send(group, at.p, j, source, self.s2.at[group, 0, k], at.peer(at.b2))
        self.send(group, at.p, j, source, self.sc.at[group, 0, k], at.peer(1))

    def second(self, group, k):
        at = self.at
        j = (1, jnp.where(self.outer(), 2, 3), jnp.where(self.outer(), 3, 2))[k - 1]
        q = at.p ^ at.b1
        self.arrived(group, q, j)
        self.send(group, q, j, at.f ^ j, self.s2.at[group, 1, k], at.peer(at.b2))
        self.send(group, q, j, at.f ^ j, self.sc.at[group, 1, k], at.peer(1))

    def third(self, group, k):
        at = self.at
        j = (1, jnp.where(self.outer(), 2, 3), jnp.where(self.outer(), 3, 2))[k - 1]
        for slot, bits in ((2, at.b2), (3, at.b1 ^ at.b2)):
            self.arrived(group, at.p ^ bits, j)
            self.send(group, at.p ^ bits, j, at.f ^ j, self.sc.at[group, slot, k], at.peer(1))

    def advance(self, count):
        each = self.at.parts - 1
        total = 4 * each
        count = max(count, 0)
        for n in range(self.done, min(self.done + count, total + 2)):
            for lag, act in ((0, self.first), (1, self.second), (2, self.third)):
                if 0 <= n - lag < total:
                    act((n - lag) // each, (n - lag) % each + 1)
            if n % each == each - 1 and n // each + 2 < 4:
                self.along(n // each + 2)
        self.done += count

    def ready(self, group):
        at = self.at
        for bits in (1, 3, 5, 7):
            for j in range(1, at.parts):
                self.arrived(group, at.p ^ bits, j)

    def finish(self):
        for item in self.sends:
            if len(item) == 8:
                self.act(*item)
            else:
                pl.when(item[0])(lambda item=item: self.act(*item[1:]))


def spread_even(at, own, out, local, ss, recv):
    p = at.p

    def copy_of(cls, slot, target, first=False):
        return remote(own if first else out.at[cls], out.at[cls], ss.at[slot], recv.at[cls], target)

    keep = pltpu.make_async_copy(own, out.at[p], local)
    b1, b2 = at.b1, at.b2
    own_sends = [(p, 0, b1, True), (p, 1, b2, True), (p, 2, 1, True)]
    steps = (
        (p ^ b1, [(p ^ b1, 3, b2, False), (p ^ b1, 4, 1, False)]),
        (p ^ b2, [(p ^ b2, 5, 1, False)]),
        (p ^ b1 ^ b2, [(p ^ b1 ^ b2, 6, 1, False)]),
    )

    def move(cls, slot, bits, first):
        return copy_of(cls, slot, at.peer(bits), first)

    def arrived(cls):
        copy_of(cls, 0, at.peer(1)).wait_recv()

    def begin():
        for item in own_sends:
            move(*item).start()
        keep.start()

    def step(k):
        cls, sends = steps[k]
        arrived(cls)
        for item in sends:
            move(*item).start()

    def finish():
        for bits in (1, 3, 5, 7):
            arrived(p ^ bits)
        for item in own_sends + [item for _, sends in steps for item in sends]:
            move(*item).wait_send()
        keep.wait()

    return begin, step, finish


def step_kernel(
    x_ref, up_ref, gains_ref, cos_ref, low_ref, high_ref, bias_ref, wq, wk, wo, wv, wg_in, wu_in, wd_in,
    m_q, m_k, m_o, m_v, m_gate, m_up, m_down,
    out_ref, grad_ref, g_out, o_out, gain_out,
    w01, wg, wu, wd, probs, kv, rot, dkv, c4r, c2r, c1r, att, gate, lifted,
    xt_in, dy_in, dv_in, xf_all, xa_all, yf_all, yv_all, za_r, ma, mq, mk, gain_s, gain_r, sq, sq_r,
    local, zs, s1, s2, sc, recv, kvs, kvr, ds, dr,
    ls, xs, xr, ps, pr, ys, yr, as_, ar, vs, vr, hs, hr, ozs, ozr, msem, gs, gr, ag_l, ag_s, ag_r, ls_l, ls_r, lr_l, lr_r,
    gsem, rsem, qs, qr, ex_s, ex_r, fx_s, fx_r, og_l, og_s, og_r, free,
):
    at = Place()
    p, f, core, parts = at.p, at.f, at.core, at.parts
    width, tokens = x_ref.shape
    half = w01.shape[2]
    keys = half - width
    group = HEADS // KV_HEADS
    scale = 1.0 / math.sqrt(HEAD)
    rows = width // parts
    columns = 2 * half // parts
    tall = width // 2
    pair = at.peer(1)
    my_rows = pl.ds(pl.multiple_of(f * rows, 16), rows)

    weights = Weights(at, (None, wg_in, wu_in, wd_in), (w01, wg, wu, wd), zs, s1, s2, sc, recv)
    keep = [
        pltpu.make_async_copy(wg_in, wg.at[my_rows], local.at[0]),
        pltpu.make_async_copy(wu_in, wu.at[my_rows], local.at[1]),
        pltpu.make_async_copy(
            wd_in, wd.at[:, pl.ds(pl.multiple_of(f * columns, 128), columns)], local.at[2]
        ),
    ]

    def moment(what):
        for cls in range(CLASSES):
            @pl.when(p == cls)
            def _(cls=cls):
                side = cls % 2
                if cls < 2:
                    pairs = [((m_q, m_o)[cls], mq, 0), ((m_k, m_v)[cls], mk, 1)]
                elif cls < WIDE:
                    whole = m_gate if cls < 4 else m_up
                    pairs = [(whole.at[:, pl.ds(side * half, half)], ma, 0)]
                else:
                    pairs = [
                        (
                            m_down.at[pl.ds(side * tall + t * rows, rows)],
                            ma.at[:, pl.ds(t * columns, columns)],
                            t,
                        )
                        for t in range(2)
                    ]
                for src, dst, index in pairs:
                    getattr(pltpu.make_async_copy(src, dst, msem.at[index]), what)()

    w01[0, my_rows, :width] = wq[...]
    w01[0, my_rows, width:] = wk[...].T
    w01[1, my_rows, :width] = wo[...]
    w01[1, my_rows, width:] = wv[...].T
    at.barrier(bits=range(1, CLASSES))
    for index in range(2):
        weights.along(index)
    for copy in keep:
        copy.start()
    moment("start")

    residual = x_ref[...].astype(F32).T
    upstream = up_ref[...].astype(F32).T
    inverse_first = lax.rsqrt(jnp.mean(residual * residual, axis=-1, keepdims=True) + EPS)
    normed_first = (residual * inverse_first * gains_ref[0:1, :]).astype(BF16)
    xt_in[0] = normed_first.T
    xt_in[3] = up_ref[...]

    each = parts - 1
    weights.advance(each + 2)
    weights.ready(0)

    def turn(value, sign):
        tiles = []
        for tile in range(half // 128):
            part = value[:, tile * 128 : (tile + 1) * 128]
            swapped = pltpu.roll(part, HEAD // 2, 1) * low_ref[...] + pltpu.roll(part, 128 - HEAD // 2, 1) * high_ref[...]
            tiles.append(part * cos_ref[...] + swapped if sign > 0 else part * cos_ref[...] - swapped)
        return tiles

    qk = jnp.dot(normed_first, w01[0], preferred_element_type=F32)
    for tile, value in enumerate(turn(qk, 1)):
        rot[:, tile * 128 : (tile + 1) * 128] = value.astype(BF16)
    values = jnp.dot(normed_first, w01[1, :, width:], preferred_element_type=F32).astype(BF16)
    kv[p, :, :keys] = rot[:, width:]
    kv[p, :, keys:] = values

    def block(q, slot, target):
        return remote(kv.at[q], kv.at[q], kvs.at[slot], kvr.at[q], target)

    sent = [block(p, 0, at.peer(at.b1)), block(p, 1, at.peer(at.b2)), block(p, 2, at.peer(1))]
    for copy in sent:
        copy.start()

    def pass_keys(q, slots):
        block(q, 0, at.peer(1)).wait_recv()
        for slot, target in slots:
            copy = block(q, slot, target)
            copy.start()
            sent.append(copy)

    weights.advance(1)
    pass_keys(p ^ at.b1, [(3, at.peer(at.b2)), (4, at.peer(1))])
    pass_keys(p ^ at.b2, [(5, at.peer(1))])
    weights.advance(1)
    pass_keys(p ^ at.b1 ^ at.b2, [(6, at.peer(1))])
    for bits in (1, 3, 5, 7):
        pass_keys(p ^ bits, [])
    weights.advance(1)

    def tokens_of(q):
        return pl.ds(pl.multiple_of(q * tokens, tokens), tokens)

    def kind_of(q):
        return jnp.where(q < 2, 0, jnp.where(q < WIDE, 2, 3))

    own_x = pltpu.make_async_copy(xt_in.at[kind_of(p)], xf_all.at[:, tokens_of(p)], ls.at[0])

    def x_move(bits):
        q = p ^ bits
        return remote(xt_in.at[kind_of(q)], xf_all.at[:, tokens_of(p)], xs.at[bits], xr.at[p], at.peer(bits))

    def a_move():
        return remote(xt_in.at[1], xa_all.at[:, tokens_of(p)], as_, ar.at[p], at.peer(p ^ 1))

    def own_a():
        return pltpu.make_async_copy(xt_in.at[1], xa_all.at[:, tokens_of(p)], ls.at[1])

    def y_move(bits):
        q = p ^ bits
        return remote(dy_in.at[q], yf_all.at[tokens_of(p)], ys.at[bits], yr.at[p], at.peer(bits))

    def own_y():
        return pltpu.make_async_copy(dy_in.at[p], yf_all.at[tokens_of(p)], ls.at[2])

    def v_move():
        return remote(dv_in, yv_all.at[tokens_of(p)], vs, vr.at[p], at.peer(p ^ 1))

    def own_v():
        return pltpu.make_async_copy(dv_in, yv_all.at[tokens_of(p)], ls.at[3])

    for bits in (2, 4, 6):
        pl.when(kind_of(p ^ bits) != 2)(lambda bits=bits: x_move(bits).start())

    def keys_of(g):
        return kv[:, :, g * HEAD : (g + 1) * HEAD].reshape(CLASSES * tokens, HEAD)

    def values_of(g):
        return kv[:, :, keys + g * HEAD : keys + (g + 1) * HEAD].reshape(CLASSES * tokens, HEAD)

    def heads_of(ref, g):
        return jnp.concatenate([ref[:, h * HEAD : (h + 1) * HEAD] for h in range(g * group, (g + 1) * group)], axis=0)

    def attend(g):
        scores = contract(keys_of(g), heads_of(rot, g), 1, 1) * scale
        bias = bias_ref[...].astype(F32)
        scores = scores + jnp.concatenate([bias] * group, axis=1)
        top = jnp.max(scores, axis=0, keepdims=True)
        expo = jnp.exp(scores - top)
        total = jnp.sum(expo, axis=0, keepdims=True)
        chance = expo * (1.0 / total)
        probs[g] = chance
        mixed = contract(values_of(g), chance.astype(BF16), 0, 0)
        turned = mixed.T.astype(BF16)
        for h in range(group):
            at_lane = (g * group + h) * HEAD
            att[:, at_lane : at_lane + HEAD] = turned[h * tokens : (h + 1) * tokens]

    for g in range(KV_HEADS):
        attend(g)
        weights.advance(1 if g < KV_HEADS - 1 else 4 * each - weights.done)
    for copy in keep:
        copy.wait()
    weights.ready(1)

    xt_in[1] = att[...].T
    middle = residual + jnp.dot(att[...], w01[1, :, :width], preferred_element_type=F32)
    inverse_second = lax.rsqrt(jnp.mean(middle * middle, axis=-1, keepdims=True) + EPS)
    normed_second = (middle * inverse_second * gains_ref[1:2, :]).astype(BF16)
    xt_in[2] = normed_second.T
    weights.advance(1)
    gate[...] = jnp.dot(normed_second, wg[...], preferred_element_type=F32)
    weights.advance(1)

    own_x.start()
    for bits in (2, 4, 6):
        pl.when(kind_of(p ^ bits) == 2)(lambda bits=bits: x_move(bits).start())
    pl.when(p != 1)(lambda: a_move().start())
    pl.when(p == 1)(lambda: own_a().start())

    def give_y(bits, low, high):
        q = p ^ bits

        @pl.when((q >= low) & (q < high))
        def _():
            y_move(bits).start()

    weights.ready(2)
    for side in range(2):
        lifted[side * tokens : (side + 1) * tokens] = jnp.dot(
            normed_second, wu[:, side * half : (side + 1) * half], preferred_element_type=F32
        )

    def lift():
        return jnp.concatenate([lifted[:tokens], lifted[tokens:]], axis=1)

    hidden = (gate[...] * jax.nn.sigmoid(gate[...]) * lift()).astype(BF16)
    dy_in[6] = hidden[:, :half]
    dy_in[7] = hidden[:, half:]
    for bits in range(1, CLASSES):
        give_y(bits, WIDE, CLASSES)
    weights.ready(3)

    grad_hidden = jnp.dot(upstream.astype(BF16), wd[...], preferred_element_type=F32)
    sigma = jax.nn.sigmoid(gate[...])
    grad_gate = (grad_hidden * lift() * sigma * (1.0 + gate[...] * (1.0 - sigma))).astype(BF16)
    grad_lifted = (grad_hidden * gate[...] * sigma).astype(BF16)
    for side in range(2):
        lanes = slice(side * half, (side + 1) * half)
        dy_in[2 + side] = grad_gate[:, lanes]
        dy_in[4 + side] = grad_lifted[:, lanes]
    for bits in range(1, CLASSES):
        give_y(bits, 2, WIDE)

    out_ref[...] = (middle + contract(hidden, wd[...], 1, 1)).T.astype(BF16)
    weights.finish()
    grad_normed = contract(grad_gate, wg[...], 1, 1) + contract(grad_lifted, wu[...], 1, 1)
    pl.semaphore_signal(free.at[0], inc=1, device_id=pair, device_id_type=MESH)

    def norm_back(value, inverse, gain, incoming):
        scaled = incoming * gain
        mean = jnp.mean(scaled * value, axis=-1, keepdims=True)
        through = inverse * scaled - value * (inverse * inverse * inverse) * mean
        return through, jnp.sum(incoming * value * inverse, axis=0, keepdims=True)

    through, gain_second = norm_back(middle, inverse_second, gains_ref[1:2, :], grad_normed)
    gain_s[0] = jnp.zeros(gain_s.shape[1:], F32)
    gain_s[0, 1:2, :] = gain_second
    grad_middle = upstream + through
    grad_branch = grad_middle.astype(BF16)
    dy_in[1, :, :width] = grad_branch
    dy_in[1, :, width:] = jnp.zeros((tokens, keys), BF16)
    att[...] = contract(grad_branch, w01[1, :, :width], 1, 1).astype(BF16)

    for bits in range(1, CLASSES):
        give_y(bits, 1, 2)

    own = lifted.at[pl.ds(0, rows)]

    def swap(slot, target):
        return remote(gain_s.at[slot], gain_r.at[slot], gs.at[slot], gr.at[slot], target)

    outer = (f == 0) | (f == parts - 1)
    lower = f < parts // 2
    beside = jnp.where(lower, 1 - f, 2 * parts - 3 - f)
    far_outer = jnp.where(lower, parts - 1, 0)
    far_inner = jnp.where(lower, parts // 2, parts // 2 - 1)

    def order(i):
        falling = jnp.where(outer, parts - 1 - i, jnp.where(i == 0, 0, parts - i))
        return jnp.where(lower, falling, parts - 1 - falling)

    cut = width // 128 * 128
    part_lanes = (pl.ds(0, cut), pl.ds(cut, half - cut))
    parts_early = (lambda: p >= 1, lambda: p >= 2)
    parts_late = (lambda: p < 1, lambda: p < 2)

    def room(r):
        return wd.at[pl.ds(pl.multiple_of(r * rows, 16), rows), pl.ds(half, half)]

    def line(r, part):
        lanes = part_lanes[part]
        near_slot = jnp.where(lower, r - 1, parts - 2 - r)
        slot = jnp.where(outer, 2 - near_slot, jnp.where(r == beside, 0, jnp.where(r == far_outer, 1, 3)))
        target = jnp.where(outer, beside, r)
        return remote(
            room(r).at[:, lanes], za_r.at[slot, :, lanes], ozs.at[part, r], ozr.at[part, slot], (at.c, target)
        )

    def arrival(slot, part):
        lanes = part_lanes[part]
        return remote(
            room(f).at[:, lanes], za_r.at[slot, :, lanes], ozs.at[part, f], ozr.at[part, slot], at.along(1)
        )

    def relay(k, part):
        r = (far_outer, far_inner)[k]
        lanes = part_lanes[part]

        @pl.when(jnp.logical_not(outer))
        def _():
            arrival(k, part).wait_recv()
            total = room(r)[:, lanes].astype(F32) + za_r[k, :, lanes].astype(F32)
            room(r)[:, lanes] = total.astype(BF16)
            line(r, part).start()

    middle_token = CLASSES // 2 * tokens

    def sides_of():
        return [
            remote(
                yf_all.at[pl.ds(side * middle_token, middle_token)],
                wu.at[pl.ds(0, middle_token), pl.ds(side * half, half)],
                hs.at[side], hr.at[side], pair,
            )
            for side in range(2)
        ]

    def produce(r, put):
        at_rows = pl.ds(pl.multiple_of(r * rows, 16), rows)
        every = slice(0, half)

        @pl.when(p == 1)
        def _():
            put(slice(0, width), jnp.dot(xa_all[at_rows, :], yf_all[:, pl.ds(0, width)], preferred_element_type=F32))

        @pl.when((p != 1) & (p < WIDE))
        def _():
            put(every, jnp.dot(xf_all[at_rows, :], yf_all[...], preferred_element_type=F32))

        @pl.when(p >= WIDE)
        def _():
            side, start = lax.div(r * columns, half), pl.multiple_of(lax.rem(r * columns, half), 128)
            for t in range(2):
                part_rows = pl.ds(pl.multiple_of((p - WIDE) * tall + t * rows, 16), rows)
                lanes = slice(t * columns, (t + 1) * columns)

                @pl.when(side == core)
                def _():
                    put(
                        lanes,
                        jnp.dot(xf_all[part_rows, :], yf_all[:, pl.ds(start, columns)], preferred_element_type=F32),
                    )

                @pl.when(side != core)
                def _():
                    put(
                        lanes,
                        jnp.dot(
                            xf_all[part_rows, pl.ds(0, middle_token)],
                            wu[pl.ds(0, middle_token), pl.ds(start, columns)],
                            preferred_element_type=F32,
                        )
                        + jnp.dot(
                            xf_all[part_rows, pl.ds(middle_token, middle_token)],
                            wu[pl.ds(0, middle_token), pl.ds(pl.multiple_of(half + start, 128), columns)],
                            preferred_element_type=F32,
                        ),
                    )

    def keep_chunk(r):
        def put(lanes, value):
            own[:, lanes] = value
            room(r)[:, lanes] = value.astype(BF16)

        return put

    def gradients(conditions):
        for bits in range(1, CLASSES):
            arrived_y(p ^ bits)

        @pl.when(p >= WIDE)
        def _():
            for copy in sides_of():
                copy.start()
            for copy in sides_of():
                copy.wait()

        def step_of(i, carry):
            r = order(i)
            produce(r, keep_chunk(r))
            goes = (i == 0) | (outer & (i < parts - 1))
            for part in range(2):
                pl.when(goes & conditions[part]())(lambda part=part: line(r, part).start())
            return carry

        lax.fori_loop(0, parts, step_of, 0)

    def value_gradient():
        for q in range(CLASSES):
            if q != 1:
                remote(dv_in, yv_all.at[tokens_of(q)], vs, vr.at[q], pair).wait_recv()

        def step_of(i, carry):
            r = order(i)
            at_rows = pl.ds(pl.multiple_of(r * rows, 16), rows)
            value = jnp.dot(xf_all[at_rows, :], yv_all[...], preferred_element_type=F32)

            @pl.when(i < parts - 1)
            def _():
                room(r)[:, pl.ds(width, keys)] = value[:, :keys].astype(BF16)
                pl.when((i == 0) | outer)(lambda: line(r, 1).start())

            @pl.when(i == parts - 1)
            def _():
                own[:, pl.ds(width, keys)] = value[:, :keys]

            return carry

        lax.fori_loop(0, parts, step_of, 0)

    def arrived_y(q):
        remote(dy_in.at[0], yf_all.at[tokens_of(q)], ys.at[1], yr.at[q], pair).wait_recv()

    def arrived_x(q):
        remote(xt_in.at[0], xf_all.at[:, tokens_of(q)], xs.at[2], xr.at[q], pair).wait_recv()

    def x_pair(bits):
        q = p ^ bits
        return remote(xf_all.at[:, tokens_of(q)], xf_all.at[:, tokens_of(q)], ps.at[bits], pr.at[q], pair)

    def attend_back(g):
        chance = probs[g]
        out_grad = heads_of(att, g)
        query = heads_of(rot, g)
        grad_probs = contract(values_of(g), out_grad, 1, 1)
        delta = jnp.sum(grad_probs * chance, axis=0, keepdims=True)
        grad_scores = (chance * (grad_probs - delta)).astype(BF16)
        grad_values = jnp.dot(chance.astype(BF16), out_grad, preferred_element_type=F32)
        grad_keys = jnp.dot(grad_scores, query, preferred_element_type=F32) * scale
        dkv[:, :, g * HEAD : (g + 1) * HEAD] = grad_keys.reshape(CLASSES, tokens, HEAD)
        dkv[:, :, keys + g * HEAD : keys + (g + 1) * HEAD] = grad_values.reshape(CLASSES, tokens, HEAD)
        turned = contract(keys_of(g), grad_scores, 0, 0).T * scale
        for h in range(group):
            at_lane = (g * group + h) * HEAD
            gate[:, at_lane : at_lane + HEAD] = turned[h * tokens : (h + 1) * tokens]

    for g in range(KV_HEADS):
        attend_back(g)

    def halve(bit, rest, sbuf, rbuf, index, between=None):
        for i, bits in enumerate(rest):
            sbuf[pl.ds(i // 2 * tokens, tokens), pl.ds(i % 2 * 2 * keys, 2 * keys)] = dkv[p ^ bit ^ bits].astype(BF16)
        copy = remote(sbuf, rbuf, ds.at[index], dr.at[index], at.peer(bit))
        copy.start()
        if between is not None:
            between()
        copy.wait()
        for i, bits in enumerate(rest):
            dkv[p ^ bits] = dkv[p ^ bits] + rbuf[pl.ds(i // 2 * tokens, tokens), pl.ds(i % 2 * 2 * keys, 2 * keys)].astype(F32)

    own_x.wait()
    for bits in (2, 4, 6):
        arrived_x(p ^ bits)
    for bits in (0, 2, 4, 6):
        x_pair(bits).start()

    def early():
        for bits in (0, 2, 4, 6):
            remote(
                xf_all.at[:, tokens_of(p ^ bits ^ 1)], xf_all.at[:, tokens_of(p ^ bits ^ 1)],
                ps.at[bits], pr.at[p ^ bits ^ 1], pair,
            ).wait_recv()
        pl.semaphore_wait(free.at[0], 1)

        @pl.when(p == 1)
        def _():
            own_a().wait()
            for q in range(CLASSES):
                if q != 1:
                    remote(xt_in.at[1], xa_all.at[:, tokens_of(q)], as_, ar.at[q], pair).wait_recv()

        @pl.when(p >= 1)
        def _():
            own_y().start()
            own_y().wait()
            gradients(parts_early)

    halve(1, (0, 2, 4, 6), wg.at[pl.ds(0, 2 * tokens), pl.ds(0, half)], c4r, 0)
    halve(at.b1, (0, at.b2), wg.at[pl.ds(2 * tokens, tokens), pl.ds(0, half)], c2r, 1, early)
    halve(at.b2, (0,), wg.at[pl.ds(3 * tokens, tokens), pl.ds(0, 2 * keys)], c1r, 2)

    gate[:, width:half] = dkv[p, :, :keys]
    for tile, value in enumerate(turn(gate[:, :half], -1)):
        dy_in[0, :, tile * 128 : (tile + 1) * 128] = value.astype(BF16)
    dv_in[...] = jnp.zeros(dv_in.shape, BF16)
    dv_in[:, :keys] = dkv[p, :, keys:].astype(BF16)
    for bits in range(1, CLASSES):
        give_y(bits, 0, 1)
    pl.when(p != 1)(lambda: v_move().start())
    pl.when(p == 1)(lambda: own_v().start())
    grad_normed = contract(dy_in[0], w01[0], 1, 1)
    grad_normed = grad_normed + contract(dv_in[:, :keys], w01[1, :, width:], 1, 1)
    through, gain_first = norm_back(residual, inverse_first, gains_ref[0:1, :], grad_normed)
    gain_s[0, 0:1, :] = gain_first
    swaps = [swap(0, pair)]
    swaps[0].start()
    grad_ref[...] = (grad_middle + through).T
    def relays(k, conditions):
        for part in range(2):
            pl.when(conditions[part]())(lambda part=part: relay(k, part))

    relays(0, parts_early)

    @pl.when(p == 0)
    def _():
        own_y().start()
        own_y().wait()
        gradients(parts_late)

    @pl.when(p == 1)
    def _():
        own_v().wait()
        value_gradient()

    relays(1, parts_early)
    relays(0, parts_late)
    relays(1, parts_late)
    swaps[0].wait()
    gain_s[1] = gain_s[0] + gain_r[0]
    swaps.append(swap(1, at.peer(2)))
    swaps[1].start()
    for bits in (0, 2, 4, 6):
        x_pair(bits).wait_send()
    for bits in range(1, CLASSES):
        y_move(bits).wait_send()
    for bits in (2, 4, 6):
        x_move(bits).wait_send()

    @pl.when(p != 1)
    def _():
        a_move().wait_send()
        v_move().wait_send()

    swaps[1].wait()
    gain_s[2] = gain_s[1] + gain_r[1]
    swaps.append(swap(2, at.peer(4)))
    swaps[2].start()

    moment("wait")

    @pl.when(p < 2)
    def _():
        ma[:, :width] = mq[...]
        ma[:, width:] = mk[...].T

    sall = wd.at[:, pl.ds(0, half)]
    ga, pa = (w01.at[1, pl.ds((parts - 1 - i) * rows, rows)] for i in range(2))

    def shard(index, part):
        return sall.at[pl.ds(pl.multiple_of(index * rows, 16), rows), part_lanes[part]]

    def rightward(index, part):
        here = shard(index, part)
        return remote(here, here, ls_r.at[part, index], lr_r.at[part, index], (at.c, lax.rem(f + 1, parts)))

    def leftward(index, part):
        here = shard(index, part)
        return remote(here, here, ls_l.at[part, index], lr_l.at[part, index], (at.c, lax.rem(f + parts - 1, parts)))

    can_right = f < parts - 1
    can_left = f > 0

    def settle_part(part):
        lanes = part_lanes[part]
        total = own[:, lanes]
        for k in range(2):
            slot = jnp.where(outer, k, 2 + k)
            arrival(slot, part).wait_recv()
            total = total + za_r[slot, :, lanes].astype(F32)
        ga[:, lanes] = total.astype(BF16)
        sall[my_rows, lanes] = (MOMENTUM * ma[:, lanes] + total).astype(BF16)
        pl.when(can_right)(lambda: rightward(f, part).start())
        pl.when(can_left)(lambda: leftward(f, part).start())

    def hop_part(hop, part):
        @pl.when(f - hop >= 0)
        def _():
            rightward(f - hop, part).wait_recv()
            pl.when(can_right)(lambda: rightward(f - hop, part).start())

        @pl.when(f + hop < parts)
        def _():
            leftward(f + hop, part).wait_recv()
            pl.when(can_left)(lambda: leftward(f + hop, part).start())

    spread_begin, spread_step, spread_finish = spread_even(at, ga, g_out, ag_l, ag_s, ag_r)
    for conditions, whole in ((parts_early, p >= 2), (parts_late, p < 2)):
        for part in range(2):
            pl.when(conditions[part]())(lambda part=part: settle_part(part))
        pl.when(whole)(spread_begin)
        for hop in range(1, parts):
            for part in range(2):
                pl.when(conditions[part]())(lambda hop=hop, part=part: hop_part(hop, part))

    swaps[2].wait()
    gain_s[3] = gain_s[2] + gain_r[2]
    line_gain = [
        remote(gain_s.at[3], gain_r.at[3 + j], gs.at[3 + j], gr.at[3 + j], at.along(j)) for j in range(1, parts)
    ]
    for copy in line_gain:
        copy.start()

    for part in range(2):
        for j in range(1, parts):
            line(f ^ j, part).wait_send()
        pl.when(can_right)(lambda: rightward(f, part).wait_send())
        pl.when(can_left)(lambda: leftward(f, part).wait_send())
        for hop in range(1, parts):
            pl.when((f - hop >= 0) & can_right)(lambda hop=hop: rightward(f - hop, part).wait_send())
            pl.when((f + hop < parts) & can_left)(lambda hop=hop: leftward(f + hop, part).wait_send())
    pl.semaphore_signal(free.at[1], inc=1, device_id=pair, device_id_type=MESH)
    pl.semaphore_wait(free.at[1], 1)

    x = w01.at[0]
    wide_gram = 1024
    gram_s, g = wg.at[:, pl.ds(0, wide_gram)], wg.at[:, pl.ds(wide_gram, wide_gram)]
    poly, xf = wd.at[:, pl.ds(0, wide_gram)], wd.at[:, pl.ds(half, columns)]
    bounds = [0, width // 3 // 16 * 16, width // 3 // 16 * 32, width - width // 8 // 16 * 16, width]
    spans = [(low, high - low) for low, high in zip(bounds, bounds[1:])]

    def gram_r(slot):
        return wu.at[:, pl.ds(slot * wide_gram, wide_gram)]

    def scale_of(total):
        return 1.0 / (jnp.sqrt(total) + 1e-07)

    def normal(ref, inverse):
        ref[...] = rounded(ref[...].astype(F32) * inverse)

    def exchange(slot, r):
        part = pl.ds(*spans[r])
        return remote(gram_s.at[part], gram_r(slot).at[part], gsem.at[r], rsem.at[slot, r], pair)

    def poly_of(start, count):
        part = g[pl.ds(start, count), pl.ds(0, width)]
        square = jnp.dot(part, g[:, pl.ds(0, width)], preferred_element_type=F32)
        return rounded(NS_B * part.astype(F32) + NS_C * square)

    def fill_poly():
        for low, count in spans:
            poly[pl.ds(low, count), pl.ds(0, width)] = poly_of(low, count)

    near = parts // 2
    mine_at = core * near
    last_core = lax.div(f, near)
    f_lanes = pl.ds(pl.multiple_of(lax.rem(f, near) * columns, 128), columns)

    kt = wd.at[pl.ds(0, keys), pl.ds(half + 256, wide_gram)]

    def xo(i):
        return w01.at[1, pl.ds(i * rows, rows)]

    def give():
        return [
            remote(
                sall.at[pl.ds(pl.multiple_of(((1 - core) * near + i) * rows, 16), rows)],
                xo(i), ex_s.at[i], ex_r.at[i], pair,
            )
            for i in range(near)
        ]

    def give_last():
        return remote(x.at[:, f_lanes], xf, fx_s, fx_r, pair)

    @pl.when(p >= 2)
    def _():
        @pl.when(p >= WIDE)
        def _():
            copies = give()
            for copy in copies:
                copy.start()
            for i in range(near):
                part = sall[pl.ds(pl.multiple_of((mine_at + i) * rows, 16), rows), :]
                for t in range(2):
                    x[pl.ds(pl.multiple_of(core * tall + t * rows, 16), rows), pl.ds(i * columns, columns)] = part[
                        :, t * columns : (t + 1) * columns
                    ]
            for i, copy in enumerate(copies):
                copy.wait()
                part = xo(i)
                for t in range(2):
                    x[pl.ds(pl.multiple_of((1 - core) * tall + t * rows, 16), rows), pl.ds(i * columns, columns)] = part[
                        :, pl.ds(t * columns, columns)
                    ]

        def squares(ref):
            wide = ref[...].astype(F32)
            sq[...] = jnp.broadcast_to(jnp.sum(wide * wide), sq.shape)

        pl.when(p < WIDE)(lambda: squares(sall))
        pl.when(p >= WIDE)(lambda: squares(x))
        copy = remote(sq, sq_r, qs, qr, pair)
        copy.start()
        copy.wait()
        inverse = scale_of(sq[...] + sq_r[...])[:1, :1]

        @pl.when(p < WIDE)
        def _():
            x[...] = rounded(sall[...].astype(F32) * inverse)

        pl.when(p >= WIDE)(lambda: normal(x, inverse))

        def grams(slot):
            for r in range(4):
                gram_s[pl.ds(*spans[r]), pl.ds(0, width)] = rounded(
                    contract(x[pl.ds(*spans[r]), :], x[...], 1, 1)
                )
                exchange(slot, r).start()
            for r in range(4):
                part = pl.ds(*spans[r])
                exchange(slot, r).wait()
                g[part, pl.ds(0, width)] = rounded(
                    gram_s[part, pl.ds(0, width)].astype(F32) + gram_r(slot)[part, pl.ds(0, width)].astype(F32)
                )

        def iterate(slot):
            grams(slot)
            fill_poly()
            for tile in range(half // 256):
                part = pl.ds(tile * 256, 256)
                x[:, part] = rounded(
                    NS_A * x[:, part].astype(F32) + jnp.dot(poly[:, pl.ds(0, width)], x[:, part], preferred_element_type=F32)
                )

        def iterate_twice(it, carry):
            iterate(0)
            pl.when(it == 1)(lambda: spread_step(1))
            iterate(1)
            pl.when(it == 0)(lambda: spread_step(0))
            pl.when(it == 1)(lambda: spread_step(2))
            return carry

        lax.fori_loop(0, (NS_ITERS - 1) // 2, iterate_twice, 0)

        @pl.when((p >= WIDE) & (core == last_core))
        def _():
            give_last().start()
            xf[...] = x[:, f_lanes]

        grams(0)

        @pl.when(p < WIDE)
        def _():
            part = poly_of(pl.multiple_of(f * rows, 16), rows)
            pa[...] = rounded(NS_A * x[my_rows, :].astype(F32) + jnp.dot(part, x[...], preferred_element_type=F32))

        @pl.when(p >= WIDE)
        def _():
            pl.when(core == last_core)(lambda: give_last().wait_send())
            pl.when(core != last_core)(lambda: give_last().wait_recv())
            for t in range(2):
                top = pl.multiple_of(core * tall + t * rows, 16)
                part = poly_of(top, rows)
                pa[:, t * columns : (t + 1) * columns] = rounded(
                    NS_A * xf[pl.ds(top, rows), :].astype(F32) + jnp.dot(part, xf[...], preferred_element_type=F32)
                )

    @pl.when(p < 2)
    def _():
        x[...] = sall[...]
        kt[:, pl.ds(0, width)] = x[:, pl.ds(width, keys)].T
        turned = kt[:, pl.ds(0, width)].astype(F32)
        kt[:, pl.ds(0, width)] = rounded(turned * scale_of(jnp.sum(turned * turned)))
        wide = x[:, pl.ds(0, width)].astype(F32)
        x[:, pl.ds(0, width)] = rounded(wide * scale_of(jnp.sum(wide * wide)))

        def narrow_step(it, carry):
            now = kt[:, pl.ds(0, width)]
            gram = rounded(contract(now, now, 1, 1))
            turned = rounded(NS_B * gram.astype(F32) + NS_C * jnp.dot(gram, gram, preferred_element_type=F32))
            kt[:, pl.ds(0, width)] = rounded(
                NS_A * now.astype(F32) + jnp.dot(turned, now, preferred_element_type=F32)
            )
            return carry

        lax.fori_loop(0, NS_ITERS, narrow_step, 0)

        def gram_of():
            for r in range(4):
                part = pl.ds(*spans[r])
                g[part, pl.ds(0, width)] = rounded(contract(x[part, pl.ds(0, width)], x[:, pl.ds(0, width)], 1, 1))

        def square_step(it, carry):
            gram_of()
            fill_poly()
            x[:, pl.ds(0, width)] = rounded(
                NS_A * x[:, pl.ds(0, width)].astype(F32) + jnp.dot(poly[:, pl.ds(0, width)], x[:, pl.ds(0, width)], preferred_element_type=F32)
            )
            for k in range(3):
                pl.when(it == k + 1)(lambda k=k: spread_step(k))
            return carry

        lax.fori_loop(0, NS_ITERS - 1, square_step, 0)
        gram_of()
        part = poly_of(pl.multiple_of(f * rows, 16), rows)
        square = rounded(
            NS_A * x[my_rows, pl.ds(0, width)].astype(F32) + jnp.dot(part, x[:, pl.ds(0, width)], preferred_element_type=F32)
        )
        x[:, pl.ds(width, keys)] = kt[:, pl.ds(0, width)].T
        pa[:, :width] = square
        pa[:, width:] = x[my_rows, pl.ds(width, keys)]

    out_begin, out_step, out_finish = spread_even(at, pa, o_out, og_l, og_s, og_r)
    out_begin()
    total = gain_s[3]
    for j in range(1, parts):
        line_gain[j - 1].wait()
        total = total + gain_r[3 + j]
    gain_out[...] = total
    spread_finish()
    for k in range(3):
        out_step(k)
    for copy in sent:
        copy.wait_send()
    out_finish()


def step_pass(x, up, gains, tables, bias, shards, moments):
    parts = lax.axis_size("fsdp")
    width, tokens = x.shape
    half = shards[4].shape[1] // 2
    rows = width // parts
    keys = half - width
    near = parts // 2
    dma = pltpu.SemaphoreType.DMA
    vm = pltpu.VMEM
    group = HEADS // KV_HEADS
    two = 2 * keys
    n_gain = 3 + parts
    return pl.pallas_call(
        step_kernel,
        out_shape=(
            jax.ShapeDtypeStruct((width, tokens), BF16),
            jax.ShapeDtypeStruct((width, tokens), F32),
            jax.ShapeDtypeStruct((CLASSES, rows, half), BF16),
            jax.ShapeDtypeStruct((CLASSES, rows, half), BF16),
            jax.ShapeDtypeStruct((8, width), F32),
        ),
        in_specs=[VMEM] * 11 + [ANY] * 10,
        out_specs=(VMEM, VMEM, ANY, ANY, VMEM),
        scratch_shapes=[
            vm((2, width, half), BF16),
            vm((width, 2 * half), BF16),
            vm((width, 2 * half), BF16),
            vm((width, 2 * half), BF16),
            vm((KV_HEADS, CLASSES * tokens, group * tokens), F32),
            vm((CLASSES, tokens, two), BF16),
            vm((tokens, half), BF16),
            vm((CLASSES, tokens, two), F32),
            vm((2 * tokens, 2 * two), BF16),
            vm((tokens, 2 * two), BF16),
            vm((tokens, two), BF16),
            vm((tokens, width), BF16),
            vm((tokens, 2 * half), F32),
            vm((2 * tokens, half), F32),
            vm((4, width, tokens), BF16),
            vm((CLASSES, tokens, half), BF16),
            vm((tokens, -(-keys // 128) * 128), BF16),
            vm((width, CLASSES * tokens), BF16),
            vm((width, CLASSES * tokens), BF16),
            vm((CLASSES * tokens, half), BF16),
            vm((CLASSES * tokens, -(-keys // 128) * 128), BF16),
            vm((4, rows, half), BF16),
            vm((rows, half), F32),
            vm((rows, width), F32),
            vm((keys, rows), F32),
            vm((4, 8, width), F32),
            vm((n_gain, 8, width), F32),
            vm((8, 128), F32),
            vm((8, 128), F32),
            dma((3,)), dma((4, 1 + parts)), dma((4, parts)), dma((4, 2, parts)), dma((4, 4, parts)),
            dma((4, CLASSES, parts)), dma((7,)), dma((CLASSES,)), dma((3,)), dma((3,)),
            dma((4,)), dma((CLASSES,)), dma((CLASSES,)), dma((CLASSES,)), dma((CLASSES,)),
            dma((CLASSES,)), dma((CLASSES,)), dma, dma((CLASSES,)), dma, dma((CLASSES,)),
            dma((2,)), dma((2,)), dma((2, parts)), dma((2, parts)),
            dma((2,)), dma((n_gain,)), dma((n_gain,)),
            dma, dma((7,)), dma((CLASSES,)),
            dma((2, parts)), dma((2, parts)), dma((2, parts)), dma((2, parts)),
            dma((4,)), dma((2, 4)), dma, dma,
            dma((near,)), dma((near,)), dma, dma,
            dma, dma((7,)), dma((CLASSES,)), pltpu.SemaphoreType.REGULAR((2,)),
        ],
        compiler_params=pltpu.CompilerParams(
            collective_id=3, has_side_effects=True, vmem_limit_bytes=63 << 20
        ),
        name="step_pass",
    )(x, up, gains, *tables, bias, *shards, *moments)


def settle_wide(factors, *refs):
    gs, os = refs[0], refs[1]
    ms, ws, outs = refs[2:6], refs[6:10], refs[10:]
    width = ms[0].shape[1]
    half = gs.shape[2]

    def one(index, g, o, lanes):
        grad, moment, weight = (outs[3 * index + i] for i in range(3))
        value = g.astype(F32)
        grad[:, lanes] = value
        moment[:, lanes] = MOMENTUM * ms[index][:, lanes] + value
        weight[:, lanes] = ws[index][:, lanes].astype(F32) + factors[index] * o.astype(F32)

    for index in range(2):
        one(index, gs[index, :, :width], os[index, :, :width], slice(0, width))
    for index in range(2):
        for side in range(2):
            cls = 2 + 2 * index + side
            one(2 + index, gs[cls], os[cls], slice(side * half, (side + 1) * half))


def settle_turned(factors, g_tall, o_tall, g_pair, o_pair, *refs):
    ms, ws, outs = refs[0:3], refs[3:6], refs[6:]
    keys = ms[1].shape[0]

    def one(index, g, o):
        grad, moment, weight = (outs[3 * index + i] for i in range(3))
        grad[...] = g
        moment[...] = MOMENTUM * ms[index][...] + g
        weight[...] = ws[index][...].astype(F32) + factors[index] * o

    one(0, g_tall[0].astype(F32), o_tall[0].astype(F32))

    @pl.when(pl.program_id(0) == 0)
    def _():
        for index in range(2):
            start = g_pair.shape[2] - keys
            one(1 + index, g_pair[index, :, start:].astype(F32).T, o_pair[index, :, start:].astype(F32).T)


def settle(g, o, moments, shards, factors):
    m_q, m_k, m_o, m_v, m_gate, m_up, m_down = moments
    w_q, w_k, w_o, w_v, w_gate, w_up, w_down = shards
    f_q, f_k, f_v, f_o, f_gate, f_up, f_down = factors
    _, rows, half = g.shape
    width, columns = m_down.shape
    block = 16 if rows % 16 == 0 else rows
    piece = pl.BlockSpec((WIDE, block, half), lambda i: (0, i, 0))

    def row_block(array):
        return pl.BlockSpec((block, array.shape[1]), lambda i: (i, 0))

    def result(arrays):
        return tuple(jax.ShapeDtypeStruct(array.shape, F32) for array in arrays for _ in range(3))

    wide = (m_q, m_o, m_gate, m_up)
    first = pl.pallas_call(
        functools.partial(settle_wide, (f_q, f_o, f_gate, f_up)),
        grid=(rows // block,),
        out_shape=result(wide),
        in_specs=[piece, piece] + [row_block(array) for array in wide] * 2,
        out_specs=tuple(row_block(array) for array in wide for _ in range(3)),
        compiler_params=pltpu.CompilerParams(vmem_limit_bytes=60 << 20),
        name="settle_wide",
    )(g, o, *wide, w_q, w_o, w_gate, w_up)

    turned = (m_down, m_k, m_v)
    halves = half // columns
    low = 80 if rows % 80 == 0 else rows
    each = rows // low
    tile = pl.BlockSpec(
        (1, low, columns), lambda i: (WIDE + i // (halves * each), i % each, i // each % halves)
    )
    both = pl.BlockSpec((2, rows, half // 2), lambda i: (0, 0, 1))
    specs = [pl.BlockSpec((low, columns), lambda i: (i, 0))] + [
        pl.BlockSpec(array.shape, lambda i: (0, 0)) for array in turned[1:]
    ]
    second = pl.pallas_call(
        functools.partial(settle_turned, (f_down, f_k, f_v)),
        grid=(width // low,),
        out_shape=result(turned),
        in_specs=[tile, tile, both, both] + specs * 2,
        out_specs=tuple(spec for spec in specs for _ in range(3)),
        compiler_params=pltpu.CompilerParams(vmem_limit_bytes=60 << 20),
        name="settle_turned",
    )(g, o, g, o, *turned, w_down, w_k, w_v)
    q, out, gate, up = (first[3 * i : 3 * i + 3] for i in range(4))
    down, k, v = (tuple(item.T for item in second[3 * i : 3 * i + 3]) for i in range(3))
    return list(zip(q, k, v, out, gate, up, down))


def rotary_tables(positions, width):
    half = width // 2
    frequency = THETA ** (-(jnp.arange(half, dtype=jnp.float32) * 2.0 / width))
    angle = positions.astype(jnp.float32)[:, None] * frequency[None, :]
    return (jnp.cos(angle)[:, None, :], jnp.sin(angle)[:, None, :])


def rotate(value, cosine, sine):
    half = value.shape[-1] // 2
    first = value[..., :half]
    second = value[..., half:]
    return jnp.concatenate(
        [first * cosine - second * sine, second * cosine + first * sine], axis=-1
    )


def unrotate(incoming, cosine, sine):
    half = incoming.shape[-1] // 2
    upper = incoming[..., :half]
    lower = incoming[..., half:]
    return jnp.concatenate([upper * cosine + lower * sine, lower * cosine - upper * sine], axis=-1)


def norm_forward(residual, gain):
    inverse = lax.rsqrt(jnp.mean(residual * residual, axis=-1, keepdims=True) + EPS)
    return ((residual * inverse * gain).astype(jnp.bfloat16), inverse)


def norm_backward(residual, inverse, gain, incoming):
    scaled = incoming * gain
    through = inverse * scaled - residual * inverse**3 * jnp.mean(
        scaled * residual, axis=-1, keepdims=True
    )
    return (through, jnp.sum(incoming * residual * inverse, axis=0))


def padded(array, axis, parts, count, full):
    if count == full:
        return array
    shape = array.shape
    split = array.reshape(shape[:axis] + (parts, count) + shape[axis + 1 :])
    pads = [(0, 0)] * split.ndim
    pads[axis + 1] = (0, full - count)
    return jnp.pad(split, pads).reshape(shape[:axis] + (parts * full,) + shape[axis + 1 :])


def trimmed(array, axis, parts, count, full):
    if count == full:
        return array
    shape = array.shape
    split = array.reshape(shape[:axis] + (parts, full) + shape[axis + 1 :])
    kept = lax.slice_in_dim(split, 0, count, axis=axis + 1)
    return kept.reshape(shape[:axis] + (parts * count,) + shape[axis + 1 :])


def plain_layer(
    layer_input, output_grad, wide, tall, norm_gains, block_order, sizes
):
    parts, width, half, kv, short, full, high = sizes
    hidden_size = 2 * half
    rows = layer_input.shape[1]
    block = rows // 2
    group = HEADS // KV_HEADS
    scale = 1.0 / math.sqrt(HEAD)
    ctx_place = lax.axis_index("ctx")
    offsets = jnp.arange(block, dtype=jnp.int32)
    own_blocks = lax.dynamic_slice_in_dim(block_order, 2 * ctx_place, 2)
    query_pos = (own_blocks[:, None] * block + offsets[None, :]).reshape(rows)
    key_pos = (block_order[:, None] * block + offsets[None, :]).reshape(-1)

    all_wide, all_tall = gather_weights(wide, tall)
    w_qk, w_ov, w_gate_0, w_gate_1, w_up_0, w_up_1 = [all_wide[i].reshape(width, half) for i in range(WIDE)]
    w_down = [all_tall[i].reshape(half, width) for i in range(2)]

    residual = layer_input[0].astype(jnp.float32)
    normed_first, inverse_first = norm_forward(residual, norm_gains[0])
    qk_pre = jnp.dot(normed_first, w_qk, preferred_element_type=jnp.float32)
    query_pre = qk_pre[:, :width].reshape(rows, HEADS, HEAD)
    key_pre = qk_pre[:, width:].reshape(rows, KV_HEADS, HEAD)
    value_low = (
        jnp.dot(normed_first, w_ov, preferred_element_type=jnp.float32)[:, width:]
        .astype(jnp.bfloat16)
        .reshape(rows, KV_HEADS, HEAD)
    )
    cosine, sine = rotary_tables(query_pos, HEAD)
    query_rot = rotate(query_pre, cosine, sine).astype(jnp.bfloat16)
    key_rot = rotate(key_pre, cosine, sine).astype(jnp.bfloat16)
    keys_all, values_all = (
        lax.all_gather(key_rot, "ctx", axis=0, tiled=True),
        lax.all_gather(value_low, "ctx", axis=0, tiled=True),
    )
    keys_head = keys_all.transpose(1, 0, 2)
    values_head = values_all.transpose(1, 0, 2)
    queries_head = (
        query_rot.reshape(rows, KV_HEADS, group, HEAD)
        .transpose(1, 2, 0, 3)
        .reshape(KV_HEADS, group * rows, HEAD)
    )
    row_pos = jnp.tile(query_pos, group)
    allowed = key_pos[None, :] <= row_pos[:, None]

    def head_forward(item):
        query, key, value = item
        scores = jnp.where(allowed, contract(query, key, 1, 1) * scale, MASKED)
        top = jnp.max(scores, axis=-1, keepdims=True)
        expo = jnp.exp(scores - top)
        total = jnp.sum(expo, axis=-1, keepdims=True)
        probs_low = (expo / total).astype(jnp.bfloat16)
        return (
            jnp.dot(probs_low, value, preferred_element_type=jnp.float32),
            (top + jnp.log(total))[:, 0],
        )

    mixed, log_total = lax.map(head_forward, (queries_head, keys_head, values_head))
    attended = (
        mixed.reshape(KV_HEADS, group, rows, HEAD)
        .transpose(2, 0, 1, 3)
        .reshape(rows, HEADS * HEAD)
        .astype(jnp.bfloat16)
    )
    w_out = w_ov[:, :width]
    middle = residual + jnp.dot(attended, w_out, preferred_element_type=jnp.float32)
    normed_second, inverse_second = norm_forward(middle, norm_gains[1])

    def sides(left, right):
        return jnp.concatenate([left, right], axis=1)

    gate = sides(
        jnp.dot(normed_second, w_gate_0, preferred_element_type=jnp.float32),
        jnp.dot(normed_second, w_gate_1, preferred_element_type=jnp.float32),
    )
    lifted = sides(
        jnp.dot(normed_second, w_up_0, preferred_element_type=jnp.float32),
        jnp.dot(normed_second, w_up_1, preferred_element_type=jnp.float32),
    )
    sigma = jax.nn.sigmoid(gate)
    hidden = (gate * sigma * lifted).astype(jnp.bfloat16)
    hidden_split = hidden.reshape(rows, parts, 2, high)
    hidden_sides = [hidden_split[:, :, i].reshape(rows, half) for i in range(2)]
    layer_output = (
        middle
        + jnp.dot(hidden_sides[0], w_down[0], preferred_element_type=jnp.float32)
        + jnp.dot(hidden_sides[1], w_down[1], preferred_element_type=jnp.float32)
    ).astype(jnp.bfloat16)
    upstream = output_grad[0]
    grad_hidden = jnp.stack(
        [contract(upstream, w_down[i], 1, 1).reshape(rows, parts, high) for i in range(2)], axis=2
    ).reshape(rows, hidden_size)
    grad_gate = (grad_hidden * lifted * sigma * (1.0 + gate * (1.0 - sigma))).astype(jnp.bfloat16)
    grad_lifted = (grad_hidden * gate * sigma).astype(jnp.bfloat16)
    grad_normed_second = (
        contract(grad_gate[:, :half], w_gate_0, 1, 1)
        + contract(grad_gate[:, half:], w_gate_1, 1, 1)
        + contract(grad_lifted[:, :half], w_up_0, 1, 1)
        + contract(grad_lifted[:, half:], w_up_1, 1, 1)
    )
    through_second, gain_second = norm_backward(
        middle, inverse_second, norm_gains[1], grad_normed_second
    )
    grad_middle = upstream.astype(jnp.float32) + through_second
    grad_branch = grad_middle.astype(jnp.bfloat16)
    grad_attended = contract(grad_branch, w_out, 1, 1).astype(jnp.bfloat16)
    grad_heads = (
        grad_attended.reshape(rows, KV_HEADS, group, HEAD)
        .transpose(1, 2, 0, 3)
        .reshape(KV_HEADS, group * rows, HEAD)
    )

    def head_backward(item):
        query, key, value, grad_out, log_row = item
        scores = jnp.where(allowed, contract(query, key, 1, 1) * scale, MASKED)
        probs = jnp.exp(scores - log_row[:, None])
        grad_value_part = contract(probs.astype(jnp.bfloat16), grad_out, 0, 0)
        grad_probs = contract(grad_out, value, 1, 1)
        grad_scores = (
            probs * (grad_probs - jnp.sum(grad_probs * probs, axis=-1, keepdims=True))
        ).astype(jnp.bfloat16)
        grad_query_part = jnp.dot(grad_scores, key, preferred_element_type=jnp.float32) * scale
        grad_key_part = contract(grad_scores, query, 0, 0) * scale
        return (grad_query_part, grad_key_part, grad_value_part)

    grad_query_rot, grad_key_all, grad_value_all = lax.map(
        head_backward, (queries_head, keys_head, values_head, grad_heads, log_total)
    )
    grad_key_own, grad_value_own = (
        lax.psum_scatter(
            grad_key_all.astype(jnp.bfloat16), "ctx", scatter_dimension=1, tiled=True
        ).astype(jnp.float32),
        lax.psum_scatter(
            grad_value_all.astype(jnp.bfloat16), "ctx", scatter_dimension=1, tiled=True
        ).astype(jnp.float32),
    )
    grad_query = (
        unrotate(
            grad_query_rot.reshape(KV_HEADS, group, rows, HEAD)
            .transpose(2, 0, 1, 3)
            .reshape(rows, HEADS, HEAD),
            cosine,
            sine,
        )
        .reshape(rows, HEADS * HEAD)
        .astype(jnp.bfloat16)
    )
    grad_key = (
        unrotate(grad_key_own.transpose(1, 0, 2), cosine, sine)
        .reshape(rows, KV_HEADS * HEAD)
        .astype(jnp.bfloat16)
    )
    grad_value = (
        grad_value_own.transpose(1, 0, 2).reshape(rows, KV_HEADS * HEAD).astype(jnp.bfloat16)
    )
    grad_qk = sides(grad_query, grad_key)
    zero_query = jnp.zeros((rows, width), jnp.bfloat16)
    grad_v = sides(zero_query, grad_value)
    grad_normed_first = contract(grad_qk, w_qk, 1, 1) + contract(grad_v, w_ov, 1, 1)
    through_first, gain_first = norm_backward(
        residual, inverse_first, norm_gains[0], grad_normed_first
    )
    input_gradient = grad_middle + through_first

    xt = jnp.stack([item.T for item in (normed_first, attended, normed_second, upstream)])
    xt = padded(xt, 1, parts, short, full)
    dy = jnp.stack(
        [
            grad_qk,
            sides(grad_branch, jnp.zeros((rows, kv), jnp.bfloat16)),
            grad_gate[:, :half],
            grad_gate[:, half:],
            grad_lifted[:, :half],
            grad_lifted[:, half:],
            hidden_sides[0],
            hidden_sides[1],
            grad_v,
        ]
    )
    gains = jnp.pad(jnp.stack([gain_first, gain_second]), ((0, 6), (0, 0)))
    return layer_output, input_gradient, xt, dy, gains


def rotation(block_order, rows):
    block = rows // 2
    ctx_place = lax.axis_index("ctx")
    offsets = jnp.arange(block, dtype=jnp.int32)
    own_blocks = lax.dynamic_slice_in_dim(block_order, 2 * ctx_place, 2)
    query_pos = (own_blocks[:, None] * block + offsets[None, :]).reshape(rows)
    key_pos = (block_order[:, None] * block + offsets[None, :]).reshape(-1)
    bias = jnp.where(key_pos[:, None] <= query_pos[None, :], 0.0, MASKED).astype(jnp.bfloat16)
    lane = jnp.arange(128, dtype=jnp.int32)
    index = (lane % (HEAD // 2)).astype(jnp.float32)
    frequency = THETA ** (-(index * 2.0 / HEAD))
    angle = query_pos.astype(jnp.float32)[:, None] * frequency[None, :]
    cosine, sine = jnp.cos(angle), jnp.sin(angle)
    early = (lane % HEAD < HEAD // 2)[None, :]
    return (cosine, jnp.where(early, 0.0, sine), jnp.where(early, -sine, 0.0)), bias


def plain_step(layer_input, output_grad, norm_gains, block_order, weights, olds, factors, sizes):
    parts, width, half, kv, short, full, high = sizes
    query_weight, key_weight, value_weight, output_weight, gate_weight, up_weight, down_weight = weights
    (
        query_momentum,
        key_momentum,
        value_momentum,
        output_momentum,
        gate_momentum,
        up_momentum,
        down_momentum,
    ) = olds

    def sides(left, right):
        return jnp.concatenate([left, right], axis=1)

    wide = jnp.stack(
        [
            jnp.concatenate([query_weight, key_weight], axis=1),
            jnp.concatenate([output_weight, value_weight], axis=1),
            gate_weight[:, :half],
            gate_weight[:, half:],
            up_weight[:, :half],
            up_weight[:, half:],
        ]
    )
    tall = down_weight.reshape(2, high, width)
    layer_output, input_gradient, xt, dy, gains = plain_layer(
        layer_input, output_grad, wide, tall, norm_gains, block_order, sizes
    )

    def pad_rows(array):
        return padded(array, 0, 1, short, full)

    def pad_columns(array):
        return padded(array, 1, parts, short, full)

    moments = (
        pad_rows(sides(query_momentum, key_momentum)),
        pad_rows(sides(output_momentum, value_momentum)),
        pad_rows(gate_momentum),
        pad_rows(up_momentum),
        pad_columns(down_momentum),
    )
    g_wide, g_tall, s_wide, s_tall, gain_sum = reduce_gradients(xt, dy, gains, moments, full, high)
    o_wide, o_tall = orthogonalize(s_wide, s_tall, full, high, width)

    def unpack(wide_pieces, tall_pieces):
        pieces = wide_pieces[:, :short]
        tall = trimmed(tall_pieces, 2, parts, short, full).reshape(2 * high, width)
        return (
            pieces[0, :, :width],
            pieces[0, :, width:],
            pieces[1, :, width:],
            pieces[1, :, :width],
            sides(pieces[2], pieces[3]),
            sides(pieces[4], pieces[5]),
            tall,
        )

    gradients = [item.astype(jnp.float32) for item in unpack(g_wide, g_tall)]
    orthos = unpack(o_wide, o_tall)
    moments = [MOMENTUM * old + new for old, new in zip(olds, gradients)]
    new_weights = [
        weight.astype(jnp.float32) + factor * ortho.astype(jnp.float32)
        for weight, factor, ortho in zip(weights, factors, orthos)
    ]
    return layer_output, input_gradient, gradients, moments, new_weights, gain_sum


def on_device(
    layer_input,
    output_grad,
    query_weight,
    key_weight,
    value_weight,
    output_weight,
    gate_weight,
    up_weight,
    down_weight,
    norm_gains,
    query_momentum,
    key_momentum,
    value_momentum,
    output_momentum,
    gate_momentum,
    up_momentum,
    down_momentum,
    gain_momentum,
    block_order,
):
    parts = lax.axis_size("fsdp")
    width = layer_input.shape[2]
    half = gate_weight.shape[1] // 2
    kv = key_weight.shape[1]
    short = width // parts
    full = -(-short // 16) * 16
    high = half // parts
    sizes = (parts, width, half, kv, short, full, high)

    weights = (query_weight, key_weight, value_weight, output_weight, gate_weight, up_weight, down_weight)
    olds = (
        query_momentum,
        key_momentum,
        value_momentum,
        output_momentum,
        gate_momentum,
        up_momentum,
        down_momentum,
    )
    factors = []
    for index, weight in enumerate(weights):
        step_rate = OUT_RATE if index == 3 else RATE
        factors.append(-step_rate * max(1.0, weight.shape[1] / (weight.shape[0] * parts)) ** 0.5)

    fused = (
        lax.axis_size("ctx") == CLASSES
        and short == full
        and parts == 4
        and half % (2 * half // parts) == 0
        and (2 * half // parts) % 128 == 0
        and layer_input.shape[1] == 128
        and short <= 256
    )
    if fused:
        tables, bias = rotation(block_order, layer_input.shape[1])

        def turned(items):
            q, k, v, o, gate, up, down = items
            return (q, k.T, o, v.T, gate, up, down.T)

        shards, moments = turned(weights), turned(olds)
        out_turned, grad_turned, g, o, gain_sum = step_pass(
            layer_input[0].T, output_grad[0].T, norm_gains, tables, bias, shards, moments
        )
        gradients, moments, new_weights = settle(g, o, moments, shards, factors)
        layer_output, input_gradient = out_turned.T, grad_turned.T
    else:
        layer_output, input_gradient, gradients, moments, new_weights, gain_sum = plain_step(
            layer_input, output_grad, norm_gains, block_order, weights, olds, factors, sizes
        )
    gain_width = norm_gains.shape[1] // parts
    place = lax.axis_index("fsdp") * gain_width
    gain_gradient = lax.dynamic_slice_in_dim(gain_sum[:2], place, gain_width, 1)
    gain_shard = lax.dynamic_slice_in_dim(norm_gains, place, gain_width, 1)
    gain_moment = MOMENTUM * gain_momentum + gain_gradient
    new_gains = gain_shard - GAIN_RATE * gain_moment
    return (
        layer_output[None],
        input_gradient[None],
        *gradients,
        gain_gradient,
        *moments,
        gain_moment,
        *new_weights,
        new_gains,
    )


def solution(mesh):
    tokens = P("fsdp", "ctx", None)
    shard = P("fsdp", None)
    gains = P(None, "fsdp")
    return jax.shard_map(
        on_device,
        mesh=mesh,
        in_specs=(tokens, tokens) + (shard,) * 7 + (P(),) + (shard,) * 7 + (gains, P()),
        out_specs=(tokens, tokens) + ((shard,) * 7 + (gains,)) * 3,
        check_vma=False,
    )
```

```python
import functools
import math

import jax
import jax.numpy as jnp
from jax import lax
from jax.experimental import pallas as pl
from jax.experimental.pallas import tpu as pltpu
from jax.sharding import PartitionSpec as P

HEADS = 15
KV_HEADS = 5
HEAD = 64
NS_ITERS = 5


EPS = 1e-05
THETA = 100000.0
NS_A = 3.4445
NS_B = -4.775
NS_C = 2.0315
MOMENTUM = 0.95
RATE = 0.2
OUT_RATE = 6.0
GAIN_RATE = 0.002
MASKED = -1e30

MESH = pl.DeviceIdType.MESH
BF16 = jnp.bfloat16
F32 = jnp.float32
ANY = pl.BlockSpec(memory_space=pl.ANY)
VMEM = pl.BlockSpec(memory_space=pltpu.VMEM)
CLASSES = 8
WIDE = 6


def contract(left, right, left_dim, right_dim):
    return lax.dot_general(
        left, right, (((left_dim,), (right_dim,)), ((), ())), preferred_element_type=jnp.float32
    )


class Place:
    def __init__(self):
        self.parts = lax.axis_size("fsdp")
        self.extra = lax.axis_size("ctx") // CLASSES
        self.c = lax.axis_index("ctx")
        self.f = lax.axis_index("fsdp")
        self.p = lax.rem(self.c, CLASSES)
        self.core = lax.rem(self.c, 2)
        self.b1 = jnp.where(self.core == 0, 2, 4)
        self.b2 = jnp.where(self.core == 0, 4, 2)

    def peer(self, bits):
        return (self.c ^ bits, self.f)

    def along(self, j):
        return (self.c, self.f ^ j)

    def other(self, j):
        groups = self.extra
        return (lax.rem(self.c + CLASSES * j, CLASSES * groups), self.f)

    def barrier(self, bits=(1, 2, 4), line=True, others=False):
        sem = pltpu.get_barrier_semaphore()
        targets = [self.peer(b) for b in bits]
        if line:
            targets += [self.along(j) for j in range(1, self.parts)]
        if others:
            targets += [self.other(j) for j in range(1, self.extra)]
        for target in targets:
            pl.semaphore_signal(sem, inc=1, device_id=target, device_id_type=MESH)
        pl.semaphore_wait(sem, len(targets))


def remote(src, dst, send, recv, target):
    return pltpu.make_async_remote_copy(
        src_ref=src, dst_ref=dst, send_sem=send, recv_sem=recv, device_id=target, device_id_type=MESH
    )


def by_kind(cls, wide, tall):
    pl.when(cls < WIDE)(wide)
    pl.when(cls >= WIDE)(tall)


def weights_kernel(in_a, in_b, out_a, out_b, local, zs, s1, s2, sc, recv):
    at = Place()
    p, f, parts = at.p, at.f, at.parts
    at.barrier()
    copies = [
        pltpu.make_async_copy(in_a, out_a.at[:, f], local.at[0]),
        pltpu.make_async_copy(in_b, out_b.at[:, f], local.at[1]),
    ]
    for copy in copies:
        copy.start()

    def act(cls, j, g, send, target, what, first=False):
        def wide():
            dst = out_a.at[cls, g]
            src = in_a.at[cls] if first else dst
            getattr(remote(src, dst, send, recv.at[cls, j], target), what)()

        def tall():
            dst = out_b.at[cls - WIDE, g]
            src = in_b.at[cls - WIDE] if first else dst
            getattr(remote(src, dst, send, recv.at[cls, j], target), what)()

        by_kind(cls, wide, tall)

    sends = []

    def send(cls, j, g, sem, target, first=False):
        act(cls, j, g, sem, target, "start", first)
        sends.append((cls, j, g, sem, target, first))

    def arrived(cls, j):
        act(cls, j, f ^ j, zs.at[j], at.along(j), "wait_recv")

    for j in range(1, parts):
        send(p, j, f, zs.at[j], at.along(j), True)
    for j in range(1, parts):
        arrived(p, j)
        send(p, j, f ^ j, s1.at[0, j], at.peer(at.b1))
        send(p, j, f ^ j, s2.at[0, j], at.peer(at.b2))
        send(p, j, f ^ j, sc.at[0, j], at.peer(1))
    for j in range(1, parts):
        arrived(p ^ at.b1, j)
        send(p ^ at.b1, j, f ^ j, s2.at[1, j], at.peer(at.b2))
        send(p ^ at.b1, j, f ^ j, sc.at[1, j], at.peer(1))
    for slot, bits in ((2, at.b2), (3, at.b1 ^ at.b2)):
        for j in range(1, parts):
            arrived(p ^ bits, j)
            send(p ^ bits, j, f ^ j, sc.at[slot, j], at.peer(1))
    for bits in (1, 3, 5, 7):
        for j in range(1, parts):
            arrived(p ^ bits, j)
    for cls, j, g, sem, target, first in sends:
        act(cls, j, g, sem, target, "wait_send", first)
    for copy in copies:
        copy.wait()


def gather_weights(wide, tall):
    parts = lax.axis_size("fsdp")
    dma = pltpu.SemaphoreType.DMA
    return pl.pallas_call(
        weights_kernel,
        out_shape=(
            jax.ShapeDtypeStruct((WIDE, parts) + wide.shape[1:], BF16),
            jax.ShapeDtypeStruct((CLASSES - WIDE, parts) + tall.shape[1:], BF16),
        ),
        in_specs=[ANY, ANY],
        out_specs=(ANY, ANY),
        scratch_shapes=[
            dma((2,)),
            dma((parts,)),
            dma((1, parts)),
            dma((2, parts)),
            dma((4, parts)),
            dma((CLASSES, parts)),
        ],
        compiler_params=pltpu.CompilerParams(collective_id=0, has_side_effects=True),
        name="gather_weights",
    )(wide, tall)


def spread(at, own_a, own_b, out_a, out_b, local, ss, recv):
    p = at.p

    def act(cls, sem, target, what, first=False):
        def wide():
            dst = out_a.at[cls]
            getattr(remote(own_a if first else dst, dst, sem, recv.at[cls], target), what)()

        def tall():
            dst = out_b.at[cls - WIDE]
            getattr(remote(own_b if first else dst, dst, sem, recv.at[cls], target), what)()

        by_kind(cls, wide, tall)

    def keep(what):
        def wide():
            getattr(pltpu.make_async_copy(own_a, out_a.at[p], local), what)()

        def tall():
            getattr(pltpu.make_async_copy(own_b, out_b.at[p - WIDE], local), what)()

        by_kind(p, wide, tall)

    sends = []

    def send(cls, slot, target, first=False):
        act(cls, ss.at[slot], target, "start", first)
        sends.append((cls, slot, target, first))

    def arrived(cls):
        act(cls, ss.at[0], at.peer(1), "wait_recv")

    send(p, 0, at.peer(at.b1), True)
    send(p, 1, at.peer(at.b2), True)
    send(p, 2, at.peer(1), True)
    keep("start")

    def finish():
        arrived(p ^ at.b1)
        send(p ^ at.b1, 3, at.peer(at.b2))
        send(p ^ at.b1, 4, at.peer(1))
        arrived(p ^ at.b2)
        send(p ^ at.b2, 5, at.peer(1))
        arrived(p ^ at.b1 ^ at.b2)
        send(p ^ at.b1 ^ at.b2, 6, at.peer(1))
        for bits in (1, 3, 5, 7):
            arrived(p ^ bits)
        for cls, slot, target, first in sends:
            act(cls, ss.at[slot], target, "wait_send", first)
        keep("wait")

    return finish


def reduce_kernel(
    parts, extra, high,
    xt_in, dy_in, gain_in, m_qk, m_ov, m_gate, m_up, m_down,
    g_a, g_b, s_a, s_b, gain_out,
    xt, dy, p1s, p1r, p2s, p2r, own, own_t, za_s, za_r, zb_s, zb_r, ma, mb, ga, gb, sa, sb, es, er, gain_s, gain_r,
    ls, xs, xr, s1, r1, s2, r2, zs, zr, esem, ersem, msem, gs, gr, ag_l, ag_s, ag_r, ss, sr, sl,
):
    at = Place()
    p, f, core = at.p, at.f, at.core
    tokens = xt_in.shape[2]
    rows = ma.shape[0]
    half = dy.shape[2]

    def moment(what):
        for cls in range(CLASSES):
            @pl.when(p == cls)
            def _(cls=cls):
                side = cls % 2
                if cls < 2:
                    src, dst = (m_qk, m_ov)[cls], ma
                elif cls < WIDE:
                    whole = m_gate if cls < 4 else m_up
                    src, dst = whole.at[:, pl.ds(side * half, half)], ma
                else:
                    src, dst = m_down.at[pl.ds(side * high, high)], mb
                getattr(pltpu.make_async_copy(src, dst, msem), what)()

    moment("start")
    mine = [pltpu.make_async_copy(xt_in, xt.at[:, :, pl.ds(0, tokens)], ls.at[0])]
    for slot in range(4):
        mine.append(
            pltpu.make_async_copy(dy_in.at[core + 2 * slot], dy.at[slot, pl.ds(0, tokens)], ls.at[1 + slot])
        )
    mine.append(pltpu.make_async_copy(dy_in.at[8], dy.at[4, pl.ds(0, tokens)], ls.at[5]))
    for copy in mine:
        copy.start()
    at.barrier(others=True)
    pair = at.peer(1)
    theirs = [remote(xt_in, xt.at[:, :, pl.ds(tokens, tokens)], xs.at[0], xr.at[0], pair)]
    for slot in range(4):
        theirs.append(
            remote(dy_in.at[1 - core + 2 * slot], dy.at[slot, pl.ds(tokens, tokens)], xs.at[1 + slot], xr.at[1 + slot], pair)
        )
    theirs.append(remote(dy_in.at[8], dy.at[4, pl.ds(tokens, tokens)], xs.at[5], xr.at[5], pair))
    for copy in theirs:
        copy.start()

    def swap(slot, target):
        return remote(gain_s.at[slot], gain_r.at[slot], gs.at[slot], gr.at[slot], target)

    gain_s[0] = gain_in[...]
    swaps = [swap(0, pair)]
    swaps[0].start()
    for copy in mine:
        copy.wait()
    for copy in theirs:
        copy.wait()

    def term(cls, r):
        at_rows = pl.ds(pl.multiple_of(r * rows, rows), rows)
        slot = lax.div(cls, 2)
        kind = jnp.where(cls == 0, 0, jnp.where(cls == 1, 1, jnp.where(cls < WIDE, 2, 3)))
        value = jnp.dot(xt[kind, at_rows, :], dy[slot], preferred_element_type=F32)
        return value

    def with_values(cls, r, put):
        at_rows = pl.ds(pl.multiple_of(r * rows, rows), rows)

        @pl.when(cls == 1)
        def _():
            put(term(cls, r) + jnp.dot(xt[0, at_rows, :], dy[4], preferred_element_type=F32))

        @pl.when(cls != 1)
        def _():
            put(term(cls, r))

    def order(i):
        return lax.rem(f + 1 + i, parts)

    def one(slot, i):
        r = order(i)
        return remote(p1s.at[slot, r], p1r.at[slot, r], s1.at[slot, r], r1.at[slot, r], at.peer(at.b1))

    for slot, bits in ((0, at.b1 ^ at.b2), (1, at.b1)):
        def first(i, carry, slot=slot, bits=bits):
            r = order(i)

            def put(value):
                p1s[slot, r] = value.astype(BF16)

            with_values(p ^ bits, r, put)
            one(slot, i).start()
            return carry

        lax.fori_loop(0, parts, first, 0)

    swaps[0].wait()
    gain_s[1] = gain_s[0] + gain_r[0]
    swaps.append(swap(1, at.peer(2)))
    swaps[1].start()

    def two(i):
        r = order(i)
        return remote(p2s.at[r], p2r.at[r], s2.at[r], r2.at[r], at.peer(at.b2))

    def second(i, carry):
        r = order(i)
        one(0, i).wait_recv()

        def put(value):
            p2s[r] = (value + p1r[0, r].astype(F32)).astype(BF16)

        with_values(p ^ at.b2, r, put)
        two(i).start()
        return carry

    lax.fori_loop(0, parts, second, 0)
    swaps[1].wait()
    gain_s[2] = gain_s[1] + gain_r[1]
    swaps.append(swap(2, at.peer(4)))
    swaps[2].start()

    def line_a(r, source):
        return remote(za_s.at[r], za_r.at[source], zs.at[r], zr.at[source], (at.c, r))

    def line_b(r, source):
        return remote(
            zb_s.at[pl.ds(pl.multiple_of(r * high, high), high)],
            zb_r.at[source], zs.at[r], zr.at[source], (at.c, r),
        )

    early = extra == 1

    def third(i, carry):
        r = order(i)
        one(1, i).wait_recv()
        two(i).wait_recv()

        def put(value):
            total = value + p1r[1, r].astype(F32) + p2r[r].astype(F32)
            own[r] = total
            if early:
                za_s[r] = total.astype(BF16)

        with_values(p, r, put)
        if early:
            @pl.when((p < WIDE) & (i < parts - 1))
            def _():
                line_a(r, f).start()
        return carry

    lax.fori_loop(0, parts, third, 0)
    swaps[2].wait()
    gain_s[3] = gain_s[2] + gain_r[2]

    if not early:
        es[...] = own[...].astype(BF16)
        group = [
            remote(es, er.at[j - 1], esem.at[j - 1], ersem.at[j - 1], at.other(j)) for j in range(1, extra)
        ]
        for copy in group:
            copy.start()
        for j in range(1, extra):
            group[j - 1].wait_recv()
            own[...] = own[...] + er[j - 1].astype(F32)
        for copy in group:
            copy.wait_send()
        za_s[...] = own[...].astype(BF16)

        @pl.when(p < WIDE)
        def _():
            for j in range(1, parts):
                line_a(f ^ j, f).start()

    @pl.when(p >= WIDE)
    def _():
        for tile in range(half // 128):
            for r in range(parts):
                block = own[r, :, pl.ds(tile * 128, 128)]
                if rows % 128 == 0:
                    own_t[pl.ds(tile * 128, 128), pl.ds(r * rows, rows)] = block.T
            if rows % 128 != 0:
                column = own[:, :, pl.ds(tile * 128, 128)].reshape(parts * rows, 128)
                own_t[pl.ds(tile * 128, 128), :] = column.T
        zb_s[...] = own_t[...].astype(BF16)
        for j in range(1, parts):
            line_b(f ^ j, f).start()

    line_gain = [
        remote(gain_s.at[3], gain_r.at[3 + j], gs.at[3 + j], gr.at[3 + j], at.along(j)) for j in range(1, parts)
    ]
    other_gain = []
    for copy in line_gain:
        copy.start()

    moment("wait")

    @pl.when(p < WIDE)
    def _():
        total = own[f]
        for j in range(1, parts):
            line_a(f ^ j, f ^ j).wait_recv()
            total = total + za_r[f ^ j].astype(F32)
        ga[...] = total.astype(BF16)
        sa[...] = (MOMENTUM * ma[...] + total).astype(BF16)

    @pl.when(p >= WIDE)
    def _():
        total = own_t[pl.ds(pl.multiple_of(f * high, high), high), :]
        for j in range(1, parts):
            line_b(f ^ j, f ^ j).wait_recv()
            total = total + zb_r[f ^ j].astype(F32)
        gb[...] = total.astype(BF16)
        sb[...] = (MOMENTUM * mb[...] + total).astype(BF16)

    def share_a(j, source):
        return remote(sa, s_a.at[pl.ds(pl.multiple_of(source * rows, rows), rows)], ss.at[j], sr.at[j], at.along(j))

    def share_b(j, source):
        return remote(sb, s_b.at[pl.ds(pl.multiple_of(source * high, high), high)], ss.at[j], sr.at[j], at.along(j))

    @pl.when(p < WIDE)
    def _():
        for j in range(1, parts):
            share_a(j, f).start()
        pltpu.make_async_copy(sa, s_a.at[pl.ds(pl.multiple_of(f * rows, rows), rows)], sl).start()

    @pl.when(p >= WIDE)
    def _():
        for j in range(1, parts):
            share_b(j, f).start()
        pltpu.make_async_copy(sb, s_b.at[pl.ds(pl.multiple_of(f * high, high), high)], sl).start()

    finish = spread(at, ga, gb, g_a, g_b, ag_l, ag_s, ag_r)
    total = gain_s[3]
    for j in range(1, parts):
        line_gain[j - 1].wait()
        total = total + gain_r[3 + j]
    if extra > 1:
        gain_s[4] = total
        other_gain = [
            remote(gain_s.at[4], gain_r.at[3 + parts + j], gs.at[3 + parts + j], gr.at[3 + parts + j], at.other(j))
            for j in range(1, extra)
        ]
        for copy in other_gain:
            copy.start()
        for j in range(1, extra):
            other_gain[j - 1].wait()
            total = total + gain_r[3 + parts + j]
    gain_out[...] = total
    finish()

    for slot in range(2):
        lax.fori_loop(0, parts, lambda i, carry, slot=slot: (one(slot, i).wait_send(), carry)[1], 0)
    lax.fori_loop(0, parts, lambda i, carry: (two(i).wait_send(), carry)[1], 0)

    @pl.when(p < WIDE)
    def _():
        for j in range(1, parts):
            line_a(f ^ j, f).wait_send()
            share_a(j, f).wait_send()
            share_a(j, f ^ j).wait_recv()
        pltpu.make_async_copy(sa, s_a.at[pl.ds(pl.multiple_of(f * rows, rows), rows)], sl).wait()

    @pl.when(p >= WIDE)
    def _():
        for j in range(1, parts):
            line_b(f ^ j, f).wait_send()
            share_b(j, f).wait_send()
            share_b(j, f ^ j).wait_recv()
        pltpu.make_async_copy(sb, s_b.at[pl.ds(pl.multiple_of(f * high, high), high)], sl).wait()


def reduce_gradients(xt, dy, gains, moments, rows, high):
    parts = lax.axis_size("fsdp")
    extra = lax.axis_size("ctx") // CLASSES
    kinds, depth, tokens = xt.shape
    half = dy.shape[2]
    dma = pltpu.SemaphoreType.DMA
    vm = pltpu.VMEM
    n_gain = 4 + parts + extra
    group = max(extra - 1, 1)
    spare = (parts, rows, half) if extra > 1 else (1, 16, 128)
    return pl.pallas_call(
        functools.partial(reduce_kernel, parts, extra, high),
        out_shape=(
            jax.ShapeDtypeStruct((WIDE, rows, half), BF16),
            jax.ShapeDtypeStruct((CLASSES - WIDE, high, depth), BF16),
            jax.ShapeDtypeStruct((depth, half), BF16),
            jax.ShapeDtypeStruct((half, depth), BF16),
            jax.ShapeDtypeStruct(gains.shape, F32),
        ),
        in_specs=[ANY, ANY, VMEM] + [ANY] * 5,
        out_specs=(ANY, ANY, ANY, ANY, VMEM),
        scratch_shapes=[
            vm((kinds, depth, 2 * tokens), BF16),
            vm((5, 2 * tokens, half), BF16),
            vm((2, parts, rows, half), BF16),
            vm((2, parts, rows, half), BF16),
            vm((parts, rows, half), BF16),
            vm((parts, rows, half), BF16),
            vm((parts, rows, half), F32),
            vm((half, depth), F32),
            vm((parts, rows, half), BF16),
            vm((parts, rows, half), BF16),
            vm((half, depth), BF16),
            vm((parts, high, depth), BF16),
            vm((rows, half), F32),
            vm((high, depth), F32),
            vm((rows, half), BF16),
            vm((high, depth), BF16),
            vm((rows, half), BF16),
            vm((high, depth), BF16),
            vm(spare, BF16),
            vm((group,) + spare, BF16),
            vm((5,) + gains.shape, F32),
            vm((n_gain,) + gains.shape, F32),
            dma((6,)), dma((6,)), dma((6,)),
            dma((2, parts)), dma((2, parts)), dma((parts,)), dma((parts,)), dma((parts,)), dma((parts,)),
            dma((group,)), dma((group,)), dma, dma((n_gain,)), dma((n_gain,)),
            dma, dma((7,)), dma((CLASSES,)), dma((parts,)), dma((parts,)), dma,
        ],
        compiler_params=pltpu.CompilerParams(
            collective_id=1, has_side_effects=True, vmem_limit_bytes=62 << 20
        ),
        name="reduce_gradients",
    )(xt, dy, gains, *moments)


def rounded(value):
    return value.astype(BF16)


def poly_rows(g, row_start, count):
    block = g[pl.ds(row_start, count), :]
    return rounded(NS_B * block.astype(F32) + NS_C * jnp.dot(block, g[...], preferred_element_type=F32))


def ortho_kernel(
    parts, rows, high, narrow,
    s_a, s_b, o_a, o_b,
    x, x_t, gs, gr, g, poly, sq, sq_r, pa, pb, kt,
    gsem, rsem, qs, qr, ag_l, ag_s, ag_r,
):
    at = Place()
    p, f = at.p, at.f
    depth, half = x.shape
    step = depth // 4
    at.barrier(line=False)
    pair = at.peer(1)

    @pl.when(p < WIDE)
    def _():
        x[...] = s_a[...]

    @pl.when(p >= WIDE)
    def _():
        for tile in range(half // 128):
            x[:, pl.ds(tile * 128, 128)] = s_b[pl.ds(tile * 128, 128), :].T

    def scale_of(total):
        return 1.0 / (jnp.sqrt(total) + 1e-07)

    def normal(ref, inverse):
        ref[...] = rounded(ref[...].astype(F32) * inverse)

    def exchange(slot, r):
        chunk = pl.ds(r * step, step)
        return remote(gs.at[chunk], gr.at[slot, chunk], gsem.at[r], rsem.at[slot, r], pair)

    def fill_poly():
        for r in range(4):
            poly[pl.ds(r * step, step), :] = poly_rows(g, r * step, step)

    my_rows = pl.ds(pl.multiple_of(f * rows, rows), rows)
    my_high = pl.ds(pl.multiple_of(f * high, high), high)

    @pl.when(p >= 2)
    def _():
        wide = x[...].astype(F32)
        sq[...] = jnp.broadcast_to(jnp.sum(wide * wide), sq.shape)
        copy = remote(sq, sq_r, qs, qr, pair)
        copy.start()
        copy.wait()
        normal(x, scale_of(sq[...] + sq_r[...])[:1, :1])

        def grams(slot):
            for r in range(4):
                gs[pl.ds(r * step, step), :] = rounded(contract(x[pl.ds(r * step, step), :], x[...], 1, 1))
                exchange(slot, r).start()
            for r in range(4):
                chunk = pl.ds(r * step, step)
                exchange(slot, r).wait()
                g[chunk, :] = rounded(gs[chunk, :].astype(F32) + gr[slot, chunk, :].astype(F32))

        def iterate(it, carry):
            grams(lax.rem(it, 2))
            fill_poly()
            for tile in range(half // 256):
                block = pl.ds(tile * 256, 256)
                x[:, block] = rounded(
                    NS_A * x[:, block].astype(F32) + jnp.dot(poly[...], x[:, block], preferred_element_type=F32)
                )
            return carry

        lax.fori_loop(0, NS_ITERS - 1, iterate, 0)
        grams((NS_ITERS - 1) % 2)

        @pl.when(p < WIDE)
        def _():
            mine = poly_rows(g, pl.multiple_of(f * rows, rows), rows)
            pa[...] = rounded(NS_A * x[my_rows, :].astype(F32) + jnp.dot(mine, x[...], preferred_element_type=F32))

        @pl.when(p >= WIDE)
        def _():
            fill_poly()
            for tile in range(half // 128):
                x_t[pl.ds(tile * 128, 128), :] = x[:, pl.ds(tile * 128, 128)].T
            block = x_t[my_high, :]
            pb[...] = rounded(NS_A * block.astype(F32) + jnp.dot(block, poly[...], preferred_element_type=F32))

    @pl.when(p < 2)
    def _():
        kt[...] = x[:, narrow:].T
        inverse_k = scale_of(jnp.sum(jnp.square(kt[...].astype(F32))))
        normal(kt, inverse_k)
        wide = x[:, :narrow].astype(F32)
        x[:, :narrow] = rounded(wide * scale_of(jnp.sum(wide * wide)))

        def narrow_step(it, carry):
            gram = rounded(contract(kt[...], kt[...], 1, 1))
            turn = rounded(NS_B * gram.astype(F32) + NS_C * jnp.dot(gram, gram, preferred_element_type=F32))
            kt[...] = rounded(NS_A * kt[...].astype(F32) + jnp.dot(turn, kt[...], preferred_element_type=F32))
            return carry

        lax.fori_loop(0, NS_ITERS, narrow_step, 0)

        def gram_of():
            for r in range(4):
                chunk = pl.ds(r * step, step)
                g[chunk, :] = rounded(contract(x[chunk, :narrow], x[:, :narrow], 1, 1))

        def square_step(it, carry):
            gram_of()
            fill_poly()
            x[:, :narrow] = rounded(
                NS_A * x[:, :narrow].astype(F32) + jnp.dot(poly[...], x[:, :narrow], preferred_element_type=F32)
            )
            return carry

        lax.fori_loop(0, NS_ITERS - 1, square_step, 0)
        gram_of()
        mine = poly_rows(g, pl.multiple_of(f * rows, rows), rows)
        square = rounded(
            NS_A * x[my_rows, :narrow].astype(F32) + jnp.dot(mine, x[:, :narrow], preferred_element_type=F32)
        )
        x[:, narrow:] = kt[...].T
        pa[:, :narrow] = square
        pa[:, narrow:] = x[my_rows, narrow:]

    spread(at, pa, pb, o_a, o_b, ag_l, ag_s, ag_r)()


def orthogonalize(s_a, s_b, rows, high, narrow):
    parts = lax.axis_size("fsdp")
    depth, half = s_a.shape
    dma = pltpu.SemaphoreType.DMA
    vm = pltpu.VMEM
    return pl.pallas_call(
        functools.partial(ortho_kernel, parts, rows, high, narrow),
        out_shape=(
            jax.ShapeDtypeStruct((WIDE, rows, half), BF16),
            jax.ShapeDtypeStruct((CLASSES - WIDE, high, depth), BF16),
        ),
        in_specs=[VMEM, VMEM],
        out_specs=(ANY, ANY),
        scratch_shapes=[
            vm((depth, half), BF16),
            vm((half, depth), BF16),
            vm((depth, depth), BF16),
            vm((2, depth, depth), BF16),
            vm((depth, depth), BF16),
            vm((depth, depth), BF16),
            vm((8, 128), F32),
            vm((8, 128), F32),
            vm((rows, half), BF16),
            vm((high, depth), BF16),
            vm((half - narrow, depth), BF16),
            dma((4,)), dma((2, 4)), dma, dma, dma, dma((7,)), dma((CLASSES,)),
        ],
        compiler_params=pltpu.CompilerParams(
            collective_id=2, has_side_effects=True, vmem_limit_bytes=62 << 20
        ),
        name="orthogonalize",
    )(s_a, s_b)


class Weights:
    def __init__(self, at, sources, homes, zs, s1, s2, sc, recv):
        self.at, self.sources, self.homes = at, sources, homes
        self.zs, self.s1, self.s2, self.sc, self.recv = zs, s1, s2, sc, recv
        self.sends = []
        self.done = 0

    def act(self, group, q, j, plane, send, target, what, first=False):
        recv = self.recv.at[group, q, j]
        home, source = self.homes[group], self.sources[group]
        rows = home.shape[-2] // (1 if group == 3 else self.at.parts)
        unit = -(-rows // (16 * CLASSES)) * 16
        last = rows - (CLASSES - 1) * unit

        def piece(count):
            def go():
                start = pl.multiple_of(q * unit, 16)
                if group == 3:
                    columns = home.shape[1] // self.at.parts
                    dst = home.at[pl.ds(start, count), pl.ds(pl.multiple_of(plane * columns, 128), columns)]
                    src = source.at[pl.ds(start, count)]
                elif group == 0:
                    dst = home.at[:, pl.ds(pl.multiple_of(plane * rows + start, 16), count)]
                    src = dst
                else:
                    dst = home.at[pl.ds(pl.multiple_of(plane * rows + start, 16), count)]
                    src = source.at[pl.ds(start, count)]
                getattr(remote(src if first else dst, dst, send, recv, target), what)()

            return go

        pl.when(q < CLASSES - 1)(piece(unit))
        pl.when(q == CLASSES - 1)(piece(last))

    def send(self, group, q, j, plane, sem, target, first=False):
        self.act(group, q, j, plane, sem, target, "start", first)
        self.sends.append((group, q, j, plane, sem, target, "wait_send", first))

    def arrived(self, group, q, j):
        at = self.at
        self.act(group, q, j, at.f ^ j, self.zs.at[group, j], at.peer(1), "wait_recv")

    def along(self, group):
        at = self.at
        for j in range(1, at.parts):
            self.send(group, at.p, j, at.f, self.zs.at[group, j], at.along(j), True)

    def first(self, group, j):
        at = self.at
        self.arrived(group, at.p, j)
        self.send(group, at.p, j, at.f ^ j, self.s1.at[group, j], at.peer(at.b1))
        self.send(group, at.p, j, at.f ^ j, self.s2.at[group, 0, j], at.peer(at.b2))
        self.send(group, at.p, j, at.f ^ j, self.sc.at[group, 0, j], at.peer(1))

    def second(self, group, j):
        at = self.at
        q = at.p ^ at.b1
        self.arrived(group, q, j)
        self.send(group, q, j, at.f ^ j, self.s2.at[group, 1, j], at.peer(at.b2))
        self.send(group, q, j, at.f ^ j, self.sc.at[group, 1, j], at.peer(1))

    def third(self, group, j):
        at = self.at
        for slot, bits in ((2, at.b2), (3, at.b1 ^ at.b2)):
            self.arrived(group, at.p ^ bits, j)
            self.send(group, at.p ^ bits, j, at.f ^ j, self.sc.at[group, slot, j], at.peer(1))

    def advance(self, count):
        each = self.at.parts - 1
        total = 4 * each
        count = max(count, 0)
        for n in range(self.done, min(self.done + count, total + 2)):
            for lag, act in ((0, self.first), (1, self.second), (2, self.third)):
                if 0 <= n - lag < total:
                    act((n - lag) // each, (n - lag) % each + 1)
        self.done += count

    def ready(self, group):
        at = self.at
        for bits in (1, 3, 5, 7):
            for j in range(1, at.parts):
                self.arrived(group, at.p ^ bits, j)

    def finish(self):
        for item in self.sends:
            self.act(*item)


def spread_even(at, own, out, local, ss, recv):
    p = at.p

    def copy_of(cls, slot, target, first=False):
        return remote(own if first else out.at[cls], out.at[cls], ss.at[slot], recv.at[cls], target)

    keep = pltpu.make_async_copy(own, out.at[p], local)
    b1, b2 = at.b1, at.b2
    own_sends = [(p, 0, b1, True), (p, 1, b2, True), (p, 2, 1, True)]
    steps = (
        (p ^ b1, [(p ^ b1, 3, b2, False), (p ^ b1, 4, 1, False)]),
        (p ^ b2, [(p ^ b2, 5, 1, False)]),
        (p ^ b1 ^ b2, [(p ^ b1 ^ b2, 6, 1, False)]),
    )

    def move(cls, slot, bits, first):
        return copy_of(cls, slot, at.peer(bits), first)

    def arrived(cls):
        copy_of(cls, 0, at.peer(1)).wait_recv()

    def begin():
        for item in own_sends:
            move(*item).start()
        keep.start()

    def step(k):
        cls, sends = steps[k]
        arrived(cls)
        for item in sends:
            move(*item).start()

    def finish():
        for bits in (1, 3, 5, 7):
            arrived(p ^ bits)
        for item in own_sends + [item for _, sends in steps for item in sends]:
            move(*item).wait_send()
        keep.wait()

    return begin, step, finish


def step_kernel(
    x_ref, up_ref, gains_ref, cos_ref, low_ref, high_ref, bias_ref, wq, wk, wo, wv, wg_in, wu_in, wd_in,
    m_q, m_k, m_o, m_v, m_gate, m_up, m_down,
    out_ref, grad_ref, g_out, o_out, gain_out,
    w01, wg, wu, wd, probs, kv, rot, dkv, c4r, c2r, c1r, att, gate, lifted,
    xt_in, dy_in, dv_in, xf_all, xa_all, yf_all, yv_all, za_r, ma, mq, mk, gain_s, gain_r, sq, sq_r,
    local, zs, s1, s2, sc, recv, kvs, kvr, ds, dr,
    ls, xs, xr, ps, pr, ys, yr, as_, ar, vs, vr, hs, hr, ozs, ozr, msem, gs, gr, ag_l, ag_s, ag_r, ls_l, ls_r, lr_l, lr_r,
    gsem, rsem, qs, qr, ex_s, ex_r, fx_s, fx_r, og_l, og_s, og_r, free,
):
    at = Place()
    p, f, core, parts = at.p, at.f, at.core, at.parts
    width, tokens = x_ref.shape
    half = w01.shape[2]
    keys = half - width
    group = HEADS // KV_HEADS
    scale = 1.0 / math.sqrt(HEAD)
    rows = width // parts
    columns = 2 * half // parts
    tall = width // 2
    pair = at.peer(1)
    my_rows = pl.ds(pl.multiple_of(f * rows, 16), rows)

    weights = Weights(at, (None, wg_in, wu_in, wd_in), (w01, wg, wu, wd), zs, s1, s2, sc, recv)
    keep = [
        pltpu.make_async_copy(wg_in, wg.at[my_rows], local.at[0]),
        pltpu.make_async_copy(wu_in, wu.at[my_rows], local.at[1]),
        pltpu.make_async_copy(
            wd_in, wd.at[:, pl.ds(pl.multiple_of(f * columns, 128), columns)], local.at[2]
        ),
    ]

    def moment(what):
        for cls in range(CLASSES):
            @pl.when(p == cls)
            def _(cls=cls):
                side = cls % 2
                if cls < 2:
                    pairs = [((m_q, m_o)[cls], mq, 0), ((m_k, m_v)[cls], mk, 1)]
                elif cls < WIDE:
                    whole = m_gate if cls < 4 else m_up
                    pairs = [(whole.at[:, pl.ds(side * half, half)], ma, 0)]
                else:
                    pairs = [
                        (
                            m_down.at[pl.ds(side * tall + t * rows, rows)],
                            ma.at[:, pl.ds(t * columns, columns)],
                            t,
                        )
                        for t in range(2)
                    ]
                for src, dst, index in pairs:
                    getattr(pltpu.make_async_copy(src, dst, msem.at[index]), what)()

    w01[0, my_rows, :width] = wq[...]
    w01[0, my_rows, width:] = wk[...].T
    w01[1, my_rows, :width] = wo[...]
    w01[1, my_rows, width:] = wv[...].T
    at.barrier(bits=range(1, CLASSES))
    for index in range(4):
        weights.along(index)
    for copy in keep:
        copy.start()
    moment("start")

    residual = x_ref[...].astype(F32).T
    upstream = up_ref[...].astype(F32).T
    inverse_first = lax.rsqrt(jnp.mean(residual * residual, axis=-1, keepdims=True) + EPS)
    normed_first = (residual * inverse_first * gains_ref[0:1, :]).astype(BF16)
    xt_in[0] = normed_first.T
    xt_in[3] = up_ref[...]

    each = parts - 1
    weights.advance(each + 2)
    weights.ready(0)

    def turn(value, sign):
        tiles = []
        for tile in range(half // 128):
            part = value[:, tile * 128 : (tile + 1) * 128]
            swapped = pltpu.roll(part, HEAD // 2, 1) * low_ref[...] + pltpu.roll(part, 128 - HEAD // 2, 1) * high_ref[...]
            tiles.append(part * cos_ref[...] + swapped if sign > 0 else part * cos_ref[...] - swapped)
        return tiles

    qk = jnp.dot(normed_first, w01[0], preferred_element_type=F32)
    for tile, value in enumerate(turn(qk, 1)):
        rot[:, tile * 128 : (tile + 1) * 128] = value.astype(BF16)
    values = jnp.dot(normed_first, w01[1, :, width:], preferred_element_type=F32).astype(BF16)
    kv[p, :, :keys] = rot[:, width:]
    kv[p, :, keys:] = values

    def block(q, slot, target):
        return remote(kv.at[q], kv.at[q], kvs.at[slot], kvr.at[q], target)

    sent = [block(p, 0, at.peer(at.b1)), block(p, 1, at.peer(at.b2)), block(p, 2, at.peer(1))]
    for copy in sent:
        copy.start()

    def pass_keys(q, slots):
        block(q, 0, at.peer(1)).wait_recv()
        for slot, target in slots:
            copy = block(q, slot, target)
            copy.start()
            sent.append(copy)

    weights.advance(1)
    pass_keys(p ^ at.b1, [(3, at.peer(at.b2)), (4, at.peer(1))])
    pass_keys(p ^ at.b2, [(5, at.peer(1))])
    weights.advance(1)
    pass_keys(p ^ at.b1 ^ at.b2, [(6, at.peer(1))])
    for bits in (1, 3, 5, 7):
        pass_keys(p ^ bits, [])
    weights.advance(1)

    def keys_of(g):
        return kv[:, :, g * HEAD : (g + 1) * HEAD].reshape(CLASSES * tokens, HEAD)

    def values_of(g):
        return kv[:, :, keys + g * HEAD : keys + (g + 1) * HEAD].reshape(CLASSES * tokens, HEAD)

    def heads_of(ref, g):
        return jnp.concatenate([ref[:, h * HEAD : (h + 1) * HEAD] for h in range(g * group, (g + 1) * group)], axis=0)

    def attend(g):
        scores = contract(keys_of(g), heads_of(rot, g), 1, 1) * scale
        bias = bias_ref[...].astype(F32)
        scores = scores + jnp.concatenate([bias] * group, axis=1)
        top = jnp.max(scores, axis=0, keepdims=True)
        expo = jnp.exp(scores - top)
        total = jnp.sum(expo, axis=0, keepdims=True)
        chance = expo * (1.0 / total)
        probs[g] = chance
        mixed = contract(values_of(g), chance.astype(BF16), 0, 0)
        turned = mixed.T.astype(BF16)
        for h in range(group):
            at_lane = (g * group + h) * HEAD
            att[:, at_lane : at_lane + HEAD] = turned[h * tokens : (h + 1) * tokens]

    for g in range(KV_HEADS):
        attend(g)
        weights.advance(1 if g < KV_HEADS - 1 else 4 * each - weights.done)
    for copy in keep:
        copy.wait()
    weights.ready(1)

    xt_in[1] = att[...].T
    middle = residual + jnp.dot(att[...], w01[1, :, :width], preferred_element_type=F32)
    inverse_second = lax.rsqrt(jnp.mean(middle * middle, axis=-1, keepdims=True) + EPS)
    normed_second = (middle * inverse_second * gains_ref[1:2, :]).astype(BF16)
    xt_in[2] = normed_second.T
    weights.advance(1)
    gate[...] = jnp.dot(normed_second, wg[...], preferred_element_type=F32)
    weights.advance(1)

    def tokens_of(q):
        return pl.ds(pl.multiple_of(q * tokens, tokens), tokens)

    def kind_of(q):
        return jnp.where(q < 2, 0, jnp.where(q < WIDE, 2, 3))

    own_x = pltpu.make_async_copy(xt_in.at[kind_of(p)], xf_all.at[:, tokens_of(p)], ls.at[0])

    def x_move(bits):
        q = p ^ bits
        return remote(xt_in.at[kind_of(q)], xf_all.at[:, tokens_of(p)], xs.at[bits], xr.at[p], at.peer(bits))

    def a_move():
        return remote(xt_in.at[1], xa_all.at[:, tokens_of(p)], as_, ar.at[p], at.peer(p ^ 1))

    def own_a():
        return pltpu.make_async_copy(xt_in.at[1], xa_all.at[:, tokens_of(p)], ls.at[1])

    def y_move(bits):
        q = p ^ bits
        return remote(dy_in.at[q], yf_all.at[tokens_of(p)], ys.at[bits], yr.at[p], at.peer(bits))

    def own_y():
        return pltpu.make_async_copy(dy_in.at[p], yf_all.at[tokens_of(p)], ls.at[2])

    def v_move():
        return remote(dv_in, yv_all.at[tokens_of(p)], vs, vr.at[p], at.peer(p ^ 1))

    def own_v():
        return pltpu.make_async_copy(dv_in, yv_all.at[tokens_of(p)], ls.at[3])

    own_x.start()
    for bits in (2, 4, 6):
        x_move(bits).start()
    pl.when(p != 1)(lambda: a_move().start())
    pl.when(p == 1)(lambda: own_a().start())

    def give_y(bits, low, high):
        q = p ^ bits

        @pl.when((q >= low) & (q < high))
        def _():
            y_move(bits).start()

    weights.ready(2)
    for side in range(2):
        lifted[side * tokens : (side + 1) * tokens] = jnp.dot(
            normed_second, wu[:, side * half : (side + 1) * half], preferred_element_type=F32
        )

    def lift():
        return jnp.concatenate([lifted[:tokens], lifted[tokens:]], axis=1)

    hidden = (gate[...] * jax.nn.sigmoid(gate[...]) * lift()).astype(BF16)
    dy_in[6] = hidden[:, :half]
    dy_in[7] = hidden[:, half:]
    for bits in range(1, CLASSES):
        give_y(bits, WIDE, CLASSES)
    weights.ready(3)

    grad_hidden = jnp.dot(upstream.astype(BF16), wd[...], preferred_element_type=F32)
    sigma = jax.nn.sigmoid(gate[...])
    grad_gate = (grad_hidden * lift() * sigma * (1.0 + gate[...] * (1.0 - sigma))).astype(BF16)
    grad_lifted = (grad_hidden * gate[...] * sigma).astype(BF16)
    for side in range(2):
        lanes = slice(side * half, (side + 1) * half)
        dy_in[2 + side] = grad_gate[:, lanes]
        dy_in[4 + side] = grad_lifted[:, lanes]
    for bits in range(1, CLASSES):
        give_y(bits, 2, WIDE)

    out_ref[...] = (middle + contract(hidden, wd[...], 1, 1)).T.astype(BF16)
    weights.finish()
    grad_normed = contract(grad_gate, wg[...], 1, 1) + contract(grad_lifted, wu[...], 1, 1)
    pl.semaphore_signal(free.at[0], inc=1, device_id=pair, device_id_type=MESH)

    def norm_back(value, inverse, gain, incoming):
        scaled = incoming * gain
        mean = jnp.mean(scaled * value, axis=-1, keepdims=True)
        through = inverse * scaled - value * (inverse * inverse * inverse) * mean
        return through, jnp.sum(incoming * value * inverse, axis=0, keepdims=True)

    through, gain_second = norm_back(middle, inverse_second, gains_ref[1:2, :], grad_normed)
    gain_s[0] = jnp.zeros(gain_s.shape[1:], F32)
    gain_s[0, 1:2, :] = gain_second
    grad_middle = upstream + through
    grad_branch = grad_middle.astype(BF16)
    dy_in[1, :, :width] = grad_branch
    dy_in[1, :, width:] = jnp.zeros((tokens, keys), BF16)
    att[...] = contract(grad_branch, w01[1, :, :width], 1, 1).astype(BF16)

    for bits in range(1, CLASSES):
        give_y(bits, 1, 2)

    own = lifted.at[pl.ds(0, rows)]

    def swap(slot, target):
        return remote(gain_s.at[slot], gain_r.at[slot], gs.at[slot], gr.at[slot], target)

    outer = (f == 0) | (f == parts - 1)
    lower = f < parts // 2
    beside = jnp.where(lower, 1 - f, 2 * parts - 3 - f)
    far_outer = jnp.where(lower, parts - 1, 0)
    far_inner = jnp.where(lower, parts // 2, parts // 2 - 1)

    def order(i):
        falling = jnp.where(outer, parts - 1 - i, jnp.where(i == 0, 0, parts - i))
        return jnp.where(lower, falling, parts - 1 - falling)

    cut = width // 128 * 128
    part_lanes = (pl.ds(0, cut), pl.ds(cut, half - cut))
    parts_early = (lambda: p >= 1, lambda: p >= 2)
    parts_late = (lambda: p < 1, lambda: p < 2)

    def room(r):
        return wd.at[pl.ds(pl.multiple_of(r * rows, 16), rows), pl.ds(half, half)]

    def line(r, part):
        lanes = part_lanes[part]
        near_slot = jnp.where(lower, r - 1, parts - 2 - r)
        slot = jnp.where(outer, 2 - near_slot, jnp.where(r == beside, 0, jnp.where(r == far_outer, 1, 3)))
        target = jnp.where(outer, beside, r)
        return remote(
            room(r).at[:, lanes], za_r.at[slot, :, lanes], ozs.at[part, r], ozr.at[part, slot], (at.c, target)
        )

    def arrival(slot, part):
        lanes = part_lanes[part]
        return remote(
            room(f).at[:, lanes], za_r.at[slot, :, lanes], ozs.at[part, f], ozr.at[part, slot], at.along(1)
        )

    def relay(k, part):
        r = (far_outer, far_inner)[k]
        lanes = part_lanes[part]

        @pl.when(jnp.logical_not(outer))
        def _():
            arrival(k, part).wait_recv()
            total = room(r)[:, lanes].astype(F32) + za_r[k, :, lanes].astype(F32)
            room(r)[:, lanes] = total.astype(BF16)
            line(r, part).start()

    middle_token = CLASSES // 2 * tokens

    def sides_of():
        return [
            remote(
                yf_all.at[pl.ds(side * middle_token, middle_token)],
                wu.at[pl.ds(0, middle_token), pl.ds(side * half, half)],
                hs.at[side], hr.at[side], pair,
            )
            for side in range(2)
        ]

    def produce(r, put):
        at_rows = pl.ds(pl.multiple_of(r * rows, 16), rows)
        every = slice(0, half)

        @pl.when(p == 1)
        def _():
            put(slice(0, width), jnp.dot(xa_all[at_rows, :], yf_all[:, pl.ds(0, width)], preferred_element_type=F32))

        @pl.when((p != 1) & (p < WIDE))
        def _():
            put(every, jnp.dot(xf_all[at_rows, :], yf_all[...], preferred_element_type=F32))

        @pl.when(p >= WIDE)
        def _():
            side, start = lax.div(r * columns, half), pl.multiple_of(lax.rem(r * columns, half), 128)
            for t in range(2):
                part_rows = pl.ds(pl.multiple_of((p - WIDE) * tall + t * rows, 16), rows)
                lanes = slice(t * columns, (t + 1) * columns)

                @pl.when(side == core)
                def _():
                    put(
                        lanes,
                        jnp.dot(xf_all[part_rows, :], yf_all[:, pl.ds(start, columns)], preferred_element_type=F32),
                    )

                @pl.when(side != core)
                def _():
                    put(
                        lanes,
                        jnp.dot(
                            xf_all[part_rows, pl.ds(0, middle_token)],
                            wu[pl.ds(0, middle_token), pl.ds(start, columns)],
                            preferred_element_type=F32,
                        )
                        + jnp.dot(
                            xf_all[part_rows, pl.ds(middle_token, middle_token)],
                            wu[pl.ds(0, middle_token), pl.ds(pl.multiple_of(half + start, 128), columns)],
                            preferred_element_type=F32,
                        ),
                    )

    def keep_chunk(r):
        def put(lanes, value):
            own[:, lanes] = value
            room(r)[:, lanes] = value.astype(BF16)

        return put

    def gradients(conditions):
        for bits in range(1, CLASSES):
            arrived_y(p ^ bits)

        @pl.when(p >= WIDE)
        def _():
            for copy in sides_of():
                copy.start()
            for copy in sides_of():
                copy.wait()

        def step_of(i, carry):
            r = order(i)
            produce(r, keep_chunk(r))
            goes = (i == 0) | (outer & (i < parts - 1))
            for part in range(2):
                pl.when(goes & conditions[part]())(lambda part=part: line(r, part).start())
            return carry

        lax.fori_loop(0, parts, step_of, 0)

    def value_gradient():
        for q in range(CLASSES):
            if q != 1:
                remote(dv_in, yv_all.at[tokens_of(q)], vs, vr.at[q], pair).wait_recv()

        def step_of(i, carry):
            r = order(i)
            at_rows = pl.ds(pl.multiple_of(r * rows, 16), rows)
            value = jnp.dot(xf_all[at_rows, :], yv_all[...], preferred_element_type=F32)

            @pl.when(i < parts - 1)
            def _():
                room(r)[:, pl.ds(width, keys)] = value[:, :keys].astype(BF16)
                pl.when((i == 0) | outer)(lambda: line(r, 1).start())

            @pl.when(i == parts - 1)
            def _():
                own[:, pl.ds(width, keys)] = value[:, :keys]

            return carry

        lax.fori_loop(0, parts, step_of, 0)

    def arrived_y(q):
        remote(dy_in.at[0], yf_all.at[tokens_of(q)], ys.at[1], yr.at[q], pair).wait_recv()

    def arrived_x(q):
        remote(xt_in.at[0], xf_all.at[:, tokens_of(q)], xs.at[2], xr.at[q], pair).wait_recv()

    def x_pair(bits):
        q = p ^ bits
        return remote(xf_all.at[:, tokens_of(q)], xf_all.at[:, tokens_of(q)], ps.at[bits], pr.at[q], pair)

    def attend_back(g):
        chance = probs[g]
        out_grad = heads_of(att, g)
        query = heads_of(rot, g)
        grad_probs = contract(values_of(g), out_grad, 1, 1)
        delta = jnp.sum(grad_probs * chance, axis=0, keepdims=True)
        grad_scores = (chance * (grad_probs - delta)).astype(BF16)
        grad_values = jnp.dot(chance.astype(BF16), out_grad, preferred_element_type=F32)
        grad_keys = jnp.dot(grad_scores, query, preferred_element_type=F32) * scale
        dkv[:, :, g * HEAD : (g + 1) * HEAD] = grad_keys.reshape(CLASSES, tokens, HEAD)
        dkv[:, :, keys + g * HEAD : keys + (g + 1) * HEAD] = grad_values.reshape(CLASSES, tokens, HEAD)
        turned = contract(keys_of(g), grad_scores, 0, 0).T * scale
        for h in range(group):
            at_lane = (g * group + h) * HEAD
            gate[:, at_lane : at_lane + HEAD] = turned[h * tokens : (h + 1) * tokens]

    for g in range(KV_HEADS):
        attend_back(g)

    def halve(bit, rest, sbuf, rbuf, index, between=None):
        for i, bits in enumerate(rest):
            sbuf[pl.ds(i // 2 * tokens, tokens), pl.ds(i % 2 * 2 * keys, 2 * keys)] = dkv[p ^ bit ^ bits].astype(BF16)
        copy = remote(sbuf, rbuf, ds.at[index], dr.at[index], at.peer(bit))
        copy.start()
        if between is not None:
            between()
        copy.wait()
        for i, bits in enumerate(rest):
            dkv[p ^ bits] = dkv[p ^ bits] + rbuf[pl.ds(i // 2 * tokens, tokens), pl.ds(i % 2 * 2 * keys, 2 * keys)].astype(F32)

    own_x.wait()
    for bits in (2, 4, 6):
        arrived_x(p ^ bits)
    for bits in (0, 2, 4, 6):
        x_pair(bits).start()

    def early():
        for bits in (0, 2, 4, 6):
            remote(
                xf_all.at[:, tokens_of(p ^ bits ^ 1)], xf_all.at[:, tokens_of(p ^ bits ^ 1)],
                ps.at[bits], pr.at[p ^ bits ^ 1], pair,
            ).wait_recv()
        pl.semaphore_wait(free.at[0], 1)

        @pl.when(p == 1)
        def _():
            own_a().wait()
            for q in range(CLASSES):
                if q != 1:
                    remote(xt_in.at[1], xa_all.at[:, tokens_of(q)], as_, ar.at[q], pair).wait_recv()

        @pl.when(p >= 1)
        def _():
            own_y().start()
            own_y().wait()
            gradients(parts_early)

    halve(1, (0, 2, 4, 6), wg.at[pl.ds(0, 2 * tokens), pl.ds(0, half)], c4r, 0)
    halve(at.b1, (0, at.b2), wg.at[pl.ds(2 * tokens, tokens), pl.ds(0, half)], c2r, 1, early)
    halve(at.b2, (0,), wg.at[pl.ds(3 * tokens, tokens), pl.ds(0, 2 * keys)], c1r, 2)

    gate[:, width:half] = dkv[p, :, :keys]
    for tile, value in enumerate(turn(gate[:, :half], -1)):
        dy_in[0, :, tile * 128 : (tile + 1) * 128] = value.astype(BF16)
    dv_in[...] = jnp.zeros(dv_in.shape, BF16)
    dv_in[:, :keys] = dkv[p, :, keys:].astype(BF16)
    for bits in range(1, CLASSES):
        give_y(bits, 0, 1)
    pl.when(p != 1)(lambda: v_move().start())
    pl.when(p == 1)(lambda: own_v().start())
    grad_normed = contract(dy_in[0], w01[0], 1, 1)
    grad_normed = grad_normed + contract(dv_in[:, :keys], w01[1, :, width:], 1, 1)
    through, gain_first = norm_back(residual, inverse_first, gains_ref[0:1, :], grad_normed)
    gain_s[0, 0:1, :] = gain_first
    swaps = [swap(0, pair)]
    swaps[0].start()
    grad_ref[...] = (grad_middle + through).T
    def relays(k, conditions):
        for part in range(2):
            pl.when(conditions[part]())(lambda part=part: relay(k, part))

    relays(0, parts_early)

    @pl.when(p == 0)
    def _():
        own_y().start()
        own_y().wait()
        gradients(parts_late)

    @pl.when(p == 1)
    def _():
        own_v().wait()
        value_gradient()

    relays(1, parts_early)
    relays(0, parts_late)
    relays(1, parts_late)
    swaps[0].wait()
    gain_s[1] = gain_s[0] + gain_r[0]
    swaps.append(swap(1, at.peer(2)))
    swaps[1].start()
    for bits in (0, 2, 4, 6):
        x_pair(bits).wait_send()
    for bits in range(1, CLASSES):
        y_move(bits).wait_send()
    for bits in (2, 4, 6):
        x_move(bits).wait_send()

    @pl.when(p != 1)
    def _():
        a_move().wait_send()
        v_move().wait_send()

    swaps[1].wait()
    gain_s[2] = gain_s[1] + gain_r[1]
    swaps.append(swap(2, at.peer(4)))
    swaps[2].start()

    moment("wait")

    @pl.when(p < 2)
    def _():
        ma[:, :width] = mq[...]
        ma[:, width:] = mk[...].T

    sall = wd.at[:, pl.ds(0, half)]
    ga, pa = (w01.at[1, pl.ds((parts - 1 - i) * rows, rows)] for i in range(2))

    def shard(index, part):
        return sall.at[pl.ds(pl.multiple_of(index * rows, 16), rows), part_lanes[part]]

    def rightward(index, part):
        here = shard(index, part)
        return remote(here, here, ls_r.at[part, index], lr_r.at[part, index], (at.c, lax.rem(f + 1, parts)))

    def leftward(index, part):
        here = shard(index, part)
        return remote(here, here, ls_l.at[part, index], lr_l.at[part, index], (at.c, lax.rem(f + parts - 1, parts)))

    can_right = f < parts - 1
    can_left = f > 0

    def settle_part(part):
        lanes = part_lanes[part]
        total = own[:, lanes]
        for k in range(2):
            slot = jnp.where(outer, k, 2 + k)
            arrival(slot, part).wait_recv()
            total = total + za_r[slot, :, lanes].astype(F32)
        ga[:, lanes] = total.astype(BF16)
        sall[my_rows, lanes] = (MOMENTUM * ma[:, lanes] + total).astype(BF16)
        pl.when(can_right)(lambda: rightward(f, part).start())
        pl.when(can_left)(lambda: leftward(f, part).start())

    def hop_part(hop, part):
        @pl.when(f - hop >= 0)
        def _():
            rightward(f - hop, part).wait_recv()
            pl.when(can_right)(lambda: rightward(f - hop, part).start())

        @pl.when(f + hop < parts)
        def _():
            leftward(f + hop, part).wait_recv()
            pl.when(can_left)(lambda: leftward(f + hop, part).start())

    spread_begin, spread_step, spread_finish = spread_even(at, ga, g_out, ag_l, ag_s, ag_r)
    for conditions, whole in ((parts_early, p >= 2), (parts_late, p < 2)):
        for part in range(2):
            pl.when(conditions[part]())(lambda part=part: settle_part(part))
        pl.when(whole)(spread_begin)
        for hop in range(1, parts):
            for part in range(2):
                pl.when(conditions[part]())(lambda hop=hop, part=part: hop_part(hop, part))

    swaps[2].wait()
    gain_s[3] = gain_s[2] + gain_r[2]
    line_gain = [
        remote(gain_s.at[3], gain_r.at[3 + j], gs.at[3 + j], gr.at[3 + j], at.along(j)) for j in range(1, parts)
    ]
    for copy in line_gain:
        copy.start()

    for part in range(2):
        for j in range(1, parts):
            line(f ^ j, part).wait_send()
        pl.when(can_right)(lambda: rightward(f, part).wait_send())
        pl.when(can_left)(lambda: leftward(f, part).wait_send())
        for hop in range(1, parts):
            pl.when((f - hop >= 0) & can_right)(lambda hop=hop: rightward(f - hop, part).wait_send())
            pl.when((f + hop < parts) & can_left)(lambda hop=hop: leftward(f + hop, part).wait_send())
    pl.semaphore_signal(free.at[1], inc=1, device_id=pair, device_id_type=MESH)
    pl.semaphore_wait(free.at[1], 1)

    x = w01.at[0]
    wide_gram = 1024
    gram_s, g = wg.at[:, pl.ds(0, wide_gram)], wg.at[:, pl.ds(wide_gram, wide_gram)]
    poly, xf = wd.at[:, pl.ds(0, wide_gram)], wd.at[:, pl.ds(half, columns)]
    bounds = [min(256 * r, width) for r in range(4)] + [width]
    spans = [(low, high - low) for low, high in zip(bounds, bounds[1:])]

    def gram_r(slot):
        return wu.at[:, pl.ds(slot * wide_gram, wide_gram)]

    def scale_of(total):
        return 1.0 / (jnp.sqrt(total) + 1e-07)

    def normal(ref, inverse):
        ref[...] = rounded(ref[...].astype(F32) * inverse)

    def exchange(slot, r):
        part = pl.ds(*spans[r])
        return remote(gram_s.at[part], gram_r(slot).at[part], gsem.at[r], rsem.at[slot, r], pair)

    def poly_of(start, count):
        part = g[pl.ds(start, count), pl.ds(0, width)]
        square = jnp.dot(part, g[:, pl.ds(0, width)], preferred_element_type=F32)
        return rounded(NS_B * part.astype(F32) + NS_C * square)

    def fill_poly():
        for low, count in spans:
            poly[pl.ds(low, count), pl.ds(0, width)] = poly_of(low, count)

    near = parts // 2
    mine_at = core * near
    last_core = lax.div(f, near)
    f_lanes = pl.ds(pl.multiple_of(lax.rem(f, near) * columns, 128), columns)

    kt = wd.at[pl.ds(0, keys), pl.ds(half + 256, wide_gram)]

    def xo(i):
        return w01.at[1, pl.ds(i * rows, rows)]

    def give():
        return [
            remote(
                sall.at[pl.ds(pl.multiple_of(((1 - core) * near + i) * rows, 16), rows)],
                xo(i), ex_s.at[i], ex_r.at[i], pair,
            )
            for i in range(near)
        ]

    def give_last():
        return remote(x.at[:, f_lanes], xf, fx_s, fx_r, pair)

    @pl.when(p >= 2)
    def _():
        @pl.when(p >= WIDE)
        def _():
            copies = give()
            for copy in copies:
                copy.start()
            for i in range(near):
                part = sall[pl.ds(pl.multiple_of((mine_at + i) * rows, 16), rows), :]
                for t in range(2):
                    x[pl.ds(pl.multiple_of(core * tall + t * rows, 16), rows), pl.ds(i * columns, columns)] = part[
                        :, t * columns : (t + 1) * columns
                    ]
            for i, copy in enumerate(copies):
                copy.wait()
                part = xo(i)
                for t in range(2):
                    x[pl.ds(pl.multiple_of((1 - core) * tall + t * rows, 16), rows), pl.ds(i * columns, columns)] = part[
                        :, pl.ds(t * columns, columns)
                    ]

        def squares(ref):
            wide = ref[...].astype(F32)
            sq[...] = jnp.broadcast_to(jnp.sum(wide * wide), sq.shape)

        pl.when(p < WIDE)(lambda: squares(sall))
        pl.when(p >= WIDE)(lambda: squares(x))
        copy = remote(sq, sq_r, qs, qr, pair)
        copy.start()
        copy.wait()
        inverse = scale_of(sq[...] + sq_r[...])[:1, :1]

        @pl.when(p < WIDE)
        def _():
            x[...] = rounded(sall[...].astype(F32) * inverse)

        pl.when(p >= WIDE)(lambda: normal(x, inverse))

        def grams(slot):
            for r in range(4):
                gram_s[pl.ds(*spans[r]), pl.ds(0, width)] = rounded(
                    contract(x[pl.ds(*spans[r]), :], x[...], 1, 1)
                )
                exchange(slot, r).start()
            for r in range(4):
                part = pl.ds(*spans[r])
                exchange(slot, r).wait()
                g[part, pl.ds(0, width)] = rounded(
                    gram_s[part, pl.ds(0, width)].astype(F32) + gram_r(slot)[part, pl.ds(0, width)].astype(F32)
                )

        def iterate(slot):
            grams(slot)
            fill_poly()
            for tile in range(half // 256):
                part = pl.ds(tile * 256, 256)
                x[:, part] = rounded(
                    NS_A * x[:, part].astype(F32) + jnp.dot(poly[:, pl.ds(0, width)], x[:, part], preferred_element_type=F32)
                )

        def iterate_twice(it, carry):
            iterate(0)
            pl.when(it == 1)(lambda: spread_step(1))
            iterate(1)
            pl.when(it == 0)(lambda: spread_step(0))
            pl.when(it == 1)(lambda: spread_step(2))
            return carry

        lax.fori_loop(0, (NS_ITERS - 1) // 2, iterate_twice, 0)

        @pl.when((p >= WIDE) & (core == last_core))
        def _():
            give_last().start()
            xf[...] = x[:, f_lanes]

        grams(0)

        @pl.when(p < WIDE)
        def _():
            part = poly_of(pl.multiple_of(f * rows, 16), rows)
            pa[...] = rounded(NS_A * x[my_rows, :].astype(F32) + jnp.dot(part, x[...], preferred_element_type=F32))

        @pl.when(p >= WIDE)
        def _():
            pl.when(core == last_core)(lambda: give_last().wait_send())
            pl.when(core != last_core)(lambda: give_last().wait_recv())
            for t in range(2):
                top = pl.multiple_of(core * tall + t * rows, 16)
                part = poly_of(top, rows)
                pa[:, t * columns : (t + 1) * columns] = rounded(
                    NS_A * xf[pl.ds(top, rows), :].astype(F32) + jnp.dot(part, xf[...], preferred_element_type=F32)
                )

    @pl.when(p < 2)
    def _():
        x[...] = sall[...]
        kt[:, pl.ds(0, width)] = x[:, pl.ds(width, keys)].T
        turned = kt[:, pl.ds(0, width)].astype(F32)
        kt[:, pl.ds(0, width)] = rounded(turned * scale_of(jnp.sum(turned * turned)))
        wide = x[:, pl.ds(0, width)].astype(F32)
        x[:, pl.ds(0, width)] = rounded(wide * scale_of(jnp.sum(wide * wide)))

        def narrow_step(it, carry):
            now = kt[:, pl.ds(0, width)]
            gram = rounded(contract(now, now, 1, 1))
            turned = rounded(NS_B * gram.astype(F32) + NS_C * jnp.dot(gram, gram, preferred_element_type=F32))
            kt[:, pl.ds(0, width)] = rounded(
                NS_A * now.astype(F32) + jnp.dot(turned, now, preferred_element_type=F32)
            )
            return carry

        lax.fori_loop(0, NS_ITERS, narrow_step, 0)

        def gram_of():
            for r in range(4):
                part = pl.ds(*spans[r])
                g[part, pl.ds(0, width)] = rounded(contract(x[part, pl.ds(0, width)], x[:, pl.ds(0, width)], 1, 1))

        def square_step(it, carry):
            gram_of()
            fill_poly()
            x[:, pl.ds(0, width)] = rounded(
                NS_A * x[:, pl.ds(0, width)].astype(F32) + jnp.dot(poly[:, pl.ds(0, width)], x[:, pl.ds(0, width)], preferred_element_type=F32)
            )
            for k in range(3):
                pl.when(it == k + 1)(lambda k=k: spread_step(k))
            return carry

        lax.fori_loop(0, NS_ITERS - 1, square_step, 0)
        gram_of()
        part = poly_of(pl.multiple_of(f * rows, 16), rows)
        square = rounded(
            NS_A * x[my_rows, pl.ds(0, width)].astype(F32) + jnp.dot(part, x[:, pl.ds(0, width)], preferred_element_type=F32)
        )
        x[:, pl.ds(width, keys)] = kt[:, pl.ds(0, width)].T
        pa[:, :width] = square
        pa[:, width:] = x[my_rows, pl.ds(width, keys)]

    out_begin, out_step, out_finish = spread_even(at, pa, o_out, og_l, og_s, og_r)
    out_begin()
    total = gain_s[3]
    for j in range(1, parts):
        line_gain[j - 1].wait()
        total = total + gain_r[3 + j]
    gain_out[...] = total
    spread_finish()
    for k in range(3):
        out_step(k)
    for copy in sent:
        copy.wait_send()
    out_finish()


def step_pass(x, up, gains, tables, bias, shards, moments):
    parts = lax.axis_size("fsdp")
    width, tokens = x.shape
    half = shards[4].shape[1] // 2
    rows = width // parts
    keys = half - width
    near = parts // 2
    dma = pltpu.SemaphoreType.DMA
    vm = pltpu.VMEM
    group = HEADS // KV_HEADS
    two = 2 * keys
    n_gain = 3 + parts
    return pl.pallas_call(
        step_kernel,
        out_shape=(
            jax.ShapeDtypeStruct((width, tokens), BF16),
            jax.ShapeDtypeStruct((width, tokens), F32),
            jax.ShapeDtypeStruct((CLASSES, rows, half), BF16),
            jax.ShapeDtypeStruct((CLASSES, rows, half), BF16),
            jax.ShapeDtypeStruct((8, width), F32),
        ),
        in_specs=[VMEM] * 11 + [ANY] * 10,
        out_specs=(VMEM, VMEM, ANY, ANY, VMEM),
        scratch_shapes=[
            vm((2, width, half), BF16),
            vm((width, 2 * half), BF16),
            vm((width, 2 * half), BF16),
            vm((width, 2 * half), BF16),
            vm((KV_HEADS, CLASSES * tokens, group * tokens), F32),
            vm((CLASSES, tokens, two), BF16),
            vm((tokens, half), BF16),
            vm((CLASSES, tokens, two), F32),
            vm((2 * tokens, 2 * two), BF16),
            vm((tokens, 2 * two), BF16),
            vm((tokens, two), BF16),
            vm((tokens, width), BF16),
            vm((tokens, 2 * half), F32),
            vm((2 * tokens, half), F32),
            vm((4, width, tokens), BF16),
            vm((CLASSES, tokens, half), BF16),
            vm((tokens, -(-keys // 128) * 128), BF16),
            vm((width, CLASSES * tokens), BF16),
            vm((width, CLASSES * tokens), BF16),
            vm((CLASSES * tokens, half), BF16),
            vm((CLASSES * tokens, -(-keys // 128) * 128), BF16),
            vm((4, rows, half), BF16),
            vm((rows, half), F32),
            vm((rows, width), F32),
            vm((keys, rows), F32),
            vm((4, 8, width), F32),
            vm((n_gain, 8, width), F32),
            vm((8, 128), F32),
            vm((8, 128), F32),
            dma((3,)), dma((4, parts)), dma((4, parts)), dma((4, 2, parts)), dma((4, 4, parts)),
            dma((4, CLASSES, parts)), dma((7,)), dma((CLASSES,)), dma((3,)), dma((3,)),
            dma((4,)), dma((CLASSES,)), dma((CLASSES,)), dma((CLASSES,)), dma((CLASSES,)),
            dma((CLASSES,)), dma((CLASSES,)), dma, dma((CLASSES,)), dma, dma((CLASSES,)),
            dma((2,)), dma((2,)), dma((2, parts)), dma((2, parts)),
            dma((2,)), dma((n_gain,)), dma((n_gain,)),
            dma, dma((7,)), dma((CLASSES,)),
            dma((2, parts)), dma((2, parts)), dma((2, parts)), dma((2, parts)),
            dma((4,)), dma((2, 4)), dma, dma,
            dma((near,)), dma((near,)), dma, dma,
            dma, dma((7,)), dma((CLASSES,)), pltpu.SemaphoreType.REGULAR((2,)),
        ],
        compiler_params=pltpu.CompilerParams(
            collective_id=3, has_side_effects=True, vmem_limit_bytes=63 << 20
        ),
        name="step_pass",
    )(x, up, gains, *tables, bias, *shards, *moments)


def settle_wide(factors, *refs):
    gs, os = refs[0], refs[1]
    ms, ws, outs = refs[2:6], refs[6:10], refs[10:]
    width = ms[0].shape[1]
    half = gs.shape[2]

    def one(index, g, o, lanes):
        grad, moment, weight = (outs[3 * index + i] for i in range(3))
        value = g.astype(F32)
        grad[:, lanes] = value
        moment[:, lanes] = MOMENTUM * ms[index][:, lanes] + value
        weight[:, lanes] = ws[index][:, lanes].astype(F32) + factors[index] * o.astype(F32)

    for index in range(2):
        one(index, gs[index, :, :width], os[index, :, :width], slice(0, width))
    for index in range(2):
        for side in range(2):
            cls = 2 + 2 * index + side
            one(2 + index, gs[cls], os[cls], slice(side * half, (side + 1) * half))


def settle_turned(factors, g_tall, o_tall, g_pair, o_pair, *refs):
    ms, ws, outs = refs[0:3], refs[3:6], refs[6:]
    keys = ms[1].shape[0]

    def one(index, g, o):
        grad, moment, weight = (outs[3 * index + i] for i in range(3))
        grad[...] = g
        moment[...] = MOMENTUM * ms[index][...] + g
        weight[...] = ws[index][...].astype(F32) + factors[index] * o

    one(0, g_tall[0].astype(F32), o_tall[0].astype(F32))

    @pl.when(pl.program_id(0) == 0)
    def _():
        for index in range(2):
            start = g_pair.shape[2] - keys
            one(1 + index, g_pair[index, :, start:].astype(F32).T, o_pair[index, :, start:].astype(F32).T)


def settle(g, o, moments, shards, factors):
    m_q, m_k, m_o, m_v, m_gate, m_up, m_down = moments
    w_q, w_k, w_o, w_v, w_gate, w_up, w_down = shards
    f_q, f_k, f_v, f_o, f_gate, f_up, f_down = factors
    _, rows, half = g.shape
    width, columns = m_down.shape
    block = 80 if rows % 80 == 0 else rows
    piece = pl.BlockSpec((WIDE, block, half), lambda i: (0, i, 0))

    def row_block(array):
        return pl.BlockSpec((block, array.shape[1]), lambda i: (i, 0))

    def result(arrays):
        return tuple(jax.ShapeDtypeStruct(array.shape, F32) for array in arrays for _ in range(3))

    wide = (m_q, m_o, m_gate, m_up)
    first = pl.pallas_call(
        functools.partial(settle_wide, (f_q, f_o, f_gate, f_up)),
        grid=(rows // block,),
        out_shape=result(wide),
        in_specs=[piece, piece] + [row_block(array) for array in wide] * 2,
        out_specs=tuple(row_block(array) for array in wide for _ in range(3)),
        compiler_params=pltpu.CompilerParams(vmem_limit_bytes=48 << 20),
        name="settle_wide",
    )(g, o, *wide, w_q, w_o, w_gate, w_up)

    turned = (m_down, m_k, m_v)
    halves = half // columns
    tile = pl.BlockSpec((1, rows, columns), lambda i: (WIDE + i // halves, 0, i % halves))
    both = pl.BlockSpec((2, rows, half), lambda i: (0, 0, 0))
    specs = [pl.BlockSpec((rows, columns), lambda i: (i, 0))] + [
        pl.BlockSpec(array.shape, lambda i: (0, 0)) for array in turned[1:]
    ]
    second = pl.pallas_call(
        functools.partial(settle_turned, (f_down, f_k, f_v)),
        grid=(width // rows,),
        out_shape=result(turned),
        in_specs=[tile, tile, both, both] + specs * 2,
        out_specs=tuple(spec for spec in specs for _ in range(3)),
        compiler_params=pltpu.CompilerParams(vmem_limit_bytes=48 << 20),
        name="settle_turned",
    )(g, o, g, o, *turned, w_down, w_k, w_v)
    q, out, gate, up = (first[3 * i : 3 * i + 3] for i in range(4))
    down, k, v = (tuple(item.T for item in second[3 * i : 3 * i + 3]) for i in range(3))
    return list(zip(q, k, v, out, gate, up, down))


def rotary_tables(positions, width):
    half = width // 2
    frequency = THETA ** (-(jnp.arange(half, dtype=jnp.float32) * 2.0 / width))
    angle = positions.astype(jnp.float32)[:, None] * frequency[None, :]
    return (jnp.cos(angle)[:, None, :], jnp.sin(angle)[:, None, :])


def rotate(value, cosine, sine):
    half = value.shape[-1] // 2
    first = value[..., :half]
    second = value[..., half:]
    return jnp.concatenate(
        [first * cosine - second * sine, second * cosine + first * sine], axis=-1
    )


def unrotate(incoming, cosine, sine):
    half = incoming.shape[-1] // 2
    upper = incoming[..., :half]
    lower = incoming[..., half:]
    return jnp.concatenate([upper * cosine + lower * sine, lower * cosine - upper * sine], axis=-1)


def norm_forward(residual, gain):
    inverse = lax.rsqrt(jnp.mean(residual * residual, axis=-1, keepdims=True) + EPS)
    return ((residual * inverse * gain).astype(jnp.bfloat16), inverse)


def norm_backward(residual, inverse, gain, incoming):
    scaled = incoming * gain
    through = inverse * scaled - residual * inverse**3 * jnp.mean(
        scaled * residual, axis=-1, keepdims=True
    )
    return (through, jnp.sum(incoming * residual * inverse, axis=0))


def padded(array, axis, parts, count, full):
    if count == full:
        return array
    shape = array.shape
    split = array.reshape(shape[:axis] + (parts, count) + shape[axis + 1 :])
    pads = [(0, 0)] * split.ndim
    pads[axis + 1] = (0, full - count)
    return jnp.pad(split, pads).reshape(shape[:axis] + (parts * full,) + shape[axis + 1 :])


def trimmed(array, axis, parts, count, full):
    if count == full:
        return array
    shape = array.shape
    split = array.reshape(shape[:axis] + (parts, full) + shape[axis + 1 :])
    kept = lax.slice_in_dim(split, 0, count, axis=axis + 1)
    return kept.reshape(shape[:axis] + (parts * count,) + shape[axis + 1 :])


def plain_layer(
    layer_input, output_grad, wide, tall, norm_gains, block_order, sizes
):
    parts, width, half, kv, short, full, high = sizes
    hidden_size = 2 * half
    rows = layer_input.shape[1]
    block = rows // 2
    group = HEADS // KV_HEADS
    scale = 1.0 / math.sqrt(HEAD)
    ctx_place = lax.axis_index("ctx")
    offsets = jnp.arange(block, dtype=jnp.int32)
    own_blocks = lax.dynamic_slice_in_dim(block_order, 2 * ctx_place, 2)
    query_pos = (own_blocks[:, None] * block + offsets[None, :]).reshape(rows)
    key_pos = (block_order[:, None] * block + offsets[None, :]).reshape(-1)

    all_wide, all_tall = gather_weights(wide, tall)
    w_qk, w_ov, w_gate_0, w_gate_1, w_up_0, w_up_1 = [all_wide[i].reshape(width, half) for i in range(WIDE)]
    w_down = [all_tall[i].reshape(half, width) for i in range(2)]

    residual = layer_input[0].astype(jnp.float32)
    normed_first, inverse_first = norm_forward(residual, norm_gains[0])
    qk_pre = jnp.dot(normed_first, w_qk, preferred_element_type=jnp.float32)
    query_pre = qk_pre[:, :width].reshape(rows, HEADS, HEAD)
    key_pre = qk_pre[:, width:].reshape(rows, KV_HEADS, HEAD)
    value_low = (
        jnp.dot(normed_first, w_ov, preferred_element_type=jnp.float32)[:, width:]
        .astype(jnp.bfloat16)
        .reshape(rows, KV_HEADS, HEAD)
    )
    cosine, sine = rotary_tables(query_pos, HEAD)
    query_rot = rotate(query_pre, cosine, sine).astype(jnp.bfloat16)
    key_rot = rotate(key_pre, cosine, sine).astype(jnp.bfloat16)
    keys_all, values_all = (
        lax.all_gather(key_rot, "ctx", axis=0, tiled=True),
        lax.all_gather(value_low, "ctx", axis=0, tiled=True),
    )
    keys_head = keys_all.transpose(1, 0, 2)
    values_head = values_all.transpose(1, 0, 2)
    queries_head = (
        query_rot.reshape(rows, KV_HEADS, group, HEAD)
        .transpose(1, 2, 0, 3)
        .reshape(KV_HEADS, group * rows, HEAD)
    )
    row_pos = jnp.tile(query_pos, group)
    allowed = key_pos[None, :] <= row_pos[:, None]

    def head_forward(item):
        query, key, value = item
        scores = jnp.where(allowed, contract(query, key, 1, 1) * scale, MASKED)
        top = jnp.max(scores, axis=-1, keepdims=True)
        expo = jnp.exp(scores - top)
        total = jnp.sum(expo, axis=-1, keepdims=True)
        probs_low = (expo / total).astype(jnp.bfloat16)
        return (
            jnp.dot(probs_low, value, preferred_element_type=jnp.float32),
            (top + jnp.log(total))[:, 0],
        )

    mixed, log_total = lax.map(head_forward, (queries_head, keys_head, values_head))
    attended = (
        mixed.reshape(KV_HEADS, group, rows, HEAD)
        .transpose(2, 0, 1, 3)
        .reshape(rows, HEADS * HEAD)
        .astype(jnp.bfloat16)
    )
    w_out = w_ov[:, :width]
    middle = residual + jnp.dot(attended, w_out, preferred_element_type=jnp.float32)
    normed_second, inverse_second = norm_forward(middle, norm_gains[1])

    def sides(left, right):
        return jnp.concatenate([left, right], axis=1)

    gate = sides(
        jnp.dot(normed_second, w_gate_0, preferred_element_type=jnp.float32),
        jnp.dot(normed_second, w_gate_1, preferred_element_type=jnp.float32),
    )
    lifted = sides(
        jnp.dot(normed_second, w_up_0, preferred_element_type=jnp.float32),
        jnp.dot(normed_second, w_up_1, preferred_element_type=jnp.float32),
    )
    sigma = jax.nn.sigmoid(gate)
    hidden = (gate * sigma * lifted).astype(jnp.bfloat16)
    hidden_split = hidden.reshape(rows, parts, 2, high)
    hidden_sides = [hidden_split[:, :, i].reshape(rows, half) for i in range(2)]
    layer_output = (
        middle
        + jnp.dot(hidden_sides[0], w_down[0], preferred_element_type=jnp.float32)
        + jnp.dot(hidden_sides[1], w_down[1], preferred_element_type=jnp.float32)
    ).astype(jnp.bfloat16)
    upstream = output_grad[0]
    grad_hidden = jnp.stack(
        [contract(upstream, w_down[i], 1, 1).reshape(rows, parts, high) for i in range(2)], axis=2
    ).reshape(rows, hidden_size)
    grad_gate = (grad_hidden * lifted * sigma * (1.0 + gate * (1.0 - sigma))).astype(jnp.bfloat16)
    grad_lifted = (grad_hidden * gate * sigma).astype(jnp.bfloat16)
    grad_normed_second = (
        contract(grad_gate[:, :half], w_gate_0, 1, 1)
        + contract(grad_gate[:, half:], w_gate_1, 1, 1)
        + contract(grad_lifted[:, :half], w_up_0, 1, 1)
        + contract(grad_lifted[:, half:], w_up_1, 1, 1)
    )
    through_second, gain_second = norm_backward(
        middle, inverse_second, norm_gains[1], grad_normed_second
    )
    grad_middle = upstream.astype(jnp.float32) + through_second
    grad_branch = grad_middle.astype(jnp.bfloat16)
    grad_attended = contract(grad_branch, w_out, 1, 1).astype(jnp.bfloat16)
    grad_heads = (
        grad_attended.reshape(rows, KV_HEADS, group, HEAD)
        .transpose(1, 2, 0, 3)
        .reshape(KV_HEADS, group * rows, HEAD)
    )

    def head_backward(item):
        query, key, value, grad_out, log_row = item
        scores = jnp.where(allowed, contract(query, key, 1, 1) * scale, MASKED)
        probs = jnp.exp(scores - log_row[:, None])
        grad_value_part = contract(probs.astype(jnp.bfloat16), grad_out, 0, 0)
        grad_probs = contract(grad_out, value, 1, 1)
        grad_scores = (
            probs * (grad_probs - jnp.sum(grad_probs * probs, axis=-1, keepdims=True))
        ).astype(jnp.bfloat16)
        grad_query_part = jnp.dot(grad_scores, key, preferred_element_type=jnp.float32) * scale
        grad_key_part = contract(grad_scores, query, 0, 0) * scale
        return (grad_query_part, grad_key_part, grad_value_part)

    grad_query_rot, grad_key_all, grad_value_all = lax.map(
        head_backward, (queries_head, keys_head, values_head, grad_heads, log_total)
    )
    grad_key_own, grad_value_own = (
        lax.psum_scatter(
            grad_key_all.astype(jnp.bfloat16), "ctx", scatter_dimension=1, tiled=True
        ).astype(jnp.float32),
        lax.psum_scatter(
            grad_value_all.astype(jnp.bfloat16), "ctx", scatter_dimension=1, tiled=True
        ).astype(jnp.float32),
    )
    grad_query = (
        unrotate(
            grad_query_rot.reshape(KV_HEADS, group, rows, HEAD)
            .transpose(2, 0, 1, 3)
            .reshape(rows, HEADS, HEAD),
            cosine,
            sine,
        )
        .reshape(rows, HEADS * HEAD)
        .astype(jnp.bfloat16)
    )
    grad_key = (
        unrotate(grad_key_own.transpose(1, 0, 2), cosine, sine)
        .reshape(rows, KV_HEADS * HEAD)
        .astype(jnp.bfloat16)
    )
    grad_value = (
        grad_value_own.transpose(1, 0, 2).reshape(rows, KV_HEADS * HEAD).astype(jnp.bfloat16)
    )
    grad_qk = sides(grad_query, grad_key)
    zero_query = jnp.zeros((rows, width), jnp.bfloat16)
    grad_v = sides(zero_query, grad_value)
    grad_normed_first = contract(grad_qk, w_qk, 1, 1) + contract(grad_v, w_ov, 1, 1)
    through_first, gain_first = norm_backward(
        residual, inverse_first, norm_gains[0], grad_normed_first
    )
    input_gradient = grad_middle + through_first

    xt = jnp.stack([item.T for item in (normed_first, attended, normed_second, upstream)])
    xt = padded(xt, 1, parts, short, full)
    dy = jnp.stack(
        [
            grad_qk,
            sides(grad_branch, jnp.zeros((rows, kv), jnp.bfloat16)),
            grad_gate[:, :half],
            grad_gate[:, half:],
            grad_lifted[:, :half],
            grad_lifted[:, half:],
            hidden_sides[0],
            hidden_sides[1],
            grad_v,
        ]
    )
    gains = jnp.pad(jnp.stack([gain_first, gain_second]), ((0, 6), (0, 0)))
    return layer_output, input_gradient, xt, dy, gains


def rotation(block_order, rows):
    block = rows // 2
    ctx_place = lax.axis_index("ctx")
    offsets = jnp.arange(block, dtype=jnp.int32)
    own_blocks = lax.dynamic_slice_in_dim(block_order, 2 * ctx_place, 2)
    query_pos = (own_blocks[:, None] * block + offsets[None, :]).reshape(rows)
    key_pos = (block_order[:, None] * block + offsets[None, :]).reshape(-1)
    bias = jnp.where(key_pos[:, None] <= query_pos[None, :], 0.0, MASKED).astype(jnp.bfloat16)
    lane = jnp.arange(128, dtype=jnp.int32)
    index = (lane % (HEAD // 2)).astype(jnp.float32)
    frequency = THETA ** (-(index * 2.0 / HEAD))
    angle = query_pos.astype(jnp.float32)[:, None] * frequency[None, :]
    cosine, sine = jnp.cos(angle), jnp.sin(angle)
    early = (lane % HEAD < HEAD // 2)[None, :]
    return (cosine, jnp.where(early, 0.0, sine), jnp.where(early, -sine, 0.0)), bias


def plain_step(layer_input, output_grad, norm_gains, block_order, weights, olds, factors, sizes):
    parts, width, half, kv, short, full, high = sizes
    query_weight, key_weight, value_weight, output_weight, gate_weight, up_weight, down_weight = weights
    (
        query_momentum,
        key_momentum,
        value_momentum,
        output_momentum,
        gate_momentum,
        up_momentum,
        down_momentum,
    ) = olds

    def sides(left, right):
        return jnp.concatenate([left, right], axis=1)

    wide = jnp.stack(
        [
            jnp.concatenate([query_weight, key_weight], axis=1),
            jnp.concatenate([output_weight, value_weight], axis=1),
            gate_weight[:, :half],
            gate_weight[:, half:],
            up_weight[:, :half],
            up_weight[:, half:],
        ]
    )
    tall = down_weight.reshape(2, high, width)
    layer_output, input_gradient, xt, dy, gains = plain_layer(
        layer_input, output_grad, wide, tall, norm_gains, block_order, sizes
    )

    def pad_rows(array):
        return padded(array, 0, 1, short, full)

    def pad_columns(array):
        return padded(array, 1, parts, short, full)

    moments = (
        pad_rows(sides(query_momentum, key_momentum)),
        pad_rows(sides(output_momentum, value_momentum)),
        pad_rows(gate_momentum),
        pad_rows(up_momentum),
        pad_columns(down_momentum),
    )
    g_wide, g_tall, s_wide, s_tall, gain_sum = reduce_gradients(xt, dy, gains, moments, full, high)
    o_wide, o_tall = orthogonalize(s_wide, s_tall, full, high, width)

    def unpack(wide_pieces, tall_pieces):
        pieces = wide_pieces[:, :short]
        tall = trimmed(tall_pieces, 2, parts, short, full).reshape(2 * high, width)
        return (
            pieces[0, :, :width],
            pieces[0, :, width:],
            pieces[1, :, width:],
            pieces[1, :, :width],
            sides(pieces[2], pieces[3]),
            sides(pieces[4], pieces[5]),
            tall,
        )

    gradients = [item.astype(jnp.float32) for item in unpack(g_wide, g_tall)]
    orthos = unpack(o_wide, o_tall)
    moments = [MOMENTUM * old + new for old, new in zip(olds, gradients)]
    new_weights = [
        weight.astype(jnp.float32) + factor * ortho.astype(jnp.float32)
        for weight, factor, ortho in zip(weights, factors, orthos)
    ]
    return layer_output, input_gradient, gradients, moments, new_weights, gain_sum


def on_device(
    layer_input,
    output_grad,
    query_weight,
    key_weight,
    value_weight,
    output_weight,
    gate_weight,
    up_weight,
    down_weight,
    norm_gains,
    query_momentum,
    key_momentum,
    value_momentum,
    output_momentum,
    gate_momentum,
    up_momentum,
    down_momentum,
    gain_momentum,
    block_order,
):
    parts = lax.axis_size("fsdp")
    width = layer_input.shape[2]
    half = gate_weight.shape[1] // 2
    kv = key_weight.shape[1]
    short = width // parts
    full = -(-short // 16) * 16
    high = half // parts
    sizes = (parts, width, half, kv, short, full, high)

    weights = (query_weight, key_weight, value_weight, output_weight, gate_weight, up_weight, down_weight)
    olds = (
        query_momentum,
        key_momentum,
        value_momentum,
        output_momentum,
        gate_momentum,
        up_momentum,
        down_momentum,
    )
    factors = []
    for index, weight in enumerate(weights):
        step_rate = OUT_RATE if index == 3 else RATE
        factors.append(-step_rate * max(1.0, weight.shape[1] / (weight.shape[0] * parts)) ** 0.5)

    fused = (
        lax.axis_size("ctx") == CLASSES
        and short == full
        and parts == 4
        and half % (2 * half // parts) == 0
        and (2 * half // parts) % 128 == 0
        and layer_input.shape[1] == 128
        and short <= 256
    )
    if fused:
        tables, bias = rotation(block_order, layer_input.shape[1])

        def turned(items):
            q, k, v, o, gate, up, down = items
            return (q, k.T, o, v.T, gate, up, down.T)

        shards, moments = turned(weights), turned(olds)
        out_turned, grad_turned, g, o, gain_sum = step_pass(
            layer_input[0].T, output_grad[0].T, norm_gains, tables, bias, shards, moments
        )
        gradients, moments, new_weights = settle(g, o, moments, shards, factors)
        layer_output, input_gradient = out_turned.T, grad_turned.T
    else:
        layer_output, input_gradient, gradients, moments, new_weights, gain_sum = plain_step(
            layer_input, output_grad, norm_gains, block_order, weights, olds, factors, sizes
        )
    gain_width = norm_gains.shape[1] // parts
    place = lax.axis_index("fsdp") * gain_width
    gain_gradient = lax.dynamic_slice_in_dim(gain_sum[:2], place, gain_width, 1)
    gain_shard = lax.dynamic_slice_in_dim(norm_gains, place, gain_width, 1)
    gain_moment = MOMENTUM * gain_momentum + gain_gradient
    new_gains = gain_shard - GAIN_RATE * gain_moment
    return (
        layer_output[None],
        input_gradient[None],
        *gradients,
        gain_gradient,
        *moments,
        gain_moment,
        *new_weights,
        new_gains,
    )


def solution(mesh):
    tokens = P("fsdp", "ctx", None)
    shard = P("fsdp", None)
    gains = P(None, "fsdp")
    return jax.shard_map(
        on_device,
        mesh=mesh,
        in_specs=(tokens, tokens) + (shard,) * 7 + (P(),) + (shard,) * 7 + (gains, P()),
        out_specs=(tokens, tokens) + ((shard,) * 7 + (gains,)) * 3,
        check_vma=False,
    )
```
